32 devices in a mesh: dp: 8 (over z, core), ctx: 4 (over y, x).
Axes of the slice: x: 2, y: 2, z: 4, core: 2. Of those that a mesh axis runs over, the one named last changes fastest.
Arguments:
- inputs: bfloat16 [8, 1024, 2048], P('dp', 'ctx'), may hold values from -6 to 6
- segments: int32 [8, 1024], P('dp'), may hold values from 0 to 3, never falling along the last dimension, each value on 1 to 512 neighbouring positions
- ln1_gain: bfloat16 [2048], P(('dp', 'ctx')), may hold values from 0.5 to 1.5
- ln1_bias: bfloat16 [2048], P(('dp', 'ctx')), may hold values from -1.5 to 1.5
- qkv_weight: bfloat16 [2048, 6144], P(('dp', 'ctx')), may hold values from -0.125 to 0.125
- qkv_bias: bfloat16 [6144], P(('dp', 'ctx')), may hold values from -2.5 to 2.5
- out_weight: bfloat16 [2048, 2048], P(('dp', 'ctx')), may hold values from -0.5 to 0.5
- ln2_gain: bfloat16 [2048], P(('dp', 'ctx')), may hold values from 0.5 to 1.5
- ln2_bias: bfloat16 [2048], P(('dp', 'ctx')), may hold values from -1.5 to 1.5
- gate_weight: bfloat16 [2048, 5632], P('dp', 'ctx'), may hold values from -0.125 to 0.125
- up_weight: bfloat16 [2048, 5632], P('dp', 'ctx'), may hold values from -0.125 to 0.125
- down_weight: bfloat16 [5632, 2048], P('ctx', 'dp'), may hold values from -0.078125 to 0.078125
- cotangent: bfloat16 [8, 1024, 2048], P('dp', 'ctx'), may hold values from -6 to 6
Outputs:
- output: bfloat16 [8, 1024, 2048], P('dp', 'ctx')
- grad_inputs: float32 [8, 1024, 2048], P('dp', 'ctx')
- grad_ln1_gain: float32 [2048], P(('dp', 'ctx'))
- grad_ln1_bias: float32 [2048], P(('dp', 'ctx'))
- grad_qkv_weight: float32 [2048, 6144], P(('dp', 'ctx'))
- grad_qkv_bias: float32 [6144], P(('dp', 'ctx'))
- grad_out_weight: float32 [2048, 2048], P(('dp', 'ctx'))
- grad_ln2_gain: float32 [2048], P(('dp', 'ctx'))
- grad_ln2_bias: float32 [2048], P(('dp', 'ctx'))
- grad_gate_weight: float32 [2048, 5632], P('dp', 'ctx')
- grad_up_weight: float32 [2048, 5632], P('dp', 'ctx')
- grad_down_weight: float32 [5632, 2048], P('ctx', 'dp')
The draws below stay inside these ranges and needn't reach their ends.
Inputs may be any that keep to these rules, and one draw needn't show every extreme that they name: `segments`: along each sequence the document numbers never fall; each document holds at most 512 tokens, and some document in the draw holds exactly that many.
All inputs are finite; a program needn't handle non-finite values.
Results may differ from the reference program's by a relative error of at most 0.015.
Values may be sent and summed in bfloat16 or wider, within the bound.
A program may use at most 256 MiB of HBM per device.

```python
import math
import jax
import jax.numpy as jnp
import numpy as np
from jax import lax

D = 2048
H = 32
HD = 64
ROT = 16
FF = 5632
LEN = 1024
DOCS = 4
NSEQ = 8


def shard_levels(rng, extent, split, smallest, largest):
    level = 1.0
    for axis_at, shards_of in split:
        steps = jax.random.uniform(jax.random.fold_in(jax.random.fold_in(rng, 6), axis_at), (shards_of,), jnp.float32, smallest / len(split), largest / len(split))
        level = level * jnp.repeat(jnp.exp(steps), extent[axis_at] // shards_of).reshape((-1,) + (1,) * (len(extent) - 1 - axis_at))
    return level


def profile(amount, total, most, lean):
    loads = [(1 << 20) // math.isqrt(standing ** lean) + 1 for standing in range(2, amount + 1)]
    surplus, counts = total - most - (amount - 1), [1] * (amount - 1)
    while surplus > 0:
        free = [i for i in range(amount - 1) if counts[i] < most]
        whole, budget = sum([loads[i] for i in free]), surplus
        for i in free:
            more = min(most - counts[i], max(1, budget * loads[i] // whole), surplus)
            counts[i] = counts[i] + more
            surplus = surplus - more
    return np.array([most] + counts)


def ragged(own_key, amount, total, most, lean):
    if amount == 2:
        one = jax.random.randint(own_key, (), max(1, total - most), min(most, total - 1) + 1)
        return jnp.stack([one, total - one])
    sizes = jnp.asarray(profile(amount, total, most, lean), jnp.int32)
    twos = (amount - 1) // 2
    donor, taker = sizes[1:1 + 2 * twos:2], sizes[2:2 + 2 * twos:2]
    room = jnp.minimum(donor - 1, most - taker)
    moved = jax.random.randint(jax.random.fold_in(own_key, 1), (twos,), 0, 1 << 20) % (room + 1)
    sizes = sizes.at[1:1 + 2 * twos:2].set(donor - moved).at[2:2 + 2 * twos:2].set(taker + moved)
    return sizes[jax.random.permutation(jax.random.fold_in(own_key, 2), amount)]


def centred(stream_key, dims, spread, reach, cuts=(), kind=jnp.bfloat16):
    level = shard_levels(stream_key, dims, cuts, -0.22, 0.18) if cuts else 1.0
    entries = jax.random.normal(stream_key, dims, jnp.float32) * spread * level
    return jnp.minimum(jnp.maximum(entries, -reach), reach).astype(kind)


def setup_inputs(seed: int = 0) -> dict:
    arg_keys = jax.random.split(jax.random.key(seed), 14)
    inputs = centred(arg_keys[0], (NSEQ, LEN, D), 1.0, 6.0, ((0, 8), (1, 4)))
    segments = jax.vmap(lambda own: jnp.searchsorted(jnp.cumsum(ragged(own, DOCS, LEN, LEN // 2, 1)), jnp.arange(LEN), side="right"))(jax.random.split(arg_keys[1], NSEQ)).reshape((NSEQ, LEN)).astype(jnp.int32)
    ln1_gain = jnp.clip(1.0 + 0.1 * jax.random.normal(arg_keys[2], (D,), jnp.float32), 0.5, 1.5).astype(jnp.bfloat16)
    ln1_bias = centred(arg_keys[3], (D,), 0.3, 1.5, ((0, 32),))
    qkv_weight = centred(arg_keys[4], (D, 3 * D), D ** -0.5, 0.125, ((0, 32),))
    qkv_bias = centred(arg_keys[5], (3 * D,), 0.5, 2.5, ((0, 32),))
    out_weight = centred(arg_keys[6], (D, D), (D // 16) ** -0.5, 0.5, ((0, 32),))
    ln2_gain = jnp.clip(1.0 + 0.1 * jax.random.normal(arg_keys[7], (D,), jnp.float32), 0.5, 1.5).astype(jnp.bfloat16)
    ln2_bias = centred(arg_keys[8], (D,), 0.3, 1.5, ((0, 32),))
    gate_weight = centred(arg_keys[9], (D, FF), D ** -0.5, 0.125, ((0, 8), (1, 4)))
    up_weight = centred(arg_keys[10], (D, FF), D ** -0.5, 0.125, ((0, 8), (1, 4)))
    down_weight = centred(arg_keys[11], (FF, D), FF ** -0.5, 0.078125, ((0, 4), (1, 8)))
    cotangent = centred(arg_keys[12], (NSEQ, LEN, D), 1.0, 6.0, ((0, 8), (1, 4)))
    return {"inputs": inputs, "segments": segments, "ln1_gain": ln1_gain, "ln1_bias": ln1_bias, "qkv_weight": qkv_weight, "qkv_bias": qkv_bias, "out_weight": out_weight, "ln2_gain": ln2_gain, "ln2_bias": ln2_bias, "gate_weight": gate_weight, "up_weight": up_weight, "down_weight": down_weight, "cotangent": cotangent}


norm_eps = 1e-05
masked_value = -1e+30
highest = lax.Precision.HIGHEST

@jax.custom_vjp
def low(v):
    return lax.optimization_barrier(v.astype(jnp.bfloat16)).astype(jnp.float32)

@jax.custom_vjp
def low_back(v):
    return v

def low_keep(v):
    return (low(v), None)

def low_pass(kept, grad):
    return (grad,)

def back_keep(v):
    return (v, None)

def back_low(kept, grad):
    return (low(grad),)
low.defvjp(low_keep, low_pass)
low_back.defvjp(back_keep, back_low)

def rotary_tables(positions, rot_dims):
    half_rot = rot_dims // 2
    freq_index = jnp.arange(half_rot, dtype=jnp.float32)
    inverse = jnp.power(jnp.float32(10000.0), -(2.0 * freq_index) / rot_dims)
    angles = positions.astype(jnp.float32)[:, None] * inverse[None, :]
    return (jnp.cos(angles), jnp.sin(angles))

def rotate(values, cosine, sine, rot_dims):
    half_rot = rot_dims // 2
    first_part = values[..., :half_rot]
    second_part = values[..., half_rot:rot_dims]
    cos_wide = cosine[:, None, :]
    sin_wide = sine[:, None, :]
    return jnp.concatenate([first_part * cos_wide - second_part * sin_wide, second_part * cos_wide + first_part * sin_wide, values[..., rot_dims:]], axis=-1)

def norm_apply(rows, gain, shift):
    row_mean = lax.optimization_barrier(jnp.mean(rows, axis=-1, keepdims=True))
    centered = rows - row_mean
    variance = lax.optimization_barrier(jnp.mean(centered * centered, axis=-1, keepdims=True))
    return centered * lax.rsqrt(variance + norm_eps) * gain + shift

def one_sequence(weights, tokens, segment_ids):
    gain_one, shift_one, joined_weight, joined_shift, out_proj, gain_two, shift_two, gate_proj, up_proj, down_proj = weights
    positions = jnp.arange(LEN, dtype=jnp.int32)
    cosine, sine = rotary_tables(positions, ROT)
    normed_one = low(norm_apply(tokens, gain_one, shift_one))
    joined = low_back(jnp.dot(normed_one, joined_weight, precision=highest) + joined_shift)
    joined = joined.reshape(LEN, 3, H, HD)
    queries = low(rotate(joined[:, 0], cosine, sine, ROT))
    keys = low(rotate(joined[:, 1], cosine, sine, ROT))
    values = low(joined[:, 2])
    scale = 1.0 / math.sqrt(HD)
    scores = low_back(jnp.einsum('qhd,khd->hqk', queries, keys, precision=highest) * scale)
    allowed = (segment_ids[:, None] == segment_ids[None, :]) & (positions[:, None] >= positions[None, :])
    scores = jnp.where(allowed[None], scores, masked_value)
    probs = low(jax.nn.softmax(scores, axis=-1))
    attended = jnp.einsum('hqk,khd->qhd', probs, values, precision=highest).reshape(LEN, D)
    attended = low(low_back(attended))
    resid = tokens + low_back(jnp.dot(attended, out_proj, precision=highest))
    normed_two = low(norm_apply(resid, gain_two, shift_two))
    gate = low_back(jnp.dot(normed_two, gate_proj, precision=highest))
    upward = low_back(jnp.dot(normed_two, up_proj, precision=highest))
    inner = low(jax.nn.silu(gate) * upward)
    return resid + jnp.dot(inner, down_proj, precision=highest)

def reference(inputs, segments, ln1_gain, ln1_bias, qkv_weight, qkv_bias, out_weight, ln2_gain, ln2_bias, gate_weight, up_weight, down_weight, cotangent):
    weights = tuple((weight_item.astype(jnp.float32) for weight_item in (ln1_gain, ln1_bias, qkv_weight, qkv_bias, out_weight, ln2_gain, ln2_bias, gate_weight, up_weight, down_weight)))
    tokens = inputs.astype(jnp.float32)
    sequence_step = jax.checkpoint(one_sequence)

    def forward(weight_set, token_set):

        def advance(carry, item):
            return (carry, sequence_step(weight_set, item[0], item[1]))
        unused, outputs = lax.scan(advance, jnp.zeros((), jnp.float32), (token_set, segments))
        return outputs
    outputs, pullback = jax.vjp(forward, weights, tokens)
    weight_grads, token_grads = pullback(cotangent.astype(jnp.float32))
    return (outputs.astype(jnp.bfloat16), token_grads, weight_grads[0], weight_grads[1], weight_grads[2], weight_grads[3], weight_grads[4], weight_grads[5], weight_grads[6], weight_grads[7], weight_grads[8], weight_grads[9])
```

```python
import functools
import math

import jax
import jax.numpy as jnp
from jax import lax
from jax.experimental import pallas as pl
from jax.experimental.pallas import tpu as pltpu
from jax.sharding import PartitionSpec as P

HD = 64
ROT = 16
DOC_MAX = 512
PAIR = 2 * HD

norm_eps = 1e-05
masked_value = -1e30
f32 = jnp.float32
bf16 = jnp.bfloat16


def dot(a, b):
    return jnp.dot(a, b, preferred_element_type=f32)


def dot_nt(a, b):
    return lax.dot_general(a, b, (((1,), (1,)), ((), ())), preferred_element_type=f32)


def dot_tn(a, b):
    return lax.dot_general(a, b, (((0,), (0,)), ((), ())), preferred_element_type=f32)


def norm_stats(rows):
    row_mean = jnp.mean(rows, axis=-1, keepdims=True)
    centered = rows - row_mean
    variance = jnp.mean(centered * centered, axis=-1, keepdims=True)
    inv_std = lax.rsqrt(variance + norm_eps)
    return centered * inv_std, inv_std


def norm_backward(grad_normed, scaled, inv_std, gain):
    grad_gain = jnp.sum(grad_normed * scaled, axis=0)
    grad_shift = jnp.sum(grad_normed, axis=0)
    inner_grad = grad_normed * gain
    grad_rows = inv_std * (
        inner_grad
        - jnp.mean(inner_grad, axis=-1, keepdims=True)
        - scaled * jnp.mean(inner_grad * scaled, axis=-1, keepdims=True)
    )
    return grad_rows, grad_gain, grad_shift


def partner(n, k):
    return [(c, c ^ k) for c in range(n)]


def hop(x, n, k):
    return lax.ppermute(x, "ctx", partner(n, k))


def gather_relative(block, n):
    if n != 4:
        return [block] + [hop(block, n, k) for k in range(1, n)]
    half = block.shape[0] // 2
    one = hop(block, n, 1)
    two = hop(block, n, 2)
    low = hop(one[:half], n, 2)
    high = hop(two[half:], n, 1)
    return [block, one, two, jnp.concatenate([low, high], axis=0)]


def gather_ctx(block, n):
    me = lax.axis_index("ctx")
    size = block.shape[0]
    parts = gather_relative(block, n)
    full = jnp.zeros((n * size,) + block.shape[1:], block.dtype)
    for k, part in enumerate(parts):
        full = lax.dynamic_update_slice_in_dim(full, part, (me ^ k) * size, 0)
    return full


def scatter_ctx(partial, n):
    me = lax.axis_index("ctx")
    size = partial.shape[0] // n

    def block(k):
        return lax.dynamic_slice_in_dim(partial, (me ^ k) * size, size, 0)

    if n != 4:
        total = block(0).astype(f32)
        for k in range(1, n):
            total = total + hop(block(k).astype(bf16), n, k).astype(f32)
        return total
    half = size // 2
    far = block(3).astype(bf16)
    low = hop(far[:half], n, 1).astype(f32)
    high = hop(far[half:], n, 2).astype(f32)
    one = block(1).astype(f32)
    two = block(2).astype(f32)
    to_one = jnp.concatenate([one[:half], one[half:] + high], axis=0).astype(bf16)
    to_two = jnp.concatenate([two[:half] + low, two[half:]], axis=0).astype(bf16)
    return block(0).astype(f32) + hop(to_one, n, 1).astype(f32) + hop(to_two, n, 2).astype(f32)


def exchange_ctx(blocks, n):
    me = lax.axis_index("ctx")
    got = lax.dynamic_update_slice_in_dim(
        jnp.zeros_like(blocks), lax.dynamic_slice_in_dim(blocks, me, 1, 0), me, 0
    )
    for k in range(1, n):
        sent = lax.dynamic_slice_in_dim(blocks, me ^ k, 1, 0)
        got = lax.dynamic_update_slice_in_dim(got, hop(sent, n, k), me ^ k, 0)
    return got


def turn(x, table_ref):
    return (
        x * table_ref[0]
        + pltpu.roll(x, PAIR - ROT // 2, 1) * table_ref[1]
        + pltpu.roll(x, ROT // 2, 1) * table_ref[2]
    )


def turn_back(x, table_ref):
    return (
        x * table_ref[0]
        - pltpu.roll(x, PAIR - ROT // 2, 1) * table_ref[1]
        - pltpu.roll(x, ROT // 2, 1) * table_ref[2]
    )


def head_lanes(shape):
    return lax.broadcasted_iota(jnp.int32, shape, 1) < HD


def span(full_len, step, at):
    return max(0, (at - DOC_MAX + 1) // step * step), at + step


def block_mask(start, at, step, low, high):
    keys = lax.broadcasted_iota(jnp.int32, (step, high - low), 1) + low
    rows = lax.broadcasted_iota(jnp.int32, (step, high - low), 0) + at
    return (keys >= start) & (keys <= rows)


def attend_kernel(step, joined_ref, bias_ref, table_ref, start_ref, out_ref, qkv_ref, lse_ref):
    full_len = joined_ref.shape[0]
    scale = 1.0 / math.sqrt(HD)
    for t in range(3):
        lanes = slice(t * PAIR, (t + 1) * PAIR)
        x = joined_ref[:, lanes] + bias_ref[:, lanes]
        if t < 2:
            x = turn(x, table_ref)
        qkv_ref[:, lanes] = x.astype(bf16)
    for at in range(0, full_len, step):
        low, high = span(full_len, step, at)
        allowed = block_mask(start_ref[at : at + step, :1], at, step, low, high)
        q = qkv_ref[at : at + step, :PAIR]
        k = qkv_ref[low:high, PAIR : 2 * PAIR]
        v = qkv_ref[low:high, 2 * PAIR :]
        total = jnp.zeros((step, PAIR), f32)
        logs = []
        for head in range(2):
            mine = head_lanes(q.shape) == (head == 0)
            s = dot_nt(jnp.where(mine, q, jnp.zeros_like(q)), k) * scale
            s = jnp.where(allowed, s, masked_value)
            top = jnp.max(s, axis=1, keepdims=True)
            e = jnp.exp(s - top)
            norm = jnp.sum(e, axis=1, keepdims=True)
            probs = (e * (1.0 / norm)).astype(bf16)
            vm = jnp.where(head_lanes(v.shape) == (head == 0), v, jnp.zeros_like(v))
            total = total + dot(probs, vm)
            logs.append(top + jnp.log(norm))
        out_ref[at : at + step, :] = total.astype(bf16)
        lse_ref[at : at + step, :] = jnp.where(head_lanes((step, PAIR)), logs[0], logs[1])


def attend_back_kernel(
    step, qkv_ref, grad_ref, lse_ref, table_ref, start_ref, out_ref, sum_ref, dk_ref, dv_ref
):
    full_len = qkv_ref.shape[0]
    scale = 1.0 / math.sqrt(HD)
    dk_ref[...] = jnp.zeros_like(dk_ref)
    dv_ref[...] = jnp.zeros_like(dv_ref)
    total = jnp.zeros((1, PAIR), f32)
    for at in range(0, full_len, step):
        low, high = span(full_len, step, at)
        rows = slice(at, at + step)
        keys = slice(low, high)
        allowed = block_mask(start_ref[rows, :1], at, step, low, high)
        q = qkv_ref[rows, :PAIR]
        k = qkv_ref[keys, PAIR : 2 * PAIR]
        v = qkv_ref[keys, 2 * PAIR :]
        g = grad_ref[rows, :]
        dq = jnp.zeros((step, PAIR), f32)
        dk = jnp.zeros((high - low, PAIR), f32)
        dv = jnp.zeros((high - low, PAIR), f32)
        for head in range(2):
            mine = head_lanes(q.shape) == (head == 0)
            qm = jnp.where(mine, q, jnp.zeros_like(q))
            gm = jnp.where(mine, g, jnp.zeros_like(g))
            km = jnp.where(head_lanes(k.shape) == (head == 0), k, jnp.zeros_like(k))
            s = dot_nt(qm, k) * scale
            probs = jnp.where(
                allowed, jnp.exp(s - lse_ref[rows, head * HD : head * HD + 1]), 0.0
            )
            dp = dot_nt(gm, v)
            mean = jnp.sum(dp * probs, axis=1, keepdims=True)
            ds = (probs * (dp - mean)).astype(bf16)
            dq = dq + dot(ds, km)
            dk = dk + dot_tn(ds, qm)
            dv = dv + dot_tn(probs.astype(bf16), gm)
        dk_ref[keys, :] += dk
        dv_ref[keys, :] += dv
        dq = turn_back(dq * scale, table_ref.at[:, rows, :]).astype(bf16)
        out_ref[rows, :PAIR] = dq
        total = total + jnp.sum(dq.astype(f32), axis=0, keepdims=True)
    sum_ref[:, :PAIR] = total
    dk = turn_back(dk_ref[...] * scale, table_ref).astype(bf16)
    out_ref[:, PAIR : 2 * PAIR] = dk
    sum_ref[:, PAIR : 2 * PAIR] = jnp.sum(dk.astype(f32), axis=0, keepdims=True)
    dv = dv_ref[...].astype(bf16)
    out_ref[:, 2 * PAIR :] = dv
    sum_ref[:, 2 * PAIR :] = jnp.sum(dv.astype(f32), axis=0, keepdims=True)


def whole(shape):
    return pl.BlockSpec(shape, lambda p: (0,) * len(shape))


def attend_step(full_len):
    return min(256, full_len)


def attend(joined, bias, table, start):
    full_len, width = joined.shape
    pairs = width // (3 * PAIR)
    step = attend_step(full_len)
    seen = sum(span(full_len, step, at)[1] - span(full_len, step, at)[0] for at in range(0, full_len, step)) * step
    wide = pl.BlockSpec((full_len, 3 * PAIR), lambda p: (0, p))
    thin = pl.BlockSpec((full_len, PAIR), lambda p: (0, p))
    return pl.pallas_call(
        functools.partial(attend_kernel, step),
        grid=(pairs,),
        in_specs=[
            wide,
            pl.BlockSpec((1, 3 * PAIR), lambda p: (0, p)),
            whole(table.shape),
            whole(start.shape),
        ],
        out_specs=[thin, wide, thin],
        out_shape=[
            jax.ShapeDtypeStruct((full_len, pairs * PAIR), bf16),
            jax.ShapeDtypeStruct((full_len, width), bf16),
            jax.ShapeDtypeStruct((full_len, pairs * PAIR), f32),
        ],
        compiler_params=pltpu.CompilerParams(vmem_limit_bytes=40 << 20),
        cost_estimate=pl.CostEstimate(
            flops=pairs * seen * PAIR * 8, transcendentals=pairs * seen * 2, bytes_accessed=full_len * width * 8
        ),
    )(joined, bias, table, start)


def attend_back(qkv, grad, lse, table, start):
    full_len, width = qkv.shape
    pairs = width // (3 * PAIR)
    step = attend_step(full_len)
    seen = sum(span(full_len, step, at)[1] - span(full_len, step, at)[0] for at in range(0, full_len, step)) * step
    wide = pl.BlockSpec((full_len, 3 * PAIR), lambda p: (0, p))
    thin = pl.BlockSpec((full_len, PAIR), lambda p: (0, p))
    return pl.pallas_call(
        functools.partial(attend_back_kernel, step),
        grid=(pairs,),
        in_specs=[wide, thin, thin, whole(table.shape), whole(start.shape)],
        out_specs=[wide, pl.BlockSpec((1, 3 * PAIR), lambda p: (0, p))],
        out_shape=[
            jax.ShapeDtypeStruct((full_len, width), bf16),
            jax.ShapeDtypeStruct((1, width), f32),
        ],
        scratch_shapes=[pltpu.VMEM((full_len, PAIR), f32), pltpu.VMEM((full_len, PAIR), f32)],
        compiler_params=pltpu.CompilerParams(vmem_limit_bytes=40 << 20),
        cost_estimate=pl.CostEstimate(
            flops=pairs * seen * PAIR * 20, transcendentals=pairs * seen * 2, bytes_accessed=full_len * width * 8
        ),
    )(qkv, grad, lse, table, start)


def rotary_table(full_len):
    half = ROT // 2
    freq = jnp.arange(half, dtype=f32)
    inverse = jnp.power(f32(10000.0), -(2.0 * freq) / ROT)
    angles = jnp.arange(full_len, dtype=jnp.int32).astype(f32)[:, None] * inverse[None, :]
    cosine, sine = jnp.cos(angles), jnp.sin(angles)
    rest = jnp.zeros((full_len, HD - ROT), f32)
    none = jnp.zeros_like(sine)
    keep = jnp.concatenate([cosine, cosine, rest + 1.0], axis=1)
    ahead = jnp.concatenate([-sine, none, rest], axis=1)
    behind = jnp.concatenate([none, sine, rest], axis=1)
    return jnp.stack([jnp.concatenate([t, t], axis=1) for t in (keep, ahead, behind)])


def shards(
    dp,
    ctx,
    inputs,
    segments,
    ln1_gain,
    ln1_bias,
    qkv_weight,
    qkv_bias,
    out_weight,
    ln2_gain,
    ln2_bias,
    gate_weight,
    up_weight,
    down_weight,
    cotangent,
):
    local_len, width = inputs.shape[1], inputs.shape[2]
    full_len = segments.shape[1]
    heads = width // HD
    near = heads // ctx
    pairs = near // 2
    me = lax.axis_index("ctx")
    own = me * local_len

    small = jnp.concatenate([ln1_gain, ln1_bias, ln2_gain, ln2_bias, qkv_bias])
    small = lax.all_gather(small[None, :], ("dp", "ctx"), axis=0, tiled=True).astype(f32)
    part = ln1_gain.shape[0]
    gain_one, shift_one, gain_two, shift_two = [
        small[:, i * part : (i + 1) * part].reshape(width) for i in range(4)
    ]
    bias = small[:, 4 * part :].reshape(3, pairs, 2, ctx, HD)
    bias = lax.dynamic_index_in_dim(bias, me, 3, keepdims=False)
    bias = bias.transpose(1, 0, 2, 3).reshape(1, near * 3 * HD)

    rows_here = qkv_weight.shape[0]
    blocks = qkv_weight.reshape(rows_here, 3, pairs, 2, ctx, HD).transpose(4, 0, 2, 1, 3, 5)
    blocks = exchange_ctx(blocks.reshape(ctx, rows_here, near * 3 * HD), ctx)
    joined_weight = lax.all_gather(
        blocks.reshape(ctx * rows_here, near * 3 * HD), "dp", axis=0, tiled=True
    )
    if part == HD:
        out_full = lax.all_gather(out_weight, "dp", axis=0, tiled=True)
    else:
        out_full = lax.all_gather(out_weight, ("dp", "ctx"), axis=0, tiled=True)
        out_full = out_full.reshape(near, ctx, HD, width)
        out_full = lax.dynamic_index_in_dim(out_full, me, 1, keepdims=False)
        out_full = out_full.reshape(near * HD, width)
    gate_full = lax.all_gather(gate_weight, "dp", axis=0, tiled=True)
    up_full = lax.all_gather(up_weight, "dp", axis=0, tiled=True)
    down_full = lax.all_gather(down_weight, "dp", axis=1, tiled=True)

    rows = inputs[0]
    rows_wide = gather_ctx(rows, ctx)
    grad_rows = cotangent[0]
    grad_wide = gather_ctx(grad_rows, ctx)

    segment = segments[0]
    start = jnp.sum((segment[None, :] < segment[:, None]).astype(jnp.int32), axis=1)
    start = jnp.broadcast_to(start[:, None], (full_len, 128))
    table = rotary_table(full_len)
    scaled_wide, _ = norm_stats(rows_wide.astype(f32))
    normed_one = (scaled_wide * gain_one + shift_one).astype(bf16)
    joined = dot(normed_one, joined_weight)
    attended, qkv, lse = attend(joined, bias, table, start)
    resid = rows.astype(f32) + scatter_ctx(dot(attended, out_full), ctx)

    scaled_two, inv_two = norm_stats(resid)
    normed_two = (scaled_two * gain_two + shift_two).astype(bf16)
    normed_wide = gather_ctx(normed_two, ctx)
    gate = dot(normed_wide, gate_full)
    upward = dot(normed_wide, up_full)
    sigma = jax.nn.sigmoid(gate)
    swish = gate * sigma
    inner = (swish * upward).astype(bf16)
    d_inner = dot_nt(grad_wide, down_full)
    d_gate = (d_inner * upward * sigma * (1.0 + gate * (1.0 - sigma))).astype(bf16)
    d_upward = (d_inner * swish).astype(bf16)
    d_normed_two = scatter_ctx(dot_nt(d_gate, gate_full) + dot_nt(d_upward, up_full), ctx)
    output = (resid + scatter_ctx(dot(inner, down_full), ctx)).astype(bf16)
    d_down = dot_tn(inner, grad_wide).astype(bf16)
    d_gate_weight = dot_tn(normed_wide, d_gate).astype(bf16)
    d_up_weight = dot_tn(normed_wide, d_upward).astype(bf16)
    d_down = lax.psum_scatter(d_down, "dp", scatter_dimension=1, tiled=True).astype(f32)
    d_gate_weight = lax.psum_scatter(d_gate_weight, "dp", scatter_dimension=0, tiled=True).astype(f32)
    d_up_weight = lax.psum_scatter(d_up_weight, "dp", scatter_dimension=0, tiled=True).astype(f32)

    d_resid_norm, d_gain_two, d_shift_two = norm_backward(d_normed_two, scaled_two, inv_two, gain_two)
    d_resid = grad_rows.astype(f32) + d_resid_norm
    d_proj = gather_ctx(d_resid.astype(bf16), ctx)
    d_attended = dot_nt(d_proj, out_full).astype(bf16)
    d_out_weight = dot_tn(attended, d_proj).astype(bf16)
    if part == HD:
        d_out_weight = lax.psum_scatter(d_out_weight, "dp", scatter_dimension=0, tiled=True)
    else:
        at_me = lax.broadcasted_iota(jnp.int32, (1, ctx, 1, 1), 1) == me
        d_out_weight = jnp.where(at_me, d_out_weight.reshape(near, 1, HD, width), jnp.zeros((), bf16))
        d_out_weight = lax.psum_scatter(
            d_out_weight.reshape(width, width), ("dp", "ctx"), scatter_dimension=0, tiled=True
        )
    d_out_weight = d_out_weight.astype(f32)

    d_joined, d_bias = attend_back(qkv, d_attended, lse, table, start)
    d_normed_one = scatter_ctx(dot_nt(d_joined, joined_weight), ctx)
    d_joined_weight = lax.psum_scatter(
        dot_tn(normed_one, d_joined).astype(bf16), "dp", scatter_dimension=0, tiled=True
    )
    blocks = exchange_ctx(d_joined_weight.reshape(ctx, rows_here, near * 3 * HD), ctx)
    blocks = blocks.reshape(ctx, rows_here, pairs, 3, 2, HD).transpose(1, 3, 2, 4, 0, 5)
    d_joined_weight = blocks.reshape(rows_here, 3 * width).astype(f32)

    scaled_one, inv_one = norm_stats(rows.astype(f32))
    d_rows_norm, d_gain_one, d_shift_one = norm_backward(d_normed_one, scaled_one, inv_one, gain_one)
    grad_input = d_resid + d_rows_norm

    d_bias = d_bias.reshape(pairs, 3, 2, HD).transpose(1, 0, 2, 3)[:, :, :, None, :]
    at_me = (lax.broadcasted_iota(jnp.int32, (1, 1, 1, ctx, 1), 3) == me).astype(f32)
    d_bias = (d_bias * at_me).reshape(dp * ctx, -1)
    small = jnp.concatenate(
        [t.reshape(dp * ctx, part) for t in (d_gain_one, d_shift_one, d_gain_two, d_shift_two)]
        + [d_bias],
        axis=1,
    )
    small = lax.psum_scatter(small, ("dp", "ctx"), scatter_dimension=0, tiled=True)[0]
    d_gain_one, d_shift_one, d_gain_two, d_shift_two = [
        small[i * part : (i + 1) * part] for i in range(4)
    ]
    return (
        output[None],
        grad_input[None],
        d_gain_one,
        d_shift_one,
        d_joined_weight,
        small[4 * part :],
        d_out_weight,
        d_gain_two,
        d_shift_two,
        d_gate_weight,
        d_up_weight,
        d_down,
    )


def solution(mesh):
    every = ("dp", "ctx")
    return jax.shard_map(
        functools.partial(shards, mesh.shape["dp"], mesh.shape["ctx"]),
        mesh=mesh,
        in_specs=(
            P("dp", "ctx", None),
            P("dp", None),
            P(every),
            P(every),
            P(every, None),
            P(every),
            P(every, None),
            P(every),
            P(every),
            P("dp", "ctx"),
            P("dp", "ctx"),
            P("ctx", "dp"),
            P("dp", "ctx", None),
        ),
        out_specs=(
            P("dp", "ctx", None),
            P("dp", "ctx", None),
            P(every),
            P(every),
            P(every, None),
            P(every),
            P(every, None),
            P(every),
            P(every),
            P("dp", "ctx"),
            P("dp", "ctx"),
            P("ctx", "dp"),
        ),
        check_vma=False,
    )
```

```python
import functools
import math

import jax
import jax.numpy as jnp
from jax import lax
from jax.experimental import pallas as pl
from jax.experimental.pallas import tpu as pltpu
from jax.sharding import PartitionSpec as P

HD = 64
ROT = 16
DOC_MAX = 512
PAIR = 2 * HD

norm_eps = 1e-05
masked_value = -1e30
f32 = jnp.float32
bf16 = jnp.bfloat16


def dot(a, b):
    return jnp.dot(a, b, preferred_element_type=f32)


def dot_nt(a, b):
    return lax.dot_general(a, b, (((1,), (1,)), ((), ())), preferred_element_type=f32)


def dot_tn(a, b):
    return lax.dot_general(a, b, (((0,), (0,)), ((), ())), preferred_element_type=f32)


def norm_stats(rows):
    row_mean = jnp.mean(rows, axis=-1, keepdims=True)
    centered = rows - row_mean
    variance = jnp.mean(centered * centered, axis=-1, keepdims=True)
    inv_std = lax.rsqrt(variance + norm_eps)
    return centered * inv_std, inv_std


def norm_backward(grad_normed, scaled, inv_std, gain):
    grad_gain = jnp.sum(grad_normed * scaled, axis=0)
    grad_shift = jnp.sum(grad_normed, axis=0)
    inner_grad = grad_normed * gain
    grad_rows = inv_std * (
        inner_grad
        - jnp.mean(inner_grad, axis=-1, keepdims=True)
        - scaled * jnp.mean(inner_grad * scaled, axis=-1, keepdims=True)
    )
    return grad_rows, grad_gain, grad_shift


def partner(n, k):
    return [(c, c ^ k) for c in range(n)]


def hop(x, n, k):
    return lax.ppermute(x, "ctx", partner(n, k))


def gather_relative(block, n):
    if n != 4:
        return [block] + [hop(block, n, k) for k in range(1, n)]
    half = block.shape[0] // 2
    one = hop(block, n, 1)
    two = hop(block, n, 2)
    low = hop(one[:half], n, 2)
    high = hop(two[half:], n, 1)
    return [block, one, two, jnp.concatenate([low, high], axis=0)]


def gather_ctx(block, n):
    me = lax.axis_index("ctx")
    size = block.shape[0]
    parts = gather_relative(block, n)
    full = jnp.zeros((n * size,) + block.shape[1:], block.dtype)
    for k, part in enumerate(parts):
        full = lax.dynamic_update_slice_in_dim(full, part, (me ^ k) * size, 0)
    return full


def scatter_ctx(partial, n, meanwhile=None):
    me = lax.axis_index("ctx")
    size = partial.shape[0] // n

    def block(k):
        return lax.dynamic_slice_in_dim(partial, (me ^ k) * size, size, 0)

    if n != 4:
        total = block(0).astype(f32)
        for k in range(1, n):
            total = total + hop(block(k).astype(bf16), n, k).astype(f32)
        return total
    half = size // 2
    far = block(3).astype(bf16)
    low = hop(far[:half], n, 1).astype(f32)
    high = hop(far[half:], n, 2).astype(f32)
    if meanwhile is not None:
        partial, _ = lax.optimization_barrier((partial, meanwhile))
    one = block(1).astype(f32)
    two = block(2).astype(f32)
    to_one = jnp.concatenate([one[:half], one[half:] + high], axis=0).astype(bf16)
    to_two = jnp.concatenate([two[:half] + low, two[half:]], axis=0).astype(bf16)
    return block(0).astype(f32) + hop(to_one, n, 1).astype(f32) + hop(to_two, n, 2).astype(f32)


def exchange_ctx(blocks, n):
    me = lax.axis_index("ctx")
    got = lax.dynamic_update_slice_in_dim(
        jnp.zeros_like(blocks), lax.dynamic_slice_in_dim(blocks, me, 1, 0), me, 0
    )
    for k in range(1, n):
        sent = lax.dynamic_slice_in_dim(blocks, me ^ k, 1, 0)
        got = lax.dynamic_update_slice_in_dim(got, hop(sent, n, k), me ^ k, 0)
    return got


MESH = pl.DeviceIdType.MESH
ANY = pl.BlockSpec(memory_space=pl.ANY)


class Place:
    def __init__(self, dp):
        self.row = lax.axis_index("dp")
        self.col = lax.axis_index("ctx")
        self.lines = dp // 2
        self.line = self.row // 2
        self.core = self.row % 2
        self.twin = (self.row + 1 - 2 * self.core, self.col)

    def other(self, k):
        col, bit = self.col, 1
        while bit <= k:
            if k & bit:
                col = col + bit * (1 - 2 * ((self.col // bit) % 2))
            bit *= 2
        return col

    def across(self, k):
        return (self.row, self.other(k))

    def above(self):
        return (self.row + 2, self.col)

    def below(self):
        return (self.row - 2, self.col)


def greet(place, ctx, column=False):
    barrier = pltpu.get_barrier_semaphore()
    for k in range(1, ctx):
        pl.semaphore_signal(barrier, 1, device_id=place.across(k), device_id_type=MESH)
    if not column:
        pl.semaphore_wait(barrier, ctx - 1)
        return
    pl.semaphore_signal(barrier, 1, device_id=place.twin, device_id_type=MESH)

    @pl.when(place.line > 0)
    def _():
        pl.semaphore_signal(barrier, 1, device_id=place.below(), device_id_type=MESH)

    @pl.when(place.line < place.lines - 1)
    def _():
        pl.semaphore_signal(barrier, 1, device_id=place.above(), device_id_type=MESH)

    peers = ctx + (place.line > 0).astype(jnp.int32) + (place.line < place.lines - 1).astype(jnp.int32)
    pl.semaphore_wait(barrier, peers)


def remote(src, dst, send, recv, device):
    return pltpu.make_async_remote_copy(
        src_ref=src, dst_ref=dst, send_sem=send, recv_sem=recv, device_id=device, device_id_type=MESH
    )


class LineGather:
    def __init__(self, place, shard, sems):
        self.place, self.shard, self.sems = place, shard, sems

    def row(self, line):
        return line * 2 + self.place.core

    def up(self, hop):
        part = self.shard(self.row(self.place.line - hop + 1))
        return remote(part, part, self.sems.at[0, hop], self.sems.at[1, hop], self.place.above())

    def down(self, hop):
        part = self.shard(self.row(self.place.line + hop - 1))
        return remote(part, part, self.sems.at[2, hop], self.sems.at[3, hop], self.place.below())

    def over(self, at, row):
        part = self.shard(row)
        return remote(part, part, self.sems.at[4, at], self.sems.at[5, at], self.place.twin)

    def sends_up(self, hop):
        return (self.place.line - hop + 1 >= 0) & (self.place.line < self.place.lines - 1)

    def sends_down(self, hop):
        return (self.place.line + hop - 1 < self.place.lines) & (self.place.line > 0)

    def send(self, hop):
        place = self.place
        pl.when(self.sends_up(hop))(lambda: self.up(hop).start())
        pl.when(self.sends_down(hop))(lambda: self.down(hop).start())
        if hop == 1:
            self.over(0, place.row).start()

    def receive(self, hop):
        place = self.place

        @pl.when(place.line - hop >= 0)
        def _():
            part = self.shard(self.row(place.line - hop))
            remote(part, part, self.sems.at[0, hop], self.sems.at[1, hop], place.twin).wait_recv()
            self.over(hop, self.row(place.line - hop)).start()

        @pl.when(place.line + hop < place.lines)
        def _():
            part = self.shard(self.row(place.line + hop))
            remote(part, part, self.sems.at[2, hop], self.sems.at[3, hop], place.twin).wait_recv()
            self.over(place.lines - 1 + hop, self.row(place.line + hop)).start()

    def finish(self):
        place = self.place
        self.over(0, place.row).wait_send()
        other = 1 - 2 * place.core
        remote(
            self.shard(place.row + other), self.shard(place.row + other),
            self.sems.at[4, 0], self.sems.at[5, 0], place.twin,
        ).wait_recv()
        for hop in range(1, place.lines):
            pl.when(self.sends_up(hop))(lambda: self.up(hop).wait_send())
            pl.when(self.sends_down(hop))(lambda: self.down(hop).wait_send())
            for at, line, there in (
                (hop, place.line - hop, place.line - hop >= 0),
                (place.lines - 1 + hop, place.line + hop, place.line + hop < place.lines),
            ):

                @pl.when(there)
                def _():
                    row = self.row(line)
                    self.over(at, row).wait_send()
                    part = self.shard(row + other)
                    remote(part, part, self.sems.at[4, at], self.sems.at[5, at], place.twin).wait_recv()

    @staticmethod
    def scratch(dp):
        return pltpu.SemaphoreType.DMA((6, dp))


class CtxGather:
    def __init__(self, place, block, full, size, sems):
        self.place, self.block, self.full, self.size, self.sems = place, block, full, size, sems

    def rows(self, col, start=0, size=None):
        size = self.size if size is None else size
        return self.full.at[pl.ds(pl.multiple_of(col * self.size + start, size), size), :]

    def copies(self):
        place, half = self.place, self.size // 2
        me = place.col
        return [
            remote(self.block, self.rows(me), self.sems.at[0, 0], self.sems.at[1, 0], place.across(1)),
            remote(self.block, self.rows(me), self.sems.at[0, 1], self.sems.at[1, 1], place.across(2)),
            remote(
                self.rows(place.other(1), 0, half), self.rows(place.other(1), 0, half),
                self.sems.at[0, 2], self.sems.at[1, 2], place.across(2),
            ),
            remote(
                self.rows(place.other(2), half, half), self.rows(place.other(2), half, half),
                self.sems.at[0, 3], self.sems.at[1, 3], place.across(1),
            ),
        ]

    def arrivals(self):
        place, half = self.place, self.size // 2
        me = place.col
        parts = [self.rows(place.other(1)), self.rows(place.other(2)), self.rows(place.other(3), 0, half), self.rows(place.other(3), half, half)]
        return [
            remote(part, part, self.sems.at[0, i], self.sems.at[1, i], place.across(1))
            for i, part in enumerate(parts)
        ]

    def first(self):
        copies = self.copies()
        copies[0].start()
        copies[1].start()

    def second(self):
        copies, arrivals = self.copies(), self.arrivals()
        arrivals[0].wait_recv()
        copies[2].start()
        arrivals[1].wait_recv()
        copies[3].start()

    def finish(self):
        copies, arrivals = self.copies(), self.arrivals()
        arrivals[2].wait_recv()
        arrivals[3].wait_recv()
        for copy in copies:
            copy.wait_send()

    @staticmethod
    def scratch():
        return pltpu.SemaphoreType.DMA((2, 4))


def opening_kernel(
    dp, ctx,
    small_ref, blocks_ref, out_weight_ref, rows_ref, cot_ref,
    small_all, joined_all, out_all, rows_all, cot_all,
    local_sem, swap_sem, line_small, line_joined, line_out, rows_sem, cot_sem,
):
    place = Place(dp)
    greet(place, ctx, column=True)
    me, row = place.col, place.row
    depth = blocks_ref.shape[1]
    length = rows_ref.shape[0]
    rows_out = out_weight_ref.shape[0]

    def joined_rows(row, col):
        return joined_all.at[pl.ds(pl.multiple_of((row * ctx + col) * depth, depth), depth), :]

    def joined_shard(row):
        return joined_all.at[pl.ds(pl.multiple_of(row * (ctx * depth), ctx * depth), ctx * depth), :]

    def out_shard(row):
        return out_all.at[pl.ds(pl.multiple_of(row * rows_out, rows_out), rows_out), :]

    local = [
        pltpu.make_async_copy(small_ref, small_all.at[row, me], local_sem.at[0]),
        pltpu.make_async_copy(blocks_ref.at[me], joined_rows(row, me), local_sem.at[1]),
        pltpu.make_async_copy(out_weight_ref, out_shard(row), local_sem.at[2]),
        pltpu.make_async_copy(rows_ref, rows_all.at[pl.ds(pl.multiple_of(me * length, length), length), :], local_sem.at[3]),
        pltpu.make_async_copy(cot_ref, cot_all.at[pl.ds(pl.multiple_of(me * length, length), length), :], local_sem.at[4]),
    ]
    swaps, arrivals = [], []
    for k in range(1, ctx):
        swaps.append(remote(small_ref, small_all.at[row, me], swap_sem.at[0, k], swap_sem.at[1, k], place.across(k)))
        swaps.append(
            remote(blocks_ref.at[place.other(k)], joined_rows(row, me), swap_sem.at[2, k], swap_sem.at[3, k], place.across(k))
        )
        arrivals.append(
            remote(small_ref, small_all.at[row, place.other(k)], swap_sem.at[0, k], swap_sem.at[1, k], place.across(k))
        )
        part = joined_rows(row, place.other(k))
        arrivals.append(remote(part, part, swap_sem.at[2, k], swap_sem.at[3, k], place.across(k)))
    for copy in swaps:
        copy.start()
    for copy in local:
        copy.start()
    rows_gather = CtxGather(place, rows_ref, rows_all, length, rows_sem)
    cot_gather = CtxGather(place, cot_ref, cot_all, length, cot_sem)
    lines = [
        LineGather(place, lambda row: small_all.at[row], line_small),
        LineGather(place, joined_shard, line_joined),
        LineGather(place, out_shard, line_out),
    ]
    rows_gather.first()
    for copy in local[:2]:
        copy.wait()
    for copy in arrivals:
        copy.wait_recv()
    lines[0].send(1)
    lines[1].send(1)
    local[2].wait()
    lines[2].send(1)
    rows_gather.second()
    cot_gather.first()
    for hop in range(1, place.lines):
        for line in lines:
            line.receive(hop)
            if hop < place.lines - 1:
                line.send(hop + 1)
        if hop == 1:
            cot_gather.second()
    for line in lines:
        line.finish()
    rows_gather.finish()
    cot_gather.finish()
    for copy in swaps:
        copy.wait_send()
    local[3].wait()
    local[4].wait()


def opening(dp, ctx, small, blocks, out_weight, rows, cot):
    depth, cols = blocks.shape[1:]
    shapes = [
        jax.ShapeDtypeStruct((dp, ctx) + small.shape, small.dtype),
        jax.ShapeDtypeStruct((dp * ctx * depth, cols), bf16),
        jax.ShapeDtypeStruct((dp * out_weight.shape[0], out_weight.shape[1]), bf16),
        jax.ShapeDtypeStruct((ctx * rows.shape[0], rows.shape[1]), bf16),
        jax.ShapeDtypeStruct((ctx * cot.shape[0], cot.shape[1]), bf16),
    ]
    return pl.pallas_call(
        functools.partial(opening_kernel, dp, ctx),
        in_specs=[ANY] * 5,
        out_specs=[ANY] * 5,
        out_shape=shapes,
        scratch_shapes=[
            pltpu.SemaphoreType.DMA((5,)),
            pltpu.SemaphoreType.DMA((4, ctx)),
            LineGather.scratch(dp),
            LineGather.scratch(dp),
            LineGather.scratch(dp),
            CtxGather.scratch(),
            CtxGather.scratch(),
        ],
        compiler_params=pltpu.CompilerParams(collective_id=0, has_side_effects=True),
        cost_estimate=pl.CostEstimate(flops=0, transcendentals=0, bytes_accessed=200 << 20),
    )(small, blocks, out_weight, rows, cot)


def closing_kernel(dp, ctx, parts_ref, out_ref, near, swap_sem, far, line_sem):
    place = Place(dp)
    me, row = place.col, place.row
    barrier = pltpu.get_barrier_semaphore()
    for k in range(1, ctx):
        pl.semaphore_signal(barrier, 1, device_id=place.across(k), device_id_type=MESH)
    for k in range(1, dp):
        pl.semaphore_signal(barrier, 1, device_id=((row + k) % dp, me), device_id_type=MESH)
    pl.semaphore_wait(barrier, ctx + dp - 2)
    swaps = [
        remote(parts_ref.at[place.other(k)], near.at[k], swap_sem.at[0, k], swap_sem.at[1, k], place.across(k))
        for k in range(1, ctx)
    ]
    for copy in swaps:
        copy.start()
    total = parts_ref[me]
    for k in range(1, ctx):
        swaps[k - 1].wait()
        total = total + near[k]
    near[0] = total
    sends = [
        remote(near.at[0, (row + k) % dp], far.at[k], line_sem.at[0, k], line_sem.at[1, k], ((row + k) % dp, me))
        for k in range(1, dp)
    ]
    for copy in sends:
        copy.start()
    total = near[0, row]
    for k in range(1, dp):
        sends[k - 1].wait()
        total = total + far[k]
    out_ref[...] = total


def closing(dp, ctx, parts):
    tile = parts.shape[2:]
    return pl.pallas_call(
        functools.partial(closing_kernel, dp, ctx),
        in_specs=[pl.BlockSpec(memory_space=pltpu.VMEM)],
        out_specs=pl.BlockSpec(memory_space=pltpu.VMEM),
        out_shape=jax.ShapeDtypeStruct(tile, f32),
        scratch_shapes=[
            pltpu.VMEM((ctx, dp) + tile, f32),
            pltpu.SemaphoreType.DMA((2, ctx)),
            pltpu.VMEM((dp,) + tile, f32),
            pltpu.SemaphoreType.DMA((2, dp)),
        ],
        compiler_params=pltpu.CompilerParams(collective_id=1, has_side_effects=True),
        cost_estimate=pl.CostEstimate(flops=0, transcendentals=0, bytes_accessed=20 << 20),
    )(parts)


def turn(x, table_ref):
    return (
        x * table_ref[0]
        + pltpu.roll(x, PAIR - ROT // 2, 1) * table_ref[1]
        + pltpu.roll(x, ROT // 2, 1) * table_ref[2]
    )


def turn_back(x, table_ref):
    return (
        x * table_ref[0]
        - pltpu.roll(x, PAIR - ROT // 2, 1) * table_ref[1]
        - pltpu.roll(x, ROT // 2, 1) * table_ref[2]
    )


def head_lanes(shape):
    return lax.broadcasted_iota(jnp.int32, shape, 1) < HD


def span(full_len, step, at):
    return max(0, (at - DOC_MAX + 1) // step * step), at + step


def block_mask(start, at, step, low, high):
    keys = lax.broadcasted_iota(jnp.int32, (step, high - low), 1) + low
    rows = lax.broadcasted_iota(jnp.int32, (step, high - low), 0) + at
    return (keys >= start) & (keys <= rows)


def attend_kernel(step, joined_ref, bias_ref, table_ref, start_ref, out_ref, qkv_ref, lse_ref):
    full_len = joined_ref.shape[0]
    scale = 1.0 / math.sqrt(HD)
    for t in range(3):
        lanes = slice(t * PAIR, (t + 1) * PAIR)
        x = joined_ref[:, lanes] + bias_ref[:, lanes]
        if t < 2:
            x = turn(x, table_ref)
        qkv_ref[:, lanes] = x.astype(bf16)
    for at in range(0, full_len, step):
        low, high = span(full_len, step, at)
        allowed = block_mask(start_ref[at : at + step, :1], at, step, low, high)
        q = qkv_ref[at : at + step, :PAIR]
        k = qkv_ref[low:high, PAIR : 2 * PAIR]
        v = qkv_ref[low:high, 2 * PAIR :]
        total = jnp.zeros((step, PAIR), f32)
        logs = []
        for head in range(2):
            mine = head_lanes(q.shape) == (head == 0)
            s = dot_nt(jnp.where(mine, q, jnp.zeros_like(q)), k) * scale
            s = jnp.where(allowed, s, masked_value)
            top = jnp.max(s, axis=1, keepdims=True)
            e = jnp.exp(s - top)
            norm = jnp.sum(e, axis=1, keepdims=True)
            probs = (e * (1.0 / norm)).astype(bf16)
            vm = jnp.where(head_lanes(v.shape) == (head == 0), v, jnp.zeros_like(v))
            total = total + dot(probs, vm)
            logs.append(top + jnp.log(norm))
        out_ref[at : at + step, :] = total.astype(bf16)
        lse_ref[at : at + step, :] = jnp.where(head_lanes((step, PAIR)), logs[0], logs[1])


def attend_back_kernel(
    step, qkv_ref, grad_ref, lse_ref, table_ref, start_ref, out_ref, sum_ref, dk_ref, dv_ref
):
    full_len = qkv_ref.shape[0]
    scale = 1.0 / math.sqrt(HD)
    dk_ref[...] = jnp.zeros_like(dk_ref)
    dv_ref[...] = jnp.zeros_like(dv_ref)
    total = jnp.zeros((1, PAIR), f32)
    for at in range(0, full_len, step):
        low, high = span(full_len, step, at)
        rows = slice(at, at + step)
        keys = slice(low, high)
        allowed = block_mask(start_ref[rows, :1], at, step, low, high)
        q = qkv_ref[rows, :PAIR]
        k = qkv_ref[keys, PAIR : 2 * PAIR]
        v = qkv_ref[keys, 2 * PAIR :]
        g = grad_ref[rows, :]
        dq = jnp.zeros((step, PAIR), f32)
        dk = jnp.zeros((high - low, PAIR), f32)
        dv = jnp.zeros((high - low, PAIR), f32)
        for head in range(2):
            mine = head_lanes(q.shape) == (head == 0)
            qm = jnp.where(mine, q, jnp.zeros_like(q))
            gm = jnp.where(mine, g, jnp.zeros_like(g))
            km = jnp.where(head_lanes(k.shape) == (head == 0), k, jnp.zeros_like(k))
            s = dot_nt(qm, k) * scale
            probs = jnp.where(
                allowed, jnp.exp(s - lse_ref[rows, head * HD : head * HD + 1]), 0.0
            )
            dp = dot_nt(gm, v)
            mean = jnp.sum(dp * probs, axis=1, keepdims=True)
            ds = (probs * (dp - mean)).astype(bf16)
            dq = dq + dot(ds, km)
            dk = dk + dot_tn(ds, qm)
            dv = dv + dot_tn(probs.astype(bf16), gm)
        dk_ref[keys, :] += dk
        dv_ref[keys, :] += dv
        dq = turn_back(dq * scale, table_ref.at[:, rows, :]).astype(bf16)
        out_ref[rows, :PAIR] = dq
        total = total + jnp.sum(dq.astype(f32), axis=0, keepdims=True)
    sum_ref[:, :PAIR] = total
    dk = turn_back(dk_ref[...] * scale, table_ref).astype(bf16)
    out_ref[:, PAIR : 2 * PAIR] = dk
    sum_ref[:, PAIR : 2 * PAIR] = jnp.sum(dk.astype(f32), axis=0, keepdims=True)
    dv = dv_ref[...].astype(bf16)
    out_ref[:, 2 * PAIR :] = dv
    sum_ref[:, 2 * PAIR :] = jnp.sum(dv.astype(f32), axis=0, keepdims=True)


def whole(shape):
    return pl.BlockSpec(shape, lambda p: (0,) * len(shape))


def attend_step(full_len):
    return min(256, full_len)


def attend(joined, bias, table, start):
    full_len, width = joined.shape
    pairs = width // (3 * PAIR)
    step = attend_step(full_len)
    seen = sum(span(full_len, step, at)[1] - span(full_len, step, at)[0] for at in range(0, full_len, step)) * step
    wide = pl.BlockSpec((full_len, 3 * PAIR), lambda p: (0, p))
    thin = pl.BlockSpec((full_len, PAIR), lambda p: (0, p))
    return pl.pallas_call(
        functools.partial(attend_kernel, step),
        grid=(pairs,),
        in_specs=[
            wide,
            pl.BlockSpec((1, 3 * PAIR), lambda p: (0, p)),
            whole(table.shape),
            whole(start.shape),
        ],
        out_specs=[thin, wide, thin],
        out_shape=[
            jax.ShapeDtypeStruct((full_len, pairs * PAIR), bf16),
            jax.ShapeDtypeStruct((full_len, width), bf16),
            jax.ShapeDtypeStruct((full_len, pairs * PAIR), f32),
        ],
        compiler_params=pltpu.CompilerParams(vmem_limit_bytes=40 << 20),
        cost_estimate=pl.CostEstimate(
            flops=pairs * seen * PAIR * 8, transcendentals=pairs * seen * 2, bytes_accessed=full_len * width * 8
        ),
    )(joined, bias, table, start)


def attend_back(qkv, grad, lse, table, start):
    full_len, width = qkv.shape
    pairs = width // (3 * PAIR)
    step = attend_step(full_len)
    seen = sum(span(full_len, step, at)[1] - span(full_len, step, at)[0] for at in range(0, full_len, step)) * step
    wide = pl.BlockSpec((full_len, 3 * PAIR), lambda p: (0, p))
    thin = pl.BlockSpec((full_len, PAIR), lambda p: (0, p))
    return pl.pallas_call(
        functools.partial(attend_back_kernel, step),
        grid=(pairs,),
        in_specs=[wide, thin, thin, whole(table.shape), whole(start.shape)],
        out_specs=[wide, pl.BlockSpec((1, 3 * PAIR), lambda p: (0, p))],
        out_shape=[
            jax.ShapeDtypeStruct((full_len, width), bf16),
            jax.ShapeDtypeStruct((1, width), f32),
        ],
        scratch_shapes=[pltpu.VMEM((full_len, PAIR), f32), pltpu.VMEM((full_len, PAIR), f32)],
        compiler_params=pltpu.CompilerParams(vmem_limit_bytes=40 << 20),
        cost_estimate=pl.CostEstimate(
            flops=pairs * seen * PAIR * 20, transcendentals=pairs * seen * 2, bytes_accessed=full_len * width * 8
        ),
    )(qkv, grad, lse, table, start)


def rotary_table(full_len):
    half = ROT // 2
    freq = jnp.arange(half, dtype=f32)
    inverse = jnp.power(f32(10000.0), -(2.0 * freq) / ROT)
    angles = jnp.arange(full_len, dtype=jnp.int32).astype(f32)[:, None] * inverse[None, :]
    cosine, sine = jnp.cos(angles), jnp.sin(angles)
    rest = jnp.zeros((full_len, HD - ROT), f32)
    none = jnp.zeros_like(sine)
    keep = jnp.concatenate([cosine, cosine, rest + 1.0], axis=1)
    ahead = jnp.concatenate([-sine, none, rest], axis=1)
    behind = jnp.concatenate([none, sine, rest], axis=1)
    return jnp.stack([jnp.concatenate([t, t], axis=1) for t in (keep, ahead, behind)])


def shards(
    dp,
    ctx,
    inputs,
    segments,
    ln1_gain,
    ln1_bias,
    qkv_weight,
    qkv_bias,
    out_weight,
    ln2_gain,
    ln2_bias,
    gate_weight,
    up_weight,
    down_weight,
    cotangent,
):
    local_len, width = inputs.shape[1], inputs.shape[2]
    full_len = segments.shape[1]
    heads = width // HD
    near = heads // ctx
    pairs = near // 2
    me = lax.axis_index("ctx")
    own = me * local_len

    part = ln1_gain.shape[0]
    small = jnp.concatenate([ln1_gain, ln1_bias, ln2_gain, ln2_bias, qkv_bias]).astype(f32)
    count = small.shape[0]
    small = jnp.pad(small, (0, 1024 - count)).reshape(8, 128)
    rows_here = qkv_weight.shape[0]
    blocks = qkv_weight.reshape(rows_here, 3, pairs, 2, ctx, HD).transpose(4, 0, 2, 1, 3, 5)
    blocks = blocks.reshape(ctx, rows_here, near * 3 * HD)
    rows, grad_rows = inputs[0], cotangent[0]
    if ctx == 4 and part == HD:
        small, joined_weight, out_full, rows_wide, grad_wide = opening(
            dp, ctx, small, blocks, out_weight, rows, grad_rows
        )
        gate_weight, up_weight, down_weight, _ = lax.optimization_barrier(
            (gate_weight, up_weight, down_weight, rows_wide)
        )
    else:
        small = lax.all_gather(small[None, :], ("dp", "ctx"), axis=0, tiled=True)
        blocks = exchange_ctx(blocks, ctx)
        joined_weight = lax.all_gather(
            blocks.reshape(ctx * rows_here, near * 3 * HD), "dp", axis=0, tiled=True
        )
        out_full = lax.all_gather(out_weight, ("dp", "ctx"), axis=0, tiled=True)
        out_full = out_full.reshape(near, ctx, HD, width)
        out_full = lax.dynamic_index_in_dim(out_full, me, 1, keepdims=False)
        out_full = out_full.reshape(near * HD, width)
        rows_wide = gather_ctx(rows, ctx)
        grad_wide = gather_ctx(grad_rows, ctx)
    small = small.reshape(dp * ctx, 1024)[:, :count]
    gain_one, shift_one, gain_two, shift_two = [
        small[:, i * part : (i + 1) * part].reshape(width) for i in range(4)
    ]
    bias = small[:, 4 * part :].reshape(3, pairs, 2, ctx, HD)
    bias = lax.dynamic_index_in_dim(bias, me, 3, keepdims=False)
    bias = bias.transpose(1, 0, 2, 3).reshape(1, near * 3 * HD)
    gate_full = lax.all_gather(gate_weight, "dp", axis=0, tiled=True)
    up_full = lax.all_gather(up_weight, "dp", axis=0, tiled=True)
    down_full = lax.all_gather(down_weight, "dp", axis=1, tiled=True)

    segment = segments[0]
    start = jnp.sum((segment[None, :] < segment[:, None]).astype(jnp.int32), axis=1)
    start = jnp.broadcast_to(start[:, None], (full_len, 128))
    table = rotary_table(full_len)
    scaled_wide, _ = norm_stats(rows_wide.astype(f32))
    normed_one = (scaled_wide * gain_one + shift_one).astype(bf16)
    joined = dot(normed_one, joined_weight)
    attended, qkv, lse = attend(joined, bias, table, start)
    resid = rows.astype(f32) + scatter_ctx(dot(attended, out_full), ctx)

    scaled_two, inv_two = norm_stats(resid)
    normed_two = (scaled_two * gain_two + shift_two).astype(bf16)
    normed_wide = gather_ctx(normed_two, ctx)
    gate = dot(normed_wide, gate_full)
    upward = dot(normed_wide, up_full)
    sigma = jax.nn.sigmoid(gate)
    swish = gate * sigma
    inner = (swish * upward).astype(bf16)
    d_inner = dot_nt(grad_wide, down_full)
    d_gate = (d_inner * upward * sigma * (1.0 + gate * (1.0 - sigma))).astype(bf16)
    d_upward = (d_inner * swish).astype(bf16)
    d_down = dot_tn(inner, grad_wide).astype(bf16)
    d_normed_two = scatter_ctx(dot_nt(d_gate, gate_full) + dot_nt(d_upward, up_full), ctx, d_down)
    d_gate_weight = dot_tn(normed_wide, d_gate).astype(bf16)
    d_up_weight = dot_tn(normed_wide, d_upward).astype(bf16)
    d_normed_two, _, _ = lax.optimization_barrier((d_normed_two, d_gate_weight, d_up_weight))
    d_down = lax.psum_scatter(d_down, "dp", scatter_dimension=1, tiled=True).astype(f32)
    d_gate_weight = lax.psum_scatter(d_gate_weight, "dp", scatter_dimension=0, tiled=True).astype(f32)
    d_up_weight = lax.psum_scatter(d_up_weight, "dp", scatter_dimension=0, tiled=True).astype(f32)
    branch = dot(inner, down_full)

    d_resid_norm, d_gain_two, d_shift_two = norm_backward(d_normed_two, scaled_two, inv_two, gain_two)
    d_resid = grad_rows.astype(f32) + d_resid_norm
    d_proj = gather_ctx(d_resid.astype(bf16), ctx)
    branch, _ = lax.optimization_barrier((branch, d_proj))
    output = (resid + scatter_ctx(branch, ctx)).astype(bf16)
    d_attended = dot_nt(d_proj, out_full).astype(bf16)
    d_out_weight = dot_tn(attended, d_proj).astype(bf16)
    if part == HD:
        d_out_weight = lax.psum_scatter(d_out_weight, "dp", scatter_dimension=0, tiled=True)
    else:
        at_me = lax.broadcasted_iota(jnp.int32, (1, ctx, 1, 1), 1) == me
        d_out_weight = jnp.where(at_me, d_out_weight.reshape(near, 1, HD, width), jnp.zeros((), bf16))
        d_out_weight = lax.psum_scatter(
            d_out_weight.reshape(width, width), ("dp", "ctx"), scatter_dimension=0, tiled=True
        )
    d_out_weight = d_out_weight.astype(f32)

    d_joined, d_bias = attend_back(qkv, d_attended, lse, table, start)
    d_normed_one = scatter_ctx(dot_nt(d_joined, joined_weight), ctx)
    d_joined_weight = lax.psum_scatter(
        dot_tn(normed_one, d_joined).astype(bf16), "dp", scatter_dimension=0, tiled=True
    )
    blocks = exchange_ctx(d_joined_weight.reshape(ctx, rows_here, near * 3 * HD), ctx)
    blocks = blocks.reshape(ctx, rows_here, pairs, 3, 2, HD).transpose(1, 3, 2, 4, 0, 5)
    d_joined_weight = blocks.reshape(rows_here, 3 * width).astype(f32)

    scaled_one, inv_one = norm_stats(rows.astype(f32))
    d_rows_norm, d_gain_one, d_shift_one = norm_backward(d_normed_one, scaled_one, inv_one, gain_one)
    grad_input = d_resid + d_rows_norm

    d_bias = d_bias.reshape(pairs, 3, 2, HD).transpose(1, 0, 2, 3)[:, :, :, None, :]
    at_me = (lax.broadcasted_iota(jnp.int32, (1, 1, 1, ctx, 1), 3) == me).astype(f32)
    d_bias = (d_bias * at_me).reshape(dp * ctx, -1)
    small = jnp.concatenate(
        [t.reshape(dp * ctx, part) for t in (d_gain_one, d_shift_one, d_gain_two, d_shift_two)]
        + [d_bias],
        axis=1,
    )
    small = jnp.pad(small, ((0, 0), (0, 1024 - count))).reshape(dp, ctx, 8, 128)
    small = closing(dp, ctx, small.transpose(1, 0, 2, 3)).reshape(1024)[:count]
    d_gain_one, d_shift_one, d_gain_two, d_shift_two = [
        small[i * part : (i + 1) * part] for i in range(4)
    ]
    return (
        output[None],
        grad_input[None],
        d_gain_one,
        d_shift_one,
        d_joined_weight,
        small[4 * part :],
        d_out_weight,
        d_gain_two,
        d_shift_two,
        d_gate_weight,
        d_up_weight,
        d_down,
    )


def solution(mesh):
    every = ("dp", "ctx")
    return jax.shard_map(
        functools.partial(shards, mesh.shape["dp"], mesh.shape["ctx"]),
        mesh=mesh,
        in_specs=(
            P("dp", "ctx", None),
            P("dp", None),
            P(every),
            P(every),
            P(every, None),
            P(every),
            P(every, None),
            P(every),
            P(every),
            P("dp", "ctx"),
            P("dp", "ctx"),
            P("ctx", "dp"),
            P("dp", "ctx", None),
        ),
        out_specs=(
            P("dp", "ctx", None),
            P("dp", "ctx", None),
            P(every),
            P(every),
            P(every, None),
            P(every),
            P(every, None),
            P(every),
            P(every),
            P("dp", "ctx"),
            P("dp", "ctx"),
            P("ctx", "dp"),
        ),
        check_vma=False,
    )
```

```python
import functools
import math

import jax
import jax.numpy as jnp
from jax import lax
from jax.experimental import pallas as pl
from jax.experimental.pallas import tpu as pltpu
from jax.sharding import PartitionSpec as P

HD = 64
ROT = 16
DOC_MAX = 512
PAIR = 2 * HD

norm_eps = 1e-05
masked_value = -1e30
f32 = jnp.float32
bf16 = jnp.bfloat16


def dot(a, b):
    return jnp.dot(a, b, preferred_element_type=f32)


def dot_nt(a, b):
    return lax.dot_general(a, b, (((1,), (1,)), ((), ())), preferred_element_type=f32)


def dot_tn(a, b):
    return lax.dot_general(a, b, (((0,), (0,)), ((), ())), preferred_element_type=f32)


def norm_stats(rows):
    row_mean = jnp.mean(rows, axis=-1, keepdims=True)
    centered = rows - row_mean
    variance = jnp.mean(centered * centered, axis=-1, keepdims=True)
    inv_std = lax.rsqrt(variance + norm_eps)
    return centered * inv_std, inv_std


def norm_backward(grad_normed, scaled, inv_std, gain):
    grad_gain = jnp.sum(grad_normed * scaled, axis=0)
    grad_shift = jnp.sum(grad_normed, axis=0)
    inner_grad = grad_normed * gain
    grad_rows = inv_std * (
        inner_grad
        - jnp.mean(inner_grad, axis=-1, keepdims=True)
        - scaled * jnp.mean(inner_grad * scaled, axis=-1, keepdims=True)
    )
    return grad_rows, grad_gain, grad_shift


def partner(n, k):
    return [(c, c ^ k) for c in range(n)]


def hop(x, n, k):
    return lax.ppermute(x, "ctx", partner(n, k))


def gather_relative(block, n):
    if n != 4:
        return [block] + [hop(block, n, k) for k in range(1, n)]
    half = block.shape[0] // 2
    one = hop(block, n, 1)
    two = hop(block, n, 2)
    low = hop(one[:half], n, 2)
    high = hop(two[half:], n, 1)
    return [block, one, two, jnp.concatenate([low, high], axis=0)]


def gather_ctx(block, n):
    me = lax.axis_index("ctx")
    size = block.shape[0]
    parts = gather_relative(block, n)
    full = jnp.zeros((n * size,) + block.shape[1:], block.dtype)
    for k, part in enumerate(parts):
        full = lax.dynamic_update_slice_in_dim(full, part, (me ^ k) * size, 0)
    return full


def scatter_ctx(partial, n, meanwhile=None):
    me = lax.axis_index("ctx")
    size = partial.shape[0] // n

    def block(k):
        return lax.dynamic_slice_in_dim(partial, (me ^ k) * size, size, 0)

    if n != 4:
        total = block(0).astype(f32)
        for k in range(1, n):
            total = total + hop(block(k).astype(bf16), n, k).astype(f32)
        return total
    half = size // 2
    far = block(3).astype(bf16)
    low = hop(far[:half], n, 1).astype(f32)
    high = hop(far[half:], n, 2).astype(f32)
    if meanwhile is not None:
        partial, _ = lax.optimization_barrier((partial, meanwhile))
    one = block(1).astype(f32)
    two = block(2).astype(f32)
    to_one = jnp.concatenate([one[:half], one[half:] + high], axis=0).astype(bf16)
    to_two = jnp.concatenate([two[:half] + low, two[half:]], axis=0).astype(bf16)
    return block(0).astype(f32) + hop(to_one, n, 1).astype(f32) + hop(to_two, n, 2).astype(f32)


def exchange_ctx(blocks, n):
    me = lax.axis_index("ctx")
    got = lax.dynamic_update_slice_in_dim(
        jnp.zeros_like(blocks), lax.dynamic_slice_in_dim(blocks, me, 1, 0), me, 0
    )
    for k in range(1, n):
        sent = lax.dynamic_slice_in_dim(blocks, me ^ k, 1, 0)
        got = lax.dynamic_update_slice_in_dim(got, hop(sent, n, k), me ^ k, 0)
    return got


MESH = pl.DeviceIdType.MESH
ANY = pl.BlockSpec(memory_space=pl.ANY)


class Place:
    def __init__(self, dp):
        self.row = lax.axis_index("dp")
        self.col = lax.axis_index("ctx")
        self.lines = dp // 2
        self.line = self.row // 2
        self.core = self.row % 2
        self.twin = (self.row + 1 - 2 * self.core, self.col)

    def other(self, k):
        col, bit = self.col, 1
        while bit <= k:
            if k & bit:
                col = col + bit * (1 - 2 * ((self.col // bit) % 2))
            bit *= 2
        return col

    def across(self, k):
        return (self.row, self.other(k))

    def above(self):
        return (self.row + 2, self.col)

    def below(self):
        return (self.row - 2, self.col)


def greet(place, ctx, column=False):
    barrier = pltpu.get_barrier_semaphore()
    for k in range(1, ctx):
        pl.semaphore_signal(barrier, 1, device_id=place.across(k), device_id_type=MESH)
    if not column:
        pl.semaphore_wait(barrier, ctx - 1)
        return
    pl.semaphore_signal(barrier, 1, device_id=place.twin, device_id_type=MESH)

    @pl.when(place.line > 0)
    def _():
        pl.semaphore_signal(barrier, 1, device_id=place.below(), device_id_type=MESH)

    @pl.when(place.line < place.lines - 1)
    def _():
        pl.semaphore_signal(barrier, 1, device_id=place.above(), device_id_type=MESH)

    peers = ctx + (place.line > 0).astype(jnp.int32) + (place.line < place.lines - 1).astype(jnp.int32)
    pl.semaphore_wait(barrier, peers)


def remote(src, dst, send, recv, device):
    return pltpu.make_async_remote_copy(
        src_ref=src, dst_ref=dst, send_sem=send, recv_sem=recv, device_id=device, device_id_type=MESH
    )


class LineGather:
    def __init__(self, place, shard, sems):
        self.place, self.shard, self.sems = place, shard, sems

    def row(self, line):
        return line * 2 + self.place.core

    def up(self, hop):
        part = self.shard(self.row(self.place.line - hop + 1))
        return remote(part, part, self.sems.at[0, hop], self.sems.at[1, hop], self.place.above())

    def down(self, hop):
        part = self.shard(self.row(self.place.line + hop - 1))
        return remote(part, part, self.sems.at[2, hop], self.sems.at[3, hop], self.place.below())

    def over(self, at, row):
        part = self.shard(row)
        return remote(part, part, self.sems.at[4, at], self.sems.at[5, at], self.place.twin)

    def sends_up(self, hop):
        return (self.place.line - hop + 1 >= 0) & (self.place.line < self.place.lines - 1)

    def sends_down(self, hop):
        return (self.place.line + hop - 1 < self.place.lines) & (self.place.line > 0)

    def send(self, hop):
        place = self.place
        pl.when(self.sends_up(hop))(lambda: self.up(hop).start())
        pl.when(self.sends_down(hop))(lambda: self.down(hop).start())
        if hop == 1:
            self.over(0, place.row).start()

    def receive(self, hop):
        place = self.place

        @pl.when(place.line - hop >= 0)
        def _():
            part = self.shard(self.row(place.line - hop))
            remote(part, part, self.sems.at[0, hop], self.sems.at[1, hop], place.twin).wait_recv()
            self.over(hop, self.row(place.line - hop)).start()

        @pl.when(place.line + hop < place.lines)
        def _():
            part = self.shard(self.row(place.line + hop))
            remote(part, part, self.sems.at[2, hop], self.sems.at[3, hop], place.twin).wait_recv()
            self.over(place.lines - 1 + hop, self.row(place.line + hop)).start()

    def finish(self):
        place = self.place
        self.over(0, place.row).wait_send()
        other = 1 - 2 * place.core
        remote(
            self.shard(place.row + other), self.shard(place.row + other),
            self.sems.at[4, 0], self.sems.at[5, 0], place.twin,
        ).wait_recv()
        for hop in range(1, place.lines):
            pl.when(self.sends_up(hop))(lambda: self.up(hop).wait_send())
            pl.when(self.sends_down(hop))(lambda: self.down(hop).wait_send())
            for at, line, there in (
                (hop, place.line - hop, place.line - hop >= 0),
                (place.lines - 1 + hop, place.line + hop, place.line + hop < place.lines),
            ):

                @pl.when(there)
                def _():
                    row = self.row(line)
                    self.over(at, row).wait_send()
                    part = self.shard(row + other)
                    remote(part, part, self.sems.at[4, at], self.sems.at[5, at], place.twin).wait_recv()

    @staticmethod
    def scratch(dp):
        return pltpu.SemaphoreType.DMA((6, dp))


class CtxGather:
    def __init__(self, place, block, full, size, sems):
        self.place, self.block, self.full, self.size, self.sems = place, block, full, size, sems

    def rows(self, col, start=0, size=None):
        size = self.size if size is None else size
        return self.full.at[pl.ds(pl.multiple_of(col * self.size + start, size), size), :]

    def copies(self):
        place, half = self.place, self.size // 2
        me = place.col
        return [
            remote(self.block, self.rows(me), self.sems.at[0, 0], self.sems.at[1, 0], place.across(1)),
            remote(self.block, self.rows(me), self.sems.at[0, 1], self.sems.at[1, 1], place.across(2)),
            remote(
                self.rows(place.other(1), 0, half), self.rows(place.other(1), 0, half),
                self.sems.at[0, 2], self.sems.at[1, 2], place.across(2),
            ),
            remote(
                self.rows(place.other(2), half, half), self.rows(place.other(2), half, half),
                self.sems.at[0, 3], self.sems.at[1, 3], place.across(1),
            ),
        ]

    def arrivals(self):
        place, half = self.place, self.size // 2
        me = place.col
        parts = [self.rows(place.other(1)), self.rows(place.other(2)), self.rows(place.other(3), 0, half), self.rows(place.other(3), half, half)]
        return [
            remote(part, part, self.sems.at[0, i], self.sems.at[1, i], place.across(1))
            for i, part in enumerate(parts)
        ]

    def first(self):
        copies = self.copies()
        copies[0].start()
        copies[1].start()

    def second(self):
        copies, arrivals = self.copies(), self.arrivals()
        arrivals[0].wait_recv()
        copies[2].start()
        arrivals[1].wait_recv()
        copies[3].start()

    def finish(self):
        copies, arrivals = self.copies(), self.arrivals()
        arrivals[2].wait_recv()
        arrivals[3].wait_recv()
        for copy in copies:
            copy.wait_send()

    @staticmethod
    def scratch():
        return pltpu.SemaphoreType.DMA((2, 4))


def opening_kernel(
    dp, ctx,
    small_ref, blocks_ref, out_weight_ref, rows_ref, cot_ref,
    small_all, joined_all, out_all, rows_all, cot_all,
    local_sem, swap_sem, line_small, line_joined, line_out, rows_sem, cot_sem,
):
    place = Place(dp)
    greet(place, ctx, column=True)
    me, row = place.col, place.row
    depth = blocks_ref.shape[1]
    length = rows_ref.shape[0]
    rows_out = out_weight_ref.shape[0]

    def joined_rows(row, col):
        return joined_all.at[pl.ds(pl.multiple_of((row * ctx + col) * depth, depth), depth), :]

    def joined_shard(row):
        return joined_all.at[pl.ds(pl.multiple_of(row * (ctx * depth), ctx * depth), ctx * depth), :]

    def out_shard(row):
        return out_all.at[pl.ds(pl.multiple_of(row * rows_out, rows_out), rows_out), :]

    local = [
        pltpu.make_async_copy(small_ref, small_all.at[row, me], local_sem.at[0]),
        pltpu.make_async_copy(blocks_ref.at[me], joined_rows(row, me), local_sem.at[1]),
        pltpu.make_async_copy(out_weight_ref, out_shard(row), local_sem.at[2]),
        pltpu.make_async_copy(rows_ref, rows_all.at[pl.ds(pl.multiple_of(me * length, length), length), :], local_sem.at[3]),
        pltpu.make_async_copy(cot_ref, cot_all.at[pl.ds(pl.multiple_of(me * length, length), length), :], local_sem.at[4]),
    ]
    swaps, arrivals = [], []
    for k in range(1, ctx):
        swaps.append(remote(small_ref, small_all.at[row, me], swap_sem.at[0, k], swap_sem.at[1, k], place.across(k)))
        swaps.append(
            remote(blocks_ref.at[place.other(k)], joined_rows(row, me), swap_sem.at[2, k], swap_sem.at[3, k], place.across(k))
        )
        arrivals.append(
            remote(small_ref, small_all.at[row, place.other(k)], swap_sem.at[0, k], swap_sem.at[1, k], place.across(k))
        )
        part = joined_rows(row, place.other(k))
        arrivals.append(remote(part, part, swap_sem.at[2, k], swap_sem.at[3, k], place.across(k)))
    for copy in swaps:
        copy.start()
    for copy in local:
        copy.start()
    rows_gather = CtxGather(place, rows_ref, rows_all, length, rows_sem)
    cot_gather = CtxGather(place, cot_ref, cot_all, length, cot_sem)
    lines = [
        LineGather(place, lambda row: small_all.at[row], line_small),
        LineGather(place, joined_shard, line_joined),
        LineGather(place, out_shard, line_out),
    ]
    rows_gather.first()
    for copy in local[:2]:
        copy.wait()
    for copy in arrivals:
        copy.wait_recv()
    lines[0].send(1)
    lines[1].send(1)
    local[2].wait()
    lines[2].send(1)
    rows_gather.second()
    cot_gather.first()
    for hop in range(1, place.lines):
        for line in lines:
            line.receive(hop)
            if hop < place.lines - 1:
                line.send(hop + 1)
        if hop == 1:
            cot_gather.second()
    for line in lines:
        line.finish()
    rows_gather.finish()
    cot_gather.finish()
    for copy in swaps:
        copy.wait_send()
    local[3].wait()
    local[4].wait()


def opening(dp, ctx, small, blocks, out_weight, rows, cot):
    depth, cols = blocks.shape[1:]
    shapes = [
        jax.ShapeDtypeStruct((dp, ctx) + small.shape, small.dtype),
        jax.ShapeDtypeStruct((dp * ctx * depth, cols), bf16),
        jax.ShapeDtypeStruct((dp * out_weight.shape[0], out_weight.shape[1]), bf16),
        jax.ShapeDtypeStruct((ctx * rows.shape[0], rows.shape[1]), bf16),
        jax.ShapeDtypeStruct((ctx * cot.shape[0], cot.shape[1]), bf16),
    ]
    return pl.pallas_call(
        functools.partial(opening_kernel, dp, ctx),
        in_specs=[ANY] * 5,
        out_specs=[ANY] * 5,
        out_shape=shapes,
        scratch_shapes=[
            pltpu.SemaphoreType.DMA((5,)),
            pltpu.SemaphoreType.DMA((4, ctx)),
            LineGather.scratch(dp),
            LineGather.scratch(dp),
            LineGather.scratch(dp),
            CtxGather.scratch(),
            CtxGather.scratch(),
        ],
        compiler_params=pltpu.CompilerParams(collective_id=0, has_side_effects=True),
        cost_estimate=pl.CostEstimate(flops=0, transcendentals=0, bytes_accessed=200 << 20),
    )(small, blocks, out_weight, rows, cot)


CHUNKS = 4


class CtxReduce:
    def __init__(self, place, block, total, sent, got, sems):
        self.place, self.block, self.total = place, block, total
        self.sent, self.got, self.sems = sent, got, sems
        self.size = total.shape[1] // CHUNKS

    def chunk(self, j):
        return pl.ds(j * self.size, self.size)

    def copy(self, kind, j):
        way = kind if kind else 1 + j % 2
        return remote(
            self.sent.at[kind, self.chunk(j)], self.got.at[kind, self.chunk(j)],
            self.sems.at[0, kind, j], self.sems.at[1, kind, j], self.place.across(way),
        )

    def start(self):
        place = self.place
        self.sent[0] = self.block(place.other(3)).astype(bf16)
        for j in range(CHUNKS):
            self.copy(0, j).start()
        for kind in (1, 2):
            self.total[kind - 1] = self.block(place.other(kind))
            for j in range(CHUNKS):
                if kind == 1 + j % 2:
                    self.sent[kind, self.chunk(j)] = self.total[kind - 1, self.chunk(j)].astype(bf16)
                    self.copy(kind, j).start()

    def relay(self):
        for j in range(CHUNKS):
            kind = 2 - j % 2
            self.copy(0, j).wait_recv()
            share = self.total[kind - 1, self.chunk(j)] + self.got[0, self.chunk(j)].astype(f32)
            self.sent[kind, self.chunk(j)] = share.astype(bf16)
            self.copy(kind, j).start()
        self.total[0] = self.block(self.place.col)

    def sum(self, j):
        for kind in (1, 2):
            self.copy(kind, j).wait_recv()
        rows = self.chunk(j)
        return self.total[0, rows] + self.got[1, rows].astype(f32) + self.got[2, rows].astype(f32)

    def finish(self):
        for kind in range(3):
            for j in range(CHUNKS):
                self.copy(kind, j).wait_send()

    @staticmethod
    def scratch(size, width):
        return [
            pltpu.VMEM((2, size, width), f32),
            pltpu.VMEM((3, size, width), bf16),
            pltpu.VMEM((3, size, width), bf16),
            pltpu.SemaphoreType.DMA((2, 3, CHUNKS)),
        ]


class CtxSpread:
    def __init__(self, place, made, full, sems):
        self.place, self.made, self.full, self.sems = place, made, full, sems
        self.size = made.shape[0] // CHUNKS

    def rows(self, col, j):
        at = (col * CHUNKS + j) * self.size
        return self.full.at[pl.ds(pl.multiple_of(at, self.size), self.size), :]

    def copy(self, kind, j):
        place = self.place
        if kind < 2:
            part, there = self.made.at[pl.ds(j * self.size, self.size), :], self.rows(place.col, j)
            way = 1 + kind
        else:
            way = 2 - j % 2
            part = there = self.rows(place.other(3 - way), j)
        return remote(part, there, self.sems.at[0, kind, j], self.sems.at[1, kind, j], place.across(way))

    def arrived(self, kind, j):
        part = self.rows(self.place.other(kind + 1), j)
        remote(
            part, part, self.sems.at[0, kind, j], self.sems.at[1, kind, j], self.place.across(1)
        ).wait_recv()

    def local(self, j):
        part = self.made.at[pl.ds(j * self.size, self.size), :]
        return pltpu.make_async_copy(part, self.rows(self.place.col, j), self.sems.at[0, 3, j])

    def send(self, j):
        self.copy(0, j).start()
        self.copy(1, j).start()
        self.local(j).start()

    def relay(self, j):
        way = 2 - j % 2
        self.arrived(2 - way, j)
        self.copy(2, j).start()

    def finish(self):
        for j in range(CHUNKS):
            way = 2 - j % 2
            self.arrived(way - 1, j)
            self.arrived(2, j)
            self.local(j).wait()
            for kind in range(3):
                self.copy(kind, j).wait_send()

    @staticmethod
    def scratch():
        return pltpu.SemaphoreType.DMA((2, 4, CHUNKS))


def rows_of(ref, col, size):
    return ref[pl.ds(pl.multiple_of(col * size, size), size), :]


def mix_kernel(
    dp, ctx, attended_ref, weight_ref, rows_ref, gain_ref, shift_ref, resid_ref, wide_ref,
    total, sent, got, made, reduce_sem, spread_sem,
):
    place = Place(dp)
    greet(place, ctx)
    size = rows_ref.shape[0]
    reduce = CtxReduce(
        place, lambda col: dot(rows_of(attended_ref, col, size), weight_ref[...]), total, sent, got, reduce_sem
    )
    spread = CtxSpread(place, made, wide_ref, spread_sem)
    reduce.start()
    reduce.relay()
    for j in range(CHUNKS):
        rows = reduce.chunk(j)
        resid = rows_ref[rows, :].astype(f32) + reduce.sum(j)
        resid_ref[rows, :] = resid
        scaled, _ = norm_stats(resid)
        made[rows, :] = (scaled * gain_ref[...] + shift_ref[...]).astype(bf16)
        spread.send(j)
        if j:
            spread.relay(j - 1)
    spread.relay(CHUNKS - 1)
    spread.finish()
    reduce.finish()


def mix(dp, ctx, attended, weight, rows, gain, shift):
    size, width = rows.shape
    vmem = pl.BlockSpec(memory_space=pltpu.VMEM)
    return pl.pallas_call(
        functools.partial(mix_kernel, dp, ctx),
        in_specs=[vmem] * 5,
        out_specs=[vmem, ANY],
        out_shape=[jax.ShapeDtypeStruct((size, width), f32), jax.ShapeDtypeStruct((ctx * size, width), bf16)],
        scratch_shapes=CtxReduce.scratch(size, width)[:3]
        + [
            pltpu.VMEM((size, width), bf16),
            CtxReduce.scratch(size, width)[3],
            CtxSpread.scratch(),
        ],
        compiler_params=pltpu.CompilerParams(
            collective_id=2, has_side_effects=True, vmem_limit_bytes=40 << 20
        ),
        cost_estimate=pl.CostEstimate(
            flops=2 * attended.size * width, transcendentals=0, bytes_accessed=180 << 20
        ),
    )(attended, weight, rows, gain.reshape(1, width), shift.reshape(1, width))


def mix_back_kernel(
    dp, ctx, gate_ref, up_ref, gate_weight_ref, up_weight_ref, resid_ref, cot_ref, gain_ref,
    d_resid_ref, sums_ref, wide_ref,
    total, sent, got, made, reduce_sem, spread_sem,
):
    place = Place(dp)
    greet(place, ctx)
    size = cot_ref.shape[0]

    def block(col):
        return dot_nt(rows_of(gate_ref, col, size), gate_weight_ref[...]) + dot_nt(
            rows_of(up_ref, col, size), up_weight_ref[...]
        )

    reduce = CtxReduce(place, block, total, sent, got, reduce_sem)
    spread = CtxSpread(place, made, wide_ref, spread_sem)
    reduce.start()
    reduce.relay()
    sums_ref[...] = jnp.zeros_like(sums_ref)
    for j in range(CHUNKS):
        rows = reduce.chunk(j)
        scaled, inv_std = norm_stats(resid_ref[rows, :])
        grad, d_gain, d_shift = norm_backward(reduce.sum(j), scaled, inv_std, gain_ref[...])
        sums_ref[0:1, :] += d_gain[None]
        sums_ref[1:2, :] += d_shift[None]
        grad = cot_ref[rows, :].astype(f32) + grad
        d_resid_ref[rows, :] = grad
        made[rows, :] = grad.astype(bf16)
        spread.send(j)
        if j:
            spread.relay(j - 1)
    spread.relay(CHUNKS - 1)
    spread.finish()
    reduce.finish()


def mix_back(dp, ctx, d_gate, d_up, gate_weight, up_weight, resid, cot, gain):
    size, width = cot.shape
    vmem = pl.BlockSpec(memory_space=pltpu.VMEM)
    return pl.pallas_call(
        functools.partial(mix_back_kernel, dp, ctx),
        in_specs=[vmem] * 7,
        out_specs=[vmem, vmem, ANY],
        out_shape=[
            jax.ShapeDtypeStruct((size, width), f32),
            jax.ShapeDtypeStruct((2, width), f32),
            jax.ShapeDtypeStruct((ctx * size, width), bf16),
        ],
        scratch_shapes=CtxReduce.scratch(size, width)[:3]
        + [
            pltpu.VMEM((size, width), bf16),
            CtxReduce.scratch(size, width)[3],
            CtxSpread.scratch(),
        ],
        compiler_params=pltpu.CompilerParams(
            collective_id=3, has_side_effects=True, vmem_limit_bytes=56 << 20
        ),
        cost_estimate=pl.CostEstimate(
            flops=4 * d_gate.size * width, transcendentals=0, bytes_accessed=180 << 20
        ),
    )(d_gate, d_up, gate_weight, up_weight, resid, cot, gain.reshape(1, width))


class LineReduce:
    def __init__(self, place, parts, pair, got, sems):
        self.place, self.parts, self.pair, self.got, self.sems = place, parts, pair, got, sems

    def swap(self, line):
        row = 2 * line + 1 - self.place.core
        return remote(
            self.parts.at[row], self.pair.at[line], self.sems.at[0, line], self.sems.at[1, line], self.place.twin
        )

    def start(self):
        for line in range(self.place.lines):
            self.swap(line).start()

    def add(self):
        for line in range(self.place.lines):
            self.swap(line).wait_recv()
            both = self.parts[2 * line + self.place.core].astype(f32) + self.pair[line].astype(f32)
            self.pair[line] = both.astype(bf16)

    def up(self, far):
        part = self.place.line + far
        return remote(
            self.pair.at[part], self.got.at[part], self.sems.at[2, far], self.sems.at[3, far], self.place.above()
        )

    def down(self, far):
        part = self.place.line - far
        slot = part if far > 1 else self.place.lines
        return remote(
            self.pair.at[part], self.got.at[slot], self.sems.at[4, far], self.sems.at[5, far], self.place.below()
        )

    def came_up(self, far):
        slot = self.got.at[self.place.line + far]
        remote(slot, slot, self.sems.at[2, far + 1], self.sems.at[3, far + 1], self.place.twin).wait_recv()

    def came_down(self, far):
        slot = self.got.at[self.place.line - far if far else self.place.lines]
        remote(slot, slot, self.sems.at[4, far + 1], self.sems.at[5, far + 1], self.place.twin).wait_recv()

    def send(self, far):
        place = self.place

        @pl.when(place.line + far < place.lines)
        def _():
            @pl.when(place.line > 0)
            def _():
                self.came_up(far)
                part = place.line + far
                self.pair[part] = (self.pair[part].astype(f32) + self.got[part].astype(f32)).astype(bf16)

            self.up(far).start()

        @pl.when(place.line - far >= 0)
        def _():
            @pl.when(place.line < place.lines - 1)
            def _():
                self.came_down(far)
                part = place.line - far
                self.pair[part] = (self.pair[part].astype(f32) + self.got[part].astype(f32)).astype(bf16)

            self.down(far).start()

    def collect(self, out):
        place = self.place
        out[...] = self.pair[place.line].astype(f32)

        @pl.when(place.line > 0)
        def _():
            self.came_up(0)
            out[...] += self.got[place.line].astype(f32)

        @pl.when(place.line < place.lines - 1)
        def _():
            self.came_down(0)
            out[...] += self.got[place.lines].astype(f32)

    def finish(self):
        place = self.place
        for line in range(place.lines):
            self.swap(line).wait_send()
        for far in range(1, place.lines):
            pl.when(place.line + far < place.lines)(lambda: self.up(far).wait_send())
            pl.when(place.line - far >= 0)(lambda: self.down(far).wait_send())

    @staticmethod
    def scratch(dp, tile):
        return [
            pltpu.VMEM((dp // 2,) + tile, bf16),
            pltpu.VMEM((dp // 2 + 1,) + tile, bf16),
            pltpu.SemaphoreType.DMA((6, dp // 2)),
        ]


def closing_kernel(
    dp, ctx,
    d_joined_ref, weight_ref, qkv_parts_ref, out_parts_ref, rows_ref, d_resid_ref, gain_ref, sums_two_ref, bias_ref,
    grad_ref, qkv_ref, out_ref, small_ref,
    total, sent, got, reduce_sem, qkv_pair, qkv_got, qkv_sem, out_pair, out_got, out_sem,
    sums, tiles, tiles_got, small_sem, mine, swap_out, swap_in, swap_sem,
):
    place = Place(dp)
    me, row = place.col, place.row
    barrier = pltpu.get_barrier_semaphore()
    for k in range(1, ctx):
        pl.semaphore_signal(barrier, 1, device_id=place.across(k), device_id_type=MESH)
    for k in range(1, dp):
        pl.semaphore_signal(barrier, 1, device_id=((row + k) % dp, me), device_id_type=MESH)
    pl.semaphore_wait(barrier, ctx + dp - 2)

    size, width = rows_ref.shape
    lines = [
        LineReduce(place, qkv_parts_ref, qkv_pair, qkv_got, qkv_sem),
        LineReduce(place, out_parts_ref, out_pair, out_got, out_sem),
    ]
    for line in lines:
        line.start()
    reduce = CtxReduce(
        place, lambda col: dot_nt(rows_of(d_joined_ref, col, size), weight_ref[...]), total, sent, got, reduce_sem
    )
    reduce.start()
    for line in lines:
        line.add()
        line.send(place.lines - 1)
    reduce.relay()
    for far in range(place.lines - 2, 1, -1):
        for line in lines:
            line.send(far)

    sums[...] = jnp.zeros_like(sums)
    for j in range(CHUNKS):
        rows = reduce.chunk(j)
        scaled, inv_std = norm_stats(rows_ref[rows, :].astype(f32))
        grad, d_gain, d_shift = norm_backward(reduce.sum(j), scaled, inv_std, gain_ref[...])
        sums[0:1, :] += d_gain[None]
        sums[1:2, :] += d_shift[None]
        grad_ref[rows, :] = d_resid_ref[rows, :] + grad
    if place.lines > 2:
        for line in lines:
            line.send(1)

    part = width // dp
    tiles[...] = jnp.zeros_like(tiles)
    for i in range(dp):
        lanes = slice(i * part, (i + 1) * part)
        tiles[i, 0:2, :] = sums[:, lanes]
        tiles[i, 2:4, :] = sums_two_ref[:, lanes]
        tiles[i, 4:5, :] = bias_ref[i : i + 1, :]
    sends = [
        remote(tiles.at[(row + k) % dp], tiles_got.at[k], small_sem.at[0, k], small_sem.at[1, k], ((row + k) % dp, me))
        for k in range(1, dp)
    ]
    for copy in sends:
        copy.start()
    tile = tiles[row]
    for k in range(1, dp):
        sends[k - 1].wait()
        tile = tile + tiles_got[k]
    tiles_got[0] = tile
    small_ref[me] = tile
    spreads = [
        remote(tiles_got.at[0], small_ref.at[me], small_sem.at[2, k], small_sem.at[3, k], place.across(k))
        for k in range(1, ctx)
    ]
    for copy in spreads:
        copy.start()

    lines[0].collect(mine)
    depth = mine.shape[0] // ctx
    swap_out[...] = mine[...].astype(bf16)
    swaps = [
        remote(
            swap_out.at[pl.ds(pl.multiple_of(place.other(k) * depth, depth), depth), :], swap_in.at[me],
            swap_sem.at[0, k], swap_sem.at[1, k], place.across(k),
        )
        for k in range(1, ctx)
    ]
    for copy in swaps:
        copy.start()
    swap_in[me] = rows_of(swap_out, me, depth)
    lines[1].collect(out_ref)
    for k in range(1, ctx):
        part = swap_in.at[place.other(k)]
        remote(part, part, swap_sem.at[0, k], swap_sem.at[1, k], place.across(k)).wait_recv()
    low = head_lanes((depth, PAIR))
    for p in range(mine.shape[1] // (3 * PAIR)):
        for t in range(3):
            lanes = slice((3 * p + t) * PAIR, (3 * p + t + 1) * PAIR)
            for c in range(0, ctx, 2):
                a = swap_in[c, :, lanes].astype(f32)
                b = swap_in[c + 1, :, lanes].astype(f32)
                at = t * width + (2 * p * ctx + c) * HD
                qkv_ref[:, at : at + PAIR] = jnp.where(low, a, pltpu.roll(b, HD, 1))
                at = at + ctx * HD
                qkv_ref[:, at : at + PAIR] = jnp.where(low, pltpu.roll(a, HD, 1), b)
    for copy in swaps:
        copy.wait_send()
    for k in range(1, ctx):
        spreads[k - 1].wait_send()
        part = small_ref.at[place.other(k)]
        remote(part, part, small_sem.at[2, k], small_sem.at[3, k], place.across(k)).wait_recv()
    for line in lines:
        line.finish()
    reduce.finish()


def closing(dp, ctx, d_joined, weight, d_qkv, d_out, rows, d_resid, gain, sums_two, bias):
    size, width = rows.shape
    near = weight.shape[1]
    own, tall = width // dp, d_out.shape[0] // dp
    vmem = pl.BlockSpec(memory_space=pltpu.VMEM)
    reduce_scratch = CtxReduce.scratch(size, width)
    max_peers = max(dp, ctx)
    return pl.pallas_call(
        functools.partial(closing_kernel, dp, ctx),
        in_specs=[vmem] * 9,
        out_specs=[vmem] * 4,
        out_shape=[
            jax.ShapeDtypeStruct((size, width), f32),
            jax.ShapeDtypeStruct((own // ctx, 3 * width), f32),
            jax.ShapeDtypeStruct((tall, width), f32),
            jax.ShapeDtypeStruct((ctx, 8, own), f32),
        ],
        scratch_shapes=reduce_scratch
        + LineReduce.scratch(dp, (own, near))
        + LineReduce.scratch(dp, (tall, width))
        + [
            pltpu.VMEM((2, width), f32),
            pltpu.VMEM((dp, 8, own), f32),
            pltpu.VMEM((dp, 8, own), f32),
            pltpu.SemaphoreType.DMA((4, max_peers)),
            pltpu.VMEM((own, near), f32),
            pltpu.VMEM((own, near), bf16),
            pltpu.VMEM((ctx, own // ctx, near), bf16),
            pltpu.SemaphoreType.DMA((2, ctx)),
        ],
        compiler_params=pltpu.CompilerParams(
            collective_id=1, has_side_effects=True, vmem_limit_bytes=60 << 20
        ),
        cost_estimate=pl.CostEstimate(
            flops=2 * d_joined.size * width, transcendentals=0, bytes_accessed=200 << 20
        ),
    )(
        d_joined, weight, d_qkv.reshape(dp, own, near), d_out.reshape(dp, tall, width),
        rows, d_resid, gain.reshape(1, width), sums_two, bias,
    )


def turn(x, table_ref):
    return (
        x * table_ref[0]
        + pltpu.roll(x, PAIR - ROT // 2, 1) * table_ref[1]
        + pltpu.roll(x, ROT // 2, 1) * table_ref[2]
    )


def turn_back(x, table_ref):
    return (
        x * table_ref[0]
        - pltpu.roll(x, PAIR - ROT // 2, 1) * table_ref[1]
        - pltpu.roll(x, ROT // 2, 1) * table_ref[2]
    )


def head_lanes(shape):
    return lax.broadcasted_iota(jnp.int32, shape, 1) < HD


def span(full_len, step, at):
    return max(0, (at - DOC_MAX + 1) // step * step), at + step


def block_mask(start, at, step, low, high):
    keys = lax.broadcasted_iota(jnp.int32, (step, high - low), 1) + low
    rows = lax.broadcasted_iota(jnp.int32, (step, high - low), 0) + at
    return (keys >= start) & (keys <= rows)


def attend_kernel(step, joined_ref, bias_ref, table_ref, start_ref, out_ref, qkv_ref, lse_ref):
    full_len = joined_ref.shape[0]
    scale = 1.0 / math.sqrt(HD)
    for t in range(3):
        lanes = slice(t * PAIR, (t + 1) * PAIR)
        x = joined_ref[:, lanes] + bias_ref[:, lanes]
        if t < 2:
            x = turn(x, table_ref)
        qkv_ref[:, lanes] = x.astype(bf16)
    for at in range(0, full_len, step):
        low, high = span(full_len, step, at)
        allowed = block_mask(start_ref[at : at + step, :1], at, step, low, high)
        q = qkv_ref[at : at + step, :PAIR]
        k = qkv_ref[low:high, PAIR : 2 * PAIR]
        v = qkv_ref[low:high, 2 * PAIR :]
        total = jnp.zeros((step, PAIR), f32)
        logs = []
        for head in range(2):
            mine = head_lanes(q.shape) == (head == 0)
            s = dot_nt(jnp.where(mine, q, jnp.zeros_like(q)), k) * scale
            s = jnp.where(allowed, s, masked_value)
            top = jnp.max(s, axis=1, keepdims=True)
            e = jnp.exp(s - top)
            norm = jnp.sum(e, axis=1, keepdims=True)
            probs = (e * (1.0 / norm)).astype(bf16)
            vm = jnp.where(head_lanes(v.shape) == (head == 0), v, jnp.zeros_like(v))
            total = total + dot(probs, vm)
            logs.append(top + jnp.log(norm))
        out_ref[at : at + step, :] = total.astype(bf16)
        lse_ref[at : at + step, :] = jnp.where(head_lanes((step, PAIR)), logs[0], logs[1])


def attend_back_kernel(
    step, qkv_ref, grad_ref, lse_ref, table_ref, start_ref, out_ref, sum_ref, dk_ref, dv_ref
):
    full_len = qkv_ref.shape[0]
    scale = 1.0 / math.sqrt(HD)
    dk_ref[...] = jnp.zeros_like(dk_ref)
    dv_ref[...] = jnp.zeros_like(dv_ref)
    total = jnp.zeros((1, PAIR), f32)
    for at in range(0, full_len, step):
        low, high = span(full_len, step, at)
        rows = slice(at, at + step)
        keys = slice(low, high)
        allowed = block_mask(start_ref[rows, :1], at, step, low, high)
        q = qkv_ref[rows, :PAIR]
        k = qkv_ref[keys, PAIR : 2 * PAIR]
        v = qkv_ref[keys, 2 * PAIR :]
        g = grad_ref[rows, :]
        dq = jnp.zeros((step, PAIR), f32)
        dk = jnp.zeros((high - low, PAIR), f32)
        dv = jnp.zeros((high - low, PAIR), f32)
        for head in range(2):
            mine = head_lanes(q.shape) == (head == 0)
            qm = jnp.where(mine, q, jnp.zeros_like(q))
            gm = jnp.where(mine, g, jnp.zeros_like(g))
            km = jnp.where(head_lanes(k.shape) == (head == 0), k, jnp.zeros_like(k))
            s = dot_nt(qm, k) * scale
            probs = jnp.where(
                allowed, jnp.exp(s - lse_ref[rows, head * HD : head * HD + 1]), 0.0
            )
            dp = dot_nt(gm, v)
            mean = jnp.sum(dp * probs, axis=1, keepdims=True)
            ds = (probs * (dp - mean)).astype(bf16)
            dq = dq + dot(ds, km)
            dk = dk + dot_tn(ds, qm)
            dv = dv + dot_tn(probs.astype(bf16), gm)
        dk_ref[keys, :] += dk
        dv_ref[keys, :] += dv
        dq = turn_back(dq * scale, table_ref.at[:, rows, :]).astype(bf16)
        out_ref[rows, :PAIR] = dq
        total = total + jnp.sum(dq.astype(f32), axis=0, keepdims=True)
    sum_ref[:, :PAIR] = total
    dk = turn_back(dk_ref[...] * scale, table_ref).astype(bf16)
    out_ref[:, PAIR : 2 * PAIR] = dk
    sum_ref[:, PAIR : 2 * PAIR] = jnp.sum(dk.astype(f32), axis=0, keepdims=True)
    dv = dv_ref[...].astype(bf16)
    out_ref[:, 2 * PAIR :] = dv
    sum_ref[:, 2 * PAIR :] = jnp.sum(dv.astype(f32), axis=0, keepdims=True)


def whole(shape):
    return pl.BlockSpec(shape, lambda p: (0,) * len(shape))


def attend_step(full_len):
    return min(256, full_len)


def attend(joined, bias, table, start):
    full_len, width = joined.shape
    pairs = width // (3 * PAIR)
    step = attend_step(full_len)
    seen = sum(span(full_len, step, at)[1] - span(full_len, step, at)[0] for at in range(0, full_len, step)) * step
    wide = pl.BlockSpec((full_len, 3 * PAIR), lambda p: (0, p))
    thin = pl.BlockSpec((full_len, PAIR), lambda p: (0, p))
    return pl.pallas_call(
        functools.partial(attend_kernel, step),
        grid=(pairs,),
        in_specs=[
            wide,
            pl.BlockSpec((1, 3 * PAIR), lambda p: (0, p)),
            whole(table.shape),
            whole(start.shape),
        ],
        out_specs=[thin, wide, thin],
        out_shape=[
            jax.ShapeDtypeStruct((full_len, pairs * PAIR), bf16),
            jax.ShapeDtypeStruct((full_len, width), bf16),
            jax.ShapeDtypeStruct((full_len, pairs * PAIR), f32),
        ],
        compiler_params=pltpu.CompilerParams(vmem_limit_bytes=40 << 20),
        cost_estimate=pl.CostEstimate(
            flops=pairs * seen * PAIR * 8, transcendentals=pairs * seen * 2, bytes_accessed=full_len * width * 8
        ),
    )(joined, bias, table, start)


def attend_back(qkv, grad, lse, table, start):
    full_len, width = qkv.shape
    pairs = width // (3 * PAIR)
    step = attend_step(full_len)
    seen = sum(span(full_len, step, at)[1] - span(full_len, step, at)[0] for at in range(0, full_len, step)) * step
    wide = pl.BlockSpec((full_len, 3 * PAIR), lambda p: (0, p))
    thin = pl.BlockSpec((full_len, PAIR), lambda p: (0, p))
    return pl.pallas_call(
        functools.partial(attend_back_kernel, step),
        grid=(pairs,),
        in_specs=[wide, thin, thin, whole(table.shape), whole(start.shape)],
        out_specs=[wide, pl.BlockSpec((1, 3 * PAIR), lambda p: (0, p))],
        out_shape=[
            jax.ShapeDtypeStruct((full_len, width), bf16),
            jax.ShapeDtypeStruct((1, width), f32),
        ],
        scratch_shapes=[pltpu.VMEM((full_len, PAIR), f32), pltpu.VMEM((full_len, PAIR), f32)],
        compiler_params=pltpu.CompilerParams(vmem_limit_bytes=40 << 20),
        cost_estimate=pl.CostEstimate(
            flops=pairs * seen * PAIR * 20, transcendentals=pairs * seen * 2, bytes_accessed=full_len * width * 8
        ),
    )(qkv, grad, lse, table, start)


def rotary_table(full_len):
    half = ROT // 2
    freq = jnp.arange(half, dtype=f32)
    inverse = jnp.power(f32(10000.0), -(2.0 * freq) / ROT)
    angles = jnp.arange(full_len, dtype=jnp.int32).astype(f32)[:, None] * inverse[None, :]
    cosine, sine = jnp.cos(angles), jnp.sin(angles)
    rest = jnp.zeros((full_len, HD - ROT), f32)
    none = jnp.zeros_like(sine)
    keep = jnp.concatenate([cosine, cosine, rest + 1.0], axis=1)
    ahead = jnp.concatenate([-sine, none, rest], axis=1)
    behind = jnp.concatenate([none, sine, rest], axis=1)
    return jnp.stack([jnp.concatenate([t, t], axis=1) for t in (keep, ahead, behind)])


def shards(
    dp,
    ctx,
    inputs,
    segments,
    ln1_gain,
    ln1_bias,
    qkv_weight,
    qkv_bias,
    out_weight,
    ln2_gain,
    ln2_bias,
    gate_weight,
    up_weight,
    down_weight,
    cotangent,
):
    local_len, width = inputs.shape[1], inputs.shape[2]
    full_len = segments.shape[1]
    heads = width // HD
    near = heads // ctx
    pairs = near // 2
    me = lax.axis_index("ctx")
    own = me * local_len

    part = ln1_gain.shape[0]
    small = jnp.concatenate([ln1_gain, ln1_bias, ln2_gain, ln2_bias, qkv_bias]).astype(f32)
    count = small.shape[0]
    small = jnp.pad(small, (0, 1024 - count)).reshape(8, 128)
    rows_here = qkv_weight.shape[0]
    blocks = qkv_weight.reshape(rows_here, 3, pairs, 2, ctx, HD).transpose(4, 0, 2, 1, 3, 5)
    blocks = blocks.reshape(ctx, rows_here, near * 3 * HD)
    rows, grad_rows = inputs[0], cotangent[0]
    fused = ctx == 4 and dp % 2 == 0 and part == HD
    if fused:
        small, joined_weight, out_full, rows_wide, grad_wide = opening(
            dp, ctx, small, blocks, out_weight, rows, grad_rows
        )
    else:
        small = lax.all_gather(small[None, :], ("dp", "ctx"), axis=0, tiled=True)
        blocks = exchange_ctx(blocks, ctx)
        joined_weight = lax.all_gather(
            blocks.reshape(ctx * rows_here, near * 3 * HD), "dp", axis=0, tiled=True
        )
        out_full = lax.all_gather(out_weight, ("dp", "ctx"), axis=0, tiled=True)
        out_full = out_full.reshape(near, ctx, HD, width)
        out_full = lax.dynamic_index_in_dim(out_full, me, 1, keepdims=False)
        out_full = out_full.reshape(near * HD, width)
        rows_wide = gather_ctx(rows, ctx)
        grad_wide = gather_ctx(grad_rows, ctx)
    small = small.reshape(dp * ctx, 1024)[:, :count]
    gain_one, shift_one, gain_two, shift_two = [
        small[:, i * part : (i + 1) * part].reshape(width) for i in range(4)
    ]
    bias = small[:, 4 * part :].reshape(3, pairs, 2, ctx, HD)
    bias = lax.dynamic_index_in_dim(bias, me, 3, keepdims=False)
    bias = bias.transpose(1, 0, 2, 3).reshape(1, near * 3 * HD)
    gate_full = lax.all_gather(gate_weight, "dp", axis=0, tiled=True)
    up_full = lax.all_gather(up_weight, "dp", axis=0, tiled=True)
    down_full = lax.all_gather(down_weight, "dp", axis=1, tiled=True)

    segment = segments[0]
    start = jnp.sum((segment[None, :] < segment[:, None]).astype(jnp.int32), axis=1)
    start = jnp.broadcast_to(start[:, None], (full_len, 128))
    table = rotary_table(full_len)
    scaled_wide, _ = norm_stats(rows_wide.astype(f32))
    normed_one = (scaled_wide * gain_one + shift_one).astype(bf16)
    joined = dot(normed_one, joined_weight)
    attended, qkv, lse = attend(joined, bias, table, start)
    if fused:
        resid, normed_wide = mix(dp, ctx, attended, out_full, rows, gain_two, shift_two)
    else:
        resid = rows.astype(f32) + scatter_ctx(dot(attended, out_full), ctx)
        scaled_two, inv_two = norm_stats(resid)
        normed_wide = gather_ctx((scaled_two * gain_two + shift_two).astype(bf16), ctx)

    gate = dot(normed_wide, gate_full)
    upward = dot(normed_wide, up_full)
    sigma = jax.nn.sigmoid(gate)
    swish = gate * sigma
    inner = (swish * upward).astype(bf16)
    d_inner = dot_nt(grad_wide, down_full)
    d_gate = (d_inner * upward * sigma * (1.0 + gate * (1.0 - sigma))).astype(bf16)
    d_upward = (d_inner * swish).astype(bf16)
    d_down = dot_tn(inner, grad_wide).astype(bf16)
    d_down = lax.psum_scatter(d_down, "dp", scatter_dimension=1, tiled=True).astype(f32)
    d_gate_weight = dot_tn(normed_wide, d_gate).astype(bf16)
    d_up_weight = dot_tn(normed_wide, d_upward).astype(bf16)
    branch = dot(inner, down_full)
    if fused:
        d_resid, sums_two, d_proj = mix_back(
            dp, ctx, d_gate, d_upward, gate_full, up_full, resid, grad_rows, gain_two
        )
    else:
        d_normed_two = scatter_ctx(dot_nt(d_gate, gate_full) + dot_nt(d_upward, up_full), ctx)
        grad, d_gain_two, d_shift_two = norm_backward(d_normed_two, scaled_two, inv_two, gain_two)
        d_resid = grad_rows.astype(f32) + grad
        d_proj = gather_ctx(d_resid.astype(bf16), ctx)
    branch, d_gate_weight, d_up_weight, _ = lax.optimization_barrier(
        (branch, d_gate_weight, d_up_weight, d_proj)
    )
    output = (resid + scatter_ctx(branch, ctx)).astype(bf16)
    d_gate_weight = lax.psum_scatter(d_gate_weight, "dp", scatter_dimension=0, tiled=True).astype(f32)
    d_up_weight = lax.psum_scatter(d_up_weight, "dp", scatter_dimension=0, tiled=True).astype(f32)

    d_attended = dot_nt(d_proj, out_full).astype(bf16)
    d_out_weight = dot_tn(attended, d_proj).astype(bf16)
    d_joined, d_bias = attend_back(qkv, d_attended, lse, table, start)
    d_joined_weight = dot_tn(normed_one, d_joined).astype(bf16)
    d_bias = d_bias.reshape(pairs, 3, 2, HD).transpose(1, 0, 2, 3)
    if fused:
        d_bias = jnp.pad(d_bias.reshape(dp, -1), ((0, 0), (0, width // dp - near * 3 * HD // dp)))
        grad_input, d_joined_weight, d_out_weight, small = closing(
            dp, ctx, d_joined, joined_weight, d_joined_weight, d_out_weight, rows, d_resid, gain_one, sums_two, d_bias
        )
        vectors = lax.dynamic_slice_in_dim(jnp.sum(small[:, :4], axis=0), me * part, part, 1)
        d_gain_one, d_shift_one, d_gain_two, d_shift_two = vectors
        d_bias = small[:, 4, : near * 3 * HD // dp].reshape(ctx, -1, HD).transpose(1, 0, 2)
        d_bias = lax.dynamic_index_in_dim(d_bias.reshape(ctx, -1), me, 0, keepdims=False)
    else:
        at_me = lax.broadcasted_iota(jnp.int32, (1, ctx, 1, 1), 1) == me
        d_out_weight = jnp.where(at_me, d_out_weight.reshape(near, 1, HD, width), jnp.zeros((), bf16))
        d_out_weight = lax.psum_scatter(
            d_out_weight.reshape(width, width), ("dp", "ctx"), scatter_dimension=0, tiled=True
        ).astype(f32)
        d_normed_one = scatter_ctx(dot_nt(d_joined, joined_weight), ctx)
        scaled_one, inv_one = norm_stats(rows.astype(f32))
        grad, d_gain_one, d_shift_one = norm_backward(d_normed_one, scaled_one, inv_one, gain_one)
        grad_input = d_resid + grad
        d_joined_weight = lax.psum_scatter(d_joined_weight, "dp", scatter_dimension=0, tiled=True)
        blocks = exchange_ctx(d_joined_weight.reshape(ctx, rows_here, near * 3 * HD), ctx)
        blocks = blocks.reshape(ctx, rows_here, pairs, 3, 2, HD).transpose(1, 3, 2, 4, 0, 5)
        d_joined_weight = blocks.reshape(rows_here, 3 * width).astype(f32)
        at_me = (lax.broadcasted_iota(jnp.int32, (1, 1, 1, ctx, 1), 3) == me).astype(f32)
        d_bias = (d_bias[:, :, :, None, :] * at_me).reshape(dp * ctx, -1)
        small = jnp.concatenate(
            [t.reshape(dp * ctx, part) for t in (d_gain_one, d_shift_one, d_gain_two, d_shift_two)]
            + [d_bias],
            axis=1,
        )
        small = lax.psum_scatter(small, ("dp", "ctx"), scatter_dimension=0, tiled=True)[0]
        d_gain_one, d_shift_one, d_gain_two, d_shift_two = [
            small[i * part : (i + 1) * part] for i in range(4)
        ]
        d_bias = small[4 * part :]
    return (
        output[None],
        grad_input[None],
        d_gain_one,
        d_shift_one,
        d_joined_weight,
        d_bias,
        d_out_weight,
        d_gain_two,
        d_shift_two,
        d_gate_weight,
        d_up_weight,
        d_down,
    )


def solution(mesh):
    every = ("dp", "ctx")
    return jax.shard_map(
        functools.partial(shards, mesh.shape["dp"], mesh.shape["ctx"]),
        mesh=mesh,
        in_specs=(
            P("dp", "ctx", None),
            P("dp", None),
            P(every),
            P(every),
            P(every, None),
            P(every),
            P(every, None),
            P(every),
            P(every),
            P("dp", "ctx"),
            P("dp", "ctx"),
            P("ctx", "dp"),
            P("dp", "ctx", None),
        ),
        out_specs=(
            P("dp", "ctx", None),
            P("dp", "ctx", None),
            P(every),
            P(every),
            P(every, None),
            P(every),
            P(every, None),
            P(every),
            P(every),
            P("dp", "ctx"),
            P("dp", "ctx"),
            P("ctx", "dp"),
        ),
        check_vma=False,
    )
```

```python
import functools
import math

import jax
import jax.numpy as jnp
import numpy as np
from jax import lax
from jax.experimental import pallas as pl
from jax.experimental.pallas import tpu as pltpu
from jax.sharding import PartitionSpec as P

HD = 64
ROT = 16
DOC_MAX = 512
PAIR = 2 * HD

norm_eps = 1e-05
masked_value = -1e30
f32 = jnp.float32
bf16 = jnp.bfloat16


def dot(a, b):
    return jnp.dot(a, b, preferred_element_type=f32)


def dot_nt(a, b):
    return lax.dot_general(a, b, (((1,), (1,)), ((), ())), preferred_element_type=f32)


def dot_tn(a, b):
    return lax.dot_general(a, b, (((0,), (0,)), ((), ())), preferred_element_type=f32)


def norm_stats(rows):
    row_mean = jnp.mean(rows, axis=-1, keepdims=True)
    centered = rows - row_mean
    variance = jnp.mean(centered * centered, axis=-1, keepdims=True)
    inv_std = lax.rsqrt(variance + norm_eps)
    return centered * inv_std, inv_std


def norm_backward(grad_normed, scaled, inv_std, gain):
    grad_gain = jnp.sum(grad_normed * scaled, axis=0)
    grad_shift = jnp.sum(grad_normed, axis=0)
    inner_grad = grad_normed * gain
    grad_rows = inv_std * (
        inner_grad
        - jnp.mean(inner_grad, axis=-1, keepdims=True)
        - scaled * jnp.mean(inner_grad * scaled, axis=-1, keepdims=True)
    )
    return grad_rows, grad_gain, grad_shift


def partner(n, k):
    return [(c, c ^ k) for c in range(n)]


def hop(x, n, k):
    return lax.ppermute(x, "ctx", partner(n, k))


def gather_relative(block, n):
    if n != 4:
        return [block] + [hop(block, n, k) for k in range(1, n)]
    half = block.shape[0] // 2
    one = hop(block, n, 1)
    two = hop(block, n, 2)
    low = hop(one[:half], n, 2)
    high = hop(two[half:], n, 1)
    return [block, one, two, jnp.concatenate([low, high], axis=0)]


def gather_ctx(block, n):
    me = lax.axis_index("ctx")
    size = block.shape[0]
    parts = gather_relative(block, n)
    full = jnp.zeros((n * size,) + block.shape[1:], block.dtype)
    for k, part in enumerate(parts):
        full = lax.dynamic_update_slice_in_dim(full, part, (me ^ k) * size, 0)
    return full


def scatter_ctx(partial, n, meanwhile=None):
    me = lax.axis_index("ctx")
    size = partial.shape[0] // n

    def block(k):
        return lax.dynamic_slice_in_dim(partial, (me ^ k) * size, size, 0)

    if n != 4:
        total = block(0).astype(f32)
        for k in range(1, n):
            total = total + hop(block(k).astype(bf16), n, k).astype(f32)
        return total
    half = size // 2
    far = block(3).astype(bf16)
    low = hop(far[:half], n, 1).astype(f32)
    high = hop(far[half:], n, 2).astype(f32)
    if meanwhile is not None:
        partial, _ = lax.optimization_barrier((partial, meanwhile))
    one = block(1).astype(f32)
    two = block(2).astype(f32)
    to_one = jnp.concatenate([one[:half], one[half:] + high], axis=0).astype(bf16)
    to_two = jnp.concatenate([two[:half] + low, two[half:]], axis=0).astype(bf16)
    return block(0).astype(f32) + hop(to_one, n, 1).astype(f32) + hop(to_two, n, 2).astype(f32)


def exchange_ctx(blocks, n):
    me = lax.axis_index("ctx")
    got = lax.dynamic_update_slice_in_dim(
        jnp.zeros_like(blocks), lax.dynamic_slice_in_dim(blocks, me, 1, 0), me, 0
    )
    for k in range(1, n):
        sent = lax.dynamic_slice_in_dim(blocks, me ^ k, 1, 0)
        got = lax.dynamic_update_slice_in_dim(got, hop(sent, n, k), me ^ k, 0)
    return got


MESH = pl.DeviceIdType.MESH
ANY = pl.BlockSpec(memory_space=pl.ANY)


class Place:
    def __init__(self, dp):
        self.row = lax.axis_index("dp")
        self.col = lax.axis_index("ctx")
        self.lines = dp // 2
        self.line = self.row // 2
        self.core = self.row % 2
        self.twin = (self.row + 1 - 2 * self.core, self.col)

    def other(self, k):
        col, bit = self.col, 1
        while bit <= k:
            if k & bit:
                col = col + bit * (1 - 2 * ((self.col // bit) % 2))
            bit *= 2
        return col

    def across(self, k):
        return (self.row, self.other(k))

    def above(self):
        return (self.row + 2, self.col)

    def below(self):
        return (self.row - 2, self.col)


def greet(place, ctx):
    barrier = pltpu.get_barrier_semaphore()
    for k in range(1, ctx):
        pl.semaphore_signal(barrier, 1, device_id=place.across(k), device_id_type=MESH)
    pl.semaphore_wait(barrier, ctx - 1)


def remote(src, dst, send, recv, device):
    return pltpu.make_async_remote_copy(
        src_ref=src, dst_ref=dst, send_sem=send, recv_sem=recv, device_id=device, device_id_type=MESH
    )


class LineGather:
    def __init__(self, place, shard, sems):
        self.place, self.shard, self.sems = place, shard, sems

    def row(self, line):
        return line * 2 + self.place.core

    def up(self, hop):
        part = self.shard(self.row(self.place.line - hop + 1))
        return remote(part, part, self.sems.at[0, hop], self.sems.at[1, hop], self.place.above())

    def down(self, hop):
        part = self.shard(self.row(self.place.line + hop - 1))
        return remote(part, part, self.sems.at[2, hop], self.sems.at[3, hop], self.place.below())

    def over(self, at, row):
        part = self.shard(row)
        return remote(part, part, self.sems.at[4, at], self.sems.at[5, at], self.place.twin)

    def sends_up(self, hop):
        return (self.place.line - hop + 1 >= 0) & (self.place.line < self.place.lines - 1)

    def sends_down(self, hop):
        return (self.place.line + hop - 1 < self.place.lines) & (self.place.line > 0)

    def send(self, hop):
        place = self.place
        pl.when(self.sends_up(hop))(lambda: self.up(hop).start())
        pl.when(self.sends_down(hop))(lambda: self.down(hop).start())
        if hop == 1:
            self.over(0, place.row).start()

    def receive(self, hop):
        place = self.place

        @pl.when(place.line - hop >= 0)
        def _():
            part = self.shard(self.row(place.line - hop))
            remote(part, part, self.sems.at[0, hop], self.sems.at[1, hop], place.twin).wait_recv()
            self.over(hop, self.row(place.line - hop)).start()

        @pl.when(place.line + hop < place.lines)
        def _():
            part = self.shard(self.row(place.line + hop))
            remote(part, part, self.sems.at[2, hop], self.sems.at[3, hop], place.twin).wait_recv()
            self.over(place.lines - 1 + hop, self.row(place.line + hop)).start()

    def finish(self):
        place = self.place
        self.over(0, place.row).wait_send()
        other = 1 - 2 * place.core
        remote(
            self.shard(place.row + other), self.shard(place.row + other),
            self.sems.at[4, 0], self.sems.at[5, 0], place.twin,
        ).wait_recv()
        for hop in range(1, place.lines):
            pl.when(self.sends_up(hop))(lambda: self.up(hop).wait_send())
            pl.when(self.sends_down(hop))(lambda: self.down(hop).wait_send())
            for at, line, there in (
                (hop, place.line - hop, place.line - hop >= 0),
                (place.lines - 1 + hop, place.line + hop, place.line + hop < place.lines),
            ):

                @pl.when(there)
                def _():
                    row = self.row(line)
                    self.over(at, row).wait_send()
                    part = self.shard(row + other)
                    remote(part, part, self.sems.at[4, at], self.sems.at[5, at], place.twin).wait_recv()

    @staticmethod
    def scratch(dp):
        return pltpu.SemaphoreType.DMA((6, dp))


class CtxGather:
    def __init__(self, place, block, full, size, sems):
        self.place, self.block, self.full, self.size, self.sems = place, block, full, size, sems

    def rows(self, col, start=0, size=None):
        size = self.size if size is None else size
        return self.full.at[pl.ds(pl.multiple_of(col * self.size + start, size), size), :]

    def copies(self):
        place, half = self.place, self.size // 2
        me = place.col
        return [
            remote(self.block, self.rows(me), self.sems.at[0, 0], self.sems.at[1, 0], place.across(1)),
            remote(self.block, self.rows(me), self.sems.at[0, 1], self.sems.at[1, 1], place.across(2)),
            remote(
                self.rows(place.other(1), 0, half), self.rows(place.other(1), 0, half),
                self.sems.at[0, 2], self.sems.at[1, 2], place.across(2),
            ),
            remote(
                self.rows(place.other(2), half, half), self.rows(place.other(2), half, half),
                self.sems.at[0, 3], self.sems.at[1, 3], place.across(1),
            ),
        ]

    def arrivals(self):
        place, half = self.place, self.size // 2
        me = place.col
        parts = [self.rows(place.other(1)), self.rows(place.other(2)), self.rows(place.other(3), 0, half), self.rows(place.other(3), half, half)]
        return [
            remote(part, part, self.sems.at[0, i], self.sems.at[1, i], place.across(1))
            for i, part in enumerate(parts)
        ]

    def first(self):
        copies = self.copies()
        copies[0].start()
        copies[1].start()

    def second(self):
        copies, arrivals = self.copies(), self.arrivals()
        arrivals[0].wait_recv()
        copies[2].start()
        arrivals[1].wait_recv()
        copies[3].start()

    def finish(self):
        copies, arrivals = self.copies(), self.arrivals()
        arrivals[2].wait_recv()
        arrivals[3].wait_recv()
        for copy in copies:
            copy.wait_send()

    @staticmethod
    def scratch():
        return pltpu.SemaphoreType.DMA((2, 4))


def greet_all(place, dp, ctx):
    barrier = pltpu.get_barrier_semaphore()
    for k in range(1, ctx):
        pl.semaphore_signal(barrier, 1, device_id=place.across(k), device_id_type=MESH)
    for k in range(1, dp):
        pl.semaphore_signal(barrier, 1, device_id=((place.row + k) % dp, place.col), device_id_type=MESH)
    pl.semaphore_wait(barrier, ctx + dp - 2)


def opening_kernel(
    dp, ctx,
    small_ref, qkv_ref, out_weight_ref, rows_ref, cot_ref,
    small_all, params_ref, joined_all, out_all, normed_ref, cot_all,
    blocks, rows_all, local_sem, swap_sem, small_sem, line_joined, line_out, rows_sem, cot_sem,
):
    place = Place(dp)
    me, row = place.col, place.row
    depth = qkv_ref.shape[0]
    length, width = rows_ref.shape
    rows_out = out_weight_ref.shape[0]

    low = head_lanes((depth, PAIR))
    for p in range(width // HD // ctx // 2):
        for t in range(3):
            lanes = slice((3 * p + t) * PAIR, (3 * p + t + 1) * PAIR)
            for c in range(0, ctx, 2):
                at = t * width + (2 * p * ctx + c) * HD
                a = qkv_ref[:, at : at + PAIR].astype(f32)
                at = at + ctx * HD
                b = qkv_ref[:, at : at + PAIR].astype(f32)
                blocks[c, :, lanes] = jnp.where(low, a, pltpu.roll(b, HD, 1)).astype(bf16)
                blocks[c + 1, :, lanes] = jnp.where(low, pltpu.roll(a, HD, 1), b).astype(bf16)
    greet_all(place, dp, ctx)

    def joined_rows(row, col):
        return joined_all.at[pl.ds(pl.multiple_of((row * ctx + col) * depth, depth), depth), :]

    def joined_shard(row):
        return joined_all.at[pl.ds(pl.multiple_of(row * (ctx * depth), ctx * depth), ctx * depth), :]

    def out_shard(row):
        return out_all.at[pl.ds(pl.multiple_of(row * rows_out, rows_out), rows_out), :]

    def block(ref, col):
        return ref.at[pl.ds(pl.multiple_of(col * length, length), length), :]

    local = [
        pltpu.make_async_copy(blocks.at[me], joined_rows(row, me), local_sem.at[0]),
        pltpu.make_async_copy(out_weight_ref, out_shard(row), local_sem.at[1]),
        pltpu.make_async_copy(rows_ref, block(rows_all, me), local_sem.at[2]),
        pltpu.make_async_copy(cot_ref, block(cot_all, me), local_sem.at[3]),
    ]
    swaps = [
        remote(small_ref, small_all.at[row, me], swap_sem.at[0, k], swap_sem.at[1, k], place.across(k))
        for k in range(1, ctx)
    ] + [
        remote(
            blocks.at[place.other(k)], joined_rows(row, me), swap_sem.at[2, k], swap_sem.at[3, k], place.across(k)
        )
        for k in range(1, ctx)
    ]
    for copy in swaps:
        copy.start()
    for copy in local:
        copy.start()
    small_all[row, me] = small_ref[...]
    rows_gather = CtxGather(place, rows_ref, rows_all, length, rows_sem)
    cot_gather = CtxGather(place, cot_ref, cot_all, length, cot_sem)
    rows_gather.first()
    for k in range(1, ctx):
        remote(
            small_ref, small_all.at[row, place.other(k)], swap_sem.at[0, k], swap_sem.at[1, k], place.across(k)
        ).wait_recv()
    small_sends = [
        remote(
            small_all.at[row], small_all.at[row], small_sem.at[0, k], small_sem.at[1, k], ((row + k) % dp, me)
        )
        for k in range(1, dp)
    ]
    for copy in small_sends:
        copy.start()
    local[0].wait()
    for k in range(1, ctx):
        part = joined_rows(row, place.other(k))
        remote(part, part, swap_sem.at[2, k], swap_sem.at[3, k], place.across(k)).wait_recv()
    lines = [LineGather(place, joined_shard, line_joined), LineGather(place, out_shard, line_out)]
    lines[0].send(1)
    local[1].wait()
    lines[1].send(1)

    for k in range(1, dp):
        part = small_all.at[(row + dp - k) % dp]
        remote(part, part, small_sem.at[0, k], small_sem.at[1, k], place.twin).wait_recv()
    low = head_lanes((1, PAIR))
    for i in range(dp * ctx // 2):
        lanes = slice(i * PAIR, (i + 1) * PAIR)
        a = small_all.at[2 * i // ctx, 2 * i % ctx]
        b = small_all.at[(2 * i + 1) // ctx, (2 * i + 1) % ctx]
        for r in range(2):
            ar, br = a[r : r + 1, :], b[r : r + 1, :]
            params_ref[2 * r : 2 * r + 1, lanes] = jnp.where(low, ar, pltpu.roll(br, HD, 1))
            params_ref[2 * r + 1 : 2 * r + 2, lanes] = jnp.where(low, pltpu.roll(ar, HD, 1), br)

    def normalize(col):
        step = 64

        @pl.loop(0, length // step)
        def _(i):
            rows = pl.ds(pl.multiple_of(col * length + i * step, step), step)
            scaled, _ = norm_stats(rows_all[rows, :].astype(f32))
            normed_ref[rows, :] = (scaled * params_ref[0:1, :] + params_ref[1:2, :]).astype(bf16)

    rows_gather.second()
    cot_gather.first()
    for hop in range(1, place.lines):
        for line in lines:
            line.receive(hop)
            if hop < place.lines - 1:
                line.send(hop + 1)
        if hop == 1:
            cot_gather.second()
            local[2].wait()
            for col in (me, place.other(1), place.other(2)):
                normalize(col)
    rows_gather.finish()
    normalize(place.other(3))
    for line in lines:
        line.finish()
    cot_gather.finish()
    for copy in swaps + small_sends:
        copy.wait_send()
    local[3].wait()


def opening(dp, ctx, small, qkv_weight, out_weight, rows, cot):
    depth, width = qkv_weight.shape[0], rows.shape[1]
    length = rows.shape[0]
    near = 3 * width // ctx
    vmem = pl.BlockSpec(memory_space=pltpu.VMEM)
    return pl.pallas_call(
        functools.partial(opening_kernel, dp, ctx),
        in_specs=[vmem, vmem, ANY, ANY, ANY],
        out_specs=[vmem, vmem, ANY, ANY, vmem, ANY],
        out_shape=[
            jax.ShapeDtypeStruct((dp, ctx) + small.shape, f32),
            jax.ShapeDtypeStruct((4, width), f32),
            jax.ShapeDtypeStruct((dp * ctx * depth, near), bf16),
            jax.ShapeDtypeStruct((dp * out_weight.shape[0], width), bf16),
            jax.ShapeDtypeStruct((ctx * length, width), bf16),
            jax.ShapeDtypeStruct((ctx * length, width), bf16),
        ],
        scratch_shapes=[
            pltpu.VMEM((ctx, depth, near), bf16),
            pltpu.VMEM((ctx * length, width), bf16),
            pltpu.SemaphoreType.DMA((4,)),
            pltpu.SemaphoreType.DMA((4, ctx)),
            pltpu.SemaphoreType.DMA((2, dp)),
            LineGather.scratch(dp),
            LineGather.scratch(dp),
            CtxGather.scratch(),
            CtxGather.scratch(),
        ],
        compiler_params=pltpu.CompilerParams(
            collective_id=0, has_side_effects=True, vmem_limit_bytes=32 << 20
        ),
        cost_estimate=pl.CostEstimate(flops=0, transcendentals=0, bytes_accessed=200 << 20),
    )(small, qkv_weight, out_weight, rows, cot)


CHUNKS = 4


class CtxReduce:
    def __init__(self, place, block, total, sent, got, sems):
        self.place, self.block, self.total = place, block, total
        self.sent, self.got, self.sems = sent, got, sems
        self.size = total.shape[1] // CHUNKS

    def chunk(self, j):
        return pl.ds(j * self.size, self.size)

    def copy(self, kind, j):
        way = kind if kind else 1 + j % 2
        return remote(
            self.sent.at[kind, self.chunk(j)], self.got.at[kind, self.chunk(j)],
            self.sems.at[0, kind, j], self.sems.at[1, kind, j], self.place.across(way),
        )

    def start(self):
        place = self.place
        self.sent[0] = self.block(place.other(3)).astype(bf16)
        for j in range(CHUNKS):
            self.copy(0, j).start()
        for kind in (1, 2):
            self.total[kind - 1] = self.block(place.other(kind))
            for j in range(CHUNKS):
                if kind == 1 + j % 2:
                    self.sent[kind, self.chunk(j)] = self.total[kind - 1, self.chunk(j)].astype(bf16)
                    self.copy(kind, j).start()

    def relay(self):
        for j in range(CHUNKS):
            kind = 2 - j % 2
            self.copy(0, j).wait_recv()
            share = self.total[kind - 1, self.chunk(j)] + self.got[0, self.chunk(j)].astype(f32)
            self.sent[kind, self.chunk(j)] = share.astype(bf16)
            self.copy(kind, j).start()
        self.total[0] = self.block(self.place.col)

    def sum(self, j):
        for kind in (1, 2):
            self.copy(kind, j).wait_recv()
        rows = self.chunk(j)
        return self.total[0, rows] + self.got[1, rows].astype(f32) + self.got[2, rows].astype(f32)

    def finish(self):
        for kind in range(3):
            for j in range(CHUNKS):
                self.copy(kind, j).wait_send()

    @staticmethod
    def scratch(size, width):
        return [
            pltpu.VMEM((2, size, width), f32),
            pltpu.VMEM((3, size, width), bf16),
            pltpu.VMEM((3, size, width), bf16),
            pltpu.SemaphoreType.DMA((2, 3, CHUNKS)),
        ]


class CtxSpread:
    def __init__(self, place, made, full, sems):
        self.place, self.made, self.full, self.sems = place, made, full, sems
        self.size = made.shape[0] // CHUNKS

    def rows(self, col, j):
        at = (col * CHUNKS + j) * self.size
        return self.full.at[pl.ds(pl.multiple_of(at, self.size), self.size), :]

    def copy(self, kind, j):
        place = self.place
        if kind < 2:
            part, there = self.made.at[pl.ds(j * self.size, self.size), :], self.rows(place.col, j)
            way = 1 + kind
        else:
            way = 2 - j % 2
            part = there = self.rows(place.other(3 - way), j)
        return remote(part, there, self.sems.at[0, kind, j], self.sems.at[1, kind, j], place.across(way))

    def arrived(self, kind, j):
        part = self.rows(self.place.other(kind + 1), j)
        remote(
            part, part, self.sems.at[0, kind, j], self.sems.at[1, kind, j], self.place.across(1)
        ).wait_recv()

    def local(self, j):
        part = self.made.at[pl.ds(j * self.size, self.size), :]
        return pltpu.make_async_copy(part, self.rows(self.place.col, j), self.sems.at[0, 3, j])

    def send(self, j):
        self.copy(0, j).start()
        self.copy(1, j).start()
        self.local(j).start()

    def relay(self, j):
        way = 2 - j % 2
        self.arrived(2 - way, j)
        self.copy(2, j).start()

    def finish(self):
        for j in range(CHUNKS):
            way = 2 - j % 2
            self.arrived(way - 1, j)
            self.arrived(2, j)
            self.local(j).wait()
            for kind in range(3):
                self.copy(kind, j).wait_send()

    @staticmethod
    def scratch():
        return pltpu.SemaphoreType.DMA((2, 4, CHUNKS))


def rows_of(ref, col, size):
    return ref[pl.ds(pl.multiple_of(col * size, size), size), :]


def mix_kernel(
    dp, ctx, attended_ref, weight_ref, rows_ref, gain_ref, shift_ref, resid_ref, wide_ref,
    total, sent, got, made, reduce_sem, spread_sem,
):
    place = Place(dp)
    greet(place, ctx)
    size = rows_ref.shape[0]
    reduce = CtxReduce(
        place, lambda col: dot(rows_of(attended_ref, col, size), weight_ref[...]), total, sent, got, reduce_sem
    )
    spread = CtxSpread(place, made, wide_ref, spread_sem)
    reduce.start()
    reduce.relay()
    for j in range(CHUNKS):
        rows = reduce.chunk(j)
        resid = rows_ref[rows, :].astype(f32) + reduce.sum(j)
        resid_ref[rows, :] = resid
        scaled, _ = norm_stats(resid)
        made[rows, :] = (scaled * gain_ref[...] + shift_ref[...]).astype(bf16)
        spread.send(j)
        if j:
            spread.relay(j - 1)
    spread.relay(CHUNKS - 1)
    spread.finish()
    reduce.finish()


def mix(dp, ctx, attended, weight, rows, gain, shift):
    size, width = rows.shape
    vmem = pl.BlockSpec(memory_space=pltpu.VMEM)
    return pl.pallas_call(
        functools.partial(mix_kernel, dp, ctx),
        in_specs=[vmem] * 5,
        out_specs=[vmem, ANY],
        out_shape=[jax.ShapeDtypeStruct((size, width), f32), jax.ShapeDtypeStruct((ctx * size, width), bf16)],
        scratch_shapes=CtxReduce.scratch(size, width)[:3]
        + [
            pltpu.VMEM((size, width), bf16),
            CtxReduce.scratch(size, width)[3],
            CtxSpread.scratch(),
        ],
        compiler_params=pltpu.CompilerParams(
            collective_id=2, has_side_effects=True, vmem_limit_bytes=40 << 20
        ),
        cost_estimate=pl.CostEstimate(
            flops=2 * attended.size * width, transcendentals=0, bytes_accessed=180 << 20
        ),
    )(attended, weight, rows, gain.reshape(1, width), shift.reshape(1, width))


def mix_back_kernel(
    dp, ctx, gate_ref, up_ref, gate_weight_ref, up_weight_ref, resid_ref, cot_ref, gain_ref,
    d_resid_ref, sums_ref, wide_ref,
    total, sent, got, made, reduce_sem, spread_sem,
):
    place = Place(dp)
    greet(place, ctx)
    size = cot_ref.shape[0]

    def block(col):
        return dot_nt(rows_of(gate_ref, col, size), gate_weight_ref[...]) + dot_nt(
            rows_of(up_ref, col, size), up_weight_ref[...]
        )

    reduce = CtxReduce(place, block, total, sent, got, reduce_sem)
    spread = CtxSpread(place, made, wide_ref, spread_sem)
    reduce.start()
    reduce.relay()
    sums_ref[...] = jnp.zeros_like(sums_ref)
    for j in range(CHUNKS):
        rows = reduce.chunk(j)
        scaled, inv_std = norm_stats(resid_ref[rows, :])
        grad, d_gain, d_shift = norm_backward(reduce.sum(j), scaled, inv_std, gain_ref[...])
        sums_ref[0:1, :] += d_gain[None]
        sums_ref[1:2, :] += d_shift[None]
        grad = cot_ref[rows, :].astype(f32) + grad
        d_resid_ref[rows, :] = grad
        made[rows, :] = grad.astype(bf16)
        spread.send(j)
        if j:
            spread.relay(j - 1)
    spread.relay(CHUNKS - 1)
    spread.finish()
    reduce.finish()


def mix_back(dp, ctx, d_gate, d_up, gate_weight, up_weight, resid, cot, gain):
    size, width = cot.shape
    vmem = pl.BlockSpec(memory_space=pltpu.VMEM)
    return pl.pallas_call(
        functools.partial(mix_back_kernel, dp, ctx),
        in_specs=[vmem] * 7,
        out_specs=[vmem, vmem, ANY],
        out_shape=[
            jax.ShapeDtypeStruct((size, width), f32),
            jax.ShapeDtypeStruct((2, width), f32),
            jax.ShapeDtypeStruct((ctx * size, width), bf16),
        ],
        scratch_shapes=CtxReduce.scratch(size, width)[:3]
        + [
            pltpu.VMEM((size, width), bf16),
            CtxReduce.scratch(size, width)[3],
            CtxSpread.scratch(),
        ],
        compiler_params=pltpu.CompilerParams(
            collective_id=3, has_side_effects=True, vmem_limit_bytes=56 << 20
        ),
        cost_estimate=pl.CostEstimate(
            flops=4 * d_gate.size * width, transcendentals=0, bytes_accessed=180 << 20
        ),
    )(d_gate, d_up, gate_weight, up_weight, resid, cot, gain.reshape(1, width))


class LineReduce:
    def __init__(self, place, parts, pair, got, sems):
        self.place, self.parts, self.pair, self.got, self.sems = place, parts, pair, got, sems

    def swap(self, line):
        row = 2 * line + 1 - self.place.core
        return remote(
            self.parts.at[row], self.pair.at[line], self.sems.at[0, line], self.sems.at[1, line], self.place.twin
        )

    def start(self):
        for line in range(self.place.lines):
            self.swap(line).start()

    def add(self):
        for line in range(self.place.lines):
            self.swap(line).wait_recv()
            both = self.parts[2 * line + self.place.core].astype(f32) + self.pair[line].astype(f32)
            self.pair[line] = both.astype(bf16)

    def up(self, far):
        part = self.place.line + far
        return remote(
            self.pair.at[part], self.got.at[part], self.sems.at[2, far], self.sems.at[3, far], self.place.above()
        )

    def down(self, far):
        part = self.place.line - far
        slot = part if far > 1 else self.place.lines
        return remote(
            self.pair.at[part], self.got.at[slot], self.sems.at[4, far], self.sems.at[5, far], self.place.below()
        )

    def came_up(self, far):
        slot = self.got.at[self.place.line + far]
        remote(slot, slot, self.sems.at[2, far + 1], self.sems.at[3, far + 1], self.place.twin).wait_recv()

    def came_down(self, far):
        slot = self.got.at[self.place.line - far if far else self.place.lines]
        remote(slot, slot, self.sems.at[4, far + 1], self.sems.at[5, far + 1], self.place.twin).wait_recv()

    def send(self, far):
        place = self.place

        @pl.when(place.line + far < place.lines)
        def _():
            @pl.when(place.line > 0)
            def _():
                self.came_up(far)
                part = place.line + far
                self.pair[part] = (self.pair[part].astype(f32) + self.got[part].astype(f32)).astype(bf16)

            self.up(far).start()

        @pl.when(place.line - far >= 0)
        def _():
            @pl.when(place.line < place.lines - 1)
            def _():
                self.came_down(far)
                part = place.line - far
                self.pair[part] = (self.pair[part].astype(f32) + self.got[part].astype(f32)).astype(bf16)

            self.down(far).start()

    def collect(self, out):
        place = self.place
        out[...] = self.pair[place.line].astype(f32)

        @pl.when(place.line > 0)
        def _():
            self.came_up(0)
            out[...] += self.got[place.line].astype(f32)

        @pl.when(place.line < place.lines - 1)
        def _():
            self.came_down(0)
            out[...] += self.got[place.lines].astype(f32)

    def finish(self):
        place = self.place
        for line in range(place.lines):
            self.swap(line).wait_send()
        for far in range(1, place.lines):
            pl.when(place.line + far < place.lines)(lambda: self.up(far).wait_send())
            pl.when(place.line - far >= 0)(lambda: self.down(far).wait_send())

    @staticmethod
    def scratch(dp, tile):
        return [
            pltpu.VMEM((dp // 2,) + tile, bf16),
            pltpu.VMEM((dp // 2 + 1,) + tile, bf16),
            pltpu.SemaphoreType.DMA((6, dp // 2)),
        ]


def closing_kernel(
    dp, ctx,
    d_joined_ref, weight_ref, qkv_parts_ref, out_parts_ref, rows_ref, d_resid_ref, gain_ref, sums_two_ref, bias_ref,
    grad_ref, qkv_ref, out_ref, small_ref,
    total, sent, got, reduce_sem, qkv_pair, qkv_got, qkv_sem, out_pair, out_got, out_sem,
    sums, tiles, tiles_got, small_sem, mine, swap_out, swap_in, swap_sem,
):
    place = Place(dp)
    me, row = place.col, place.row
    greet_all(place, dp, ctx)
    size, width = rows_ref.shape
    lines = [
        LineReduce(place, qkv_parts_ref, qkv_pair, qkv_got, qkv_sem),
        LineReduce(place, out_parts_ref, out_pair, out_got, out_sem),
    ]
    for line in lines:
        line.start()
    reduce = CtxReduce(
        place, lambda col: dot_nt(rows_of(d_joined_ref, col, size), weight_ref[...]), total, sent, got, reduce_sem
    )
    reduce.start()
    for line in lines:
        line.add()
        line.send(place.lines - 1)
    reduce.relay()
    for far in range(place.lines - 2, 1, -1):
        for line in lines:
            line.send(far)

    sums[...] = jnp.zeros_like(sums)
    for j in range(CHUNKS):
        rows = reduce.chunk(j)
        scaled, inv_std = norm_stats(rows_ref[rows, :].astype(f32))
        grad, d_gain, d_shift = norm_backward(reduce.sum(j), scaled, inv_std, gain_ref[...])
        sums[0:1, :] += d_gain[None]
        sums[1:2, :] += d_shift[None]
        grad_ref[rows, :] = d_resid_ref[rows, :] + grad
    if place.lines > 2:
        for line in lines:
            line.send(1)

    part = width // dp
    tiles[...] = jnp.zeros_like(tiles)
    for i in range(dp):
        lanes = slice(i * part, (i + 1) * part)
        tiles[i, 0:2, :] = sums[:, lanes]
        tiles[i, 2:4, :] = sums_two_ref[:, lanes]
        tiles[i, 4:5, :] = bias_ref[i : i + 1, :]
    sends = [
        remote(tiles.at[(row + k) % dp], tiles_got.at[k], small_sem.at[0, k], small_sem.at[1, k], ((row + k) % dp, me))
        for k in range(1, dp)
    ]
    for copy in sends:
        copy.start()
    tile = tiles[row]
    for k in range(1, dp):
        sends[k - 1].wait()
        tile = tile + tiles_got[k]
    tiles_got[0] = tile
    small_ref[me] = tile
    spreads = [
        remote(tiles_got.at[0], small_ref.at[me], small_sem.at[2, k], small_sem.at[3, k], place.across(k))
        for k in range(1, ctx)
    ]
    for copy in spreads:
        copy.start()

    lines[0].collect(mine)
    depth = mine.shape[0] // ctx
    swap_out[...] = mine[...].astype(bf16)
    swaps = [
        remote(
            swap_out.at[pl.ds(pl.multiple_of(place.other(k) * depth, depth), depth), :], swap_in.at[me],
            swap_sem.at[0, k], swap_sem.at[1, k], place.across(k),
        )
        for k in range(1, ctx)
    ]
    for copy in swaps:
        copy.start()
    swap_in[me] = rows_of(swap_out, me, depth)
    lines[1].collect(out_ref)
    for k in range(1, ctx):
        part = swap_in.at[place.other(k)]
        remote(part, part, swap_sem.at[0, k], swap_sem.at[1, k], place.across(k)).wait_recv()
    low = head_lanes((depth, PAIR))
    for p in range(mine.shape[1] // (3 * PAIR)):
        for t in range(3):
            lanes = slice((3 * p + t) * PAIR, (3 * p + t + 1) * PAIR)
            for c in range(0, ctx, 2):
                a = swap_in[c, :, lanes].astype(f32)
                b = swap_in[c + 1, :, lanes].astype(f32)
                at = t * width + (2 * p * ctx + c) * HD
                qkv_ref[:, at : at + PAIR] = jnp.where(low, a, pltpu.roll(b, HD, 1))
                at = at + ctx * HD
                qkv_ref[:, at : at + PAIR] = jnp.where(low, pltpu.roll(a, HD, 1), b)
    for copy in swaps:
        copy.wait_send()
    for k in range(1, ctx):
        spreads[k - 1].wait_send()
        part = small_ref.at[place.other(k)]
        remote(part, part, small_sem.at[2, k], small_sem.at[3, k], place.across(k)).wait_recv()
    for line in lines:
        line.finish()
    reduce.finish()


def closing(dp, ctx, d_joined, weight, d_qkv, d_out, rows, d_resid, gain, sums_two, bias):
    size, width = rows.shape
    near = weight.shape[1]
    own, tall = width // dp, d_out.shape[0] // dp
    vmem = pl.BlockSpec(memory_space=pltpu.VMEM)
    reduce_scratch = CtxReduce.scratch(size, width)
    max_peers = max(dp, ctx)
    return pl.pallas_call(
        functools.partial(closing_kernel, dp, ctx),
        in_specs=[vmem] * 9,
        out_specs=[vmem] * 4,
        out_shape=[
            jax.ShapeDtypeStruct((size, width), f32),
            jax.ShapeDtypeStruct((own // ctx, 3 * width), f32),
            jax.ShapeDtypeStruct((tall, width), f32),
            jax.ShapeDtypeStruct((ctx, 8, own), f32),
        ],
        scratch_shapes=reduce_scratch
        + LineReduce.scratch(dp, (own, near))
        + LineReduce.scratch(dp, (tall, width))
        + [
            pltpu.VMEM((2, width), f32),
            pltpu.VMEM((dp, 8, own), f32),
            pltpu.VMEM((dp, 8, own), f32),
            pltpu.SemaphoreType.DMA((4, max_peers)),
            pltpu.VMEM((own, near), f32),
            pltpu.VMEM((own, near), bf16),
            pltpu.VMEM((ctx, own // ctx, near), bf16),
            pltpu.SemaphoreType.DMA((2, ctx)),
        ],
        compiler_params=pltpu.CompilerParams(
            collective_id=1, has_side_effects=True, vmem_limit_bytes=60 << 20
        ),
        cost_estimate=pl.CostEstimate(
            flops=2 * d_joined.size * width, transcendentals=0, bytes_accessed=200 << 20
        ),
    )(
        d_joined, weight, d_qkv.reshape(dp, own, near), d_out.reshape(dp, tall, width),
        rows, d_resid, gain.reshape(1, width), sums_two, bias,
    )


def turn(x, table_ref):
    return (
        x * table_ref[0]
        + pltpu.roll(x, PAIR - ROT // 2, 1) * table_ref[1]
        + pltpu.roll(x, ROT // 2, 1) * table_ref[2]
    )


def turn_back(x, table_ref):
    return (
        x * table_ref[0]
        - pltpu.roll(x, PAIR - ROT // 2, 1) * table_ref[1]
        - pltpu.roll(x, ROT // 2, 1) * table_ref[2]
    )


def head_lanes(shape):
    return lax.broadcasted_iota(jnp.int32, shape, 1) < HD


def span(full_len, step, at):
    return max(0, (at - DOC_MAX + 1) // step * step), at + step


def block_mask(start, at, step, low, high):
    keys = lax.broadcasted_iota(jnp.int32, (step, high - low), 1) + low
    rows = lax.broadcasted_iota(jnp.int32, (step, high - low), 0) + at
    return (keys >= start) & (keys <= rows)


def attend_kernel(step, joined_ref, bias_ref, table_ref, start_ref, out_ref, qkv_ref, lse_ref):
    full_len = joined_ref.shape[0]
    scale = 1.0 / math.sqrt(HD)
    for t in range(3):
        lanes = slice(t * PAIR, (t + 1) * PAIR)
        x = joined_ref[:, lanes] + bias_ref[:, lanes]
        if t < 2:
            x = turn(x, table_ref)
        qkv_ref[:, lanes] = x.astype(bf16)
    for at in range(0, full_len, step):
        low, high = span(full_len, step, at)
        allowed = block_mask(start_ref[at : at + step, :1], at, step, low, high)
        q = qkv_ref[at : at + step, :PAIR]
        k = qkv_ref[low:high, PAIR : 2 * PAIR]
        v = qkv_ref[low:high, 2 * PAIR :]
        total = jnp.zeros((step, PAIR), f32)
        logs = []
        for head in range(2):
            mine = head_lanes(q.shape) == (head == 0)
            s = dot_nt(jnp.where(mine, q, jnp.zeros_like(q)), k) * scale
            s = jnp.where(allowed, s, masked_value)
            top = jnp.max(s, axis=1, keepdims=True)
            e = jnp.exp(s - top)
            norm = jnp.sum(e, axis=1, keepdims=True)
            probs = (e * (1.0 / norm)).astype(bf16)
            vm = jnp.where(head_lanes(v.shape) == (head == 0), v, jnp.zeros_like(v))
            total = total + dot(probs, vm)
            logs.append(top + jnp.log(norm))
        out_ref[at : at + step, :] = total.astype(bf16)
        lse_ref[at : at + step, :] = jnp.where(head_lanes((step, PAIR)), logs[0], logs[1])


def attend_back_kernel(
    step, qkv_ref, grad_ref, lse_ref, table_ref, start_ref, out_ref, sum_ref, dk_ref, dv_ref
):
    full_len = qkv_ref.shape[0]
    scale = 1.0 / math.sqrt(HD)
    dk_ref[...] = jnp.zeros_like(dk_ref)
    dv_ref[...] = jnp.zeros_like(dv_ref)
    total = jnp.zeros((1, PAIR), f32)
    for at in range(0, full_len, step):
        low, high = span(full_len, step, at)
        rows = slice(at, at + step)
        keys = slice(low, high)
        allowed = block_mask(start_ref[rows, :1], at, step, low, high)
        q = qkv_ref[rows, :PAIR]
        k = qkv_ref[keys, PAIR : 2 * PAIR]
        v = qkv_ref[keys, 2 * PAIR :]
        g = grad_ref[rows, :]
        dq = jnp.zeros((step, PAIR), f32)
        dk = jnp.zeros((high - low, PAIR), f32)
        dv = jnp.zeros((high - low, PAIR), f32)
        for head in range(2):
            mine = head_lanes(q.shape) == (head == 0)
            qm = jnp.where(mine, q, jnp.zeros_like(q))
            gm = jnp.where(mine, g, jnp.zeros_like(g))
            km = jnp.where(head_lanes(k.shape) == (head == 0), k, jnp.zeros_like(k))
            s = dot_nt(qm, k) * scale
            probs = jnp.where(
                allowed, jnp.exp(s - lse_ref[rows, head * HD : head * HD + 1]), 0.0
            )
            dp = dot_nt(gm, v)
            mean = jnp.sum(dp * probs, axis=1, keepdims=True)
            ds = (probs * (dp - mean)).astype(bf16)
            dq = dq + dot(ds, km)
            dk = dk + dot_tn(ds, qm)
            dv = dv + dot_tn(probs.astype(bf16), gm)
        dk_ref[keys, :] += dk
        dv_ref[keys, :] += dv
        dq = turn_back(dq * scale, table_ref.at[:, rows, :]).astype(bf16)
        out_ref[rows, :PAIR] = dq
        total = total + jnp.sum(dq.astype(f32), axis=0, keepdims=True)
    sum_ref[:, :PAIR] = total
    dk = turn_back(dk_ref[...] * scale, table_ref).astype(bf16)
    out_ref[:, PAIR : 2 * PAIR] = dk
    sum_ref[:, PAIR : 2 * PAIR] = jnp.sum(dk.astype(f32), axis=0, keepdims=True)
    dv = dv_ref[...].astype(bf16)
    out_ref[:, 2 * PAIR :] = dv
    sum_ref[:, 2 * PAIR :] = jnp.sum(dv.astype(f32), axis=0, keepdims=True)


def whole(shape):
    return pl.BlockSpec(shape, lambda p: (0,) * len(shape))


def attend_step(full_len):
    return min(256, full_len)


def attend(joined, bias, table, start):
    full_len, width = joined.shape
    pairs = width // (3 * PAIR)
    step = attend_step(full_len)
    seen = sum(span(full_len, step, at)[1] - span(full_len, step, at)[0] for at in range(0, full_len, step)) * step
    wide = pl.BlockSpec((full_len, 3 * PAIR), lambda p: (0, p))
    thin = pl.BlockSpec((full_len, PAIR), lambda p: (0, p))
    return pl.pallas_call(
        functools.partial(attend_kernel, step),
        grid=(pairs,),
        in_specs=[
            wide,
            pl.BlockSpec((1, 3 * PAIR), lambda p: (0, p)),
            whole(table.shape),
            whole(start.shape),
        ],
        out_specs=[thin, wide, thin],
        out_shape=[
            jax.ShapeDtypeStruct((full_len, pairs * PAIR), bf16),
            jax.ShapeDtypeStruct((full_len, width), bf16),
            jax.ShapeDtypeStruct((full_len, pairs * PAIR), f32),
        ],
        compiler_params=pltpu.CompilerParams(vmem_limit_bytes=40 << 20),
        cost_estimate=pl.CostEstimate(
            flops=pairs * seen * PAIR * 8, transcendentals=pairs * seen * 2, bytes_accessed=full_len * width * 8
        ),
    )(joined, bias, table, start)


def attend_back(qkv, grad, lse, table, start):
    full_len, width = qkv.shape
    pairs = width // (3 * PAIR)
    step = attend_step(full_len)
    seen = sum(span(full_len, step, at)[1] - span(full_len, step, at)[0] for at in range(0, full_len, step)) * step
    wide = pl.BlockSpec((full_len, 3 * PAIR), lambda p: (0, p))
    thin = pl.BlockSpec((full_len, PAIR), lambda p: (0, p))
    return pl.pallas_call(
        functools.partial(attend_back_kernel, step),
        grid=(pairs,),
        in_specs=[wide, thin, thin, whole(table.shape), whole(start.shape)],
        out_specs=[wide, pl.BlockSpec((1, 3 * PAIR), lambda p: (0, p))],
        out_shape=[
            jax.ShapeDtypeStruct((full_len, width), bf16),
            jax.ShapeDtypeStruct((1, width), f32),
        ],
        scratch_shapes=[pltpu.VMEM((full_len, PAIR), f32), pltpu.VMEM((full_len, PAIR), f32)],
        compiler_params=pltpu.CompilerParams(vmem_limit_bytes=40 << 20),
        cost_estimate=pl.CostEstimate(
            flops=pairs * seen * PAIR * 20, transcendentals=pairs * seen * 2, bytes_accessed=full_len * width * 8
        ),
    )(qkv, grad, lse, table, start)


def rotary_table(full_len):
    half = ROT // 2
    inverse = 10000.0 ** (-2.0 * np.arange(half) / ROT)
    angles = np.arange(full_len)[:, None] * inverse[None, :]
    table = np.zeros((3, full_len, HD), np.float32)
    table[0, :, :half] = table[0, :, half:ROT] = np.cos(angles)
    table[0, :, ROT:] = 1.0
    table[1, :, :half] = -np.sin(angles)
    table[2, :, half:ROT] = np.sin(angles)
    return jnp.asarray(np.concatenate([table, table], axis=2))


def shards(
    dp,
    ctx,
    inputs,
    segments,
    ln1_gain,
    ln1_bias,
    qkv_weight,
    qkv_bias,
    out_weight,
    ln2_gain,
    ln2_bias,
    gate_weight,
    up_weight,
    down_weight,
    cotangent,
):
    local_len, width = inputs.shape[1], inputs.shape[2]
    full_len = segments.shape[1]
    heads = width // HD
    near = heads // ctx
    pairs = near // 2
    me = lax.axis_index("ctx")
    own = me * local_len

    part = ln1_gain.shape[0]
    small = jnp.concatenate([ln1_gain, ln1_bias, ln2_gain, ln2_bias, qkv_bias]).astype(f32)
    count = small.shape[0]
    small = jnp.pad(small, (0, 1024 - count)).reshape(8, 128)
    rows_here = qkv_weight.shape[0]
    rows, grad_rows = inputs[0], cotangent[0]
    fused = ctx == 4 and dp % 2 == 0 and part == HD
    if fused:
        small, params, joined_weight, out_full, normed_one, grad_wide = opening(
            dp, ctx, small, qkv_weight, out_weight, rows, grad_rows
        )
        gain_one, shift_one, gain_two, shift_two = params
        gate_weight, up_weight, down_weight, _ = lax.optimization_barrier(
            (gate_weight, up_weight, down_weight, normed_one)
        )
        small = small.reshape(dp * ctx, 1024)[:, :count]
    else:
        small = lax.all_gather(small[None, :], ("dp", "ctx"), axis=0, tiled=True)
        blocks = qkv_weight.reshape(rows_here, 3, pairs, 2, ctx, HD).transpose(4, 0, 2, 1, 3, 5)
        blocks = exchange_ctx(blocks.reshape(ctx, rows_here, near * 3 * HD), ctx)
        joined_weight = lax.all_gather(
            blocks.reshape(ctx * rows_here, near * 3 * HD), "dp", axis=0, tiled=True
        )
        out_full = lax.all_gather(out_weight, ("dp", "ctx"), axis=0, tiled=True)
        out_full = out_full.reshape(near, ctx, HD, width)
        out_full = lax.dynamic_index_in_dim(out_full, me, 1, keepdims=False)
        out_full = out_full.reshape(near * HD, width)
        small = small.reshape(dp * ctx, 1024)[:, :count]
        gain_one, shift_one, gain_two, shift_two = [
            small[:, i * part : (i + 1) * part].reshape(width) for i in range(4)
        ]
        scaled_wide, _ = norm_stats(gather_ctx(rows, ctx).astype(f32))
        normed_one = (scaled_wide * gain_one + shift_one).astype(bf16)
        grad_wide = gather_ctx(grad_rows, ctx)
    bias = small[:, 4 * part :].reshape(3, pairs, 2, ctx, HD)
    bias = lax.dynamic_index_in_dim(bias, me, 3, keepdims=False)
    bias = bias.transpose(1, 0, 2, 3).reshape(1, near * 3 * HD)
    gate_full = lax.all_gather(gate_weight, "dp", axis=0, tiled=True)
    up_full = lax.all_gather(up_weight, "dp", axis=0, tiled=True)
    down_full = lax.all_gather(down_weight, "dp", axis=1, tiled=True)

    segment = segments[0]
    start = jnp.sum((segment[None, :] < segment[:, None]).astype(jnp.int32), axis=1)
    start = jnp.broadcast_to(start[:, None], (full_len, 128))
    table = rotary_table(full_len)
    joined = dot(normed_one, joined_weight)
    attended, qkv, lse = attend(joined, bias, table, start)
    if fused:
        resid, normed_wide = mix(dp, ctx, attended, out_full, rows, gain_two, shift_two)
    else:
        resid = rows.astype(f32) + scatter_ctx(dot(attended, out_full), ctx)
        scaled_two, inv_two = norm_stats(resid)
        normed_wide = gather_ctx((scaled_two * gain_two + shift_two).astype(bf16), ctx)

    gate = dot(normed_wide, gate_full)
    upward = dot(normed_wide, up_full)
    sigma = jax.nn.sigmoid(gate)
    swish = gate * sigma
    inner = (swish * upward).astype(bf16)
    d_inner = dot_nt(grad_wide, down_full)
    d_gate = (d_inner * upward * sigma * (1.0 + gate * (1.0 - sigma))).astype(bf16)
    d_upward = (d_inner * swish).astype(bf16)
    d_down = dot_tn(inner, grad_wide).astype(bf16)
    d_down = lax.psum_scatter(d_down, "dp", scatter_dimension=1, tiled=True).astype(f32)
    d_gate_weight = dot_tn(normed_wide, d_gate).astype(bf16)
    d_up_weight = dot_tn(normed_wide, d_upward).astype(bf16)
    branch = dot(inner, down_full)
    d_gate_ready, d_gate_weight = lax.optimization_barrier((d_gate, d_gate_weight))
    d_gate_weight = lax.psum_scatter(d_gate_weight, "dp", scatter_dimension=0, tiled=True).astype(f32)
    if fused:
        d_resid, sums_two, d_proj = mix_back(
            dp, ctx, d_gate_ready, d_upward, gate_full, up_full, resid, grad_rows, gain_two
        )
    else:
        d_normed_two = scatter_ctx(dot_nt(d_gate, gate_full) + dot_nt(d_upward, up_full), ctx)
        grad, d_gain_two, d_shift_two = norm_backward(d_normed_two, scaled_two, inv_two, gain_two)
        d_resid = grad_rows.astype(f32) + grad
        d_proj = gather_ctx(d_resid.astype(bf16), ctx)
    branch, _ = lax.optimization_barrier((branch, d_proj))
    output = (resid + scatter_ctx(branch, ctx)).astype(bf16)
    d_up_weight = lax.psum_scatter(d_up_weight, "dp", scatter_dimension=0, tiled=True).astype(f32)

    d_attended = dot_nt(d_proj, out_full).astype(bf16)
    d_out_weight = dot_tn(attended, d_proj).astype(bf16)
    d_joined, d_bias = attend_back(qkv, d_attended, lse, table, start)
    d_joined_weight = dot_tn(normed_one, d_joined).astype(bf16)
    d_bias = d_bias.reshape(pairs, 3, 2, HD).transpose(1, 0, 2, 3)
    if fused:
        d_bias = jnp.pad(d_bias.reshape(dp, -1), ((0, 0), (0, width // dp - near * 3 * HD // dp)))
        grad_input, d_joined_weight, d_out_weight, small = closing(
            dp, ctx, d_joined, joined_weight, d_joined_weight, d_out_weight, rows, d_resid, gain_one, sums_two, d_bias
        )
        vectors = lax.dynamic_slice_in_dim(jnp.sum(small[:, :4], axis=0), me * part, part, 1)
        d_gain_one, d_shift_one, d_gain_two, d_shift_two = vectors
        d_bias = small[:, 4, : near * 3 * HD // dp].reshape(ctx, -1, HD).transpose(1, 0, 2)
        d_bias = lax.dynamic_index_in_dim(d_bias.reshape(ctx, -1), me, 0, keepdims=False)
    else:
        at_me = lax.broadcasted_iota(jnp.int32, (1, ctx, 1, 1), 1) == me
        d_out_weight = jnp.where(at_me, d_out_weight.reshape(near, 1, HD, width), jnp.zeros((), bf16))
        d_out_weight = lax.psum_scatter(
            d_out_weight.reshape(width, width), ("dp", "ctx"), scatter_dimension=0, tiled=True
        ).astype(f32)
        d_normed_one = scatter_ctx(dot_nt(d_joined, joined_weight), ctx)
        scaled_one, inv_one = norm_stats(rows.astype(f32))
        grad, d_gain_one, d_shift_one = norm_backward(d_normed_one, scaled_one, inv_one, gain_one)
        grad_input = d_resid + grad
        d_joined_weight = lax.psum_scatter(d_joined_weight, "dp", scatter_dimension=0, tiled=True)
        blocks = exchange_ctx(d_joined_weight.reshape(ctx, rows_here, near * 3 * HD), ctx)
        blocks = blocks.reshape(ctx, rows_here, pairs, 3, 2, HD).transpose(1, 3, 2, 4, 0, 5)
        d_joined_weight = blocks.reshape(rows_here, 3 * width).astype(f32)
        at_me = (lax.broadcasted_iota(jnp.int32, (1, 1, 1, ctx, 1), 3) == me).astype(f32)
        d_bias = (d_bias[:, :, :, None, :] * at_me).reshape(dp * ctx, -1)
        small = jnp.concatenate(
            [t.reshape(dp * ctx, part) for t in (d_gain_one, d_shift_one, d_gain_two, d_shift_two)]
            + [d_bias],
            axis=1,
        )
        small = lax.psum_scatter(small, ("dp", "ctx"), scatter_dimension=0, tiled=True)[0]
        d_gain_one, d_shift_one, d_gain_two, d_shift_two = [
            small[i * part : (i + 1) * part] for i in range(4)
        ]
        d_bias = small[4 * part :]
    return (
        output[None],
        grad_input[None],
        d_gain_one,
        d_shift_one,
        d_joined_weight,
        d_bias,
        d_out_weight,
        d_gain_two,
        d_shift_two,
        d_gate_weight,
        d_up_weight,
        d_down,
    )


def solution(mesh):
    every = ("dp", "ctx")
    return jax.shard_map(
        functools.partial(shards, mesh.shape["dp"], mesh.shape["ctx"]),
        mesh=mesh,
        in_specs=(
            P("dp", "ctx", None),
            P("dp", None),
            P(every),
            P(every),
            P(every, None),
            P(every),
            P(every, None),
            P(every),
            P(every),
            P("dp", "ctx"),
            P("dp", "ctx"),
            P("ctx", "dp"),
            P("dp", "ctx", None),
        ),
        out_specs=(
            P("dp", "ctx", None),
            P("dp", "ctx", None),
            P(every),
            P(every),
            P(every, None),
            P(every),
            P(every, None),
            P(every),
            P(every),
            P("dp", "ctx"),
            P("dp", "ctx"),
            P("ctx", "dp"),
        ),
        check_vma=False,
    )
```

```python
import functools
import math

import jax
import jax.numpy as jnp
import numpy as np
from jax import lax
from jax.experimental import pallas as pl
from jax.experimental.pallas import tpu as pltpu
from jax.sharding import PartitionSpec as P

HD = 64
ROT = 16
DOC_MAX = 512
PAIR = 2 * HD

norm_eps = 1e-05
masked_value = -1e30
f32 = jnp.float32
bf16 = jnp.bfloat16


def dot(a, b):
    return jnp.dot(a, b, preferred_element_type=f32)


def dot_nt(a, b):
    return lax.dot_general(a, b, (((1,), (1,)), ((), ())), preferred_element_type=f32)


def dot_tn(a, b):
    return lax.dot_general(a, b, (((0,), (0,)), ((), ())), preferred_element_type=f32)


def norm_stats(rows):
    row_mean = jnp.mean(rows, axis=-1, keepdims=True)
    centered = rows - row_mean
    variance = jnp.mean(centered * centered, axis=-1, keepdims=True)
    inv_std = lax.rsqrt(variance + norm_eps)
    return centered * inv_std, inv_std


def norm_backward(grad_normed, scaled, inv_std, gain):
    grad_gain = jnp.sum(grad_normed * scaled, axis=0)
    grad_shift = jnp.sum(grad_normed, axis=0)
    inner_grad = grad_normed * gain
    grad_rows = inv_std * (
        inner_grad
        - jnp.mean(inner_grad, axis=-1, keepdims=True)
        - scaled * jnp.mean(inner_grad * scaled, axis=-1, keepdims=True)
    )
    return grad_rows, grad_gain, grad_shift


def partner(n, k):
    return [(c, c ^ k) for c in range(n)]


def hop(x, n, k):
    return lax.ppermute(x, "ctx", partner(n, k))


def gather_relative(block, n):
    if n != 4:
        return [block] + [hop(block, n, k) for k in range(1, n)]
    half = block.shape[0] // 2
    one = hop(block, n, 1)
    two = hop(block, n, 2)
    low = hop(one[:half], n, 2)
    high = hop(two[half:], n, 1)
    return [block, one, two, jnp.concatenate([low, high], axis=0)]


def gather_ctx(block, n):
    me = lax.axis_index("ctx")
    size = block.shape[0]
    parts = gather_relative(block, n)
    full = jnp.zeros((n * size,) + block.shape[1:], block.dtype)
    for k, part in enumerate(parts):
        full = lax.dynamic_update_slice_in_dim(full, part, (me ^ k) * size, 0)
    return full


def scatter_ctx(partial, n, meanwhile=None):
    me = lax.axis_index("ctx")
    size = partial.shape[0] // n

    def block(k):
        return lax.dynamic_slice_in_dim(partial, (me ^ k) * size, size, 0)

    if n != 4:
        total = block(0).astype(f32)
        for k in range(1, n):
            total = total + hop(block(k).astype(bf16), n, k).astype(f32)
        return total
    half = size // 2
    far = block(3).astype(bf16)
    low = hop(far[:half], n, 1).astype(f32)
    high = hop(far[half:], n, 2).astype(f32)
    if meanwhile is not None:
        partial, _ = lax.optimization_barrier((partial, meanwhile))
    one = block(1).astype(f32)
    two = block(2).astype(f32)
    to_one = jnp.concatenate([one[:half], one[half:] + high], axis=0).astype(bf16)
    to_two = jnp.concatenate([two[:half] + low, two[half:]], axis=0).astype(bf16)
    return block(0).astype(f32) + hop(to_one, n, 1).astype(f32) + hop(to_two, n, 2).astype(f32)


def exchange_ctx(blocks, n):
    me = lax.axis_index("ctx")
    got = lax.dynamic_update_slice_in_dim(
        jnp.zeros_like(blocks), lax.dynamic_slice_in_dim(blocks, me, 1, 0), me, 0
    )
    for k in range(1, n):
        sent = lax.dynamic_slice_in_dim(blocks, me ^ k, 1, 0)
        got = lax.dynamic_update_slice_in_dim(got, hop(sent, n, k), me ^ k, 0)
    return got


MESH = pl.DeviceIdType.MESH
ANY = pl.BlockSpec(memory_space=pl.ANY)


class Place:
    def __init__(self, dp):
        self.row = lax.axis_index("dp")
        self.col = lax.axis_index("ctx")
        self.lines = dp // 2
        self.line = self.row // 2
        self.core = self.row % 2
        self.twin = (self.row + 1 - 2 * self.core, self.col)

    def other(self, k):
        col, bit = self.col, 1
        while bit <= k:
            if k & bit:
                col = col + bit * (1 - 2 * ((self.col // bit) % 2))
            bit *= 2
        return col

    def across(self, k):
        return (self.row, self.other(k))

    def above(self):
        return (self.row + 2, self.col)

    def below(self):
        return (self.row - 2, self.col)


def greet(place, ctx):
    barrier = pltpu.get_barrier_semaphore()
    for k in range(1, ctx):
        pl.semaphore_signal(barrier, 1, device_id=place.across(k), device_id_type=MESH)
    pl.semaphore_wait(barrier, ctx - 1)


def remote(src, dst, send, recv, device):
    return pltpu.make_async_remote_copy(
        src_ref=src, dst_ref=dst, send_sem=send, recv_sem=recv, device_id=device, device_id_type=MESH
    )


class LineGather:
    def __init__(self, place, shard, sems):
        self.place, self.shard, self.sems = place, shard, sems

    def row(self, line):
        return line * 2 + self.place.core

    def up(self, hop):
        part = self.shard(self.row(self.place.line - hop + 1))
        return remote(part, part, self.sems.at[0, hop], self.sems.at[1, hop], self.place.above())

    def down(self, hop):
        part = self.shard(self.row(self.place.line + hop - 1))
        return remote(part, part, self.sems.at[2, hop], self.sems.at[3, hop], self.place.below())

    def over(self, at, row):
        part = self.shard(row)
        return remote(part, part, self.sems.at[4, at], self.sems.at[5, at], self.place.twin)

    def sends_up(self, hop):
        return (self.place.line - hop + 1 >= 0) & (self.place.line < self.place.lines - 1)

    def sends_down(self, hop):
        return (self.place.line + hop - 1 < self.place.lines) & (self.place.line > 0)

    def send(self, hop):
        place = self.place
        pl.when(self.sends_up(hop))(lambda: self.up(hop).start())
        pl.when(self.sends_down(hop))(lambda: self.down(hop).start())
        if hop == 1:
            self.over(0, place.row).start()

    def receive(self, hop):
        place = self.place

        @pl.when(place.line - hop >= 0)
        def _():
            part = self.shard(self.row(place.line - hop))
            remote(part, part, self.sems.at[0, hop], self.sems.at[1, hop], place.twin).wait_recv()
            self.over(hop, self.row(place.line - hop)).start()

        @pl.when(place.line + hop < place.lines)
        def _():
            part = self.shard(self.row(place.line + hop))
            remote(part, part, self.sems.at[2, hop], self.sems.at[3, hop], place.twin).wait_recv()
            self.over(place.lines - 1 + hop, self.row(place.line + hop)).start()

    def came_over(self, at, row):
        part = self.shard(row)
        remote(part, part, self.sems.at[4, at], self.sems.at[5, at], self.place.twin).wait_recv()

    def settle(self, hop, use=None):
        place = self.place
        other = 1 - 2 * place.core
        if hop == 0:
            if use:
                use(place.row)
            self.came_over(0, place.row + other)
            if use:
                use(place.row + other)
            return
        for at, line, there in (
            (hop, place.line - hop, place.line - hop >= 0),
            (place.lines - 1 + hop, place.line + hop, place.line + hop < place.lines),
        ):

            @pl.when(there)
            def _():
                row = self.row(line)
                if use:
                    use(row)
                self.came_over(at, row + other)
                if use:
                    use(row + other)

    def finish(self):
        place = self.place
        self.over(0, place.row).wait_send()
        for hop in range(1, place.lines):
            pl.when(self.sends_up(hop))(lambda: self.up(hop).wait_send())
            pl.when(self.sends_down(hop))(lambda: self.down(hop).wait_send())
            for at, line, there in (
                (hop, place.line - hop, place.line - hop >= 0),
                (place.lines - 1 + hop, place.line + hop, place.line + hop < place.lines),
            ):
                pl.when(there)(lambda: self.over(at, self.row(line)).wait_send())

    @staticmethod
    def scratch(dp):
        return pltpu.SemaphoreType.DMA((6, dp))


class CtxGather:
    def __init__(self, place, block, full, size, sems):
        self.place, self.block, self.full, self.size, self.sems = place, block, full, size, sems

    def rows(self, col, start=0, size=None):
        size = self.size if size is None else size
        return self.full.at[pl.ds(pl.multiple_of(col * self.size + start, size), size), :]

    def copies(self):
        place, half = self.place, self.size // 2
        me = place.col
        return [
            remote(self.block, self.rows(me), self.sems.at[0, 0], self.sems.at[1, 0], place.across(1)),
            remote(self.block, self.rows(me), self.sems.at[0, 1], self.sems.at[1, 1], place.across(2)),
            remote(
                self.rows(place.other(1), 0, half), self.rows(place.other(1), 0, half),
                self.sems.at[0, 2], self.sems.at[1, 2], place.across(2),
            ),
            remote(
                self.rows(place.other(2), half, half), self.rows(place.other(2), half, half),
                self.sems.at[0, 3], self.sems.at[1, 3], place.across(1),
            ),
        ]

    def arrivals(self):
        place, half = self.place, self.size // 2
        me = place.col
        parts = [self.rows(place.other(1)), self.rows(place.other(2)), self.rows(place.other(3), 0, half), self.rows(place.other(3), half, half)]
        return [
            remote(part, part, self.sems.at[0, i], self.sems.at[1, i], place.across(1))
            for i, part in enumerate(parts)
        ]

    def first(self):
        copies = self.copies()
        copies[0].start()
        copies[1].start()

    def second(self):
        copies, arrivals = self.copies(), self.arrivals()
        arrivals[0].wait_recv()
        copies[2].start()
        arrivals[1].wait_recv()
        copies[3].start()

    def finish(self):
        copies, arrivals = self.copies(), self.arrivals()
        arrivals[2].wait_recv()
        arrivals[3].wait_recv()
        for copy in copies:
            copy.wait_send()

    @staticmethod
    def scratch():
        return pltpu.SemaphoreType.DMA((2, 4))


def greet_all(place, dp, ctx):
    barrier = pltpu.get_barrier_semaphore()
    for k in range(1, ctx):
        pl.semaphore_signal(barrier, 1, device_id=place.across(k), device_id_type=MESH)
    for k in range(1, dp):
        pl.semaphore_signal(barrier, 1, device_id=((place.row + k) % dp, place.col), device_id_type=MESH)
    pl.semaphore_wait(barrier, ctx + dp - 2)


PARTS = 2


def opening_kernel(
    dp, ctx,
    small_ref, qkv_ref, out_weight_ref, rows_ref, cot_ref,
    small_all, params_ref, weight_ref, out_all, normed_ref, joined_ref, cot_all,
    blocks, rows_all, local_sem, swap_sem, small_sem, line_joined, line_out, rows_sem, cot_sem,
):
    place = Place(dp)
    me, row = place.col, place.row
    depth = qkv_ref.shape[0]
    length, width = rows_ref.shape
    rows_out = out_weight_ref.shape[0]
    tall = ctx * depth

    low = head_lanes((depth, PAIR))
    for p in range(width // HD // ctx // 2):
        for t in range(3):
            lanes = slice((3 * p + t) * PAIR, (3 * p + t + 1) * PAIR)
            for c in range(0, ctx, 2):
                at = t * width + (2 * p * ctx + c) * HD
                a = qkv_ref[:, at : at + PAIR].astype(f32)
                at = at + ctx * HD
                b = qkv_ref[:, at : at + PAIR].astype(f32)
                blocks[c, :, lanes] = jnp.where(low, a, pltpu.roll(b, HD, 1)).astype(bf16)
                blocks[c + 1, :, lanes] = jnp.where(low, pltpu.roll(a, HD, 1), b).astype(bf16)
    small_all[row, me] = small_ref[...]
    greet_all(place, dp, ctx)

    def weight_rows(row, col):
        return weight_ref.at[pl.ds(pl.multiple_of((row * ctx + col) * depth, depth), depth), :]

    def out_shard(row):
        return out_all.at[pl.ds(pl.multiple_of(row * rows_out, rows_out), rows_out), :]

    def block(ref, col):
        return ref.at[pl.ds(pl.multiple_of(col * length, length), length), :]

    part_cols = weight_ref.shape[1] // PARTS

    def weight_part(i, row):
        return weight_ref.at[
            pl.ds(pl.multiple_of(row * tall, tall), tall), pl.ds(i * part_cols, part_cols)
        ]

    local = [
        pltpu.make_async_copy(blocks.at[me], weight_rows(row, me), local_sem.at[0]),
        pltpu.make_async_copy(out_weight_ref, out_shard(row), local_sem.at[1]),
        pltpu.make_async_copy(rows_ref, block(rows_all, me), local_sem.at[2]),
        pltpu.make_async_copy(cot_ref, block(cot_all, me), local_sem.at[3]),
    ]
    swaps = [
        remote(small_ref, small_all.at[row, me], swap_sem.at[0, k], swap_sem.at[1, k], place.across(k))
        for k in range(1, ctx)
    ] + [
        remote(
            blocks.at[place.other(k)], weight_rows(row, me), swap_sem.at[2, k], swap_sem.at[3, k], place.across(k)
        )
        for k in range(1, ctx)
    ]
    for copy in swaps:
        copy.start()
    for copy in local:
        copy.start()
    rows_gather = CtxGather(place, rows_ref, rows_all, length, rows_sem)
    cot_gather = CtxGather(place, cot_ref, cot_all, length, cot_sem)
    out_line = LineGather(place, out_shard, line_out)
    lines = [
        LineGather(place, functools.partial(weight_part, i), line_joined.at[i]) for i in range(PARTS)
    ] + [out_line]
    local[1].wait()
    out_line.send(1)
    rows_gather.first()
    for k in range(1, ctx):
        remote(
            small_ref, small_all.at[row, place.other(k)], swap_sem.at[0, k], swap_sem.at[1, k], place.across(k)
        ).wait_recv()
    small_sends = [
        remote(
            small_all.at[row], small_all.at[row], small_sem.at[0, k], small_sem.at[1, k], ((row + k) % dp, me)
        )
        for k in range(1, dp)
    ]
    for copy in small_sends:
        copy.start()
    local[0].wait()
    for k in range(1, ctx):
        part = weight_rows(row, place.other(k))
        remote(part, part, swap_sem.at[2, k], swap_sem.at[3, k], place.across(k)).wait_recv()
    for line in lines[:PARTS]:
        line.send(1)

    for k in range(1, dp):
        part = small_all.at[(row + dp - k) % dp]
        remote(part, part, small_sem.at[0, k], small_sem.at[1, k], place.twin).wait_recv()
    low = head_lanes((1, PAIR))
    for i in range(dp * ctx // 2):
        lanes = slice(i * PAIR, (i + 1) * PAIR)
        a = small_all[2 * i // ctx, 2 * i % ctx]
        b = small_all[(2 * i + 1) // ctx, (2 * i + 1) % ctx]
        for r in range(2):
            ar, br = a[r : r + 1, :], b[r : r + 1, :]
            params_ref[2 * r : 2 * r + 1, lanes] = jnp.where(low, ar, pltpu.roll(br, HD, 1))
            params_ref[2 * r + 1 : 2 * r + 2, lanes] = jnp.where(low, pltpu.roll(ar, HD, 1), br)

    def normalize(col):
        step = 64

        @pl.loop(0, length // step)
        def _(i):
            rows = pl.ds(pl.multiple_of(col * length + i * step, step), step)
            scaled, _ = norm_stats(rows_all[rows, :].astype(f32))
            normed_ref[rows, :] = (scaled * params_ref[0:1, :] + params_ref[1:2, :]).astype(bf16)

    def multiply(i, row):
        at = pl.multiple_of(row * tall, tall)
        cols = slice(i * part_cols, (i + 1) * part_cols)

        @pl.loop(0, ctx)
        def _(b):
            rows = pl.ds(pl.multiple_of(b * length, length), length)
            joined_ref[rows, cols] += dot(normed_ref[rows, pl.ds(at, tall)], weight_ref[pl.ds(at, tall), cols])

    def forward(hop):
        for line in lines:
            line.receive(hop)
            if hop < place.lines - 1:
                line.send(hop + 1)

    def absorb(hop):
        for i in range(PARTS):
            lines[i].settle(hop, functools.partial(multiply, i))

    joined_ref[...] = jnp.zeros_like(joined_ref)
    local[2].wait()
    normalize(me)
    rows_gather.second()
    cot_gather.first()
    for hop in range(1, place.lines):
        forward(hop)
        if hop == 1:
            for col in (place.other(1), place.other(2)):
                normalize(col)
            rows_gather.finish()
            normalize(place.other(3))
            cot_gather.second()
        absorb(hop - 1)
    absorb(place.lines - 1)
    for hop in range(place.lines):
        out_line.settle(hop)
    for line in lines:
        line.finish()
    cot_gather.finish()
    for copy in swaps + small_sends:
        copy.wait_send()
    local[3].wait()


def opening(dp, ctx, small, qkv_weight, out_weight, rows, cot):
    depth, width = qkv_weight.shape[0], rows.shape[1]
    length = rows.shape[0]
    near = 3 * width // ctx
    vmem = pl.BlockSpec(memory_space=pltpu.VMEM)
    return pl.pallas_call(
        functools.partial(opening_kernel, dp, ctx),
        in_specs=[vmem, vmem, ANY, ANY, ANY],
        out_specs=[vmem, vmem, vmem, ANY, vmem, vmem, ANY],
        out_shape=[
            jax.ShapeDtypeStruct((dp, ctx) + small.shape, f32),
            jax.ShapeDtypeStruct((4, width), f32),
            jax.ShapeDtypeStruct((dp * ctx * depth, near), bf16),
            jax.ShapeDtypeStruct((dp * out_weight.shape[0], width), bf16),
            jax.ShapeDtypeStruct((ctx * length, width), bf16),
            jax.ShapeDtypeStruct((ctx * length, near), f32),
            jax.ShapeDtypeStruct((ctx * length, width), bf16),
        ],
        scratch_shapes=[
            pltpu.VMEM((ctx, depth, near), bf16),
            pltpu.VMEM((ctx * length, width), bf16),
            pltpu.SemaphoreType.DMA((4,)),
            pltpu.SemaphoreType.DMA((4, ctx)),
            pltpu.SemaphoreType.DMA((2, dp)),
            pltpu.SemaphoreType.DMA((PARTS, 6, dp)),
            LineGather.scratch(dp),
            CtxGather.scratch(),
            CtxGather.scratch(),
        ],
        compiler_params=pltpu.CompilerParams(
            collective_id=0, has_side_effects=True, vmem_limit_bytes=40 << 20
        ),
        cost_estimate=pl.CostEstimate(
            flops=2 * ctx * length * width * near, transcendentals=0, bytes_accessed=200 << 20
        ),
    )(small, qkv_weight, out_weight, rows, cot)


CHUNKS = 4


class CtxReduce:
    def __init__(self, place, block, total, sent, got, sems):
        self.place, self.block, self.total = place, block, total
        self.sent, self.got, self.sems = sent, got, sems
        self.size = total.shape[1] // CHUNKS

    def chunk(self, j):
        return pl.ds(j * self.size, self.size)

    def copy(self, kind, j):
        way = kind if kind else 1 + j % 2
        return remote(
            self.sent.at[kind, self.chunk(j)], self.got.at[kind, self.chunk(j)],
            self.sems.at[0, kind, j], self.sems.at[1, kind, j], self.place.across(way),
        )

    def start(self):
        place = self.place
        self.sent[0] = self.block(place.other(3)).astype(bf16)
        for j in range(CHUNKS):
            self.copy(0, j).start()
        for kind in (1, 2):
            self.total[kind - 1] = self.block(place.other(kind))
            for j in range(CHUNKS):
                if kind == 1 + j % 2:
                    self.sent[kind, self.chunk(j)] = self.total[kind - 1, self.chunk(j)].astype(bf16)
                    self.copy(kind, j).start()

    def relay(self):
        for j in range(CHUNKS):
            kind = 2 - j % 2
            self.copy(0, j).wait_recv()
            share = self.total[kind - 1, self.chunk(j)] + self.got[0, self.chunk(j)].astype(f32)
            self.sent[kind, self.chunk(j)] = share.astype(bf16)
            self.copy(kind, j).start()
        self.total[0] = self.block(self.place.col)

    def sum(self, j):
        for kind in (1, 2):
            self.copy(kind, j).wait_recv()
        rows = self.chunk(j)
        return self.total[0, rows] + self.got[1, rows].astype(f32) + self.got[2, rows].astype(f32)

    def finish(self):
        for kind in range(3):
            for j in range(CHUNKS):
                self.copy(kind, j).wait_send()

    @staticmethod
    def scratch(size, width):
        return [
            pltpu.VMEM((2, size, width), f32),
            pltpu.VMEM((3, size, width), bf16),
            pltpu.VMEM((3, size, width), bf16),
            pltpu.SemaphoreType.DMA((2, 3, CHUNKS)),
        ]


class CtxSpread:
    def __init__(self, place, made, full, sems):
        self.place, self.made, self.full, self.sems = place, made, full, sems
        self.size = made.shape[0] // CHUNKS

    def rows(self, col, j):
        at = (col * CHUNKS + j) * self.size
        return self.full.at[pl.ds(pl.multiple_of(at, self.size), self.size), :]

    def copy(self, kind, j):
        place = self.place
        if kind < 2:
            part, there = self.made.at[pl.ds(j * self.size, self.size), :], self.rows(place.col, j)
            way = 1 + kind
        else:
            way = 2 - j % 2
            part = there = self.rows(place.other(3 - way), j)
        return remote(part, there, self.sems.at[0, kind, j], self.sems.at[1, kind, j], place.across(way))

    def arrived(self, kind, j):
        part = self.rows(self.place.other(kind + 1), j)
        remote(
            part, part, self.sems.at[0, kind, j], self.sems.at[1, kind, j], self.place.across(1)
        ).wait_recv()

    def local(self, j):
        part = self.made.at[pl.ds(j * self.size, self.size), :]
        return pltpu.make_async_copy(part, self.rows(self.place.col, j), self.sems.at[0, 3, j])

    def send(self, j):
        self.copy(0, j).start()
        self.copy(1, j).start()
        self.local(j).start()

    def relay(self, j):
        way = 2 - j % 2
        self.arrived(2 - way, j)
        self.copy(2, j).start()

    def finish(self):
        for j in range(CHUNKS):
            way = 2 - j % 2
            self.arrived(way - 1, j)
            self.arrived(2, j)
            self.local(j).wait()
            for kind in range(3):
                self.copy(kind, j).wait_send()

    @staticmethod
    def scratch():
        return pltpu.SemaphoreType.DMA((2, 4, CHUNKS))


def rows_of(ref, col, size):
    return ref[pl.ds(pl.multiple_of(col * size, size), size), :]


def mix_kernel(
    dp, ctx, attended_ref, weight_ref, rows_ref, gain_ref, shift_ref, down_ref, resid_ref, wide_ref, down_all,
    total, sent, got, made, reduce_sem, spread_sem, line_sem, local_sem,
):
    place = Place(dp)
    greet_all(place, dp, ctx)
    size = rows_ref.shape[0]
    cols = down_ref.shape[1]

    def shard(row):
        return down_all.at[:, pl.ds(pl.multiple_of(row * cols, cols), cols)]

    line = LineGather(place, shard, line_sem)
    local = pltpu.make_async_copy(down_ref, shard(place.row), local_sem)
    local.start()
    reduce = CtxReduce(
        place, lambda col: dot(rows_of(attended_ref, col, size), weight_ref[...]), total, sent, got, reduce_sem
    )
    spread = CtxSpread(place, made, wide_ref, spread_sem)
    reduce.start()
    local.wait()
    line.send(1)
    reduce.relay()
    for j in range(CHUNKS):
        rows = reduce.chunk(j)
        resid = rows_ref[rows, :].astype(f32) + reduce.sum(j)
        resid_ref[rows, :] = resid
        scaled, _ = norm_stats(resid)
        made[rows, :] = (scaled * gain_ref[...] + shift_ref[...]).astype(bf16)
        spread.send(j)
        if j:
            spread.relay(j - 1)
        if j == CHUNKS // 2:
            line.receive(1)
            if place.lines > 2:
                line.send(2)
    spread.relay(CHUNKS - 1)
    for hop in range(2, place.lines):
        line.receive(hop)
        if hop < place.lines - 1:
            line.send(hop + 1)
    spread.finish()
    for hop in range(place.lines):
        line.settle(hop)
    line.finish()
    reduce.finish()


def mix(dp, ctx, attended, weight, rows, gain, shift, down):
    size, width = rows.shape
    vmem = pl.BlockSpec(memory_space=pltpu.VMEM)
    return pl.pallas_call(
        functools.partial(mix_kernel, dp, ctx),
        in_specs=[vmem] * 5 + [ANY],
        out_specs=[vmem, ANY, ANY],
        out_shape=[
            jax.ShapeDtypeStruct((size, width), f32),
            jax.ShapeDtypeStruct((ctx * size, width), bf16),
            jax.ShapeDtypeStruct((down.shape[0], dp * down.shape[1]), bf16),
        ],
        scratch_shapes=CtxReduce.scratch(size, width)[:3]
        + [
            pltpu.VMEM((size, width), bf16),
            CtxReduce.scratch(size, width)[3],
            CtxSpread.scratch(),
            LineGather.scratch(dp),
            pltpu.SemaphoreType.DMA,
        ],
        compiler_params=pltpu.CompilerParams(
            collective_id=2, has_side_effects=True, vmem_limit_bytes=40 << 20
        ),
        cost_estimate=pl.CostEstimate(
            flops=2 * attended.size * width, transcendentals=0, bytes_accessed=180 << 20
        ),
    )(attended, weight, rows, gain.reshape(1, width), shift.reshape(1, width), down)


def mix_back_kernel(
    dp, ctx, gate_ref, up_ref, gate_weight_ref, up_weight_ref, resid_ref, cot_ref, gain_ref,
    d_resid_ref, sums_ref, wide_ref,
    total, sent, got, made, reduce_sem, spread_sem,
):
    place = Place(dp)
    greet(place, ctx)
    size = cot_ref.shape[0]

    def block(col):
        return dot_nt(rows_of(gate_ref, col, size), gate_weight_ref[...]) + dot_nt(
            rows_of(up_ref, col, size), up_weight_ref[...]
        )

    reduce = CtxReduce(place, block, total, sent, got, reduce_sem)
    spread = CtxSpread(place, made, wide_ref, spread_sem)
    reduce.start()
    reduce.relay()
    sums_ref[...] = jnp.zeros_like(sums_ref)
    for j in range(CHUNKS):
        rows = reduce.chunk(j)
        scaled, inv_std = norm_stats(resid_ref[rows, :])
        grad, d_gain, d_shift = norm_backward(reduce.sum(j), scaled, inv_std, gain_ref[...])
        sums_ref[0:1, :] += d_gain[None]
        sums_ref[1:2, :] += d_shift[None]
        grad = cot_ref[rows, :].astype(f32) + grad
        d_resid_ref[rows, :] = grad
        made[rows, :] = grad.astype(bf16)
        spread.send(j)
        if j:
            spread.relay(j - 1)
    spread.relay(CHUNKS - 1)
    spread.finish()
    reduce.finish()


def mix_back(dp, ctx, d_gate, d_up, gate_weight, up_weight, resid, cot, gain):
    size, width = cot.shape
    vmem = pl.BlockSpec(memory_space=pltpu.VMEM)
    return pl.pallas_call(
        functools.partial(mix_back_kernel, dp, ctx),
        in_specs=[vmem] * 7,
        out_specs=[vmem, vmem, ANY],
        out_shape=[
            jax.ShapeDtypeStruct((size, width), f32),
            jax.ShapeDtypeStruct((2, width), f32),
            jax.ShapeDtypeStruct((ctx * size, width), bf16),
        ],
        scratch_shapes=CtxReduce.scratch(size, width)[:3]
        + [
            pltpu.VMEM((size, width), bf16),
            CtxReduce.scratch(size, width)[3],
            CtxSpread.scratch(),
        ],
        compiler_params=pltpu.CompilerParams(
            collective_id=3, has_side_effects=True, vmem_limit_bytes=56 << 20
        ),
        cost_estimate=pl.CostEstimate(
            flops=4 * d_gate.size * width, transcendentals=0, bytes_accessed=180 << 20
        ),
    )(d_gate, d_up, gate_weight, up_weight, resid, cot, gain.reshape(1, width))


class LineReduce:
    def __init__(self, place, parts, pair, got, sems):
        self.place, self.parts, self.pair, self.got, self.sems = place, parts, pair, got, sems

    def swap(self, line):
        row = 2 * line + 1 - self.place.core
        return remote(
            self.parts.at[row], self.pair.at[line], self.sems.at[0, line], self.sems.at[1, line], self.place.twin
        )

    def start(self):
        for line in range(self.place.lines):
            self.swap(line).start()

    def add(self):
        for line in range(self.place.lines):
            self.swap(line).wait_recv()
            both = self.parts[2 * line + self.place.core].astype(f32) + self.pair[line].astype(f32)
            self.pair[line] = both.astype(bf16)

    def up(self, far):
        part = self.place.line + far
        return remote(
            self.pair.at[part], self.got.at[part], self.sems.at[2, far], self.sems.at[3, far], self.place.above()
        )

    def down(self, far):
        part = self.place.line - far
        slot = part if far > 1 else self.place.lines
        return remote(
            self.pair.at[part], self.got.at[slot], self.sems.at[4, far], self.sems.at[5, far], self.place.below()
        )

    def came_up(self, far):
        slot = self.got.at[self.place.line + far]
        remote(slot, slot, self.sems.at[2, far + 1], self.sems.at[3, far + 1], self.place.twin).wait_recv()

    def came_down(self, far):
        slot = self.got.at[self.place.line - far if far else self.place.lines]
        remote(slot, slot, self.sems.at[4, far + 1], self.sems.at[5, far + 1], self.place.twin).wait_recv()

    def send(self, far):
        place = self.place

        @pl.when(place.line + far < place.lines)
        def _():
            @pl.when(place.line > 0)
            def _():
                self.came_up(far)
                part = place.line + far
                self.pair[part] = (self.pair[part].astype(f32) + self.got[part].astype(f32)).astype(bf16)

            self.up(far).start()

        @pl.when(place.line - far >= 0)
        def _():
            @pl.when(place.line < place.lines - 1)
            def _():
                self.came_down(far)
                part = place.line - far
                self.pair[part] = (self.pair[part].astype(f32) + self.got[part].astype(f32)).astype(bf16)

            self.down(far).start()

    def collect(self, out):
        place = self.place
        out[...] = self.pair[place.line].astype(f32)

        @pl.when(place.line > 0)
        def _():
            self.came_up(0)
            out[...] += self.got[place.line].astype(f32)

        @pl.when(place.line < place.lines - 1)
        def _():
            self.came_down(0)
            out[...] += self.got[place.lines].astype(f32)

    def finish(self):
        place = self.place
        for line in range(place.lines):
            self.swap(line).wait_send()
        for far in range(1, place.lines):
            pl.when(place.line + far < place.lines)(lambda: self.up(far).wait_send())
            pl.when(place.line - far >= 0)(lambda: self.down(far).wait_send())

    @staticmethod
    def scratch(dp, tile):
        return [
            pltpu.VMEM((dp // 2,) + tile, bf16),
            pltpu.VMEM((dp // 2 + 1,) + tile, bf16),
            pltpu.SemaphoreType.DMA((6, dp // 2)),
        ]


def closing_kernel(
    dp, ctx,
    d_joined_ref, weight_ref, qkv_parts_ref, out_parts_ref, rows_ref, d_resid_ref, gain_ref, sums_two_ref, bias_ref,
    grad_ref, qkv_ref, out_ref, small_ref,
    total, sent, got, reduce_sem, qkv_pair, qkv_got, qkv_sem, out_pair, out_got, out_sem,
    sums, tiles, tiles_got, small_sem, mine, swap_out, swap_in, swap_sem,
):
    place = Place(dp)
    me, row = place.col, place.row
    greet_all(place, dp, ctx)
    size, width = rows_ref.shape
    lines = [
        LineReduce(place, qkv_parts_ref, qkv_pair, qkv_got, qkv_sem),
        LineReduce(place, out_parts_ref, out_pair, out_got, out_sem),
    ]
    for line in lines:
        line.start()
    reduce = CtxReduce(
        place, lambda col: dot_nt(rows_of(d_joined_ref, col, size), weight_ref[...]), total, sent, got, reduce_sem
    )
    reduce.start()
    for line in lines:
        line.add()
        line.send(place.lines - 1)
    reduce.relay()
    for far in range(place.lines - 2, 1, -1):
        for line in lines:
            line.send(far)

    sums[...] = jnp.zeros_like(sums)
    for j in range(CHUNKS):
        rows = reduce.chunk(j)
        scaled, inv_std = norm_stats(rows_ref[rows, :].astype(f32))
        grad, d_gain, d_shift = norm_backward(reduce.sum(j), scaled, inv_std, gain_ref[...])
        sums[0:1, :] += d_gain[None]
        sums[1:2, :] += d_shift[None]
        grad_ref[rows, :] = d_resid_ref[rows, :] + grad
    if place.lines > 2:
        for line in lines:
            line.send(1)

    part = width // dp
    tiles[...] = jnp.zeros_like(tiles)
    for i in range(dp):
        lanes = slice(i * part, (i + 1) * part)
        tiles[i, 0:2, :] = sums[:, lanes]
        tiles[i, 2:4, :] = sums_two_ref[:, lanes]
        tiles[i, 4:5, :] = bias_ref[i : i + 1, :]
    sends = [
        remote(tiles.at[(row + k) % dp], tiles_got.at[k], small_sem.at[0, k], small_sem.at[1, k], ((row + k) % dp, me))
        for k in range(1, dp)
    ]
    for copy in sends:
        copy.start()
    tile = tiles[row]
    for k in range(1, dp):
        sends[k - 1].wait()
        tile = tile + tiles_got[k]
    tiles_got[0] = tile
    small_ref[me] = tile
    spreads = [
        remote(tiles_got.at[0], small_ref.at[me], small_sem.at[2, k], small_sem.at[3, k], place.across(k))
        for k in range(1, ctx)
    ]
    for copy in spreads:
        copy.start()

    lines[0].collect(mine)
    depth = mine.shape[0] // ctx
    swap_out[...] = mine[...].astype(bf16)
    swaps = [
        remote(
            swap_out.at[pl.ds(pl.multiple_of(place.other(k) * depth, depth), depth), :], swap_in.at[me],
            swap_sem.at[0, k], swap_sem.at[1, k], place.across(k),
        )
        for k in range(1, ctx)
    ]
    for copy in swaps:
        copy.start()
    swap_in[me] = rows_of(swap_out, me, depth)
    lines[1].collect(out_ref)
    for k in range(1, ctx):
        part = swap_in.at[place.other(k)]
        remote(part, part, swap_sem.at[0, k], swap_sem.at[1, k], place.across(k)).wait_recv()
    low = head_lanes((depth, PAIR))
    for p in range(mine.shape[1] // (3 * PAIR)):
        for t in range(3):
            lanes = slice((3 * p + t) * PAIR, (3 * p + t + 1) * PAIR)
            for c in range(0, ctx, 2):
                a = swap_in[c, :, lanes].astype(f32)
                b = swap_in[c + 1, :, lanes].astype(f32)
                at = t * width + (2 * p * ctx + c) * HD
                qkv_ref[:, at : at + PAIR] = jnp.where(low, a, pltpu.roll(b, HD, 1))
                at = at + ctx * HD
                qkv_ref[:, at : at + PAIR] = jnp.where(low, pltpu.roll(a, HD, 1), b)
    for copy in swaps:
        copy.wait_send()
    for k in range(1, ctx):
        spreads[k - 1].wait_send()
        part = small_ref.at[place.other(k)]
        remote(part, part, small_sem.at[2, k], small_sem.at[3, k], place.across(k)).wait_recv()
    for line in lines:
        line.finish()
    reduce.finish()


def closing(dp, ctx, d_joined, weight, d_qkv, d_out, rows, d_resid, gain, sums_two, bias):
    size, width = rows.shape
    near = weight.shape[1]
    own, tall = width // dp, d_out.shape[0] // dp
    vmem = pl.BlockSpec(memory_space=pltpu.VMEM)
    reduce_scratch = CtxReduce.scratch(size, width)
    max_peers = max(dp, ctx)
    return pl.pallas_call(
        functools.partial(closing_kernel, dp, ctx),
        in_specs=[vmem] * 9,
        out_specs=[vmem] * 4,
        out_shape=[
            jax.ShapeDtypeStruct((size, width), f32),
            jax.ShapeDtypeStruct((own // ctx, 3 * width), f32),
            jax.ShapeDtypeStruct((tall, width), f32),
            jax.ShapeDtypeStruct((ctx, 8, own), f32),
        ],
        scratch_shapes=reduce_scratch
        + LineReduce.scratch(dp, (own, near))
        + LineReduce.scratch(dp, (tall, width))
        + [
            pltpu.VMEM((2, width), f32),
            pltpu.VMEM((dp, 8, own), f32),
            pltpu.VMEM((dp, 8, own), f32),
            pltpu.SemaphoreType.DMA((4, max_peers)),
            pltpu.VMEM((own, near), f32),
            pltpu.VMEM((own, near), bf16),
            pltpu.VMEM((ctx, own // ctx, near), bf16),
            pltpu.SemaphoreType.DMA((2, ctx)),
        ],
        compiler_params=pltpu.CompilerParams(
            collective_id=1, has_side_effects=True, vmem_limit_bytes=60 << 20
        ),
        cost_estimate=pl.CostEstimate(
            flops=2 * d_joined.size * width, transcendentals=0, bytes_accessed=200 << 20
        ),
    )(
        d_joined, weight, d_qkv.reshape(dp, own, near), d_out.reshape(dp, tall, width),
        rows, d_resid, gain.reshape(1, width), sums_two, bias,
    )


def turn(x, table_ref):
    return (
        x * table_ref[0]
        + pltpu.roll(x, PAIR - ROT // 2, 1) * table_ref[1]
        + pltpu.roll(x, ROT // 2, 1) * table_ref[2]
    )


def turn_back(x, table_ref):
    return (
        x * table_ref[0]
        - pltpu.roll(x, PAIR - ROT // 2, 1) * table_ref[1]
        - pltpu.roll(x, ROT // 2, 1) * table_ref[2]
    )


def head_lanes(shape):
    return lax.broadcasted_iota(jnp.int32, shape, 1) < HD


def span(full_len, step, at):
    return max(0, (at - DOC_MAX + 1) // step * step), at + step


def block_mask(start, at, step, low, high):
    keys = lax.broadcasted_iota(jnp.int32, (step, high - low), 1) + low
    rows = lax.broadcasted_iota(jnp.int32, (step, high - low), 0) + at
    return (keys >= start) & (keys <= rows)


def attend_kernel(step, joined_ref, bias_ref, table_ref, start_ref, out_ref, qkv_ref, lse_ref):
    full_len = joined_ref.shape[0]
    scale = 1.0 / math.sqrt(HD)
    for t in range(3):
        lanes = slice(t * PAIR, (t + 1) * PAIR)
        x = joined_ref[:, lanes] + bias_ref[:, lanes]
        if t < 2:
            x = turn(x, table_ref)
        qkv_ref[:, lanes] = x.astype(bf16)
    for at in range(0, full_len, step):
        low, high = span(full_len, step, at)
        allowed = block_mask(start_ref[at : at + step, :1], at, step, low, high)
        q = qkv_ref[at : at + step, :PAIR]
        k = qkv_ref[low:high, PAIR : 2 * PAIR]
        v = qkv_ref[low:high, 2 * PAIR :]
        total = jnp.zeros((step, PAIR), f32)
        logs = []
        for head in range(2):
            mine = head_lanes(q.shape) == (head == 0)
            s = dot_nt(jnp.where(mine, q, jnp.zeros_like(q)), k) * scale
            s = jnp.where(allowed, s, masked_value)
            top = jnp.max(s, axis=1, keepdims=True)
            e = jnp.exp(s - top)
            norm = jnp.sum(e, axis=1, keepdims=True)
            probs = (e * (1.0 / norm)).astype(bf16)
            vm = jnp.where(head_lanes(v.shape) == (head == 0), v, jnp.zeros_like(v))
            total = total + dot(probs, vm)
            logs.append(top + jnp.log(norm))
        out_ref[at : at + step, :] = total.astype(bf16)
        lse_ref[at : at + step, :] = jnp.where(head_lanes((step, PAIR)), logs[0], logs[1])


def attend_back_kernel(
    step, qkv_ref, grad_ref, lse_ref, table_ref, start_ref, out_ref, sum_ref, dk_ref, dv_ref
):
    full_len = qkv_ref.shape[0]
    scale = 1.0 / math.sqrt(HD)
    dk_ref[...] = jnp.zeros_like(dk_ref)
    dv_ref[...] = jnp.zeros_like(dv_ref)
    total = jnp.zeros((1, PAIR), f32)
    for at in range(0, full_len, step):
        low, high = span(full_len, step, at)
        rows = slice(at, at + step)
        keys = slice(low, high)
        allowed = block_mask(start_ref[rows, :1], at, step, low, high)
        q = qkv_ref[rows, :PAIR]
        k = qkv_ref[keys, PAIR : 2 * PAIR]
        v = qkv_ref[keys, 2 * PAIR :]
        g = grad_ref[rows, :]
        dq = jnp.zeros((step, PAIR), f32)
        dk = jnp.zeros((high - low, PAIR), f32)
        dv = jnp.zeros((high - low, PAIR), f32)
        for head in range(2):
            mine = head_lanes(q.shape) == (head == 0)
            qm = jnp.where(mine, q, jnp.zeros_like(q))
            gm = jnp.where(mine, g, jnp.zeros_like(g))
            km = jnp.where(head_lanes(k.shape) == (head == 0), k, jnp.zeros_like(k))
            s = dot_nt(qm, k) * scale
            probs = jnp.where(
                allowed, jnp.exp(s - lse_ref[rows, head * HD : head * HD + 1]), 0.0
            )
            dp = dot_nt(gm, v)
            mean = jnp.sum(dp * probs, axis=1, keepdims=True)
            ds = (probs * (dp - mean)).astype(bf16)
            dq = dq + dot(ds, km)
            dk = dk + dot_tn(ds, qm)
            dv = dv + dot_tn(probs.astype(bf16), gm)
        dk_ref[keys, :] += dk
        dv_ref[keys, :] += dv
        dq = turn_back(dq * scale, table_ref.at[:, rows, :]).astype(bf16)
        out_ref[rows, :PAIR] = dq
        total = total + jnp.sum(dq.astype(f32), axis=0, keepdims=True)
    sum_ref[:, :PAIR] = total
    dk = turn_back(dk_ref[...] * scale, table_ref).astype(bf16)
    out_ref[:, PAIR : 2 * PAIR] = dk
    sum_ref[:, PAIR : 2 * PAIR] = jnp.sum(dk.astype(f32), axis=0, keepdims=True)
    dv = dv_ref[...].astype(bf16)
    out_ref[:, 2 * PAIR :] = dv
    sum_ref[:, 2 * PAIR :] = jnp.sum(dv.astype(f32), axis=0, keepdims=True)


def whole(shape):
    return pl.BlockSpec(shape, lambda p: (0,) * len(shape))


def attend_step(full_len):
    return min(256, full_len)


def attend(joined, bias, table, start):
    full_len, width = joined.shape
    pairs = width // (3 * PAIR)
    step = attend_step(full_len)
    seen = sum(span(full_len, step, at)[1] - span(full_len, step, at)[0] for at in range(0, full_len, step)) * step
    wide = pl.BlockSpec((full_len, 3 * PAIR), lambda p: (0, p))
    thin = pl.BlockSpec((full_len, PAIR), lambda p: (0, p))
    return pl.pallas_call(
        functools.partial(attend_kernel, step),
        grid=(pairs,),
        in_specs=[
            wide,
            pl.BlockSpec((1, 3 * PAIR), lambda p: (0, p)),
            whole(table.shape),
            whole(start.shape),
        ],
        out_specs=[thin, wide, thin],
        out_shape=[
            jax.ShapeDtypeStruct((full_len, pairs * PAIR), bf16),
            jax.ShapeDtypeStruct((full_len, width), bf16),
            jax.ShapeDtypeStruct((full_len, pairs * PAIR), f32),
        ],
        compiler_params=pltpu.CompilerParams(vmem_limit_bytes=40 << 20),
        cost_estimate=pl.CostEstimate(
            flops=pairs * seen * PAIR * 8, transcendentals=pairs * seen * 2, bytes_accessed=full_len * width * 8
        ),
    )(joined, bias, table, start)


def attend_back(qkv, grad, lse, table, start):
    full_len, width = qkv.shape
    pairs = width // (3 * PAIR)
    step = attend_step(full_len)
    seen = sum(span(full_len, step, at)[1] - span(full_len, step, at)[0] for at in range(0, full_len, step)) * step
    wide = pl.BlockSpec((full_len, 3 * PAIR), lambda p: (0, p))
    thin = pl.BlockSpec((full_len, PAIR), lambda p: (0, p))
    return pl.pallas_call(
        functools.partial(attend_back_kernel, step),
        grid=(pairs,),
        in_specs=[wide, thin, thin, whole(table.shape), whole(start.shape)],
        out_specs=[wide, pl.BlockSpec((1, 3 * PAIR), lambda p: (0, p))],
        out_shape=[
            jax.ShapeDtypeStruct((full_len, width), bf16),
            jax.ShapeDtypeStruct((1, width), f32),
        ],
        scratch_shapes=[pltpu.VMEM((full_len, PAIR), f32), pltpu.VMEM((full_len, PAIR), f32)],
        compiler_params=pltpu.CompilerParams(vmem_limit_bytes=40 << 20),
        cost_estimate=pl.CostEstimate(
            flops=pairs * seen * PAIR * 20, transcendentals=pairs * seen * 2, bytes_accessed=full_len * width * 8
        ),
    )(qkv, grad, lse, table, start)


def rotary_table(full_len):
    half = ROT // 2
    inverse = 10000.0 ** (-2.0 * np.arange(half) / ROT)
    angles = np.arange(full_len)[:, None] * inverse[None, :]
    table = np.zeros((3, full_len, HD), np.float32)
    table[0, :, :half] = table[0, :, half:ROT] = np.cos(angles)
    table[0, :, ROT:] = 1.0
    table[1, :, :half] = -np.sin(angles)
    table[2, :, half:ROT] = np.sin(angles)
    return jnp.asarray(np.concatenate([table, table], axis=2))


def shards(
    dp,
    ctx,
    inputs,
    segments,
    ln1_gain,
    ln1_bias,
    qkv_weight,
    qkv_bias,
    out_weight,
    ln2_gain,
    ln2_bias,
    gate_weight,
    up_weight,
    down_weight,
    cotangent,
):
    local_len, width = inputs.shape[1], inputs.shape[2]
    full_len = segments.shape[1]
    heads = width // HD
    near = heads // ctx
    pairs = near // 2
    me = lax.axis_index("ctx")
    own = me * local_len

    part = ln1_gain.shape[0]
    small = jnp.concatenate([ln1_gain, ln1_bias, ln2_gain, ln2_bias, qkv_bias]).astype(f32)
    count = small.shape[0]
    small = jnp.pad(small, (0, 1024 - count)).reshape(8, 128)
    rows_here = qkv_weight.shape[0]
    rows, grad_rows = inputs[0], cotangent[0]
    fused = ctx == 4 and dp % 2 == 0 and part == HD
    if fused:
        small, params, joined_weight, out_full, normed_one, joined, grad_wide = opening(
            dp, ctx, small, qkv_weight, out_weight, rows, grad_rows
        )
        gain_one, shift_one, gain_two, shift_two = params
        gate_weight, up_weight, _ = lax.optimization_barrier((gate_weight, up_weight, normed_one))
        small = small.reshape(dp * ctx, 1024)[:, :count]
    else:
        small = lax.all_gather(small[None, :], ("dp", "ctx"), axis=0, tiled=True)
        blocks = qkv_weight.reshape(rows_here, 3, pairs, 2, ctx, HD).transpose(4, 0, 2, 1, 3, 5)
        blocks = exchange_ctx(blocks.reshape(ctx, rows_here, near * 3 * HD), ctx)
        joined_weight = lax.all_gather(
            blocks.reshape(ctx * rows_here, near * 3 * HD), "dp", axis=0, tiled=True
        )
        out_full = lax.all_gather(out_weight, ("dp", "ctx"), axis=0, tiled=True)
        out_full = out_full.reshape(near, ctx, HD, width)
        out_full = lax.dynamic_index_in_dim(out_full, me, 1, keepdims=False)
        out_full = out_full.reshape(near * HD, width)
        small = small.reshape(dp * ctx, 1024)[:, :count]
        gain_one, shift_one, gain_two, shift_two = [
            small[:, i * part : (i + 1) * part].reshape(width) for i in range(4)
        ]
        scaled_wide, _ = norm_stats(gather_ctx(rows, ctx).astype(f32))
        normed_one = (scaled_wide * gain_one + shift_one).astype(bf16)
        grad_wide = gather_ctx(grad_rows, ctx)
    bias = small[:, 4 * part :].reshape(3, pairs, 2, ctx, HD)
    bias = lax.dynamic_index_in_dim(bias, me, 3, keepdims=False)
    bias = bias.transpose(1, 0, 2, 3).reshape(1, near * 3 * HD)
    gate_full = lax.all_gather(gate_weight, "dp", axis=0, tiled=True)
    up_full = lax.all_gather(up_weight, "dp", axis=0, tiled=True)

    segment = segments[0]
    start = jnp.sum((segment[None, :] < segment[:, None]).astype(jnp.int32), axis=1)
    start = jnp.broadcast_to(start[:, None], (full_len, 128))
    table = rotary_table(full_len)
    if not fused:
        joined = dot(normed_one, joined_weight)
    attended, qkv, lse = attend(joined, bias, table, start)
    if fused:
        resid, normed_wide, down_full = mix(
            dp, ctx, attended, out_full, rows, gain_two, shift_two, down_weight
        )
    else:
        down_full = lax.all_gather(down_weight, "dp", axis=1, tiled=True)
        resid = rows.astype(f32) + scatter_ctx(dot(attended, out_full), ctx)
        scaled_two, inv_two = norm_stats(resid)
        normed_wide = gather_ctx((scaled_two * gain_two + shift_two).astype(bf16), ctx)

    gate = dot(normed_wide, gate_full)
    upward = dot(normed_wide, up_full)
    sigma = jax.nn.sigmoid(gate)
    swish = gate * sigma
    inner = (swish * upward).astype(bf16)
    d_down = dot_tn(inner, grad_wide).astype(bf16)
    grad_wide, d_down = lax.optimization_barrier((grad_wide, d_down))
    d_down = lax.psum_scatter(d_down, "dp", scatter_dimension=1, tiled=True).astype(f32)
    d_inner = dot_nt(grad_wide, down_full)
    d_gate = (d_inner * upward * sigma * (1.0 + gate * (1.0 - sigma))).astype(bf16)
    d_upward = (d_inner * swish).astype(bf16)
    d_gate_weight = dot_tn(normed_wide, d_gate).astype(bf16)
    d_up_weight = dot_tn(normed_wide, d_upward).astype(bf16)
    branch = dot(inner, down_full)
    d_gate_ready, d_gate_weight = lax.optimization_barrier((d_gate, d_gate_weight))
    d_gate_weight = lax.psum_scatter(d_gate_weight, "dp", scatter_dimension=0, tiled=True).astype(f32)
    if fused:
        d_resid, sums_two, d_proj = mix_back(
            dp, ctx, d_gate_ready, d_upward, gate_full, up_full, resid, grad_rows, gain_two
        )
    else:
        d_normed_two = scatter_ctx(dot_nt(d_gate, gate_full) + dot_nt(d_upward, up_full), ctx)
        grad, d_gain_two, d_shift_two = norm_backward(d_normed_two, scaled_two, inv_two, gain_two)
        d_resid = grad_rows.astype(f32) + grad
        d_proj = gather_ctx(d_resid.astype(bf16), ctx)
    branch, _ = lax.optimization_barrier((branch, d_proj))
    output = (resid + scatter_ctx(branch, ctx)).astype(bf16)
    d_up_weight = lax.psum_scatter(d_up_weight, "dp", scatter_dimension=0, tiled=True).astype(f32)

    d_attended = dot_nt(d_proj, out_full).astype(bf16)
    d_out_weight = dot_tn(attended, d_proj).astype(bf16)
    d_joined, d_bias = attend_back(qkv, d_attended, lse, table, start)
    d_joined_weight = dot_tn(normed_one, d_joined).astype(bf16)
    d_bias = d_bias.reshape(pairs, 3, 2, HD).transpose(1, 0, 2, 3)
    if fused:
        d_bias = jnp.pad(d_bias.reshape(dp, -1), ((0, 0), (0, width // dp - near * 3 * HD // dp)))
        grad_input, d_joined_weight, d_out_weight, small = closing(
            dp, ctx, d_joined, joined_weight, d_joined_weight, d_out_weight, rows, d_resid, gain_one, sums_two, d_bias
        )
        vectors = lax.dynamic_slice_in_dim(jnp.sum(small[:, :4], axis=0), me * part, part, 1)
        d_gain_one, d_shift_one, d_gain_two, d_shift_two = vectors
        d_bias = small[:, 4, : near * 3 * HD // dp].reshape(ctx, -1, HD).transpose(1, 0, 2)
        d_bias = lax.dynamic_index_in_dim(d_bias.reshape(ctx, -1), me, 0, keepdims=False)
    else:
        at_me = lax.broadcasted_iota(jnp.int32, (1, ctx, 1, 1), 1) == me
        d_out_weight = jnp.where(at_me, d_out_weight.reshape(near, 1, HD, width), jnp.zeros((), bf16))
        d_out_weight = lax.psum_scatter(
            d_out_weight.reshape(width, width), ("dp", "ctx"), scatter_dimension=0, tiled=True
        ).astype(f32)
        d_normed_one = scatter_ctx(dot_nt(d_joined, joined_weight), ctx)
        scaled_one, inv_one = norm_stats(rows.astype(f32))
        grad, d_gain_one, d_shift_one = norm_backward(d_normed_one, scaled_one, inv_one, gain_one)
        grad_input = d_resid + grad
        d_joined_weight = lax.psum_scatter(d_joined_weight, "dp", scatter_dimension=0, tiled=True)
        blocks = exchange_ctx(d_joined_weight.reshape(ctx, rows_here, near * 3 * HD), ctx)
        blocks = blocks.reshape(ctx, rows_here, pairs, 3, 2, HD).transpose(1, 3, 2, 4, 0, 5)
        d_joined_weight = blocks.reshape(rows_here, 3 * width).astype(f32)
        at_me = (lax.broadcasted_iota(jnp.int32, (1, 1, 1, ctx, 1), 3) == me).astype(f32)
        d_bias = (d_bias[:, :, :, None, :] * at_me).reshape(dp * ctx, -1)
        small = jnp.concatenate(
            [t.reshape(dp * ctx, part) for t in (d_gain_one, d_shift_one, d_gain_two, d_shift_two)]
            + [d_bias],
            axis=1,
        )
        small = lax.psum_scatter(small, ("dp", "ctx"), scatter_dimension=0, tiled=True)[0]
        d_gain_one, d_shift_one, d_gain_two, d_shift_two = [
            small[i * part : (i + 1) * part] for i in range(4)
        ]
        d_bias = small[4 * part :]
    return (
        output[None],
        grad_input[None],
        d_gain_one,
        d_shift_one,
        d_joined_weight,
        d_bias,
        d_out_weight,
        d_gain_two,
        d_shift_two,
        d_gate_weight,
        d_up_weight,
        d_down,
    )


def solution(mesh):
    every = ("dp", "ctx")
    return jax.shard_map(
        functools.partial(shards, mesh.shape["dp"], mesh.shape["ctx"]),
        mesh=mesh,
        in_specs=(
            P("dp", "ctx", None),
            P("dp", None),
            P(every),
            P(every),
            P(every, None),
            P(every),
            P(every, None),
            P(every),
            P(every),
            P("dp", "ctx"),
            P("dp", "ctx"),
            P("ctx", "dp"),
            P("dp", "ctx", None),
        ),
        out_specs=(
            P("dp", "ctx", None),
            P("dp", "ctx", None),
            P(every),
            P(every),
            P(every, None),
            P(every),
            P(every, None),
            P(every),
            P(every),
            P("dp", "ctx"),
            P("dp", "ctx"),
            P("ctx", "dp"),
        ),
        check_vma=False,
    )
```

```python
import functools
import math

import jax
import jax.numpy as jnp
import numpy as np
from jax import lax
from jax.experimental import pallas as pl
from jax.experimental.pallas import tpu as pltpu
from jax.sharding import PartitionSpec as P

HD = 64
ROT = 16
DOC_MAX = 512
PAIR = 2 * HD

norm_eps = 1e-05
masked_value = -1e30
f32 = jnp.float32
bf16 = jnp.bfloat16


def dot(a, b):
    return jnp.dot(a, b, preferred_element_type=f32)


def dot_nt(a, b):
    return lax.dot_general(a, b, (((1,), (1,)), ((), ())), preferred_element_type=f32)


def dot_tn(a, b):
    return lax.dot_general(a, b, (((0,), (0,)), ((), ())), preferred_element_type=f32)


def norm_stats(rows):
    row_mean = jnp.mean(rows, axis=-1, keepdims=True)
    centered = rows - row_mean
    variance = jnp.mean(centered * centered, axis=-1, keepdims=True)
    inv_std = lax.rsqrt(variance + norm_eps)
    return centered * inv_std, inv_std


def norm_backward(grad_normed, scaled, inv_std, gain):
    grad_gain = jnp.sum(grad_normed * scaled, axis=0)
    grad_shift = jnp.sum(grad_normed, axis=0)
    inner_grad = grad_normed * gain
    grad_rows = inv_std * (
        inner_grad
        - jnp.mean(inner_grad, axis=-1, keepdims=True)
        - scaled * jnp.mean(inner_grad * scaled, axis=-1, keepdims=True)
    )
    return grad_rows, grad_gain, grad_shift


def partner(n, k):
    return [(c, c ^ k) for c in range(n)]


def hop(x, n, k):
    return lax.ppermute(x, "ctx", partner(n, k))


def gather_relative(block, n):
    if n != 4:
        return [block] + [hop(block, n, k) for k in range(1, n)]
    half = block.shape[0] // 2
    one = hop(block, n, 1)
    two = hop(block, n, 2)
    low = hop(one[:half], n, 2)
    high = hop(two[half:], n, 1)
    return [block, one, two, jnp.concatenate([low, high], axis=0)]


def gather_ctx(block, n):
    me = lax.axis_index("ctx")
    size = block.shape[0]
    parts = gather_relative(block, n)
    full = jnp.zeros((n * size,) + block.shape[1:], block.dtype)
    for k, part in enumerate(parts):
        full = lax.dynamic_update_slice_in_dim(full, part, (me ^ k) * size, 0)
    return full


def scatter_ctx(partial, n, meanwhile=None):
    me = lax.axis_index("ctx")
    size = partial.shape[0] // n

    def block(k):
        return lax.dynamic_slice_in_dim(partial, (me ^ k) * size, size, 0)

    if n != 4:
        total = block(0).astype(f32)
        for k in range(1, n):
            total = total + hop(block(k).astype(bf16), n, k).astype(f32)
        return total
    half = size // 2
    far = block(3).astype(bf16)
    low = hop(far[:half], n, 1).astype(f32)
    high = hop(far[half:], n, 2).astype(f32)
    if meanwhile is not None:
        partial, _ = lax.optimization_barrier((partial, meanwhile))
    one = block(1).astype(f32)
    two = block(2).astype(f32)
    to_one = jnp.concatenate([one[:half], one[half:] + high], axis=0).astype(bf16)
    to_two = jnp.concatenate([two[:half] + low, two[half:]], axis=0).astype(bf16)
    return block(0).astype(f32) + hop(to_one, n, 1).astype(f32) + hop(to_two, n, 2).astype(f32)


def exchange_ctx(blocks, n):
    me = lax.axis_index("ctx")
    got = lax.dynamic_update_slice_in_dim(
        jnp.zeros_like(blocks), lax.dynamic_slice_in_dim(blocks, me, 1, 0), me, 0
    )
    for k in range(1, n):
        sent = lax.dynamic_slice_in_dim(blocks, me ^ k, 1, 0)
        got = lax.dynamic_update_slice_in_dim(got, hop(sent, n, k), me ^ k, 0)
    return got


MESH = pl.DeviceIdType.MESH
ANY = pl.BlockSpec(memory_space=pl.ANY)


class Place:
    def __init__(self, dp):
        self.row = lax.axis_index("dp")
        self.col = lax.axis_index("ctx")
        self.lines = dp // 2
        self.line = self.row // 2
        self.core = self.row % 2
        self.twin = (self.row + 1 - 2 * self.core, self.col)

    def other(self, k):
        col, bit = self.col, 1
        while bit <= k:
            if k & bit:
                col = col + bit * (1 - 2 * ((self.col // bit) % 2))
            bit *= 2
        return col

    def across(self, k):
        return (self.row, self.other(k))

    def above(self):
        return (self.row + 2, self.col)

    def below(self):
        return (self.row - 2, self.col)


def greet(place, ctx):
    barrier = pltpu.get_barrier_semaphore()
    for k in range(1, ctx):
        pl.semaphore_signal(barrier, 1, device_id=place.across(k), device_id_type=MESH)
    pl.semaphore_wait(barrier, ctx - 1)


def remote(src, dst, send, recv, device):
    return pltpu.make_async_remote_copy(
        src_ref=src, dst_ref=dst, send_sem=send, recv_sem=recv, device_id=device, device_id_type=MESH
    )


class LineGather:
    def __init__(self, place, shard, sems):
        self.place, self.shard, self.sems = place, shard, sems

    def row(self, line):
        return line * 2 + self.place.core

    def up(self, hop):
        part = self.shard(self.row(self.place.line - hop + 1))
        return remote(part, part, self.sems.at[0, hop], self.sems.at[1, hop], self.place.above())

    def down(self, hop):
        part = self.shard(self.row(self.place.line + hop - 1))
        return remote(part, part, self.sems.at[2, hop], self.sems.at[3, hop], self.place.below())

    def over(self, at, row):
        part = self.shard(row)
        return remote(part, part, self.sems.at[4, at], self.sems.at[5, at], self.place.twin)

    def sends_up(self, hop):
        return (self.place.line - hop + 1 >= 0) & (self.place.line < self.place.lines - 1)

    def sends_down(self, hop):
        return (self.place.line + hop - 1 < self.place.lines) & (self.place.line > 0)

    def send(self, hop):
        place = self.place
        pl.when(self.sends_up(hop))(lambda: self.up(hop).start())
        pl.when(self.sends_down(hop))(lambda: self.down(hop).start())
        if hop == 1:
            self.over(0, place.row).start()

    def receive(self, hop):
        place = self.place

        @pl.when(place.line - hop >= 0)
        def _():
            part = self.shard(self.row(place.line - hop))
            remote(part, part, self.sems.at[0, hop], self.sems.at[1, hop], place.twin).wait_recv()
            self.over(hop, self.row(place.line - hop)).start()

        @pl.when(place.line + hop < place.lines)
        def _():
            part = self.shard(self.row(place.line + hop))
            remote(part, part, self.sems.at[2, hop], self.sems.at[3, hop], place.twin).wait_recv()
            self.over(place.lines - 1 + hop, self.row(place.line + hop)).start()

    def came_over(self, at, row):
        part = self.shard(row)
        remote(part, part, self.sems.at[4, at], self.sems.at[5, at], self.place.twin).wait_recv()

    def settle(self, hop, use=None):
        place = self.place
        other = 1 - 2 * place.core
        if hop == 0:
            self.came_over(0, place.row + other)
            if use:
                use(place.line)
            return
        for at, line, there in (
            (hop, place.line - hop, place.line - hop >= 0),
            (place.lines - 1 + hop, place.line + hop, place.line + hop < place.lines),
        ):

            @pl.when(there)
            def _():
                self.came_over(at, self.row(line) + other)
                if use:
                    use(line)

    def finish(self):
        place = self.place
        self.over(0, place.row).wait_send()
        for hop in range(1, place.lines):
            pl.when(self.sends_up(hop))(lambda: self.up(hop).wait_send())
            pl.when(self.sends_down(hop))(lambda: self.down(hop).wait_send())
            for at, line, there in (
                (hop, place.line - hop, place.line - hop >= 0),
                (place.lines - 1 + hop, place.line + hop, place.line + hop < place.lines),
            ):
                pl.when(there)(lambda: self.over(at, self.row(line)).wait_send())

    @staticmethod
    def scratch(dp):
        return pltpu.SemaphoreType.DMA((6, dp))


class CtxGather:
    def __init__(self, place, block, full, size, sems):
        self.place, self.block, self.full, self.size, self.sems = place, block, full, size, sems

    def rows(self, col, start=0, size=None):
        size = self.size if size is None else size
        return self.full.at[pl.ds(pl.multiple_of(col * self.size + start, size), size), :]

    def copies(self):
        place, half = self.place, self.size // 2
        me = place.col
        return [
            remote(self.block, self.rows(me), self.sems.at[0, 0], self.sems.at[1, 0], place.across(1)),
            remote(self.block, self.rows(me), self.sems.at[0, 1], self.sems.at[1, 1], place.across(2)),
            remote(
                self.rows(place.other(1), 0, half), self.rows(place.other(1), 0, half),
                self.sems.at[0, 2], self.sems.at[1, 2], place.across(2),
            ),
            remote(
                self.rows(place.other(2), half, half), self.rows(place.other(2), half, half),
                self.sems.at[0, 3], self.sems.at[1, 3], place.across(1),
            ),
        ]

    def arrivals(self):
        place, half = self.place, self.size // 2
        me = place.col
        parts = [self.rows(place.other(1)), self.rows(place.other(2)), self.rows(place.other(3), 0, half), self.rows(place.other(3), half, half)]
        return [
            remote(part, part, self.sems.at[0, i], self.sems.at[1, i], place.across(1))
            for i, part in enumerate(parts)
        ]

    def first(self):
        copies = self.copies()
        copies[0].start()
        copies[1].start()

    def second(self):
        copies, arrivals = self.copies(), self.arrivals()
        arrivals[0].wait_recv()
        copies[2].start()
        arrivals[1].wait_recv()
        copies[3].start()

    def finish(self):
        copies, arrivals = self.copies(), self.arrivals()
        arrivals[2].wait_recv()
        arrivals[3].wait_recv()
        for copy in copies:
            copy.wait_send()

    @staticmethod
    def scratch():
        return pltpu.SemaphoreType.DMA((2, 4))


def greet_all(place, dp, ctx, signal=True, wait=True):
    barrier = pltpu.get_barrier_semaphore()
    if signal:
        for k in range(1, ctx):
            pl.semaphore_signal(barrier, 1, device_id=place.across(k), device_id_type=MESH)
        for k in range(1, dp):
            pl.semaphore_signal(barrier, 1, device_id=((place.row + k) % dp, place.col), device_id_type=MESH)
    if wait:
        pl.semaphore_wait(barrier, ctx + dp - 2)


PARTS = 2


def opening_kernel(
    dp, ctx,
    gain_one, shift_one, gain_two, shift_two, bias, qkv_hbm, out_weight_ref, rows_ref, cot_ref,
    small_all, params_ref, weight_ref, out_all, normed_ref, joined_ref, cot_all,
    small_ref, qkv_ref, blocks, rows_all, local_sem, swap_sem, small_sem, line_joined, line_out, rows_sem, cot_sem,
):
    place = Place(dp)
    me, row = place.col, place.row
    depth = qkv_ref.shape[0]
    length, width = rows_ref.shape
    rows_out = out_weight_ref.shape[0]
    tall = ctx * depth

    qkv_copy = pltpu.make_async_copy(qkv_hbm, qkv_ref, local_sem.at[4])
    qkv_copy.start()
    greet_all(place, dp, ctx, wait=False)
    small_ref[...] = jnp.zeros_like(small_ref)
    for i, vector in enumerate((gain_one, shift_one, gain_two, shift_two)):
        small_ref[i // 2 : i // 2 + 1, i % 2 * HD : (i % 2 + 1) * HD] = vector[...].astype(f32)
    for i in range(bias.shape[1] // HD):
        small_ref[2 + i // 2 : 3 + i // 2, i % 2 * HD : (i % 2 + 1) * HD] = bias[
            :, i * HD : (i + 1) * HD
        ].astype(f32)
    small_all[row, me] = small_ref[...]
    qkv_copy.wait()

    low = head_lanes((depth, PAIR))
    for p in range(width // HD // ctx // 2):
        for t in range(3):
            lanes = slice((3 * p + t) * PAIR, (3 * p + t + 1) * PAIR)
            for c in range(0, ctx, 2):
                at = t * width + (2 * p * ctx + c) * HD
                a = qkv_ref[:, at : at + PAIR].astype(f32)
                at = at + ctx * HD
                b = qkv_ref[:, at : at + PAIR].astype(f32)
                blocks[c, :, lanes] = jnp.where(low, a, pltpu.roll(b, HD, 1)).astype(bf16)
                blocks[c + 1, :, lanes] = jnp.where(low, pltpu.roll(a, HD, 1), b).astype(bf16)
    greet_all(place, dp, ctx, signal=False)

    def weight_rows(row, col):
        return weight_ref.at[pl.ds(pl.multiple_of((row * ctx + col) * depth, depth), depth), :]

    def out_shard(row):
        return out_all.at[pl.ds(pl.multiple_of(row * rows_out, rows_out), rows_out), :]

    def block(ref, col):
        return ref.at[pl.ds(pl.multiple_of(col * length, length), length), :]

    part_cols = weight_ref.shape[1] // PARTS

    def weight_part(i, row):
        return weight_ref.at[
            pl.ds(pl.multiple_of(row * tall, tall), tall), pl.ds(i * part_cols, part_cols)
        ]

    local = [
        pltpu.make_async_copy(blocks.at[me], weight_rows(row, me), local_sem.at[0]),
        pltpu.make_async_copy(out_weight_ref, out_shard(row), local_sem.at[1]),
        pltpu.make_async_copy(rows_ref, block(rows_all, me), local_sem.at[2]),
        pltpu.make_async_copy(cot_ref, block(cot_all, me), local_sem.at[3]),
    ]
    swaps = [
        remote(small_ref, small_all.at[row, me], swap_sem.at[0, k], swap_sem.at[1, k], place.across(k))
        for k in range(1, ctx)
    ] + [
        remote(
            blocks.at[place.other(k)], weight_rows(row, me), swap_sem.at[2, k], swap_sem.at[3, k], place.across(k)
        )
        for k in range(1, ctx)
    ]
    for copy in swaps:
        copy.start()
    for copy in local:
        copy.start()
    rows_gather = CtxGather(place, rows_ref, rows_all, length, rows_sem)
    cot_gather = CtxGather(place, cot_ref, cot_all, length, cot_sem)
    out_line = LineGather(place, out_shard, line_out)
    lines = [
        LineGather(place, functools.partial(weight_part, i), line_joined.at[i]) for i in range(PARTS)
    ] + [out_line]
    local[1].wait()
    out_line.send(1)
    rows_gather.first()
    for k in range(1, ctx):
        remote(
            small_ref, small_all.at[row, place.other(k)], swap_sem.at[0, k], swap_sem.at[1, k], place.across(k)
        ).wait_recv()
    small_sends = [
        remote(
            small_all.at[row], small_all.at[row], small_sem.at[0, k], small_sem.at[1, k], ((row + k) % dp, me)
        )
        for k in range(1, dp)
    ]
    for copy in small_sends:
        copy.start()
    local[0].wait()
    for k in range(1, ctx):
        part = weight_rows(row, place.other(k))
        remote(part, part, swap_sem.at[2, k], swap_sem.at[3, k], place.across(k)).wait_recv()
    for line in lines[:PARTS]:
        line.send(1)

    for k in range(1, dp):
        part = small_all.at[(row + dp - k) % dp]
        remote(part, part, small_sem.at[0, k], small_sem.at[1, k], place.twin).wait_recv()
    low = head_lanes((1, PAIR))
    for i in range(dp * ctx // 2):
        lanes = slice(i * PAIR, (i + 1) * PAIR)
        a = small_all[2 * i // ctx, 2 * i % ctx]
        b = small_all[(2 * i + 1) // ctx, (2 * i + 1) % ctx]
        for r in range(2):
            ar, br = a[r : r + 1, :], b[r : r + 1, :]
            params_ref[2 * r : 2 * r + 1, lanes] = jnp.where(low, ar, pltpu.roll(br, HD, 1))
            params_ref[2 * r + 1 : 2 * r + 2, lanes] = jnp.where(low, pltpu.roll(ar, HD, 1), br)

    def normalize(col):
        step = 64

        @pl.loop(0, length // step)
        def _(i):
            rows = pl.ds(pl.multiple_of(col * length + i * step, step), step)
            scaled, _ = norm_stats(rows_all[rows, :].astype(f32))
            normed_ref[rows, :] = (scaled * params_ref[0:1, :] + params_ref[1:2, :]).astype(bf16)

    def multiply(i, line):
        at = pl.multiple_of(line * (2 * tall), 2 * tall)
        cols = slice(i * part_cols, (i + 1) * part_cols)

        @pl.loop(0, ctx)
        def _(b):
            rows = pl.ds(pl.multiple_of(b * length, length), length)
            joined_ref[rows, cols] += dot(
                normed_ref[rows, pl.ds(at, 2 * tall)], weight_ref[pl.ds(at, 2 * tall), cols]
            )

    def forward(hop):
        for line in lines:
            line.receive(hop)
            if hop < place.lines - 1:
                line.send(hop + 1)

    def absorb(hop):
        for i in range(PARTS):
            lines[i].settle(hop, functools.partial(multiply, i))

    joined_ref[...] = jnp.zeros_like(joined_ref)
    local[2].wait()
    normalize(me)
    rows_gather.second()
    cot_gather.first()
    for hop in range(1, place.lines):
        forward(hop)
        if hop == 1:
            for col in (place.other(1), place.other(2)):
                normalize(col)
            rows_gather.finish()
            normalize(place.other(3))
        if hop == min(2, place.lines - 1):
            cot_gather.second()
        absorb(hop - 1)
    absorb(place.lines - 1)
    for hop in range(place.lines):
        out_line.settle(hop)
    for line in lines:
        line.finish()
    cot_gather.finish()
    for copy in swaps + small_sends:
        copy.wait_send()
    local[3].wait()


def opening(dp, ctx, vectors, qkv_weight, out_weight, rows, cot):
    depth, width = qkv_weight.shape[0], rows.shape[1]
    length = rows.shape[0]
    near = 3 * width // ctx
    vmem = pl.BlockSpec(memory_space=pltpu.VMEM)
    return pl.pallas_call(
        functools.partial(opening_kernel, dp, ctx),
        in_specs=[vmem] * len(vectors) + [ANY] * 4,
        out_specs=[vmem, vmem, vmem, ANY, vmem, vmem, ANY],
        out_shape=[
            jax.ShapeDtypeStruct((dp, ctx, 8, PAIR), f32),
            jax.ShapeDtypeStruct((4, width), f32),
            jax.ShapeDtypeStruct((dp * ctx * depth, near), bf16),
            jax.ShapeDtypeStruct((dp * out_weight.shape[0], width), bf16),
            jax.ShapeDtypeStruct((ctx * length, width), bf16),
            jax.ShapeDtypeStruct((ctx * length, near), f32),
            jax.ShapeDtypeStruct((ctx * length, width), bf16),
        ],
        scratch_shapes=[
            pltpu.VMEM((8, PAIR), f32),
            pltpu.VMEM((depth, 3 * width), bf16),
            pltpu.VMEM((ctx, depth, near), bf16),
            pltpu.VMEM((ctx * length, width), bf16),
            pltpu.SemaphoreType.DMA((5,)),
            pltpu.SemaphoreType.DMA((4, ctx)),
            pltpu.SemaphoreType.DMA((2, dp)),
            pltpu.SemaphoreType.DMA((PARTS, 6, dp)),
            LineGather.scratch(dp),
            CtxGather.scratch(),
            CtxGather.scratch(),
        ],
        compiler_params=pltpu.CompilerParams(
            collective_id=0, has_side_effects=True, vmem_limit_bytes=40 << 20
        ),
        cost_estimate=pl.CostEstimate(
            flops=2 * ctx * length * width * near, transcendentals=0, bytes_accessed=200 << 20
        ),
    )(*vectors, qkv_weight, out_weight, rows, cot)


CHUNKS = 4


class CtxReduce:
    def __init__(self, place, block, total, sent, got, sems):
        self.place, self.block, self.total = place, block, total
        self.sent, self.got, self.sems = sent, got, sems
        self.size = total.shape[1] // CHUNKS

    def chunk(self, j):
        return pl.ds(j * self.size, self.size)

    def copy(self, kind, j):
        way = kind if kind else 1 + j % 2
        return remote(
            self.sent.at[kind, self.chunk(j)], self.got.at[kind, self.chunk(j)],
            self.sems.at[0, kind, j], self.sems.at[1, kind, j], self.place.across(way),
        )

    def start(self):
        place = self.place
        self.sent[0] = self.block(place.other(3)).astype(bf16)
        for j in range(CHUNKS):
            self.copy(0, j).start()
        for kind in (1, 2):
            self.total[kind - 1] = self.block(place.other(kind))
            for j in range(CHUNKS):
                if kind == 1 + j % 2:
                    self.sent[kind, self.chunk(j)] = self.total[kind - 1, self.chunk(j)].astype(bf16)
                    self.copy(kind, j).start()

    def relay(self):
        for j in range(CHUNKS):
            kind = 2 - j % 2
            self.copy(0, j).wait_recv()
            share = self.total[kind - 1, self.chunk(j)] + self.got[0, self.chunk(j)].astype(f32)
            self.sent[kind, self.chunk(j)] = share.astype(bf16)
            self.copy(kind, j).start()
        self.total[0] = self.block(self.place.col)

    def sum(self, j):
        for kind in (1, 2):
            self.copy(kind, j).wait_recv()
        rows = self.chunk(j)
        return self.total[0, rows] + self.got[1, rows].astype(f32) + self.got[2, rows].astype(f32)

    def finish(self):
        for kind in range(3):
            for j in range(CHUNKS):
                self.copy(kind, j).wait_send()

    @staticmethod
    def scratch(size, width):
        return [
            pltpu.VMEM((2, size, width), f32),
            pltpu.VMEM((3, size, width), bf16),
            pltpu.VMEM((3, size, width), bf16),
            pltpu.SemaphoreType.DMA((2, 3, CHUNKS)),
        ]


class CtxSpread:
    def __init__(self, place, made, full, sems):
        self.place, self.made, self.full, self.sems = place, made, full, sems
        self.size = made.shape[0] // CHUNKS

    def rows(self, col, j):
        at = (col * CHUNKS + j) * self.size
        return self.full.at[pl.ds(pl.multiple_of(at, self.size), self.size), :]

    def copy(self, kind, j):
        place = self.place
        if kind < 2:
            part, there = self.made.at[pl.ds(j * self.size, self.size), :], self.rows(place.col, j)
            way = 1 + kind
        else:
            way = 2 - j % 2
            part = there = self.rows(place.other(3 - way), j)
        return remote(part, there, self.sems.at[0, kind, j], self.sems.at[1, kind, j], place.across(way))

    def arrived(self, kind, j):
        part = self.rows(self.place.other(kind + 1), j)
        remote(
            part, part, self.sems.at[0, kind, j], self.sems.at[1, kind, j], self.place.across(1)
        ).wait_recv()

    def local(self, j):
        part = self.made.at[pl.ds(j * self.size, self.size), :]
        return pltpu.make_async_copy(part, self.rows(self.place.col, j), self.sems.at[0, 3, j])

    def send(self, j):
        self.copy(0, j).start()
        self.copy(1, j).start()
        self.local(j).start()

    def relay(self, j):
        way = 2 - j % 2
        self.arrived(2 - way, j)
        self.copy(2, j).start()

    def finish(self):
        for j in range(CHUNKS):
            way = 2 - j % 2
            self.arrived(way - 1, j)
            self.arrived(2, j)
            self.local(j).wait()
            for kind in range(3):
                self.copy(kind, j).wait_send()

    @staticmethod
    def scratch():
        return pltpu.SemaphoreType.DMA((2, 4, CHUNKS))


def rows_of(ref, col, size):
    return ref[pl.ds(pl.multiple_of(col * size, size), size), :]


def mix_kernel(
    dp, ctx, attended_ref, weight_ref, rows_ref, gain_ref, shift_ref, resid_ref, wide_ref,
    total, sent, got, made, reduce_sem, spread_sem,
):
    place = Place(dp)
    greet(place, ctx)
    size = rows_ref.shape[0]
    reduce = CtxReduce(
        place, lambda col: dot(rows_of(attended_ref, col, size), weight_ref[...]), total, sent, got, reduce_sem
    )
    spread = CtxSpread(place, made, wide_ref, spread_sem)
    reduce.start()
    reduce.relay()
    for j in range(CHUNKS):
        rows = reduce.chunk(j)
        resid = rows_ref[rows, :].astype(f32) + reduce.sum(j)
        resid_ref[rows, :] = resid
        scaled, _ = norm_stats(resid)
        made[rows, :] = (scaled * gain_ref[...] + shift_ref[...]).astype(bf16)
        spread.send(j)
        if j:
            spread.relay(j - 1)
    spread.relay(CHUNKS - 1)
    spread.finish()
    reduce.finish()


def mix(dp, ctx, attended, weight, rows, gain, shift):
    size, width = rows.shape
    vmem = pl.BlockSpec(memory_space=pltpu.VMEM)
    return pl.pallas_call(
        functools.partial(mix_kernel, dp, ctx),
        in_specs=[vmem] * 5,
        out_specs=[vmem, ANY],
        out_shape=[jax.ShapeDtypeStruct((size, width), f32), jax.ShapeDtypeStruct((ctx * size, width), bf16)],
        scratch_shapes=CtxReduce.scratch(size, width)[:3]
        + [
            pltpu.VMEM((size, width), bf16),
            CtxReduce.scratch(size, width)[3],
            CtxSpread.scratch(),
        ],
        compiler_params=pltpu.CompilerParams(
            collective_id=2, has_side_effects=True, vmem_limit_bytes=40 << 20
        ),
        cost_estimate=pl.CostEstimate(
            flops=2 * attended.size * width, transcendentals=0, bytes_accessed=180 << 20
        ),
    )(attended, weight, rows, gain.reshape(1, width), shift.reshape(1, width))


def mix_back_kernel(
    dp, ctx, gate_ref, up_ref, gate_weight_hbm, up_weight_hbm, inner_hbm, down_hbm, normed_hbm,
    resid_ref, cot_ref, gain_ref,
    d_resid_ref, sums_ref, wide_ref, branch_hbm, d_up_hbm,
    total, sent, got, made, gate_weight_ref, up_weight_ref, inner_ref, down_ref, normed_ref, branch, d_up,
    reduce_sem, spread_sem, load_sem, branch_sem, d_up_sem,
):
    place = Place(dp)
    loads = [
        pltpu.make_async_copy(src, dst, load_sem.at[i])
        for i, (src, dst) in enumerate(
            (
                (gate_weight_hbm, gate_weight_ref), (up_weight_hbm, up_weight_ref), (normed_hbm, normed_ref),
                (inner_hbm, inner_ref), (down_hbm, down_ref),
            )
        )
    ]
    for load in loads[:2]:
        load.start()
    greet(place, ctx)
    size, width = cot_ref.shape
    cols = width // ctx // 2
    for load in loads[:2]:
        load.wait()

    def block(col):
        return dot_nt(rows_of(gate_ref, col, size), gate_weight_ref[...]) + dot_nt(
            rows_of(up_ref, col, size), up_weight_ref[...]
        )

    def d_up_copy(i):
        return pltpu.make_async_copy(
            d_up.at[i % 2], d_up_hbm.at[pl.ds(i * cols, cols), :], d_up_sem.at[i % 2]
        )

    def branch_copy(i):
        return pltpu.make_async_copy(
            branch.at[i % 2], branch_hbm.at[pl.ds(i * size, size), :], branch_sem.at[i % 2]
        )

    def d_up_piece(i):
        if i == 0:
            loads[2].wait()
        if i > 1:
            d_up_copy(i - 2).wait()
        d_up[i % 2] = dot_tn(normed_ref[:, i * cols : (i + 1) * cols], up_ref[...]).astype(bf16)
        d_up_copy(i).start()

    def branch_piece(i):
        if i == 0:
            loads[3].wait()
            loads[4].wait()
        if i > 1:
            branch_copy(i - 2).wait()
        branch[i % 2] = dot(inner_ref[i * size : (i + 1) * size, :], down_ref[...]).astype(bf16)
        branch_copy(i).start()

    pieces = [functools.partial(d_up_piece, i) for i in range(2 * ctx)]
    pieces += [functools.partial(branch_piece, i) for i in range(ctx)]

    reduce = CtxReduce(place, block, total, sent, got, reduce_sem)
    spread = CtxSpread(place, made, wide_ref, spread_sem)
    reduce.start()
    for load in loads[2:]:
        load.start()
    reduce.relay()
    sums_ref[...] = jnp.zeros_like(sums_ref)
    for j in range(CHUNKS):
        for piece in pieces[2 * j : 2 * j + 2]:
            piece()
        rows = reduce.chunk(j)
        scaled, inv_std = norm_stats(resid_ref[rows, :])
        grad, d_gain, d_shift = norm_backward(reduce.sum(j), scaled, inv_std, gain_ref[...])
        sums_ref[0:1, :] += d_gain[None]
        sums_ref[1:2, :] += d_shift[None]
        grad = cot_ref[rows, :].astype(f32) + grad
        d_resid_ref[rows, :] = grad
        made[rows, :] = grad.astype(bf16)
        spread.send(j)
        if j:
            spread.relay(j - 1)
    pieces[2 * CHUNKS]()
    spread.relay(CHUNKS - 1)
    for piece in pieces[2 * CHUNKS + 1 :]:
        piece()
    spread.finish()
    reduce.finish()
    for i in (1, 2):
        d_up_copy(2 * ctx - i).wait()
        branch_copy(ctx - i).wait()


def mix_back(dp, ctx, d_gate, d_up, gate_weight, up_weight, inner, down, normed, resid, cot, gain):
    size, width = cot.shape
    hidden = d_up.shape[1]
    vmem = pl.BlockSpec(memory_space=pltpu.VMEM)
    return pl.pallas_call(
        functools.partial(mix_back_kernel, dp, ctx),
        in_specs=[vmem] * 2 + [ANY] * 5 + [vmem] * 3,
        out_specs=[vmem, vmem, ANY, ANY, ANY],
        out_shape=[
            jax.ShapeDtypeStruct((size, width), f32),
            jax.ShapeDtypeStruct((2, width), f32),
            jax.ShapeDtypeStruct((ctx * size, width), bf16),
            jax.ShapeDtypeStruct((ctx * size, width), bf16),
            jax.ShapeDtypeStruct((width, hidden), bf16),
        ],
        scratch_shapes=CtxReduce.scratch(size, width)[:3]
        + [
            pltpu.VMEM((size, width), bf16),
            pltpu.VMEM((width, hidden), bf16),
            pltpu.VMEM((width, hidden), bf16),
            pltpu.VMEM((ctx * size, hidden), bf16),
            pltpu.VMEM((hidden, width), bf16),
            pltpu.VMEM((ctx * size, width), bf16),
            pltpu.VMEM((2, size, width), bf16),
            pltpu.VMEM((2, width // ctx // 2, hidden), bf16),
            CtxReduce.scratch(size, width)[3],
            CtxSpread.scratch(),
            pltpu.SemaphoreType.DMA((5,)),
            pltpu.SemaphoreType.DMA((2,)),
            pltpu.SemaphoreType.DMA((2,)),
        ],
        compiler_params=pltpu.CompilerParams(
            collective_id=3, has_side_effects=True, vmem_limit_bytes=60 << 20
        ),
        cost_estimate=pl.CostEstimate(
            flops=8 * d_gate.size * width, transcendentals=0, bytes_accessed=180 << 20
        ),
    )(d_gate, d_up, gate_weight, up_weight, inner, down, normed, resid, cot, gain.reshape(1, width))


class LineReduce:
    def __init__(self, place, parts, pair, got, sems):
        self.place, self.parts, self.pair, self.got, self.sems = place, parts, pair, got, sems

    def swap(self, line):
        row = 2 * line + 1 - self.place.core
        return remote(
            self.parts.at[row], self.pair.at[line], self.sems.at[0, line], self.sems.at[1, line], self.place.twin
        )

    def start(self):
        for line in range(self.place.lines):
            self.swap(line).start()

    def add(self):
        for line in range(self.place.lines):
            self.swap(line).wait_recv()
            both = self.parts[2 * line + self.place.core].astype(f32) + self.pair[line].astype(f32)
            self.pair[line] = both.astype(bf16)

    def up(self, far):
        part = self.place.line + far
        return remote(
            self.pair.at[part], self.got.at[part], self.sems.at[2, far], self.sems.at[3, far], self.place.above()
        )

    def down(self, far):
        part = self.place.line - far
        slot = part if far > 1 else self.place.lines
        return remote(
            self.pair.at[part], self.got.at[slot], self.sems.at[4, far], self.sems.at[5, far], self.place.below()
        )

    def came_up(self, far):
        slot = self.got.at[self.place.line + far]
        remote(slot, slot, self.sems.at[2, far + 1], self.sems.at[3, far + 1], self.place.twin).wait_recv()

    def came_down(self, far):
        slot = self.got.at[self.place.line - far if far else self.place.lines]
        remote(slot, slot, self.sems.at[4, far + 1], self.sems.at[5, far + 1], self.place.twin).wait_recv()

    def send(self, far):
        place = self.place

        @pl.when(place.line + far < place.lines)
        def _():
            @pl.when(place.line > 0)
            def _():
                self.came_up(far)
                part = place.line + far
                self.pair[part] = (self.pair[part].astype(f32) + self.got[part].astype(f32)).astype(bf16)

            self.up(far).start()

        @pl.when(place.line - far >= 0)
        def _():
            @pl.when(place.line < place.lines - 1)
            def _():
                self.came_down(far)
                part = place.line - far
                self.pair[part] = (self.pair[part].astype(f32) + self.got[part].astype(f32)).astype(bf16)

            self.down(far).start()

    def collect(self, out):
        place = self.place
        out[...] = self.pair[place.line].astype(f32)

        @pl.when(place.line > 0)
        def _():
            self.came_up(0)
            out[...] += self.got[place.line].astype(f32)

        @pl.when(place.line < place.lines - 1)
        def _():
            self.came_down(0)
            out[...] += self.got[place.lines].astype(f32)

    def finish(self):
        place = self.place
        for line in range(place.lines):
            self.swap(line).wait_send()
        for far in range(1, place.lines):
            pl.when(place.line + far < place.lines)(lambda: self.up(far).wait_send())
            pl.when(place.line - far >= 0)(lambda: self.down(far).wait_send())

    @staticmethod
    def scratch(dp, tile):
        return [
            pltpu.VMEM((dp // 2,) + tile, bf16),
            pltpu.VMEM((dp // 2 + 1,) + tile, bf16),
            pltpu.SemaphoreType.DMA((6, dp // 2)),
        ]


def closing_kernel(
    dp, ctx,
    d_joined_ref, weight_ref, qkv_parts_ref, out_parts_ref, rows_ref, d_resid_ref, gain_ref, sums_two_ref, bias_ref,
    grad_ref, qkv_ref, out_ref, small_ref,
    total, sent, got, reduce_sem, qkv_pair, qkv_got, qkv_sem, out_pair, out_got, out_sem,
    sums, tiles, tiles_got, small_sem, mine, swap_out, swap_in, swap_sem,
):
    place = Place(dp)
    me, row = place.col, place.row
    greet_all(place, dp, ctx)
    size, width = rows_ref.shape
    lines = [
        LineReduce(place, qkv_parts_ref, qkv_pair, qkv_got, qkv_sem),
        LineReduce(place, out_parts_ref, out_pair, out_got, out_sem),
    ]
    for line in lines:
        line.start()
    reduce = CtxReduce(
        place, lambda col: dot_nt(rows_of(d_joined_ref, col, size), weight_ref[...]), total, sent, got, reduce_sem
    )
    reduce.start()
    for line in lines:
        line.add()
        line.send(place.lines - 1)
    reduce.relay()
    for far in range(place.lines - 2, 1, -1):
        for line in lines:
            line.send(far)

    sums[...] = jnp.zeros_like(sums)
    for j in range(CHUNKS):
        rows = reduce.chunk(j)
        scaled, inv_std = norm_stats(rows_ref[rows, :].astype(f32))
        grad, d_gain, d_shift = norm_backward(reduce.sum(j), scaled, inv_std, gain_ref[...])
        sums[0:1, :] += d_gain[None]
        sums[1:2, :] += d_shift[None]
        grad_ref[rows, :] = d_resid_ref[rows, :] + grad
    if place.lines > 2:
        for line in lines:
            line.send(1)

    part = width // dp
    tiles[...] = jnp.zeros_like(tiles)
    for i in range(dp):
        lanes = slice(i * part, (i + 1) * part)
        tiles[i, 0:2, :] = sums[:, lanes]
        tiles[i, 2:4, :] = sums_two_ref[:, lanes]
        tiles[i, 4:5, :] = bias_ref[i : i + 1, :]
    sends = [
        remote(tiles.at[(row + k) % dp], tiles_got.at[k], small_sem.at[0, k], small_sem.at[1, k], ((row + k) % dp, me))
        for k in range(1, dp)
    ]
    for copy in sends:
        copy.start()
    tile = tiles[row]
    for k in range(1, dp):
        sends[k - 1].wait()
        tile = tile + tiles_got[k]
    tiles_got[0] = tile
    small_ref[me] = tile
    spreads = [
        remote(tiles_got.at[0], small_ref.at[me], small_sem.at[2, k], small_sem.at[3, k], place.across(k))
        for k in range(1, ctx)
    ]
    for copy in spreads:
        copy.start()

    lines[0].collect(mine)
    depth = mine.shape[0] // ctx
    swap_out[...] = mine[...].astype(bf16)
    swaps = [
        remote(
            swap_out.at[pl.ds(pl.multiple_of(place.other(k) * depth, depth), depth), :], swap_in.at[me],
            swap_sem.at[0, k], swap_sem.at[1, k], place.across(k),
        )
        for k in range(1, ctx)
    ]
    for copy in swaps:
        copy.start()
    swap_in[me] = rows_of(swap_out, me, depth)
    lines[1].collect(out_ref)
    for k in range(1, ctx):
        part = swap_in.at[place.other(k)]
        remote(part, part, swap_sem.at[0, k], swap_sem.at[1, k], place.across(k)).wait_recv()
    low = head_lanes((depth, PAIR))
    for p in range(mine.shape[1] // (3 * PAIR)):
        for t in range(3):
            lanes = slice((3 * p + t) * PAIR, (3 * p + t + 1) * PAIR)
            for c in range(0, ctx, 2):
                a = swap_in[c, :, lanes].astype(f32)
                b = swap_in[c + 1, :, lanes].astype(f32)
                at = t * width + (2 * p * ctx + c) * HD
                qkv_ref[:, at : at + PAIR] = jnp.where(low, a, pltpu.roll(b, HD, 1))
                at = at + ctx * HD
                qkv_ref[:, at : at + PAIR] = jnp.where(low, pltpu.roll(a, HD, 1), b)
    for copy in swaps:
        copy.wait_send()
    for k in range(1, ctx):
        spreads[k - 1].wait_send()
        part = small_ref.at[place.other(k)]
        remote(part, part, small_sem.at[2, k], small_sem.at[3, k], place.across(k)).wait_recv()
    for line in lines:
        line.finish()
    reduce.finish()


def closing(dp, ctx, d_joined, weight, d_qkv, d_out, rows, d_resid, gain, sums_two, bias):
    size, width = rows.shape
    near = weight.shape[1]
    own, tall = width // dp, d_out.shape[0] // dp
    vmem = pl.BlockSpec(memory_space=pltpu.VMEM)
    reduce_scratch = CtxReduce.scratch(size, width)
    max_peers = max(dp, ctx)
    return pl.pallas_call(
        functools.partial(closing_kernel, dp, ctx),
        in_specs=[vmem] * 9,
        out_specs=[vmem] * 4,
        out_shape=[
            jax.ShapeDtypeStruct((size, width), f32),
            jax.ShapeDtypeStruct((own // ctx, 3 * width), f32),
            jax.ShapeDtypeStruct((tall, width), f32),
            jax.ShapeDtypeStruct((ctx, 8, own), f32),
        ],
        scratch_shapes=reduce_scratch
        + LineReduce.scratch(dp, (own, near))
        + LineReduce.scratch(dp, (tall, width))
        + [
            pltpu.VMEM((2, width), f32),
            pltpu.VMEM((dp, 8, own), f32),
            pltpu.VMEM((dp, 8, own), f32),
            pltpu.SemaphoreType.DMA((4, max_peers)),
            pltpu.VMEM((own, near), f32),
            pltpu.VMEM((own, near), bf16),
            pltpu.VMEM((ctx, own // ctx, near), bf16),
            pltpu.SemaphoreType.DMA((2, ctx)),
        ],
        compiler_params=pltpu.CompilerParams(
            collective_id=1, has_side_effects=True, vmem_limit_bytes=60 << 20
        ),
        cost_estimate=pl.CostEstimate(
            flops=2 * d_joined.size * width, transcendentals=0, bytes_accessed=200 << 20
        ),
    )(
        d_joined, weight, d_qkv.reshape(dp, own, near), d_out.reshape(dp, tall, width),
        rows, d_resid, gain.reshape(1, width), sums_two, bias,
    )


def turn(x, table_ref):
    return (
        x * table_ref[0]
        + pltpu.roll(x, PAIR - ROT // 2, 1) * table_ref[1]
        + pltpu.roll(x, ROT // 2, 1) * table_ref[2]
    )


def turn_back(x, table_ref):
    return (
        x * table_ref[0]
        - pltpu.roll(x, PAIR - ROT // 2, 1) * table_ref[1]
        - pltpu.roll(x, ROT // 2, 1) * table_ref[2]
    )


def head_lanes(shape):
    return lax.broadcasted_iota(jnp.int32, shape, 1) < HD


def span(full_len, step, at):
    return max(0, (at - DOC_MAX + 1) // step * step), at + step


def block_mask(start, at, step, low, high):
    keys = lax.broadcasted_iota(jnp.int32, (step, high - low), 1) + low
    rows = lax.broadcasted_iota(jnp.int32, (step, high - low), 0) + at
    return (keys >= start) & (keys <= rows)


def attend_kernel(step, joined_ref, bias_ref, table_ref, start_ref, out_ref, qkv_ref, lse_ref):
    full_len = joined_ref.shape[0]
    scale = 1.0 / math.sqrt(HD)
    for t in range(3):
        lanes = slice(t * PAIR, (t + 1) * PAIR)
        x = joined_ref[:, lanes] + bias_ref[:, lanes]
        if t < 2:
            x = turn(x, table_ref)
        qkv_ref[:, lanes] = x.astype(bf16)
    for at in range(0, full_len, step):
        low, high = span(full_len, step, at)
        allowed = block_mask(start_ref[at : at + step, :1], at, step, low, high)
        q = qkv_ref[at : at + step, :PAIR]
        k = qkv_ref[low:high, PAIR : 2 * PAIR]
        v = qkv_ref[low:high, 2 * PAIR :]
        total = jnp.zeros((step, PAIR), f32)
        logs = []
        for head in range(2):
            mine = head_lanes(q.shape) == (head == 0)
            s = dot_nt(jnp.where(mine, q, jnp.zeros_like(q)), k) * scale
            s = jnp.where(allowed, s, masked_value)
            top = jnp.max(s, axis=1, keepdims=True)
            e = jnp.exp(s - top)
            norm = jnp.sum(e, axis=1, keepdims=True)
            probs = (e * (1.0 / norm)).astype(bf16)
            vm = jnp.where(head_lanes(v.shape) == (head == 0), v, jnp.zeros_like(v))
            total = total + dot(probs, vm)
            logs.append(top + jnp.log(norm))
        out_ref[at : at + step, :] = total.astype(bf16)
        lse_ref[at : at + step, :] = jnp.where(head_lanes((step, PAIR)), logs[0], logs[1])


def attend_back_kernel(
    step, qkv_ref, grad_ref, lse_ref, table_ref, start_ref, out_ref, sum_ref, dk_ref, dv_ref
):
    full_len = qkv_ref.shape[0]
    scale = 1.0 / math.sqrt(HD)
    dk_ref[...] = jnp.zeros_like(dk_ref)
    dv_ref[...] = jnp.zeros_like(dv_ref)
    total = jnp.zeros((1, PAIR), f32)
    for at in range(0, full_len, step):
        low, high = span(full_len, step, at)
        rows = slice(at, at + step)
        keys = slice(low, high)
        allowed = block_mask(start_ref[rows, :1], at, step, low, high)
        q = qkv_ref[rows, :PAIR]
        k = qkv_ref[keys, PAIR : 2 * PAIR]
        v = qkv_ref[keys, 2 * PAIR :]
        g = grad_ref[rows, :]
        dq = jnp.zeros((step, PAIR), f32)
        dk = jnp.zeros((high - low, PAIR), f32)
        dv = jnp.zeros((high - low, PAIR), f32)
        for head in range(2):
            mine = head_lanes(q.shape) == (head == 0)
            qm = jnp.where(mine, q, jnp.zeros_like(q))
            gm = jnp.where(mine, g, jnp.zeros_like(g))
            km = jnp.where(head_lanes(k.shape) == (head == 0), k, jnp.zeros_like(k))
            s = dot_nt(qm, k) * scale
            probs = jnp.where(
                allowed, jnp.exp(s - lse_ref[rows, head * HD : head * HD + 1]), 0.0
            )
            dp = dot_nt(gm, v)
            mean = jnp.sum(dp * probs, axis=1, keepdims=True)
            ds = (probs * (dp - mean)).astype(bf16)
            dq = dq + dot(ds, km)
            dk = dk + dot_tn(ds, qm)
            dv = dv + dot_tn(probs.astype(bf16), gm)
        dk_ref[keys, :] += dk
        dv_ref[keys, :] += dv
        dq = turn_back(dq * scale, table_ref.at[:, rows, :]).astype(bf16)
        out_ref[rows, :PAIR] = dq
        total = total + jnp.sum(dq.astype(f32), axis=0, keepdims=True)
    sum_ref[:, :PAIR] = total
    dk = turn_back(dk_ref[...] * scale, table_ref).astype(bf16)
    out_ref[:, PAIR : 2 * PAIR] = dk
    sum_ref[:, PAIR : 2 * PAIR] = jnp.sum(dk.astype(f32), axis=0, keepdims=True)
    dv = dv_ref[...].astype(bf16)
    out_ref[:, 2 * PAIR :] = dv
    sum_ref[:, 2 * PAIR :] = jnp.sum(dv.astype(f32), axis=0, keepdims=True)


def whole(shape):
    return pl.BlockSpec(shape, lambda p: (0,) * len(shape))


def attend_step(full_len):
    return min(256, full_len)


def attend(joined, bias, table, start):
    full_len, width = joined.shape
    pairs = width // (3 * PAIR)
    step = attend_step(full_len)
    seen = sum(span(full_len, step, at)[1] - span(full_len, step, at)[0] for at in range(0, full_len, step)) * step
    wide = pl.BlockSpec((full_len, 3 * PAIR), lambda p: (0, p))
    thin = pl.BlockSpec((full_len, PAIR), lambda p: (0, p))
    return pl.pallas_call(
        functools.partial(attend_kernel, step),
        grid=(pairs,),
        in_specs=[
            wide,
            pl.BlockSpec((1, 3 * PAIR), lambda p: (0, p)),
            whole(table.shape),
            whole(start.shape),
        ],
        out_specs=[thin, wide, thin],
        out_shape=[
            jax.ShapeDtypeStruct((full_len, pairs * PAIR), bf16),
            jax.ShapeDtypeStruct((full_len, width), bf16),
            jax.ShapeDtypeStruct((full_len, pairs * PAIR), f32),
        ],
        compiler_params=pltpu.CompilerParams(vmem_limit_bytes=40 << 20),
        cost_estimate=pl.CostEstimate(
            flops=pairs * seen * PAIR * 8, transcendentals=pairs * seen * 2, bytes_accessed=full_len * width * 8
        ),
    )(joined, bias, table, start)


def attend_back(qkv, grad, lse, table, start):
    full_len, width = qkv.shape
    pairs = width // (3 * PAIR)
    step = attend_step(full_len)
    seen = sum(span(full_len, step, at)[1] - span(full_len, step, at)[0] for at in range(0, full_len, step)) * step
    wide = pl.BlockSpec((full_len, 3 * PAIR), lambda p: (0, p))
    thin = pl.BlockSpec((full_len, PAIR), lambda p: (0, p))
    return pl.pallas_call(
        functools.partial(attend_back_kernel, step),
        grid=(pairs,),
        in_specs=[wide, thin, thin, whole(table.shape), whole(start.shape)],
        out_specs=[wide, pl.BlockSpec((1, 3 * PAIR), lambda p: (0, p))],
        out_shape=[
            jax.ShapeDtypeStruct((full_len, width), bf16),
            jax.ShapeDtypeStruct((1, width), f32),
        ],
        scratch_shapes=[pltpu.VMEM((full_len, PAIR), f32), pltpu.VMEM((full_len, PAIR), f32)],
        compiler_params=pltpu.CompilerParams(vmem_limit_bytes=40 << 20),
        cost_estimate=pl.CostEstimate(
            flops=pairs * seen * PAIR * 20, transcendentals=pairs * seen * 2, bytes_accessed=full_len * width * 8
        ),
    )(qkv, grad, lse, table, start)


def rotary_table(full_len):
    half = ROT // 2
    inverse = 10000.0 ** (-2.0 * np.arange(half) / ROT)
    angles = np.arange(full_len)[:, None] * inverse[None, :]
    table = np.zeros((3, full_len, HD), np.float32)
    table[0, :, :half] = table[0, :, half:ROT] = np.cos(angles)
    table[0, :, ROT:] = 1.0
    table[1, :, :half] = -np.sin(angles)
    table[2, :, half:ROT] = np.sin(angles)
    return jnp.asarray(np.concatenate([table, table], axis=2))


def shards(
    dp,
    ctx,
    inputs,
    segments,
    ln1_gain,
    ln1_bias,
    qkv_weight,
    qkv_bias,
    out_weight,
    ln2_gain,
    ln2_bias,
    gate_weight,
    up_weight,
    down_weight,
    cotangent,
):
    local_len, width = inputs.shape[1], inputs.shape[2]
    full_len = segments.shape[1]
    heads = width // HD
    near = heads // ctx
    pairs = near // 2
    me = lax.axis_index("ctx")
    own = me * local_len

    part = ln1_gain.shape[0]
    vectors = [v[None, :] for v in (ln1_gain, ln1_bias, ln2_gain, ln2_bias, qkv_bias)]
    count = 4 * part + qkv_bias.shape[0]
    rows_here = qkv_weight.shape[0]
    rows, grad_rows = inputs[0], cotangent[0]
    fused = ctx == 4 and dp % 2 == 0 and part == HD
    if fused:
        small, params, joined_weight, out_full, normed_one, joined, grad_wide = opening(
            dp, ctx, vectors, qkv_weight, out_weight, rows, grad_rows
        )
        gain_one, shift_one, gain_two, shift_two = params
        gate_weight, up_weight, down_weight, _ = lax.optimization_barrier(
            (gate_weight, up_weight, down_weight, normed_one)
        )
        small = small.reshape(dp * ctx, 1024)[:, :count]
    else:
        small = jnp.concatenate(vectors, axis=1).astype(f32)
        small = lax.all_gather(small, ("dp", "ctx"), axis=0, tiled=True)
        blocks = qkv_weight.reshape(rows_here, 3, pairs, 2, ctx, HD).transpose(4, 0, 2, 1, 3, 5)
        blocks = exchange_ctx(blocks.reshape(ctx, rows_here, near * 3 * HD), ctx)
        joined_weight = lax.all_gather(
            blocks.reshape(ctx * rows_here, near * 3 * HD), "dp", axis=0, tiled=True
        )
        out_full = lax.all_gather(out_weight, ("dp", "ctx"), axis=0, tiled=True)
        out_full = out_full.reshape(near, ctx, HD, width)
        out_full = lax.dynamic_index_in_dim(out_full, me, 1, keepdims=False)
        out_full = out_full.reshape(near * HD, width)
        gain_one, shift_one, gain_two, shift_two = [
            small[:, i * part : (i + 1) * part].reshape(width) for i in range(4)
        ]
        scaled_wide, _ = norm_stats(gather_ctx(rows, ctx).astype(f32))
        normed_one = (scaled_wide * gain_one + shift_one).astype(bf16)
        grad_wide = gather_ctx(grad_rows, ctx)
    bias = small[:, 4 * part :].reshape(3, pairs, 2, ctx, HD)
    bias = lax.dynamic_index_in_dim(bias, me, 3, keepdims=False)
    bias = bias.transpose(1, 0, 2, 3).reshape(1, near * 3 * HD)
    gate_full = lax.all_gather(gate_weight, "dp", axis=0, tiled=True)
    up_full = lax.all_gather(up_weight, "dp", axis=0, tiled=True)
    down_full = lax.all_gather(down_weight, "dp", axis=1, tiled=True)

    segment = segments[0]
    start = jnp.sum((segment[None, :] < segment[:, None]).astype(jnp.int32), axis=1)
    start = jnp.broadcast_to(start[:, None], (full_len, 128))
    table = rotary_table(full_len)
    if not fused:
        joined = dot(normed_one, joined_weight)
    attended, qkv, lse = attend(joined, bias, table, start)
    if fused:
        resid, normed_wide = mix(dp, ctx, attended, out_full, rows, gain_two, shift_two)
    else:
        resid = rows.astype(f32) + scatter_ctx(dot(attended, out_full), ctx)
        scaled_two, inv_two = norm_stats(resid)
        normed_wide = gather_ctx((scaled_two * gain_two + shift_two).astype(bf16), ctx)

    gate = dot(normed_wide, gate_full)
    upward = dot(normed_wide, up_full)
    sigma = jax.nn.sigmoid(gate)
    swish = gate * sigma
    inner = (swish * upward).astype(bf16)
    d_down = dot_tn(inner, grad_wide).astype(bf16)
    grad_wide, d_down = lax.optimization_barrier((grad_wide, d_down))
    d_down = lax.psum_scatter(d_down, "dp", scatter_dimension=1, tiled=True).astype(f32)
    d_inner = dot_nt(grad_wide, down_full)
    d_gate = (d_inner * upward * sigma * (1.0 + gate * (1.0 - sigma))).astype(bf16)
    d_upward = (d_inner * swish).astype(bf16)
    d_gate_weight = dot_tn(normed_wide, d_gate).astype(bf16)
    d_gate_ready, d_gate_weight = lax.optimization_barrier((d_gate, d_gate_weight))
    d_gate_weight = lax.psum_scatter(d_gate_weight, "dp", scatter_dimension=0, tiled=True).astype(f32)
    if fused:
        d_resid, sums_two, d_proj, branch, d_up_weight = mix_back(
            dp, ctx, d_gate_ready, d_upward, gate_full, up_full, inner, down_full, normed_wide, resid,
            grad_rows, gain_two,
        )
    else:
        branch = dot(inner, down_full)
        d_up_weight = dot_tn(normed_wide, d_upward).astype(bf16)
        d_normed_two = scatter_ctx(dot_nt(d_gate, gate_full) + dot_nt(d_upward, up_full), ctx)
        grad, d_gain_two, d_shift_two = norm_backward(d_normed_two, scaled_two, inv_two, gain_two)
        d_resid = grad_rows.astype(f32) + grad
        d_proj = gather_ctx(d_resid.astype(bf16), ctx)
    d_up_weight = lax.psum_scatter(d_up_weight, "dp", scatter_dimension=0, tiled=True).astype(f32)

    d_attended = dot_nt(d_proj, out_full).astype(bf16)
    d_out_weight = dot_tn(attended, d_proj).astype(bf16)
    d_attended, d_down = lax.optimization_barrier((d_attended, d_down))
    d_joined, d_bias = attend_back(qkv, d_attended, lse, table, start)
    output = (resid + scatter_ctx(branch, ctx, d_joined)).astype(bf16)
    d_joined_weight = dot_tn(normed_one, d_joined).astype(bf16)
    d_bias = d_bias.reshape(pairs, 3, 2, HD).transpose(1, 0, 2, 3)
    d_joined, d_gate_weight = lax.optimization_barrier((d_joined, d_gate_weight))
    if fused:
        d_bias = jnp.pad(d_bias.reshape(dp, -1), ((0, 0), (0, width // dp - near * 3 * HD // dp)))
        grad_input, d_joined_weight, d_out_weight, small = closing(
            dp, ctx, d_joined, joined_weight, d_joined_weight, d_out_weight, rows, d_resid, gain_one, sums_two, d_bias
        )
        vectors = lax.dynamic_slice_in_dim(jnp.sum(small[:, :4], axis=0), me * part, part, 1)
        d_gain_one, d_shift_one, d_gain_two, d_shift_two = vectors
        d_bias = small[:, 4, : near * 3 * HD // dp].reshape(ctx, -1, HD).transpose(1, 0, 2)
        d_bias = lax.dynamic_index_in_dim(d_bias.reshape(ctx, -1), me, 0, keepdims=False)
    else:
        at_me = lax.broadcasted_iota(jnp.int32, (1, ctx, 1, 1), 1) == me
        d_out_weight = jnp.where(at_me, d_out_weight.reshape(near, 1, HD, width), jnp.zeros((), bf16))
        d_out_weight = lax.psum_scatter(
            d_out_weight.reshape(width, width), ("dp", "ctx"), scatter_dimension=0, tiled=True
        ).astype(f32)
        d_normed_one = scatter_ctx(dot_nt(d_joined, joined_weight), ctx)
        scaled_one, inv_one = norm_stats(rows.astype(f32))
        grad, d_gain_one, d_shift_one = norm_backward(d_normed_one, scaled_one, inv_one, gain_one)
        grad_input = d_resid + grad
        d_joined_weight = lax.psum_scatter(d_joined_weight, "dp", scatter_dimension=0, tiled=True)
        blocks = exchange_ctx(d_joined_weight.reshape(ctx, rows_here, near * 3 * HD), ctx)
        blocks = blocks.reshape(ctx, rows_here, pairs, 3, 2, HD).transpose(1, 3, 2, 4, 0, 5)
        d_joined_weight = blocks.reshape(rows_here, 3 * width).astype(f32)
        at_me = (lax.broadcasted_iota(jnp.int32, (1, 1, 1, ctx, 1), 3) == me).astype(f32)
        d_bias = (d_bias[:, :, :, None, :] * at_me).reshape(dp * ctx, -1)
        small = jnp.concatenate(
            [t.reshape(dp * ctx, part) for t in (d_gain_one, d_shift_one, d_gain_two, d_shift_two)]
            + [d_bias],
            axis=1,
        )
        small = lax.psum_scatter(small, ("dp", "ctx"), scatter_dimension=0, tiled=True)[0]
        d_gain_one, d_shift_one, d_gain_two, d_shift_two = [
            small[i * part : (i + 1) * part] for i in range(4)
        ]
        d_bias = small[4 * part :]
    return (
        output[None],
        grad_input[None],
        d_gain_one,
        d_shift_one,
        d_joined_weight,
        d_bias,
        d_out_weight,
        d_gain_two,
        d_shift_two,
        d_gate_weight,
        d_up_weight,
        d_down,
    )


def solution(mesh):
    every = ("dp", "ctx")
    return jax.shard_map(
        functools.partial(shards, mesh.shape["dp"], mesh.shape["ctx"]),
        mesh=mesh,
        in_specs=(
            P("dp", "ctx", None),
            P("dp", None),
            P(every),
            P(every),
            P(every, None),
            P(every),
            P(every, None),
            P(every),
            P(every),
            P("dp", "ctx"),
            P("dp", "ctx"),
            P("ctx", "dp"),
            P("dp", "ctx", None),
        ),
        out_specs=(
            P("dp", "ctx", None),
            P("dp", "ctx", None),
            P(every),
            P(every),
            P(every, None),
            P(every),
            P(every, None),
            P(every),
            P(every),
            P("dp", "ctx"),
            P("dp", "ctx"),
            P("ctx", "dp"),
        ),
        check_vma=False,
    )
```

```python
import functools
import math

import jax
import jax.numpy as jnp
import numpy as np
from jax import lax
from jax.experimental import pallas as pl
from jax.experimental.pallas import tpu as pltpu
from jax.sharding import PartitionSpec as P

HD = 64
ROT = 16
DOC_MAX = 512
PAIR = 2 * HD

norm_eps = 1e-05
masked_value = -1e30
f32 = jnp.float32
bf16 = jnp.bfloat16


def dot(a, b):
    return jnp.dot(a, b, preferred_element_type=f32)


def dot_nt(a, b):
    return lax.dot_general(a, b, (((1,), (1,)), ((), ())), preferred_element_type=f32)


def dot_tn(a, b):
    return lax.dot_general(a, b, (((0,), (0,)), ((), ())), preferred_element_type=f32)


def norm_stats(rows):
    row_mean = jnp.mean(rows, axis=-1, keepdims=True)
    centered = rows - row_mean
    variance = jnp.mean(centered * centered, axis=-1, keepdims=True)
    inv_std = lax.rsqrt(variance + norm_eps)
    return centered * inv_std, inv_std


def norm_backward(grad_normed, scaled, inv_std, gain):
    grad_gain = jnp.sum(grad_normed * scaled, axis=0)
    grad_shift = jnp.sum(grad_normed, axis=0)
    inner_grad = grad_normed * gain
    grad_rows = inv_std * (
        inner_grad
        - jnp.mean(inner_grad, axis=-1, keepdims=True)
        - scaled * jnp.mean(inner_grad * scaled, axis=-1, keepdims=True)
    )
    return grad_rows, grad_gain, grad_shift


def partner(n, k):
    return [(c, c ^ k) for c in range(n)]


def hop(x, n, k):
    return lax.ppermute(x, "ctx", partner(n, k))


def gather_relative(block, n):
    if n != 4:
        return [block] + [hop(block, n, k) for k in range(1, n)]
    half = block.shape[0] // 2
    one = hop(block, n, 1)
    two = hop(block, n, 2)
    low = hop(one[:half], n, 2)
    high = hop(two[half:], n, 1)
    return [block, one, two, jnp.concatenate([low, high], axis=0)]


def gather_ctx(block, n):
    me = lax.axis_index("ctx")
    size = block.shape[0]
    parts = gather_relative(block, n)
    full = jnp.zeros((n * size,) + block.shape[1:], block.dtype)
    for k, part in enumerate(parts):
        full = lax.dynamic_update_slice_in_dim(full, part, (me ^ k) * size, 0)
    return full


def scatter_ctx(partial, n):
    me = lax.axis_index("ctx")
    size = partial.shape[0] // n

    def block(k):
        return lax.dynamic_slice_in_dim(partial, (me ^ k) * size, size, 0)

    if n != 4:
        total = block(0).astype(f32)
        for k in range(1, n):
            total = total + hop(block(k).astype(bf16), n, k).astype(f32)
        return total
    half = size // 2
    far = block(3).astype(bf16)
    low = hop(far[:half], n, 1).astype(f32)
    high = hop(far[half:], n, 2).astype(f32)
    one = block(1).astype(f32)
    two = block(2).astype(f32)
    to_one = jnp.concatenate([one[:half], one[half:] + high], axis=0).astype(bf16)
    to_two = jnp.concatenate([two[:half] + low, two[half:]], axis=0).astype(bf16)
    return block(0).astype(f32) + hop(to_one, n, 1).astype(f32) + hop(to_two, n, 2).astype(f32)


def exchange_ctx(blocks, n):
    me = lax.axis_index("ctx")
    got = lax.dynamic_update_slice_in_dim(
        jnp.zeros_like(blocks), lax.dynamic_slice_in_dim(blocks, me, 1, 0), me, 0
    )
    for k in range(1, n):
        sent = lax.dynamic_slice_in_dim(blocks, me ^ k, 1, 0)
        got = lax.dynamic_update_slice_in_dim(got, hop(sent, n, k), me ^ k, 0)
    return got


MESH = pl.DeviceIdType.MESH
HBM = pl.BlockSpec(memory_space=pltpu.HBM)


class Place:
    def __init__(self, dp):
        self.row = lax.axis_index("dp")
        self.col = lax.axis_index("ctx")
        self.lines = dp // 2
        self.line = self.row // 2
        self.core = self.row % 2
        self.twin = (self.row + 1 - 2 * self.core, self.col)

    def other(self, k):
        col, bit = self.col, 1
        while bit <= k:
            if k & bit:
                col = col + bit * (1 - 2 * ((self.col // bit) % 2))
            bit *= 2
        return col

    def across(self, k):
        return (self.row, self.other(k))

    def above(self):
        return (self.row + 2, self.col)

    def below(self):
        return (self.row - 2, self.col)


def greet(place, ctx):
    barrier = pltpu.get_barrier_semaphore()
    for k in range(1, ctx):
        pl.semaphore_signal(barrier, 1, device_id=place.across(k), device_id_type=MESH)
    pl.semaphore_wait(barrier, ctx - 1)


def remote(src, dst, send, recv, device):
    return pltpu.make_async_remote_copy(
        src_ref=src, dst_ref=dst, send_sem=send, recv_sem=recv, device_id=device, device_id_type=MESH
    )


class LineGather:
    def __init__(self, place, shard, sems):
        self.place, self.shard, self.sems = place, shard, sems

    def row(self, line):
        return line * 2 + self.place.core

    def up(self, hop):
        part = self.shard(self.row(self.place.line - hop + 1))
        return remote(part, part, self.sems.at[0, hop], self.sems.at[1, hop], self.place.above())

    def down(self, hop):
        part = self.shard(self.row(self.place.line + hop - 1))
        return remote(part, part, self.sems.at[2, hop], self.sems.at[3, hop], self.place.below())

    def over(self, at, row):
        part = self.shard(row)
        return remote(part, part, self.sems.at[4, at], self.sems.at[5, at], self.place.twin)

    def sends_up(self, hop):
        return (self.place.line - hop + 1 >= 0) & (self.place.line < self.place.lines - 1)

    def sends_down(self, hop):
        return (self.place.line + hop - 1 < self.place.lines) & (self.place.line > 0)

    def send(self, hop):
        place = self.place
        pl.when(self.sends_up(hop))(lambda: self.up(hop).start())
        pl.when(self.sends_down(hop))(lambda: self.down(hop).start())
        if hop == 1:
            self.over(0, place.row).start()

    def receive(self, hop):
        place = self.place

        @pl.when(place.line - hop >= 0)
        def _():
            part = self.shard(self.row(place.line - hop))
            remote(part, part, self.sems.at[0, hop], self.sems.at[1, hop], place.twin).wait_recv()
            self.over(hop, self.row(place.line - hop)).start()

        @pl.when(place.line + hop < place.lines)
        def _():
            part = self.shard(self.row(place.line + hop))
            remote(part, part, self.sems.at[2, hop], self.sems.at[3, hop], place.twin).wait_recv()
            self.over(place.lines - 1 + hop, self.row(place.line + hop)).start()

    def came_over(self, at, row):
        part = self.shard(row)
        remote(part, part, self.sems.at[4, at], self.sems.at[5, at], self.place.twin).wait_recv()

    def settle(self, hop, use=None):
        place = self.place
        other = 1 - 2 * place.core
        if hop == 0:
            self.came_over(0, place.row + other)
            if use:
                use(place.line)
            return
        for at, line, there in (
            (hop, place.line - hop, place.line - hop >= 0),
            (place.lines - 1 + hop, place.line + hop, place.line + hop < place.lines),
        ):

            @pl.when(there)
            def _():
                self.came_over(at, self.row(line) + other)
                if use:
                    use(line)

    def finish(self):
        place = self.place
        self.over(0, place.row).wait_send()
        for hop in range(1, place.lines):
            pl.when(self.sends_up(hop))(lambda: self.up(hop).wait_send())
            pl.when(self.sends_down(hop))(lambda: self.down(hop).wait_send())
            for at, line, there in (
                (hop, place.line - hop, place.line - hop >= 0),
                (place.lines - 1 + hop, place.line + hop, place.line + hop < place.lines),
            ):
                pl.when(there)(lambda: self.over(at, self.row(line)).wait_send())

    @staticmethod
    def scratch(dp):
        return pltpu.SemaphoreType.DMA((6, dp))


class CtxGather:
    def __init__(self, place, block, full, size, sems):
        self.place, self.block, self.full, self.size, self.sems = place, block, full, size, sems

    def rows(self, col, start=0, size=None):
        size = self.size if size is None else size
        return self.full.at[pl.ds(pl.multiple_of(col * self.size + start, size), size), :]

    def copies(self):
        place, half = self.place, self.size // 2
        me = place.col
        return [
            remote(self.block, self.rows(me), self.sems.at[0, 0], self.sems.at[1, 0], place.across(1)),
            remote(self.block, self.rows(me), self.sems.at[0, 1], self.sems.at[1, 1], place.across(2)),
            remote(
                self.rows(place.other(1), 0, half), self.rows(place.other(1), 0, half),
                self.sems.at[0, 2], self.sems.at[1, 2], place.across(2),
            ),
            remote(
                self.rows(place.other(2), half, half), self.rows(place.other(2), half, half),
                self.sems.at[0, 3], self.sems.at[1, 3], place.across(1),
            ),
        ]

    def arrivals(self):
        place, half = self.place, self.size // 2
        me = place.col
        parts = [self.rows(place.other(1)), self.rows(place.other(2)), self.rows(place.other(3), 0, half), self.rows(place.other(3), half, half)]
        return [
            remote(part, part, self.sems.at[0, i], self.sems.at[1, i], place.across(1))
            for i, part in enumerate(parts)
        ]

    def first(self):
        copies = self.copies()
        copies[0].start()
        copies[1].start()

    def second(self):
        copies, arrivals = self.copies(), self.arrivals()
        arrivals[0].wait_recv()
        copies[2].start()
        arrivals[1].wait_recv()
        copies[3].start()

    def finish(self):
        copies, arrivals = self.copies(), self.arrivals()
        arrivals[2].wait_recv()
        arrivals[3].wait_recv()
        for copy in copies:
            copy.wait_send()

    @staticmethod
    def scratch():
        return pltpu.SemaphoreType.DMA((2, 4))


def greet_all(place, dp, ctx, signal=True, wait=True):
    barrier = pltpu.get_barrier_semaphore()
    if signal:
        for k in range(1, ctx):
            pl.semaphore_signal(barrier, 1, device_id=place.across(k), device_id_type=MESH)
        for k in range(1, dp):
            pl.semaphore_signal(barrier, 1, device_id=((place.row + k) % dp, place.col), device_id_type=MESH)
    if wait:
        pl.semaphore_wait(barrier, ctx + dp - 2)


PARTS = 2


def opening_kernel(
    dp, ctx,
    gain_one, shift_one, gain_two, shift_two, bias, qkv_hbm, out_weight_ref, rows_ref, cot_ref,
    small_all, params_ref, weight_hbm, out_all, normed_hbm, joined_ref, cot_all,
    small_ref, qkv_ref, blocks, rows_all, weight_ref, normed_ref, normed_sem, weight_sem, local_sem, swap_sem, small_sem, line_joined, line_out, rows_sem, cot_sem,
):
    place = Place(dp)
    me, row = place.col, place.row
    depth = qkv_ref.shape[0]
    length, width = rows_ref.shape
    rows_out = out_weight_ref.shape[0]
    tall = ctx * depth

    qkv_copy = pltpu.make_async_copy(qkv_hbm, qkv_ref, local_sem.at[4])
    qkv_copy.start()
    greet_all(place, dp, ctx, wait=False)
    small_ref[...] = jnp.zeros_like(small_ref)
    for i, vector in enumerate((gain_one, shift_one, gain_two, shift_two)):
        small_ref[i // 2 : i // 2 + 1, i % 2 * HD : (i % 2 + 1) * HD] = vector[...].astype(f32)
    for i in range(bias.shape[1] // HD):
        small_ref[2 + i // 2 : 3 + i // 2, i % 2 * HD : (i % 2 + 1) * HD] = bias[
            :, i * HD : (i + 1) * HD
        ].astype(f32)
    small_all[row, me] = small_ref[...]
    qkv_copy.wait()

    low = head_lanes((depth, PAIR))
    for p in range(width // HD // ctx // 2):
        for t in range(3):
            lanes = slice((3 * p + t) * PAIR, (3 * p + t + 1) * PAIR)
            for c in range(0, ctx, 2):
                at = t * width + (2 * p * ctx + c) * HD
                a = qkv_ref[:, at : at + PAIR].astype(f32)
                at = at + ctx * HD
                b = qkv_ref[:, at : at + PAIR].astype(f32)
                blocks[c, :, lanes] = jnp.where(low, a, pltpu.roll(b, HD, 1)).astype(bf16)
                blocks[c + 1, :, lanes] = jnp.where(low, pltpu.roll(a, HD, 1), b).astype(bf16)
    greet_all(place, dp, ctx, signal=False)

    def weight_rows(row, col):
        return weight_ref.at[pl.ds(pl.multiple_of((row * ctx + col) * depth, depth), depth), :]

    def out_shard(row):
        return out_all.at[pl.ds(pl.multiple_of(row * rows_out, rows_out), rows_out), :]

    def block(ref, col):
        return ref.at[pl.ds(pl.multiple_of(col * length, length), length), :]

    part_cols = weight_ref.shape[1] // PARTS

    def weight_part(i, row):
        return weight_ref.at[
            pl.ds(pl.multiple_of(row * tall, tall), tall), pl.ds(i * part_cols, part_cols)
        ]

    local = [
        pltpu.make_async_copy(blocks.at[me], weight_rows(row, me), local_sem.at[0]),
        pltpu.make_async_copy(out_weight_ref, out_shard(row), local_sem.at[1]),
        pltpu.make_async_copy(rows_ref, block(rows_all, me), local_sem.at[2]),
        pltpu.make_async_copy(cot_ref, block(cot_all, me), local_sem.at[3]),
    ]
    swaps = [
        remote(small_ref, small_all.at[row, me], swap_sem.at[0, k], swap_sem.at[1, k], place.across(k))
        for k in range(1, ctx)
    ] + [
        remote(
            blocks.at[place.other(k)], weight_rows(row, me), swap_sem.at[2, k], swap_sem.at[3, k], place.across(k)
        )
        for k in range(1, ctx)
    ]
    for copy in swaps:
        copy.start()
    for copy in local:
        copy.start()
    rows_gather = CtxGather(place, rows_ref, rows_all, length, rows_sem)
    cot_gather = CtxGather(place, cot_ref, cot_all, length, cot_sem)
    out_line = LineGather(place, out_shard, line_out)
    lines = [
        LineGather(place, functools.partial(weight_part, i), line_joined.at[i]) for i in range(PARTS)
    ] + [out_line]
    local[1].wait()
    out_line.send(1)
    rows_gather.first()
    for k in range(1, ctx):
        remote(
            small_ref, small_all.at[row, place.other(k)], swap_sem.at[0, k], swap_sem.at[1, k], place.across(k)
        ).wait_recv()
    small_sends = [
        remote(
            small_all.at[row], small_all.at[row], small_sem.at[0, k], small_sem.at[1, k], ((row + k) % dp, me)
        )
        for k in range(1, dp)
    ]
    for copy in small_sends:
        copy.start()
    local[0].wait()
    for k in range(1, ctx):
        part = weight_rows(row, place.other(k))
        remote(part, part, swap_sem.at[2, k], swap_sem.at[3, k], place.across(k)).wait_recv()
    for line in lines[:PARTS]:
        line.send(1)

    for k in range(1, dp):
        part = small_all.at[(row + dp - k) % dp]
        remote(part, part, small_sem.at[0, k], small_sem.at[1, k], place.twin).wait_recv()
    low = head_lanes((1, PAIR))
    for i in range(dp * ctx // 2):
        lanes = slice(i * PAIR, (i + 1) * PAIR)
        a = small_all[2 * i // ctx, 2 * i % ctx]
        b = small_all[(2 * i + 1) // ctx, (2 * i + 1) % ctx]
        for r in range(2):
            ar, br = a[r : r + 1, :], b[r : r + 1, :]
            params_ref[2 * r : 2 * r + 1, lanes] = jnp.where(low, ar, pltpu.roll(br, HD, 1))
            params_ref[2 * r + 1 : 2 * r + 2, lanes] = jnp.where(low, pltpu.roll(ar, HD, 1), br)

    def normalize(col):
        step = 64

        @pl.loop(0, length // step)
        def _(i):
            rows = pl.ds(pl.multiple_of(col * length + i * step, step), step)
            scaled, _ = norm_stats(rows_all[rows, :].astype(f32))
            normed_ref[rows, :] = (scaled * params_ref[0:1, :] + params_ref[1:2, :]).astype(bf16)

        normed_copy(col).start()

    def normed_copy(col):
        return pltpu.make_async_copy(block(normed_ref, col), block(normed_hbm, col), normed_sem.at[col])

    def weight_copy(i, line):
        part = (
            pl.ds(pl.multiple_of(line * (2 * tall), 2 * tall), 2 * tall),
            pl.ds(i * part_cols, part_cols),
        )
        return pltpu.make_async_copy(weight_ref.at[part], weight_hbm.at[part], weight_sem.at[i, line])

    def multiply(i, line):
        weight_copy(i, line).start()
        at = pl.multiple_of(line * (2 * tall), 2 * tall)
        cols = slice(i * part_cols, (i + 1) * part_cols)

        @pl.loop(0, ctx)
        def _(b):
            rows = pl.ds(pl.multiple_of(b * length, length), length)
            joined_ref[rows, cols] += dot(
                normed_ref[rows, pl.ds(at, 2 * tall)], weight_ref[pl.ds(at, 2 * tall), cols]
            )

    def forward(hop):
        for line in lines:
            line.receive(hop)
            if hop < place.lines - 1:
                line.send(hop + 1)

    def absorb(hop):
        for i in range(PARTS):
            lines[i].settle(hop, functools.partial(multiply, i))

    joined_ref[...] = jnp.zeros_like(joined_ref)
    local[2].wait()
    normalize(me)
    rows_gather.second()
    cot_gather.first()
    for hop in range(1, place.lines):
        forward(hop)
        if hop == 1:
            for col in (place.other(1), place.other(2)):
                normalize(col)
            rows_gather.finish()
            normalize(place.other(3))
        if hop == min(2, place.lines - 1):
            cot_gather.second()
        absorb(hop - 1)
    absorb(place.lines - 1)
    for hop in range(place.lines):
        out_line.settle(hop)
    for line in lines:
        line.finish()
    cot_gather.finish()
    for copy in swaps + small_sends:
        copy.wait_send()
    local[3].wait()
    for col in range(ctx):
        normed_copy(col).wait()
    for line in range(place.lines):
        for i in range(PARTS):
            weight_copy(i, line).wait()


def opening(dp, ctx, vectors, qkv_weight, out_weight, rows, cot):
    depth, width = qkv_weight.shape[0], rows.shape[1]
    length = rows.shape[0]
    near = 3 * width // ctx
    vmem = pl.BlockSpec(memory_space=pltpu.VMEM)
    return pl.pallas_call(
        functools.partial(opening_kernel, dp, ctx),
        in_specs=[vmem] * len(vectors) + [HBM] * 4,
        out_specs=[vmem, vmem, HBM, HBM, HBM, vmem, HBM],
        out_shape=[
            jax.ShapeDtypeStruct((dp, ctx, 8, PAIR), f32),
            jax.ShapeDtypeStruct((4, width), f32),
            jax.ShapeDtypeStruct((dp * ctx * depth, near), bf16),
            jax.ShapeDtypeStruct((dp * out_weight.shape[0], width), bf16),
            jax.ShapeDtypeStruct((ctx * length, width), bf16),
            jax.ShapeDtypeStruct((ctx * length, near), f32),
            jax.ShapeDtypeStruct((ctx * length, width), bf16),
        ],
        scratch_shapes=[
            pltpu.VMEM((8, PAIR), f32),
            pltpu.VMEM((depth, 3 * width), bf16),
            pltpu.VMEM((ctx, depth, near), bf16),
            pltpu.VMEM((ctx * length, width), bf16),
            pltpu.VMEM((dp * ctx * depth, near), bf16),
            pltpu.VMEM((ctx * length, width), bf16),
            pltpu.SemaphoreType.DMA((ctx,)),
            pltpu.SemaphoreType.DMA((PARTS, dp // 2)),
            pltpu.SemaphoreType.DMA((5,)),
            pltpu.SemaphoreType.DMA((4, ctx)),
            pltpu.SemaphoreType.DMA((2, dp)),
            pltpu.SemaphoreType.DMA((PARTS, 6, dp)),
            LineGather.scratch(dp),
            CtxGather.scratch(),
            CtxGather.scratch(),
        ],
        compiler_params=pltpu.CompilerParams(
            collective_id=0, has_side_effects=True, vmem_limit_bytes=40 << 20
        ),
        cost_estimate=pl.CostEstimate(
            flops=2 * ctx * length * width * near, transcendentals=0, bytes_accessed=200 << 20
        ),
    )(*vectors, qkv_weight, out_weight, rows, cot)


CHUNKS = 4


class CtxReduce:
    def __init__(self, place, block, total, sent, got, sems):
        self.place, self.block, self.total = place, block, total
        self.sent, self.got, self.sems = sent, got, sems
        self.size = total.shape[1] // CHUNKS

    def chunk(self, j):
        return pl.ds(j * self.size, self.size)

    def copy(self, kind, j):
        way = kind if kind else 1 + j % 2
        return remote(
            self.sent.at[kind, self.chunk(j)], self.got.at[kind, self.chunk(j)],
            self.sems.at[0, kind, j], self.sems.at[1, kind, j], self.place.across(way),
        )

    def start(self):
        self.start_far()
        self.start_near()

    def start_far(self):
        self.sent[0] = self.block(self.place.other(3)).astype(bf16)
        for j in range(CHUNKS):
            self.copy(0, j).start()

    def start_near(self):
        place = self.place
        for kind in (1, 2):
            self.total[kind - 1] = self.block(place.other(kind))
            for j in range(CHUNKS):
                if kind == 1 + j % 2:
                    self.sent[kind, self.chunk(j)] = self.total[kind - 1, self.chunk(j)].astype(bf16)
                    self.copy(kind, j).start()

    def relay(self):
        for j in range(CHUNKS):
            kind = 2 - j % 2
            self.copy(0, j).wait_recv()
            share = self.total[kind - 1, self.chunk(j)] + self.got[0, self.chunk(j)].astype(f32)
            self.sent[kind, self.chunk(j)] = share.astype(bf16)
            self.copy(kind, j).start()
        self.total[0] = self.block(self.place.col)

    def sum(self, j):
        for kind in (1, 2):
            self.copy(kind, j).wait_recv()
        rows = self.chunk(j)
        return self.total[0, rows] + self.got[1, rows].astype(f32) + self.got[2, rows].astype(f32)

    def finish(self):
        for kind in range(3):
            for j in range(CHUNKS):
                self.copy(kind, j).wait_send()

    @staticmethod
    def scratch(size, width):
        return [
            pltpu.VMEM((2, size, width), f32),
            pltpu.VMEM((3, size, width), bf16),
            pltpu.VMEM((3, size, width), bf16),
            pltpu.SemaphoreType.DMA((2, 3, CHUNKS)),
        ]


class CtxSpread:
    def __init__(self, place, made, full, sems):
        self.place, self.made, self.full, self.sems = place, made, full, sems
        self.size = made.shape[0] // CHUNKS

    def rows(self, col, j):
        at = (col * CHUNKS + j) * self.size
        return self.full.at[pl.ds(pl.multiple_of(at, self.size), self.size), :]

    def copy(self, kind, j):
        place = self.place
        if kind < 2:
            part, there = self.made.at[pl.ds(j * self.size, self.size), :], self.rows(place.col, j)
            way = 1 + kind
        else:
            way = 2 - j % 2
            part = there = self.rows(place.other(3 - way), j)
        return remote(part, there, self.sems.at[0, kind, j], self.sems.at[1, kind, j], place.across(way))

    def arrived(self, kind, j):
        part = self.rows(self.place.other(kind + 1), j)
        remote(
            part, part, self.sems.at[0, kind, j], self.sems.at[1, kind, j], self.place.across(1)
        ).wait_recv()

    def local(self, j):
        part = self.made.at[pl.ds(j * self.size, self.size), :]
        return pltpu.make_async_copy(part, self.rows(self.place.col, j), self.sems.at[0, 3, j])

    def send(self, j):
        self.copy(0, j).start()
        self.copy(1, j).start()
        self.local(j).start()

    def relay(self, j):
        way = 2 - j % 2
        self.arrived(2 - way, j)
        self.copy(2, j).start()

    def finish(self):
        for j in range(CHUNKS):
            way = 2 - j % 2
            self.arrived(way - 1, j)
            self.arrived(2, j)
            self.local(j).wait()
            for kind in range(3):
                self.copy(kind, j).wait_send()

    @staticmethod
    def scratch():
        return pltpu.SemaphoreType.DMA((2, 4, CHUNKS))


def rows_of(ref, col, size):
    return ref[pl.ds(pl.multiple_of(col * size, size), size), :]


def mix_kernel(
    dp, ctx, attended_ref, weight_ref, rows_ref, gain_ref, shift_ref, resid_hbm, wide_ref,
    total, sent, got, made, resid_ref, reduce_sem, spread_sem, resid_sem,
):
    place = Place(dp)
    greet(place, ctx)
    size = rows_ref.shape[0]
    reduce = CtxReduce(
        place, lambda col: dot(rows_of(attended_ref, col, size), weight_ref[...]), total, sent, got, reduce_sem
    )
    spread = CtxSpread(place, made, wide_ref, spread_sem)
    reduce.start()
    reduce.relay()

    def resid_copy(j):
        rows = reduce.chunk(j)
        return pltpu.make_async_copy(resid_ref.at[rows, :], resid_hbm.at[rows, :], resid_sem.at[j])

    for j in range(CHUNKS):
        rows = reduce.chunk(j)
        resid = rows_ref[rows, :].astype(f32) + reduce.sum(j)
        resid_ref[rows, :] = resid
        resid_copy(j).start()
        scaled, _ = norm_stats(resid)
        made[rows, :] = (scaled * gain_ref[...] + shift_ref[...]).astype(bf16)
        spread.send(j)
        if j:
            spread.relay(j - 1)
    spread.relay(CHUNKS - 1)
    spread.finish()
    reduce.finish()
    for j in range(CHUNKS):
        resid_copy(j).wait()


def mix(dp, ctx, attended, weight, rows, gain, shift):
    size, width = rows.shape
    vmem = pl.BlockSpec(memory_space=pltpu.VMEM)
    return pl.pallas_call(
        functools.partial(mix_kernel, dp, ctx),
        in_specs=[vmem] * 5,
        out_specs=[HBM, HBM],
        out_shape=[jax.ShapeDtypeStruct((size, width), f32), jax.ShapeDtypeStruct((ctx * size, width), bf16)],
        scratch_shapes=CtxReduce.scratch(size, width)[:3]
        + [
            pltpu.VMEM((size, width), bf16),
            pltpu.VMEM((size, width), f32),
            CtxReduce.scratch(size, width)[3],
            CtxSpread.scratch(),
            pltpu.SemaphoreType.DMA((CHUNKS,)),
        ],
        compiler_params=pltpu.CompilerParams(
            collective_id=2, has_side_effects=True, vmem_limit_bytes=40 << 20
        ),
        cost_estimate=pl.CostEstimate(
            flops=2 * attended.size * width, transcendentals=0, bytes_accessed=180 << 20
        ),
    )(attended, weight, rows, gain.reshape(1, width), shift.reshape(1, width))


def mix_back_kernel(
    dp, ctx, gate_ref, up_ref, gate_weight_hbm, up_weight_hbm, inner_hbm, down_hbm, normed_hbm,
    resid_ref, cot_ref, gain_ref,
    d_resid_hbm, sums_ref, wide_ref, branch_hbm, d_up_hbm,
    total, sent, got, made, d_resid_ref, gate_weight_ref, up_weight_ref, inner_ref, down_ref, normed_ref, branch, d_up,
    reduce_sem, spread_sem, load_sem, branch_sem, d_up_sem, d_resid_sem,
):
    place = Place(dp)
    loads = [
        pltpu.make_async_copy(src, dst, load_sem.at[i])
        for i, (src, dst) in enumerate(
            (
                (gate_weight_hbm, gate_weight_ref), (up_weight_hbm, up_weight_ref), (normed_hbm, normed_ref),
                (inner_hbm, inner_ref), (down_hbm, down_ref),
            )
        )
    ]
    for load in loads[:2]:
        load.start()
    greet(place, ctx)
    size, width = cot_ref.shape
    cols = width // ctx // 2
    for load in loads[:2]:
        load.wait()

    def block(col):
        return dot_nt(rows_of(gate_ref, col, size), gate_weight_ref[...]) + dot_nt(
            rows_of(up_ref, col, size), up_weight_ref[...]
        )

    def d_up_copy(i):
        return pltpu.make_async_copy(
            d_up.at[i % 2], d_up_hbm.at[pl.ds(i * cols, cols), :], d_up_sem.at[i % 2]
        )

    def branch_copy(i):
        return pltpu.make_async_copy(
            branch.at[i % 2], branch_hbm.at[pl.ds(i * size, size), :], branch_sem.at[i % 2]
        )

    def d_up_piece(i):
        if i == 0:
            loads[2].wait()
        if i > 1:
            d_up_copy(i - 2).wait()
        d_up[i % 2] = dot_tn(normed_ref[:, i * cols : (i + 1) * cols], up_ref[...]).astype(bf16)
        d_up_copy(i).start()

    def branch_piece(i):
        if i == 0:
            loads[3].wait()
            loads[4].wait()
        if i > 1:
            branch_copy(i - 2).wait()
        branch[i % 2] = dot(inner_ref[i * size : (i + 1) * size, :], down_ref[...]).astype(bf16)
        branch_copy(i).start()

    def d_resid_copy(j):
        rows = reduce.chunk(j)
        return pltpu.make_async_copy(d_resid_ref.at[rows, :], d_resid_hbm.at[rows, :], d_resid_sem.at[j])

    pieces = [functools.partial(d_up_piece, i) for i in range(2 * ctx)]
    pieces += [functools.partial(branch_piece, i) for i in range(ctx)]

    reduce = CtxReduce(place, block, total, sent, got, reduce_sem)
    spread = CtxSpread(place, made, wide_ref, spread_sem)
    reduce.start()
    for load in loads[2:]:
        load.start()
    reduce.relay()
    sums_ref[...] = jnp.zeros_like(sums_ref)
    for j in range(CHUNKS):
        for piece in pieces[2 * j : 2 * j + 2]:
            piece()
        rows = reduce.chunk(j)
        scaled, inv_std = norm_stats(resid_ref[rows, :])
        grad, d_gain, d_shift = norm_backward(reduce.sum(j), scaled, inv_std, gain_ref[...])
        sums_ref[0:1, :] += d_gain[None]
        sums_ref[1:2, :] += d_shift[None]
        grad = cot_ref[rows, :].astype(f32) + grad
        d_resid_ref[rows, :] = grad
        d_resid_copy(j).start()
        made[rows, :] = grad.astype(bf16)
        spread.send(j)
        if j:
            spread.relay(j - 1)
    pieces[2 * CHUNKS]()
    spread.relay(CHUNKS - 1)
    for piece in pieces[2 * CHUNKS + 1 :]:
        piece()
    spread.finish()
    reduce.finish()
    for i in (1, 2):
        d_up_copy(2 * ctx - i).wait()
        branch_copy(ctx - i).wait()
    for j in range(CHUNKS):
        d_resid_copy(j).wait()


def mix_back(dp, ctx, d_gate, d_up, gate_weight, up_weight, inner, down, normed, resid, cot, gain):
    size, width = cot.shape
    hidden = d_up.shape[1]
    vmem = pl.BlockSpec(memory_space=pltpu.VMEM)
    return pl.pallas_call(
        functools.partial(mix_back_kernel, dp, ctx),
        in_specs=[vmem] * 2 + [HBM] * 5 + [vmem] * 3,
        out_specs=[HBM, vmem, HBM, HBM, HBM],
        out_shape=[
            jax.ShapeDtypeStruct((size, width), f32),
            jax.ShapeDtypeStruct((2, width), f32),
            jax.ShapeDtypeStruct((ctx * size, width), bf16),
            jax.ShapeDtypeStruct((ctx * size, width), bf16),
            jax.ShapeDtypeStruct((width, hidden), bf16),
        ],
        scratch_shapes=CtxReduce.scratch(size, width)[:3]
        + [
            pltpu.VMEM((size, width), bf16),
            pltpu.VMEM((size, width), f32),
            pltpu.VMEM((width, hidden), bf16),
            pltpu.VMEM((width, hidden), bf16),
            pltpu.VMEM((ctx * size, hidden), bf16),
            pltpu.VMEM((hidden, width), bf16),
            pltpu.VMEM((ctx * size, width), bf16),
            pltpu.VMEM((2, size, width), bf16),
            pltpu.VMEM((2, width // ctx // 2, hidden), bf16),
            CtxReduce.scratch(size, width)[3],
            CtxSpread.scratch(),
            pltpu.SemaphoreType.DMA((5,)),
            pltpu.SemaphoreType.DMA((2,)),
            pltpu.SemaphoreType.DMA((2,)),
            pltpu.SemaphoreType.DMA((CHUNKS,)),
        ],
        compiler_params=pltpu.CompilerParams(
            collective_id=3, has_side_effects=True, vmem_limit_bytes=60 << 20
        ),
        cost_estimate=pl.CostEstimate(
            flops=8 * d_gate.size * width, transcendentals=0, bytes_accessed=180 << 20
        ),
    )(d_gate, d_up, gate_weight, up_weight, inner, down, normed, resid, cot, gain.reshape(1, width))


class LineReduce:
    def __init__(self, place, parts, own, pair, got, sems):
        self.place, self.parts, self.own, self.pair, self.got, self.sems = place, parts, own, pair, got, sems

    def load(self, line):
        return pltpu.make_async_copy(
            self.parts.at[2 * line + self.place.core], self.own.at[line], self.sems.at[6, line]
        )

    def swap(self, line):
        row = 2 * line + 1 - self.place.core
        return remote(
            self.parts.at[row], self.pair.at[line], self.sems.at[0, line], self.sems.at[1, line], self.place.twin
        )

    def start(self):
        for line in range(self.place.lines):
            self.swap(line).start()

    def add(self):
        for line in range(self.place.lines):
            self.load(line).wait()
            self.swap(line).wait_recv()
            self.pair[line] = (self.own[line].astype(f32) + self.pair[line].astype(f32)).astype(bf16)

    def up(self, far):
        part = self.place.line + far
        return remote(
            self.pair.at[part], self.got.at[part], self.sems.at[2, far], self.sems.at[3, far], self.place.above()
        )

    def down(self, far):
        part = self.place.line - far
        slot = part if far > 1 else self.place.lines
        return remote(
            self.pair.at[part], self.got.at[slot], self.sems.at[4, far], self.sems.at[5, far], self.place.below()
        )

    def came_up(self, far):
        slot = self.got.at[self.place.line + far]
        remote(slot, slot, self.sems.at[2, far + 1], self.sems.at[3, far + 1], self.place.twin).wait_recv()

    def came_down(self, far):
        slot = self.got.at[self.place.line - far if far else self.place.lines]
        remote(slot, slot, self.sems.at[4, far + 1], self.sems.at[5, far + 1], self.place.twin).wait_recv()

    def send(self, far):
        place = self.place

        @pl.when(place.line + far < place.lines)
        def _():
            @pl.when(place.line > 0)
            def _():
                self.came_up(far)
                part = place.line + far
                self.pair[part] = (self.pair[part].astype(f32) + self.got[part].astype(f32)).astype(bf16)

            self.up(far).start()

        @pl.when(place.line - far >= 0)
        def _():
            @pl.when(place.line < place.lines - 1)
            def _():
                self.came_down(far)
                part = place.line - far
                self.pair[part] = (self.pair[part].astype(f32) + self.got[part].astype(f32)).astype(bf16)

            self.down(far).start()

    def collect(self, out):
        place = self.place
        out[...] = self.pair[place.line].astype(f32)

        @pl.when(place.line > 0)
        def _():
            self.came_up(0)
            out[...] += self.got[place.line].astype(f32)

        @pl.when(place.line < place.lines - 1)
        def _():
            self.came_down(0)
            out[...] += self.got[place.lines].astype(f32)

    def finish(self):
        place = self.place
        for line in range(place.lines):
            self.swap(line).wait_send()
        for far in range(1, place.lines):
            pl.when(place.line + far < place.lines)(lambda: self.up(far).wait_send())
            pl.when(place.line - far >= 0)(lambda: self.down(far).wait_send())

    @staticmethod
    def scratch(dp, tile):
        return [
            pltpu.VMEM((dp // 2,) + tile, bf16),
            pltpu.VMEM((dp // 2,) + tile, bf16),
            pltpu.VMEM((dp // 2 + 1,) + tile, bf16),
            pltpu.SemaphoreType.DMA((7, dp // 2)),
        ]


class CtxReduceReady:
    def __init__(self, place, full, have, got, sems, load_sems):
        self.place, self.full, self.have, self.got, self.sems, self.load_sems = place, full, have, got, sems, load_sems
        self.height = have.shape[1]
        self.size = self.height // CHUNKS

    def chunk(self, j):
        return pl.ds(j * self.size, self.size)

    def load(self, kind):
        col = self.place.other(kind)
        rows = pl.ds(pl.multiple_of(col * self.height, self.height), self.height)
        return pltpu.make_async_copy(self.full.at[rows, :], self.have.at[kind], self.load_sems.at[kind])

    def copy(self, kind, j):
        place = self.place
        if kind:
            part, way = self.have.at[kind, self.chunk(j)], kind
        else:
            at = (place.other(3) * CHUNKS + j) * self.size
            part, way = self.full.at[pl.ds(pl.multiple_of(at, self.size), self.size), :], 1 + j % 2
        return remote(
            part, self.got.at[kind, self.chunk(j)], self.sems.at[0, kind, j], self.sems.at[1, kind, j],
            place.across(way),
        )

    def start(self):
        for j in range(CHUNKS):
            self.copy(0, j).start()
        for kind in (1, 2):
            self.load(kind).wait()
            for j in range(CHUNKS):
                if kind == 1 + j % 2:
                    self.copy(kind, j).start()

    def relay(self):
        for j in range(CHUNKS):
            kind, rows = 2 - j % 2, self.chunk(j)
            self.copy(0, j).wait_recv()
            share = self.have[kind, rows].astype(f32) + self.got[0, rows].astype(f32)
            self.have[kind, rows] = share.astype(bf16)
            self.copy(kind, j).start()

    def sum(self, j):
        for kind in (1, 2):
            self.copy(kind, j).wait_recv()
        rows = self.chunk(j)
        return self.have[0, rows].astype(f32) + self.got[1, rows].astype(f32) + self.got[2, rows].astype(f32)

    def finish(self):
        for kind in range(3):
            for j in range(CHUNKS):
                self.copy(kind, j).wait_send()


def closing_kernel(
    dp, ctx,
    d_joined_hbm, weight_hbm, qkv_parts, out_parts, branch_hbm, rows_hbm, d_resid_hbm, resid_hbm,
    gain_ref, sums_two_ref, bias_ref,
    grad_ref, qkv_ref, out_ref, output_ref, vectors_ref, d_bias_ref,
    d_joined_ref, weight_ref, rows_ref, d_resid_ref, resid_ref, load_sem,
    total, sent, got, reduce_sem, qkv_own, qkv_pair, qkv_got, qkv_sem, out_own, out_pair, out_got, out_sem,
    have, branch_got, branch_sem, branch_load_sem,
    sums, tiles, tiles_got, small, small_sem, mine, swap_out, swap_in, swap_sem,
):
    place = Place(dp)
    me, row = place.col, place.row
    lines = [
        LineReduce(place, qkv_parts, qkv_own, qkv_pair, qkv_got, qkv_sem),
        LineReduce(place, out_parts, out_own, out_pair, out_got, out_sem),
    ]
    loads = [
        pltpu.make_async_copy(src, dst, load_sem.at[i])
        for i, (src, dst) in enumerate(
            (
                (d_joined_hbm, d_joined_ref), (weight_hbm, weight_ref), (rows_hbm, rows_ref),
                (d_resid_hbm, d_resid_ref), (resid_hbm, resid_ref),
            )
        )
    ]
    for load in loads[:2]:
        load.start()
    greet_all(place, dp, ctx)
    for line in lines:
        line.start()
    for i in range(place.lines):
        for line in lines:
            line.load(i).start()
    branch = CtxReduceReady(place, branch_hbm, have, branch_got, branch_sem, branch_load_sem)
    for kind in range(3):
        branch.load(kind).start()
    for load in loads[2:]:
        load.start()

    size, width = rows_ref.shape
    for load in loads[:2]:
        load.wait()
    reduce = CtxReduce(
        place, lambda col: dot_nt(rows_of(d_joined_ref, col, size), weight_ref[...]), total, sent, got, reduce_sem
    )
    reduce.start_far()
    for line in lines:
        line.add()
        line.send(place.lines - 1)
    reduce.start_near()
    branch.start()
    reduce.relay()
    for far in range(place.lines - 2, 1, -1):
        for line in lines:
            line.send(far)

    sums[...] = jnp.zeros_like(sums)
    for load in loads[2:]:
        load.wait()
    branch.load(0).wait()
    for j in range(CHUNKS):
        rows = reduce.chunk(j)
        scaled, inv_std = norm_stats(rows_ref[rows, :].astype(f32))
        grad, d_gain, d_shift = norm_backward(reduce.sum(j), scaled, inv_std, gain_ref[...])
        sums[0:1, :] += d_gain[None]
        sums[1:2, :] += d_shift[None]
        grad_ref[rows, :] = d_resid_ref[rows, :] + grad
    branch.relay()
    if place.lines > 2:
        for line in lines:
            line.send(1)

    part = width // dp
    tiles[...] = jnp.zeros_like(tiles)
    for i in range(dp):
        lanes = slice(i * part, (i + 1) * part)
        tiles[i, 0:2, :] = sums[:, lanes]
        tiles[i, 2:4, :] = sums_two_ref[:, lanes]
        tiles[i, 4:5, :] = bias_ref[i : i + 1, :]
    sends = [
        remote(tiles.at[(row + k) % dp], tiles_got.at[k], small_sem.at[0, k], small_sem.at[1, k], ((row + k) % dp, me))
        for k in range(1, dp)
    ]
    for copy in sends:
        copy.start()
    tile = tiles[row]
    for k in range(1, dp):
        sends[k - 1].wait()
        tile = tile + tiles_got[k]
    tiles_got[0] = tile
    small[me] = tile
    spreads = [
        remote(tiles_got.at[0], small.at[me], small_sem.at[2, k], small_sem.at[3, k], place.across(k))
        for k in range(1, ctx)
    ]
    for copy in spreads:
        copy.start()

    for j in range(CHUNKS):
        rows = branch.chunk(j)
        output_ref[rows, :] = (resid_ref[rows, :] + branch.sum(j)).astype(bf16)

    for k in range(1, ctx):
        spreads[k - 1].wait_send()
        part = small.at[place.other(k)]
        remote(part, part, small_sem.at[2, k], small_sem.at[3, k], place.across(k)).wait_recv()
    four = sum(small[c, 0:4, :] for c in range(ctx))
    piece = vectors_ref.shape[1]
    slots = d_bias_ref.shape[1] // HD
    vectors = four[:, :piece]
    biases = [small[i % ctx, 4:5, i // ctx * HD : (i // ctx + 1) * HD] for i in range(slots * ctx)]
    chosen = biases[:slots]
    for c in range(1, ctx):
        vectors = jnp.where(me == c, four[:, c * piece : (c + 1) * piece], vectors)
        chosen = [jnp.where(me == c, biases[slots * c + i], chosen[i]) for i in range(slots)]
    vectors_ref[...] = vectors
    for i in range(slots):
        d_bias_ref[:, i * HD : (i + 1) * HD] = chosen[i]

    lines[0].collect(mine)
    depth = mine.shape[0] // ctx
    swap_out[...] = mine[...].astype(bf16)
    swaps = [
        remote(
            swap_out.at[pl.ds(pl.multiple_of(place.other(k) * depth, depth), depth), :], swap_in.at[me],
            swap_sem.at[0, k], swap_sem.at[1, k], place.across(k),
        )
        for k in range(1, ctx)
    ]
    for copy in swaps:
        copy.start()
    swap_in[me] = rows_of(swap_out, me, depth)
    lines[1].collect(out_ref)
    for k in range(1, ctx):
        part = swap_in.at[place.other(k)]
        remote(part, part, swap_sem.at[0, k], swap_sem.at[1, k], place.across(k)).wait_recv()
    low = head_lanes((depth, PAIR))
    for p in range(mine.shape[1] // (3 * PAIR)):
        for t in range(3):
            lanes = slice((3 * p + t) * PAIR, (3 * p + t + 1) * PAIR)
            for c in range(0, ctx, 2):
                a = swap_in[c, :, lanes].astype(f32)
                b = swap_in[c + 1, :, lanes].astype(f32)
                at = t * width + (2 * p * ctx + c) * HD
                qkv_ref[:, at : at + PAIR] = jnp.where(low, a, pltpu.roll(b, HD, 1))
                at = at + ctx * HD
                qkv_ref[:, at : at + PAIR] = jnp.where(low, pltpu.roll(a, HD, 1), b)
    for copy in swaps:
        copy.wait_send()
    for line in lines:
        line.finish()
    branch.finish()
    reduce.finish()


def closing(dp, ctx, d_joined, weight, d_qkv, d_out, branch, rows, d_resid, resid, gain, sums_two, bias):
    size, width = rows.shape
    near = weight.shape[1]
    own, tall = width // dp, d_out.shape[0] // dp
    vmem = pl.BlockSpec(memory_space=pltpu.VMEM)
    reduce_scratch = CtxReduce.scratch(size, width)
    max_peers = max(dp, ctx)
    return pl.pallas_call(
        functools.partial(closing_kernel, dp, ctx),
        in_specs=[HBM] * 8 + [vmem] * 3,
        out_specs=[vmem] * 6,
        out_shape=[
            jax.ShapeDtypeStruct((size, width), f32),
            jax.ShapeDtypeStruct((own // ctx, 3 * width), f32),
            jax.ShapeDtypeStruct((tall, width), f32),
            jax.ShapeDtypeStruct((size, width), bf16),
            jax.ShapeDtypeStruct((4, own // ctx), f32),
            jax.ShapeDtypeStruct((1, 3 * own // ctx), f32),
        ],
        scratch_shapes=[
            pltpu.VMEM((ctx * size, near), bf16),
            pltpu.VMEM((width, near), bf16),
            pltpu.VMEM((size, width), bf16),
            pltpu.VMEM((size, width), f32),
            pltpu.VMEM((size, width), f32),
            pltpu.SemaphoreType.DMA((5,)),
        ]
        + reduce_scratch
        + LineReduce.scratch(dp, (own, near))
        + LineReduce.scratch(dp, (tall, width))
        + reduce_scratch[1:]
        + [
            pltpu.SemaphoreType.DMA((3,)),
            pltpu.VMEM((2, width), f32),
            pltpu.VMEM((dp, 8, own), f32),
            pltpu.VMEM((dp, 8, own), f32),
            pltpu.VMEM((ctx, 8, own), f32),
            pltpu.SemaphoreType.DMA((4, max_peers)),
            pltpu.VMEM((own, near), f32),
            pltpu.VMEM((own, near), bf16),
            pltpu.VMEM((ctx, own // ctx, near), bf16),
            pltpu.SemaphoreType.DMA((2, ctx)),
        ],
        compiler_params=pltpu.CompilerParams(
            collective_id=1, has_side_effects=True, vmem_limit_bytes=62 << 20
        ),
        cost_estimate=pl.CostEstimate(
            flops=2 * d_joined.size * width, transcendentals=0, bytes_accessed=200 << 20
        ),
    )(
        d_joined, weight, d_qkv.reshape(dp, own, near), d_out.reshape(dp, tall, width), branch,
        rows, d_resid, resid, gain.reshape(1, width), sums_two, bias,
    )


def turn(x, table_ref):
    return (
        x * table_ref[0]
        + pltpu.roll(x, PAIR - ROT // 2, 1) * table_ref[1]
        + pltpu.roll(x, ROT // 2, 1) * table_ref[2]
    )


def turn_back(x, table_ref):
    return (
        x * table_ref[0]
        - pltpu.roll(x, PAIR - ROT // 2, 1) * table_ref[1]
        - pltpu.roll(x, ROT // 2, 1) * table_ref[2]
    )


def head_lanes(shape):
    return lax.broadcasted_iota(jnp.int32, shape, 1) < HD


def span(full_len, step, at):
    return max(0, (at - DOC_MAX + 1) // step * step), at + step


def block_mask(start, at, step, low, high):
    keys = lax.broadcasted_iota(jnp.int32, (step, high - low), 1) + low
    rows = lax.broadcasted_iota(jnp.int32, (step, high - low), 0) + at
    return (keys >= start) & (keys <= rows)


def attend_kernel(step, joined_ref, bias_ref, table_ref, start_ref, out_ref, qkv_ref, lse_ref):
    full_len = joined_ref.shape[0]
    scale = 1.0 / math.sqrt(HD)
    for t in range(3):
        lanes = slice(t * PAIR, (t + 1) * PAIR)
        x = joined_ref[:, lanes] + bias_ref[:, lanes]
        if t < 2:
            x = turn(x, table_ref)
        qkv_ref[:, lanes] = x.astype(bf16)
    for at in range(0, full_len, step):
        low, high = span(full_len, step, at)
        allowed = block_mask(start_ref[at : at + step, :1], at, step, low, high)
        q = qkv_ref[at : at + step, :PAIR]
        k = qkv_ref[low:high, PAIR : 2 * PAIR]
        v = qkv_ref[low:high, 2 * PAIR :]
        total = jnp.zeros((step, PAIR), f32)
        logs = []
        for head in range(2):
            mine = head_lanes(q.shape) == (head == 0)
            s = dot_nt(jnp.where(mine, q, jnp.zeros_like(q)), k) * scale
            s = jnp.where(allowed, s, masked_value)
            top = jnp.max(s, axis=1, keepdims=True)
            e = jnp.exp(s - top)
            norm = jnp.sum(e, axis=1, keepdims=True)
            probs = (e * (1.0 / norm)).astype(bf16)
            vm = jnp.where(head_lanes(v.shape) == (head == 0), v, jnp.zeros_like(v))
            total = total + dot(probs, vm)
            logs.append(top + jnp.log(norm))
        out_ref[at : at + step, :] = total.astype(bf16)
        lse_ref[at : at + step, :] = jnp.where(head_lanes((step, PAIR)), logs[0], logs[1])


def attend_back_kernel(
    step, qkv_ref, grad_ref, lse_ref, table_ref, start_ref, out_ref, sum_ref, dk_ref, dv_ref
):
    full_len = qkv_ref.shape[0]
    scale = 1.0 / math.sqrt(HD)
    dk_ref[...] = jnp.zeros_like(dk_ref)
    dv_ref[...] = jnp.zeros_like(dv_ref)
    total = jnp.zeros((1, PAIR), f32)
    for at in range(0, full_len, step):
        low, high = span(full_len, step, at)
        rows = slice(at, at + step)
        keys = slice(low, high)
        allowed = block_mask(start_ref[rows, :1], at, step, low, high)
        q = qkv_ref[rows, :PAIR]
        k = qkv_ref[keys, PAIR : 2 * PAIR]
        v = qkv_ref[keys, 2 * PAIR :]
        g = grad_ref[rows, :]
        dq = jnp.zeros((step, PAIR), f32)
        dk = jnp.zeros((high - low, PAIR), f32)
        dv = jnp.zeros((high - low, PAIR), f32)
        for head in range(2):
            mine = head_lanes(q.shape) == (head == 0)
            qm = jnp.where(mine, q, jnp.zeros_like(q))
            gm = jnp.where(mine, g, jnp.zeros_like(g))
            km = jnp.where(head_lanes(k.shape) == (head == 0), k, jnp.zeros_like(k))
            s = dot_nt(qm, k) * scale
            probs = jnp.where(
                allowed, jnp.exp(s - lse_ref[rows, head * HD : head * HD + 1]), 0.0
            )
            dp = dot_nt(gm, v)
            mean = jnp.sum(dp * probs, axis=1, keepdims=True)
            ds = (probs * (dp - mean)).astype(bf16)
            dq = dq + dot(ds, km)
            dk = dk + dot_tn(ds, qm)
            dv = dv + dot_tn(probs.astype(bf16), gm)
        dk_ref[keys, :] += dk
        dv_ref[keys, :] += dv
        dq = turn_back(dq * scale, table_ref.at[:, rows, :]).astype(bf16)
        out_ref[rows, :PAIR] = dq
        total = total + jnp.sum(dq.astype(f32), axis=0, keepdims=True)
    sum_ref[:, :PAIR] = total
    dk = turn_back(dk_ref[...] * scale, table_ref).astype(bf16)
    out_ref[:, PAIR : 2 * PAIR] = dk
    sum_ref[:, PAIR : 2 * PAIR] = jnp.sum(dk.astype(f32), axis=0, keepdims=True)
    dv = dv_ref[...].astype(bf16)
    out_ref[:, 2 * PAIR :] = dv
    sum_ref[:, 2 * PAIR :] = jnp.sum(dv.astype(f32), axis=0, keepdims=True)


def whole(shape):
    return pl.BlockSpec(shape, lambda p: (0,) * len(shape))


def attend_step(full_len):
    return min(256, full_len)


def attend(joined, bias, table, start):
    full_len, width = joined.shape
    pairs = width // (3 * PAIR)
    step = attend_step(full_len)
    seen = sum(span(full_len, step, at)[1] - span(full_len, step, at)[0] for at in range(0, full_len, step)) * step
    wide = pl.BlockSpec((full_len, 3 * PAIR), lambda p: (0, p))
    thin = pl.BlockSpec((full_len, PAIR), lambda p: (0, p))
    return pl.pallas_call(
        functools.partial(attend_kernel, step),
        grid=(pairs,),
        in_specs=[
            wide,
            pl.BlockSpec((1, 3 * PAIR), lambda p: (0, p)),
            whole(table.shape),
            whole(start.shape),
        ],
        out_specs=[thin, wide, thin],
        out_shape=[
            jax.ShapeDtypeStruct((full_len, pairs * PAIR), bf16),
            jax.ShapeDtypeStruct((full_len, width), bf16),
            jax.ShapeDtypeStruct((full_len, pairs * PAIR), f32),
        ],
        compiler_params=pltpu.CompilerParams(vmem_limit_bytes=40 << 20),
        cost_estimate=pl.CostEstimate(
            flops=pairs * seen * PAIR * 8, transcendentals=pairs * seen * 2, bytes_accessed=full_len * width * 8
        ),
    )(joined, bias, table, start)


def attend_back(qkv, grad, lse, table, start):
    full_len, width = qkv.shape
    pairs = width // (3 * PAIR)
    step = attend_step(full_len)
    seen = sum(span(full_len, step, at)[1] - span(full_len, step, at)[0] for at in range(0, full_len, step)) * step
    wide = pl.BlockSpec((full_len, 3 * PAIR), lambda p: (0, p))
    thin = pl.BlockSpec((full_len, PAIR), lambda p: (0, p))
    return pl.pallas_call(
        functools.partial(attend_back_kernel, step),
        grid=(pairs,),
        in_specs=[wide, thin, thin, whole(table.shape), whole(start.shape)],
        out_specs=[wide, pl.BlockSpec((1, 3 * PAIR), lambda p: (0, p))],
        out_shape=[
            jax.ShapeDtypeStruct((full_len, width), bf16),
            jax.ShapeDtypeStruct((1, width), f32),
        ],
        scratch_shapes=[pltpu.VMEM((full_len, PAIR), f32), pltpu.VMEM((full_len, PAIR), f32)],
        compiler_params=pltpu.CompilerParams(vmem_limit_bytes=40 << 20),
        cost_estimate=pl.CostEstimate(
            flops=pairs * seen * PAIR * 20, transcendentals=pairs * seen * 2, bytes_accessed=full_len * width * 8
        ),
    )(qkv, grad, lse, table, start)


def rotary_table(full_len):
    half = ROT // 2
    inverse = 10000.0 ** (-2.0 * np.arange(half) / ROT)
    angles = np.arange(full_len)[:, None] * inverse[None, :]
    table = np.zeros((3, full_len, HD), np.float32)
    table[0, :, :half] = table[0, :, half:ROT] = np.cos(angles)
    table[0, :, ROT:] = 1.0
    table[1, :, :half] = -np.sin(angles)
    table[2, :, half:ROT] = np.sin(angles)
    return jnp.asarray(np.concatenate([table, table], axis=2))


def shards(
    dp,
    ctx,
    inputs,
    segments,
    ln1_gain,
    ln1_bias,
    qkv_weight,
    qkv_bias,
    out_weight,
    ln2_gain,
    ln2_bias,
    gate_weight,
    up_weight,
    down_weight,
    cotangent,
):
    local_len, width = inputs.shape[1], inputs.shape[2]
    full_len = segments.shape[1]
    heads = width // HD
    near = heads // ctx
    pairs = near // 2
    me = lax.axis_index("ctx")
    own = me * local_len

    part = ln1_gain.shape[0]
    vectors = [v[None, :] for v in (ln1_gain, ln1_bias, ln2_gain, ln2_bias, qkv_bias)]
    count = 4 * part + qkv_bias.shape[0]
    rows_here = qkv_weight.shape[0]
    rows, grad_rows = inputs[0], cotangent[0]
    fused = ctx == 4 and dp % 2 == 0 and part == HD
    if fused:
        small, params, joined_weight, out_full, normed_one, joined, grad_wide = opening(
            dp, ctx, vectors, qkv_weight, out_weight, rows, grad_rows
        )
        gain_one, shift_one, gain_two, shift_two = params
        up_weight, down_weight, _ = lax.optimization_barrier((up_weight, down_weight, normed_one))
        small = small.reshape(dp * ctx, 1024)[:, :count]
    else:
        small = jnp.concatenate(vectors, axis=1).astype(f32)
        small = lax.all_gather(small, ("dp", "ctx"), axis=0, tiled=True)
        blocks = qkv_weight.reshape(rows_here, 3, pairs, 2, ctx, HD).transpose(4, 0, 2, 1, 3, 5)
        blocks = exchange_ctx(blocks.reshape(ctx, rows_here, near * 3 * HD), ctx)
        joined_weight = lax.all_gather(
            blocks.reshape(ctx * rows_here, near * 3 * HD), "dp", axis=0, tiled=True
        )
        out_full = lax.all_gather(out_weight, ("dp", "ctx"), axis=0, tiled=True)
        out_full = out_full.reshape(near, ctx, HD, width)
        out_full = lax.dynamic_index_in_dim(out_full, me, 1, keepdims=False)
        out_full = out_full.reshape(near * HD, width)
        gain_one, shift_one, gain_two, shift_two = [
            small[:, i * part : (i + 1) * part].reshape(width) for i in range(4)
        ]
        scaled_wide, _ = norm_stats(gather_ctx(rows, ctx).astype(f32))
        normed_one = (scaled_wide * gain_one + shift_one).astype(bf16)
        grad_wide = gather_ctx(grad_rows, ctx)
    bias = small[:, 4 * part :].reshape(3, pairs, 2, ctx, HD)
    bias = lax.dynamic_index_in_dim(bias, me, 3, keepdims=False)
    bias = bias.transpose(1, 0, 2, 3).reshape(1, near * 3 * HD)
    gate_full = lax.all_gather(gate_weight, "dp", axis=0, tiled=True)
    up_full = lax.all_gather(up_weight, "dp", axis=0, tiled=True)
    down_full = lax.all_gather(down_weight, "dp", axis=1, tiled=True)

    segment = segments[0]
    start = jnp.sum((segment[None, :] < segment[:, None]).astype(jnp.int32), axis=1)
    start = jnp.broadcast_to(start[:, None], (full_len, 128))
    table = rotary_table(full_len)
    if not fused:
        joined = dot(normed_one, joined_weight)
    attended, qkv, lse = attend(joined, bias, table, start)
    if fused:
        resid, normed_wide = mix(dp, ctx, attended, out_full, rows, gain_two, shift_two)
    else:
        resid = rows.astype(f32) + scatter_ctx(dot(attended, out_full), ctx)
        scaled_two, inv_two = norm_stats(resid)
        normed_wide = gather_ctx((scaled_two * gain_two + shift_two).astype(bf16), ctx)

    gate = dot(normed_wide, gate_full)
    upward = dot(normed_wide, up_full)
    sigma = jax.nn.sigmoid(gate)
    swish = gate * sigma
    inner = (swish * upward).astype(bf16)
    d_down = dot_tn(inner, grad_wide).astype(bf16)
    grad_wide, d_down = lax.optimization_barrier((grad_wide, d_down))
    d_down = lax.psum_scatter(d_down, "dp", scatter_dimension=1, tiled=True).astype(f32)
    d_inner = dot_nt(grad_wide, down_full)
    d_gate = (d_inner * upward * sigma * (1.0 + gate * (1.0 - sigma))).astype(bf16)
    d_upward = (d_inner * swish).astype(bf16)
    d_gate_weight = dot_tn(normed_wide, d_gate).astype(bf16)
    d_gate_ready, d_gate_weight = lax.optimization_barrier((d_gate, d_gate_weight))
    d_gate_weight = lax.psum_scatter(d_gate_weight, "dp", scatter_dimension=0, tiled=True).astype(f32)
    if fused:
        d_resid, sums_two, d_proj, branch, d_up_weight = mix_back(
            dp, ctx, d_gate_ready, d_upward, gate_full, up_full, inner, down_full, normed_wide, resid,
            grad_rows, gain_two,
        )
    else:
        branch = dot(inner, down_full)
        d_up_weight = dot_tn(normed_wide, d_upward).astype(bf16)
        d_normed_two = scatter_ctx(dot_nt(d_gate, gate_full) + dot_nt(d_upward, up_full), ctx)
        grad, d_gain_two, d_shift_two = norm_backward(d_normed_two, scaled_two, inv_two, gain_two)
        d_resid = grad_rows.astype(f32) + grad
        d_proj = gather_ctx(d_resid.astype(bf16), ctx)
    d_up_weight = lax.psum_scatter(d_up_weight, "dp", scatter_dimension=0, tiled=True).astype(f32)

    d_attended = dot_nt(d_proj, out_full).astype(bf16)
    d_out_weight = dot_tn(attended, d_proj).astype(bf16)
    d_attended, d_down = lax.optimization_barrier((d_attended, d_down))
    d_joined, d_bias = attend_back(qkv, d_attended, lse, table, start)
    d_joined_weight = dot_tn(normed_one, d_joined).astype(bf16)
    d_bias = d_bias.reshape(pairs, 3, 2, HD).transpose(1, 0, 2, 3)
    d_joined, d_gate_weight = lax.optimization_barrier((d_joined, d_gate_weight))
    if fused:
        d_bias = jnp.pad(d_bias.reshape(dp, -1), ((0, 0), (0, width // dp - near * 3 * HD // dp)))
        grad_input, d_joined_weight, d_out_weight, output, vectors, d_bias = closing(
            dp, ctx, d_joined, joined_weight, d_joined_weight, d_out_weight, branch, rows, d_resid, resid,
            gain_one, sums_two, d_bias,
        )
        d_gain_one, d_shift_one, d_gain_two, d_shift_two = vectors
        d_bias = d_bias[0]
    else:
        output = (resid + scatter_ctx(branch, ctx)).astype(bf16)
        at_me = lax.broadcasted_iota(jnp.int32, (1, ctx, 1, 1), 1) == me
        d_out_weight = jnp.where(at_me, d_out_weight.reshape(near, 1, HD, width), jnp.zeros((), bf16))
        d_out_weight = lax.psum_scatter(
            d_out_weight.reshape(width, width), ("dp", "ctx"), scatter_dimension=0, tiled=True
        ).astype(f32)
        d_normed_one = scatter_ctx(dot_nt(d_joined, joined_weight), ctx)
        scaled_one, inv_one = norm_stats(rows.astype(f32))
        grad, d_gain_one, d_shift_one = norm_backward(d_normed_one, scaled_one, inv_one, gain_one)
        grad_input = d_resid + grad
        d_joined_weight = lax.psum_scatter(d_joined_weight, "dp", scatter_dimension=0, tiled=True)
        blocks = exchange_ctx(d_joined_weight.reshape(ctx, rows_here, near * 3 * HD), ctx)
        blocks = blocks.reshape(ctx, rows_here, pairs, 3, 2, HD).transpose(1, 3, 2, 4, 0, 5)
        d_joined_weight = blocks.reshape(rows_here, 3 * width).astype(f32)
        at_me = (lax.broadcasted_iota(jnp.int32, (1, 1, 1, ctx, 1), 3) == me).astype(f32)
        d_bias = (d_bias[:, :, :, None, :] * at_me).reshape(dp * ctx, -1)
        small = jnp.concatenate(
            [t.reshape(dp * ctx, part) for t in (d_gain_one, d_shift_one, d_gain_two, d_shift_two)]
            + [d_bias],
            axis=1,
        )
        small = lax.psum_scatter(small, ("dp", "ctx"), scatter_dimension=0, tiled=True)[0]
        d_gain_one, d_shift_one, d_gain_two, d_shift_two = [
            small[i * part : (i + 1) * part] for i in range(4)
        ]
        d_bias = small[4 * part :]
    return (
        output[None],
        grad_input[None],
        d_gain_one,
        d_shift_one,
        d_joined_weight,
        d_bias,
        d_out_weight,
        d_gain_two,
        d_shift_two,
        d_gate_weight,
        d_up_weight,
        d_down,
    )


def solution(mesh):
    every = ("dp", "ctx")
    return jax.shard_map(
        functools.partial(shards, mesh.shape["dp"], mesh.shape["ctx"]),
        mesh=mesh,
        in_specs=(
            P("dp", "ctx", None),
            P("dp", None),
            P(every),
            P(every),
            P(every, None),
            P(every),
            P(every, None),
            P(every),
            P(every),
            P("dp", "ctx"),
            P("dp", "ctx"),
            P("ctx", "dp"),
            P("dp", "ctx", None),
        ),
        out_specs=(
            P("dp", "ctx", None),
            P("dp", "ctx", None),
            P(every),
            P(every),
            P(every, None),
            P(every),
            P(every, None),
            P(every),
            P(every),
            P("dp", "ctx"),
            P("dp", "ctx"),
            P("ctx", "dp"),
        ),
        check_vma=False,
    )
```

```python
import functools
import math

import jax
import jax.numpy as jnp
import numpy as np
from jax import lax
from jax.experimental import pallas as pl
from jax.experimental.pallas import tpu as pltpu
from jax.sharding import PartitionSpec as P

HD = 64
ROT = 16
DOC_MAX = 512
PAIR = 2 * HD

norm_eps = 1e-05
masked_value = -1e30
f32 = jnp.float32
bf16 = jnp.bfloat16


def dot(a, b):
    return jnp.dot(a, b, preferred_element_type=f32)


def dot_nt(a, b):
    return lax.dot_general(a, b, (((1,), (1,)), ((), ())), preferred_element_type=f32)


def dot_tn(a, b):
    return lax.dot_general(a, b, (((0,), (0,)), ((), ())), preferred_element_type=f32)


def norm_stats(rows):
    row_mean = jnp.mean(rows, axis=-1, keepdims=True)
    centered = rows - row_mean
    variance = jnp.mean(centered * centered, axis=-1, keepdims=True)
    inv_std = lax.rsqrt(variance + norm_eps)
    return centered * inv_std, inv_std


def norm_backward(grad_normed, scaled, inv_std, gain):
    grad_gain = jnp.sum(grad_normed * scaled, axis=0)
    grad_shift = jnp.sum(grad_normed, axis=0)
    inner_grad = grad_normed * gain
    grad_rows = inv_std * (
        inner_grad
        - jnp.mean(inner_grad, axis=-1, keepdims=True)
        - scaled * jnp.mean(inner_grad * scaled, axis=-1, keepdims=True)
    )
    return grad_rows, grad_gain, grad_shift


def partner(n, k):
    return [(c, c ^ k) for c in range(n)]


def hop(x, n, k):
    return lax.ppermute(x, "ctx", partner(n, k))


def gather_relative(block, n):
    if n != 4:
        return [block] + [hop(block, n, k) for k in range(1, n)]
    half = block.shape[0] // 2
    one = hop(block, n, 1)
    two = hop(block, n, 2)
    low = hop(one[:half], n, 2)
    high = hop(two[half:], n, 1)
    return [block, one, two, jnp.concatenate([low, high], axis=0)]


def gather_ctx(block, n):
    me = lax.axis_index("ctx")
    size = block.shape[0]
    parts = gather_relative(block, n)
    full = jnp.zeros((n * size,) + block.shape[1:], block.dtype)
    for k, part in enumerate(parts):
        full = lax.dynamic_update_slice_in_dim(full, part, (me ^ k) * size, 0)
    return full


def scatter_ctx(partial, n):
    me = lax.axis_index("ctx")
    size = partial.shape[0] // n

    def block(k):
        return lax.dynamic_slice_in_dim(partial, (me ^ k) * size, size, 0)

    if n != 4:
        total = block(0).astype(f32)
        for k in range(1, n):
            total = total + hop(block(k).astype(bf16), n, k).astype(f32)
        return total
    half = size // 2
    far = block(3).astype(bf16)
    low = hop(far[:half], n, 1).astype(f32)
    high = hop(far[half:], n, 2).astype(f32)
    one = block(1).astype(f32)
    two = block(2).astype(f32)
    to_one = jnp.concatenate([one[:half], one[half:] + high], axis=0).astype(bf16)
    to_two = jnp.concatenate([two[:half] + low, two[half:]], axis=0).astype(bf16)
    return block(0).astype(f32) + hop(to_one, n, 1).astype(f32) + hop(to_two, n, 2).astype(f32)


def exchange_ctx(blocks, n):
    me = lax.axis_index("ctx")
    got = lax.dynamic_update_slice_in_dim(
        jnp.zeros_like(blocks), lax.dynamic_slice_in_dim(blocks, me, 1, 0), me, 0
    )
    for k in range(1, n):
        sent = lax.dynamic_slice_in_dim(blocks, me ^ k, 1, 0)
        got = lax.dynamic_update_slice_in_dim(got, hop(sent, n, k), me ^ k, 0)
    return got


MESH = pl.DeviceIdType.MESH
HBM = pl.BlockSpec(memory_space=pltpu.HBM)


class Place:
    def __init__(self, dp):
        self.row = lax.axis_index("dp")
        self.col = lax.axis_index("ctx")
        self.lines = dp // 2
        self.line = self.row // 2
        self.core = self.row % 2
        self.twin = (self.row + 1 - 2 * self.core, self.col)

    def other(self, k):
        col, bit = self.col, 1
        while bit <= k:
            if k & bit:
                col = col + bit * (1 - 2 * ((self.col // bit) % 2))
            bit *= 2
        return col

    def across(self, k):
        return (self.row, self.other(k))

    def above(self):
        return (self.row + 2, self.col)

    def below(self):
        return (self.row - 2, self.col)


def greet(place, ctx):
    barrier = pltpu.get_barrier_semaphore()
    for k in range(1, ctx):
        pl.semaphore_signal(barrier, 1, device_id=place.across(k), device_id_type=MESH)
    pl.semaphore_wait(barrier, ctx - 1)


def remote(src, dst, send, recv, device):
    return pltpu.make_async_remote_copy(
        src_ref=src, dst_ref=dst, send_sem=send, recv_sem=recv, device_id=device, device_id_type=MESH
    )


class LineGather:
    def __init__(self, place, shard, sems):
        self.place, self.shard, self.sems = place, shard, sems

    def row(self, line):
        return line * 2 + self.place.core

    def up(self, hop):
        part = self.shard(self.row(self.place.line - hop + 1))
        return remote(part, part, self.sems.at[0, hop], self.sems.at[1, hop], self.place.above())

    def down(self, hop):
        part = self.shard(self.row(self.place.line + hop - 1))
        return remote(part, part, self.sems.at[2, hop], self.sems.at[3, hop], self.place.below())

    def over(self, at, row):
        part = self.shard(row)
        return remote(part, part, self.sems.at[4, at], self.sems.at[5, at], self.place.twin)

    def sends_up(self, hop):
        return (self.place.line - hop + 1 >= 0) & (self.place.line < self.place.lines - 1)

    def sends_down(self, hop):
        return (self.place.line + hop - 1 < self.place.lines) & (self.place.line > 0)

    def send(self, hop):
        place = self.place
        pl.when(self.sends_up(hop))(lambda: self.up(hop).start())
        pl.when(self.sends_down(hop))(lambda: self.down(hop).start())
        if hop == 1:
            self.over(0, place.row).start()

    def receive(self, hop):
        place = self.place

        @pl.when(place.line - hop >= 0)
        def _():
            part = self.shard(self.row(place.line - hop))
            remote(part, part, self.sems.at[0, hop], self.sems.at[1, hop], place.twin).wait_recv()
            self.over(hop, self.row(place.line - hop)).start()

        @pl.when(place.line + hop < place.lines)
        def _():
            part = self.shard(self.row(place.line + hop))
            remote(part, part, self.sems.at[2, hop], self.sems.at[3, hop], place.twin).wait_recv()
            self.over(place.lines - 1 + hop, self.row(place.line + hop)).start()

    def came_over(self, at, row):
        part = self.shard(row)
        remote(part, part, self.sems.at[4, at], self.sems.at[5, at], self.place.twin).wait_recv()

    def settle(self, hop, use=None):
        place = self.place
        other = 1 - 2 * place.core
        if hop == 0:
            self.came_over(0, place.row + other)
            if use:
                use(place.line)
            return
        for at, line, there in (
            (hop, place.line - hop, place.line - hop >= 0),
            (place.lines - 1 + hop, place.line + hop, place.line + hop < place.lines),
        ):

            @pl.when(there)
            def _():
                self.came_over(at, self.row(line) + other)
                if use:
                    use(line)

    def finish(self):
        place = self.place
        self.over(0, place.row).wait_send()
        for hop in range(1, place.lines):
            pl.when(self.sends_up(hop))(lambda: self.up(hop).wait_send())
            pl.when(self.sends_down(hop))(lambda: self.down(hop).wait_send())
            for at, line, there in (
                (hop, place.line - hop, place.line - hop >= 0),
                (place.lines - 1 + hop, place.line + hop, place.line + hop < place.lines),
            ):
                pl.when(there)(lambda: self.over(at, self.row(line)).wait_send())

    @staticmethod
    def scratch(dp):
        return pltpu.SemaphoreType.DMA((6, dp))


class CtxGather:
    def __init__(self, place, block, full, size, sems):
        self.place, self.block, self.full, self.size, self.sems = place, block, full, size, sems

    def rows(self, col, start=0, size=None):
        size = self.size if size is None else size
        return self.full.at[pl.ds(pl.multiple_of(col * self.size + start, size), size), :]

    def copies(self):
        place, half = self.place, self.size // 2
        me = place.col
        return [
            remote(self.block, self.rows(me), self.sems.at[0, 0], self.sems.at[1, 0], place.across(1)),
            remote(self.block, self.rows(me), self.sems.at[0, 1], self.sems.at[1, 1], place.across(2)),
            remote(
                self.rows(place.other(1), 0, half), self.rows(place.other(1), 0, half),
                self.sems.at[0, 2], self.sems.at[1, 2], place.across(2),
            ),
            remote(
                self.rows(place.other(2), half, half), self.rows(place.other(2), half, half),
                self.sems.at[0, 3], self.sems.at[1, 3], place.across(1),
            ),
        ]

    def arrivals(self):
        place, half = self.place, self.size // 2
        me = place.col
        parts = [self.rows(place.other(1)), self.rows(place.other(2)), self.rows(place.other(3), 0, half), self.rows(place.other(3), half, half)]
        return [
            remote(part, part, self.sems.at[0, i], self.sems.at[1, i], place.across(1))
            for i, part in enumerate(parts)
        ]

    def first(self):
        copies = self.copies()
        copies[0].start()
        copies[1].start()

    def second(self):
        copies, arrivals = self.copies(), self.arrivals()
        arrivals[0].wait_recv()
        copies[2].start()
        arrivals[1].wait_recv()
        copies[3].start()

    def finish(self):
        copies, arrivals = self.copies(), self.arrivals()
        arrivals[2].wait_recv()
        arrivals[3].wait_recv()
        for copy in copies:
            copy.wait_send()

    @staticmethod
    def scratch():
        return pltpu.SemaphoreType.DMA((2, 4))


def greet_all(place, dp, ctx, signal=True, wait=True):
    barrier = pltpu.get_barrier_semaphore()
    if signal:
        for k in range(1, ctx):
            pl.semaphore_signal(barrier, 1, device_id=place.across(k), device_id_type=MESH)
        for k in range(1, dp):
            pl.semaphore_signal(barrier, 1, device_id=((place.row + k) % dp, place.col), device_id_type=MESH)
    if wait:
        pl.semaphore_wait(barrier, ctx + dp - 2)


CHUNKS = 4
PARTS = 2


class CtxReduce:
    def __init__(self, place, block, total, sent, got, sems):
        self.place, self.block, self.total = place, block, total
        self.sent, self.got, self.sems = sent, got, sems
        self.size = total.shape[1] // CHUNKS

    def chunk(self, j):
        return pl.ds(j * self.size, self.size)

    def copy(self, kind, j):
        way = kind if kind else 1 + j % 2
        return remote(
            self.sent.at[kind, self.chunk(j)], self.got.at[kind, self.chunk(j)],
            self.sems.at[0, kind, j], self.sems.at[1, kind, j], self.place.across(way),
        )

    def start(self):
        self.start_far()
        self.start_near()

    def start_far(self):
        self.sent[0] = self.block(self.place.other(3)).astype(bf16)
        for j in range(CHUNKS):
            self.copy(0, j).start()

    def start_near(self):
        place = self.place
        for kind in (1, 2):
            self.total[kind - 1] = self.block(place.other(kind))
            for j in range(CHUNKS):
                if kind == 1 + j % 2:
                    self.sent[kind, self.chunk(j)] = self.total[kind - 1, self.chunk(j)].astype(bf16)
                    self.copy(kind, j).start()

    def relay(self):
        for j in range(CHUNKS):
            kind = 2 - j % 2
            self.copy(0, j).wait_recv()
            share = self.total[kind - 1, self.chunk(j)] + self.got[0, self.chunk(j)].astype(f32)
            self.sent[kind, self.chunk(j)] = share.astype(bf16)
            self.copy(kind, j).start()
        self.total[0] = self.block(self.place.col)

    def sum(self, j):
        for kind in (1, 2):
            self.copy(kind, j).wait_recv()
        rows = self.chunk(j)
        return self.total[0, rows] + self.got[1, rows].astype(f32) + self.got[2, rows].astype(f32)

    def finish(self):
        for kind in range(3):
            for j in range(CHUNKS):
                self.copy(kind, j).wait_send()

    @staticmethod
    def scratch(size, width):
        return [
            pltpu.VMEM((2, size, width), f32),
            pltpu.VMEM((3, size, width), bf16),
            pltpu.VMEM((3, size, width), bf16),
            pltpu.SemaphoreType.DMA((2, 3, CHUNKS)),
        ]


class CtxSpread:
    def __init__(self, place, made, full, sems):
        self.place, self.made, self.full, self.sems = place, made, full, sems
        self.size = made.shape[0] // CHUNKS

    def rows(self, col, j):
        at = (col * CHUNKS + j) * self.size
        return self.full.at[pl.ds(pl.multiple_of(at, self.size), self.size), :]

    def copy(self, kind, j):
        place = self.place
        if kind < 2:
            part, there = self.made.at[pl.ds(j * self.size, self.size), :], self.rows(place.col, j)
            way = 1 + kind
        else:
            way = 2 - j % 2
            part = there = self.rows(place.other(3 - way), j)
        return remote(part, there, self.sems.at[0, kind, j], self.sems.at[1, kind, j], place.across(way))

    def arrived(self, kind, j):
        part = self.rows(self.place.other(kind + 1), j)
        remote(
            part, part, self.sems.at[0, kind, j], self.sems.at[1, kind, j], self.place.across(1)
        ).wait_recv()

    def local(self, j):
        part = self.made.at[pl.ds(j * self.size, self.size), :]
        return pltpu.make_async_copy(part, self.rows(self.place.col, j), self.sems.at[0, 3, j])

    def send(self, j):
        self.copy(0, j).start()
        self.copy(1, j).start()
        self.local(j).start()

    def relay(self, j):
        way = 2 - j % 2
        self.arrived(2 - way, j)
        self.copy(2, j).start()

    def finish(self):
        for j in range(CHUNKS):
            way = 2 - j % 2
            self.arrived(way - 1, j)
            self.arrived(2, j)
            self.local(j).wait()
            for kind in range(3):
                self.copy(kind, j).wait_send()

    @staticmethod
    def scratch():
        return pltpu.SemaphoreType.DMA((2, 4, CHUNKS))


def rows_of(ref, col, size):
    return ref[pl.ds(pl.multiple_of(col * size, size), size), :]


def mix_back_kernel(
    dp, ctx, gate_ref, up_ref, gate_weight_hbm, up_weight_hbm, inner_hbm, down_hbm, normed_hbm,
    resid_ref, cot_ref, gain_ref,
    d_resid_hbm, sums_ref, wide_ref, branch_hbm, d_up_hbm,
    total, sent, got, made, d_resid_ref, gate_weight_ref, up_weight_ref, inner_ref, down_ref, normed_ref, branch, d_up,
    reduce_sem, spread_sem, load_sem, branch_sem, d_up_sem, d_resid_sem,
):
    place = Place(dp)
    loads = [
        pltpu.make_async_copy(src, dst, load_sem.at[i])
        for i, (src, dst) in enumerate(
            (
                (gate_weight_hbm, gate_weight_ref), (up_weight_hbm, up_weight_ref), (normed_hbm, normed_ref),
                (inner_hbm, inner_ref), (down_hbm, down_ref),
            )
        )
    ]
    for load in loads[:2]:
        load.start()
    greet(place, ctx)
    size, width = cot_ref.shape
    cols = width // ctx // 2
    for load in loads[:2]:
        load.wait()

    def block(col):
        return dot_nt(rows_of(gate_ref, col, size), gate_weight_ref[...]) + dot_nt(
            rows_of(up_ref, col, size), up_weight_ref[...]
        )

    def d_up_copy(i):
        return pltpu.make_async_copy(
            d_up.at[i % 2], d_up_hbm.at[pl.ds(i * cols, cols), :], d_up_sem.at[i % 2]
        )

    def branch_copy(i):
        return pltpu.make_async_copy(
            branch.at[i % 2], branch_hbm.at[pl.ds(i * size, size), :], branch_sem.at[i % 2]
        )

    def d_up_piece(i):
        if i == 0:
            loads[2].wait()
        if i > 1:
            d_up_copy(i - 2).wait()
        d_up[i % 2] = dot_tn(normed_ref[:, i * cols : (i + 1) * cols], up_ref[...]).astype(bf16)
        d_up_copy(i).start()

    def branch_piece(i):
        if i == 0:
            loads[3].wait()
            loads[4].wait()
        if i > 1:
            branch_copy(i - 2).wait()
        branch[i % 2] = dot(inner_ref[i * size : (i + 1) * size, :], down_ref[...]).astype(bf16)
        branch_copy(i).start()

    def d_resid_copy(j):
        rows = reduce.chunk(j)
        return pltpu.make_async_copy(d_resid_ref.at[rows, :], d_resid_hbm.at[rows, :], d_resid_sem.at[j])

    pieces = [functools.partial(d_up_piece, i) for i in range(2 * ctx)]
    pieces += [functools.partial(branch_piece, i) for i in range(ctx)]

    reduce = CtxReduce(place, block, total, sent, got, reduce_sem)
    spread = CtxSpread(place, made, wide_ref, spread_sem)
    reduce.start()
    for load in loads[2:]:
        load.start()
    reduce.relay()
    sums_ref[...] = jnp.zeros_like(sums_ref)
    for j in range(CHUNKS):
        for piece in pieces[2 * j : 2 * j + 2]:
            piece()
        rows = reduce.chunk(j)
        scaled, inv_std = norm_stats(resid_ref[rows, :])
        grad, d_gain, d_shift = norm_backward(reduce.sum(j), scaled, inv_std, gain_ref[...])
        sums_ref[0:1, :] += d_gain[None]
        sums_ref[1:2, :] += d_shift[None]
        grad = cot_ref[rows, :].astype(f32) + grad
        d_resid_ref[rows, :] = grad
        d_resid_copy(j).start()
        made[rows, :] = grad.astype(bf16)
        spread.send(j)
        if j:
            spread.relay(j - 1)
    pieces[2 * CHUNKS]()
    spread.relay(CHUNKS - 1)
    for piece in pieces[2 * CHUNKS + 1 :]:
        piece()
    spread.finish()
    reduce.finish()
    for i in (1, 2):
        d_up_copy(2 * ctx - i).wait()
        branch_copy(ctx - i).wait()
    for j in range(CHUNKS):
        d_resid_copy(j).wait()


def mix_back(dp, ctx, d_gate, d_up, gate_weight, up_weight, inner, down, normed, resid, cot, gain):
    size, width = cot.shape
    hidden = d_up.shape[1]
    vmem = pl.BlockSpec(memory_space=pltpu.VMEM)
    return pl.pallas_call(
        functools.partial(mix_back_kernel, dp, ctx),
        in_specs=[vmem] * 2 + [HBM] * 5 + [vmem] * 3,
        out_specs=[HBM, vmem, HBM, HBM, HBM],
        out_shape=[
            jax.ShapeDtypeStruct((size, width), f32),
            jax.ShapeDtypeStruct((2, width), f32),
            jax.ShapeDtypeStruct((ctx * size, width), bf16),
            jax.ShapeDtypeStruct((ctx * size, width), bf16),
            jax.ShapeDtypeStruct((width, hidden), bf16),
        ],
        scratch_shapes=CtxReduce.scratch(size, width)[:3]
        + [
            pltpu.VMEM((size, width), bf16),
            pltpu.VMEM((size, width), f32),
            pltpu.VMEM((width, hidden), bf16),
            pltpu.VMEM((width, hidden), bf16),
            pltpu.VMEM((ctx * size, hidden), bf16),
            pltpu.VMEM((hidden, width), bf16),
            pltpu.VMEM((ctx * size, width), bf16),
            pltpu.VMEM((2, size, width), bf16),
            pltpu.VMEM((2, width // ctx // 2, hidden), bf16),
            CtxReduce.scratch(size, width)[3],
            CtxSpread.scratch(),
            pltpu.SemaphoreType.DMA((5,)),
            pltpu.SemaphoreType.DMA((2,)),
            pltpu.SemaphoreType.DMA((2,)),
            pltpu.SemaphoreType.DMA((CHUNKS,)),
        ],
        compiler_params=pltpu.CompilerParams(
            collective_id=3, has_side_effects=True, vmem_limit_bytes=60 << 20
        ),
        cost_estimate=pl.CostEstimate(
            flops=8 * d_gate.size * width, transcendentals=0, bytes_accessed=180 << 20
        ),
    )(d_gate, d_up, gate_weight, up_weight, inner, down, normed, resid, cot, gain.reshape(1, width))


class LineReduce:
    def __init__(self, place, parts, own, pair, got, sems):
        self.place, self.parts, self.own, self.pair, self.got, self.sems = place, parts, own, pair, got, sems

    def load(self, line):
        return pltpu.make_async_copy(
            self.parts.at[2 * line + self.place.core], self.own.at[line], self.sems.at[6, line]
        )

    def swap(self, line):
        row = 2 * line + 1 - self.place.core
        return remote(
            self.parts.at[row], self.pair.at[line], self.sems.at[0, line], self.sems.at[1, line], self.place.twin
        )

    def start(self):
        for line in range(self.place.lines):
            self.swap(line).start()

    def add(self):
        for line in range(self.place.lines):
            self.load(line).wait()
            self.swap(line).wait_recv()
            self.pair[line] = (self.own[line].astype(f32) + self.pair[line].astype(f32)).astype(bf16)

    def up(self, far):
        part = self.place.line + far
        return remote(
            self.pair.at[part], self.got.at[part], self.sems.at[2, far], self.sems.at[3, far], self.place.above()
        )

    def down(self, far):
        part = self.place.line - far
        slot = part if far > 1 else self.place.lines
        return remote(
            self.pair.at[part], self.got.at[slot], self.sems.at[4, far], self.sems.at[5, far], self.place.below()
        )

    def came_up(self, far):
        slot = self.got.at[self.place.line + far]
        remote(slot, slot, self.sems.at[2, far + 1], self.sems.at[3, far + 1], self.place.twin).wait_recv()

    def came_down(self, far):
        slot = self.got.at[self.place.line - far if far else self.place.lines]
        remote(slot, slot, self.sems.at[4, far + 1], self.sems.at[5, far + 1], self.place.twin).wait_recv()

    def send(self, far):
        place = self.place

        @pl.when(place.line + far < place.lines)
        def _():
            @pl.when(place.line > 0)
            def _():
                self.came_up(far)
                part = place.line + far
                self.pair[part] = (self.pair[part].astype(f32) + self.got[part].astype(f32)).astype(bf16)

            self.up(far).start()

        @pl.when(place.line - far >= 0)
        def _():
            @pl.when(place.line < place.lines - 1)
            def _():
                self.came_down(far)
                part = place.line - far
                self.pair[part] = (self.pair[part].astype(f32) + self.got[part].astype(f32)).astype(bf16)

            self.down(far).start()

    def collect(self, out):
        place = self.place
        out[...] = self.pair[place.line].astype(f32)

        @pl.when(place.line > 0)
        def _():
            self.came_up(0)
            out[...] += self.got[place.line].astype(f32)

        @pl.when(place.line < place.lines - 1)
        def _():
            self.came_down(0)
            out[...] += self.got[place.lines].astype(f32)

    def finish(self):
        place = self.place
        for line in range(place.lines):
            self.swap(line).wait_send()
        for far in range(1, place.lines):
            pl.when(place.line + far < place.lines)(lambda: self.up(far).wait_send())
            pl.when(place.line - far >= 0)(lambda: self.down(far).wait_send())

    @staticmethod
    def scratch(dp, tile):
        return [
            pltpu.VMEM((dp // 2,) + tile, bf16),
            pltpu.VMEM((dp // 2,) + tile, bf16),
            pltpu.VMEM((dp // 2 + 1,) + tile, bf16),
            pltpu.SemaphoreType.DMA((7, dp // 2)),
        ]


class CtxReduceReady:
    def __init__(self, place, full, have, got, sems, load_sems):
        self.place, self.full, self.have, self.got, self.sems, self.load_sems = place, full, have, got, sems, load_sems
        self.height = have.shape[1]
        self.size = self.height // CHUNKS

    def chunk(self, j):
        return pl.ds(j * self.size, self.size)

    def load(self, kind):
        col = self.place.other(kind)
        rows = pl.ds(pl.multiple_of(col * self.height, self.height), self.height)
        return pltpu.make_async_copy(self.full.at[rows, :], self.have.at[kind], self.load_sems.at[kind])

    def copy(self, kind, j):
        place = self.place
        if kind:
            part, way = self.have.at[kind, self.chunk(j)], kind
        else:
            at = (place.other(3) * CHUNKS + j) * self.size
            part, way = self.full.at[pl.ds(pl.multiple_of(at, self.size), self.size), :], 1 + j % 2
        return remote(
            part, self.got.at[kind, self.chunk(j)], self.sems.at[0, kind, j], self.sems.at[1, kind, j],
            place.across(way),
        )

    def start(self):
        for j in range(CHUNKS):
            self.copy(0, j).start()
        for kind in (1, 2):
            self.load(kind).wait()
            for j in range(CHUNKS):
                if kind == 1 + j % 2:
                    self.copy(kind, j).start()

    def relay(self):
        for j in range(CHUNKS):
            kind, rows = 2 - j % 2, self.chunk(j)
            self.copy(0, j).wait_recv()
            share = self.have[kind, rows].astype(f32) + self.got[0, rows].astype(f32)
            self.have[kind, rows] = share.astype(bf16)
            self.copy(kind, j).start()

    def sum(self, j):
        for kind in (1, 2):
            self.copy(kind, j).wait_recv()
        rows = self.chunk(j)
        return self.have[0, rows].astype(f32) + self.got[1, rows].astype(f32) + self.got[2, rows].astype(f32)

    def finish(self):
        for kind in range(3):
            for j in range(CHUNKS):
                self.copy(kind, j).wait_send()


def closing_kernel(
    dp, ctx,
    d_joined_hbm, weight_hbm, qkv_parts, out_parts, branch_hbm, rows_hbm, d_resid_hbm, resid_hbm,
    gain_ref, sums_two_ref, bias_ref,
    grad_ref, qkv_ref, out_ref, output_ref, vectors_ref, d_bias_ref,
    d_joined_ref, weight_ref, rows_ref, d_resid_ref, resid_ref, load_sem,
    total, sent, got, reduce_sem, qkv_own, qkv_pair, qkv_got, qkv_sem, out_own, out_pair, out_got, out_sem,
    have, branch_got, branch_sem, branch_load_sem,
    sums, tiles, tiles_got, small, small_sem, mine, swap_out, swap_in, swap_sem,
):
    place = Place(dp)
    me, row = place.col, place.row
    lines = [
        LineReduce(place, qkv_parts, qkv_own, qkv_pair, qkv_got, qkv_sem),
        LineReduce(place, out_parts, out_own, out_pair, out_got, out_sem),
    ]
    loads = [
        pltpu.make_async_copy(src, dst, load_sem.at[i])
        for i, (src, dst) in enumerate(
            (
                (d_joined_hbm, d_joined_ref), (weight_hbm, weight_ref), (rows_hbm, rows_ref),
                (d_resid_hbm, d_resid_ref), (resid_hbm, resid_ref),
            )
        )
    ]
    for load in loads[:2]:
        load.start()
    greet_all(place, dp, ctx)
    for line in lines:
        line.start()
    for i in range(place.lines):
        for line in lines:
            line.load(i).start()
    branch = CtxReduceReady(place, branch_hbm, have, branch_got, branch_sem, branch_load_sem)
    for kind in range(3):
        branch.load(kind).start()
    for load in loads[2:]:
        load.start()

    size, width = rows_ref.shape
    for load in loads[:2]:
        load.wait()
    reduce = CtxReduce(
        place, lambda col: dot_nt(rows_of(d_joined_ref, col, size), weight_ref[...]), total, sent, got, reduce_sem
    )
    reduce.start_far()
    for line in lines:
        line.add()
        line.send(place.lines - 1)
    reduce.start_near()
    branch.start()
    reduce.relay()
    for far in range(place.lines - 2, 1, -1):
        for line in lines:
            line.send(far)

    sums[...] = jnp.zeros_like(sums)
    for load in loads[2:]:
        load.wait()
    branch.load(0).wait()
    for j in range(CHUNKS):
        rows = reduce.chunk(j)
        scaled, inv_std = norm_stats(rows_ref[rows, :].astype(f32))
        grad, d_gain, d_shift = norm_backward(reduce.sum(j), scaled, inv_std, gain_ref[...])
        sums[0:1, :] += d_gain[None]
        sums[1:2, :] += d_shift[None]
        grad_ref[rows, :] = d_resid_ref[rows, :] + grad
    branch.relay()
    if place.lines > 2:
        for line in lines:
            line.send(1)

    part = width // dp
    tiles[...] = jnp.zeros_like(tiles)
    for i in range(dp):
        lanes = slice(i * part, (i + 1) * part)
        tiles[i, 0:2, :] = sums[:, lanes]
        tiles[i, 2:4, :] = sums_two_ref[:, lanes]
        tiles[i, 4:5, :] = bias_ref[i : i + 1, :]
    sends = [
        remote(tiles.at[(row + k) % dp], tiles_got.at[k], small_sem.at[0, k], small_sem.at[1, k], ((row + k) % dp, me))
        for k in range(1, dp)
    ]
    for copy in sends:
        copy.start()
    tile = tiles[row]
    for k in range(1, dp):
        sends[k - 1].wait()
        tile = tile + tiles_got[k]
    tiles_got[0] = tile
    small[me] = tile
    spreads = [
        remote(tiles_got.at[0], small.at[me], small_sem.at[2, k], small_sem.at[3, k], place.across(k))
        for k in range(1, ctx)
    ]
    for copy in spreads:
        copy.start()

    for j in range(CHUNKS):
        rows = branch.chunk(j)
        output_ref[rows, :] = (resid_ref[rows, :] + branch.sum(j)).astype(bf16)

    for k in range(1, ctx):
        spreads[k - 1].wait_send()
        part = small.at[place.other(k)]
        remote(part, part, small_sem.at[2, k], small_sem.at[3, k], place.across(k)).wait_recv()
    four = sum(small[c, 0:4, :] for c in range(ctx))
    piece = vectors_ref.shape[1]
    slots = d_bias_ref.shape[1] // HD
    vectors = four[:, :piece]
    biases = [small[i % ctx, 4:5, i // ctx * HD : (i // ctx + 1) * HD] for i in range(slots * ctx)]
    chosen = biases[:slots]
    for c in range(1, ctx):
        vectors = jnp.where(me == c, four[:, c * piece : (c + 1) * piece], vectors)
        chosen = [jnp.where(me == c, biases[slots * c + i], chosen[i]) for i in range(slots)]
    vectors_ref[...] = vectors
    for i in range(slots):
        d_bias_ref[:, i * HD : (i + 1) * HD] = chosen[i]

    lines[0].collect(mine)
    depth = mine.shape[0] // ctx
    swap_out[...] = mine[...].astype(bf16)
    swaps = [
        remote(
            swap_out.at[pl.ds(pl.multiple_of(place.other(k) * depth, depth), depth), :], swap_in.at[me],
            swap_sem.at[0, k], swap_sem.at[1, k], place.across(k),
        )
        for k in range(1, ctx)
    ]
    for copy in swaps:
        copy.start()
    swap_in[me] = rows_of(swap_out, me, depth)
    lines[1].collect(out_ref)
    for k in range(1, ctx):
        part = swap_in.at[place.other(k)]
        remote(part, part, swap_sem.at[0, k], swap_sem.at[1, k], place.across(k)).wait_recv()
    low = head_lanes((depth, PAIR))
    for p in range(mine.shape[1] // (3 * PAIR)):
        for t in range(3):
            lanes = slice((3 * p + t) * PAIR, (3 * p + t + 1) * PAIR)
            for c in range(0, ctx, 2):
                a = swap_in[c, :, lanes].astype(f32)
                b = swap_in[c + 1, :, lanes].astype(f32)
                at = t * width + (2 * p * ctx + c) * HD
                qkv_ref[:, at : at + PAIR] = jnp.where(low, a, pltpu.roll(b, HD, 1))
                at = at + ctx * HD
                qkv_ref[:, at : at + PAIR] = jnp.where(low, pltpu.roll(a, HD, 1), b)
    for copy in swaps:
        copy.wait_send()
    for line in lines:
        line.finish()
    branch.finish()
    reduce.finish()


def closing(dp, ctx, d_joined, weight, d_qkv, d_out, branch, rows, d_resid, resid, gain, sums_two, bias):
    size, width = rows.shape
    near = weight.shape[1]
    own, tall = width // dp, d_out.shape[0] // dp
    vmem = pl.BlockSpec(memory_space=pltpu.VMEM)
    reduce_scratch = CtxReduce.scratch(size, width)
    max_peers = max(dp, ctx)
    return pl.pallas_call(
        functools.partial(closing_kernel, dp, ctx),
        in_specs=[HBM] * 8 + [vmem] * 3,
        out_specs=[vmem] * 6,
        out_shape=[
            jax.ShapeDtypeStruct((size, width), f32),
            jax.ShapeDtypeStruct((own // ctx, 3 * width), f32),
            jax.ShapeDtypeStruct((tall, width), f32),
            jax.ShapeDtypeStruct((size, width), bf16),
            jax.ShapeDtypeStruct((4, own // ctx), f32),
            jax.ShapeDtypeStruct((1, 3 * own // ctx), f32),
        ],
        scratch_shapes=[
            pltpu.VMEM((ctx * size, near), bf16),
            pltpu.VMEM((width, near), bf16),
            pltpu.VMEM((size, width), bf16),
            pltpu.VMEM((size, width), f32),
            pltpu.VMEM((size, width), f32),
            pltpu.SemaphoreType.DMA((5,)),
        ]
        + reduce_scratch
        + LineReduce.scratch(dp, (own, near))
        + LineReduce.scratch(dp, (tall, width))
        + reduce_scratch[1:]
        + [
            pltpu.SemaphoreType.DMA((3,)),
            pltpu.VMEM((2, width), f32),
            pltpu.VMEM((dp, 8, own), f32),
            pltpu.VMEM((dp, 8, own), f32),
            pltpu.VMEM((ctx, 8, own), f32),
            pltpu.SemaphoreType.DMA((4, max_peers)),
            pltpu.VMEM((own, near), f32),
            pltpu.VMEM((own, near), bf16),
            pltpu.VMEM((ctx, own // ctx, near), bf16),
            pltpu.SemaphoreType.DMA((2, ctx)),
        ],
        compiler_params=pltpu.CompilerParams(
            collective_id=1, has_side_effects=True, vmem_limit_bytes=62 << 20
        ),
        cost_estimate=pl.CostEstimate(
            flops=2 * d_joined.size * width, transcendentals=0, bytes_accessed=200 << 20
        ),
    )(
        d_joined, weight, d_qkv.reshape(dp, own, near), d_out.reshape(dp, tall, width), branch,
        rows, d_resid, resid, gain.reshape(1, width), sums_two, bias,
    )


def turn(x, table_ref):
    return (
        x * table_ref[0]
        + pltpu.roll(x, PAIR - ROT // 2, 1) * table_ref[1]
        + pltpu.roll(x, ROT // 2, 1) * table_ref[2]
    )


def turn_back(x, table_ref):
    return (
        x * table_ref[0]
        - pltpu.roll(x, PAIR - ROT // 2, 1) * table_ref[1]
        - pltpu.roll(x, ROT // 2, 1) * table_ref[2]
    )


def head_lanes(shape):
    return lax.broadcasted_iota(jnp.int32, shape, 1) < HD


def span(full_len, step, at):
    return max(0, (at - DOC_MAX + 1) // step * step), at + step


def parts_of(low, at, step):
    return ([(low, at, False)] if low < at else []) + [(at, at + step, True)]


def masked(scores, start, first, causal):
    keys = lax.broadcasted_iota(jnp.int32, scores.shape, 1)
    allowed = keys >= start - first
    if causal:
        allowed = allowed & (keys <= lax.broadcasted_iota(jnp.int32, scores.shape, 0))
    return jnp.where(allowed, scores, masked_value)


def one_head(x, head):
    return jnp.where(head_lanes(x.shape) == (head == 0), x, jnp.zeros_like(x))


def attend_kernel(step, joined_ref, bias_ref, table_ref, start_ref, out_ref, qkv_ref, lse_ref):
    full_len = joined_ref.shape[0]
    scale = 1.0 / math.sqrt(HD)
    for t in range(3):
        lanes = slice(t * PAIR, (t + 1) * PAIR)
        x = joined_ref[:, lanes] + bias_ref[:, lanes]
        if t < 2:
            x = turn(x, table_ref)
        qkv_ref[:, lanes] = x.astype(bf16)
    for at in range(0, full_len, step):
        parts = parts_of(span(full_len, step, at)[0], at, step)
        start = start_ref[at : at + step, :1]
        q = qkv_ref[at : at + step, :PAIR] * bf16(scale)
        total = jnp.zeros((step, PAIR), f32)
        logs = []
        for head in range(2):
            qm = one_head(q, head)
            scores = [
                masked(dot_nt(qm, qkv_ref[low:high, PAIR : 2 * PAIR]), start, low, causal)
                for low, high, causal in parts
            ]
            tops = [jnp.max(s, axis=1, keepdims=True) for s in scores]
            top = functools.reduce(jnp.maximum, tops)
            norm, sums = 0.0, 0.0
            for s, (low, high, _) in zip(scores, parts):
                e = jnp.exp(s - top)
                norm = norm + jnp.sum(e, axis=1, keepdims=True)
                sums = sums + dot(e.astype(bf16), one_head(qkv_ref[low:high, 2 * PAIR :], head))
            total = total + sums * (1.0 / norm)
            logs.append(top + jnp.log(norm))
        out_ref[at : at + step, :] = total.astype(bf16)
        lse_ref[at : at + step, :] = jnp.where(head_lanes((step, PAIR)), logs[0], logs[1])


def attend_back_kernel(
    step, qkv_ref, grad_ref, lse_ref, table_ref, start_ref, out_ref, sum_ref, dk_ref, dv_ref
):
    full_len = qkv_ref.shape[0]
    scale = 1.0 / math.sqrt(HD)
    dk_ref[...] = jnp.zeros_like(dk_ref)
    dv_ref[...] = jnp.zeros_like(dv_ref)
    total = jnp.zeros((1, PAIR), f32)
    for at in range(0, full_len, step):
        rows = slice(at, at + step)
        parts = parts_of(span(full_len, step, at)[0], at, step)
        start = start_ref[rows, :1]
        q = qkv_ref[rows, :PAIR] * bf16(scale)
        g = grad_ref[rows, :]
        dq = jnp.zeros((step, PAIR), f32)
        dk = [jnp.zeros((high - low, PAIR), f32) for low, high, _ in parts]
        dv = [jnp.zeros((high - low, PAIR), f32) for low, high, _ in parts]
        for head in range(2):
            qm, gm = one_head(q, head), one_head(g, head)
            lse = lse_ref[rows, head * HD : head * HD + 1]
            probs, dps, mean = [], [], 0.0
            for low, high, causal in parts:
                s = masked(dot_nt(qm, qkv_ref[low:high, PAIR : 2 * PAIR]), start, low, causal)
                probs.append(jnp.exp(s - lse))
                dps.append(dot_nt(gm, qkv_ref[low:high, 2 * PAIR :]))
                mean = mean + jnp.sum(dps[-1] * probs[-1], axis=1, keepdims=True)
            for i, (low, high, _) in enumerate(parts):
                ds = (probs[i] * (dps[i] - mean)).astype(bf16)
                dq = dq + dot(ds, one_head(qkv_ref[low:high, PAIR : 2 * PAIR], head))
                dk[i] = dk[i] + dot_tn(ds, qm)
                dv[i] = dv[i] + dot_tn(probs[i].astype(bf16), gm)
        for i, (low, high, _) in enumerate(parts):
            dk_ref[low:high, :] += dk[i]
            dv_ref[low:high, :] += dv[i]
        dq = turn_back(dq * scale, table_ref.at[:, rows, :]).astype(bf16)
        out_ref[rows, :PAIR] = dq
        total = total + jnp.sum(dq.astype(f32), axis=0, keepdims=True)
    sum_ref[:, :PAIR] = total
    dk = turn_back(dk_ref[...], table_ref).astype(bf16)
    out_ref[:, PAIR : 2 * PAIR] = dk
    sum_ref[:, PAIR : 2 * PAIR] = jnp.sum(dk.astype(f32), axis=0, keepdims=True)
    dv = dv_ref[...].astype(bf16)
    out_ref[:, 2 * PAIR :] = dv
    sum_ref[:, 2 * PAIR :] = jnp.sum(dv.astype(f32), axis=0, keepdims=True)


def whole(shape):
    return pl.BlockSpec(shape, lambda p: (0,) * len(shape))


def attend_step(full_len):
    return min(256, full_len)


def attend(joined, bias, table, start):
    full_len, width = joined.shape
    pairs = width // (3 * PAIR)
    step = attend_step(full_len)
    seen = sum(span(full_len, step, at)[1] - span(full_len, step, at)[0] for at in range(0, full_len, step)) * step
    wide = pl.BlockSpec((full_len, 3 * PAIR), lambda p: (0, p))
    thin = pl.BlockSpec((full_len, PAIR), lambda p: (0, p))
    return pl.pallas_call(
        functools.partial(attend_kernel, step),
        grid=(pairs,),
        in_specs=[
            wide,
            pl.BlockSpec((1, 3 * PAIR), lambda p: (0, p)),
            whole(table.shape),
            whole(start.shape),
        ],
        out_specs=[thin, wide, thin],
        out_shape=[
            jax.ShapeDtypeStruct((full_len, pairs * PAIR), bf16),
            jax.ShapeDtypeStruct((full_len, width), bf16),
            jax.ShapeDtypeStruct((full_len, pairs * PAIR), f32),
        ],
        compiler_params=pltpu.CompilerParams(vmem_limit_bytes=40 << 20),
        cost_estimate=pl.CostEstimate(
            flops=pairs * seen * PAIR * 8, transcendentals=pairs * seen * 2, bytes_accessed=full_len * width * 8
        ),
    )(joined, bias, table, start)


def attend_back(qkv, grad, lse, table, start):
    full_len, width = qkv.shape
    pairs = width // (3 * PAIR)
    step = attend_step(full_len)
    seen = sum(span(full_len, step, at)[1] - span(full_len, step, at)[0] for at in range(0, full_len, step)) * step
    wide = pl.BlockSpec((full_len, 3 * PAIR), lambda p: (0, p))
    thin = pl.BlockSpec((full_len, PAIR), lambda p: (0, p))
    return pl.pallas_call(
        functools.partial(attend_back_kernel, step),
        grid=(pairs,),
        in_specs=[wide, thin, thin, whole(table.shape), whole(start.shape)],
        out_specs=[wide, pl.BlockSpec((1, 3 * PAIR), lambda p: (0, p))],
        out_shape=[
            jax.ShapeDtypeStruct((full_len, width), bf16),
            jax.ShapeDtypeStruct((1, width), f32),
        ],
        scratch_shapes=[pltpu.VMEM((full_len, PAIR), f32), pltpu.VMEM((full_len, PAIR), f32)],
        compiler_params=pltpu.CompilerParams(vmem_limit_bytes=40 << 20),
        cost_estimate=pl.CostEstimate(
            flops=pairs * seen * PAIR * 20, transcendentals=pairs * seen * 2, bytes_accessed=full_len * width * 8
        ),
    )(qkv, grad, lse, table, start)


def forward_kernel(
    dp, ctx, step,
    gain_one, shift_one, gain_two, shift_two, bias, start_ref, table_hbm,
    qkv_hbm, out_weight_ref, rows_ref, cot_ref, gate_hbm, up_hbm,
    params_ref, weight_hbm, out_hbm, normed_hbm, cot_all, attended_hbm, heads_hbm, lse_hbm, resid_hbm, wide_ref,
    gate_all, up_all,
    small_all, table_ref, small_ref, qkv_ref, blocks, rows_all, weight_ref, normed_ref, joined_ref, bias_ref, out_all,
    attended_ref, heads_ref, lse_ref, total, sent, got, made, resid_ref,
    normed_sem, weight_sem, local_sem, swap_sem, small_sem, line_joined, line_out, line_gate, line_up, rows_sem, cot_sem,
    late_sem, reduce_sem, spread_sem, resid_sem,
):
    place = Place(dp)
    me, row = place.col, place.row
    depth = qkv_ref.shape[0]
    length, width = rows_ref.shape
    rows_out = out_weight_ref.shape[0]
    tall = ctx * depth

    qkv_copy = pltpu.make_async_copy(qkv_hbm, qkv_ref, local_sem.at[4])
    qkv_copy.start()
    table_copy = pltpu.make_async_copy(table_hbm, table_ref, late_sem.at[0])
    table_copy.start()
    greet_all(place, dp, ctx, wait=False)
    small_ref[...] = jnp.zeros_like(small_ref)
    for i, vector in enumerate((gain_one, shift_one, gain_two, shift_two)):
        small_ref[i // 2 : i // 2 + 1, i % 2 * HD : (i % 2 + 1) * HD] = vector[...].astype(f32)
    for i in range(bias.shape[1] // HD):
        small_ref[2 + i // 2 : 3 + i // 2, i % 2 * HD : (i % 2 + 1) * HD] = bias[
            :, i * HD : (i + 1) * HD
        ].astype(f32)
    small_all[row, me] = small_ref[...]
    qkv_copy.wait()

    low = head_lanes((depth, PAIR))
    for p in range(width // HD // ctx // 2):
        for t in range(3):
            lanes = slice((3 * p + t) * PAIR, (3 * p + t + 1) * PAIR)
            for c in range(0, ctx, 2):
                at = t * width + (2 * p * ctx + c) * HD
                a = qkv_ref[:, at : at + PAIR].astype(f32)
                at = at + ctx * HD
                b = qkv_ref[:, at : at + PAIR].astype(f32)
                blocks[c, :, lanes] = jnp.where(low, a, pltpu.roll(b, HD, 1)).astype(bf16)
                blocks[c + 1, :, lanes] = jnp.where(low, pltpu.roll(a, HD, 1), b).astype(bf16)
    greet_all(place, dp, ctx, signal=False)

    def weight_rows(row, col):
        return weight_ref.at[pl.ds(pl.multiple_of((row * ctx + col) * depth, depth), depth), :]

    def out_shard(row):
        return out_all.at[pl.ds(pl.multiple_of(row * rows_out, rows_out), rows_out), :]

    def block(ref, col):
        return ref.at[pl.ds(pl.multiple_of(col * length, length), length), :]

    part_cols = weight_ref.shape[1] // PARTS

    def weight_part(i, row):
        return weight_ref.at[
            pl.ds(pl.multiple_of(row * tall, tall), tall), pl.ds(i * part_cols, part_cols)
        ]

    local = [
        pltpu.make_async_copy(blocks.at[me], weight_rows(row, me), local_sem.at[0]),
        pltpu.make_async_copy(out_weight_ref, out_shard(row), local_sem.at[1]),
        pltpu.make_async_copy(rows_ref, block(rows_all, me), local_sem.at[2]),
        pltpu.make_async_copy(cot_ref, block(cot_all, me), local_sem.at[3]),
    ]
    swaps = [
        remote(small_ref, small_all.at[row, me], swap_sem.at[0, k], swap_sem.at[1, k], place.across(k))
        for k in range(1, ctx)
    ] + [
        remote(
            blocks.at[place.other(k)], weight_rows(row, me), swap_sem.at[2, k], swap_sem.at[3, k], place.across(k)
        )
        for k in range(1, ctx)
    ]
    for copy in swaps:
        copy.start()
    for copy in local:
        copy.start()
    def gate_shard(row):
        tall = gate_hbm.shape[0]
        return gate_all.at[pl.ds(pl.multiple_of(row * tall, tall), tall), :]

    def up_shard(row):
        tall = up_hbm.shape[0]
        return up_all.at[pl.ds(pl.multiple_of(row * tall, tall), tall), :]

    gate_line, up_line = LineGather(place, gate_shard, line_gate), LineGather(place, up_shard, line_up)
    late = [
        pltpu.make_async_copy(gate_hbm, gate_shard(row), late_sem.at[1]),
        pltpu.make_async_copy(up_hbm, up_shard(row), late_sem.at[2]),
    ]
    rows_gather = CtxGather(place, rows_ref, rows_all, length, rows_sem)
    cot_gather = CtxGather(place, cot_ref, cot_all, length, cot_sem)
    out_line = LineGather(place, out_shard, line_out)
    lines = [
        LineGather(place, functools.partial(weight_part, i), line_joined.at[i]) for i in range(PARTS)
    ] + [out_line]
    local[1].wait()
    out_line.send(1)
    rows_gather.first()
    for k in range(1, ctx):
        remote(
            small_ref, small_all.at[row, place.other(k)], swap_sem.at[0, k], swap_sem.at[1, k], place.across(k)
        ).wait_recv()
    small_sends = [
        remote(
            small_all.at[row], small_all.at[row], small_sem.at[0, k], small_sem.at[1, k], ((row + k) % dp, me)
        )
        for k in range(1, dp)
    ]
    for copy in small_sends:
        copy.start()
    local[0].wait()
    for k in range(1, ctx):
        part = weight_rows(row, place.other(k))
        remote(part, part, swap_sem.at[2, k], swap_sem.at[3, k], place.across(k)).wait_recv()
    for line in lines[:PARTS]:
        line.send(1)

    for k in range(1, dp):
        part = small_all.at[(row + dp - k) % dp]
        remote(part, part, small_sem.at[0, k], small_sem.at[1, k], place.twin).wait_recv()
    low = head_lanes((1, PAIR))
    for i in range(dp * ctx // 2):
        lanes = slice(i * PAIR, (i + 1) * PAIR)
        a = small_all[2 * i // ctx, 2 * i % ctx]
        b = small_all[(2 * i + 1) // ctx, (2 * i + 1) % ctx]
        for r in range(2):
            ar, br = a[r : r + 1, :], b[r : r + 1, :]
            params_ref[2 * r : 2 * r + 1, lanes] = jnp.where(low, ar, pltpu.roll(br, HD, 1))
            params_ref[2 * r + 1 : 2 * r + 2, lanes] = jnp.where(low, pltpu.roll(ar, HD, 1), br)

    def normalize(col):
        step = 64

        @pl.loop(0, length // step)
        def _(i):
            rows = pl.ds(pl.multiple_of(col * length + i * step, step), step)
            scaled, _ = norm_stats(rows_all[rows, :].astype(f32))
            normed_ref[rows, :] = (scaled * params_ref[0:1, :] + params_ref[1:2, :]).astype(bf16)

        normed_copy(col).start()

    def normed_copy(col):
        return pltpu.make_async_copy(block(normed_ref, col), block(normed_hbm, col), normed_sem.at[col])

    def weight_copy(i, line):
        part = (
            pl.ds(pl.multiple_of(line * (2 * tall), 2 * tall), 2 * tall),
            pl.ds(i * part_cols, part_cols),
        )
        return pltpu.make_async_copy(weight_ref.at[part], weight_hbm.at[part], weight_sem.at[i, line])

    def multiply(i, line):
        weight_copy(i, line).start()
        at = pl.multiple_of(line * (2 * tall), 2 * tall)
        cols = slice(i * part_cols, (i + 1) * part_cols)

        @pl.loop(0, ctx)
        def _(b):
            rows = pl.ds(pl.multiple_of(b * length, length), length)
            joined_ref[rows, cols] += dot(
                normed_ref[rows, pl.ds(at, 2 * tall)], weight_ref[pl.ds(at, 2 * tall), cols]
            )

    def forward(hop):
        for line in lines:
            line.receive(hop)
            if hop < place.lines - 1:
                line.send(hop + 1)

    def absorb(hop):
        for i in range(PARTS):
            lines[i].settle(hop, functools.partial(multiply, i))

    joined_ref[...] = jnp.zeros_like(joined_ref)
    local[2].wait()
    normalize(me)
    rows_gather.second()
    cot_gather.first()
    for hop in range(1, place.lines):
        forward(hop)
        if hop == 1:
            for col in (place.other(1), place.other(2)):
                normalize(col)
            rows_gather.finish()
            normalize(place.other(3))
        if hop == min(2, place.lines - 1):
            cot_gather.second()
        absorb(hop - 1)
    late[0].start()
    late[1].start()
    absorb(place.lines - 1)
    late[0].wait()
    late[1].wait()
    gate_line.send(1)

    low = head_lanes((1, PAIR))
    pairs = joined_ref.shape[1] // (3 * PAIR)
    per_device = bias.shape[1] // HD
    for p in range(pairs):
        for t in range(3):
            chosen = [None, None]
            for c in range(ctx):
                for half in range(2):
                    slot = t * (width // HD) + (2 * p + half) * ctx + c
                    owner, at = slot // per_device, slot % per_device
                    piece = small_all[owner // ctx, owner % ctx, 2 + at // 2 : 3 + at // 2, :]
                    if at % 2 != half:
                        piece = pltpu.roll(piece, HD, 1)
                    chosen[half] = piece if c == 0 else jnp.where(me == c, piece, chosen[half])
            lanes = slice((3 * p + t) * PAIR, (3 * p + t + 1) * PAIR)
            bias_ref[:, lanes] = jnp.where(low, chosen[0], chosen[1])

    def heads_copies():
        return [
            pltpu.make_async_copy(attended_ref, attended_hbm, late_sem.at[3]),
            pltpu.make_async_copy(heads_ref, heads_hbm, late_sem.at[4]),
            pltpu.make_async_copy(lse_ref, lse_hbm, late_sem.at[5]),
            pltpu.make_async_copy(out_all, out_hbm, late_sem.at[6]),
        ]

    def attend_pairs(first, last):
        @pl.loop(first, last)
        def _(p):
            wide = pl.ds(pl.multiple_of(p * (3 * PAIR), 3 * PAIR), 3 * PAIR)
            thin = pl.ds(pl.multiple_of(p * PAIR, PAIR), PAIR)
            attend_kernel(
                step, joined_ref.at[:, wide], bias_ref.at[:, wide], table_ref, start_ref,
                attended_ref.at[:, thin], heads_ref.at[:, wide], lse_ref.at[:, thin],
            )

    def pass_on(line, hop):
        line.receive(hop)
        if hop < place.lines - 1:
            line.send(hop + 1)

    table_copy.wait()
    attend_pairs(0, pairs // 2)
    if place.lines > 1:
        pass_on(gate_line, 1)
    attend_pairs(pairs // 2, pairs)
    for hop in range(place.lines):
        out_line.settle(hop)
    for line in lines:
        line.finish()
    cot_gather.finish()
    for copy in heads_copies():
        copy.start()

    reduce = CtxReduce(
        place, lambda col: dot(rows_of(attended_ref, col, length), out_all[...]), total, sent, got, reduce_sem
    )
    spread = CtxSpread(place, made, wide_ref, spread_sem)

    def resid_copy(j):
        rows = reduce.chunk(j)
        return pltpu.make_async_copy(resid_ref.at[rows, :], resid_hbm.at[rows, :], resid_sem.at[j])

    reduce.start()
    if place.lines > 2:
        pass_on(gate_line, 2)
    up_line.send(1)
    reduce.relay()
    for j in range(CHUNKS):
        rows = reduce.chunk(j)
        at = pl.multiple_of(me * length + j * reduce.size, reduce.size)
        resid = rows_all[pl.ds(at, reduce.size), :].astype(f32) + reduce.sum(j)
        resid_ref[rows, :] = resid
        resid_copy(j).start()
        scaled, _ = norm_stats(resid)
        made[rows, :] = (scaled * params_ref[2:3, :] + params_ref[3:4, :]).astype(bf16)
        spread.send(j)
        if j:
            spread.relay(j - 1)
        if j == 1 and place.lines > 1:
            pass_on(up_line, 1)
    spread.relay(CHUNKS - 1)
    for hop in range(3, place.lines):
        pass_on(gate_line, hop)
    for hop in range(2, place.lines):
        pass_on(up_line, hop)
    spread.finish()
    for line in (gate_line, up_line):
        for hop in range(place.lines):
            line.settle(hop)
        line.finish()
    reduce.finish()
    for copy in swaps + small_sends:
        copy.wait_send()
    local[3].wait()
    for col in range(ctx):
        normed_copy(col).wait()
    for line in range(place.lines):
        for i in range(PARTS):
            weight_copy(i, line).wait()
    for j in range(CHUNKS):
        resid_copy(j).wait()
    for copy in heads_copies():
        copy.wait()


def forward(dp, ctx, vectors, start, table, qkv_weight, out_weight, rows, cot, gate_weight, up_weight):
    depth, width = qkv_weight.shape[0], rows.shape[1]
    length = rows.shape[0]
    full_len = ctx * length
    near = 3 * width // ctx
    thin = near // 3
    hidden = gate_weight.shape[1]
    vmem = pl.BlockSpec(memory_space=pltpu.VMEM)
    reduce_scratch = CtxReduce.scratch(length, width)
    return pl.pallas_call(
        functools.partial(forward_kernel, dp, ctx, attend_step(full_len)),
        in_specs=[vmem] * (len(vectors) + 1) + [HBM] * 7,
        out_specs=[vmem] + [HBM] * 11,
        out_shape=[
            jax.ShapeDtypeStruct((4, width), f32),
            jax.ShapeDtypeStruct((dp * ctx * depth, near), bf16),
            jax.ShapeDtypeStruct((dp * out_weight.shape[0], width), bf16),
            jax.ShapeDtypeStruct((full_len, width), bf16),
            jax.ShapeDtypeStruct((full_len, width), bf16),
            jax.ShapeDtypeStruct((full_len, thin), bf16),
            jax.ShapeDtypeStruct((full_len, near), bf16),
            jax.ShapeDtypeStruct((full_len, thin), f32),
            jax.ShapeDtypeStruct((length, width), f32),
            jax.ShapeDtypeStruct((full_len, width), bf16),
            jax.ShapeDtypeStruct((dp * gate_weight.shape[0], hidden), bf16),
            jax.ShapeDtypeStruct((dp * up_weight.shape[0], hidden), bf16),
        ],
        scratch_shapes=[
            pltpu.VMEM((dp, ctx, 8, PAIR), f32),
            pltpu.VMEM(table.shape, f32),
            pltpu.VMEM((8, PAIR), f32),
            pltpu.VMEM((depth, 3 * width), bf16),
            pltpu.VMEM((ctx, depth, near), bf16),
            pltpu.VMEM((full_len, width), bf16),
            pltpu.VMEM((dp * ctx * depth, near), bf16),
            pltpu.VMEM((full_len, width), bf16),
            pltpu.VMEM((full_len, near), f32),
            pltpu.VMEM((1, near), f32),
            pltpu.VMEM((dp * out_weight.shape[0], width), bf16),
            pltpu.VMEM((full_len, thin), bf16),
            pltpu.VMEM((full_len, near), bf16),
            pltpu.VMEM((full_len, thin), f32),
        ]
        + reduce_scratch[:3]
        + [
            pltpu.VMEM((length, width), bf16),
            pltpu.VMEM((length, width), f32),
            pltpu.SemaphoreType.DMA((ctx,)),
            pltpu.SemaphoreType.DMA((PARTS, dp // 2)),
            pltpu.SemaphoreType.DMA((5,)),
            pltpu.SemaphoreType.DMA((4, ctx)),
            pltpu.SemaphoreType.DMA((2, dp)),
            pltpu.SemaphoreType.DMA((PARTS, 6, dp)),
            LineGather.scratch(dp),
            LineGather.scratch(dp),
            LineGather.scratch(dp),
            CtxGather.scratch(),
            CtxGather.scratch(),
            pltpu.SemaphoreType.DMA((7,)),
            reduce_scratch[3],
            CtxSpread.scratch(),
            pltpu.SemaphoreType.DMA((CHUNKS,)),
        ],
        compiler_params=pltpu.CompilerParams(
            collective_id=0, has_side_effects=True, vmem_limit_bytes=62 << 20
        ),
        cost_estimate=pl.CostEstimate(
            flops=2 * full_len * width * near, transcendentals=0, bytes_accessed=400 << 20
        ),
    )(*vectors, start, table, qkv_weight, out_weight, rows, cot, gate_weight, up_weight)


def rotary_table(full_len):
    half = ROT // 2
    inverse = 10000.0 ** (-2.0 * np.arange(half) / ROT)
    angles = np.arange(full_len)[:, None] * inverse[None, :]
    table = np.zeros((3, full_len, HD), np.float32)
    table[0, :, :half] = table[0, :, half:ROT] = np.cos(angles)
    table[0, :, ROT:] = 1.0
    table[1, :, :half] = -np.sin(angles)
    table[2, :, half:ROT] = np.sin(angles)
    return jnp.asarray(np.concatenate([table, table], axis=2))


def shards(
    dp,
    ctx,
    inputs,
    segments,
    ln1_gain,
    ln1_bias,
    qkv_weight,
    qkv_bias,
    out_weight,
    ln2_gain,
    ln2_bias,
    gate_weight,
    up_weight,
    down_weight,
    cotangent,
):
    local_len, width = inputs.shape[1], inputs.shape[2]
    full_len = segments.shape[1]
    heads = width // HD
    near = heads // ctx
    pairs = near // 2
    me = lax.axis_index("ctx")
    own = me * local_len

    segment = segments[0]
    start = jnp.sum((segment[None, :] < segment[:, None]).astype(jnp.int32), axis=1)
    start = jnp.broadcast_to(start[:, None], (full_len, 128))
    table = rotary_table(full_len)
    part = ln1_gain.shape[0]
    vectors = [v[None, :] for v in (ln1_gain, ln1_bias, ln2_gain, ln2_bias, qkv_bias)]
    rows_here = qkv_weight.shape[0]
    rows, grad_rows = inputs[0], cotangent[0]
    fused = ctx == 4 and dp % 2 == 0 and part == HD
    if fused:
        (
            params, joined_weight, out_full, normed_one, grad_wide, attended, qkv, lse, resid, normed_wide,
            gate_full, up_full,
        ) = forward(
            dp, ctx, vectors, start, table, qkv_weight, out_weight, rows, grad_rows, gate_weight, up_weight
        )
        gain_one, _, gain_two, _ = params
        down_weight, _ = lax.optimization_barrier((down_weight, normed_wide))
    else:
        small = jnp.concatenate(vectors, axis=1).astype(f32)
        small = lax.all_gather(small, ("dp", "ctx"), axis=0, tiled=True)
        blocks = qkv_weight.reshape(rows_here, 3, pairs, 2, ctx, HD).transpose(4, 0, 2, 1, 3, 5)
        blocks = exchange_ctx(blocks.reshape(ctx, rows_here, near * 3 * HD), ctx)
        joined_weight = lax.all_gather(
            blocks.reshape(ctx * rows_here, near * 3 * HD), "dp", axis=0, tiled=True
        )
        out_full = lax.all_gather(out_weight, ("dp", "ctx"), axis=0, tiled=True)
        out_full = out_full.reshape(near, ctx, HD, width)
        out_full = lax.dynamic_index_in_dim(out_full, me, 1, keepdims=False)
        out_full = out_full.reshape(near * HD, width)
        gain_one, shift_one, gain_two, shift_two = [
            small[:, i * part : (i + 1) * part].reshape(width) for i in range(4)
        ]
        scaled_wide, _ = norm_stats(gather_ctx(rows, ctx).astype(f32))
        normed_one = (scaled_wide * gain_one + shift_one).astype(bf16)
        grad_wide = gather_ctx(grad_rows, ctx)
        bias = small[:, 4 * part :].reshape(3, pairs, 2, ctx, HD)
        bias = lax.dynamic_index_in_dim(bias, me, 3, keepdims=False)
        bias = bias.transpose(1, 0, 2, 3).reshape(1, near * 3 * HD)
        attended, qkv, lse = attend(dot(normed_one, joined_weight), bias, table, start)
        resid = rows.astype(f32) + scatter_ctx(dot(attended, out_full), ctx)
        scaled_two, inv_two = norm_stats(resid)
        normed_wide = gather_ctx((scaled_two * gain_two + shift_two).astype(bf16), ctx)
        gate_full = lax.all_gather(gate_weight, "dp", axis=0, tiled=True)
        up_full = lax.all_gather(up_weight, "dp", axis=0, tiled=True)
    down_full = lax.all_gather(down_weight, "dp", axis=1, tiled=True)

    gate = dot(normed_wide, gate_full)
    upward = dot(normed_wide, up_full)
    sigma = jax.nn.sigmoid(gate)
    swish = gate * sigma
    inner = (swish * upward).astype(bf16)
    d_down = dot_tn(inner, grad_wide).astype(bf16)
    grad_wide, d_down = lax.optimization_barrier((grad_wide, d_down))
    d_down = lax.psum_scatter(d_down, "dp", scatter_dimension=1, tiled=True).astype(f32)
    d_inner = dot_nt(grad_wide, down_full)
    d_gate = (d_inner * upward * sigma * (1.0 + gate * (1.0 - sigma))).astype(bf16)
    d_upward = (d_inner * swish).astype(bf16)
    d_gate_weight = dot_tn(normed_wide, d_gate).astype(bf16)
    d_gate_ready, d_gate_weight = lax.optimization_barrier((d_gate, d_gate_weight))
    d_gate_weight = lax.psum_scatter(d_gate_weight, "dp", scatter_dimension=0, tiled=True).astype(f32)
    if fused:
        d_resid, sums_two, d_proj, branch, d_up_weight = mix_back(
            dp, ctx, d_gate_ready, d_upward, gate_full, up_full, inner, down_full, normed_wide, resid,
            grad_rows, gain_two,
        )
    else:
        branch = dot(inner, down_full)
        d_up_weight = dot_tn(normed_wide, d_upward).astype(bf16)
        d_normed_two = scatter_ctx(dot_nt(d_gate, gate_full) + dot_nt(d_upward, up_full), ctx)
        grad, d_gain_two, d_shift_two = norm_backward(d_normed_two, scaled_two, inv_two, gain_two)
        d_resid = grad_rows.astype(f32) + grad
        d_proj = gather_ctx(d_resid.astype(bf16), ctx)
    d_up_weight = lax.psum_scatter(d_up_weight, "dp", scatter_dimension=0, tiled=True).astype(f32)

    d_attended = dot_nt(d_proj, out_full).astype(bf16)
    d_out_weight = dot_tn(attended, d_proj).astype(bf16)
    d_attended, d_down = lax.optimization_barrier((d_attended, d_down))
    d_joined, d_bias = attend_back(qkv, d_attended, lse, table, start)
    d_joined_weight = dot_tn(normed_one, d_joined).astype(bf16)
    d_bias = d_bias.reshape(pairs, 3, 2, HD).transpose(1, 0, 2, 3)
    d_joined, d_gate_weight = lax.optimization_barrier((d_joined, d_gate_weight))
    if fused:
        d_bias = jnp.pad(d_bias.reshape(dp, -1), ((0, 0), (0, width // dp - near * 3 * HD // dp)))
        grad_input, d_joined_weight, d_out_weight, output, vectors, d_bias = closing(
            dp, ctx, d_joined, joined_weight, d_joined_weight, d_out_weight, branch, rows, d_resid, resid,
            gain_one, sums_two, d_bias,
        )
        d_gain_one, d_shift_one, d_gain_two, d_shift_two = vectors
        d_bias = d_bias[0]
    else:
        output = (resid + scatter_ctx(branch, ctx)).astype(bf16)
        at_me = lax.broadcasted_iota(jnp.int32, (1, ctx, 1, 1), 1) == me
        d_out_weight = jnp.where(at_me, d_out_weight.reshape(near, 1, HD, width), jnp.zeros((), bf16))
        d_out_weight = lax.psum_scatter(
            d_out_weight.reshape(width, width), ("dp", "ctx"), scatter_dimension=0, tiled=True
        ).astype(f32)
        d_normed_one = scatter_ctx(dot_nt(d_joined, joined_weight), ctx)
        scaled_one, inv_one = norm_stats(rows.astype(f32))
        grad, d_gain_one, d_shift_one = norm_backward(d_normed_one, scaled_one, inv_one, gain_one)
        grad_input = d_resid + grad
        d_joined_weight = lax.psum_scatter(d_joined_weight, "dp", scatter_dimension=0, tiled=True)
        blocks = exchange_ctx(d_joined_weight.reshape(ctx, rows_here, near * 3 * HD), ctx)
        blocks = blocks.reshape(ctx, rows_here, pairs, 3, 2, HD).transpose(1, 3, 2, 4, 0, 5)
        d_joined_weight = blocks.reshape(rows_here, 3 * width).astype(f32)
        at_me = (lax.broadcasted_iota(jnp.int32, (1, 1, 1, ctx, 1), 3) == me).astype(f32)
        d_bias = (d_bias[:, :, :, None, :] * at_me).reshape(dp * ctx, -1)
        small = jnp.concatenate(
            [t.reshape(dp * ctx, part) for t in (d_gain_one, d_shift_one, d_gain_two, d_shift_two)]
            + [d_bias],
            axis=1,
        )
        small = lax.psum_scatter(small, ("dp", "ctx"), scatter_dimension=0, tiled=True)[0]
        d_gain_one, d_shift_one, d_gain_two, d_shift_two = [
            small[i * part : (i + 1) * part] for i in range(4)
        ]
        d_bias = small[4 * part :]
    return (
        output[None],
        grad_input[None],
        d_gain_one,
        d_shift_one,
        d_joined_weight,
        d_bias,
        d_out_weight,
        d_gain_two,
        d_shift_two,
        d_gate_weight,
        d_up_weight,
        d_down,
    )


def solution(mesh):
    every = ("dp", "ctx")
    return jax.shard_map(
        functools.partial(shards, mesh.shape["dp"], mesh.shape["ctx"]),
        mesh=mesh,
        in_specs=(
            P("dp", "ctx", None),
            P("dp", None),
            P(every),
            P(every),
            P(every, None),
            P(every),
            P(every, None),
            P(every),
            P(every),
            P("dp", "ctx"),
            P("dp", "ctx"),
            P("ctx", "dp"),
            P("dp", "ctx", None),
        ),
        out_specs=(
            P("dp", "ctx", None),
            P("dp", "ctx", None),
            P(every),
            P(every),
            P(every, None),
            P(every),
            P(every, None),
            P(every),
            P(every),
            P("dp", "ctx"),
            P("dp", "ctx"),
            P("ctx", "dp"),
        ),
        check_vma=False,
    )
```

```python
import functools
import math

import jax
import jax.numpy as jnp
import numpy as np
from jax import lax
from jax.experimental import pallas as pl
from jax.experimental.pallas import tpu as pltpu
from jax.sharding import PartitionSpec as P

HD = 64
ROT = 16
DOC_MAX = 512
PAIR = 2 * HD

norm_eps = 1e-05
masked_value = -1e30
f32 = jnp.float32
bf16 = jnp.bfloat16


def dot(a, b):
    return jnp.dot(a, b, preferred_element_type=f32)


def dot_nt(a, b):
    return lax.dot_general(a, b, (((1,), (1,)), ((), ())), preferred_element_type=f32)


def dot_tn(a, b):
    return lax.dot_general(a, b, (((0,), (0,)), ((), ())), preferred_element_type=f32)


def norm_stats(rows):
    row_mean = jnp.mean(rows, axis=-1, keepdims=True)
    centered = rows - row_mean
    variance = jnp.mean(centered * centered, axis=-1, keepdims=True)
    inv_std = lax.rsqrt(variance + norm_eps)
    return centered * inv_std, inv_std


def norm_backward(grad_normed, scaled, inv_std, gain):
    grad_gain = jnp.sum(grad_normed * scaled, axis=0)
    grad_shift = jnp.sum(grad_normed, axis=0)
    inner_grad = grad_normed * gain
    grad_rows = inv_std * (
        inner_grad
        - jnp.mean(inner_grad, axis=-1, keepdims=True)
        - scaled * jnp.mean(inner_grad * scaled, axis=-1, keepdims=True)
    )
    return grad_rows, grad_gain, grad_shift


def partner(n, k):
    return [(c, c ^ k) for c in range(n)]


def hop(x, n, k):
    return lax.ppermute(x, "ctx", partner(n, k))


def gather_relative(block, n):
    if n != 4:
        return [block] + [hop(block, n, k) for k in range(1, n)]
    half = block.shape[0] // 2
    one = hop(block, n, 1)
    two = hop(block, n, 2)
    low = hop(one[:half], n, 2)
    high = hop(two[half:], n, 1)
    return [block, one, two, jnp.concatenate([low, high], axis=0)]


def gather_ctx(block, n):
    me = lax.axis_index("ctx")
    size = block.shape[0]
    parts = gather_relative(block, n)
    full = jnp.zeros((n * size,) + block.shape[1:], block.dtype)
    for k, part in enumerate(parts):
        full = lax.dynamic_update_slice_in_dim(full, part, (me ^ k) * size, 0)
    return full


def scatter_ctx(partial, n):
    me = lax.axis_index("ctx")
    size = partial.shape[0] // n

    def block(k):
        return lax.dynamic_slice_in_dim(partial, (me ^ k) * size, size, 0)

    if n != 4:
        total = block(0).astype(f32)
        for k in range(1, n):
            total = total + hop(block(k).astype(bf16), n, k).astype(f32)
        return total
    half = size // 2
    far = block(3).astype(bf16)
    low = hop(far[:half], n, 1).astype(f32)
    high = hop(far[half:], n, 2).astype(f32)
    one = block(1).astype(f32)
    two = block(2).astype(f32)
    to_one = jnp.concatenate([one[:half], one[half:] + high], axis=0).astype(bf16)
    to_two = jnp.concatenate([two[:half] + low, two[half:]], axis=0).astype(bf16)
    return block(0).astype(f32) + hop(to_one, n, 1).astype(f32) + hop(to_two, n, 2).astype(f32)


def exchange_ctx(blocks, n):
    me = lax.axis_index("ctx")
    got = lax.dynamic_update_slice_in_dim(
        jnp.zeros_like(blocks), lax.dynamic_slice_in_dim(blocks, me, 1, 0), me, 0
    )
    for k in range(1, n):
        sent = lax.dynamic_slice_in_dim(blocks, me ^ k, 1, 0)
        got = lax.dynamic_update_slice_in_dim(got, hop(sent, n, k), me ^ k, 0)
    return got


MESH = pl.DeviceIdType.MESH
HBM = pl.BlockSpec(memory_space=pltpu.HBM)


class Place:
    def __init__(self, dp):
        self.row = lax.axis_index("dp")
        self.col = lax.axis_index("ctx")
        self.lines = dp // 2
        self.line = self.row // 2
        self.core = self.row % 2
        self.twin = (self.row + 1 - 2 * self.core, self.col)

    def other(self, k):
        col, bit = self.col, 1
        while bit <= k:
            if k & bit:
                col = col + bit * (1 - 2 * ((self.col // bit) % 2))
            bit *= 2
        return col

    def across(self, k):
        return (self.row, self.other(k))

    def above(self):
        return (self.row + 2, self.col)

    def below(self):
        return (self.row - 2, self.col)


def greet(place, ctx):
    barrier = pltpu.get_barrier_semaphore()
    for k in range(1, ctx):
        pl.semaphore_signal(barrier, 1, device_id=place.across(k), device_id_type=MESH)
    pl.semaphore_wait(barrier, ctx - 1)


def remote(src, dst, send, recv, device):
    return pltpu.make_async_remote_copy(
        src_ref=src, dst_ref=dst, send_sem=send, recv_sem=recv, device_id=device, device_id_type=MESH
    )


class LineGather:
    def __init__(self, place, shard, sems):
        self.place, self.shard, self.sems = place, shard, sems

    def row(self, line):
        return line * 2 + self.place.core

    def up(self, hop):
        part = self.shard(self.row(self.place.line - hop + 1))
        return remote(part, part, self.sems.at[0, hop], self.sems.at[1, hop], self.place.above())

    def down(self, hop):
        part = self.shard(self.row(self.place.line + hop - 1))
        return remote(part, part, self.sems.at[2, hop], self.sems.at[3, hop], self.place.below())

    def over(self, at, row):
        part = self.shard(row)
        return remote(part, part, self.sems.at[4, at], self.sems.at[5, at], self.place.twin)

    def sends_up(self, hop):
        return (self.place.line - hop + 1 >= 0) & (self.place.line < self.place.lines - 1)

    def sends_down(self, hop):
        return (self.place.line + hop - 1 < self.place.lines) & (self.place.line > 0)

    def send(self, hop):
        place = self.place
        pl.when(self.sends_up(hop))(lambda: self.up(hop).start())
        pl.when(self.sends_down(hop))(lambda: self.down(hop).start())
        if hop == 1:
            self.over(0, place.row).start()

    def receive(self, hop):
        place = self.place

        @pl.when(place.line - hop >= 0)
        def _():
            part = self.shard(self.row(place.line - hop))
            remote(part, part, self.sems.at[0, hop], self.sems.at[1, hop], place.twin).wait_recv()
            self.over(hop, self.row(place.line - hop)).start()

        @pl.when(place.line + hop < place.lines)
        def _():
            part = self.shard(self.row(place.line + hop))
            remote(part, part, self.sems.at[2, hop], self.sems.at[3, hop], place.twin).wait_recv()
            self.over(place.lines - 1 + hop, self.row(place.line + hop)).start()

    def came_over(self, at, row):
        part = self.shard(row)
        remote(part, part, self.sems.at[4, at], self.sems.at[5, at], self.place.twin).wait_recv()

    def settle(self, hop, use=None):
        place = self.place
        other = 1 - 2 * place.core
        if hop == 0:
            self.came_over(0, place.row + other)
            if use:
                use(place.line)
            return
        for at, line, there in (
            (hop, place.line - hop, place.line - hop >= 0),
            (place.lines - 1 + hop, place.line + hop, place.line + hop < place.lines),
        ):

            @pl.when(there)
            def _():
                self.came_over(at, self.row(line) + other)
                if use:
                    use(line)

    def finish(self):
        place = self.place
        self.over(0, place.row).wait_send()
        for hop in range(1, place.lines):
            pl.when(self.sends_up(hop))(lambda: self.up(hop).wait_send())
            pl.when(self.sends_down(hop))(lambda: self.down(hop).wait_send())
            for at, line, there in (
                (hop, place.line - hop, place.line - hop >= 0),
                (place.lines - 1 + hop, place.line + hop, place.line + hop < place.lines),
            ):
                pl.when(there)(lambda: self.over(at, self.row(line)).wait_send())

    @staticmethod
    def scratch(dp):
        return pltpu.SemaphoreType.DMA((6, dp))


class CtxGather:
    def __init__(self, place, block, full, size, sems):
        self.place, self.block, self.full, self.size, self.sems = place, block, full, size, sems

    def rows(self, col, start=0, size=None):
        size = self.size if size is None else size
        return self.full.at[pl.ds(pl.multiple_of(col * self.size + start, size), size), :]

    def copies(self):
        place, half = self.place, self.size // 2
        me = place.col
        return [
            remote(self.block, self.rows(me), self.sems.at[0, 0], self.sems.at[1, 0], place.across(1)),
            remote(self.block, self.rows(me), self.sems.at[0, 1], self.sems.at[1, 1], place.across(2)),
            remote(
                self.rows(place.other(1), 0, half), self.rows(place.other(1), 0, half),
                self.sems.at[0, 2], self.sems.at[1, 2], place.across(2),
            ),
            remote(
                self.rows(place.other(2), half, half), self.rows(place.other(2), half, half),
                self.sems.at[0, 3], self.sems.at[1, 3], place.across(1),
            ),
        ]

    def arrivals(self):
        place, half = self.place, self.size // 2
        me = place.col
        parts = [self.rows(place.other(1)), self.rows(place.other(2)), self.rows(place.other(3), 0, half), self.rows(place.other(3), half, half)]
        return [
            remote(part, part, self.sems.at[0, i], self.sems.at[1, i], place.across(1))
            for i, part in enumerate(parts)
        ]

    def first(self):
        copies = self.copies()
        copies[0].start()
        copies[1].start()

    def second(self):
        copies, arrivals = self.copies(), self.arrivals()
        arrivals[0].wait_recv()
        copies[2].start()
        arrivals[1].wait_recv()
        copies[3].start()

    def finish(self):
        copies, arrivals = self.copies(), self.arrivals()
        arrivals[2].wait_recv()
        arrivals[3].wait_recv()
        for copy in copies:
            copy.wait_send()

    @staticmethod
    def scratch():
        return pltpu.SemaphoreType.DMA((2, 4))


def greet_all(place, dp, ctx, signal=True, wait=True):
    barrier = pltpu.get_barrier_semaphore()
    if signal:
        for k in range(1, ctx):
            pl.semaphore_signal(barrier, 1, device_id=place.across(k), device_id_type=MESH)
        for k in range(1, dp):
            pl.semaphore_signal(barrier, 1, device_id=((place.row + k) % dp, place.col), device_id_type=MESH)
    if wait:
        pl.semaphore_wait(barrier, ctx + dp - 2)


CHUNKS = 4
PARTS = 2


class CtxReduce:
    def __init__(self, place, block, total, sent, got, sems):
        self.place, self.block, self.total = place, block, total
        self.sent, self.got, self.sems = sent, got, sems
        self.size = total.shape[1] // CHUNKS

    def chunk(self, j):
        return pl.ds(j * self.size, self.size)

    def copy(self, kind, j):
        way = kind if kind else 1 + j % 2
        return remote(
            self.sent.at[kind, self.chunk(j)], self.got.at[kind, self.chunk(j)],
            self.sems.at[0, kind, j], self.sems.at[1, kind, j], self.place.across(way),
        )

    def start(self):
        self.start_far()
        self.start_near()

    def start_far(self):
        self.sent[0] = self.block(self.place.other(3)).astype(bf16)
        for j in range(CHUNKS):
            self.copy(0, j).start()

    def start_near(self):
        place = self.place
        for kind in (1, 2):
            self.total[kind - 1] = self.block(place.other(kind))
            for j in range(CHUNKS):
                if kind == 1 + j % 2:
                    self.sent[kind, self.chunk(j)] = self.total[kind - 1, self.chunk(j)].astype(bf16)
                    self.copy(kind, j).start()

    def relay(self):
        for j in range(CHUNKS):
            kind = 2 - j % 2
            self.copy(0, j).wait_recv()
            share = self.total[kind - 1, self.chunk(j)] + self.got[0, self.chunk(j)].astype(f32)
            self.sent[kind, self.chunk(j)] = share.astype(bf16)
            self.copy(kind, j).start()
        self.total[0] = self.block(self.place.col)

    def sum(self, j):
        for kind in (1, 2):
            self.copy(kind, j).wait_recv()
        rows = self.chunk(j)
        return self.total[0, rows] + self.got[1, rows].astype(f32) + self.got[2, rows].astype(f32)

    def finish(self):
        for kind in range(3):
            for j in range(CHUNKS):
                self.copy(kind, j).wait_send()

    @staticmethod
    def scratch(size, width):
        return [
            pltpu.VMEM((2, size, width), f32),
            pltpu.VMEM((3, size, width), bf16),
            pltpu.VMEM((3, size, width), bf16),
            pltpu.SemaphoreType.DMA((2, 3, CHUNKS)),
        ]


class CtxSpread:
    def __init__(self, place, made, full, sems):
        self.place, self.made, self.full, self.sems = place, made, full, sems
        self.size = made.shape[0] // CHUNKS

    def rows(self, col, j):
        at = (col * CHUNKS + j) * self.size
        return self.full.at[pl.ds(pl.multiple_of(at, self.size), self.size), :]

    def copy(self, kind, j):
        place = self.place
        if kind < 2:
            part, there = self.made.at[pl.ds(j * self.size, self.size), :], self.rows(place.col, j)
            way = 1 + kind
        else:
            way = 2 - j % 2
            part = there = self.rows(place.other(3 - way), j)
        return remote(part, there, self.sems.at[0, kind, j], self.sems.at[1, kind, j], place.across(way))

    def arrived(self, kind, j):
        part = self.rows(self.place.other(kind + 1), j)
        remote(
            part, part, self.sems.at[0, kind, j], self.sems.at[1, kind, j], self.place.across(1)
        ).wait_recv()

    def local(self, j):
        part = self.made.at[pl.ds(j * self.size, self.size), :]
        return pltpu.make_async_copy(part, self.rows(self.place.col, j), self.sems.at[0, 3, j])

    def send(self, j):
        self.copy(0, j).start()
        self.copy(1, j).start()
        self.local(j).start()

    def relay(self, j):
        way = 2 - j % 2
        self.arrived(2 - way, j)
        self.copy(2, j).start()

    def finish(self):
        for j in range(CHUNKS):
            way = 2 - j % 2
            self.arrived(way - 1, j)
            self.arrived(2, j)
            self.local(j).wait()
            for kind in range(3):
                self.copy(kind, j).wait_send()

    @staticmethod
    def scratch():
        return pltpu.SemaphoreType.DMA((2, 4, CHUNKS))


def rows_of(ref, col, size):
    return ref[pl.ds(pl.multiple_of(col * size, size), size), :]


def mix_back_kernel(
    dp, ctx, gate_ref, up_ref, gate_weight_hbm, up_weight_hbm, inner_hbm, down_hbm, normed_hbm,
    resid_ref, cot_ref, gain_ref,
    d_resid_hbm, sums_ref, wide_ref, branch_hbm, d_up_hbm,
    total, sent, got, made, d_resid_ref, gate_weight_ref, up_weight_ref, inner_ref, down_ref, normed_ref, branch, d_up,
    reduce_sem, spread_sem, load_sem, branch_sem, d_up_sem, d_resid_sem,
):
    place = Place(dp)
    loads = [
        pltpu.make_async_copy(src, dst, load_sem.at[i])
        for i, (src, dst) in enumerate(
            (
                (gate_weight_hbm, gate_weight_ref), (up_weight_hbm, up_weight_ref), (normed_hbm, normed_ref),
                (inner_hbm, inner_ref), (down_hbm, down_ref),
            )
        )
    ]
    for load in loads[:2]:
        load.start()
    greet(place, ctx)
    size, width = cot_ref.shape
    cols = width // ctx // 2
    for load in loads[:2]:
        load.wait()

    def block(col):
        return dot_nt(rows_of(gate_ref, col, size), gate_weight_ref[...]) + dot_nt(
            rows_of(up_ref, col, size), up_weight_ref[...]
        )

    def d_up_copy(i):
        return pltpu.make_async_copy(
            d_up.at[i % 2], d_up_hbm.at[pl.ds(i * cols, cols), :], d_up_sem.at[i % 2]
        )

    def branch_copy(i):
        return pltpu.make_async_copy(
            branch.at[i % 2], branch_hbm.at[pl.ds(i * size, size), :], branch_sem.at[i % 2]
        )

    def d_up_piece(i):
        if i == 0:
            loads[2].wait()
        if i > 1:
            d_up_copy(i - 2).wait()
        d_up[i % 2] = dot_tn(normed_ref[:, i * cols : (i + 1) * cols], up_ref[...]).astype(bf16)
        d_up_copy(i).start()

    def branch_piece(i):
        if i == 0:
            loads[3].wait()
            loads[4].wait()
        if i > 1:
            branch_copy(i - 2).wait()
        branch[i % 2] = dot(inner_ref[i * size : (i + 1) * size, :], down_ref[...]).astype(bf16)
        branch_copy(i).start()

    def d_resid_copy(j):
        rows = reduce.chunk(j)
        return pltpu.make_async_copy(d_resid_ref.at[rows, :], d_resid_hbm.at[rows, :], d_resid_sem.at[j])

    pieces = [functools.partial(d_up_piece, i) for i in range(2 * ctx)]
    pieces += [functools.partial(branch_piece, i) for i in range(ctx)]

    reduce = CtxReduce(place, block, total, sent, got, reduce_sem)
    spread = CtxSpread(place, made, wide_ref, spread_sem)
    reduce.start()
    for load in loads[2:]:
        load.start()
    reduce.relay()
    sums_ref[...] = jnp.zeros_like(sums_ref)
    for j in range(CHUNKS):
        for piece in pieces[2 * j : 2 * j + 2]:
            piece()
        rows = reduce.chunk(j)
        scaled, inv_std = norm_stats(resid_ref[rows, :])
        grad, d_gain, d_shift = norm_backward(reduce.sum(j), scaled, inv_std, gain_ref[...])
        sums_ref[0:1, :] += d_gain[None]
        sums_ref[1:2, :] += d_shift[None]
        grad = cot_ref[rows, :].astype(f32) + grad
        d_resid_ref[rows, :] = grad
        d_resid_copy(j).start()
        made[rows, :] = grad.astype(bf16)
        spread.send(j)
        if j:
            spread.relay(j - 1)
    pieces[2 * CHUNKS]()
    spread.relay(CHUNKS - 1)
    for piece in pieces[2 * CHUNKS + 1 :]:
        piece()
    spread.finish()
    reduce.finish()
    for i in (1, 2):
        d_up_copy(2 * ctx - i).wait()
        branch_copy(ctx - i).wait()
    for j in range(CHUNKS):
        d_resid_copy(j).wait()


def mix_back(dp, ctx, d_gate, d_up, gate_weight, up_weight, inner, down, normed, resid, cot, gain):
    size, width = cot.shape
    hidden = d_up.shape[1]
    vmem = pl.BlockSpec(memory_space=pltpu.VMEM)
    return pl.pallas_call(
        functools.partial(mix_back_kernel, dp, ctx),
        in_specs=[vmem] * 2 + [HBM] * 5 + [vmem] * 3,
        out_specs=[HBM, vmem, HBM, HBM, HBM],
        out_shape=[
            jax.ShapeDtypeStruct((size, width), f32),
            jax.ShapeDtypeStruct((2, width), f32),
            jax.ShapeDtypeStruct((ctx * size, width), bf16),
            jax.ShapeDtypeStruct((ctx * size, width), bf16),
            jax.ShapeDtypeStruct((width, hidden), bf16),
        ],
        scratch_shapes=CtxReduce.scratch(size, width)[:3]
        + [
            pltpu.VMEM((size, width), bf16),
            pltpu.VMEM((size, width), f32),
            pltpu.VMEM((width, hidden), bf16),
            pltpu.VMEM((width, hidden), bf16),
            pltpu.VMEM((ctx * size, hidden), bf16),
            pltpu.VMEM((hidden, width), bf16),
            pltpu.VMEM((ctx * size, width), bf16),
            pltpu.VMEM((2, size, width), bf16),
            pltpu.VMEM((2, width // ctx // 2, hidden), bf16),
            CtxReduce.scratch(size, width)[3],
            CtxSpread.scratch(),
            pltpu.SemaphoreType.DMA((5,)),
            pltpu.SemaphoreType.DMA((2,)),
            pltpu.SemaphoreType.DMA((2,)),
            pltpu.SemaphoreType.DMA((CHUNKS,)),
        ],
        compiler_params=pltpu.CompilerParams(
            collective_id=3, has_side_effects=True, vmem_limit_bytes=60 << 20
        ),
        cost_estimate=pl.CostEstimate(
            flops=8 * d_gate.size * width, transcendentals=0, bytes_accessed=180 << 20
        ),
    )(d_gate, d_up, gate_weight, up_weight, inner, down, normed, resid, cot, gain.reshape(1, width))


class LineReduce:
    def __init__(self, place, parts, own, pair, got, sems):
        self.place, self.parts, self.own, self.pair, self.got, self.sems = place, parts, own, pair, got, sems

    def load(self, line):
        return pltpu.make_async_copy(
            self.parts.at[2 * line + self.place.core], self.own.at[line], self.sems.at[6, line]
        )

    def swap(self, line):
        row = 2 * line + 1 - self.place.core
        return remote(
            self.parts.at[row], self.pair.at[line], self.sems.at[0, line], self.sems.at[1, line], self.place.twin
        )

    def start(self):
        for line in range(self.place.lines):
            self.swap(line).start()

    def add(self):
        for line in range(self.place.lines):
            self.load(line).wait()
            self.swap(line).wait_recv()
            self.pair[line] = (self.own[line].astype(f32) + self.pair[line].astype(f32)).astype(bf16)

    def up(self, far):
        part = self.place.line + far
        return remote(
            self.pair.at[part], self.got.at[part], self.sems.at[2, far], self.sems.at[3, far], self.place.above()
        )

    def down(self, far):
        part = self.place.line - far
        slot = part if far > 1 else self.place.lines
        return remote(
            self.pair.at[part], self.got.at[slot], self.sems.at[4, far], self.sems.at[5, far], self.place.below()
        )

    def came_up(self, far):
        slot = self.got.at[self.place.line + far]
        remote(slot, slot, self.sems.at[2, far + 1], self.sems.at[3, far + 1], self.place.twin).wait_recv()

    def came_down(self, far):
        slot = self.got.at[self.place.line - far if far else self.place.lines]
        remote(slot, slot, self.sems.at[4, far + 1], self.sems.at[5, far + 1], self.place.twin).wait_recv()

    def send(self, far):
        place = self.place

        @pl.when(place.line + far < place.lines)
        def _():
            @pl.when(place.line > 0)
            def _():
                self.came_up(far)
                part = place.line + far
                self.pair[part] = (self.pair[part].astype(f32) + self.got[part].astype(f32)).astype(bf16)

            self.up(far).start()

        @pl.when(place.line - far >= 0)
        def _():
            @pl.when(place.line < place.lines - 1)
            def _():
                self.came_down(far)
                part = place.line - far
                self.pair[part] = (self.pair[part].astype(f32) + self.got[part].astype(f32)).astype(bf16)

            self.down(far).start()

    def collect(self, out):
        place = self.place
        out[...] = self.pair[place.line].astype(f32)

        @pl.when(place.line > 0)
        def _():
            self.came_up(0)
            out[...] += self.got[place.line].astype(f32)

        @pl.when(place.line < place.lines - 1)
        def _():
            self.came_down(0)
            out[...] += self.got[place.lines].astype(f32)

    def finish(self):
        place = self.place
        for line in range(place.lines):
            self.swap(line).wait_send()
        for far in range(1, place.lines):
            pl.when(place.line + far < place.lines)(lambda: self.up(far).wait_send())
            pl.when(place.line - far >= 0)(lambda: self.down(far).wait_send())

    @staticmethod
    def scratch(dp, tile):
        return [
            pltpu.VMEM((dp // 2,) + tile, bf16),
            pltpu.VMEM((dp // 2,) + tile, bf16),
            pltpu.VMEM((dp // 2 + 1,) + tile, bf16),
            pltpu.SemaphoreType.DMA((7, dp // 2)),
        ]


class CtxReduceReady:
    def __init__(self, place, full, have, got, sems, load_sems):
        self.place, self.full, self.have, self.got, self.sems, self.load_sems = place, full, have, got, sems, load_sems
        self.height = have.shape[1]
        self.size = self.height // CHUNKS

    def chunk(self, j):
        return pl.ds(j * self.size, self.size)

    def load(self, kind):
        col = self.place.other(kind)
        rows = pl.ds(pl.multiple_of(col * self.height, self.height), self.height)
        return pltpu.make_async_copy(self.full.at[rows, :], self.have.at[kind], self.load_sems.at[kind])

    def copy(self, kind, j):
        place = self.place
        if kind:
            part, way = self.have.at[kind, self.chunk(j)], kind
        else:
            at = (place.other(3) * CHUNKS + j) * self.size
            part, way = self.full.at[pl.ds(pl.multiple_of(at, self.size), self.size), :], 1 + j % 2
        return remote(
            part, self.got.at[kind, self.chunk(j)], self.sems.at[0, kind, j], self.sems.at[1, kind, j],
            place.across(way),
        )

    def start(self):
        for j in range(CHUNKS):
            self.copy(0, j).start()
        for kind in (1, 2):
            self.load(kind).wait()
            for j in range(CHUNKS):
                if kind == 1 + j % 2:
                    self.copy(kind, j).start()

    def relay(self):
        for j in range(CHUNKS):
            kind, rows = 2 - j % 2, self.chunk(j)
            self.copy(0, j).wait_recv()
            share = self.have[kind, rows].astype(f32) + self.got[0, rows].astype(f32)
            self.have[kind, rows] = share.astype(bf16)
            self.copy(kind, j).start()

    def sum(self, j):
        for kind in (1, 2):
            self.copy(kind, j).wait_recv()
        rows = self.chunk(j)
        return self.have[0, rows].astype(f32) + self.got[1, rows].astype(f32) + self.got[2, rows].astype(f32)

    def finish(self):
        for kind in range(3):
            for j in range(CHUNKS):
                self.copy(kind, j).wait_send()


def closing_kernel(
    dp, ctx,
    d_joined_hbm, weight_hbm, qkv_parts, out_parts, branch_hbm, rows_hbm, d_resid_hbm, resid_hbm,
    gain_ref, sums_two_ref, bias_ref,
    grad_ref, qkv_ref, out_ref, output_ref, vectors_ref, d_bias_ref,
    d_joined_ref, weight_ref, rows_ref, d_resid_ref, resid_ref, load_sem,
    total, sent, got, reduce_sem, qkv_own, qkv_pair, qkv_got, qkv_sem, out_own, out_pair, out_got, out_sem,
    have, branch_got, branch_sem, branch_load_sem,
    sums, tiles, tiles_got, small, small_sem, mine, swap_out, swap_in, swap_sem,
):
    place = Place(dp)
    me, row = place.col, place.row
    lines = [
        LineReduce(place, qkv_parts, qkv_own, qkv_pair, qkv_got, qkv_sem),
        LineReduce(place, out_parts, out_own, out_pair, out_got, out_sem),
    ]
    loads = [
        pltpu.make_async_copy(src, dst, load_sem.at[i])
        for i, (src, dst) in enumerate(
            (
                (d_joined_hbm, d_joined_ref), (weight_hbm, weight_ref), (rows_hbm, rows_ref),
                (d_resid_hbm, d_resid_ref), (resid_hbm, resid_ref),
            )
        )
    ]
    for load in loads[:2]:
        load.start()
    greet_all(place, dp, ctx)
    for line in lines:
        line.start()
    for i in range(place.lines):
        for line in lines:
            line.load(i).start()
    branch = CtxReduceReady(place, branch_hbm, have, branch_got, branch_sem, branch_load_sem)
    for kind in range(3):
        branch.load(kind).start()
    for load in loads[2:]:
        load.start()

    size, width = rows_ref.shape
    for load in loads[:2]:
        load.wait()
    reduce = CtxReduce(
        place, lambda col: dot_nt(rows_of(d_joined_ref, col, size), weight_ref[...]), total, sent, got, reduce_sem
    )
    reduce.start_far()
    for line in lines:
        line.add()
        line.send(place.lines - 1)
    reduce.start_near()
    branch.start()
    reduce.relay()
    for far in range(place.lines - 2, 1, -1):
        for line in lines:
            line.send(far)

    sums[...] = jnp.zeros_like(sums)
    for load in loads[2:]:
        load.wait()
    branch.load(0).wait()
    for j in range(CHUNKS):
        rows = reduce.chunk(j)
        scaled, inv_std = norm_stats(rows_ref[rows, :].astype(f32))
        grad, d_gain, d_shift = norm_backward(reduce.sum(j), scaled, inv_std, gain_ref[...])
        sums[0:1, :] += d_gain[None]
        sums[1:2, :] += d_shift[None]
        grad_ref[rows, :] = d_resid_ref[rows, :] + grad
    branch.relay()
    if place.lines > 2:
        for line in lines:
            line.send(1)

    part = width // dp
    tiles[...] = jnp.zeros_like(tiles)
    for i in range(dp):
        lanes = slice(i * part, (i + 1) * part)
        tiles[i, 0:2, :] = sums[:, lanes]
        tiles[i, 2:4, :] = sums_two_ref[:, lanes]
        tiles[i, 4:5, :] = bias_ref[i : i + 1, :]
    sends = [
        remote(tiles.at[(row + k) % dp], tiles_got.at[k], small_sem.at[0, k], small_sem.at[1, k], ((row + k) % dp, me))
        for k in range(1, dp)
    ]
    for copy in sends:
        copy.start()
    tile = tiles[row]
    for k in range(1, dp):
        sends[k - 1].wait()
        tile = tile + tiles_got[k]
    tiles_got[0] = tile
    small[me] = tile
    spreads = [
        remote(tiles_got.at[0], small.at[me], small_sem.at[2, k], small_sem.at[3, k], place.across(k))
        for k in range(1, ctx)
    ]
    for copy in spreads:
        copy.start()

    for j in range(CHUNKS):
        rows = branch.chunk(j)
        output_ref[rows, :] = (resid_ref[rows, :] + branch.sum(j)).astype(bf16)

    for k in range(1, ctx):
        spreads[k - 1].wait_send()
        part = small.at[place.other(k)]
        remote(part, part, small_sem.at[2, k], small_sem.at[3, k], place.across(k)).wait_recv()
    four = sum(small[c, 0:4, :] for c in range(ctx))
    piece = vectors_ref.shape[1]
    slots = d_bias_ref.shape[1] // HD
    vectors = four[:, :piece]
    biases = [small[i % ctx, 4:5, i // ctx * HD : (i // ctx + 1) * HD] for i in range(slots * ctx)]
    chosen = biases[:slots]
    for c in range(1, ctx):
        vectors = jnp.where(me == c, four[:, c * piece : (c + 1) * piece], vectors)
        chosen = [jnp.where(me == c, biases[slots * c + i], chosen[i]) for i in range(slots)]
    vectors_ref[...] = vectors
    for i in range(slots):
        d_bias_ref[:, i * HD : (i + 1) * HD] = chosen[i]

    lines[0].collect(mine)
    depth = mine.shape[0] // ctx
    swap_out[...] = mine[...].astype(bf16)
    swaps = [
        remote(
            swap_out.at[pl.ds(pl.multiple_of(place.other(k) * depth, depth), depth), :], swap_in.at[me],
            swap_sem.at[0, k], swap_sem.at[1, k], place.across(k),
        )
        for k in range(1, ctx)
    ]
    for copy in swaps:
        copy.start()
    swap_in[me] = rows_of(swap_out, me, depth)
    lines[1].collect(out_ref)
    for k in range(1, ctx):
        part = swap_in.at[place.other(k)]
        remote(part, part, swap_sem.at[0, k], swap_sem.at[1, k], place.across(k)).wait_recv()
    low = head_lanes((depth, PAIR))
    for p in range(mine.shape[1] // (3 * PAIR)):
        for t in range(3):
            lanes = slice((3 * p + t) * PAIR, (3 * p + t + 1) * PAIR)
            for c in range(0, ctx, 2):
                a = swap_in[c, :, lanes].astype(f32)
                b = swap_in[c + 1, :, lanes].astype(f32)
                at = t * width + (2 * p * ctx + c) * HD
                qkv_ref[:, at : at + PAIR] = jnp.where(low, a, pltpu.roll(b, HD, 1))
                at = at + ctx * HD
                qkv_ref[:, at : at + PAIR] = jnp.where(low, pltpu.roll(a, HD, 1), b)
    for copy in swaps:
        copy.wait_send()
    for line in lines:
        line.finish()
    branch.finish()
    reduce.finish()


def closing(dp, ctx, d_joined, weight, d_qkv, d_out, branch, rows, d_resid, resid, gain, sums_two, bias):
    size, width = rows.shape
    near = weight.shape[1]
    own, tall = width // dp, d_out.shape[0] // dp
    vmem = pl.BlockSpec(memory_space=pltpu.VMEM)
    reduce_scratch = CtxReduce.scratch(size, width)
    max_peers = max(dp, ctx)
    return pl.pallas_call(
        functools.partial(closing_kernel, dp, ctx),
        in_specs=[HBM] * 8 + [vmem] * 3,
        out_specs=[vmem] * 6,
        out_shape=[
            jax.ShapeDtypeStruct((size, width), f32),
            jax.ShapeDtypeStruct((own // ctx, 3 * width), f32),
            jax.ShapeDtypeStruct((tall, width), f32),
            jax.ShapeDtypeStruct((size, width), bf16),
            jax.ShapeDtypeStruct((4, own // ctx), f32),
            jax.ShapeDtypeStruct((1, 3 * own // ctx), f32),
        ],
        scratch_shapes=[
            pltpu.VMEM((ctx * size, near), bf16),
            pltpu.VMEM((width, near), bf16),
            pltpu.VMEM((size, width), bf16),
            pltpu.VMEM((size, width), f32),
            pltpu.VMEM((size, width), f32),
            pltpu.SemaphoreType.DMA((5,)),
        ]
        + reduce_scratch
        + LineReduce.scratch(dp, (own, near))
        + LineReduce.scratch(dp, (tall, width))
        + reduce_scratch[1:]
        + [
            pltpu.SemaphoreType.DMA((3,)),
            pltpu.VMEM((2, width), f32),
            pltpu.VMEM((dp, 8, own), f32),
            pltpu.VMEM((dp, 8, own), f32),
            pltpu.VMEM((ctx, 8, own), f32),
            pltpu.SemaphoreType.DMA((4, max_peers)),
            pltpu.VMEM((own, near), f32),
            pltpu.VMEM((own, near), bf16),
            pltpu.VMEM((ctx, own // ctx, near), bf16),
            pltpu.SemaphoreType.DMA((2, ctx)),
        ],
        compiler_params=pltpu.CompilerParams(
            collective_id=1, has_side_effects=True, vmem_limit_bytes=62 << 20
        ),
        cost_estimate=pl.CostEstimate(
            flops=2 * d_joined.size * width, transcendentals=0, bytes_accessed=200 << 20
        ),
    )(
        d_joined, weight, d_qkv.reshape(dp, own, near), d_out.reshape(dp, tall, width), branch,
        rows, d_resid, resid, gain.reshape(1, width), sums_two, bias,
    )


def turn(x, table_ref):
    return (
        x * table_ref[0]
        + pltpu.roll(x, PAIR - ROT // 2, 1) * table_ref[1]
        + pltpu.roll(x, ROT // 2, 1) * table_ref[2]
    )


def turn_back(x, table_ref):
    return (
        x * table_ref[0]
        - pltpu.roll(x, PAIR - ROT // 2, 1) * table_ref[1]
        - pltpu.roll(x, ROT // 2, 1) * table_ref[2]
    )


def head_lanes(shape):
    return lax.broadcasted_iota(jnp.int32, shape, 1) < HD


def span(full_len, step, at):
    return max(0, (at - DOC_MAX + 1) // step * step), at + step


def parts_of(low, at, step):
    return ([(low, at, False)] if low < at else []) + [(at, at + step, True)]


def masked(scores, start, first, causal):
    keys = lax.broadcasted_iota(jnp.int32, scores.shape, 1)
    allowed = keys >= start - first
    if causal:
        allowed = allowed & (keys <= lax.broadcasted_iota(jnp.int32, scores.shape, 0))
    return jnp.where(allowed, scores, masked_value)


def one_head(x, head):
    return jnp.where(head_lanes(x.shape) == (head == 0), x, jnp.zeros_like(x))


def attend_kernel(step, joined_ref, bias_ref, table_ref, start_ref, out_ref, qkv_ref, lse_ref):
    full_len = joined_ref.shape[0]
    scale = 1.0 / math.sqrt(HD)
    for t in range(3):
        lanes = slice(t * PAIR, (t + 1) * PAIR)
        x = joined_ref[:, lanes] + bias_ref[:, lanes]
        if t < 2:
            x = turn(x, table_ref)
        qkv_ref[:, lanes] = x.astype(bf16)
    for at in range(0, full_len, step):
        parts = parts_of(span(full_len, step, at)[0], at, step)
        start = start_ref[at : at + step, :1]
        q = qkv_ref[at : at + step, :PAIR] * bf16(scale)
        total = jnp.zeros((step, PAIR), f32)
        logs = []
        for head in range(2):
            qm = one_head(q, head)
            scores = [
                masked(dot_nt(qm, qkv_ref[low:high, PAIR : 2 * PAIR]), start, low, causal)
                for low, high, causal in parts
            ]
            tops = [jnp.max(s, axis=1, keepdims=True) for s in scores]
            top = functools.reduce(jnp.maximum, tops)
            norm, sums = 0.0, 0.0
            for s, (low, high, _) in zip(scores, parts):
                e = jnp.exp(s - top)
                norm = norm + jnp.sum(e, axis=1, keepdims=True)
                sums = sums + dot(e.astype(bf16), one_head(qkv_ref[low:high, 2 * PAIR :], head))
            total = total + sums * (1.0 / norm)
            logs.append(top + jnp.log(norm))
        out_ref[at : at + step, :] = total.astype(bf16)
        lse_ref[at : at + step, :] = jnp.where(head_lanes((step, PAIR)), logs[0], logs[1])


def attend_back_kernel(
    step, qkv_ref, grad_ref, lse_ref, table_ref, start_ref, out_ref, sum_ref, dk_ref, dv_ref
):
    full_len = qkv_ref.shape[0]
    scale = 1.0 / math.sqrt(HD)
    dk_ref[...] = jnp.zeros_like(dk_ref)
    dv_ref[...] = jnp.zeros_like(dv_ref)
    total = jnp.zeros((1, PAIR), f32)
    for at in range(0, full_len, step):
        rows = slice(at, at + step)
        parts = parts_of(span(full_len, step, at)[0], at, step)
        start = start_ref[rows, :1]
        q = qkv_ref[rows, :PAIR] * bf16(scale)
        g = grad_ref[rows, :]
        dq = jnp.zeros((step, PAIR), f32)
        dk = [jnp.zeros((high - low, PAIR), f32) for low, high, _ in parts]
        dv = [jnp.zeros((high - low, PAIR), f32) for low, high, _ in parts]
        for head in range(2):
            qm, gm = one_head(q, head), one_head(g, head)
            lse = lse_ref[rows, head * HD : head * HD + 1]
            probs, dps, mean = [], [], 0.0
            for low, high, causal in parts:
                s = masked(dot_nt(qm, qkv_ref[low:high, PAIR : 2 * PAIR]), start, low, causal)
                probs.append(jnp.exp(s - lse))
                dps.append(dot_nt(gm, qkv_ref[low:high, 2 * PAIR :]))
                mean = mean + jnp.sum(dps[-1] * probs[-1], axis=1, keepdims=True)
            for i, (low, high, _) in enumerate(parts):
                ds = (probs[i] * (dps[i] - mean)).astype(bf16)
                dq = dq + dot(ds, one_head(qkv_ref[low:high, PAIR : 2 * PAIR], head))
                dk[i] = dk[i] + dot_tn(ds, qm)
                dv[i] = dv[i] + dot_tn(probs[i].astype(bf16), gm)
        for i, (low, high, _) in enumerate(parts):
            dk_ref[low:high, :] += dk[i]
            dv_ref[low:high, :] += dv[i]
        dq = turn_back(dq * scale, table_ref.at[:, rows, :]).astype(bf16)
        out_ref[rows, :PAIR] = dq
        total = total + jnp.sum(dq.astype(f32), axis=0, keepdims=True)
    sum_ref[:, :PAIR] = total
    dk = turn_back(dk_ref[...], table_ref).astype(bf16)
    out_ref[:, PAIR : 2 * PAIR] = dk
    sum_ref[:, PAIR : 2 * PAIR] = jnp.sum(dk.astype(f32), axis=0, keepdims=True)
    dv = dv_ref[...].astype(bf16)
    out_ref[:, 2 * PAIR :] = dv
    sum_ref[:, 2 * PAIR :] = jnp.sum(dv.astype(f32), axis=0, keepdims=True)


def whole(shape):
    return pl.BlockSpec(shape, lambda p: (0,) * len(shape))


def attend_step(full_len):
    return min(256, full_len)


def attend(joined, bias, table, start):
    full_len, width = joined.shape
    pairs = width // (3 * PAIR)
    step = attend_step(full_len)
    seen = sum(span(full_len, step, at)[1] - span(full_len, step, at)[0] for at in range(0, full_len, step)) * step
    wide = pl.BlockSpec((full_len, 3 * PAIR), lambda p: (0, p))
    thin = pl.BlockSpec((full_len, PAIR), lambda p: (0, p))
    return pl.pallas_call(
        functools.partial(attend_kernel, step),
        grid=(pairs,),
        in_specs=[
            wide,
            pl.BlockSpec((1, 3 * PAIR), lambda p: (0, p)),
            whole(table.shape),
            whole(start.shape),
        ],
        out_specs=[thin, wide, thin],
        out_shape=[
            jax.ShapeDtypeStruct((full_len, pairs * PAIR), bf16),
            jax.ShapeDtypeStruct((full_len, width), bf16),
            jax.ShapeDtypeStruct((full_len, pairs * PAIR), f32),
        ],
        compiler_params=pltpu.CompilerParams(vmem_limit_bytes=40 << 20),
        cost_estimate=pl.CostEstimate(
            flops=pairs * seen * PAIR * 8, transcendentals=pairs * seen * 2, bytes_accessed=full_len * width * 8
        ),
    )(joined, bias, table, start)


def attend_back(qkv, grad, lse, table, start):
    full_len, width = qkv.shape
    pairs = width // (3 * PAIR)
    step = attend_step(full_len)
    seen = sum(span(full_len, step, at)[1] - span(full_len, step, at)[0] for at in range(0, full_len, step)) * step
    wide = pl.BlockSpec((full_len, 3 * PAIR), lambda p: (0, p))
    thin = pl.BlockSpec((full_len, PAIR), lambda p: (0, p))
    return pl.pallas_call(
        functools.partial(attend_back_kernel, step),
        grid=(pairs,),
        in_specs=[wide, thin, thin, whole(table.shape), whole(start.shape)],
        out_specs=[wide, pl.BlockSpec((1, 3 * PAIR), lambda p: (0, p))],
        out_shape=[
            jax.ShapeDtypeStruct((full_len, width), bf16),
            jax.ShapeDtypeStruct((1, width), f32),
        ],
        scratch_shapes=[pltpu.VMEM((full_len, PAIR), f32), pltpu.VMEM((full_len, PAIR), f32)],
        compiler_params=pltpu.CompilerParams(vmem_limit_bytes=40 << 20),
        cost_estimate=pl.CostEstimate(
            flops=pairs * seen * PAIR * 20, transcendentals=pairs * seen * 2, bytes_accessed=full_len * width * 8
        ),
    )(qkv, grad, lse, table, start)


def forward_kernel(
    dp, ctx, step,
    gain_one, shift_one, gain_two, shift_two, bias, start_ref, table_hbm,
    qkv_hbm, out_weight_ref, rows_ref, cot_ref, gate_hbm, up_hbm,
    params_ref, weight_hbm, out_hbm, normed_hbm, cot_all, attended_hbm, heads_hbm, lse_hbm, resid_hbm, wide_ref,
    gate_all, up_all,
    small_all, table_ref, small_ref, qkv_ref, blocks, rows_all, weight_ref, normed_ref, joined_ref, bias_ref, out_all,
    attended_ref, heads_ref, lse_ref, total, sent, got, made, resid_ref,
    normed_sem, weight_sem, local_sem, swap_sem, small_sem, line_joined, line_out, line_gate, line_up, rows_sem, cot_sem,
    late_sem, reduce_sem, spread_sem, resid_sem,
):
    place = Place(dp)
    me, row = place.col, place.row
    depth = qkv_ref.shape[0]
    length, width = rows_ref.shape
    rows_out = out_weight_ref.shape[0]
    tall = ctx * depth

    qkv_copy = pltpu.make_async_copy(qkv_hbm, qkv_ref, local_sem.at[4])
    qkv_copy.start()
    table_copy = pltpu.make_async_copy(table_hbm, table_ref, late_sem.at[0])
    table_copy.start()
    greet_all(place, dp, ctx, wait=False)
    small_ref[...] = jnp.zeros_like(small_ref)
    for i, vector in enumerate((gain_one, shift_one, gain_two, shift_two)):
        small_ref[i // 2 : i // 2 + 1, i % 2 * HD : (i % 2 + 1) * HD] = vector[...].astype(f32)
    for i in range(bias.shape[1] // HD):
        small_ref[2 + i // 2 : 3 + i // 2, i % 2 * HD : (i % 2 + 1) * HD] = bias[
            :, i * HD : (i + 1) * HD
        ].astype(f32)
    small_all[row, me] = small_ref[...]
    qkv_copy.wait()

    low = head_lanes((depth, PAIR))
    for p in range(width // HD // ctx // 2):
        for t in range(3):
            lanes = slice((3 * p + t) * PAIR, (3 * p + t + 1) * PAIR)
            for c in range(0, ctx, 2):
                at = t * width + (2 * p * ctx + c) * HD
                a = qkv_ref[:, at : at + PAIR].astype(f32)
                at = at + ctx * HD
                b = qkv_ref[:, at : at + PAIR].astype(f32)
                blocks[c, :, lanes] = jnp.where(low, a, pltpu.roll(b, HD, 1)).astype(bf16)
                blocks[c + 1, :, lanes] = jnp.where(low, pltpu.roll(a, HD, 1), b).astype(bf16)
    greet_all(place, dp, ctx, signal=False)

    def weight_rows(row, col):
        return weight_ref.at[pl.ds(pl.multiple_of((row * ctx + col) * depth, depth), depth), :]

    def out_shard(row):
        return out_all.at[pl.ds(pl.multiple_of(row * rows_out, rows_out), rows_out), :]

    def block(ref, col):
        return ref.at[pl.ds(pl.multiple_of(col * length, length), length), :]

    part_cols = weight_ref.shape[1] // PARTS

    def weight_part(i, row):
        return weight_ref.at[
            pl.ds(pl.multiple_of(row * tall, tall), tall), pl.ds(i * part_cols, part_cols)
        ]

    local = [
        pltpu.make_async_copy(blocks.at[me], weight_rows(row, me), local_sem.at[0]),
        pltpu.make_async_copy(out_weight_ref, out_shard(row), local_sem.at[1]),
        pltpu.make_async_copy(rows_ref, block(rows_all, me), local_sem.at[2]),
        pltpu.make_async_copy(cot_ref, block(cot_all, me), local_sem.at[3]),
    ]
    swaps = [
        remote(small_ref, small_all.at[row, me], swap_sem.at[0, k], swap_sem.at[1, k], place.across(k))
        for k in range(1, ctx)
    ] + [
        remote(
            blocks.at[place.other(k)], weight_rows(row, me), swap_sem.at[2, k], swap_sem.at[3, k], place.across(k)
        )
        for k in range(1, ctx)
    ]
    for copy in swaps:
        copy.start()
    for copy in local:
        copy.start()

    def gate_shard(row):
        tall = gate_hbm.shape[0]
        return gate_all.at[pl.ds(pl.multiple_of(row * tall, tall), tall), :]

    def up_shard(row):
        tall = up_hbm.shape[0]
        return up_all.at[pl.ds(pl.multiple_of(row * tall, tall), tall), :]

    gate_line, up_line = LineGather(place, gate_shard, line_gate), LineGather(place, up_shard, line_up)
    late = [
        pltpu.make_async_copy(gate_hbm, gate_shard(row), late_sem.at[1]),
        pltpu.make_async_copy(up_hbm, up_shard(row), late_sem.at[2]),
    ]
    for copy in late:
        copy.start()
    rows_gather = CtxGather(place, rows_ref, rows_all, length, rows_sem)
    cot_gather = CtxGather(place, cot_ref, cot_all, length, cot_sem)
    out_line = LineGather(place, out_shard, line_out)
    lines = [
        LineGather(place, functools.partial(weight_part, i), line_joined.at[i]) for i in range(PARTS)
    ] + [out_line]
    local[1].wait()
    out_line.send(1)
    rows_gather.first()
    for k in range(1, ctx):
        remote(
            small_ref, small_all.at[row, place.other(k)], swap_sem.at[0, k], swap_sem.at[1, k], place.across(k)
        ).wait_recv()
    small_sends = [
        remote(
            small_all.at[row], small_all.at[row], small_sem.at[0, k], small_sem.at[1, k], ((row + k) % dp, me)
        )
        for k in range(1, dp)
    ]
    for copy in small_sends:
        copy.start()
    local[0].wait()
    for k in range(1, ctx):
        part = weight_rows(row, place.other(k))
        remote(part, part, swap_sem.at[2, k], swap_sem.at[3, k], place.across(k)).wait_recv()
    for line in lines[:PARTS]:
        line.send(1)

    for k in range(1, dp):
        part = small_all.at[(row + dp - k) % dp]
        remote(part, part, small_sem.at[0, k], small_sem.at[1, k], place.twin).wait_recv()
    low = head_lanes((1, PAIR))
    for i in range(dp * ctx // 2):
        lanes = slice(i * PAIR, (i + 1) * PAIR)
        a = small_all[2 * i // ctx, 2 * i % ctx]
        b = small_all[(2 * i + 1) // ctx, (2 * i + 1) % ctx]
        for r in range(2):
            ar, br = a[r : r + 1, :], b[r : r + 1, :]
            params_ref[2 * r : 2 * r + 1, lanes] = jnp.where(low, ar, pltpu.roll(br, HD, 1))
            params_ref[2 * r + 1 : 2 * r + 2, lanes] = jnp.where(low, pltpu.roll(ar, HD, 1), br)

    def normalize(col):
        step = 64

        @pl.loop(0, length // step)
        def _(i):
            rows = pl.ds(pl.multiple_of(col * length + i * step, step), step)
            scaled, _ = norm_stats(rows_all[rows, :].astype(f32))
            normed_ref[rows, :] = (scaled * params_ref[0:1, :] + params_ref[1:2, :]).astype(bf16)

        normed_copy(col).start()

    def normed_copy(col):
        return pltpu.make_async_copy(block(normed_ref, col), block(normed_hbm, col), normed_sem.at[col])

    def weight_copy(i, line):
        part = (
            pl.ds(pl.multiple_of(line * (2 * tall), 2 * tall), 2 * tall),
            pl.ds(i * part_cols, part_cols),
        )
        return pltpu.make_async_copy(weight_ref.at[part], weight_hbm.at[part], weight_sem.at[i, line])

    def multiply(i, line):
        weight_copy(i, line).start()
        at = pl.multiple_of(line * (2 * tall), 2 * tall)
        cols = slice(i * part_cols, (i + 1) * part_cols)

        @pl.loop(0, ctx)
        def _(b):
            rows = pl.ds(pl.multiple_of(b * length, length), length)
            joined_ref[rows, cols] += dot(
                normed_ref[rows, pl.ds(at, 2 * tall)], weight_ref[pl.ds(at, 2 * tall), cols]
            )

    def forward(hop):
        for line in lines:
            line.receive(hop)
            if hop < place.lines - 1:
                line.send(hop + 1)

    def absorb(hop):
        for i in range(PARTS):
            lines[i].settle(hop, functools.partial(multiply, i))

    joined_ref[...] = jnp.zeros_like(joined_ref)
    local[2].wait()
    normalize(me)
    rows_gather.second()
    cot_gather.first()
    for hop in range(1, place.lines):
        forward(hop)
        if hop == 1:
            for col in (place.other(1), place.other(2)):
                normalize(col)
            rows_gather.finish()
            normalize(place.other(3))
        if hop == min(2, place.lines - 1):
            cot_gather.second()
        absorb(hop - 1)
    late[0].wait()
    gate_line.send(1)
    absorb(place.lines - 1)
    late[1].wait()

    low = head_lanes((1, PAIR))
    pairs = joined_ref.shape[1] // (3 * PAIR)
    per_device = bias.shape[1] // HD
    for p in range(pairs):
        for t in range(3):
            chosen = [None, None]
            for c in range(ctx):
                for half in range(2):
                    slot = t * (width // HD) + (2 * p + half) * ctx + c
                    owner, at = slot // per_device, slot % per_device
                    piece = small_all[owner // ctx, owner % ctx, 2 + at // 2 : 3 + at // 2, :]
                    if at % 2 != half:
                        piece = pltpu.roll(piece, HD, 1)
                    chosen[half] = piece if c == 0 else jnp.where(me == c, piece, chosen[half])
            lanes = slice((3 * p + t) * PAIR, (3 * p + t + 1) * PAIR)
            bias_ref[:, lanes] = jnp.where(low, chosen[0], chosen[1])

    def heads_copies():
        return [
            pltpu.make_async_copy(attended_ref, attended_hbm, late_sem.at[3]),
            pltpu.make_async_copy(heads_ref, heads_hbm, late_sem.at[4]),
            pltpu.make_async_copy(lse_ref, lse_hbm, late_sem.at[5]),
            pltpu.make_async_copy(out_all, out_hbm, late_sem.at[6]),
        ]

    def attend_pairs(first, last):
        @pl.loop(first, last)
        def _(p):
            wide = pl.ds(pl.multiple_of(p * (3 * PAIR), 3 * PAIR), 3 * PAIR)
            thin = pl.ds(pl.multiple_of(p * PAIR, PAIR), PAIR)
            attend_kernel(
                step, joined_ref.at[:, wide], bias_ref.at[:, wide], table_ref, start_ref,
                attended_ref.at[:, thin], heads_ref.at[:, wide], lse_ref.at[:, thin],
            )

    def pass_on(line, hop):
        line.receive(hop)
        if hop < place.lines - 1:
            line.send(hop + 1)

    table_copy.wait()
    attend_pairs(0, pairs // 2)
    if place.lines > 1:
        pass_on(gate_line, 1)
    up_line.send(1)
    attend_pairs(pairs // 2, pairs)
    for hop in range(place.lines):
        out_line.settle(hop)
    for line in lines:
        line.finish()
    cot_gather.finish()
    for copy in heads_copies():
        copy.start()

    reduce = CtxReduce(
        place, lambda col: dot(rows_of(attended_ref, col, length), out_all[...]), total, sent, got, reduce_sem
    )
    spread = CtxSpread(place, made, wide_ref, spread_sem)

    def resid_copy(j):
        rows = reduce.chunk(j)
        return pltpu.make_async_copy(resid_ref.at[rows, :], resid_hbm.at[rows, :], resid_sem.at[j])

    reduce.start()
    reduce.relay()
    if place.lines > 2:
        pass_on(gate_line, 2)
    for j in range(CHUNKS):
        rows = reduce.chunk(j)
        at = pl.multiple_of(me * length + j * reduce.size, reduce.size)
        resid = rows_all[pl.ds(at, reduce.size), :].astype(f32) + reduce.sum(j)
        resid_ref[rows, :] = resid
        resid_copy(j).start()
        scaled, _ = norm_stats(resid)
        made[rows, :] = (scaled * params_ref[2:3, :] + params_ref[3:4, :]).astype(bf16)
        spread.send(j)
        if j:
            spread.relay(j - 1)
        if j == 1 and place.lines > 1:
            pass_on(up_line, 1)
    spread.relay(CHUNKS - 1)
    for hop in range(3, place.lines):
        pass_on(gate_line, hop)
    for hop in range(2, place.lines):
        pass_on(up_line, hop)
    spread.finish()
    for line in (gate_line, up_line):
        for hop in range(place.lines):
            line.settle(hop)
        line.finish()
    reduce.finish()
    for copy in swaps + small_sends:
        copy.wait_send()
    local[3].wait()
    for col in range(ctx):
        normed_copy(col).wait()
    for line in range(place.lines):
        for i in range(PARTS):
            weight_copy(i, line).wait()
    for j in range(CHUNKS):
        resid_copy(j).wait()
    for copy in heads_copies():
        copy.wait()


def forward(dp, ctx, vectors, start, table, qkv_weight, out_weight, rows, cot, gate_weight, up_weight):
    depth, width = qkv_weight.shape[0], rows.shape[1]
    length = rows.shape[0]
    full_len = ctx * length
    near = 3 * width // ctx
    thin = near // 3
    hidden = gate_weight.shape[1]
    vmem = pl.BlockSpec(memory_space=pltpu.VMEM)
    reduce_scratch = CtxReduce.scratch(length, width)
    return pl.pallas_call(
        functools.partial(forward_kernel, dp, ctx, attend_step(full_len)),
        in_specs=[vmem] * (len(vectors) + 1) + [HBM] * 7,
        out_specs=[vmem] + [HBM] * 11,
        out_shape=[
            jax.ShapeDtypeStruct((4, width), f32),
            jax.ShapeDtypeStruct((dp * ctx * depth, near), bf16),
            jax.ShapeDtypeStruct((dp * out_weight.shape[0], width), bf16),
            jax.ShapeDtypeStruct((full_len, width), bf16),
            jax.ShapeDtypeStruct((full_len, width), bf16),
            jax.ShapeDtypeStruct((full_len, thin), bf16),
            jax.ShapeDtypeStruct((full_len, near), bf16),
            jax.ShapeDtypeStruct((full_len, thin), f32),
            jax.ShapeDtypeStruct((length, width), f32),
            jax.ShapeDtypeStruct((full_len, width), bf16),
            jax.ShapeDtypeStruct((dp * gate_weight.shape[0], hidden), bf16),
            jax.ShapeDtypeStruct((dp * up_weight.shape[0], hidden), bf16),
        ],
        scratch_shapes=[
            pltpu.VMEM((dp, ctx, 8, PAIR), f32),
            pltpu.VMEM(table.shape, f32),
            pltpu.VMEM((8, PAIR), f32),
            pltpu.VMEM((depth, 3 * width), bf16),
            pltpu.VMEM((ctx, depth, near), bf16),
            pltpu.VMEM((full_len, width), bf16),
            pltpu.VMEM((dp * ctx * depth, near), bf16),
            pltpu.VMEM((full_len, width), bf16),
            pltpu.VMEM((full_len, near), f32),
            pltpu.VMEM((1, near), f32),
            pltpu.VMEM((dp * out_weight.shape[0], width), bf16),
            pltpu.VMEM((full_len, thin), bf16),
            pltpu.VMEM((full_len, near), bf16),
            pltpu.VMEM((full_len, thin), f32),
        ]
        + reduce_scratch[:3]
        + [
            pltpu.VMEM((length, width), bf16),
            pltpu.VMEM((length, width), f32),
            pltpu.SemaphoreType.DMA((ctx,)),
            pltpu.SemaphoreType.DMA((PARTS, dp // 2)),
            pltpu.SemaphoreType.DMA((5,)),
            pltpu.SemaphoreType.DMA((4, ctx)),
            pltpu.SemaphoreType.DMA((2, dp)),
            pltpu.SemaphoreType.DMA((PARTS, 6, dp)),
            LineGather.scratch(dp),
            LineGather.scratch(dp),
            LineGather.scratch(dp),
            CtxGather.scratch(),
            CtxGather.scratch(),
            pltpu.SemaphoreType.DMA((7,)),
            reduce_scratch[3],
            CtxSpread.scratch(),
            pltpu.SemaphoreType.DMA((CHUNKS,)),
        ],
        compiler_params=pltpu.CompilerParams(
            collective_id=0, has_side_effects=True, vmem_limit_bytes=62 << 20
        ),
        cost_estimate=pl.CostEstimate(
            flops=2 * full_len * width * near, transcendentals=0, bytes_accessed=400 << 20
        ),
    )(*vectors, start, table, qkv_weight, out_weight, rows, cot, gate_weight, up_weight)


def rotary_table(full_len):
    half = ROT // 2
    inverse = 10000.0 ** (-2.0 * np.arange(half) / ROT)
    angles = np.arange(full_len)[:, None] * inverse[None, :]
    table = np.zeros((3, full_len, HD), np.float32)
    table[0, :, :half] = table[0, :, half:ROT] = np.cos(angles)
    table[0, :, ROT:] = 1.0
    table[1, :, :half] = -np.sin(angles)
    table[2, :, half:ROT] = np.sin(angles)
    return jnp.asarray(np.concatenate([table, table], axis=2))


def shards(
    dp,
    ctx,
    inputs,
    segments,
    ln1_gain,
    ln1_bias,
    qkv_weight,
    qkv_bias,
    out_weight,
    ln2_gain,
    ln2_bias,
    gate_weight,
    up_weight,
    down_weight,
    cotangent,
):
    local_len, width = inputs.shape[1], inputs.shape[2]
    full_len = segments.shape[1]
    heads = width // HD
    near = heads // ctx
    pairs = near // 2
    me = lax.axis_index("ctx")
    own = me * local_len

    segment = segments[0]
    start = jnp.sum((segment[None, :] < segment[:, None]).astype(jnp.int32), axis=1)
    start = jnp.broadcast_to(start[:, None], (full_len, 128))
    table = rotary_table(full_len)
    part = ln1_gain.shape[0]
    vectors = [v[None, :] for v in (ln1_gain, ln1_bias, ln2_gain, ln2_bias, qkv_bias)]
    rows_here = qkv_weight.shape[0]
    rows, grad_rows = inputs[0], cotangent[0]
    fused = ctx == 4 and dp % 2 == 0 and part == HD
    if fused:
        (
            params, joined_weight, out_full, normed_one, grad_wide, attended, qkv, lse, resid, normed_wide,
            gate_full, up_full,
        ) = forward(
            dp, ctx, vectors, start, table, qkv_weight, out_weight, rows, grad_rows, gate_weight, up_weight
        )
        gain_one, _, gain_two, _ = params
        down_weight, _ = lax.optimization_barrier((down_weight, normed_wide))
    else:
        small = jnp.concatenate(vectors, axis=1).astype(f32)
        small = lax.all_gather(small, ("dp", "ctx"), axis=0, tiled=True)
        blocks = qkv_weight.reshape(rows_here, 3, pairs, 2, ctx, HD).transpose(4, 0, 2, 1, 3, 5)
        blocks = exchange_ctx(blocks.reshape(ctx, rows_here, near * 3 * HD), ctx)
        joined_weight = lax.all_gather(
            blocks.reshape(ctx * rows_here, near * 3 * HD), "dp", axis=0, tiled=True
        )
        out_full = lax.all_gather(out_weight, ("dp", "ctx"), axis=0, tiled=True)
        out_full = out_full.reshape(near, ctx, HD, width)
        out_full = lax.dynamic_index_in_dim(out_full, me, 1, keepdims=False)
        out_full = out_full.reshape(near * HD, width)
        gain_one, shift_one, gain_two, shift_two = [
            small[:, i * part : (i + 1) * part].reshape(width) for i in range(4)
        ]
        scaled_wide, _ = norm_stats(gather_ctx(rows, ctx).astype(f32))
        normed_one = (scaled_wide * gain_one + shift_one).astype(bf16)
        grad_wide = gather_ctx(grad_rows, ctx)
        bias = small[:, 4 * part :].reshape(3, pairs, 2, ctx, HD)
        bias = lax.dynamic_index_in_dim(bias, me, 3, keepdims=False)
        bias = bias.transpose(1, 0, 2, 3).reshape(1, near * 3 * HD)
        attended, qkv, lse = attend(dot(normed_one, joined_weight), bias, table, start)
        resid = rows.astype(f32) + scatter_ctx(dot(attended, out_full), ctx)
        scaled_two, inv_two = norm_stats(resid)
        normed_wide = gather_ctx((scaled_two * gain_two + shift_two).astype(bf16), ctx)
        gate_full = lax.all_gather(gate_weight, "dp", axis=0, tiled=True)
        up_full = lax.all_gather(up_weight, "dp", axis=0, tiled=True)
    down_full = lax.all_gather(down_weight, "dp", axis=1, tiled=True)

    gate = dot(normed_wide, gate_full)
    upward = dot(normed_wide, up_full)
    sigma = jax.nn.sigmoid(gate)
    swish = gate * sigma
    inner = (swish * upward).astype(bf16)
    d_down = dot_tn(inner, grad_wide).astype(bf16)
    grad_wide, d_down = lax.optimization_barrier((grad_wide, d_down))
    d_down = lax.psum_scatter(d_down, "dp", scatter_dimension=1, tiled=True).astype(f32)
    d_inner = dot_nt(grad_wide, down_full)
    d_gate = (d_inner * upward * sigma * (1.0 + gate * (1.0 - sigma))).astype(bf16)
    d_upward = (d_inner * swish).astype(bf16)
    d_gate_weight = dot_tn(normed_wide, d_gate).astype(bf16)
    d_gate_ready, d_gate_weight = lax.optimization_barrier((d_gate, d_gate_weight))
    d_gate_weight = lax.psum_scatter(d_gate_weight, "dp", scatter_dimension=0, tiled=True).astype(f32)
    if fused:
        d_resid, sums_two, d_proj, branch, d_up_weight = mix_back(
            dp, ctx, d_gate_ready, d_upward, gate_full, up_full, inner, down_full, normed_wide, resid,
            grad_rows, gain_two,
        )
    else:
        branch = dot(inner, down_full)
        d_up_weight = dot_tn(normed_wide, d_upward).astype(bf16)
        d_normed_two = scatter_ctx(dot_nt(d_gate, gate_full) + dot_nt(d_upward, up_full), ctx)
        grad, d_gain_two, d_shift_two = norm_backward(d_normed_two, scaled_two, inv_two, gain_two)
        d_resid = grad_rows.astype(f32) + grad
        d_proj = gather_ctx(d_resid.astype(bf16), ctx)
    d_up_weight = lax.psum_scatter(d_up_weight, "dp", scatter_dimension=0, tiled=True).astype(f32)

    d_attended = dot_nt(d_proj, out_full).astype(bf16)
    d_out_weight = dot_tn(attended, d_proj).astype(bf16)
    d_attended, d_down = lax.optimization_barrier((d_attended, d_down))
    d_joined, d_bias = attend_back(qkv, d_attended, lse, table, start)
    d_joined_weight = dot_tn(normed_one, d_joined).astype(bf16)
    d_bias = d_bias.reshape(pairs, 3, 2, HD).transpose(1, 0, 2, 3)
    d_joined, d_gate_weight = lax.optimization_barrier((d_joined, d_gate_weight))
    if fused:
        d_bias = jnp.pad(d_bias.reshape(dp, -1), ((0, 0), (0, width // dp - near * 3 * HD // dp)))
        grad_input, d_joined_weight, d_out_weight, output, vectors, d_bias = closing(
            dp, ctx, d_joined, joined_weight, d_joined_weight, d_out_weight, branch, rows, d_resid, resid,
            gain_one, sums_two, d_bias,
        )
        d_gain_one, d_shift_one, d_gain_two, d_shift_two = vectors
        d_bias = d_bias[0]
    else:
        output = (resid + scatter_ctx(branch, ctx)).astype(bf16)
        at_me = lax.broadcasted_iota(jnp.int32, (1, ctx, 1, 1), 1) == me
        d_out_weight = jnp.where(at_me, d_out_weight.reshape(near, 1, HD, width), jnp.zeros((), bf16))
        d_out_weight = lax.psum_scatter(
            d_out_weight.reshape(width, width), ("dp", "ctx"), scatter_dimension=0, tiled=True
        ).astype(f32)
        d_normed_one = scatter_ctx(dot_nt(d_joined, joined_weight), ctx)
        scaled_one, inv_one = norm_stats(rows.astype(f32))
        grad, d_gain_one, d_shift_one = norm_backward(d_normed_one, scaled_one, inv_one, gain_one)
        grad_input = d_resid + grad
        d_joined_weight = lax.psum_scatter(d_joined_weight, "dp", scatter_dimension=0, tiled=True)
        blocks = exchange_ctx(d_joined_weight.reshape(ctx, rows_here, near * 3 * HD), ctx)
        blocks = blocks.reshape(ctx, rows_here, pairs, 3, 2, HD).transpose(1, 3, 2, 4, 0, 5)
        d_joined_weight = blocks.reshape(rows_here, 3 * width).astype(f32)
        at_me = (lax.broadcasted_iota(jnp.int32, (1, 1, 1, ctx, 1), 3) == me).astype(f32)
        d_bias = (d_bias[:, :, :, None, :] * at_me).reshape(dp * ctx, -1)
        small = jnp.concatenate(
            [t.reshape(dp * ctx, part) for t in (d_gain_one, d_shift_one, d_gain_two, d_shift_two)]
            + [d_bias],
            axis=1,
        )
        small = lax.psum_scatter(small, ("dp", "ctx"), scatter_dimension=0, tiled=True)[0]
        d_gain_one, d_shift_one, d_gain_two, d_shift_two = [
            small[i * part : (i + 1) * part] for i in range(4)
        ]
        d_bias = small[4 * part :]
    return (
        output[None],
        grad_input[None],
        d_gain_one,
        d_shift_one,
        d_joined_weight,
        d_bias,
        d_out_weight,
        d_gain_two,
        d_shift_two,
        d_gate_weight,
        d_up_weight,
        d_down,
    )


def solution(mesh):
    every = ("dp", "ctx")
    return jax.shard_map(
        functools.partial(shards, mesh.shape["dp"], mesh.shape["ctx"]),
        mesh=mesh,
        in_specs=(
            P("dp", "ctx", None),
            P("dp", None),
            P(every),
            P(every),
            P(every, None),
            P(every),
            P(every, None),
            P(every),
            P(every),
            P("dp", "ctx"),
            P("dp", "ctx"),
            P("ctx", "dp"),
            P("dp", "ctx", None),
        ),
        out_specs=(
            P("dp", "ctx", None),
            P("dp", "ctx", None),
            P(every),
            P(every),
            P(every, None),
            P(every),
            P(every, None),
            P(every),
            P(every),
            P("dp", "ctx"),
            P("dp", "ctx"),
            P("ctx", "dp"),
        ),
        check_vma=False,
    )
```

```python
import functools
import math

import jax
import jax.numpy as jnp
import numpy as np
from jax import lax
from jax.experimental import pallas as pl
from jax.experimental.pallas import tpu as pltpu
from jax.sharding import PartitionSpec as P

HD = 64
ROT = 16
DOC_MAX = 512
PAIR = 2 * HD

norm_eps = 1e-05
masked_value = -1e30
f32 = jnp.float32
bf16 = jnp.bfloat16


def dot(a, b):
    return jnp.dot(a, b, preferred_element_type=f32)


def dot_nt(a, b):
    return lax.dot_general(a, b, (((1,), (1,)), ((), ())), preferred_element_type=f32)


def dot_tn(a, b):
    return lax.dot_general(a, b, (((0,), (0,)), ((), ())), preferred_element_type=f32)


def norm_stats(rows):
    row_mean = jnp.mean(rows, axis=-1, keepdims=True)
    centered = rows - row_mean
    variance = jnp.mean(centered * centered, axis=-1, keepdims=True)
    inv_std = lax.rsqrt(variance + norm_eps)
    return centered * inv_std, inv_std


def norm_backward(grad_normed, scaled, inv_std, gain):
    grad_gain = jnp.sum(grad_normed * scaled, axis=0)
    grad_shift = jnp.sum(grad_normed, axis=0)
    inner_grad = grad_normed * gain
    grad_rows = inv_std * (
        inner_grad
        - jnp.mean(inner_grad, axis=-1, keepdims=True)
        - scaled * jnp.mean(inner_grad * scaled, axis=-1, keepdims=True)
    )
    return grad_rows, grad_gain, grad_shift


def partner(n, k):
    return [(c, c ^ k) for c in range(n)]


def hop(x, n, k):
    return lax.ppermute(x, "ctx", partner(n, k))


def gather_relative(block, n):
    if n != 4:
        return [block] + [hop(block, n, k) for k in range(1, n)]
    half = block.shape[0] // 2
    one = hop(block, n, 1)
    two = hop(block, n, 2)
    low = hop(one[:half], n, 2)
    high = hop(two[half:], n, 1)
    return [block, one, two, jnp.concatenate([low, high], axis=0)]


def gather_ctx(block, n):
    me = lax.axis_index("ctx")
    size = block.shape[0]
    parts = gather_relative(block, n)
    full = jnp.zeros((n * size,) + block.shape[1:], block.dtype)
    for k, part in enumerate(parts):
        full = lax.dynamic_update_slice_in_dim(full, part, (me ^ k) * size, 0)
    return full


def scatter_ctx(partial, n):
    me = lax.axis_index("ctx")
    size = partial.shape[0] // n

    def block(k):
        return lax.dynamic_slice_in_dim(partial, (me ^ k) * size, size, 0)

    if n != 4:
        total = block(0).astype(f32)
        for k in range(1, n):
            total = total + hop(block(k).astype(bf16), n, k).astype(f32)
        return total
    half = size // 2
    far = block(3).astype(bf16)
    low = hop(far[:half], n, 1).astype(f32)
    high = hop(far[half:], n, 2).astype(f32)
    one = block(1).astype(f32)
    two = block(2).astype(f32)
    to_one = jnp.concatenate([one[:half], one[half:] + high], axis=0).astype(bf16)
    to_two = jnp.concatenate([two[:half] + low, two[half:]], axis=0).astype(bf16)
    return block(0).astype(f32) + hop(to_one, n, 1).astype(f32) + hop(to_two, n, 2).astype(f32)


def exchange_ctx(blocks, n):
    me = lax.axis_index("ctx")
    got = lax.dynamic_update_slice_in_dim(
        jnp.zeros_like(blocks), lax.dynamic_slice_in_dim(blocks, me, 1, 0), me, 0
    )
    for k in range(1, n):
        sent = lax.dynamic_slice_in_dim(blocks, me ^ k, 1, 0)
        got = lax.dynamic_update_slice_in_dim(got, hop(sent, n, k), me ^ k, 0)
    return got


MESH = pl.DeviceIdType.MESH
HBM = pl.BlockSpec(memory_space=pltpu.HBM)


class Place:
    def __init__(self, dp):
        self.row = lax.axis_index("dp")
        self.col = lax.axis_index("ctx")
        self.lines = dp // 2
        self.line = self.row // 2
        self.core = self.row % 2
        self.twin = (self.row + 1 - 2 * self.core, self.col)

    def other(self, k):
        col, bit = self.col, 1
        while bit <= k:
            if k & bit:
                col = col + bit * (1 - 2 * ((self.col // bit) % 2))
            bit *= 2
        return col

    def across(self, k):
        return (self.row, self.other(k))

    def above(self):
        return (self.row + 2, self.col)

    def below(self):
        return (self.row - 2, self.col)


def greet(place, ctx):
    barrier = pltpu.get_barrier_semaphore()
    for k in range(1, ctx):
        pl.semaphore_signal(barrier, 1, device_id=place.across(k), device_id_type=MESH)
    pl.semaphore_wait(barrier, ctx - 1)


def remote(src, dst, send, recv, device):
    return pltpu.make_async_remote_copy(
        src_ref=src, dst_ref=dst, send_sem=send, recv_sem=recv, device_id=device, device_id_type=MESH
    )


class LineGather:
    def __init__(self, place, shard, sems):
        self.place, self.shard, self.sems = place, shard, sems

    def row(self, line):
        return line * 2 + self.place.core

    def up(self, hop):
        part = self.shard(self.row(self.place.line - hop + 1))
        return remote(part, part, self.sems.at[0, hop], self.sems.at[1, hop], self.place.above())

    def down(self, hop):
        part = self.shard(self.row(self.place.line + hop - 1))
        return remote(part, part, self.sems.at[2, hop], self.sems.at[3, hop], self.place.below())

    def over(self, at, row):
        part = self.shard(row)
        return remote(part, part, self.sems.at[4, at], self.sems.at[5, at], self.place.twin)

    def sends_up(self, hop):
        return (self.place.line - hop + 1 >= 0) & (self.place.line < self.place.lines - 1)

    def sends_down(self, hop):
        return (self.place.line + hop - 1 < self.place.lines) & (self.place.line > 0)

    def send(self, hop):
        place = self.place
        pl.when(self.sends_up(hop))(lambda: self.up(hop).start())
        pl.when(self.sends_down(hop))(lambda: self.down(hop).start())
        if hop == 1:
            self.over(0, place.row).start()

    def receive(self, hop):
        place = self.place

        @pl.when(place.line - hop >= 0)
        def _():
            part = self.shard(self.row(place.line - hop))
            remote(part, part, self.sems.at[0, hop], self.sems.at[1, hop], place.twin).wait_recv()
            self.over(hop, self.row(place.line - hop)).start()

        @pl.when(place.line + hop < place.lines)
        def _():
            part = self.shard(self.row(place.line + hop))
            remote(part, part, self.sems.at[2, hop], self.sems.at[3, hop], place.twin).wait_recv()
            self.over(place.lines - 1 + hop, self.row(place.line + hop)).start()

    def came_over(self, at, row):
        part = self.shard(row)
        remote(part, part, self.sems.at[4, at], self.sems.at[5, at], self.place.twin).wait_recv()

    def settle(self, hop, use=None):
        place = self.place
        other = 1 - 2 * place.core
        if hop == 0:
            self.came_over(0, place.row + other)
            if use:
                use(place.line)
            return
        for at, line, there in (
            (hop, place.line - hop, place.line - hop >= 0),
            (place.lines - 1 + hop, place.line + hop, place.line + hop < place.lines),
        ):

            @pl.when(there)
            def _():
                self.came_over(at, self.row(line) + other)
                if use:
                    use(line)

    def finish(self):
        place = self.place
        self.over(0, place.row).wait_send()
        for hop in range(1, place.lines):
            pl.when(self.sends_up(hop))(lambda: self.up(hop).wait_send())
            pl.when(self.sends_down(hop))(lambda: self.down(hop).wait_send())
            for at, line, there in (
                (hop, place.line - hop, place.line - hop >= 0),
                (place.lines - 1 + hop, place.line + hop, place.line + hop < place.lines),
            ):
                pl.when(there)(lambda: self.over(at, self.row(line)).wait_send())

    @staticmethod
    def scratch(dp):
        return pltpu.SemaphoreType.DMA((6, dp))


class CtxGather:
    def __init__(self, place, block, full, size, sems):
        self.place, self.block, self.full, self.size, self.sems = place, block, full, size, sems

    def rows(self, col, start=0, size=None):
        size = self.size if size is None else size
        return self.full.at[pl.ds(pl.multiple_of(col * self.size + start, size), size), :]

    def copies(self):
        place, half = self.place, self.size // 2
        me = place.col
        return [
            remote(self.block, self.rows(me), self.sems.at[0, 0], self.sems.at[1, 0], place.across(1)),
            remote(self.block, self.rows(me), self.sems.at[0, 1], self.sems.at[1, 1], place.across(2)),
            remote(
                self.rows(place.other(1), 0, half), self.rows(place.other(1), 0, half),
                self.sems.at[0, 2], self.sems.at[1, 2], place.across(2),
            ),
            remote(
                self.rows(place.other(2), half, half), self.rows(place.other(2), half, half),
                self.sems.at[0, 3], self.sems.at[1, 3], place.across(1),
            ),
        ]

    def arrivals(self):
        place, half = self.place, self.size // 2
        me = place.col
        parts = [self.rows(place.other(1)), self.rows(place.other(2)), self.rows(place.other(3), 0, half), self.rows(place.other(3), half, half)]
        return [
            remote(part, part, self.sems.at[0, i], self.sems.at[1, i], place.across(1))
            for i, part in enumerate(parts)
        ]

    def first(self):
        copies = self.copies()
        copies[0].start()
        copies[1].start()

    def second(self):
        copies, arrivals = self.copies(), self.arrivals()
        arrivals[0].wait_recv()
        copies[2].start()
        arrivals[1].wait_recv()
        copies[3].start()

    def finish(self):
        copies, arrivals = self.copies(), self.arrivals()
        arrivals[2].wait_recv()
        arrivals[3].wait_recv()
        for copy in copies:
            copy.wait_send()

    @staticmethod
    def scratch():
        return pltpu.SemaphoreType.DMA((2, 4))


def greet_all(place, dp, ctx, signal=True, wait=True):
    barrier = pltpu.get_barrier_semaphore()
    if signal:
        for k in range(1, ctx):
            pl.semaphore_signal(barrier, 1, device_id=place.across(k), device_id_type=MESH)
        for k in range(1, dp):
            pl.semaphore_signal(barrier, 1, device_id=((place.row + k) % dp, place.col), device_id_type=MESH)
    if wait:
        pl.semaphore_wait(barrier, ctx + dp - 2)


CHUNKS = 4
PARTS = 2


class CtxReduce:
    def __init__(self, place, block, total, sent, got, sems):
        self.place, self.block, self.total = place, block, total
        self.sent, self.got, self.sems = sent, got, sems
        self.size = total.shape[1] // CHUNKS

    def chunk(self, j):
        return pl.ds(j * self.size, self.size)

    def copy(self, kind, j):
        way = kind if kind else 1 + j % 2
        return remote(
            self.sent.at[kind, self.chunk(j)], self.got.at[kind, self.chunk(j)],
            self.sems.at[0, kind, j], self.sems.at[1, kind, j], self.place.across(way),
        )

    def start(self):
        self.start_far()
        self.start_near()

    def start_far(self):
        self.sent[0] = self.block(self.place.other(3)).astype(bf16)
        for j in range(CHUNKS):
            self.copy(0, j).start()

    def start_near(self):
        place = self.place
        for kind in (1, 2):
            self.total[kind - 1] = self.block(place.other(kind))
            for j in range(CHUNKS):
                if kind == 1 + j % 2:
                    self.sent[kind, self.chunk(j)] = self.total[kind - 1, self.chunk(j)].astype(bf16)
                    self.copy(kind, j).start()

    def relay(self):
        for j in range(CHUNKS):
            kind = 2 - j % 2
            self.copy(0, j).wait_recv()
            share = self.total[kind - 1, self.chunk(j)] + self.got[0, self.chunk(j)].astype(f32)
            self.sent[kind, self.chunk(j)] = share.astype(bf16)
            self.copy(kind, j).start()
        self.total[0] = self.block(self.place.col)

    def sum(self, j):
        for kind in (1, 2):
            self.copy(kind, j).wait_recv()
        rows = self.chunk(j)
        return self.total[0, rows] + self.got[1, rows].astype(f32) + self.got[2, rows].astype(f32)

    def finish(self):
        for kind in range(3):
            for j in range(CHUNKS):
                self.copy(kind, j).wait_send()

    @staticmethod
    def scratch(size, width):
        return [
            pltpu.VMEM((2, size, width), f32),
            pltpu.VMEM((3, size, width), bf16),
            pltpu.VMEM((3, size, width), bf16),
            pltpu.SemaphoreType.DMA((2, 3, CHUNKS)),
        ]


class CtxSpread:
    def __init__(self, place, made, full, sems):
        self.place, self.made, self.full, self.sems = place, made, full, sems
        self.size = made.shape[0] // CHUNKS

    def rows(self, col, j):
        at = (col * CHUNKS + j) * self.size
        return self.full.at[pl.ds(pl.multiple_of(at, self.size), self.size), :]

    def copy(self, kind, j):
        place = self.place
        if kind < 2:
            part, there = self.made.at[pl.ds(j * self.size, self.size), :], self.rows(place.col, j)
            way = 1 + kind
        else:
            way = 2 - j % 2
            part = there = self.rows(place.other(3 - way), j)
        return remote(part, there, self.sems.at[0, kind, j], self.sems.at[1, kind, j], place.across(way))

    def arrived(self, kind, j):
        part = self.rows(self.place.other(kind + 1), j)
        remote(
            part, part, self.sems.at[0, kind, j], self.sems.at[1, kind, j], self.place.across(1)
        ).wait_recv()

    def local(self, j):
        part = self.made.at[pl.ds(j * self.size, self.size), :]
        return pltpu.make_async_copy(part, self.rows(self.place.col, j), self.sems.at[0, 3, j])

    def send(self, j):
        self.copy(0, j).start()
        self.copy(1, j).start()
        self.local(j).start()

    def relay(self, j):
        way = 2 - j % 2
        self.arrived(2 - way, j)
        self.copy(2, j).start()

    def finish(self):
        for j in range(CHUNKS):
            way = 2 - j % 2
            self.arrived(way - 1, j)
            self.arrived(2, j)
            self.local(j).wait()
            for kind in range(3):
                self.copy(kind, j).wait_send()

    @staticmethod
    def scratch():
        return pltpu.SemaphoreType.DMA((2, 4, CHUNKS))


def rows_of(ref, col, size):
    return ref[pl.ds(pl.multiple_of(col * size, size), size), :]


class LineReduce:
    def __init__(self, place, parts, own, pair, got, sems):
        self.place, self.parts, self.own, self.pair, self.got, self.sems = place, parts, own, pair, got, sems

    def load(self, line):
        return pltpu.make_async_copy(
            self.parts.at[2 * line + self.place.core], self.own.at[line], self.sems.at[6, line]
        )

    def swap(self, line):
        row = 2 * line + 1 - self.place.core
        return remote(
            self.parts.at[row], self.pair.at[line], self.sems.at[0, line], self.sems.at[1, line], self.place.twin
        )

    def start(self):
        for line in range(self.place.lines):
            self.swap(line).start()

    def add(self):
        for line in range(self.place.lines):
            self.load(line).wait()
            self.swap(line).wait_recv()
            self.pair[line] = (self.own[line].astype(f32) + self.pair[line].astype(f32)).astype(bf16)

    def up(self, far):
        part = self.place.line + far
        return remote(
            self.pair.at[part], self.got.at[part], self.sems.at[2, far], self.sems.at[3, far], self.place.above()
        )

    def down(self, far):
        part = self.place.line - far
        slot = part if far > 1 else self.place.lines
        return remote(
            self.pair.at[part], self.got.at[slot], self.sems.at[4, far], self.sems.at[5, far], self.place.below()
        )

    def came_up(self, far):
        slot = self.got.at[self.place.line + far]
        remote(slot, slot, self.sems.at[2, far + 1], self.sems.at[3, far + 1], self.place.twin).wait_recv()

    def came_down(self, far):
        slot = self.got.at[self.place.line - far if far else self.place.lines]
        remote(slot, slot, self.sems.at[4, far + 1], self.sems.at[5, far + 1], self.place.twin).wait_recv()

    def send(self, far):
        place = self.place

        @pl.when(place.line + far < place.lines)
        def _():
            @pl.when(place.line > 0)
            def _():
                self.came_up(far)
                part = place.line + far
                self.pair[part] = (self.pair[part].astype(f32) + self.got[part].astype(f32)).astype(bf16)

            self.up(far).start()

        @pl.when(place.line - far >= 0)
        def _():
            @pl.when(place.line < place.lines - 1)
            def _():
                self.came_down(far)
                part = place.line - far
                self.pair[part] = (self.pair[part].astype(f32) + self.got[part].astype(f32)).astype(bf16)

            self.down(far).start()

    def collect(self, out):
        place = self.place
        out[...] = self.pair[place.line].astype(f32)

        @pl.when(place.line > 0)
        def _():
            self.came_up(0)
            out[...] += self.got[place.line].astype(f32)

        @pl.when(place.line < place.lines - 1)
        def _():
            self.came_down(0)
            out[...] += self.got[place.lines].astype(f32)

    def finish(self):
        place = self.place
        for line in range(place.lines):
            self.swap(line).wait_send()
        for far in range(1, place.lines):
            pl.when(place.line + far < place.lines)(lambda: self.up(far).wait_send())
            pl.when(place.line - far >= 0)(lambda: self.down(far).wait_send())

    @staticmethod
    def scratch(dp, tile):
        return [
            pltpu.VMEM((dp // 2,) + tile, bf16),
            pltpu.VMEM((dp // 2,) + tile, bf16),
            pltpu.VMEM((dp // 2 + 1,) + tile, bf16),
            pltpu.SemaphoreType.DMA((7, dp // 2)),
        ]


def mix_back_kernel(
    dp, ctx, gate_ref, up_ref, gate_weight_hbm, up_weight_hbm, inner_hbm, down_hbm, normed_hbm, gate_parts,
    resid_ref, cot_ref, gain_ref,
    d_resid_hbm, sums_ref, wide_ref, branch_hbm, d_up_hbm, d_gate_ref,
    total, sent, got, made, gate_weight_ref, up_weight_ref, inner, down_ref, normed, branch, d_up,
    own, pair, line_got, line_sem,
    reduce_sem, spread_sem, load_sem, inner_sem, normed_sem, branch_sem, d_up_sem, d_resid_sem,
):
    place = Place(dp)
    size, width = cot_ref.shape
    cols = normed.shape[2]
    loads = [
        pltpu.make_async_copy(src, dst, load_sem.at[i])
        for i, (src, dst) in enumerate(
            ((gate_weight_hbm, gate_weight_ref), (up_weight_hbm, up_weight_ref), (down_hbm, down_ref))
        )
    ]
    for load in loads[:2]:
        load.start()
    greet_all(place, dp, ctx)
    line = LineReduce(place, gate_parts, own, pair, line_got, line_sem)
    line.start()
    for i in range(place.lines):
        line.load(i).start()
    for load in loads[:2]:
        load.wait()

    def block(col):
        return dot_nt(rows_of(gate_ref, col, size), gate_weight_ref[...]) + dot_nt(
            rows_of(up_ref, col, size), up_weight_ref[...]
        )

    d_up_count, branch_count = width // cols, ctx

    def normed_load(i):
        return pltpu.make_async_copy(
            normed_hbm.at[:, pl.ds(i * cols, cols)], normed.at[i % 2], normed_sem.at[i % 2]
        )

    def inner_load(i):
        return pltpu.make_async_copy(
            inner_hbm.at[pl.ds(i * size, size), :], inner.at[i % 2], inner_sem.at[i % 2]
        )

    def d_up_copy(i):
        return pltpu.make_async_copy(
            d_up.at[i % 2], d_up_hbm.at[pl.ds(i * cols, cols), :], d_up_sem.at[i % 2]
        )

    def branch_copy(i):
        return pltpu.make_async_copy(
            branch.at[i % 2], branch_hbm.at[pl.ds(i * size, size), :], branch_sem.at[i % 2]
        )

    def d_up_piece(i):
        normed_load(i).wait()
        if i > 1:
            d_up_copy(i - 2).wait()
        d_up[i % 2] = dot_tn(normed[i % 2], up_ref[...]).astype(bf16)
        d_up_copy(i).start()
        if i + 2 < d_up_count:
            normed_load(i + 2).start()

    def branch_piece(i):
        if i == 0:
            loads[2].wait()
        inner_load(i).wait()
        if i > 1:
            branch_copy(i - 2).wait()
        branch[i % 2] = dot(inner[i % 2], down_ref[...]).astype(bf16)
        branch_copy(i).start()
        if i + 2 < branch_count:
            inner_load(i + 2).start()

    def d_resid_copy(j):
        rows = reduce.chunk(j)
        return pltpu.make_async_copy(total.at[1, rows, :], d_resid_hbm.at[rows, :], d_resid_sem.at[j])

    pieces = [functools.partial(d_up_piece, i) for i in range(d_up_count)]
    pieces += [functools.partial(branch_piece, i) for i in range(branch_count)]

    reduce = CtxReduce(place, block, total, sent, got, reduce_sem)
    spread = CtxSpread(place, made, wide_ref, spread_sem)
    reduce.start_far()
    loads[2].start()
    for i in range(2):
        normed_load(i).start()
        inner_load(i).start()
    reduce.start_near()
    line.add()
    line.send(place.lines - 1)
    reduce.relay()
    sums_ref[...] = jnp.zeros_like(sums_ref)
    far = place.lines - 2
    for j in range(CHUNKS):
        for piece in pieces[2 * j : 2 * j + 2]:
            piece()
        rows = reduce.chunk(j)
        scaled, inv_std = norm_stats(resid_ref[rows, :])
        grad, d_gain, d_shift = norm_backward(reduce.sum(j), scaled, inv_std, gain_ref[...])
        sums_ref[0:1, :] += d_gain[None]
        sums_ref[1:2, :] += d_shift[None]
        grad = cot_ref[rows, :].astype(f32) + grad
        total[1, rows, :] = grad
        d_resid_copy(j).start()
        made[rows, :] = grad.astype(bf16)
        spread.send(j)
        if j:
            spread.relay(j - 1)
        if j == 1 and far > 0:
            line.send(far)
            far -= 1
    pieces[2 * CHUNKS]()
    spread.relay(CHUNKS - 1)
    while far > 0:
        line.send(far)
        far -= 1
    for piece in pieces[2 * CHUNKS + 1 :]:
        piece()
    spread.finish()
    line.collect(d_gate_ref)
    line.finish()
    reduce.finish()
    for i in (1, 2):
        d_up_copy(d_up_count - i).wait()
        branch_copy(branch_count - i).wait()
    for j in range(CHUNKS):
        d_resid_copy(j).wait()


def mix_back(dp, ctx, d_gate, d_up, gate_weight, up_weight, inner, down, normed, gate_parts, resid, cot, gain):
    size, width = cot.shape
    hidden = d_up.shape[1]
    own = width // dp
    cols = width // ctx // 2
    vmem = pl.BlockSpec(memory_space=pltpu.VMEM)
    return pl.pallas_call(
        functools.partial(mix_back_kernel, dp, ctx),
        in_specs=[vmem] * 2 + [HBM] * 6 + [vmem] * 3,
        out_specs=[HBM, vmem, HBM, HBM, HBM, vmem],
        out_shape=[
            jax.ShapeDtypeStruct((size, width), f32),
            jax.ShapeDtypeStruct((2, width), f32),
            jax.ShapeDtypeStruct((ctx * size, width), bf16),
            jax.ShapeDtypeStruct((ctx * size, width), bf16),
            jax.ShapeDtypeStruct((width, hidden), bf16),
            jax.ShapeDtypeStruct((own, hidden), f32),
        ],
        scratch_shapes=CtxReduce.scratch(size, width)[:3]
        + [
            pltpu.VMEM((size, width), bf16),
            pltpu.VMEM((width, hidden), bf16),
            pltpu.VMEM((width, hidden), bf16),
            pltpu.VMEM((2, size, hidden), bf16),
            pltpu.VMEM((hidden, width), bf16),
            pltpu.VMEM((2, ctx * size, cols), bf16),
            pltpu.VMEM((2, size, width), bf16),
            pltpu.VMEM((2, cols, hidden), bf16),
        ]
        + LineReduce.scratch(dp, (own, hidden))
        + [
            CtxReduce.scratch(size, width)[3],
            CtxSpread.scratch(),
            pltpu.SemaphoreType.DMA((3,)),
            pltpu.SemaphoreType.DMA((2,)),
            pltpu.SemaphoreType.DMA((2,)),
            pltpu.SemaphoreType.DMA((2,)),
            pltpu.SemaphoreType.DMA((2,)),
            pltpu.SemaphoreType.DMA((CHUNKS,)),
        ],
        compiler_params=pltpu.CompilerParams(
            collective_id=3, has_side_effects=True, vmem_limit_bytes=62 << 20
        ),
        cost_estimate=pl.CostEstimate(
            flops=8 * d_gate.size * width, transcendentals=0, bytes_accessed=180 << 20
        ),
    )(
        d_gate, d_up, gate_weight, up_weight, inner, down, normed, gate_parts.reshape(dp, own, hidden),
        resid, cot, gain.reshape(1, width),
    )


class CtxReduceReady:
    def __init__(self, place, full, have, got, sems, load_sems):
        self.place, self.full, self.have, self.got, self.sems, self.load_sems = place, full, have, got, sems, load_sems
        self.height = have.shape[1]
        self.size = self.height // CHUNKS

    def chunk(self, j):
        return pl.ds(j * self.size, self.size)

    def load(self, kind):
        col = self.place.other(kind)
        rows = pl.ds(pl.multiple_of(col * self.height, self.height), self.height)
        return pltpu.make_async_copy(self.full.at[rows, :], self.have.at[kind], self.load_sems.at[kind])

    def copy(self, kind, j):
        place = self.place
        if kind:
            part, way = self.have.at[kind, self.chunk(j)], kind
        else:
            at = (place.other(3) * CHUNKS + j) * self.size
            part, way = self.full.at[pl.ds(pl.multiple_of(at, self.size), self.size), :], 1 + j % 2
        return remote(
            part, self.got.at[kind, self.chunk(j)], self.sems.at[0, kind, j], self.sems.at[1, kind, j],
            place.across(way),
        )

    def start(self):
        for j in range(CHUNKS):
            self.copy(0, j).start()
        for kind in (1, 2):
            self.load(kind).wait()
            for j in range(CHUNKS):
                if kind == 1 + j % 2:
                    self.copy(kind, j).start()

    def relay(self):
        for j in range(CHUNKS):
            kind, rows = 2 - j % 2, self.chunk(j)
            self.copy(0, j).wait_recv()
            share = self.have[kind, rows].astype(f32) + self.got[0, rows].astype(f32)
            self.have[kind, rows] = share.astype(bf16)
            self.copy(kind, j).start()

    def sum(self, j):
        for kind in (1, 2):
            self.copy(kind, j).wait_recv()
        rows = self.chunk(j)
        return self.have[0, rows].astype(f32) + self.got[1, rows].astype(f32) + self.got[2, rows].astype(f32)

    def finish(self):
        for kind in range(3):
            for j in range(CHUNKS):
                self.copy(kind, j).wait_send()


def closing_kernel(
    dp, ctx,
    d_joined_hbm, weight_hbm, qkv_parts, out_parts, branch_hbm, rows_hbm, d_resid_hbm, resid_hbm,
    gain_ref, sums_two_ref, bias_ref,
    grad_ref, qkv_ref, out_ref, output_ref, vectors_ref, d_bias_ref,
    d_joined_ref, weight_ref, rows_ref, d_resid_ref, resid_ref, load_sem,
    total, sent, got, reduce_sem, qkv_own, qkv_pair, qkv_got, qkv_sem, out_own, out_pair, out_got, out_sem,
    have, branch_got, branch_sem, branch_load_sem,
    sums, tiles, tiles_got, small, small_sem, mine, swap_out, swap_in, swap_sem,
):
    place = Place(dp)
    me, row = place.col, place.row
    lines = [
        LineReduce(place, qkv_parts, qkv_own, qkv_pair, qkv_got, qkv_sem),
        LineReduce(place, out_parts, out_own, out_pair, out_got, out_sem),
    ]
    loads = [
        pltpu.make_async_copy(src, dst, load_sem.at[i])
        for i, (src, dst) in enumerate(
            (
                (d_joined_hbm, d_joined_ref), (weight_hbm, weight_ref), (rows_hbm, rows_ref),
                (d_resid_hbm, d_resid_ref), (resid_hbm, resid_ref),
            )
        )
    ]
    for load in loads[:2]:
        load.start()
    greet_all(place, dp, ctx)
    for line in lines:
        line.start()
    for i in range(place.lines):
        for line in lines:
            line.load(i).start()
    branch = CtxReduceReady(place, branch_hbm, have, branch_got, branch_sem, branch_load_sem)
    for kind in range(3):
        branch.load(kind).start()
    for load in loads[2:]:
        load.start()

    size, width = rows_ref.shape
    for load in loads[:2]:
        load.wait()
    reduce = CtxReduce(
        place, lambda col: dot_nt(rows_of(d_joined_ref, col, size), weight_ref[...]), total, sent, got, reduce_sem
    )
    reduce.start_far()
    for line in lines:
        line.add()
        line.send(place.lines - 1)
    reduce.start_near()
    branch.start()
    reduce.relay()
    for far in range(place.lines - 2, 1, -1):
        for line in lines:
            line.send(far)

    sums[...] = jnp.zeros_like(sums)
    for load in loads[2:]:
        load.wait()
    branch.load(0).wait()
    for j in range(CHUNKS):
        rows = reduce.chunk(j)
        scaled, inv_std = norm_stats(rows_ref[rows, :].astype(f32))
        grad, d_gain, d_shift = norm_backward(reduce.sum(j), scaled, inv_std, gain_ref[...])
        sums[0:1, :] += d_gain[None]
        sums[1:2, :] += d_shift[None]
        grad_ref[rows, :] = d_resid_ref[rows, :] + grad
    branch.relay()
    if place.lines > 2:
        for line in lines:
            line.send(1)

    part = width // dp
    tiles[...] = jnp.zeros_like(tiles)
    for i in range(dp):
        lanes = slice(i * part, (i + 1) * part)
        tiles[i, 0:2, :] = sums[:, lanes]
        tiles[i, 2:4, :] = sums_two_ref[:, lanes]
        tiles[i, 4:5, :] = bias_ref[i : i + 1, :]
    sends = [
        remote(tiles.at[(row + k) % dp], tiles_got.at[k], small_sem.at[0, k], small_sem.at[1, k], ((row + k) % dp, me))
        for k in range(1, dp)
    ]
    for copy in sends:
        copy.start()
    tile = tiles[row]
    for k in range(1, dp):
        sends[k - 1].wait()
        tile = tile + tiles_got[k]
    tiles_got[0] = tile
    small[me] = tile
    spreads = [
        remote(tiles_got.at[0], small.at[me], small_sem.at[2, k], small_sem.at[3, k], place.across(k))
        for k in range(1, ctx)
    ]
    for copy in spreads:
        copy.start()

    for j in range(CHUNKS):
        rows = branch.chunk(j)
        output_ref[rows, :] = (resid_ref[rows, :] + branch.sum(j)).astype(bf16)

    for k in range(1, ctx):
        spreads[k - 1].wait_send()
        part = small.at[place.other(k)]
        remote(part, part, small_sem.at[2, k], small_sem.at[3, k], place.across(k)).wait_recv()
    four = sum(small[c, 0:4, :] for c in range(ctx))
    piece = vectors_ref.shape[1]
    slots = d_bias_ref.shape[1] // HD
    vectors = four[:, :piece]
    biases = [small[i % ctx, 4:5, i // ctx * HD : (i // ctx + 1) * HD] for i in range(slots * ctx)]
    chosen = biases[:slots]
    for c in range(1, ctx):
        vectors = jnp.where(me == c, four[:, c * piece : (c + 1) * piece], vectors)
        chosen = [jnp.where(me == c, biases[slots * c + i], chosen[i]) for i in range(slots)]
    vectors_ref[...] = vectors
    for i in range(slots):
        d_bias_ref[:, i * HD : (i + 1) * HD] = chosen[i]

    lines[0].collect(mine)
    depth = mine.shape[0] // ctx
    swap_out[...] = mine[...].astype(bf16)
    swaps = [
        remote(
            swap_out.at[pl.ds(pl.multiple_of(place.other(k) * depth, depth), depth), :], swap_in.at[me],
            swap_sem.at[0, k], swap_sem.at[1, k], place.across(k),
        )
        for k in range(1, ctx)
    ]
    for copy in swaps:
        copy.start()
    swap_in[me] = rows_of(swap_out, me, depth)
    lines[1].collect(out_ref)
    for k in range(1, ctx):
        part = swap_in.at[place.other(k)]
        remote(part, part, swap_sem.at[0, k], swap_sem.at[1, k], place.across(k)).wait_recv()
    low = head_lanes((depth, PAIR))
    for p in range(mine.shape[1] // (3 * PAIR)):
        for t in range(3):
            lanes = slice((3 * p + t) * PAIR, (3 * p + t + 1) * PAIR)
            for c in range(0, ctx, 2):
                a = swap_in[c, :, lanes].astype(f32)
                b = swap_in[c + 1, :, lanes].astype(f32)
                at = t * width + (2 * p * ctx + c) * HD
                qkv_ref[:, at : at + PAIR] = jnp.where(low, a, pltpu.roll(b, HD, 1))
                at = at + ctx * HD
                qkv_ref[:, at : at + PAIR] = jnp.where(low, pltpu.roll(a, HD, 1), b)
    for copy in swaps:
        copy.wait_send()
    for line in lines:
        line.finish()
    branch.finish()
    reduce.finish()


def closing(dp, ctx, d_joined, weight, d_qkv, d_out, branch, rows, d_resid, resid, gain, sums_two, bias):
    size, width = rows.shape
    near = weight.shape[1]
    own, tall = width // dp, d_out.shape[0] // dp
    vmem = pl.BlockSpec(memory_space=pltpu.VMEM)
    reduce_scratch = CtxReduce.scratch(size, width)
    max_peers = max(dp, ctx)
    return pl.pallas_call(
        functools.partial(closing_kernel, dp, ctx),
        in_specs=[HBM] * 8 + [vmem] * 3,
        out_specs=[vmem] * 6,
        out_shape=[
            jax.ShapeDtypeStruct((size, width), f32),
            jax.ShapeDtypeStruct((own // ctx, 3 * width), f32),
            jax.ShapeDtypeStruct((tall, width), f32),
            jax.ShapeDtypeStruct((size, width), bf16),
            jax.ShapeDtypeStruct((4, own // ctx), f32),
            jax.ShapeDtypeStruct((1, 3 * own // ctx), f32),
        ],
        scratch_shapes=[
            pltpu.VMEM((ctx * size, near), bf16),
            pltpu.VMEM((width, near), bf16),
            pltpu.VMEM((size, width), bf16),
            pltpu.VMEM((size, width), f32),
            pltpu.VMEM((size, width), f32),
            pltpu.SemaphoreType.DMA((5,)),
        ]
        + reduce_scratch
        + LineReduce.scratch(dp, (own, near))
        + LineReduce.scratch(dp, (tall, width))
        + reduce_scratch[1:]
        + [
            pltpu.SemaphoreType.DMA((3,)),
            pltpu.VMEM((2, width), f32),
            pltpu.VMEM((dp, 8, own), f32),
            pltpu.VMEM((dp, 8, own), f32),
            pltpu.VMEM((ctx, 8, own), f32),
            pltpu.SemaphoreType.DMA((4, max_peers)),
            pltpu.VMEM((own, near), f32),
            pltpu.VMEM((own, near), bf16),
            pltpu.VMEM((ctx, own // ctx, near), bf16),
            pltpu.SemaphoreType.DMA((2, ctx)),
        ],
        compiler_params=pltpu.CompilerParams(
            collective_id=1, has_side_effects=True, vmem_limit_bytes=62 << 20
        ),
        cost_estimate=pl.CostEstimate(
            flops=2 * d_joined.size * width, transcendentals=0, bytes_accessed=200 << 20
        ),
    )(
        d_joined, weight, d_qkv.reshape(dp, own, near), d_out.reshape(dp, tall, width), branch,
        rows, d_resid, resid, gain.reshape(1, width), sums_two, bias,
    )


def turn(x, table_ref):
    return (
        x * table_ref[0]
        + pltpu.roll(x, PAIR - ROT // 2, 1) * table_ref[1]
        + pltpu.roll(x, ROT // 2, 1) * table_ref[2]
    )


def turn_back(x, table_ref):
    return (
        x * table_ref[0]
        - pltpu.roll(x, PAIR - ROT // 2, 1) * table_ref[1]
        - pltpu.roll(x, ROT // 2, 1) * table_ref[2]
    )


def head_lanes(shape):
    return lax.broadcasted_iota(jnp.int32, shape, 1) < HD


def span(full_len, step, at):
    return max(0, (at - DOC_MAX + 1) // step * step), at + step


def parts_of(low, at, step):
    return ([(low, at, False)] if low < at else []) + [(at, at + step, True)]


def masked(scores, start, first, causal):
    keys = lax.broadcasted_iota(jnp.int32, scores.shape, 1)
    allowed = keys >= start - first
    if causal:
        allowed = allowed & (keys <= lax.broadcasted_iota(jnp.int32, scores.shape, 0))
    return jnp.where(allowed, scores, masked_value)


def one_head(x, head):
    return jnp.where(head_lanes(x.shape) == (head == 0), x, jnp.zeros_like(x))


def attend_kernel(step, joined_ref, bias_ref, table_ref, start_ref, out_ref, qkv_ref, lse_ref):
    full_len = joined_ref.shape[0]
    scale = 1.0 / math.sqrt(HD)
    for t in range(3):
        lanes = slice(t * PAIR, (t + 1) * PAIR)
        x = joined_ref[:, lanes] + bias_ref[:, lanes]
        if t < 2:
            x = turn(x, table_ref)
        qkv_ref[:, lanes] = x.astype(bf16)
    for at in range(0, full_len, step):
        parts = parts_of(span(full_len, step, at)[0], at, step)
        start = start_ref[at : at + step, :1]
        q = qkv_ref[at : at + step, :PAIR] * bf16(scale)
        total = jnp.zeros((step, PAIR), f32)
        logs = []
        for head in range(2):
            qm = one_head(q, head)
            scores = [
                masked(dot_nt(qm, qkv_ref[low:high, PAIR : 2 * PAIR]), start, low, causal)
                for low, high, causal in parts
            ]
            tops = [jnp.max(s, axis=1, keepdims=True) for s in scores]
            top = functools.reduce(jnp.maximum, tops)
            norm, sums = 0.0, 0.0
            for s, (low, high, _) in zip(scores, parts):
                e = jnp.exp(s - top)
                norm = norm + jnp.sum(e, axis=1, keepdims=True)
                sums = sums + dot(e.astype(bf16), one_head(qkv_ref[low:high, 2 * PAIR :], head))
            total = total + sums * (1.0 / norm)
            logs.append(top + jnp.log(norm))
        out_ref[at : at + step, :] = total.astype(bf16)
        lse_ref[at : at + step, :] = jnp.where(head_lanes((step, PAIR)), logs[0], logs[1])


def attend_back_kernel(
    step, qkv_ref, grad_ref, lse_ref, table_ref, start_ref, out_ref, sum_ref, dk_ref, dv_ref
):
    full_len = qkv_ref.shape[0]
    scale = 1.0 / math.sqrt(HD)
    dk_ref[...] = jnp.zeros_like(dk_ref)
    dv_ref[...] = jnp.zeros_like(dv_ref)
    total = jnp.zeros((1, PAIR), f32)
    for at in range(0, full_len, step):
        rows = slice(at, at + step)
        parts = parts_of(span(full_len, step, at)[0], at, step)
        start = start_ref[rows, :1]
        q = qkv_ref[rows, :PAIR] * bf16(scale)
        g = grad_ref[rows, :]
        dq = jnp.zeros((step, PAIR), f32)
        dk = [jnp.zeros((high - low, PAIR), f32) for low, high, _ in parts]
        dv = [jnp.zeros((high - low, PAIR), f32) for low, high, _ in parts]
        for head in range(2):
            qm, gm = one_head(q, head), one_head(g, head)
            lse = lse_ref[rows, head * HD : head * HD + 1]
            probs, dps, mean = [], [], 0.0
            for low, high, causal in parts:
                s = masked(dot_nt(qm, qkv_ref[low:high, PAIR : 2 * PAIR]), start, low, causal)
                probs.append(jnp.exp(s - lse))
                dps.append(dot_nt(gm, qkv_ref[low:high, 2 * PAIR :]))
                mean = mean + jnp.sum(dps[-1] * probs[-1], axis=1, keepdims=True)
            for i, (low, high, _) in enumerate(parts):
                ds = (probs[i] * (dps[i] - mean)).astype(bf16)
                dq = dq + dot(ds, one_head(qkv_ref[low:high, PAIR : 2 * PAIR], head))
                dk[i] = dk[i] + dot_tn(ds, qm)
                dv[i] = dv[i] + dot_tn(probs[i].astype(bf16), gm)
        for i, (low, high, _) in enumerate(parts):
            dk_ref[low:high, :] += dk[i]
            dv_ref[low:high, :] += dv[i]
        dq = turn_back(dq * scale, table_ref.at[:, rows, :]).astype(bf16)
        out_ref[rows, :PAIR] = dq
        total = total + jnp.sum(dq.astype(f32), axis=0, keepdims=True)
    sum_ref[:, :PAIR] = total
    dk = turn_back(dk_ref[...], table_ref).astype(bf16)
    out_ref[:, PAIR : 2 * PAIR] = dk
    sum_ref[:, PAIR : 2 * PAIR] = jnp.sum(dk.astype(f32), axis=0, keepdims=True)
    dv = dv_ref[...].astype(bf16)
    out_ref[:, 2 * PAIR :] = dv
    sum_ref[:, 2 * PAIR :] = jnp.sum(dv.astype(f32), axis=0, keepdims=True)


def whole(shape):
    return pl.BlockSpec(shape, lambda p: (0,) * len(shape))


def attend_step(full_len):
    return min(256, full_len)


def attend(joined, bias, table, start):
    full_len, width = joined.shape
    pairs = width // (3 * PAIR)
    step = attend_step(full_len)
    seen = sum(span(full_len, step, at)[1] - span(full_len, step, at)[0] for at in range(0, full_len, step)) * step
    wide = pl.BlockSpec((full_len, 3 * PAIR), lambda p: (0, p))
    thin = pl.BlockSpec((full_len, PAIR), lambda p: (0, p))
    return pl.pallas_call(
        functools.partial(attend_kernel, step),
        grid=(pairs,),
        in_specs=[
            wide,
            pl.BlockSpec((1, 3 * PAIR), lambda p: (0, p)),
            whole(table.shape),
            whole(start.shape),
        ],
        out_specs=[thin, wide, thin],
        out_shape=[
            jax.ShapeDtypeStruct((full_len, pairs * PAIR), bf16),
            jax.ShapeDtypeStruct((full_len, width), bf16),
            jax.ShapeDtypeStruct((full_len, pairs * PAIR), f32),
        ],
        compiler_params=pltpu.CompilerParams(vmem_limit_bytes=40 << 20),
        cost_estimate=pl.CostEstimate(
            flops=pairs * seen * PAIR * 8, transcendentals=pairs * seen * 2, bytes_accessed=full_len * width * 8
        ),
    )(joined, bias, table, start)


def attend_back(qkv, grad, lse, table, start):
    full_len, width = qkv.shape
    pairs = width // (3 * PAIR)
    step = attend_step(full_len)
    seen = sum(span(full_len, step, at)[1] - span(full_len, step, at)[0] for at in range(0, full_len, step)) * step
    wide = pl.BlockSpec((full_len, 3 * PAIR), lambda p: (0, p))
    thin = pl.BlockSpec((full_len, PAIR), lambda p: (0, p))
    return pl.pallas_call(
        functools.partial(attend_back_kernel, step),
        grid=(pairs,),
        in_specs=[wide, thin, thin, whole(table.shape), whole(start.shape)],
        out_specs=[wide, pl.BlockSpec((1, 3 * PAIR), lambda p: (0, p))],
        out_shape=[
            jax.ShapeDtypeStruct((full_len, width), bf16),
            jax.ShapeDtypeStruct((1, width), f32),
        ],
        scratch_shapes=[pltpu.VMEM((full_len, PAIR), f32), pltpu.VMEM((full_len, PAIR), f32)],
        compiler_params=pltpu.CompilerParams(vmem_limit_bytes=40 << 20),
        cost_estimate=pl.CostEstimate(
            flops=pairs * seen * PAIR * 20, transcendentals=pairs * seen * 2, bytes_accessed=full_len * width * 8
        ),
    )(*[pltpu.with_memory_space_constraint(x, pltpu.HBM) for x in (qkv, grad, lse, table, start)])


def forward_kernel(
    dp, ctx, step,
    gain_one, shift_one, gain_two, shift_two, bias, start_ref, table_hbm,
    qkv_hbm, out_weight_ref, rows_ref, cot_ref, gate_hbm, up_hbm,
    params_ref, weight_hbm, out_hbm, normed_hbm, cot_all, attended_hbm, heads_hbm, lse_hbm, resid_hbm, wide_ref,
    gate_all, up_all,
    small_all, table_ref, small_ref, qkv_ref, blocks, rows_all, weight_ref, normed_ref, joined_ref, bias_ref, out_all,
    attended_ref, heads_ref, lse_ref, total, sent, got, made, resid_ref,
    normed_sem, weight_sem, local_sem, swap_sem, small_sem, line_joined, line_out, line_gate, line_up, rows_sem, cot_sem,
    late_sem, reduce_sem, spread_sem, resid_sem,
):
    place = Place(dp)
    me, row = place.col, place.row
    depth = qkv_ref.shape[0]
    length, width = rows_ref.shape
    rows_out = out_weight_ref.shape[0]
    tall = ctx * depth

    qkv_copy = pltpu.make_async_copy(qkv_hbm, qkv_ref, local_sem.at[4])
    qkv_copy.start()
    table_copy = pltpu.make_async_copy(table_hbm, table_ref, late_sem.at[0])
    table_copy.start()
    greet_all(place, dp, ctx, wait=False)
    small_ref[...] = jnp.zeros_like(small_ref)
    for i, vector in enumerate((gain_one, shift_one, gain_two, shift_two)):
        small_ref[i // 2 : i // 2 + 1, i % 2 * HD : (i % 2 + 1) * HD] = vector[...].astype(f32)
    for i in range(bias.shape[1] // HD):
        small_ref[2 + i // 2 : 3 + i // 2, i % 2 * HD : (i % 2 + 1) * HD] = bias[
            :, i * HD : (i + 1) * HD
        ].astype(f32)
    small_all[row, me] = small_ref[...]
    qkv_copy.wait()

    low = head_lanes((depth, PAIR))
    for p in range(width // HD // ctx // 2):
        for t in range(3):
            lanes = slice((3 * p + t) * PAIR, (3 * p + t + 1) * PAIR)
            for c in range(0, ctx, 2):
                at = t * width + (2 * p * ctx + c) * HD
                a = qkv_ref[:, at : at + PAIR].astype(f32)
                at = at + ctx * HD
                b = qkv_ref[:, at : at + PAIR].astype(f32)
                blocks[c, :, lanes] = jnp.where(low, a, pltpu.roll(b, HD, 1)).astype(bf16)
                blocks[c + 1, :, lanes] = jnp.where(low, pltpu.roll(a, HD, 1), b).astype(bf16)
    greet_all(place, dp, ctx, signal=False)

    def weight_rows(row, col):
        return weight_ref.at[pl.ds(pl.multiple_of((row * ctx + col) * depth, depth), depth), :]

    def out_shard(row):
        return out_all.at[pl.ds(pl.multiple_of(row * rows_out, rows_out), rows_out), :]

    def block(ref, col):
        return ref.at[pl.ds(pl.multiple_of(col * length, length), length), :]

    part_cols = weight_ref.shape[1] // PARTS

    def weight_part(i, row):
        return weight_ref.at[
            pl.ds(pl.multiple_of(row * tall, tall), tall), pl.ds(i * part_cols, part_cols)
        ]

    local = [
        pltpu.make_async_copy(blocks.at[me], weight_rows(row, me), local_sem.at[0]),
        pltpu.make_async_copy(out_weight_ref, out_shard(row), local_sem.at[1]),
        pltpu.make_async_copy(rows_ref, block(rows_all, me), local_sem.at[2]),
        pltpu.make_async_copy(cot_ref, block(cot_all, me), local_sem.at[3]),
    ]
    swaps = [
        remote(small_ref, small_all.at[row, me], swap_sem.at[0, k], swap_sem.at[1, k], place.across(k))
        for k in range(1, ctx)
    ] + [
        remote(
            blocks.at[place.other(k)], weight_rows(row, me), swap_sem.at[2, k], swap_sem.at[3, k], place.across(k)
        )
        for k in range(1, ctx)
    ]
    for copy in swaps:
        copy.start()
    for copy in local:
        copy.start()

    def gate_shard(row):
        tall = gate_hbm.shape[0]
        return gate_all.at[pl.ds(pl.multiple_of(row * tall, tall), tall), :]

    def up_shard(row):
        tall = up_hbm.shape[0]
        return up_all.at[pl.ds(pl.multiple_of(row * tall, tall), tall), :]

    gate_line, up_line = LineGather(place, gate_shard, line_gate), LineGather(place, up_shard, line_up)
    late = [
        pltpu.make_async_copy(gate_hbm, gate_shard(row), late_sem.at[1]),
        pltpu.make_async_copy(up_hbm, up_shard(row), late_sem.at[2]),
    ]
    for copy in late:
        copy.start()
    rows_gather = CtxGather(place, rows_ref, rows_all, length, rows_sem)
    cot_gather = CtxGather(place, cot_ref, cot_all, length, cot_sem)
    out_line = LineGather(place, out_shard, line_out)
    lines = [
        LineGather(place, functools.partial(weight_part, i), line_joined.at[i]) for i in range(PARTS)
    ] + [out_line]
    local[1].wait()
    out_line.send(1)
    rows_gather.first()
    for k in range(1, ctx):
        remote(
            small_ref, small_all.at[row, place.other(k)], swap_sem.at[0, k], swap_sem.at[1, k], place.across(k)
        ).wait_recv()
    small_sends = [
        remote(
            small_all.at[row], small_all.at[row], small_sem.at[0, k], small_sem.at[1, k], ((row + k) % dp, me)
        )
        for k in range(1, dp)
    ]
    for copy in small_sends:
        copy.start()
    local[0].wait()
    for k in range(1, ctx):
        part = weight_rows(row, place.other(k))
        remote(part, part, swap_sem.at[2, k], swap_sem.at[3, k], place.across(k)).wait_recv()
    for line in lines[:PARTS]:
        line.send(1)

    for k in range(1, dp):
        part = small_all.at[(row + dp - k) % dp]
        remote(part, part, small_sem.at[0, k], small_sem.at[1, k], place.twin).wait_recv()
    low = head_lanes((1, PAIR))
    for i in range(dp * ctx // 2):
        lanes = slice(i * PAIR, (i + 1) * PAIR)
        a = small_all[2 * i // ctx, 2 * i % ctx]
        b = small_all[(2 * i + 1) // ctx, (2 * i + 1) % ctx]
        for r in range(2):
            ar, br = a[r : r + 1, :], b[r : r + 1, :]
            params_ref[2 * r : 2 * r + 1, lanes] = jnp.where(low, ar, pltpu.roll(br, HD, 1))
            params_ref[2 * r + 1 : 2 * r + 2, lanes] = jnp.where(low, pltpu.roll(ar, HD, 1), br)

    def normalize(col):
        step = 64

        @pl.loop(0, length // step)
        def _(i):
            rows = pl.ds(pl.multiple_of(col * length + i * step, step), step)
            scaled, _ = norm_stats(rows_all[rows, :].astype(f32))
            normed_ref[rows, :] = (scaled * params_ref[0:1, :] + params_ref[1:2, :]).astype(bf16)

        normed_copy(col).start()

    def normed_copy(col):
        return pltpu.make_async_copy(block(normed_ref, col), block(normed_hbm, col), normed_sem.at[col])

    def weight_copy(i, line):
        part = (
            pl.ds(pl.multiple_of(line * (2 * tall), 2 * tall), 2 * tall),
            pl.ds(i * part_cols, part_cols),
        )
        return pltpu.make_async_copy(weight_ref.at[part], weight_hbm.at[part], weight_sem.at[i, line])

    def multiply(i, line):
        weight_copy(i, line).start()
        at = pl.multiple_of(line * (2 * tall), 2 * tall)
        cols = slice(i * part_cols, (i + 1) * part_cols)

        @pl.loop(0, ctx)
        def _(b):
            rows = pl.ds(pl.multiple_of(b * length, length), length)
            joined_ref[rows, cols] += dot(
                normed_ref[rows, pl.ds(at, 2 * tall)], weight_ref[pl.ds(at, 2 * tall), cols]
            )

    def forward(hop):
        for line in lines:
            line.receive(hop)
            if hop < place.lines - 1:
                line.send(hop + 1)

    def absorb(hop):
        for i in range(PARTS):
            lines[i].settle(hop, functools.partial(multiply, i))

    joined_ref[...] = jnp.zeros_like(joined_ref)
    local[2].wait()
    normalize(me)
    rows_gather.second()
    cot_gather.first()
    for hop in range(1, place.lines):
        forward(hop)
        if hop == 1:
            for col in (place.other(1), place.other(2)):
                normalize(col)
            rows_gather.finish()
            normalize(place.other(3))
        if hop == min(2, place.lines - 1):
            cot_gather.second()
        absorb(hop - 1)
    late[0].wait()
    gate_line.send(1)
    absorb(place.lines - 1)
    late[1].wait()

    low = head_lanes((1, PAIR))
    pairs = joined_ref.shape[1] // (3 * PAIR)
    per_device = bias.shape[1] // HD
    for p in range(pairs):
        for t in range(3):
            chosen = [None, None]
            for c in range(ctx):
                for half in range(2):
                    slot = t * (width // HD) + (2 * p + half) * ctx + c
                    owner, at = slot // per_device, slot % per_device
                    piece = small_all[owner // ctx, owner % ctx, 2 + at // 2 : 3 + at // 2, :]
                    if at % 2 != half:
                        piece = pltpu.roll(piece, HD, 1)
                    chosen[half] = piece if c == 0 else jnp.where(me == c, piece, chosen[half])
            lanes = slice((3 * p + t) * PAIR, (3 * p + t + 1) * PAIR)
            bias_ref[:, lanes] = jnp.where(low, chosen[0], chosen[1])

    def heads_copies():
        return [
            pltpu.make_async_copy(attended_ref, attended_hbm, late_sem.at[3]),
            pltpu.make_async_copy(heads_ref, heads_hbm, late_sem.at[4]),
            pltpu.make_async_copy(lse_ref, lse_hbm, late_sem.at[5]),
            pltpu.make_async_copy(out_all, out_hbm, late_sem.at[6]),
        ]

    def attend_pairs(first, last):
        @pl.loop(first, last)
        def _(p):
            wide = pl.ds(pl.multiple_of(p * (3 * PAIR), 3 * PAIR), 3 * PAIR)
            thin = pl.ds(pl.multiple_of(p * PAIR, PAIR), PAIR)
            attend_kernel(
                step, joined_ref.at[:, wide], bias_ref.at[:, wide], table_ref, start_ref,
                attended_ref.at[:, thin], heads_ref.at[:, wide], lse_ref.at[:, thin],
            )

    def pass_on(line, hop):
        line.receive(hop)
        if hop < place.lines - 1:
            line.send(hop + 1)

    table_copy.wait()
    attend_pairs(0, pairs // 2)
    if place.lines > 1:
        pass_on(gate_line, 1)
    up_line.send(1)
    attend_pairs(pairs // 2, pairs)
    for hop in range(place.lines):
        out_line.settle(hop)
    for line in lines:
        line.finish()
    cot_gather.finish()
    for copy in heads_copies():
        copy.start()

    reduce = CtxReduce(
        place, lambda col: dot(rows_of(attended_ref, col, length), out_all[...]), total, sent, got, reduce_sem
    )
    spread = CtxSpread(place, made, wide_ref, spread_sem)

    def resid_copy(j):
        rows = reduce.chunk(j)
        return pltpu.make_async_copy(resid_ref.at[rows, :], resid_hbm.at[rows, :], resid_sem.at[j])

    reduce.start()
    reduce.relay()
    if place.lines > 2:
        pass_on(gate_line, 2)
    for j in range(CHUNKS):
        rows = reduce.chunk(j)
        at = pl.multiple_of(me * length + j * reduce.size, reduce.size)
        resid = rows_all[pl.ds(at, reduce.size), :].astype(f32) + reduce.sum(j)
        resid_ref[rows, :] = resid
        resid_copy(j).start()
        scaled, _ = norm_stats(resid)
        made[rows, :] = (scaled * params_ref[2:3, :] + params_ref[3:4, :]).astype(bf16)
        spread.send(j)
        if j:
            spread.relay(j - 1)
        if j == 1 and place.lines > 1:
            pass_on(up_line, 1)
    spread.relay(CHUNKS - 1)
    for hop in range(3, place.lines):
        pass_on(gate_line, hop)
    for hop in range(2, place.lines):
        pass_on(up_line, hop)
    spread.finish()
    for line in (gate_line, up_line):
        for hop in range(place.lines):
            line.settle(hop)
        line.finish()
    reduce.finish()
    for copy in swaps + small_sends:
        copy.wait_send()
    local[3].wait()
    for col in range(ctx):
        normed_copy(col).wait()
    for line in range(place.lines):
        for i in range(PARTS):
            weight_copy(i, line).wait()
    for j in range(CHUNKS):
        resid_copy(j).wait()
    for copy in heads_copies():
        copy.wait()


def forward(dp, ctx, vectors, start, table, qkv_weight, out_weight, rows, cot, gate_weight, up_weight):
    depth, width = qkv_weight.shape[0], rows.shape[1]
    length = rows.shape[0]
    full_len = ctx * length
    near = 3 * width // ctx
    thin = near // 3
    hidden = gate_weight.shape[1]
    vmem = pl.BlockSpec(memory_space=pltpu.VMEM)
    reduce_scratch = CtxReduce.scratch(length, width)
    return pl.pallas_call(
        functools.partial(forward_kernel, dp, ctx, attend_step(full_len)),
        in_specs=[vmem] * (len(vectors) + 1) + [HBM] * 7,
        out_specs=[vmem] + [HBM] * 11,
        out_shape=[
            jax.ShapeDtypeStruct((4, width), f32),
            jax.ShapeDtypeStruct((dp * ctx * depth, near), bf16),
            jax.ShapeDtypeStruct((dp * out_weight.shape[0], width), bf16),
            jax.ShapeDtypeStruct((full_len, width), bf16),
            jax.ShapeDtypeStruct((full_len, width), bf16),
            jax.ShapeDtypeStruct((full_len, thin), bf16),
            jax.ShapeDtypeStruct((full_len, near), bf16),
            jax.ShapeDtypeStruct((full_len, thin), f32),
            jax.ShapeDtypeStruct((length, width), f32),
            jax.ShapeDtypeStruct((full_len, width), bf16),
            jax.ShapeDtypeStruct((dp * gate_weight.shape[0], hidden), bf16),
            jax.ShapeDtypeStruct((dp * up_weight.shape[0], hidden), bf16),
        ],
        scratch_shapes=[
            pltpu.VMEM((dp, ctx, 8, PAIR), f32),
            pltpu.VMEM(table.shape, f32),
            pltpu.VMEM((8, PAIR), f32),
            pltpu.VMEM((depth, 3 * width), bf16),
            pltpu.VMEM((ctx, depth, near), bf16),
            pltpu.VMEM((full_len, width), bf16),
            pltpu.VMEM((dp * ctx * depth, near), bf16),
            pltpu.VMEM((full_len, width), bf16),
            pltpu.VMEM((full_len, near), f32),
            pltpu.VMEM((1, near), f32),
            pltpu.VMEM((dp * out_weight.shape[0], width), bf16),
            pltpu.VMEM((full_len, thin), bf16),
            pltpu.VMEM((full_len, near), bf16),
            pltpu.VMEM((full_len, thin), f32),
        ]
        + reduce_scratch[:3]
        + [
            pltpu.VMEM((length, width), bf16),
            pltpu.VMEM((length, width), f32),
            pltpu.SemaphoreType.DMA((ctx,)),
            pltpu.SemaphoreType.DMA((PARTS, dp // 2)),
            pltpu.SemaphoreType.DMA((5,)),
            pltpu.SemaphoreType.DMA((4, ctx)),
            pltpu.SemaphoreType.DMA((2, dp)),
            pltpu.SemaphoreType.DMA((PARTS, 6, dp)),
            LineGather.scratch(dp),
            LineGather.scratch(dp),
            LineGather.scratch(dp),
            CtxGather.scratch(),
            CtxGather.scratch(),
            pltpu.SemaphoreType.DMA((7,)),
            reduce_scratch[3],
            CtxSpread.scratch(),
            pltpu.SemaphoreType.DMA((CHUNKS,)),
        ],
        compiler_params=pltpu.CompilerParams(
            collective_id=0, has_side_effects=True, vmem_limit_bytes=62 << 20
        ),
        cost_estimate=pl.CostEstimate(
            flops=2 * full_len * width * near, transcendentals=0, bytes_accessed=400 << 20
        ),
    )(*vectors, start, table, qkv_weight, out_weight, rows, cot, gate_weight, up_weight)


def rotary_table(full_len):
    half = ROT // 2
    inverse = 10000.0 ** (-2.0 * np.arange(half) / ROT)
    angles = np.arange(full_len)[:, None] * inverse[None, :]
    table = np.zeros((3, full_len, HD), np.float32)
    table[0, :, :half] = table[0, :, half:ROT] = np.cos(angles)
    table[0, :, ROT:] = 1.0
    table[1, :, :half] = -np.sin(angles)
    table[2, :, half:ROT] = np.sin(angles)
    return jnp.asarray(np.concatenate([table, table], axis=2))


def shards(
    dp,
    ctx,
    inputs,
    segments,
    ln1_gain,
    ln1_bias,
    qkv_weight,
    qkv_bias,
    out_weight,
    ln2_gain,
    ln2_bias,
    gate_weight,
    up_weight,
    down_weight,
    cotangent,
):
    local_len, width = inputs.shape[1], inputs.shape[2]
    full_len = segments.shape[1]
    heads = width // HD
    near = heads // ctx
    pairs = near // 2
    me = lax.axis_index("ctx")
    own = me * local_len

    segment = segments[0]
    start = jnp.sum((segment[None, :] < segment[:, None]).astype(jnp.int32), axis=1)
    start = jnp.broadcast_to(start[:, None], (full_len, 128))
    table = rotary_table(full_len)
    part = ln1_gain.shape[0]
    vectors = [v[None, :] for v in (ln1_gain, ln1_bias, ln2_gain, ln2_bias, qkv_bias)]
    rows_here = qkv_weight.shape[0]
    rows, grad_rows = inputs[0], cotangent[0]
    fused = ctx == 4 and dp % 2 == 0 and part == HD
    if fused:
        (
            params, joined_weight, out_full, normed_one, grad_wide, attended, qkv, lse, resid, normed_wide,
            gate_full, up_full,
        ) = forward(
            dp, ctx, vectors, start, table, qkv_weight, out_weight, rows, grad_rows, gate_weight, up_weight
        )
        gain_one, _, gain_two, _ = params
        down_weight, _ = lax.optimization_barrier((down_weight, normed_wide))
    else:
        small = jnp.concatenate(vectors, axis=1).astype(f32)
        small = lax.all_gather(small, ("dp", "ctx"), axis=0, tiled=True)
        blocks = qkv_weight.reshape(rows_here, 3, pairs, 2, ctx, HD).transpose(4, 0, 2, 1, 3, 5)
        blocks = exchange_ctx(blocks.reshape(ctx, rows_here, near * 3 * HD), ctx)
        joined_weight = lax.all_gather(
            blocks.reshape(ctx * rows_here, near * 3 * HD), "dp", axis=0, tiled=True
        )
        out_full = lax.all_gather(out_weight, ("dp", "ctx"), axis=0, tiled=True)
        out_full = out_full.reshape(near, ctx, HD, width)
        out_full = lax.dynamic_index_in_dim(out_full, me, 1, keepdims=False)
        out_full = out_full.reshape(near * HD, width)
        gain_one, shift_one, gain_two, shift_two = [
            small[:, i * part : (i + 1) * part].reshape(width) for i in range(4)
        ]
        scaled_wide, _ = norm_stats(gather_ctx(rows, ctx).astype(f32))
        normed_one = (scaled_wide * gain_one + shift_one).astype(bf16)
        grad_wide = gather_ctx(grad_rows, ctx)
        bias = small[:, 4 * part :].reshape(3, pairs, 2, ctx, HD)
        bias = lax.dynamic_index_in_dim(bias, me, 3, keepdims=False)
        bias = bias.transpose(1, 0, 2, 3).reshape(1, near * 3 * HD)
        attended, qkv, lse = attend(dot(normed_one, joined_weight), bias, table, start)
        resid = rows.astype(f32) + scatter_ctx(dot(attended, out_full), ctx)
        scaled_two, inv_two = norm_stats(resid)
        normed_wide = gather_ctx((scaled_two * gain_two + shift_two).astype(bf16), ctx)
        gate_full = lax.all_gather(gate_weight, "dp", axis=0, tiled=True)
        up_full = lax.all_gather(up_weight, "dp", axis=0, tiled=True)
    down_full = lax.all_gather(down_weight, "dp", axis=1, tiled=True)

    gate = dot(normed_wide, gate_full)
    upward = dot(normed_wide, up_full)
    sigma = jax.nn.sigmoid(gate)
    swish = gate * sigma
    inner = (swish * upward).astype(bf16)
    d_down = dot_tn(inner, grad_wide).astype(bf16)
    grad_wide, d_down = lax.optimization_barrier((grad_wide, d_down))
    d_down = lax.psum_scatter(d_down, "dp", scatter_dimension=1, tiled=True).astype(f32)
    d_inner = dot_nt(grad_wide, down_full)
    d_gate = (d_inner * upward * sigma * (1.0 + gate * (1.0 - sigma))).astype(bf16)
    d_upward = (d_inner * swish).astype(bf16)
    d_gate_weight = dot_tn(normed_wide, d_gate).astype(bf16)
    if fused:
        d_resid, sums_two, d_proj, branch, d_up_weight, d_gate_weight = mix_back(
            dp, ctx, d_gate, d_upward, gate_full, up_full, inner, down_full, normed_wide, d_gate_weight, resid,
            grad_rows, gain_two,
        )
    else:
        d_gate_weight = lax.psum_scatter(d_gate_weight, "dp", scatter_dimension=0, tiled=True).astype(f32)
        branch = dot(inner, down_full)
        d_up_weight = dot_tn(normed_wide, d_upward).astype(bf16)
        d_normed_two = scatter_ctx(dot_nt(d_gate, gate_full) + dot_nt(d_upward, up_full), ctx)
        grad, d_gain_two, d_shift_two = norm_backward(d_normed_two, scaled_two, inv_two, gain_two)
        d_resid = grad_rows.astype(f32) + grad
        d_proj = gather_ctx(d_resid.astype(bf16), ctx)
    d_up_weight = lax.psum_scatter(d_up_weight, "dp", scatter_dimension=0, tiled=True).astype(f32)

    d_attended = dot_nt(d_proj, out_full).astype(bf16)
    d_out_weight = dot_tn(attended, d_proj).astype(bf16)
    d_attended, d_down = lax.optimization_barrier((d_attended, d_down))
    d_joined, d_bias = attend_back(qkv, d_attended, lse, table, start)
    d_joined_weight = dot_tn(normed_one, d_joined).astype(bf16)
    d_bias = d_bias.reshape(pairs, 3, 2, HD).transpose(1, 0, 2, 3)
    if fused:
        d_bias = jnp.pad(d_bias.reshape(dp, -1), ((0, 0), (0, width // dp - near * 3 * HD // dp)))
        grad_input, d_joined_weight, d_out_weight, output, vectors, d_bias = closing(
            dp, ctx, d_joined, joined_weight, d_joined_weight, d_out_weight, branch, rows, d_resid, resid,
            gain_one, sums_two, d_bias,
        )
        d_gain_one, d_shift_one, d_gain_two, d_shift_two = vectors
        d_bias = d_bias[0]
    else:
        output = (resid + scatter_ctx(branch, ctx)).astype(bf16)
        at_me = lax.broadcasted_iota(jnp.int32, (1, ctx, 1, 1), 1) == me
        d_out_weight = jnp.where(at_me, d_out_weight.reshape(near, 1, HD, width), jnp.zeros((), bf16))
        d_out_weight = lax.psum_scatter(
            d_out_weight.reshape(width, width), ("dp", "ctx"), scatter_dimension=0, tiled=True
        ).astype(f32)
        d_normed_one = scatter_ctx(dot_nt(d_joined, joined_weight), ctx)
        scaled_one, inv_one = norm_stats(rows.astype(f32))
        grad, d_gain_one, d_shift_one = norm_backward(d_normed_one, scaled_one, inv_one, gain_one)
        grad_input = d_resid + grad
        d_joined_weight = lax.psum_scatter(d_joined_weight, "dp", scatter_dimension=0, tiled=True)
        blocks = exchange_ctx(d_joined_weight.reshape(ctx, rows_here, near * 3 * HD), ctx)
        blocks = blocks.reshape(ctx, rows_here, pairs, 3, 2, HD).transpose(1, 3, 2, 4, 0, 5)
        d_joined_weight = blocks.reshape(rows_here, 3 * width).astype(f32)
        at_me = (lax.broadcasted_iota(jnp.int32, (1, 1, 1, ctx, 1), 3) == me).astype(f32)
        d_bias = (d_bias[:, :, :, None, :] * at_me).reshape(dp * ctx, -1)
        small = jnp.concatenate(
            [t.reshape(dp * ctx, part) for t in (d_gain_one, d_shift_one, d_gain_two, d_shift_two)]
            + [d_bias],
            axis=1,
        )
        small = lax.psum_scatter(small, ("dp", "ctx"), scatter_dimension=0, tiled=True)[0]
        d_gain_one, d_shift_one, d_gain_two, d_shift_two = [
            small[i * part : (i + 1) * part] for i in range(4)
        ]
        d_bias = small[4 * part :]
    return (
        output[None],
        grad_input[None],
        d_gain_one,
        d_shift_one,
        d_joined_weight,
        d_bias,
        d_out_weight,
        d_gain_two,
        d_shift_two,
        d_gate_weight,
        d_up_weight,
        d_down,
    )


def solution(mesh):
    every = ("dp", "ctx")
    return jax.shard_map(
        functools.partial(shards, mesh.shape["dp"], mesh.shape["ctx"]),
        mesh=mesh,
        in_specs=(
            P("dp", "ctx", None),
            P("dp", None),
            P(every),
            P(every),
            P(every, None),
            P(every),
            P(every, None),
            P(every),
            P(every),
            P("dp", "ctx"),
            P("dp", "ctx"),
            P("ctx", "dp"),
            P("dp", "ctx", None),
        ),
        out_specs=(
            P("dp", "ctx", None),
            P("dp", "ctx", None),
            P(every),
            P(every),
            P(every, None),
            P(every),
            P(every, None),
            P(every),
            P(every),
            P("dp", "ctx"),
            P("dp", "ctx"),
            P("ctx", "dp"),
        ),
        check_vma=False,
    )
```

```python
import functools
import math

import jax
import jax.numpy as jnp
import numpy as np
from jax import lax
from jax.experimental import pallas as pl
from jax.experimental.pallas import tpu as pltpu
from jax.sharding import PartitionSpec as P

HD = 64
ROT = 16
DOC_MAX = 512
PAIR = 2 * HD

norm_eps = 1e-05
masked_value = -1e30
f32 = jnp.float32
bf16 = jnp.bfloat16


def dot(a, b):
    return jnp.dot(a, b, preferred_element_type=f32)


def dot_nt(a, b):
    return lax.dot_general(a, b, (((1,), (1,)), ((), ())), preferred_element_type=f32)


def dot_tn(a, b):
    return lax.dot_general(a, b, (((0,), (0,)), ((), ())), preferred_element_type=f32)


def norm_stats(rows):
    row_mean = jnp.mean(rows, axis=-1, keepdims=True)
    centered = rows - row_mean
    variance = jnp.mean(centered * centered, axis=-1, keepdims=True)
    inv_std = lax.rsqrt(variance + norm_eps)
    return centered * inv_std, inv_std


def norm_backward(grad_normed, scaled, inv_std, gain):
    grad_gain = jnp.sum(grad_normed * scaled, axis=0)
    grad_shift = jnp.sum(grad_normed, axis=0)
    inner_grad = grad_normed * gain
    grad_rows = inv_std * (
        inner_grad
        - jnp.mean(inner_grad, axis=-1, keepdims=True)
        - scaled * jnp.mean(inner_grad * scaled, axis=-1, keepdims=True)
    )
    return grad_rows, grad_gain, grad_shift


def partner(n, k):
    return [(c, c ^ k) for c in range(n)]


def hop(x, n, k):
    return lax.ppermute(x, "ctx", partner(n, k))


def gather_relative(block, n):
    if n != 4:
        return [block] + [hop(block, n, k) for k in range(1, n)]
    half = block.shape[0] // 2
    one = hop(block, n, 1)
    two = hop(block, n, 2)
    low = hop(one[:half], n, 2)
    high = hop(two[half:], n, 1)
    return [block, one, two, jnp.concatenate([low, high], axis=0)]


def gather_ctx(block, n):
    me = lax.axis_index("ctx")
    size = block.shape[0]
    parts = gather_relative(block, n)
    full = jnp.zeros((n * size,) + block.shape[1:], block.dtype)
    for k, part in enumerate(parts):
        full = lax.dynamic_update_slice_in_dim(full, part, (me ^ k) * size, 0)
    return full


def scatter_ctx(partial, n):
    me = lax.axis_index("ctx")
    size = partial.shape[0] // n

    def block(k):
        return lax.dynamic_slice_in_dim(partial, (me ^ k) * size, size, 0)

    if n != 4:
        total = block(0).astype(f32)
        for k in range(1, n):
            total = total + hop(block(k).astype(bf16), n, k).astype(f32)
        return total
    half = size // 2
    far = block(3).astype(bf16)
    low = hop(far[:half], n, 1).astype(f32)
    high = hop(far[half:], n, 2).astype(f32)
    one = block(1).astype(f32)
    two = block(2).astype(f32)
    to_one = jnp.concatenate([one[:half], one[half:] + high], axis=0).astype(bf16)
    to_two = jnp.concatenate([two[:half] + low, two[half:]], axis=0).astype(bf16)
    return block(0).astype(f32) + hop(to_one, n, 1).astype(f32) + hop(to_two, n, 2).astype(f32)


def exchange_ctx(blocks, n):
    me = lax.axis_index("ctx")
    got = lax.dynamic_update_slice_in_dim(
        jnp.zeros_like(blocks), lax.dynamic_slice_in_dim(blocks, me, 1, 0), me, 0
    )
    for k in range(1, n):
        sent = lax.dynamic_slice_in_dim(blocks, me ^ k, 1, 0)
        got = lax.dynamic_update_slice_in_dim(got, hop(sent, n, k), me ^ k, 0)
    return got


MESH = pl.DeviceIdType.MESH
HBM = pl.BlockSpec(memory_space=pltpu.HBM)


class Place:
    def __init__(self, dp):
        self.row = lax.axis_index("dp")
        self.col = lax.axis_index("ctx")
        self.lines = dp // 2
        self.line = self.row // 2
        self.core = self.row % 2
        self.twin = (self.row + 1 - 2 * self.core, self.col)

    def other(self, k):
        col, bit = self.col, 1
        while bit <= k:
            if k & bit:
                col = col + bit * (1 - 2 * ((self.col // bit) % 2))
            bit *= 2
        return col

    def across(self, k):
        return (self.row, self.other(k))

    def above(self):
        return (self.row + 2, self.col)

    def below(self):
        return (self.row - 2, self.col)


def greet(place, ctx):
    barrier = pltpu.get_barrier_semaphore()
    for k in range(1, ctx):
        pl.semaphore_signal(barrier, 1, device_id=place.across(k), device_id_type=MESH)
    pl.semaphore_wait(barrier, ctx - 1)


def remote(src, dst, send, recv, device):
    return pltpu.make_async_remote_copy(
        src_ref=src, dst_ref=dst, send_sem=send, recv_sem=recv, device_id=device, device_id_type=MESH
    )


class LineGather:
    def __init__(self, place, shard, sems):
        self.place, self.shard, self.sems = place, shard, sems

    def row(self, line):
        return line * 2 + self.place.core

    def up(self, hop):
        part = self.shard(self.row(self.place.line - hop + 1))
        return remote(part, part, self.sems.at[0, hop], self.sems.at[1, hop], self.place.above())

    def down(self, hop):
        part = self.shard(self.row(self.place.line + hop - 1))
        return remote(part, part, self.sems.at[2, hop], self.sems.at[3, hop], self.place.below())

    def over(self, at, row):
        part = self.shard(row)
        return remote(part, part, self.sems.at[4, at], self.sems.at[5, at], self.place.twin)

    def sends_up(self, hop):
        return (self.place.line - hop + 1 >= 0) & (self.place.line < self.place.lines - 1)

    def sends_down(self, hop):
        return (self.place.line + hop - 1 < self.place.lines) & (self.place.line > 0)

    def send(self, hop):
        place = self.place
        pl.when(self.sends_up(hop))(lambda: self.up(hop).start())
        pl.when(self.sends_down(hop))(lambda: self.down(hop).start())
        if hop == 1:
            self.over(0, place.row).start()

    def receive(self, hop):
        place = self.place

        @pl.when(place.line - hop >= 0)
        def _():
            part = self.shard(self.row(place.line - hop))
            remote(part, part, self.sems.at[0, hop], self.sems.at[1, hop], place.twin).wait_recv()
            self.over(hop, self.row(place.line - hop)).start()

        @pl.when(place.line + hop < place.lines)
        def _():
            part = self.shard(self.row(place.line + hop))
            remote(part, part, self.sems.at[2, hop], self.sems.at[3, hop], place.twin).wait_recv()
            self.over(place.lines - 1 + hop, self.row(place.line + hop)).start()

    def came_over(self, at, row):
        part = self.shard(row)
        remote(part, part, self.sems.at[4, at], self.sems.at[5, at], self.place.twin).wait_recv()

    def settle(self, hop, use=None):
        place = self.place
        other = 1 - 2 * place.core
        if hop == 0:
            self.came_over(0, place.row + other)
            if use:
                use(place.line)
            return
        for at, line, there in (
            (hop, place.line - hop, place.line - hop >= 0),
            (place.lines - 1 + hop, place.line + hop, place.line + hop < place.lines),
        ):

            @pl.when(there)
            def _():
                self.came_over(at, self.row(line) + other)
                if use:
                    use(line)

    def finish(self):
        place = self.place
        self.over(0, place.row).wait_send()
        for hop in range(1, place.lines):
            pl.when(self.sends_up(hop))(lambda: self.up(hop).wait_send())
            pl.when(self.sends_down(hop))(lambda: self.down(hop).wait_send())
            for at, line, there in (
                (hop, place.line - hop, place.line - hop >= 0),
                (place.lines - 1 + hop, place.line + hop, place.line + hop < place.lines),
            ):
                pl.when(there)(lambda: self.over(at, self.row(line)).wait_send())

    @staticmethod
    def scratch(dp):
        return pltpu.SemaphoreType.DMA((6, dp))


class CtxGather:
    def __init__(self, place, block, full, size, sems):
        self.place, self.block, self.full, self.size, self.sems = place, block, full, size, sems

    def rows(self, col, start=0, size=None):
        size = self.size if size is None else size
        return self.full.at[pl.ds(pl.multiple_of(col * self.size + start, size), size), :]

    def copies(self):
        place, half = self.place, self.size // 2
        me = place.col
        return [
            remote(self.block, self.rows(me), self.sems.at[0, 0], self.sems.at[1, 0], place.across(1)),
            remote(self.block, self.rows(me), self.sems.at[0, 1], self.sems.at[1, 1], place.across(2)),
            remote(
                self.rows(place.other(1), 0, half), self.rows(place.other(1), 0, half),
                self.sems.at[0, 2], self.sems.at[1, 2], place.across(2),
            ),
            remote(
                self.rows(place.other(2), half, half), self.rows(place.other(2), half, half),
                self.sems.at[0, 3], self.sems.at[1, 3], place.across(1),
            ),
        ]

    def arrivals(self):
        place, half = self.place, self.size // 2
        me = place.col
        parts = [self.rows(place.other(1)), self.rows(place.other(2)), self.rows(place.other(3), 0, half), self.rows(place.other(3), half, half)]
        return [
            remote(part, part, self.sems.at[0, i], self.sems.at[1, i], place.across(1))
            for i, part in enumerate(parts)
        ]

    def first(self):
        copies = self.copies()
        copies[0].start()
        copies[1].start()

    def second(self):
        copies, arrivals = self.copies(), self.arrivals()
        arrivals[0].wait_recv()
        copies[2].start()
        arrivals[1].wait_recv()
        copies[3].start()

    def finish(self):
        copies, arrivals = self.copies(), self.arrivals()
        arrivals[2].wait_recv()
        arrivals[3].wait_recv()
        for copy in copies:
            copy.wait_send()

    @staticmethod
    def scratch():
        return pltpu.SemaphoreType.DMA((2, 4))


def greet_all(place, dp, ctx, signal=True, wait=True):
    barrier = pltpu.get_barrier_semaphore()
    if signal:
        for k in range(1, ctx):
            pl.semaphore_signal(barrier, 1, device_id=place.across(k), device_id_type=MESH)
        for k in range(1, dp):
            pl.semaphore_signal(barrier, 1, device_id=((place.row + k) % dp, place.col), device_id_type=MESH)
    if wait:
        pl.semaphore_wait(barrier, ctx + dp - 2)


CHUNKS = 4
PARTS = 2


class CtxReduce:
    def __init__(self, place, block, total, sent, got, sems):
        self.place, self.block, self.total = place, block, total
        self.sent, self.got, self.sems = sent, got, sems
        self.size = total.shape[1] // CHUNKS

    def chunk(self, j):
        return pl.ds(j * self.size, self.size)

    def copy(self, kind, j):
        way = kind if kind else 1 + j % 2
        return remote(
            self.sent.at[kind, self.chunk(j)], self.got.at[kind, self.chunk(j)],
            self.sems.at[0, kind, j], self.sems.at[1, kind, j], self.place.across(way),
        )

    def start(self):
        self.start_far()
        self.start_near()

    def start_far(self):
        self.sent[0] = self.block(self.place.other(3)).astype(bf16)
        for j in range(CHUNKS):
            self.copy(0, j).start()

    def start_near(self):
        place = self.place
        for kind in (1, 2):
            self.total[kind - 1] = self.block(place.other(kind))
            for j in range(CHUNKS):
                if kind == 1 + j % 2:
                    self.sent[kind, self.chunk(j)] = self.total[kind - 1, self.chunk(j)].astype(bf16)
                    self.copy(kind, j).start()

    def relay(self):
        for j in range(CHUNKS):
            kind = 2 - j % 2
            self.copy(0, j).wait_recv()
            share = self.total[kind - 1, self.chunk(j)] + self.got[0, self.chunk(j)].astype(f32)
            self.sent[kind, self.chunk(j)] = share.astype(bf16)
            self.copy(kind, j).start()
        self.total[0] = self.block(self.place.col)

    def sum(self, j):
        for kind in (1, 2):
            self.copy(kind, j).wait_recv()
        rows = self.chunk(j)
        return self.total[0, rows] + self.got[1, rows].astype(f32) + self.got[2, rows].astype(f32)

    def finish(self):
        for kind in range(3):
            for j in range(CHUNKS):
                self.copy(kind, j).wait_send()

    @staticmethod
    def scratch(size, width):
        return [
            pltpu.VMEM((2, size, width), f32),
            pltpu.VMEM((3, size, width), bf16),
            pltpu.VMEM((3, size, width), bf16),
            pltpu.SemaphoreType.DMA((2, 3, CHUNKS)),
        ]


class CtxSpread:
    def __init__(self, place, made, full, sems):
        self.place, self.made, self.full, self.sems = place, made, full, sems
        self.size = made.shape[0] // CHUNKS

    def rows(self, col, j):
        at = (col * CHUNKS + j) * self.size
        return self.full.at[pl.ds(pl.multiple_of(at, self.size), self.size), :]

    def copy(self, kind, j):
        place = self.place
        if kind < 2:
            part, there = self.made.at[pl.ds(j * self.size, self.size), :], self.rows(place.col, j)
            way = 1 + kind
        else:
            way = 2 - j % 2
            part = there = self.rows(place.other(3 - way), j)
        return remote(part, there, self.sems.at[0, kind, j], self.sems.at[1, kind, j], place.across(way))

    def arrived(self, kind, j):
        part = self.rows(self.place.other(kind + 1), j)
        remote(
            part, part, self.sems.at[0, kind, j], self.sems.at[1, kind, j], self.place.across(1)
        ).wait_recv()

    def local(self, j):
        part = self.made.at[pl.ds(j * self.size, self.size), :]
        return pltpu.make_async_copy(part, self.rows(self.place.col, j), self.sems.at[0, 3, j])

    def send(self, j):
        self.copy(0, j).start()
        self.copy(1, j).start()
        self.local(j).start()

    def relay(self, j):
        way = 2 - j % 2
        self.arrived(2 - way, j)
        self.copy(2, j).start()

    def finish(self):
        for j in range(CHUNKS):
            way = 2 - j % 2
            self.arrived(way - 1, j)
            self.arrived(2, j)
            self.local(j).wait()
            for kind in range(3):
                self.copy(kind, j).wait_send()

    @staticmethod
    def scratch():
        return pltpu.SemaphoreType.DMA((2, 4, CHUNKS))


def rows_of(ref, col, size):
    return ref[pl.ds(pl.multiple_of(col * size, size), size), :]


class LineReduce:
    def __init__(self, place, parts, own, pair, got, sems):
        self.place, self.parts, self.own, self.pair, self.got, self.sems = place, parts, own, pair, got, sems

    def load(self, line):
        return pltpu.make_async_copy(
            self.parts.at[2 * line + self.place.core], self.own.at[line], self.sems.at[6, line]
        )

    def swap(self, line):
        row = 2 * line + 1 - self.place.core
        return remote(
            self.parts.at[row], self.pair.at[line], self.sems.at[0, line], self.sems.at[1, line], self.place.twin
        )

    def start(self):
        for line in range(self.place.lines):
            self.swap(line).start()

    def add(self):
        for line in range(self.place.lines):
            self.load(line).wait()
            self.swap(line).wait_recv()
            self.pair[line] = (self.own[line].astype(f32) + self.pair[line].astype(f32)).astype(bf16)

    def up(self, far):
        part = self.place.line + far
        return remote(
            self.pair.at[part], self.got.at[part], self.sems.at[2, far], self.sems.at[3, far], self.place.above()
        )

    def down(self, far):
        part = self.place.line - far
        slot = part if far > 1 else self.place.lines
        return remote(
            self.pair.at[part], self.got.at[slot], self.sems.at[4, far], self.sems.at[5, far], self.place.below()
        )

    def came_up(self, far):
        slot = self.got.at[self.place.line + far]
        remote(slot, slot, self.sems.at[2, far + 1], self.sems.at[3, far + 1], self.place.twin).wait_recv()

    def came_down(self, far):
        slot = self.got.at[self.place.line - far if far else self.place.lines]
        remote(slot, slot, self.sems.at[4, far + 1], self.sems.at[5, far + 1], self.place.twin).wait_recv()

    def send(self, far):
        place = self.place

        @pl.when(place.line + far < place.lines)
        def _():
            @pl.when(place.line > 0)
            def _():
                self.came_up(far)
                part = place.line + far
                self.pair[part] = (self.pair[part].astype(f32) + self.got[part].astype(f32)).astype(bf16)

            self.up(far).start()

        @pl.when(place.line - far >= 0)
        def _():
            @pl.when(place.line < place.lines - 1)
            def _():
                self.came_down(far)
                part = place.line - far
                self.pair[part] = (self.pair[part].astype(f32) + self.got[part].astype(f32)).astype(bf16)

            self.down(far).start()

    def collect(self, out):
        place = self.place
        out[...] = self.pair[place.line].astype(f32)

        @pl.when(place.line > 0)
        def _():
            self.came_up(0)
            out[...] += self.got[place.line].astype(f32)

        @pl.when(place.line < place.lines - 1)
        def _():
            self.came_down(0)
            out[...] += self.got[place.lines].astype(f32)

    def finish(self):
        place = self.place
        for line in range(place.lines):
            self.swap(line).wait_send()
        for far in range(1, place.lines):
            pl.when(place.line + far < place.lines)(lambda: self.up(far).wait_send())
            pl.when(place.line - far >= 0)(lambda: self.down(far).wait_send())

    @staticmethod
    def scratch(dp, tile):
        return [
            pltpu.VMEM((dp // 2,) + tile, bf16),
            pltpu.VMEM((dp // 2,) + tile, bf16),
            pltpu.VMEM((dp // 2 + 1,) + tile, bf16),
            pltpu.SemaphoreType.DMA((7, dp // 2)),
        ]


def mix_back_kernel(
    dp, ctx, gate_ref, up_ref, gate_weight_hbm, up_weight_hbm, inner_hbm, down_hbm, gate_parts,
    resid_ref, cot_ref, gain_ref,
    d_resid_hbm, sums_ref, wide_ref, branch_hbm, d_gate_ref,
    total, sent, got, made, gate_weight_ref, up_weight_ref, inner, down_ref, branch,
    own, pair, line_got, line_sem,
    reduce_sem, spread_sem, load_sem, inner_sem, branch_sem, d_resid_sem,
):
    place = Place(dp)
    size, width = cot_ref.shape
    loads = [
        pltpu.make_async_copy(src, dst, load_sem.at[i])
        for i, (src, dst) in enumerate(
            ((gate_weight_hbm, gate_weight_ref), (up_weight_hbm, up_weight_ref), (down_hbm, down_ref))
        )
    ]
    for load in loads[:2]:
        load.start()
    greet_all(place, dp, ctx)
    line = LineReduce(place, gate_parts, own, pair, line_got, line_sem)
    line.start()
    for i in range(place.lines):
        line.load(i).start()
    for load in loads[:2]:
        load.wait()

    def block(col):
        return dot_nt(rows_of(gate_ref, col, size), gate_weight_ref[...]) + dot_nt(
            rows_of(up_ref, col, size), up_weight_ref[...]
        )

    branch_count = ctx

    def inner_load(i):
        return pltpu.make_async_copy(
            inner_hbm.at[pl.ds(i * size, size), :], inner.at[i % 2], inner_sem.at[i % 2]
        )

    def branch_copy(i):
        return pltpu.make_async_copy(
            branch.at[i % 2], branch_hbm.at[pl.ds(i * size, size), :], branch_sem.at[i % 2]
        )

    def branch_piece(i):
        if i == 0:
            loads[2].wait()
        inner_load(i).wait()
        if i > 1:
            branch_copy(i - 2).wait()
        branch[i % 2] = dot(inner[i % 2], down_ref[...]).astype(bf16)
        branch_copy(i).start()
        if i + 2 < branch_count:
            inner_load(i + 2).start()

    def d_resid_copy(j):
        rows = reduce.chunk(j)
        return pltpu.make_async_copy(total.at[1, rows, :], d_resid_hbm.at[rows, :], d_resid_sem.at[j])

    pieces = [functools.partial(branch_piece, i) for i in range(branch_count)]

    reduce = CtxReduce(place, block, total, sent, got, reduce_sem)
    spread = CtxSpread(place, made, wide_ref, spread_sem)
    reduce.start_far()
    loads[2].start()
    for i in range(2):
        inner_load(i).start()
    reduce.start_near()
    line.add()
    line.send(place.lines - 1)
    reduce.relay()
    sums_ref[...] = jnp.zeros_like(sums_ref)
    far = place.lines - 2
    for j in range(CHUNKS):
        for piece in pieces[j : j + 1]:
            piece()
        rows = reduce.chunk(j)
        scaled, inv_std = norm_stats(resid_ref[rows, :])
        grad, d_gain, d_shift = norm_backward(reduce.sum(j), scaled, inv_std, gain_ref[...])
        sums_ref[0:1, :] += d_gain[None]
        sums_ref[1:2, :] += d_shift[None]
        grad = cot_ref[rows, :].astype(f32) + grad
        total[1, rows, :] = grad
        d_resid_copy(j).start()
        made[rows, :] = grad.astype(bf16)
        spread.send(j)
        if j:
            spread.relay(j - 1)
        if j == 1 and far > 0:
            line.send(far)
            far -= 1
    spread.relay(CHUNKS - 1)
    while far > 0:
        line.send(far)
        far -= 1
    for piece in pieces[CHUNKS:]:
        piece()
    spread.finish()
    line.collect(d_gate_ref)
    line.finish()
    reduce.finish()
    for i in (1, 2):
        branch_copy(branch_count - i).wait()
    for j in range(CHUNKS):
        d_resid_copy(j).wait()


def mix_back(dp, ctx, d_gate, d_up, gate_weight, up_weight, inner, down, gate_parts, resid, cot, gain):
    size, width = cot.shape
    hidden = d_up.shape[1]
    own = width // dp
    vmem = pl.BlockSpec(memory_space=pltpu.VMEM)
    return pl.pallas_call(
        functools.partial(mix_back_kernel, dp, ctx),
        in_specs=[vmem] * 2 + [HBM] * 5 + [vmem] * 3,
        out_specs=[HBM, vmem, HBM, HBM, vmem],
        out_shape=[
            jax.ShapeDtypeStruct((size, width), f32),
            jax.ShapeDtypeStruct((2, width), f32),
            jax.ShapeDtypeStruct((ctx * size, width), bf16),
            jax.ShapeDtypeStruct((ctx * size, width), bf16),
            jax.ShapeDtypeStruct((own, hidden), f32),
        ],
        scratch_shapes=CtxReduce.scratch(size, width)[:3]
        + [
            pltpu.VMEM((size, width), bf16),
            pltpu.VMEM((width, hidden), bf16),
            pltpu.VMEM((width, hidden), bf16),
            pltpu.VMEM((2, size, hidden), bf16),
            pltpu.VMEM((hidden, width), bf16),
            pltpu.VMEM((2, size, width), bf16),
        ]
        + LineReduce.scratch(dp, (own, hidden))
        + [
            CtxReduce.scratch(size, width)[3],
            CtxSpread.scratch(),
            pltpu.SemaphoreType.DMA((3,)),
            pltpu.SemaphoreType.DMA((2,)),
            pltpu.SemaphoreType.DMA((2,)),
            pltpu.SemaphoreType.DMA((CHUNKS,)),
        ],
        compiler_params=pltpu.CompilerParams(
            collective_id=3, has_side_effects=True, vmem_limit_bytes=62 << 20
        ),
        cost_estimate=pl.CostEstimate(
            flops=8 * d_gate.size * width, transcendentals=0, bytes_accessed=180 << 20
        ),
    )(
        d_gate, d_up, gate_weight, up_weight, inner, down, gate_parts.reshape(dp, own, hidden),
        resid, cot, gain.reshape(1, width),
    )


class CtxReduceReady:
    def __init__(self, place, full, have, got, sems, load_sems):
        self.place, self.full, self.have, self.got, self.sems, self.load_sems = place, full, have, got, sems, load_sems
        self.height = have.shape[1]
        self.size = self.height // CHUNKS

    def chunk(self, j):
        return pl.ds(j * self.size, self.size)

    def load(self, kind):
        col = self.place.other(kind)
        rows = pl.ds(pl.multiple_of(col * self.height, self.height), self.height)
        return pltpu.make_async_copy(self.full.at[rows, :], self.have.at[kind], self.load_sems.at[kind])

    def copy(self, kind, j):
        place = self.place
        if kind:
            part, way = self.have.at[kind, self.chunk(j)], kind
        else:
            at = (place.other(3) * CHUNKS + j) * self.size
            part, way = self.full.at[pl.ds(pl.multiple_of(at, self.size), self.size), :], 1 + j % 2
        return remote(
            part, self.got.at[kind, self.chunk(j)], self.sems.at[0, kind, j], self.sems.at[1, kind, j],
            place.across(way),
        )

    def start(self):
        for j in range(CHUNKS):
            self.copy(0, j).start()
        for kind in (1, 2):
            self.load(kind).wait()
            for j in range(CHUNKS):
                if kind == 1 + j % 2:
                    self.copy(kind, j).start()

    def relay(self):
        for j in range(CHUNKS):
            kind, rows = 2 - j % 2, self.chunk(j)
            self.copy(0, j).wait_recv()
            share = self.have[kind, rows].astype(f32) + self.got[0, rows].astype(f32)
            self.have[kind, rows] = share.astype(bf16)
            self.copy(kind, j).start()

    def sum(self, j):
        for kind in (1, 2):
            self.copy(kind, j).wait_recv()
        rows = self.chunk(j)
        return self.have[0, rows].astype(f32) + self.got[1, rows].astype(f32) + self.got[2, rows].astype(f32)

    def finish(self):
        for kind in range(3):
            for j in range(CHUNKS):
                self.copy(kind, j).wait_send()


def closing_kernel(
    dp, ctx,
    d_joined_hbm, weight_hbm, qkv_parts, branch_hbm, rows_hbm, d_resid_hbm, resid_hbm,
    gain_ref, sums_two_ref, bias_ref,
    grad_ref, qkv_ref, output_ref, vectors_ref, d_bias_ref,
    d_joined_ref, weight_ref, rows_ref, d_resid_ref, resid_ref, load_sem,
    total, sent, got, reduce_sem, qkv_own, qkv_pair, qkv_got, qkv_sem,
    have, branch_got, branch_sem, branch_load_sem,
    sums, tiles, tiles_got, small, small_sem, mine, swap_out, swap_in, swap_sem,
):
    place = Place(dp)
    me, row = place.col, place.row
    lines = [
        LineReduce(place, qkv_parts, qkv_own, qkv_pair, qkv_got, qkv_sem),
    ]
    loads = [
        pltpu.make_async_copy(src, dst, load_sem.at[i])
        for i, (src, dst) in enumerate(
            (
                (d_joined_hbm, d_joined_ref), (weight_hbm, weight_ref), (rows_hbm, rows_ref),
                (d_resid_hbm, d_resid_ref), (resid_hbm, resid_ref),
            )
        )
    ]
    for load in loads[:2]:
        load.start()
    greet_all(place, dp, ctx)
    for line in lines:
        line.start()
    for i in range(place.lines):
        for line in lines:
            line.load(i).start()
    branch = CtxReduceReady(place, branch_hbm, have, branch_got, branch_sem, branch_load_sem)
    for kind in range(3):
        branch.load(kind).start()
    for load in loads[2:]:
        load.start()

    size, width = rows_ref.shape
    for load in loads[:2]:
        load.wait()
    reduce = CtxReduce(
        place, lambda col: dot_nt(rows_of(d_joined_ref, col, size), weight_ref[...]), total, sent, got, reduce_sem
    )
    reduce.start_far()
    for line in lines:
        line.add()
        line.send(place.lines - 1)
    reduce.start_near()
    branch.start()
    reduce.relay()
    for far in range(place.lines - 2, 1, -1):
        for line in lines:
            line.send(far)

    sums[...] = jnp.zeros_like(sums)
    for load in loads[2:]:
        load.wait()
    branch.load(0).wait()
    for j in range(CHUNKS):
        rows = reduce.chunk(j)
        scaled, inv_std = norm_stats(rows_ref[rows, :].astype(f32))
        grad, d_gain, d_shift = norm_backward(reduce.sum(j), scaled, inv_std, gain_ref[...])
        sums[0:1, :] += d_gain[None]
        sums[1:2, :] += d_shift[None]
        grad_ref[rows, :] = d_resid_ref[rows, :] + grad
    branch.relay()
    if place.lines > 2:
        for line in lines:
            line.send(1)

    part = width // dp
    tiles[...] = jnp.zeros_like(tiles)
    for i in range(dp):
        lanes = slice(i * part, (i + 1) * part)
        tiles[i, 0:2, :] = sums[:, lanes]
        tiles[i, 2:4, :] = sums_two_ref[:, lanes]
        tiles[i, 4:5, :] = bias_ref[i : i + 1, :]
    sends = [
        remote(tiles.at[(row + k) % dp], tiles_got.at[k], small_sem.at[0, k], small_sem.at[1, k], ((row + k) % dp, me))
        for k in range(1, dp)
    ]
    for copy in sends:
        copy.start()
    tile = tiles[row]
    for k in range(1, dp):
        sends[k - 1].wait()
        tile = tile + tiles_got[k]
    tiles_got[0] = tile
    small[me] = tile
    spreads = [
        remote(tiles_got.at[0], small.at[me], small_sem.at[2, k], small_sem.at[3, k], place.across(k))
        for k in range(1, ctx)
    ]
    for copy in spreads:
        copy.start()

    for j in range(CHUNKS):
        rows = branch.chunk(j)
        output_ref[rows, :] = (resid_ref[rows, :] + branch.sum(j)).astype(bf16)

    for k in range(1, ctx):
        spreads[k - 1].wait_send()
        part = small.at[place.other(k)]
        remote(part, part, small_sem.at[2, k], small_sem.at[3, k], place.across(k)).wait_recv()
    four = sum(small[c, 0:4, :] for c in range(ctx))
    piece = vectors_ref.shape[1]
    slots = d_bias_ref.shape[1] // HD
    vectors = four[:, :piece]
    biases = [small[i % ctx, 4:5, i // ctx * HD : (i // ctx + 1) * HD] for i in range(slots * ctx)]
    chosen = biases[:slots]
    for c in range(1, ctx):
        vectors = jnp.where(me == c, four[:, c * piece : (c + 1) * piece], vectors)
        chosen = [jnp.where(me == c, biases[slots * c + i], chosen[i]) for i in range(slots)]
    vectors_ref[...] = vectors
    for i in range(slots):
        d_bias_ref[:, i * HD : (i + 1) * HD] = chosen[i]

    lines[0].collect(mine)
    depth = mine.shape[0] // ctx
    swap_out[...] = mine[...].astype(bf16)
    swaps = [
        remote(
            swap_out.at[pl.ds(pl.multiple_of(place.other(k) * depth, depth), depth), :], swap_in.at[me],
            swap_sem.at[0, k], swap_sem.at[1, k], place.across(k),
        )
        for k in range(1, ctx)
    ]
    for copy in swaps:
        copy.start()
    swap_in[me] = rows_of(swap_out, me, depth)
    for k in range(1, ctx):
        part = swap_in.at[place.other(k)]
        remote(part, part, swap_sem.at[0, k], swap_sem.at[1, k], place.across(k)).wait_recv()
    low = head_lanes((depth, PAIR))
    for p in range(mine.shape[1] // (3 * PAIR)):
        for t in range(3):
            lanes = slice((3 * p + t) * PAIR, (3 * p + t + 1) * PAIR)
            for c in range(0, ctx, 2):
                a = swap_in[c, :, lanes].astype(f32)
                b = swap_in[c + 1, :, lanes].astype(f32)
                at = t * width + (2 * p * ctx + c) * HD
                qkv_ref[:, at : at + PAIR] = jnp.where(low, a, pltpu.roll(b, HD, 1))
                at = at + ctx * HD
                qkv_ref[:, at : at + PAIR] = jnp.where(low, pltpu.roll(a, HD, 1), b)
    for copy in swaps:
        copy.wait_send()
    for line in lines:
        line.finish()
    branch.finish()
    reduce.finish()


def closing(dp, ctx, d_joined, weight, d_qkv, branch, rows, d_resid, resid, gain, sums_two, bias):
    size, width = rows.shape
    near = weight.shape[1]
    own = width // dp
    vmem = pl.BlockSpec(memory_space=pltpu.VMEM)
    reduce_scratch = CtxReduce.scratch(size, width)
    max_peers = max(dp, ctx)
    return pl.pallas_call(
        functools.partial(closing_kernel, dp, ctx),
        in_specs=[HBM] * 7 + [vmem] * 3,
        out_specs=[vmem] * 5,
        out_shape=[
            jax.ShapeDtypeStruct((size, width), f32),
            jax.ShapeDtypeStruct((own // ctx, 3 * width), f32),
            jax.ShapeDtypeStruct((size, width), bf16),
            jax.ShapeDtypeStruct((4, own // ctx), f32),
            jax.ShapeDtypeStruct((1, 3 * own // ctx), f32),
        ],
        scratch_shapes=[
            pltpu.VMEM((ctx * size, near), bf16),
            pltpu.VMEM((width, near), bf16),
            pltpu.VMEM((size, width), bf16),
            pltpu.VMEM((size, width), f32),
            pltpu.VMEM((size, width), f32),
            pltpu.SemaphoreType.DMA((5,)),
        ]
        + reduce_scratch
        + LineReduce.scratch(dp, (own, near))
        + reduce_scratch[1:]
        + [
            pltpu.SemaphoreType.DMA((3,)),
            pltpu.VMEM((2, width), f32),
            pltpu.VMEM((dp, 8, own), f32),
            pltpu.VMEM((dp, 8, own), f32),
            pltpu.VMEM((ctx, 8, own), f32),
            pltpu.SemaphoreType.DMA((4, max_peers)),
            pltpu.VMEM((own, near), f32),
            pltpu.VMEM((own, near), bf16),
            pltpu.VMEM((ctx, own // ctx, near), bf16),
            pltpu.SemaphoreType.DMA((2, ctx)),
        ],
        compiler_params=pltpu.CompilerParams(
            collective_id=1, has_side_effects=True, vmem_limit_bytes=62 << 20
        ),
        cost_estimate=pl.CostEstimate(
            flops=2 * d_joined.size * width, transcendentals=0, bytes_accessed=200 << 20
        ),
    )(
        d_joined, weight, d_qkv.reshape(dp, own, near), branch,
        rows, d_resid, resid, gain.reshape(1, width), sums_two, bias,
    )


def turn(x, table_ref):
    return (
        x * table_ref[0]
        + pltpu.roll(x, PAIR - ROT // 2, 1) * table_ref[1]
        + pltpu.roll(x, ROT // 2, 1) * table_ref[2]
    )


def turn_back(x, table_ref):
    return (
        x * table_ref[0]
        - pltpu.roll(x, PAIR - ROT // 2, 1) * table_ref[1]
        - pltpu.roll(x, ROT // 2, 1) * table_ref[2]
    )


def head_lanes(shape):
    return lax.broadcasted_iota(jnp.int32, shape, 1) < HD


def span(full_len, step, at):
    return max(0, (at - DOC_MAX + 1) // step * step), at + step


def parts_of(low, at, step):
    return ([(low, at, False)] if low < at else []) + [(at, at + step, True)]


def masked(scores, start, first, causal):
    keys = lax.broadcasted_iota(jnp.int32, scores.shape, 1)
    allowed = keys >= start - first
    if causal:
        allowed = allowed & (keys <= lax.broadcasted_iota(jnp.int32, scores.shape, 0))
    return jnp.where(allowed, scores, masked_value)


def one_head(x, head):
    return jnp.where(head_lanes(x.shape) == (head == 0), x, jnp.zeros_like(x))


def attend_kernel(step, joined_ref, bias_ref, table_ref, start_ref, out_ref, qkv_ref, lse_ref):
    full_len = joined_ref.shape[0]
    scale = 1.0 / math.sqrt(HD)
    for t in range(3):
        lanes = slice(t * PAIR, (t + 1) * PAIR)
        x = joined_ref[:, lanes] + bias_ref[:, lanes]
        if t < 2:
            x = turn(x, table_ref)
        qkv_ref[:, lanes] = x.astype(bf16)
    for at in range(0, full_len, step):
        parts = parts_of(span(full_len, step, at)[0], at, step)
        start = start_ref[at : at + step, :1]
        q = qkv_ref[at : at + step, :PAIR] * bf16(scale)
        total = jnp.zeros((step, PAIR), f32)
        logs = []
        for head in range(2):
            qm = one_head(q, head)
            scores = [
                masked(dot_nt(qm, qkv_ref[low:high, PAIR : 2 * PAIR]), start, low, causal)
                for low, high, causal in parts
            ]
            tops = [jnp.max(s, axis=1, keepdims=True) for s in scores]
            top = functools.reduce(jnp.maximum, tops)
            norm, sums = 0.0, 0.0
            for s, (low, high, _) in zip(scores, parts):
                e = jnp.exp(s - top)
                norm = norm + jnp.sum(e, axis=1, keepdims=True)
                sums = sums + dot(e.astype(bf16), one_head(qkv_ref[low:high, 2 * PAIR :], head))
            total = total + sums * (1.0 / norm)
            logs.append(top + jnp.log(norm))
        out_ref[at : at + step, :] = total.astype(bf16)
        lse_ref[at : at + step, :] = jnp.where(head_lanes((step, PAIR)), logs[0], logs[1])


def attend_back_kernel(
    step, qkv_ref, grad_ref, lse_ref, table_ref, start_ref, out_ref, sum_ref, dk_ref, dv_ref
):
    full_len = qkv_ref.shape[0]
    scale = 1.0 / math.sqrt(HD)
    dk_ref[...] = jnp.zeros_like(dk_ref)
    dv_ref[...] = jnp.zeros_like(dv_ref)
    total = jnp.zeros((1, PAIR), f32)
    for at in range(0, full_len, step):
        rows = slice(at, at + step)
        parts = parts_of(span(full_len, step, at)[0], at, step)
        start = start_ref[rows, :1]
        q = qkv_ref[rows, :PAIR] * bf16(scale)
        g = grad_ref[rows, :]
        dq = jnp.zeros((step, PAIR), f32)
        dk = [jnp.zeros((high - low, PAIR), f32) for low, high, _ in parts]
        dv = [jnp.zeros((high - low, PAIR), f32) for low, high, _ in parts]
        for head in range(2):
            qm, gm = one_head(q, head), one_head(g, head)
            lse = lse_ref[rows, head * HD : head * HD + 1]
            probs, dps, mean = [], [], 0.0
            for low, high, causal in parts:
                s = masked(dot_nt(qm, qkv_ref[low:high, PAIR : 2 * PAIR]), start, low, causal)
                probs.append(jnp.exp(s - lse))
                dps.append(dot_nt(gm, qkv_ref[low:high, 2 * PAIR :]))
                mean = mean + jnp.sum(dps[-1] * probs[-1], axis=1, keepdims=True)
            for i, (low, high, _) in enumerate(parts):
                ds = (probs[i] * (dps[i] - mean)).astype(bf16)
                dq = dq + dot(ds, one_head(qkv_ref[low:high, PAIR : 2 * PAIR], head))
                dk[i] = dk[i] + dot_tn(ds, qm)
                dv[i] = dv[i] + dot_tn(probs[i].astype(bf16), gm)
        for i, (low, high, _) in enumerate(parts):
            dk_ref[low:high, :] += dk[i]
            dv_ref[low:high, :] += dv[i]
        dq = turn_back(dq * scale, table_ref.at[:, rows, :]).astype(bf16)
        out_ref[rows, :PAIR] = dq
        total = total + jnp.sum(dq.astype(f32), axis=0, keepdims=True)
    sum_ref[:, :PAIR] = total
    dk = turn_back(dk_ref[...], table_ref).astype(bf16)
    out_ref[:, PAIR : 2 * PAIR] = dk
    sum_ref[:, PAIR : 2 * PAIR] = jnp.sum(dk.astype(f32), axis=0, keepdims=True)
    dv = dv_ref[...].astype(bf16)
    out_ref[:, 2 * PAIR :] = dv
    sum_ref[:, 2 * PAIR :] = jnp.sum(dv.astype(f32), axis=0, keepdims=True)


def whole(shape):
    return pl.BlockSpec(shape, lambda p: (0,) * len(shape))


def attend_step(full_len):
    return min(256, full_len)


def attend(joined, bias, table, start):
    full_len, width = joined.shape
    pairs = width // (3 * PAIR)
    step = attend_step(full_len)
    seen = sum(span(full_len, step, at)[1] - span(full_len, step, at)[0] for at in range(0, full_len, step)) * step
    wide = pl.BlockSpec((full_len, 3 * PAIR), lambda p: (0, p))
    thin = pl.BlockSpec((full_len, PAIR), lambda p: (0, p))
    return pl.pallas_call(
        functools.partial(attend_kernel, step),
        grid=(pairs,),
        in_specs=[
            wide,
            pl.BlockSpec((1, 3 * PAIR), lambda p: (0, p)),
            whole(table.shape),
            whole(start.shape),
        ],
        out_specs=[thin, wide, thin],
        out_shape=[
            jax.ShapeDtypeStruct((full_len, pairs * PAIR), bf16),
            jax.ShapeDtypeStruct((full_len, width), bf16),
            jax.ShapeDtypeStruct((full_len, pairs * PAIR), f32),
        ],
        compiler_params=pltpu.CompilerParams(vmem_limit_bytes=40 << 20),
        cost_estimate=pl.CostEstimate(
            flops=pairs * seen * PAIR * 8, transcendentals=pairs * seen * 2, bytes_accessed=full_len * width * 8
        ),
    )(joined, bias, table, start)


def attend_back(qkv, grad, lse, table, start):
    full_len, width = qkv.shape
    pairs = width // (3 * PAIR)
    step = attend_step(full_len)
    seen = sum(span(full_len, step, at)[1] - span(full_len, step, at)[0] for at in range(0, full_len, step)) * step
    wide = pl.BlockSpec((full_len, 3 * PAIR), lambda p: (0, p))
    thin = pl.BlockSpec((full_len, PAIR), lambda p: (0, p))
    return pl.pallas_call(
        functools.partial(attend_back_kernel, step),
        grid=(pairs,),
        in_specs=[wide, thin, thin, whole(table.shape), whole(start.shape)],
        out_specs=[wide, pl.BlockSpec((1, 3 * PAIR), lambda p: (0, p))],
        out_shape=[
            jax.ShapeDtypeStruct((full_len, width), bf16),
            jax.ShapeDtypeStruct((1, width), f32),
        ],
        scratch_shapes=[pltpu.VMEM((full_len, PAIR), f32), pltpu.VMEM((full_len, PAIR), f32)],
        compiler_params=pltpu.CompilerParams(vmem_limit_bytes=40 << 20),
        cost_estimate=pl.CostEstimate(
            flops=pairs * seen * PAIR * 20, transcendentals=pairs * seen * 2, bytes_accessed=full_len * width * 8
        ),
    )(*[pltpu.with_memory_space_constraint(x, pltpu.HBM) for x in (qkv, grad, lse, table, start)])


def forward_kernel(
    dp, ctx, step,
    gain_one, shift_one, gain_two, shift_two, bias, start_ref, table_hbm,
    qkv_hbm, out_weight_ref, rows_ref, cot_ref, gate_hbm, up_hbm,
    params_ref, weight_hbm, out_hbm, normed_hbm, cot_all, attended_hbm, heads_hbm, lse_hbm, resid_hbm, wide_ref,
    gate_all, up_all,
    small_all, table_ref, small_ref, qkv_ref, blocks, rows_all, weight_ref, normed_ref, joined_ref, bias_ref, out_all,
    attended_ref, heads_ref, lse_ref, total, sent, got, made, resid_ref,
    normed_sem, weight_sem, local_sem, swap_sem, small_sem, line_joined, line_out, line_gate, line_up, rows_sem, cot_sem,
    late_sem, reduce_sem, spread_sem, resid_sem,
):
    place = Place(dp)
    me, row = place.col, place.row
    depth = qkv_ref.shape[0]
    length, width = rows_ref.shape
    rows_out = out_weight_ref.shape[0]
    tall = ctx * depth

    qkv_copy = pltpu.make_async_copy(qkv_hbm, qkv_ref, local_sem.at[4])
    qkv_copy.start()
    table_copy = pltpu.make_async_copy(table_hbm, table_ref, late_sem.at[0])
    table_copy.start()
    greet_all(place, dp, ctx, wait=False)
    small_ref[...] = jnp.zeros_like(small_ref)
    for i, vector in enumerate((gain_one, shift_one, gain_two, shift_two)):
        small_ref[i // 2 : i // 2 + 1, i % 2 * HD : (i % 2 + 1) * HD] = vector[...].astype(f32)
    for i in range(bias.shape[1] // HD):
        small_ref[2 + i // 2 : 3 + i // 2, i % 2 * HD : (i % 2 + 1) * HD] = bias[
            :, i * HD : (i + 1) * HD
        ].astype(f32)
    small_all[row, me] = small_ref[...]
    qkv_copy.wait()

    low = head_lanes((depth, PAIR))
    for p in range(width // HD // ctx // 2):
        for t in range(3):
            lanes = slice((3 * p + t) * PAIR, (3 * p + t + 1) * PAIR)
            for c in range(0, ctx, 2):
                at = t * width + (2 * p * ctx + c) * HD
                a = qkv_ref[:, at : at + PAIR].astype(f32)
                at = at + ctx * HD
                b = qkv_ref[:, at : at + PAIR].astype(f32)
                blocks[c, :, lanes] = jnp.where(low, a, pltpu.roll(b, HD, 1)).astype(bf16)
                blocks[c + 1, :, lanes] = jnp.where(low, pltpu.roll(a, HD, 1), b).astype(bf16)
    greet_all(place, dp, ctx, signal=False)

    def weight_rows(row, col):
        return weight_ref.at[pl.ds(pl.multiple_of((row * ctx + col) * depth, depth), depth), :]

    def out_shard(row):
        return out_all.at[pl.ds(pl.multiple_of(row * rows_out, rows_out), rows_out), :]

    def block(ref, col):
        return ref.at[pl.ds(pl.multiple_of(col * length, length), length), :]

    part_cols = weight_ref.shape[1] // PARTS

    def weight_part(i, row):
        return weight_ref.at[
            pl.ds(pl.multiple_of(row * tall, tall), tall), pl.ds(i * part_cols, part_cols)
        ]

    local = [
        pltpu.make_async_copy(blocks.at[me], weight_rows(row, me), local_sem.at[0]),
        pltpu.make_async_copy(out_weight_ref, out_shard(row), local_sem.at[1]),
        pltpu.make_async_copy(rows_ref, block(rows_all, me), local_sem.at[2]),
        pltpu.make_async_copy(cot_ref, block(cot_all, me), local_sem.at[3]),
    ]
    swaps = [
        remote(small_ref, small_all.at[row, me], swap_sem.at[0, k], swap_sem.at[1, k], place.across(k))
        for k in range(1, ctx)
    ] + [
        remote(
            blocks.at[place.other(k)], weight_rows(row, me), swap_sem.at[2, k], swap_sem.at[3, k], place.across(k)
        )
        for k in range(1, ctx)
    ]
    for copy in swaps:
        copy.start()
    for copy in local:
        copy.start()

    def gate_shard(row):
        tall = gate_hbm.shape[0]
        return gate_all.at[pl.ds(pl.multiple_of(row * tall, tall), tall), :]

    def up_shard(row):
        tall = up_hbm.shape[0]
        return up_all.at[pl.ds(pl.multiple_of(row * tall, tall), tall), :]

    gate_line, up_line = LineGather(place, gate_shard, line_gate), LineGather(place, up_shard, line_up)
    late = [
        pltpu.make_async_copy(gate_hbm, gate_shard(row), late_sem.at[1]),
        pltpu.make_async_copy(up_hbm, up_shard(row), late_sem.at[2]),
    ]
    for copy in late:
        copy.start()
    rows_gather = CtxGather(place, rows_ref, rows_all, length, rows_sem)
    cot_gather = CtxGather(place, cot_ref, cot_all, length, cot_sem)
    out_line = LineGather(place, out_shard, line_out)
    lines = [
        LineGather(place, functools.partial(weight_part, i), line_joined.at[i]) for i in range(PARTS)
    ] + [out_line]
    local[1].wait()
    out_line.send(1)
    rows_gather.first()
    for k in range(1, ctx):
        remote(
            small_ref, small_all.at[row, place.other(k)], swap_sem.at[0, k], swap_sem.at[1, k], place.across(k)
        ).wait_recv()
    small_sends = [
        remote(
            small_all.at[row], small_all.at[row], small_sem.at[0, k], small_sem.at[1, k], ((row + k) % dp, me)
        )
        for k in range(1, dp)
    ]
    for copy in small_sends:
        copy.start()
    local[0].wait()
    for k in range(1, ctx):
        part = weight_rows(row, place.other(k))
        remote(part, part, swap_sem.at[2, k], swap_sem.at[3, k], place.across(k)).wait_recv()
    for line in lines[:PARTS]:
        line.send(1)

    for k in range(1, dp):
        part = small_all.at[(row + dp - k) % dp]
        remote(part, part, small_sem.at[0, k], small_sem.at[1, k], place.twin).wait_recv()
    low = head_lanes((1, PAIR))
    for i in range(dp * ctx // 2):
        lanes = slice(i * PAIR, (i + 1) * PAIR)
        a = small_all[2 * i // ctx, 2 * i % ctx]
        b = small_all[(2 * i + 1) // ctx, (2 * i + 1) % ctx]
        for r in range(2):
            ar, br = a[r : r + 1, :], b[r : r + 1, :]
            params_ref[2 * r : 2 * r + 1, lanes] = jnp.where(low, ar, pltpu.roll(br, HD, 1))
            params_ref[2 * r + 1 : 2 * r + 2, lanes] = jnp.where(low, pltpu.roll(ar, HD, 1), br)

    def normalize(col):
        step = 64

        @pl.loop(0, length // step)
        def _(i):
            rows = pl.ds(pl.multiple_of(col * length + i * step, step), step)
            scaled, _ = norm_stats(rows_all[rows, :].astype(f32))
            normed_ref[rows, :] = (scaled * params_ref[0:1, :] + params_ref[1:2, :]).astype(bf16)

        normed_copy(col).start()

    def normed_copy(col):
        return pltpu.make_async_copy(block(normed_ref, col), block(normed_hbm, col), normed_sem.at[col])

    def weight_copy(i, line):
        part = (
            pl.ds(pl.multiple_of(line * (2 * tall), 2 * tall), 2 * tall),
            pl.ds(i * part_cols, part_cols),
        )
        return pltpu.make_async_copy(weight_ref.at[part], weight_hbm.at[part], weight_sem.at[i, line])

    def multiply(i, line):
        weight_copy(i, line).start()
        at = pl.multiple_of(line * (2 * tall), 2 * tall)
        cols = slice(i * part_cols, (i + 1) * part_cols)

        @pl.loop(0, ctx)
        def _(b):
            rows = pl.ds(pl.multiple_of(b * length, length), length)
            joined_ref[rows, cols] += dot(
                normed_ref[rows, pl.ds(at, 2 * tall)], weight_ref[pl.ds(at, 2 * tall), cols]
            )

    def forward(hop):
        for line in lines:
            line.receive(hop)
            if hop < place.lines - 1:
                line.send(hop + 1)

    def absorb(hop):
        for i in range(PARTS):
            lines[i].settle(hop, functools.partial(multiply, i))

    joined_ref[...] = jnp.zeros_like(joined_ref)
    local[2].wait()
    normalize(me)
    rows_gather.second()
    cot_gather.first()
    for hop in range(1, place.lines):
        forward(hop)
        if hop == 1:
            for col in (place.other(1), place.other(2)):
                normalize(col)
            rows_gather.finish()
            normalize(place.other(3))
        if hop == min(2, place.lines - 1):
            cot_gather.second()
        absorb(hop - 1)
    late[0].wait()
    gate_line.send(1)
    absorb(place.lines - 1)
    late[1].wait()

    low = head_lanes((1, PAIR))
    pairs = joined_ref.shape[1] // (3 * PAIR)
    per_device = bias.shape[1] // HD
    for p in range(pairs):
        for t in range(3):
            chosen = [None, None]
            for c in range(ctx):
                for half in range(2):
                    slot = t * (width // HD) + (2 * p + half) * ctx + c
                    owner, at = slot // per_device, slot % per_device
                    piece = small_all[owner // ctx, owner % ctx, 2 + at // 2 : 3 + at // 2, :]
                    if at % 2 != half:
                        piece = pltpu.roll(piece, HD, 1)
                    chosen[half] = piece if c == 0 else jnp.where(me == c, piece, chosen[half])
            lanes = slice((3 * p + t) * PAIR, (3 * p + t + 1) * PAIR)
            bias_ref[:, lanes] = jnp.where(low, chosen[0], chosen[1])

    def heads_copies():
        return [
            pltpu.make_async_copy(attended_ref, attended_hbm, late_sem.at[3]),
            pltpu.make_async_copy(heads_ref, heads_hbm, late_sem.at[4]),
            pltpu.make_async_copy(lse_ref, lse_hbm, late_sem.at[5]),
            pltpu.make_async_copy(out_all, out_hbm, late_sem.at[6]),
        ]

    def attend_pairs(first, last):
        @pl.loop(first, last)
        def _(p):
            wide = pl.ds(pl.multiple_of(p * (3 * PAIR), 3 * PAIR), 3 * PAIR)
            thin = pl.ds(pl.multiple_of(p * PAIR, PAIR), PAIR)
            attend_kernel(
                step, joined_ref.at[:, wide], bias_ref.at[:, wide], table_ref, start_ref,
                attended_ref.at[:, thin], heads_ref.at[:, wide], lse_ref.at[:, thin],
            )

    def pass_on(line, hop):
        line.receive(hop)
        if hop < place.lines - 1:
            line.send(hop + 1)

    table_copy.wait()
    attend_pairs(0, pairs // 2)
    if place.lines > 1:
        pass_on(gate_line, 1)
    up_line.send(1)
    attend_pairs(pairs // 2, pairs)
    for hop in range(place.lines):
        out_line.settle(hop)
    for line in lines:
        line.finish()
    cot_gather.finish()
    for copy in heads_copies():
        copy.start()

    reduce = CtxReduce(
        place, lambda col: dot(rows_of(attended_ref, col, length), out_all[...]), total, sent, got, reduce_sem
    )
    spread = CtxSpread(place, made, wide_ref, spread_sem)

    def resid_copy(j):
        rows = reduce.chunk(j)
        return pltpu.make_async_copy(resid_ref.at[rows, :], resid_hbm.at[rows, :], resid_sem.at[j])

    reduce.start()
    reduce.relay()
    if place.lines > 2:
        pass_on(gate_line, 2)
    for j in range(CHUNKS):
        rows = reduce.chunk(j)
        at = pl.multiple_of(me * length + j * reduce.size, reduce.size)
        resid = rows_all[pl.ds(at, reduce.size), :].astype(f32) + reduce.sum(j)
        resid_ref[rows, :] = resid
        resid_copy(j).start()
        scaled, _ = norm_stats(resid)
        made[rows, :] = (scaled * params_ref[2:3, :] + params_ref[3:4, :]).astype(bf16)
        spread.send(j)
        if j:
            spread.relay(j - 1)
        if j == 1 and place.lines > 1:
            pass_on(up_line, 1)
    spread.relay(CHUNKS - 1)
    for hop in range(3, place.lines):
        pass_on(gate_line, hop)
    for hop in range(2, place.lines):
        pass_on(up_line, hop)
    spread.finish()
    for line in (gate_line, up_line):
        for hop in range(place.lines):
            line.settle(hop)
        line.finish()
    reduce.finish()
    for copy in swaps + small_sends:
        copy.wait_send()
    local[3].wait()
    for col in range(ctx):
        normed_copy(col).wait()
    for line in range(place.lines):
        for i in range(PARTS):
            weight_copy(i, line).wait()
    for j in range(CHUNKS):
        resid_copy(j).wait()
    for copy in heads_copies():
        copy.wait()


def forward(dp, ctx, vectors, start, table, qkv_weight, out_weight, rows, cot, gate_weight, up_weight):
    depth, width = qkv_weight.shape[0], rows.shape[1]
    length = rows.shape[0]
    full_len = ctx * length
    near = 3 * width // ctx
    thin = near // 3
    hidden = gate_weight.shape[1]
    vmem = pl.BlockSpec(memory_space=pltpu.VMEM)
    reduce_scratch = CtxReduce.scratch(length, width)
    return pl.pallas_call(
        functools.partial(forward_kernel, dp, ctx, attend_step(full_len)),
        in_specs=[vmem] * (len(vectors) + 1) + [HBM] * 7,
        out_specs=[vmem] + [HBM] * 11,
        out_shape=[
            jax.ShapeDtypeStruct((4, width), f32),
            jax.ShapeDtypeStruct((dp * ctx * depth, near), bf16),
            jax.ShapeDtypeStruct((dp * out_weight.shape[0], width), bf16),
            jax.ShapeDtypeStruct((full_len, width), bf16),
            jax.ShapeDtypeStruct((full_len, width), bf16),
            jax.ShapeDtypeStruct((full_len, thin), bf16),
            jax.ShapeDtypeStruct((full_len, near), bf16),
            jax.ShapeDtypeStruct((full_len, thin), f32),
            jax.ShapeDtypeStruct((length, width), f32),
            jax.ShapeDtypeStruct((full_len, width), bf16),
            jax.ShapeDtypeStruct((dp * gate_weight.shape[0], hidden), bf16),
            jax.ShapeDtypeStruct((dp * up_weight.shape[0], hidden), bf16),
        ],
        scratch_shapes=[
            pltpu.VMEM((dp, ctx, 8, PAIR), f32),
            pltpu.VMEM(table.shape, f32),
            pltpu.VMEM((8, PAIR), f32),
            pltpu.VMEM((depth, 3 * width), bf16),
            pltpu.VMEM((ctx, depth, near), bf16),
            pltpu.VMEM((full_len, width), bf16),
            pltpu.VMEM((dp * ctx * depth, near), bf16),
            pltpu.VMEM((full_len, width), bf16),
            pltpu.VMEM((full_len, near), f32),
            pltpu.VMEM((1, near), f32),
            pltpu.VMEM((dp * out_weight.shape[0], width), bf16),
            pltpu.VMEM((full_len, thin), bf16),
            pltpu.VMEM((full_len, near), bf16),
            pltpu.VMEM((full_len, thin), f32),
        ]
        + reduce_scratch[:3]
        + [
            pltpu.VMEM((length, width), bf16),
            pltpu.VMEM((length, width), f32),
            pltpu.SemaphoreType.DMA((ctx,)),
            pltpu.SemaphoreType.DMA((PARTS, dp // 2)),
            pltpu.SemaphoreType.DMA((5,)),
            pltpu.SemaphoreType.DMA((4, ctx)),
            pltpu.SemaphoreType.DMA((2, dp)),
            pltpu.SemaphoreType.DMA((PARTS, 6, dp)),
            LineGather.scratch(dp),
            LineGather.scratch(dp),
            LineGather.scratch(dp),
            CtxGather.scratch(),
            CtxGather.scratch(),
            pltpu.SemaphoreType.DMA((7,)),
            reduce_scratch[3],
            CtxSpread.scratch(),
            pltpu.SemaphoreType.DMA((CHUNKS,)),
        ],
        compiler_params=pltpu.CompilerParams(
            collective_id=0, has_side_effects=True, vmem_limit_bytes=62 << 20
        ),
        cost_estimate=pl.CostEstimate(
            flops=2 * full_len * width * near, transcendentals=0, bytes_accessed=400 << 20
        ),
    )(*vectors, start, table, qkv_weight, out_weight, rows, cot, gate_weight, up_weight)


def rotary_table(full_len):
    half = ROT // 2
    inverse = 10000.0 ** (-2.0 * np.arange(half) / ROT)
    angles = np.arange(full_len)[:, None] * inverse[None, :]
    table = np.zeros((3, full_len, HD), np.float32)
    table[0, :, :half] = table[0, :, half:ROT] = np.cos(angles)
    table[0, :, ROT:] = 1.0
    table[1, :, :half] = -np.sin(angles)
    table[2, :, half:ROT] = np.sin(angles)
    return jnp.asarray(np.concatenate([table, table], axis=2))


def shards(
    dp,
    ctx,
    inputs,
    segments,
    ln1_gain,
    ln1_bias,
    qkv_weight,
    qkv_bias,
    out_weight,
    ln2_gain,
    ln2_bias,
    gate_weight,
    up_weight,
    down_weight,
    cotangent,
):
    local_len, width = inputs.shape[1], inputs.shape[2]
    full_len = segments.shape[1]
    heads = width // HD
    near = heads // ctx
    pairs = near // 2
    me = lax.axis_index("ctx")
    own = me * local_len

    segment = segments[0]
    start = jnp.sum((segment[None, :] < segment[:, None]).astype(jnp.int32), axis=1)
    start = jnp.broadcast_to(start[:, None], (full_len, 128))
    table = rotary_table(full_len)
    part = ln1_gain.shape[0]
    vectors = [v[None, :] for v in (ln1_gain, ln1_bias, ln2_gain, ln2_bias, qkv_bias)]
    rows_here = qkv_weight.shape[0]
    rows, grad_rows = inputs[0], cotangent[0]
    fused = ctx == 4 and dp % 2 == 0 and part == HD
    if fused:
        (
            params, joined_weight, out_full, normed_one, grad_wide, attended, qkv, lse, resid, normed_wide,
            gate_full, up_full,
        ) = forward(
            dp, ctx, vectors, start, table, qkv_weight, out_weight, rows, grad_rows, gate_weight, up_weight
        )
        gain_one, _, gain_two, _ = params
        down_weight, _ = lax.optimization_barrier((down_weight, normed_wide))
    else:
        small = jnp.concatenate(vectors, axis=1).astype(f32)
        small = lax.all_gather(small, ("dp", "ctx"), axis=0, tiled=True)
        blocks = qkv_weight.reshape(rows_here, 3, pairs, 2, ctx, HD).transpose(4, 0, 2, 1, 3, 5)
        blocks = exchange_ctx(blocks.reshape(ctx, rows_here, near * 3 * HD), ctx)
        joined_weight = lax.all_gather(
            blocks.reshape(ctx * rows_here, near * 3 * HD), "dp", axis=0, tiled=True
        )
        out_full = lax.all_gather(out_weight, ("dp", "ctx"), axis=0, tiled=True)
        out_full = out_full.reshape(near, ctx, HD, width)
        out_full = lax.dynamic_index_in_dim(out_full, me, 1, keepdims=False)
        out_full = out_full.reshape(near * HD, width)
        gain_one, shift_one, gain_two, shift_two = [
            small[:, i * part : (i + 1) * part].reshape(width) for i in range(4)
        ]
        scaled_wide, _ = norm_stats(gather_ctx(rows, ctx).astype(f32))
        normed_one = (scaled_wide * gain_one + shift_one).astype(bf16)
        grad_wide = gather_ctx(grad_rows, ctx)
        bias = small[:, 4 * part :].reshape(3, pairs, 2, ctx, HD)
        bias = lax.dynamic_index_in_dim(bias, me, 3, keepdims=False)
        bias = bias.transpose(1, 0, 2, 3).reshape(1, near * 3 * HD)
        attended, qkv, lse = attend(dot(normed_one, joined_weight), bias, table, start)
        resid = rows.astype(f32) + scatter_ctx(dot(attended, out_full), ctx)
        scaled_two, inv_two = norm_stats(resid)
        normed_wide = gather_ctx((scaled_two * gain_two + shift_two).astype(bf16), ctx)
        gate_full = lax.all_gather(gate_weight, "dp", axis=0, tiled=True)
        up_full = lax.all_gather(up_weight, "dp", axis=0, tiled=True)
    down_full = lax.all_gather(down_weight, "dp", axis=1, tiled=True)

    gate = dot(normed_wide, gate_full)
    upward = dot(normed_wide, up_full)
    sigma = jax.nn.sigmoid(gate)
    swish = gate * sigma
    inner = (swish * upward).astype(bf16)
    d_down = dot_tn(inner, grad_wide).astype(bf16)
    grad_wide, d_down = lax.optimization_barrier((grad_wide, d_down))
    d_down = lax.psum_scatter(d_down, "dp", scatter_dimension=1, tiled=True).astype(f32)
    d_inner = dot_nt(grad_wide, down_full)
    d_gate = (d_inner * upward * sigma * (1.0 + gate * (1.0 - sigma))).astype(bf16)
    d_upward = (d_inner * swish).astype(bf16)
    d_gate_weight = dot_tn(normed_wide, d_gate).astype(bf16)
    d_up_weight = dot_tn(normed_wide, d_upward).astype(bf16)
    d_upward, d_up_weight = lax.optimization_barrier((d_upward, d_up_weight))
    d_up_weight = lax.psum_scatter(d_up_weight, "dp", scatter_dimension=0, tiled=True).astype(f32)
    if fused:
        d_resid, sums_two, d_proj, branch, d_gate_weight = mix_back(
            dp, ctx, d_gate, d_upward, gate_full, up_full, inner, down_full, d_gate_weight, resid,
            grad_rows, gain_two,
        )
    else:
        d_gate_weight = lax.psum_scatter(d_gate_weight, "dp", scatter_dimension=0, tiled=True).astype(f32)
        branch = dot(inner, down_full)
        d_normed_two = scatter_ctx(dot_nt(d_gate, gate_full) + dot_nt(d_upward, up_full), ctx)
        grad, d_gain_two, d_shift_two = norm_backward(d_normed_two, scaled_two, inv_two, gain_two)
        d_resid = grad_rows.astype(f32) + grad
        d_proj = gather_ctx(d_resid.astype(bf16), ctx)

    d_attended = dot_nt(d_proj, out_full).astype(bf16)
    d_out_weight = dot_tn(attended, d_proj).astype(bf16)
    d_attended, d_down = lax.optimization_barrier((d_attended, d_down))
    d_joined, d_bias = attend_back(qkv, d_attended, lse, table, start)
    d_joined, d_up_weight, d_out_weight = lax.optimization_barrier((d_joined, d_up_weight, d_out_weight))
    d_joined_weight = dot_tn(normed_one, d_joined).astype(bf16)
    d_bias = d_bias.reshape(pairs, 3, 2, HD).transpose(1, 0, 2, 3)
    if fused:
        d_out_weight = lax.psum_scatter(d_out_weight, "dp", scatter_dimension=0, tiled=True).astype(f32)
        d_bias = jnp.pad(d_bias.reshape(dp, -1), ((0, 0), (0, width // dp - near * 3 * HD // dp)))
        grad_input, d_joined_weight, output, vectors, d_bias = closing(
            dp, ctx, d_joined, joined_weight, d_joined_weight, branch, rows, d_resid, resid,
            gain_one, sums_two, d_bias,
        )
        d_gain_one, d_shift_one, d_gain_two, d_shift_two = vectors
        d_bias = d_bias[0]
    else:
        output = (resid + scatter_ctx(branch, ctx)).astype(bf16)
        at_me = lax.broadcasted_iota(jnp.int32, (1, ctx, 1, 1), 1) == me
        d_out_weight = jnp.where(at_me, d_out_weight.reshape(near, 1, HD, width), jnp.zeros((), bf16))
        d_out_weight = lax.psum_scatter(
            d_out_weight.reshape(width, width), ("dp", "ctx"), scatter_dimension=0, tiled=True
        ).astype(f32)
        d_normed_one = scatter_ctx(dot_nt(d_joined, joined_weight), ctx)
        scaled_one, inv_one = norm_stats(rows.astype(f32))
        grad, d_gain_one, d_shift_one = norm_backward(d_normed_one, scaled_one, inv_one, gain_one)
        grad_input = d_resid + grad
        d_joined_weight = lax.psum_scatter(d_joined_weight, "dp", scatter_dimension=0, tiled=True)
        blocks = exchange_ctx(d_joined_weight.reshape(ctx, rows_here, near * 3 * HD), ctx)
        blocks = blocks.reshape(ctx, rows_here, pairs, 3, 2, HD).transpose(1, 3, 2, 4, 0, 5)
        d_joined_weight = blocks.reshape(rows_here, 3 * width).astype(f32)
        at_me = (lax.broadcasted_iota(jnp.int32, (1, 1, 1, ctx, 1), 3) == me).astype(f32)
        d_bias = (d_bias[:, :, :, None, :] * at_me).reshape(dp * ctx, -1)
        small = jnp.concatenate(
            [t.reshape(dp * ctx, part) for t in (d_gain_one, d_shift_one, d_gain_two, d_shift_two)]
            + [d_bias],
            axis=1,
        )
        small = lax.psum_scatter(small, ("dp", "ctx"), scatter_dimension=0, tiled=True)[0]
        d_gain_one, d_shift_one, d_gain_two, d_shift_two = [
            small[i * part : (i + 1) * part] for i in range(4)
        ]
        d_bias = small[4 * part :]
    return (
        output[None],
        grad_input[None],
        d_gain_one,
        d_shift_one,
        d_joined_weight,
        d_bias,
        d_out_weight,
        d_gain_two,
        d_shift_two,
        d_gate_weight,
        d_up_weight,
        d_down,
    )


def solution(mesh):
    every = ("dp", "ctx")
    return jax.shard_map(
        functools.partial(shards, mesh.shape["dp"], mesh.shape["ctx"]),
        mesh=mesh,
        in_specs=(
            P("dp", "ctx", None),
            P("dp", None),
            P(every),
            P(every),
            P(every, None),
            P(every),
            P(every, None),
            P(every),
            P(every),
            P("dp", "ctx"),
            P("dp", "ctx"),
            P("ctx", "dp"),
            P("dp", "ctx", None),
        ),
        out_specs=(
            P("dp", "ctx", None),
            P("dp", "ctx", None),
            P(every),
            P(every),
            P(every, None),
            P(every),
            P(every, None),
            P(every),
            P(every),
            P("dp", "ctx"),
            P("dp", "ctx"),
            P("ctx", "dp"),
        ),
        check_vma=False,
    )
```

```python
import functools
import math

import jax
import jax.numpy as jnp
import numpy as np
from jax import lax
from jax.experimental import pallas as pl
from jax.experimental.pallas import tpu as pltpu
from jax.sharding import PartitionSpec as P

HD = 64
ROT = 16
DOC_MAX = 512
PAIR = 2 * HD

norm_eps = 1e-05
masked_value = -1e30
f32 = jnp.float32
bf16 = jnp.bfloat16


def dot(a, b):
    return jnp.dot(a, b, preferred_element_type=f32)


def dot_nt(a, b):
    return lax.dot_general(a, b, (((1,), (1,)), ((), ())), preferred_element_type=f32)


def dot_tn(a, b):
    return lax.dot_general(a, b, (((0,), (0,)), ((), ())), preferred_element_type=f32)


def norm_stats(rows):
    row_mean = jnp.mean(rows, axis=-1, keepdims=True)
    centered = rows - row_mean
    variance = jnp.mean(centered * centered, axis=-1, keepdims=True)
    inv_std = lax.rsqrt(variance + norm_eps)
    return centered * inv_std, inv_std


def norm_backward(grad_normed, scaled, inv_std, gain):
    grad_gain = jnp.sum(grad_normed * scaled, axis=0)
    grad_shift = jnp.sum(grad_normed, axis=0)
    inner_grad = grad_normed * gain
    grad_rows = inv_std * (
        inner_grad
        - jnp.mean(inner_grad, axis=-1, keepdims=True)
        - scaled * jnp.mean(inner_grad * scaled, axis=-1, keepdims=True)
    )
    return grad_rows, grad_gain, grad_shift


def partner(n, k):
    return [(c, c ^ k) for c in range(n)]


def hop(x, n, k):
    return lax.ppermute(x, "ctx", partner(n, k))


def gather_relative(block, n):
    if n != 4:
        return [block] + [hop(block, n, k) for k in range(1, n)]
    half = block.shape[0] // 2
    one = hop(block, n, 1)
    two = hop(block, n, 2)
    low = hop(one[:half], n, 2)
    high = hop(two[half:], n, 1)
    return [block, one, two, jnp.concatenate([low, high], axis=0)]


def gather_ctx(block, n):
    me = lax.axis_index("ctx")
    size = block.shape[0]
    parts = gather_relative(block, n)
    full = jnp.zeros((n * size,) + block.shape[1:], block.dtype)
    for k, part in enumerate(parts):
        full = lax.dynamic_update_slice_in_dim(full, part, (me ^ k) * size, 0)
    return full


def scatter_ctx(partial, n):
    me = lax.axis_index("ctx")
    size = partial.shape[0] // n

    def block(k):
        return lax.dynamic_slice_in_dim(partial, (me ^ k) * size, size, 0)

    if n != 4:
        total = block(0).astype(f32)
        for k in range(1, n):
            total = total + hop(block(k).astype(bf16), n, k).astype(f32)
        return total
    half = size // 2
    far = block(3).astype(bf16)
    low = hop(far[:half], n, 1).astype(f32)
    high = hop(far[half:], n, 2).astype(f32)
    one = block(1).astype(f32)
    two = block(2).astype(f32)
    to_one = jnp.concatenate([one[:half], one[half:] + high], axis=0).astype(bf16)
    to_two = jnp.concatenate([two[:half] + low, two[half:]], axis=0).astype(bf16)
    return block(0).astype(f32) + hop(to_one, n, 1).astype(f32) + hop(to_two, n, 2).astype(f32)


def exchange_ctx(blocks, n):
    me = lax.axis_index("ctx")
    got = lax.dynamic_update_slice_in_dim(
        jnp.zeros_like(blocks), lax.dynamic_slice_in_dim(blocks, me, 1, 0), me, 0
    )
    for k in range(1, n):
        sent = lax.dynamic_slice_in_dim(blocks, me ^ k, 1, 0)
        got = lax.dynamic_update_slice_in_dim(got, hop(sent, n, k), me ^ k, 0)
    return got


MESH = pl.DeviceIdType.MESH
HBM = pl.BlockSpec(memory_space=pltpu.HBM)


class Place:
    def __init__(self, dp):
        self.row = lax.axis_index("dp")
        self.col = lax.axis_index("ctx")
        self.lines = dp // 2
        self.line = self.row // 2
        self.core = self.row % 2
        self.twin = (self.row + 1 - 2 * self.core, self.col)

    def other(self, k):
        col, bit = self.col, 1
        while bit <= k:
            if k & bit:
                col = col + bit * (1 - 2 * ((self.col // bit) % 2))
            bit *= 2
        return col

    def across(self, k):
        return (self.row, self.other(k))

    def above(self):
        return (self.row + 2, self.col)

    def below(self):
        return (self.row - 2, self.col)


def greet(place, ctx):
    barrier = pltpu.get_barrier_semaphore()
    for k in range(1, ctx):
        pl.semaphore_signal(barrier, 1, device_id=place.across(k), device_id_type=MESH)
    pl.semaphore_wait(barrier, ctx - 1)


def remote(src, dst, send, recv, device):
    return pltpu.make_async_remote_copy(
        src_ref=src, dst_ref=dst, send_sem=send, recv_sem=recv, device_id=device, device_id_type=MESH
    )


class LineGather:
    def __init__(self, place, shard, sems):
        self.place, self.shard, self.sems = place, shard, sems

    def row(self, line):
        return line * 2 + self.place.core

    def up(self, hop):
        part = self.shard(self.row(self.place.line - hop + 1))
        return remote(part, part, self.sems.at[0, hop], self.sems.at[1, hop], self.place.above())

    def down(self, hop):
        part = self.shard(self.row(self.place.line + hop - 1))
        return remote(part, part, self.sems.at[2, hop], self.sems.at[3, hop], self.place.below())

    def over(self, at, row):
        part = self.shard(row)
        return remote(part, part, self.sems.at[4, at], self.sems.at[5, at], self.place.twin)

    def sends_up(self, hop):
        return (self.place.line - hop + 1 >= 0) & (self.place.line < self.place.lines - 1)

    def sends_down(self, hop):
        return (self.place.line + hop - 1 < self.place.lines) & (self.place.line > 0)

    def send(self, hop):
        place = self.place
        pl.when(self.sends_up(hop))(lambda: self.up(hop).start())
        pl.when(self.sends_down(hop))(lambda: self.down(hop).start())
        if hop == 1:
            self.over(0, place.row).start()

    def receive(self, hop):
        place = self.place

        @pl.when(place.line - hop >= 0)
        def _():
            part = self.shard(self.row(place.line - hop))
            remote(part, part, self.sems.at[0, hop], self.sems.at[1, hop], place.twin).wait_recv()
            self.over(hop, self.row(place.line - hop)).start()

        @pl.when(place.line + hop < place.lines)
        def _():
            part = self.shard(self.row(place.line + hop))
            remote(part, part, self.sems.at[2, hop], self.sems.at[3, hop], place.twin).wait_recv()
            self.over(place.lines - 1 + hop, self.row(place.line + hop)).start()

    def came_over(self, at, row):
        part = self.shard(row)
        remote(part, part, self.sems.at[4, at], self.sems.at[5, at], self.place.twin).wait_recv()

    def settle(self, hop, use=None):
        place = self.place
        other = 1 - 2 * place.core
        if hop == 0:
            self.came_over(0, place.row + other)
            if use:
                use(place.line)
            return
        for at, line, there in (
            (hop, place.line - hop, place.line - hop >= 0),
            (place.lines - 1 + hop, place.line + hop, place.line + hop < place.lines),
        ):

            @pl.when(there)
            def _():
                self.came_over(at, self.row(line) + other)
                if use:
                    use(line)

    def finish(self):
        place = self.place
        self.over(0, place.row).wait_send()
        for hop in range(1, place.lines):
            pl.when(self.sends_up(hop))(lambda: self.up(hop).wait_send())
            pl.when(self.sends_down(hop))(lambda: self.down(hop).wait_send())
            for at, line, there in (
                (hop, place.line - hop, place.line - hop >= 0),
                (place.lines - 1 + hop, place.line + hop, place.line + hop < place.lines),
            ):
                pl.when(there)(lambda: self.over(at, self.row(line)).wait_send())

    @staticmethod
    def scratch(dp):
        return pltpu.SemaphoreType.DMA((6, dp))


class CtxGather:
    def __init__(self, place, block, full, size, sems):
        self.place, self.block, self.full, self.size, self.sems = place, block, full, size, sems

    def rows(self, col, start=0, size=None):
        size = self.size if size is None else size
        return self.full.at[pl.ds(pl.multiple_of(col * self.size + start, size), size), :]

    def copies(self):
        place, half = self.place, self.size // 2
        me = place.col
        return [
            remote(self.block, self.rows(me), self.sems.at[0, 0], self.sems.at[1, 0], place.across(1)),
            remote(self.block, self.rows(me), self.sems.at[0, 1], self.sems.at[1, 1], place.across(2)),
            remote(
                self.rows(place.other(1), 0, half), self.rows(place.other(1), 0, half),
                self.sems.at[0, 2], self.sems.at[1, 2], place.across(2),
            ),
            remote(
                self.rows(place.other(2), half, half), self.rows(place.other(2), half, half),
                self.sems.at[0, 3], self.sems.at[1, 3], place.across(1),
            ),
        ]

    def arrivals(self):
        place, half = self.place, self.size // 2
        me = place.col
        parts = [self.rows(place.other(1)), self.rows(place.other(2)), self.rows(place.other(3), 0, half), self.rows(place.other(3), half, half)]
        return [
            remote(part, part, self.sems.at[0, i], self.sems.at[1, i], place.across(1))
            for i, part in enumerate(parts)
        ]

    def first(self):
        copies = self.copies()
        copies[0].start()
        copies[1].start()

    def second(self):
        copies, arrivals = self.copies(), self.arrivals()
        arrivals[0].wait_recv()
        copies[2].start()
        arrivals[1].wait_recv()
        copies[3].start()

    def finish(self):
        copies, arrivals = self.copies(), self.arrivals()
        arrivals[2].wait_recv()
        arrivals[3].wait_recv()
        for copy in copies:
            copy.wait_send()

    @staticmethod
    def scratch():
        return pltpu.SemaphoreType.DMA((2, 4))


def greet_all(place, dp, ctx, signal=True, wait=True):
    barrier = pltpu.get_barrier_semaphore()
    if signal:
        for k in range(1, ctx):
            pl.semaphore_signal(barrier, 1, device_id=place.across(k), device_id_type=MESH)
        for k in range(1, dp):
            pl.semaphore_signal(barrier, 1, device_id=((place.row + k) % dp, place.col), device_id_type=MESH)
    if wait:
        pl.semaphore_wait(barrier, ctx + dp - 2)


CHUNKS = 4
PARTS = 2


class CtxReduce:
    def __init__(self, place, block, total, sent, got, sems):
        self.place, self.block, self.total = place, block, total
        self.sent, self.got, self.sems = sent, got, sems
        self.size = total.shape[1] // CHUNKS

    def chunk(self, j):
        return pl.ds(j * self.size, self.size)

    def copy(self, kind, j):
        way = kind if kind else 1 + j % 2
        return remote(
            self.sent.at[kind, self.chunk(j)], self.got.at[kind, self.chunk(j)],
            self.sems.at[0, kind, j], self.sems.at[1, kind, j], self.place.across(way),
        )

    def start(self):
        self.start_far()
        self.start_near()

    def start_far(self):
        self.sent[0] = self.block(self.place.other(3)).astype(bf16)
        for j in range(CHUNKS):
            self.copy(0, j).start()

    def start_near(self):
        place = self.place
        for kind in (1, 2):
            self.total[kind - 1] = self.block(place.other(kind))
            for j in range(CHUNKS):
                if kind == 1 + j % 2:
                    self.sent[kind, self.chunk(j)] = self.total[kind - 1, self.chunk(j)].astype(bf16)
                    self.copy(kind, j).start()

    def relay(self):
        for j in range(CHUNKS):
            kind = 2 - j % 2
            self.copy(0, j).wait_recv()
            share = self.total[kind - 1, self.chunk(j)] + self.got[0, self.chunk(j)].astype(f32)
            self.sent[kind, self.chunk(j)] = share.astype(bf16)
            self.copy(kind, j).start()
        self.total[0] = self.block(self.place.col)

    def sum(self, j):
        for kind in (1, 2):
            self.copy(kind, j).wait_recv()
        rows = self.chunk(j)
        return self.total[0, rows] + self.got[1, rows].astype(f32) + self.got[2, rows].astype(f32)

    def finish(self):
        for kind in range(3):
            for j in range(CHUNKS):
                self.copy(kind, j).wait_send()

    @staticmethod
    def scratch(size, width):
        return [
            pltpu.VMEM((2, size, width), f32),
            pltpu.VMEM((3, size, width), bf16),
            pltpu.VMEM((3, size, width), bf16),
            pltpu.SemaphoreType.DMA((2, 3, CHUNKS)),
        ]


class CtxSpread:
    def __init__(self, place, made, full, sems):
        self.place, self.made, self.full, self.sems = place, made, full, sems
        self.size = made.shape[0] // CHUNKS

    def rows(self, col, j):
        at = (col * CHUNKS + j) * self.size
        return self.full.at[pl.ds(pl.multiple_of(at, self.size), self.size), :]

    def copy(self, kind, j):
        place = self.place
        if kind < 2:
            part, there = self.made.at[pl.ds(j * self.size, self.size), :], self.rows(place.col, j)
            way = 1 + kind
        else:
            way = 2 - j % 2
            part = there = self.rows(place.other(3 - way), j)
        return remote(part, there, self.sems.at[0, kind, j], self.sems.at[1, kind, j], place.across(way))

    def arrived(self, kind, j):
        part = self.rows(self.place.other(kind + 1), j)
        remote(
            part, part, self.sems.at[0, kind, j], self.sems.at[1, kind, j], self.place.across(1)
        ).wait_recv()

    def local(self, j):
        part = self.made.at[pl.ds(j * self.size, self.size), :]
        return pltpu.make_async_copy(part, self.rows(self.place.col, j), self.sems.at[0, 3, j])

    def send(self, j):
        self.copy(0, j).start()
        self.copy(1, j).start()
        self.local(j).start()

    def relay(self, j):
        way = 2 - j % 2
        self.arrived(2 - way, j)
        self.copy(2, j).start()

    def finish(self):
        for j in range(CHUNKS):
            way = 2 - j % 2
            self.arrived(way - 1, j)
            self.arrived(2, j)
            self.local(j).wait()
            for kind in range(3):
                self.copy(kind, j).wait_send()

    @staticmethod
    def scratch():
        return pltpu.SemaphoreType.DMA((2, 4, CHUNKS))


def rows_of(ref, col, size):
    return ref[pl.ds(pl.multiple_of(col * size, size), size), :]


class LineReduce:
    def __init__(self, place, parts, own, pair, got, sems):
        self.place, self.parts, self.own, self.pair, self.got, self.sems = place, parts, own, pair, got, sems

    def load(self, line):
        return pltpu.make_async_copy(
            self.parts.at[2 * line + self.place.core], self.own.at[line], self.sems.at[6, line]
        )

    def swap(self, line):
        row = 2 * line + 1 - self.place.core
        return remote(
            self.parts.at[row], self.pair.at[line], self.sems.at[0, line], self.sems.at[1, line], self.place.twin
        )

    def start(self):
        for line in range(self.place.lines):
            self.swap(line).start()

    def add(self):
        for line in range(self.place.lines):
            self.load(line).wait()
            self.swap(line).wait_recv()
            self.pair[line] = (self.own[line].astype(f32) + self.pair[line].astype(f32)).astype(bf16)

    def up(self, far):
        part = self.place.line + far
        return remote(
            self.pair.at[part], self.got.at[part], self.sems.at[2, far], self.sems.at[3, far], self.place.above()
        )

    def down(self, far):
        part = self.place.line - far
        slot = part if far > 1 else self.place.lines
        return remote(
            self.pair.at[part], self.got.at[slot], self.sems.at[4, far], self.sems.at[5, far], self.place.below()
        )

    def came_up(self, far):
        slot = self.got.at[self.place.line + far]
        remote(slot, slot, self.sems.at[2, far + 1], self.sems.at[3, far + 1], self.place.twin).wait_recv()

    def came_down(self, far):
        slot = self.got.at[self.place.line - far if far else self.place.lines]
        remote(slot, slot, self.sems.at[4, far + 1], self.sems.at[5, far + 1], self.place.twin).wait_recv()

    def send(self, far):
        place = self.place

        @pl.when(place.line + far < place.lines)
        def _():
            @pl.when(place.line > 0)
            def _():
                self.came_up(far)
                part = place.line + far
                self.pair[part] = (self.pair[part].astype(f32) + self.got[part].astype(f32)).astype(bf16)

            self.up(far).start()

        @pl.when(place.line - far >= 0)
        def _():
            @pl.when(place.line < place.lines - 1)
            def _():
                self.came_down(far)
                part = place.line - far
                self.pair[part] = (self.pair[part].astype(f32) + self.got[part].astype(f32)).astype(bf16)

            self.down(far).start()

    def collect(self, out):
        place = self.place
        out[...] = self.pair[place.line].astype(f32)

        @pl.when(place.line > 0)
        def _():
            self.came_up(0)
            out[...] += self.got[place.line].astype(f32)

        @pl.when(place.line < place.lines - 1)
        def _():
            self.came_down(0)
            out[...] += self.got[place.lines].astype(f32)

    def finish(self):
        place = self.place
        for line in range(place.lines):
            self.swap(line).wait_send()
        for far in range(1, place.lines):
            pl.when(place.line + far < place.lines)(lambda: self.up(far).wait_send())
            pl.when(place.line - far >= 0)(lambda: self.down(far).wait_send())

    @staticmethod
    def scratch(dp, tile):
        return [
            pltpu.VMEM((dp // 2,) + tile, bf16),
            pltpu.VMEM((dp // 2,) + tile, bf16),
            pltpu.VMEM((dp // 2 + 1,) + tile, bf16),
            pltpu.SemaphoreType.DMA((7, dp // 2)),
        ]


def mix_back_kernel(
    dp, ctx, gate_ref, up_ref, gate_weight_hbm, up_weight_hbm, inner_hbm, down_hbm, normed_hbm, gate_parts,
    resid_ref, cot_ref, gain_ref,
    d_resid_hbm, sums_ref, wide_ref, branch_hbm, d_up_hbm, d_gate_ref,
    total, sent, got, made, gate_weight_ref, up_weight_ref, inner, down_ref, normed, branch, d_up,
    own, pair, line_got, line_sem,
    reduce_sem, spread_sem, load_sem, inner_sem, normed_sem, branch_sem, d_up_sem, d_resid_sem,
):
    place = Place(dp)
    size, width = cot_ref.shape
    cols = normed.shape[2]
    loads = [
        pltpu.make_async_copy(src, dst, load_sem.at[i])
        for i, (src, dst) in enumerate(
            ((gate_weight_hbm, gate_weight_ref), (up_weight_hbm, up_weight_ref), (down_hbm, down_ref))
        )
    ]
    for load in loads[:2]:
        load.start()
    greet_all(place, dp, ctx)
    line = LineReduce(place, gate_parts, own, pair, line_got, line_sem)
    line.start()
    for i in range(place.lines):
        line.load(i).start()
    for load in loads[:2]:
        load.wait()

    def block(col):
        return dot_nt(rows_of(gate_ref, col, size), gate_weight_ref[...]) + dot_nt(
            rows_of(up_ref, col, size), up_weight_ref[...]
        )

    d_up_count, branch_count = width // cols, ctx

    def normed_load(i):
        return pltpu.make_async_copy(
            normed_hbm.at[:, pl.ds(i * cols, cols)], normed.at[i % 2], normed_sem.at[i % 2]
        )

    def inner_load(i):
        return pltpu.make_async_copy(
            inner_hbm.at[pl.ds(i * size, size), :], inner.at[i % 2], inner_sem.at[i % 2]
        )

    def d_up_copy(i):
        return pltpu.make_async_copy(
            d_up.at[i % 2], d_up_hbm.at[pl.ds(i * cols, cols), :], d_up_sem.at[i % 2]
        )

    def branch_copy(i):
        return pltpu.make_async_copy(
            branch.at[i % 2], branch_hbm.at[pl.ds(i * size, size), :], branch_sem.at[i % 2]
        )

    def d_up_piece(i):
        normed_load(i).wait()
        if i > 1:
            d_up_copy(i - 2).wait()
        d_up[i % 2] = dot_tn(normed[i % 2], up_ref[...]).astype(bf16)
        d_up_copy(i).start()
        if i + 2 < d_up_count:
            normed_load(i + 2).start()

    def branch_piece(i):
        if i == 0:
            loads[2].wait()
        inner_load(i).wait()
        if i > 1:
            branch_copy(i - 2).wait()
        branch[i % 2] = dot(inner[i % 2], down_ref[...]).astype(bf16)
        branch_copy(i).start()
        if i + 2 < branch_count:
            inner_load(i + 2).start()

    def d_resid_copy(j):
        rows = reduce.chunk(j)
        return pltpu.make_async_copy(total.at[1, rows, :], d_resid_hbm.at[rows, :], d_resid_sem.at[j])

    pieces = [functools.partial(d_up_piece, i) for i in range(d_up_count)]
    pieces += [functools.partial(branch_piece, i) for i in range(branch_count)]

    reduce = CtxReduce(place, block, total, sent, got, reduce_sem)
    spread = CtxSpread(place, made, wide_ref, spread_sem)
    reduce.start_far()
    loads[2].start()
    for i in range(2):
        normed_load(i).start()
        inner_load(i).start()
    reduce.start_near()
    line.add()
    line.send(place.lines - 1)
    reduce.relay()
    sums_ref[...] = jnp.zeros_like(sums_ref)
    far = place.lines - 2
    for j in range(CHUNKS):
        for piece in pieces[2 * j : 2 * j + 2]:
            piece()
        rows = reduce.chunk(j)
        scaled, inv_std = norm_stats(resid_ref[rows, :])
        grad, d_gain, d_shift = norm_backward(reduce.sum(j), scaled, inv_std, gain_ref[...])
        sums_ref[0:1, :] += d_gain[None]
        sums_ref[1:2, :] += d_shift[None]
        grad = cot_ref[rows, :].astype(f32) + grad
        total[1, rows, :] = grad
        d_resid_copy(j).start()
        made[rows, :] = grad.astype(bf16)
        spread.send(j)
        if j:
            spread.relay(j - 1)
        if j % 2 == 0 and far > 0:
            line.send(far)
            far -= 1
    pieces[2 * CHUNKS]()
    spread.relay(CHUNKS - 1)
    while far > 0:
        line.send(far)
        far -= 1
    for piece in pieces[2 * CHUNKS + 1 :]:
        piece()
    spread.finish()
    line.collect(d_gate_ref)
    line.finish()
    reduce.finish()
    for i in (1, 2):
        d_up_copy(d_up_count - i).wait()
        branch_copy(branch_count - i).wait()
    for j in range(CHUNKS):
        d_resid_copy(j).wait()


def mix_back(dp, ctx, d_gate, d_up, gate_weight, up_weight, inner, down, normed, gate_parts, resid, cot, gain):
    size, width = cot.shape
    hidden = d_up.shape[1]
    own = width // dp
    cols = width // ctx // 2
    vmem = pl.BlockSpec(memory_space=pltpu.VMEM)
    return pl.pallas_call(
        functools.partial(mix_back_kernel, dp, ctx),
        in_specs=[vmem] * 2 + [HBM] * 6 + [vmem] * 3,
        out_specs=[HBM, vmem, HBM, HBM, HBM, vmem],
        out_shape=[
            jax.ShapeDtypeStruct((size, width), f32),
            jax.ShapeDtypeStruct((2, width), f32),
            jax.ShapeDtypeStruct((ctx * size, width), bf16),
            jax.ShapeDtypeStruct((ctx * size, width), bf16),
            jax.ShapeDtypeStruct((width, hidden), bf16),
            jax.ShapeDtypeStruct((own, hidden), f32),
        ],
        scratch_shapes=CtxReduce.scratch(size, width)[:3]
        + [
            pltpu.VMEM((size, width), bf16),
            pltpu.VMEM((width, hidden), bf16),
            pltpu.VMEM((width, hidden), bf16),
            pltpu.VMEM((2, size, hidden), bf16),
            pltpu.VMEM((hidden, width), bf16),
            pltpu.VMEM((2, ctx * size, cols), bf16),
            pltpu.VMEM((2, size, width), bf16),
            pltpu.VMEM((2, cols, hidden), bf16),
        ]
        + LineReduce.scratch(dp, (own, hidden))
        + [
            CtxReduce.scratch(size, width)[3],
            CtxSpread.scratch(),
            pltpu.SemaphoreType.DMA((3,)),
            pltpu.SemaphoreType.DMA((2,)),
            pltpu.SemaphoreType.DMA((2,)),
            pltpu.SemaphoreType.DMA((2,)),
            pltpu.SemaphoreType.DMA((2,)),
            pltpu.SemaphoreType.DMA((CHUNKS,)),
        ],
        compiler_params=pltpu.CompilerParams(
            collective_id=3, has_side_effects=True, vmem_limit_bytes=62 << 20
        ),
        cost_estimate=pl.CostEstimate(
            flops=8 * d_gate.size * width, transcendentals=0, bytes_accessed=180 << 20
        ),
    )(
        d_gate, d_up, gate_weight, up_weight, inner, down, normed, gate_parts.reshape(dp, own, hidden),
        resid, cot, gain.reshape(1, width),
    )


class CtxReduceReady:
    def __init__(self, place, full, have, got, sems, load_sems):
        self.place, self.full, self.have, self.got, self.sems, self.load_sems = place, full, have, got, sems, load_sems
        self.height = have.shape[1]
        self.size = self.height // CHUNKS

    def chunk(self, j):
        return pl.ds(j * self.size, self.size)

    def load(self, kind):
        col = self.place.other(kind)
        rows = pl.ds(pl.multiple_of(col * self.height, self.height), self.height)
        return pltpu.make_async_copy(self.full.at[rows, :], self.have.at[kind], self.load_sems.at[kind])

    def copy(self, kind, j):
        place = self.place
        if kind:
            part, way = self.have.at[kind, self.chunk(j)], kind
        else:
            at = (place.other(3) * CHUNKS + j) * self.size
            part, way = self.full.at[pl.ds(pl.multiple_of(at, self.size), self.size), :], 1 + j % 2
        return remote(
            part, self.got.at[kind, self.chunk(j)], self.sems.at[0, kind, j], self.sems.at[1, kind, j],
            place.across(way),
        )

    def start(self):
        for j in range(CHUNKS):
            self.copy(0, j).start()
        for kind in (1, 2):
            self.load(kind).wait()
            for j in range(CHUNKS):
                if kind == 1 + j % 2:
                    self.copy(kind, j).start()

    def relay(self):
        for j in range(CHUNKS):
            kind, rows = 2 - j % 2, self.chunk(j)
            self.copy(0, j).wait_recv()
            share = self.have[kind, rows].astype(f32) + self.got[0, rows].astype(f32)
            self.have[kind, rows] = share.astype(bf16)
            self.copy(kind, j).start()

    def sum(self, j):
        for kind in (1, 2):
            self.copy(kind, j).wait_recv()
        rows = self.chunk(j)
        return self.have[0, rows].astype(f32) + self.got[1, rows].astype(f32) + self.got[2, rows].astype(f32)

    def finish(self):
        for kind in range(3):
            for j in range(CHUNKS):
                self.copy(kind, j).wait_send()


def closing_kernel(
    dp, ctx,
    d_joined_hbm, weight_hbm, qkv_parts, out_parts, branch_hbm, rows_hbm, d_resid_hbm, resid_hbm,
    gain_ref, sums_two_ref, bias_ref,
    grad_ref, qkv_ref, out_ref, output_ref, vectors_ref, d_bias_ref,
    d_joined_ref, weight_ref, rows_ref, d_resid_ref, resid_ref, load_sem,
    total, sent, got, reduce_sem, qkv_own, qkv_pair, qkv_got, qkv_sem, out_own, out_pair, out_got, out_sem,
    have, branch_got, branch_sem, branch_load_sem,
    sums, tiles, tiles_got, small, small_sem, mine, swap_out, swap_in, swap_sem,
):
    place = Place(dp)
    me, row = place.col, place.row
    lines = [
        LineReduce(place, qkv_parts, qkv_own, qkv_pair, qkv_got, qkv_sem),
        LineReduce(place, out_parts, out_own, out_pair, out_got, out_sem),
    ]
    loads = [
        pltpu.make_async_copy(src, dst, load_sem.at[i])
        for i, (src, dst) in enumerate(
            (
                (d_joined_hbm, d_joined_ref), (weight_hbm, weight_ref), (rows_hbm, rows_ref),
                (d_resid_hbm, d_resid_ref), (resid_hbm, resid_ref),
            )
        )
    ]
    for load in loads[:2]:
        load.start()
    greet_all(place, dp, ctx)
    for line in lines:
        line.start()
    for i in range(place.lines):
        for line in lines:
            line.load(i).start()
    branch = CtxReduceReady(place, branch_hbm, have, branch_got, branch_sem, branch_load_sem)
    for kind in range(3):
        branch.load(kind).start()
    for load in loads[2:]:
        load.start()

    size, width = rows_ref.shape
    for load in loads[:2]:
        load.wait()
    reduce = CtxReduce(
        place, lambda col: dot_nt(rows_of(d_joined_ref, col, size), weight_ref[...]), total, sent, got, reduce_sem
    )
    reduce.start_far()
    for line in lines:
        line.add()
        line.send(place.lines - 1)
    reduce.start_near()
    reduce.relay()
    branch.start()
    for far in range(place.lines - 2, 1, -1):
        for line in lines:
            line.send(far)

    sums[...] = jnp.zeros_like(sums)
    for load in loads[2:]:
        load.wait()
    branch.load(0).wait()
    for j in range(CHUNKS):
        rows = reduce.chunk(j)
        scaled, inv_std = norm_stats(rows_ref[rows, :].astype(f32))
        grad, d_gain, d_shift = norm_backward(reduce.sum(j), scaled, inv_std, gain_ref[...])
        sums[0:1, :] += d_gain[None]
        sums[1:2, :] += d_shift[None]
        grad_ref[rows, :] = d_resid_ref[rows, :] + grad
    branch.relay()
    if place.lines > 2:
        for line in lines:
            line.send(1)

    part = width // dp
    tiles[...] = jnp.zeros_like(tiles)
    for i in range(dp):
        lanes = slice(i * part, (i + 1) * part)
        tiles[i, 0:2, :] = sums[:, lanes]
        tiles[i, 2:4, :] = sums_two_ref[:, lanes]
        tiles[i, 4:5, :] = bias_ref[i : i + 1, :]
    sends = [
        remote(tiles.at[(row + k) % dp], tiles_got.at[k], small_sem.at[0, k], small_sem.at[1, k], ((row + k) % dp, me))
        for k in range(1, dp)
    ]
    for copy in sends:
        copy.start()
    tile = tiles[row]
    for k in range(1, dp):
        sends[k - 1].wait()
        tile = tile + tiles_got[k]
    tiles_got[0] = tile
    small[me] = tile
    spreads = [
        remote(tiles_got.at[0], small.at[me], small_sem.at[2, k], small_sem.at[3, k], place.across(k))
        for k in range(1, ctx)
    ]
    for copy in spreads:
        copy.start()

    for j in range(CHUNKS):
        rows = branch.chunk(j)
        output_ref[rows, :] = (resid_ref[rows, :] + branch.sum(j)).astype(bf16)

    for k in range(1, ctx):
        spreads[k - 1].wait_send()
        part = small.at[place.other(k)]
        remote(part, part, small_sem.at[2, k], small_sem.at[3, k], place.across(k)).wait_recv()
    four = sum(small[c, 0:4, :] for c in range(ctx))
    piece = vectors_ref.shape[1]
    slots = d_bias_ref.shape[1] // HD
    vectors = four[:, :piece]
    biases = [small[i % ctx, 4:5, i // ctx * HD : (i // ctx + 1) * HD] for i in range(slots * ctx)]
    chosen = biases[:slots]
    for c in range(1, ctx):
        vectors = jnp.where(me == c, four[:, c * piece : (c + 1) * piece], vectors)
        chosen = [jnp.where(me == c, biases[slots * c + i], chosen[i]) for i in range(slots)]
    vectors_ref[...] = vectors
    for i in range(slots):
        d_bias_ref[:, i * HD : (i + 1) * HD] = chosen[i]

    lines[0].collect(mine)
    depth = mine.shape[0] // ctx
    swap_out[...] = mine[...].astype(bf16)
    swaps = [
        remote(
            swap_out.at[pl.ds(pl.multiple_of(place.other(k) * depth, depth), depth), :], swap_in.at[me],
            swap_sem.at[0, k], swap_sem.at[1, k], place.across(k),
        )
        for k in range(1, ctx)
    ]
    for copy in swaps:
        copy.start()
    swap_in[me] = rows_of(swap_out, me, depth)
    lines[1].collect(out_ref)
    for k in range(1, ctx):
        part = swap_in.at[place.other(k)]
        remote(part, part, swap_sem.at[0, k], swap_sem.at[1, k], place.across(k)).wait_recv()
    low = head_lanes((depth, PAIR))
    for p in range(mine.shape[1] // (3 * PAIR)):
        for t in range(3):
            lanes = slice((3 * p + t) * PAIR, (3 * p + t + 1) * PAIR)
            for c in range(0, ctx, 2):
                a = swap_in[c, :, lanes].astype(f32)
                b = swap_in[c + 1, :, lanes].astype(f32)
                at = t * width + (2 * p * ctx + c) * HD
                qkv_ref[:, at : at + PAIR] = jnp.where(low, a, pltpu.roll(b, HD, 1))
                at = at + ctx * HD
                qkv_ref[:, at : at + PAIR] = jnp.where(low, pltpu.roll(a, HD, 1), b)
    for copy in swaps:
        copy.wait_send()
    for line in lines:
        line.finish()
    branch.finish()
    reduce.finish()


def closing(dp, ctx, d_joined, weight, d_qkv, d_out, branch, rows, d_resid, resid, gain, sums_two, bias):
    size, width = rows.shape
    near = weight.shape[1]
    own, tall = width // dp, d_out.shape[0] // dp
    vmem = pl.BlockSpec(memory_space=pltpu.VMEM)
    reduce_scratch = CtxReduce.scratch(size, width)
    max_peers = max(dp, ctx)
    return pl.pallas_call(
        functools.partial(closing_kernel, dp, ctx),
        in_specs=[HBM] * 8 + [vmem] * 3,
        out_specs=[vmem] * 6,
        out_shape=[
            jax.ShapeDtypeStruct((size, width), f32),
            jax.ShapeDtypeStruct((own // ctx, 3 * width), f32),
            jax.ShapeDtypeStruct((tall, width), f32),
            jax.ShapeDtypeStruct((size, width), bf16),
            jax.ShapeDtypeStruct((4, own // ctx), f32),
            jax.ShapeDtypeStruct((1, 3 * own // ctx), f32),
        ],
        scratch_shapes=[
            pltpu.VMEM((ctx * size, near), bf16),
            pltpu.VMEM((width, near), bf16),
            pltpu.VMEM((size, width), bf16),
            pltpu.VMEM((size, width), f32),
            pltpu.VMEM((size, width), f32),
            pltpu.SemaphoreType.DMA((5,)),
        ]
        + reduce_scratch
        + LineReduce.scratch(dp, (own, near))
        + LineReduce.scratch(dp, (tall, width))
        + reduce_scratch[1:]
        + [
            pltpu.SemaphoreType.DMA((3,)),
            pltpu.VMEM((2, width), f32),
            pltpu.VMEM((dp, 8, own), f32),
            pltpu.VMEM((dp, 8, own), f32),
            pltpu.VMEM((ctx, 8, own), f32),
            pltpu.SemaphoreType.DMA((4, max_peers)),
            pltpu.VMEM((own, near), f32),
            pltpu.VMEM((own, near), bf16),
            pltpu.VMEM((ctx, own // ctx, near), bf16),
            pltpu.SemaphoreType.DMA((2, ctx)),
        ],
        compiler_params=pltpu.CompilerParams(
            collective_id=1, has_side_effects=True, vmem_limit_bytes=62 << 20
        ),
        cost_estimate=pl.CostEstimate(
            flops=2 * d_joined.size * width, transcendentals=0, bytes_accessed=200 << 20
        ),
    )(
        d_joined, weight, d_qkv.reshape(dp, own, near), d_out.reshape(dp, tall, width), branch,
        rows, d_resid, resid, gain.reshape(1, width), sums_two, bias,
    )


def turn(x, table_ref):
    return (
        x * table_ref[0]
        + pltpu.roll(x, PAIR - ROT // 2, 1) * table_ref[1]
        + pltpu.roll(x, ROT // 2, 1) * table_ref[2]
    )


def turn_back(x, table_ref):
    return (
        x * table_ref[0]
        - pltpu.roll(x, PAIR - ROT // 2, 1) * table_ref[1]
        - pltpu.roll(x, ROT // 2, 1) * table_ref[2]
    )


def head_lanes(shape):
    return lax.broadcasted_iota(jnp.int32, shape, 1) < HD


def span(full_len, step, at):
    return max(0, (at - DOC_MAX + 1) // step * step), at + step


def parts_of(low, at, step):
    return ([(low, at, False)] if low < at else []) + [(at, at + step, True)]


def masked(scores, start, first, causal):
    keys = lax.broadcasted_iota(jnp.int32, scores.shape, 1)
    allowed = keys >= start - first
    if causal:
        allowed = allowed & (keys <= lax.broadcasted_iota(jnp.int32, scores.shape, 0))
    return jnp.where(allowed, scores, masked_value)


def one_head(x, head):
    return jnp.where(head_lanes(x.shape) == (head == 0), x, jnp.zeros_like(x))


def attend_kernel(step, joined_ref, bias_ref, table_ref, start_ref, out_ref, qkv_ref, lse_ref):
    full_len = joined_ref.shape[0]
    scale = 1.0 / math.sqrt(HD)
    for t in range(3):
        lanes = slice(t * PAIR, (t + 1) * PAIR)
        x = joined_ref[:, lanes] + bias_ref[:, lanes]
        if t < 2:
            x = turn(x, table_ref)
        qkv_ref[:, lanes] = x.astype(bf16)
    for at in range(0, full_len, step):
        parts = parts_of(span(full_len, step, at)[0], at, step)
        start = start_ref[at : at + step, :1]
        q = qkv_ref[at : at + step, :PAIR] * bf16(scale)
        total = jnp.zeros((step, PAIR), f32)
        logs = []
        for head in range(2):
            qm = one_head(q, head)
            scores = [
                masked(dot_nt(qm, qkv_ref[low:high, PAIR : 2 * PAIR]), start, low, causal)
                for low, high, causal in parts
            ]
            tops = [jnp.max(s, axis=1, keepdims=True) for s in scores]
            top = functools.reduce(jnp.maximum, tops)
            norm, sums = 0.0, 0.0
            for s, (low, high, _) in zip(scores, parts):
                e = jnp.exp(s - top)
                norm = norm + jnp.sum(e, axis=1, keepdims=True)
                sums = sums + dot(e.astype(bf16), one_head(qkv_ref[low:high, 2 * PAIR :], head))
            total = total + sums * (1.0 / norm)
            logs.append(top + jnp.log(norm))
        out_ref[at : at + step, :] = total.astype(bf16)
        lse_ref[at : at + step, :] = jnp.where(head_lanes((step, PAIR)), logs[0], logs[1])


def attend_back_kernel(
    step, qkv_ref, grad_ref, lse_ref, table_ref, start_ref, out_ref, sum_ref, dk_ref, dv_ref
):
    full_len = qkv_ref.shape[0]
    scale = 1.0 / math.sqrt(HD)
    dk_ref[...] = jnp.zeros_like(dk_ref)
    dv_ref[...] = jnp.zeros_like(dv_ref)
    total = jnp.zeros((1, PAIR), f32)
    for at in range(0, full_len, step):
        rows = slice(at, at + step)
        parts = parts_of(span(full_len, step, at)[0], at, step)
        start = start_ref[rows, :1]
        q = qkv_ref[rows, :PAIR] * bf16(scale)
        g = grad_ref[rows, :]
        dq = jnp.zeros((step, PAIR), f32)
        dk = [jnp.zeros((high - low, PAIR), f32) for low, high, _ in parts]
        dv = [jnp.zeros((high - low, PAIR), f32) for low, high, _ in parts]
        for head in range(2):
            qm, gm = one_head(q, head), one_head(g, head)
            lse = lse_ref[rows, head * HD : head * HD + 1]
            probs, dps, mean = [], [], 0.0
            for low, high, causal in parts:
                s = masked(dot_nt(qm, qkv_ref[low:high, PAIR : 2 * PAIR]), start, low, causal)
                probs.append(jnp.exp(s - lse))
                dps.append(dot_nt(gm, qkv_ref[low:high, 2 * PAIR :]))
                mean = mean + jnp.sum(dps[-1] * probs[-1], axis=1, keepdims=True)
            for i, (low, high, _) in enumerate(parts):
                ds = (probs[i] * (dps[i] - mean)).astype(bf16)
                dq = dq + dot(ds, one_head(qkv_ref[low:high, PAIR : 2 * PAIR], head))
                dk[i] = dk[i] + dot_tn(ds, qm)
                dv[i] = dv[i] + dot_tn(probs[i].astype(bf16), gm)
        for i, (low, high, _) in enumerate(parts):
            dk_ref[low:high, :] += dk[i]
            dv_ref[low:high, :] += dv[i]
        dq = turn_back(dq * scale, table_ref.at[:, rows, :]).astype(bf16)
        out_ref[rows, :PAIR] = dq
        total = total + jnp.sum(dq.astype(f32), axis=0, keepdims=True)
    sum_ref[:, :PAIR] = total
    dk = turn_back(dk_ref[...], table_ref).astype(bf16)
    out_ref[:, PAIR : 2 * PAIR] = dk
    sum_ref[:, PAIR : 2 * PAIR] = jnp.sum(dk.astype(f32), axis=0, keepdims=True)
    dv = dv_ref[...].astype(bf16)
    out_ref[:, 2 * PAIR :] = dv
    sum_ref[:, 2 * PAIR :] = jnp.sum(dv.astype(f32), axis=0, keepdims=True)


def whole(shape):
    return pl.BlockSpec(shape, lambda p: (0,) * len(shape))


def attend_step(full_len):
    return min(256, full_len)


def attend(joined, bias, table, start):
    full_len, width = joined.shape
    pairs = width // (3 * PAIR)
    step = attend_step(full_len)
    seen = sum(span(full_len, step, at)[1] - span(full_len, step, at)[0] for at in range(0, full_len, step)) * step
    wide = pl.BlockSpec((full_len, 3 * PAIR), lambda p: (0, p))
    thin = pl.BlockSpec((full_len, PAIR), lambda p: (0, p))
    return pl.pallas_call(
        functools.partial(attend_kernel, step),
        grid=(pairs,),
        in_specs=[
            wide,
            pl.BlockSpec((1, 3 * PAIR), lambda p: (0, p)),
            whole(table.shape),
            whole(start.shape),
        ],
        out_specs=[thin, wide, thin],
        out_shape=[
            jax.ShapeDtypeStruct((full_len, pairs * PAIR), bf16),
            jax.ShapeDtypeStruct((full_len, width), bf16),
            jax.ShapeDtypeStruct((full_len, pairs * PAIR), f32),
        ],
        compiler_params=pltpu.CompilerParams(vmem_limit_bytes=40 << 20),
        cost_estimate=pl.CostEstimate(
            flops=pairs * seen * PAIR * 8, transcendentals=pairs * seen * 2, bytes_accessed=full_len * width * 8
        ),
    )(joined, bias, table, start)


def attend_back(qkv, grad, lse, table, start):
    full_len, width = qkv.shape
    pairs = width // (3 * PAIR)
    step = attend_step(full_len)
    seen = sum(span(full_len, step, at)[1] - span(full_len, step, at)[0] for at in range(0, full_len, step)) * step
    wide = pl.BlockSpec((full_len, 3 * PAIR), lambda p: (0, p))
    thin = pl.BlockSpec((full_len, PAIR), lambda p: (0, p))
    return pl.pallas_call(
        functools.partial(attend_back_kernel, step),
        grid=(pairs,),
        in_specs=[wide, thin, thin, whole(table.shape), whole(start.shape)],
        out_specs=[wide, pl.BlockSpec((1, 3 * PAIR), lambda p: (0, p))],
        out_shape=[
            jax.ShapeDtypeStruct((full_len, width), bf16),
            jax.ShapeDtypeStruct((1, width), f32),
        ],
        scratch_shapes=[pltpu.VMEM((full_len, PAIR), f32), pltpu.VMEM((full_len, PAIR), f32)],
        compiler_params=pltpu.CompilerParams(vmem_limit_bytes=40 << 20),
        cost_estimate=pl.CostEstimate(
            flops=pairs * seen * PAIR * 20, transcendentals=pairs * seen * 2, bytes_accessed=full_len * width * 8
        ),
    )(*[pltpu.with_memory_space_constraint(x, pltpu.HBM) for x in (qkv, grad, lse, table, start)])


def forward_kernel(
    dp, ctx, step,
    gain_one, shift_one, gain_two, shift_two, bias, start_ref, table_hbm,
    qkv_hbm, out_weight_ref, rows_ref, cot_ref, gate_hbm, up_hbm,
    params_ref, weight_hbm, out_hbm, normed_hbm, cot_all, attended_hbm, heads_hbm, lse_hbm, resid_hbm, wide_ref,
    gate_all, up_all,
    small_all, table_ref, small_ref, qkv_ref, blocks, rows_all, weight_ref, normed_ref, joined_ref, bias_ref, out_all,
    attended_ref, heads_ref, lse_ref, total, sent, got, made, resid_ref,
    normed_sem, weight_sem, local_sem, swap_sem, small_sem, line_joined, line_out, line_gate, line_up, rows_sem, cot_sem,
    late_sem, reduce_sem, spread_sem, resid_sem,
):
    place = Place(dp)
    me, row = place.col, place.row
    depth = qkv_ref.shape[0]
    length, width = rows_ref.shape
    rows_out = out_weight_ref.shape[0]
    tall = ctx * depth

    qkv_copy = pltpu.make_async_copy(qkv_hbm, qkv_ref, local_sem.at[4])
    qkv_copy.start()
    table_copy = pltpu.make_async_copy(table_hbm, table_ref, late_sem.at[0])
    table_copy.start()
    greet_all(place, dp, ctx, wait=False)
    small_ref[...] = jnp.zeros_like(small_ref)
    for i, vector in enumerate((gain_one, shift_one, gain_two, shift_two)):
        small_ref[i // 2 : i // 2 + 1, i % 2 * HD : (i % 2 + 1) * HD] = vector[...].astype(f32)
    for i in range(bias.shape[1] // HD):
        small_ref[2 + i // 2 : 3 + i // 2, i % 2 * HD : (i % 2 + 1) * HD] = bias[
            :, i * HD : (i + 1) * HD
        ].astype(f32)
    small_all[row, me] = small_ref[...]
    qkv_copy.wait()

    low = head_lanes((depth, PAIR))
    for p in range(width // HD // ctx // 2):
        for t in range(3):
            lanes = slice((3 * p + t) * PAIR, (3 * p + t + 1) * PAIR)
            for c in range(0, ctx, 2):
                at = t * width + (2 * p * ctx + c) * HD
                a = qkv_ref[:, at : at + PAIR].astype(f32)
                at = at + ctx * HD
                b = qkv_ref[:, at : at + PAIR].astype(f32)
                blocks[c, :, lanes] = jnp.where(low, a, pltpu.roll(b, HD, 1)).astype(bf16)
                blocks[c + 1, :, lanes] = jnp.where(low, pltpu.roll(a, HD, 1), b).astype(bf16)
    greet_all(place, dp, ctx, signal=False)

    def weight_rows(row, col):
        return weight_ref.at[pl.ds(pl.multiple_of((row * ctx + col) * depth, depth), depth), :]

    def out_shard(row):
        return out_all.at[pl.ds(pl.multiple_of(row * rows_out, rows_out), rows_out), :]

    def block(ref, col):
        return ref.at[pl.ds(pl.multiple_of(col * length, length), length), :]

    part_cols = weight_ref.shape[1] // PARTS

    def weight_part(i, row):
        return weight_ref.at[
            pl.ds(pl.multiple_of(row * tall, tall), tall), pl.ds(i * part_cols, part_cols)
        ]

    local = [
        pltpu.make_async_copy(blocks.at[me], weight_rows(row, me), local_sem.at[0]),
        pltpu.make_async_copy(out_weight_ref, out_shard(row), local_sem.at[1]),
        pltpu.make_async_copy(rows_ref, block(rows_all, me), local_sem.at[2]),
        pltpu.make_async_copy(cot_ref, block(cot_all, me), local_sem.at[3]),
    ]
    swaps = [
        remote(small_ref, small_all.at[row, me], swap_sem.at[0, k], swap_sem.at[1, k], place.across(k))
        for k in range(1, ctx)
    ] + [
        remote(
            blocks.at[place.other(k)], weight_rows(row, me), swap_sem.at[2, k], swap_sem.at[3, k], place.across(k)
        )
        for k in range(1, ctx)
    ]
    for copy in swaps:
        copy.start()
    for copy in local:
        copy.start()

    def gate_shard(row):
        tall = gate_hbm.shape[0]
        return gate_all.at[pl.ds(pl.multiple_of(row * tall, tall), tall), :]

    def up_shard(row):
        tall = up_hbm.shape[0]
        return up_all.at[pl.ds(pl.multiple_of(row * tall, tall), tall), :]

    gate_line, up_line = LineGather(place, gate_shard, line_gate), LineGather(place, up_shard, line_up)
    late = [
        pltpu.make_async_copy(gate_hbm, gate_shard(row), late_sem.at[1]),
        pltpu.make_async_copy(up_hbm, up_shard(row), late_sem.at[2]),
    ]
    for copy in late:
        copy.start()
    rows_gather = CtxGather(place, rows_ref, rows_all, length, rows_sem)
    cot_gather = CtxGather(place, cot_ref, cot_all, length, cot_sem)
    out_line = LineGather(place, out_shard, line_out)
    lines = [
        LineGather(place, functools.partial(weight_part, i), line_joined.at[i]) for i in range(PARTS)
    ] + [out_line]
    local[1].wait()
    out_line.send(1)
    rows_gather.first()
    for k in range(1, ctx):
        remote(
            small_ref, small_all.at[row, place.other(k)], swap_sem.at[0, k], swap_sem.at[1, k], place.across(k)
        ).wait_recv()
    small_sends = [
        remote(
            small_all.at[row], small_all.at[row], small_sem.at[0, k], small_sem.at[1, k], ((row + k) % dp, me)
        )
        for k in range(1, dp)
    ]
    for copy in small_sends:
        copy.start()
    local[0].wait()
    for k in range(1, ctx):
        part = weight_rows(row, place.other(k))
        remote(part, part, swap_sem.at[2, k], swap_sem.at[3, k], place.across(k)).wait_recv()
    for line in lines[:PARTS]:
        line.send(1)

    for k in range(1, dp):
        part = small_all.at[(row + dp - k) % dp]
        remote(part, part, small_sem.at[0, k], small_sem.at[1, k], place.twin).wait_recv()
    low = head_lanes((1, PAIR))
    for i in range(dp * ctx // 2):
        lanes = slice(i * PAIR, (i + 1) * PAIR)
        a = small_all[2 * i // ctx, 2 * i % ctx]
        b = small_all[(2 * i + 1) // ctx, (2 * i + 1) % ctx]
        for r in range(2):
            ar, br = a[r : r + 1, :], b[r : r + 1, :]
            params_ref[2 * r : 2 * r + 1, lanes] = jnp.where(low, ar, pltpu.roll(br, HD, 1))
            params_ref[2 * r + 1 : 2 * r + 2, lanes] = jnp.where(low, pltpu.roll(ar, HD, 1), br)

    def normalize(col):
        step = 64

        @pl.loop(0, length // step)
        def _(i):
            rows = pl.ds(pl.multiple_of(col * length + i * step, step), step)
            scaled, _ = norm_stats(rows_all[rows, :].astype(f32))
            normed_ref[rows, :] = (scaled * params_ref[0:1, :] + params_ref[1:2, :]).astype(bf16)

        normed_copy(col).start()

    def normed_copy(col):
        return pltpu.make_async_copy(block(normed_ref, col), block(normed_hbm, col), normed_sem.at[col])

    def weight_copy(i, line):
        part = (
            pl.ds(pl.multiple_of(line * (2 * tall), 2 * tall), 2 * tall),
            pl.ds(i * part_cols, part_cols),
        )
        return pltpu.make_async_copy(weight_ref.at[part], weight_hbm.at[part], weight_sem.at[i, line])

    def multiply(i, line):
        weight_copy(i, line).start()
        at = pl.multiple_of(line * (2 * tall), 2 * tall)
        cols = slice(i * part_cols, (i + 1) * part_cols)

        @pl.loop(0, ctx)
        def _(b):
            rows = pl.ds(pl.multiple_of(b * length, length), length)
            joined_ref[rows, cols] += dot(
                normed_ref[rows, pl.ds(at, 2 * tall)], weight_ref[pl.ds(at, 2 * tall), cols]
            )

    def forward(hop):
        for line in lines:
            line.receive(hop)
            if hop < place.lines - 1:
                line.send(hop + 1)

    def absorb(hop):
        for i in range(PARTS):
            lines[i].settle(hop, functools.partial(multiply, i))

    joined_ref[...] = jnp.zeros_like(joined_ref)
    local[2].wait()
    normalize(me)
    rows_gather.second()
    cot_gather.first()
    for hop in range(1, place.lines):
        forward(hop)
        if hop == 1:
            for col in (place.other(1), place.other(2)):
                normalize(col)
            rows_gather.finish()
            normalize(place.other(3))
        if hop == min(2, place.lines - 1):
            cot_gather.second()
        absorb(hop - 1)
    late[0].wait()
    gate_line.send(1)
    absorb(place.lines - 1)
    late[1].wait()

    low = head_lanes((1, PAIR))
    pairs = joined_ref.shape[1] // (3 * PAIR)
    per_device = bias.shape[1] // HD
    for p in range(pairs):
        for t in range(3):
            chosen = [None, None]
            for c in range(ctx):
                for half in range(2):
                    slot = t * (width // HD) + (2 * p + half) * ctx + c
                    owner, at = slot // per_device, slot % per_device
                    piece = small_all[owner // ctx, owner % ctx, 2 + at // 2 : 3 + at // 2, :]
                    if at % 2 != half:
                        piece = pltpu.roll(piece, HD, 1)
                    chosen[half] = piece if c == 0 else jnp.where(me == c, piece, chosen[half])
            lanes = slice((3 * p + t) * PAIR, (3 * p + t + 1) * PAIR)
            bias_ref[:, lanes] = jnp.where(low, chosen[0], chosen[1])

    def heads_copies():
        return [
            pltpu.make_async_copy(attended_ref, attended_hbm, late_sem.at[3]),
            pltpu.make_async_copy(heads_ref, heads_hbm, late_sem.at[4]),
            pltpu.make_async_copy(lse_ref, lse_hbm, late_sem.at[5]),
            pltpu.make_async_copy(out_all, out_hbm, late_sem.at[6]),
        ]

    def attend_pairs(first, last):
        @pl.loop(first, last)
        def _(p):
            wide = pl.ds(pl.multiple_of(p * (3 * PAIR), 3 * PAIR), 3 * PAIR)
            thin = pl.ds(pl.multiple_of(p * PAIR, PAIR), PAIR)
            attend_kernel(
                step, joined_ref.at[:, wide], bias_ref.at[:, wide], table_ref, start_ref,
                attended_ref.at[:, thin], heads_ref.at[:, wide], lse_ref.at[:, thin],
            )

    def pass_on(line, hop):
        line.receive(hop)
        if hop < place.lines - 1:
            line.send(hop + 1)

    table_copy.wait()
    attend_pairs(0, pairs // 2)
    if place.lines > 1:
        pass_on(gate_line, 1)
    up_line.send(1)
    attend_pairs(pairs // 2, pairs)
    for hop in range(place.lines):
        out_line.settle(hop)
    for line in lines:
        line.finish()
    cot_gather.finish()
    for copy in heads_copies():
        copy.start()

    reduce = CtxReduce(
        place, lambda col: dot(rows_of(attended_ref, col, length), out_all[...]), total, sent, got, reduce_sem
    )
    spread = CtxSpread(place, made, wide_ref, spread_sem)

    def resid_copy(j):
        rows = reduce.chunk(j)
        return pltpu.make_async_copy(resid_ref.at[rows, :], resid_hbm.at[rows, :], resid_sem.at[j])

    reduce.start()
    reduce.relay()
    if place.lines > 2:
        pass_on(gate_line, 2)
    for j in range(CHUNKS):
        rows = reduce.chunk(j)
        at = pl.multiple_of(me * length + j * reduce.size, reduce.size)
        resid = rows_all[pl.ds(at, reduce.size), :].astype(f32) + reduce.sum(j)
        resid_ref[rows, :] = resid
        resid_copy(j).start()
        scaled, _ = norm_stats(resid)
        made[rows, :] = (scaled * params_ref[2:3, :] + params_ref[3:4, :]).astype(bf16)
        spread.send(j)
        if j:
            spread.relay(j - 1)
        if j == 1 and place.lines > 1:
            pass_on(up_line, 1)
    spread.relay(CHUNKS - 1)
    for hop in range(3, place.lines):
        pass_on(gate_line, hop)
    for hop in range(2, place.lines):
        pass_on(up_line, hop)
    spread.finish()
    for line in (gate_line, up_line):
        for hop in range(place.lines):
            line.settle(hop)
        line.finish()
    reduce.finish()
    for copy in swaps + small_sends:
        copy.wait_send()
    local[3].wait()
    for col in range(ctx):
        normed_copy(col).wait()
    for line in range(place.lines):
        for i in range(PARTS):
            weight_copy(i, line).wait()
    for j in range(CHUNKS):
        resid_copy(j).wait()
    for copy in heads_copies():
        copy.wait()


def forward(dp, ctx, vectors, start, table, qkv_weight, out_weight, rows, cot, gate_weight, up_weight):
    depth, width = qkv_weight.shape[0], rows.shape[1]
    length = rows.shape[0]
    full_len = ctx * length
    near = 3 * width // ctx
    thin = near // 3
    hidden = gate_weight.shape[1]
    vmem = pl.BlockSpec(memory_space=pltpu.VMEM)
    reduce_scratch = CtxReduce.scratch(length, width)
    return pl.pallas_call(
        functools.partial(forward_kernel, dp, ctx, attend_step(full_len)),
        in_specs=[vmem] * (len(vectors) + 1) + [HBM] * 7,
        out_specs=[vmem] + [HBM] * 11,
        out_shape=[
            jax.ShapeDtypeStruct((4, width), f32),
            jax.ShapeDtypeStruct((dp * ctx * depth, near), bf16),
            jax.ShapeDtypeStruct((dp * out_weight.shape[0], width), bf16),
            jax.ShapeDtypeStruct((full_len, width), bf16),
            jax.ShapeDtypeStruct((full_len, width), bf16),
            jax.ShapeDtypeStruct((full_len, thin), bf16),
            jax.ShapeDtypeStruct((full_len, near), bf16),
            jax.ShapeDtypeStruct((full_len, thin), f32),
            jax.ShapeDtypeStruct((length, width), f32),
            jax.ShapeDtypeStruct((full_len, width), bf16),
            jax.ShapeDtypeStruct((dp * gate_weight.shape[0], hidden), bf16),
            jax.ShapeDtypeStruct((dp * up_weight.shape[0], hidden), bf16),
        ],
        scratch_shapes=[
            pltpu.VMEM((dp, ctx, 8, PAIR), f32),
            pltpu.VMEM(table.shape, f32),
            pltpu.VMEM((8, PAIR), f32),
            pltpu.VMEM((depth, 3 * width), bf16),
            pltpu.VMEM((ctx, depth, near), bf16),
            pltpu.VMEM((full_len, width), bf16),
            pltpu.VMEM((dp * ctx * depth, near), bf16),
            pltpu.VMEM((full_len, width), bf16),
            pltpu.VMEM((full_len, near), f32),
            pltpu.VMEM((1, near), f32),
            pltpu.VMEM((dp * out_weight.shape[0], width), bf16),
            pltpu.VMEM((full_len, thin), bf16),
            pltpu.VMEM((full_len, near), bf16),
            pltpu.VMEM((full_len, thin), f32),
        ]
        + reduce_scratch[:3]
        + [
            pltpu.VMEM((length, width), bf16),
            pltpu.VMEM((length, width), f32),
            pltpu.SemaphoreType.DMA((ctx,)),
            pltpu.SemaphoreType.DMA((PARTS, dp // 2)),
            pltpu.SemaphoreType.DMA((5,)),
            pltpu.SemaphoreType.DMA((4, ctx)),
            pltpu.SemaphoreType.DMA((2, dp)),
            pltpu.SemaphoreType.DMA((PARTS, 6, dp)),
            LineGather.scratch(dp),
            LineGather.scratch(dp),
            LineGather.scratch(dp),
            CtxGather.scratch(),
            CtxGather.scratch(),
            pltpu.SemaphoreType.DMA((7,)),
            reduce_scratch[3],
            CtxSpread.scratch(),
            pltpu.SemaphoreType.DMA((CHUNKS,)),
        ],
        compiler_params=pltpu.CompilerParams(
            collective_id=0, has_side_effects=True, vmem_limit_bytes=62 << 20
        ),
        cost_estimate=pl.CostEstimate(
            flops=2 * full_len * width * near, transcendentals=0, bytes_accessed=400 << 20
        ),
    )(*vectors, start, table, qkv_weight, out_weight, rows, cot, gate_weight, up_weight)


def rotary_table(full_len):
    half = ROT // 2
    inverse = 10000.0 ** (-2.0 * np.arange(half) / ROT)
    angles = np.arange(full_len)[:, None] * inverse[None, :]
    table = np.zeros((3, full_len, HD), np.float32)
    table[0, :, :half] = table[0, :, half:ROT] = np.cos(angles)
    table[0, :, ROT:] = 1.0
    table[1, :, :half] = -np.sin(angles)
    table[2, :, half:ROT] = np.sin(angles)
    return jnp.asarray(np.concatenate([table, table], axis=2))


def shards(
    dp,
    ctx,
    inputs,
    segments,
    ln1_gain,
    ln1_bias,
    qkv_weight,
    qkv_bias,
    out_weight,
    ln2_gain,
    ln2_bias,
    gate_weight,
    up_weight,
    down_weight,
    cotangent,
):
    local_len, width = inputs.shape[1], inputs.shape[2]
    full_len = segments.shape[1]
    heads = width // HD
    near = heads // ctx
    pairs = near // 2
    me = lax.axis_index("ctx")
    own = me * local_len

    segment = segments[0]
    start = jnp.sum((segment[None, :] < segment[:, None]).astype(jnp.int32), axis=1)
    start = jnp.broadcast_to(start[:, None], (full_len, 128))
    table = rotary_table(full_len)
    part = ln1_gain.shape[0]
    vectors = [v[None, :] for v in (ln1_gain, ln1_bias, ln2_gain, ln2_bias, qkv_bias)]
    rows_here = qkv_weight.shape[0]
    rows, grad_rows = inputs[0], cotangent[0]
    fused = ctx == 4 and dp % 2 == 0 and part == HD
    if fused:
        (
            params, joined_weight, out_full, normed_one, grad_wide, attended, qkv, lse, resid, normed_wide,
            gate_full, up_full,
        ) = forward(
            dp, ctx, vectors, start, table, qkv_weight, out_weight, rows, grad_rows, gate_weight, up_weight
        )
        gain_one, _, gain_two, _ = params
        down_weight, _ = lax.optimization_barrier((down_weight, normed_wide))
    else:
        small = jnp.concatenate(vectors, axis=1).astype(f32)
        small = lax.all_gather(small, ("dp", "ctx"), axis=0, tiled=True)
        blocks = qkv_weight.reshape(rows_here, 3, pairs, 2, ctx, HD).transpose(4, 0, 2, 1, 3, 5)
        blocks = exchange_ctx(blocks.reshape(ctx, rows_here, near * 3 * HD), ctx)
        joined_weight = lax.all_gather(
            blocks.reshape(ctx * rows_here, near * 3 * HD), "dp", axis=0, tiled=True
        )
        out_full = lax.all_gather(out_weight, ("dp", "ctx"), axis=0, tiled=True)
        out_full = out_full.reshape(near, ctx, HD, width)
        out_full = lax.dynamic_index_in_dim(out_full, me, 1, keepdims=False)
        out_full = out_full.reshape(near * HD, width)
        gain_one, shift_one, gain_two, shift_two = [
            small[:, i * part : (i + 1) * part].reshape(width) for i in range(4)
        ]
        scaled_wide, _ = norm_stats(gather_ctx(rows, ctx).astype(f32))
        normed_one = (scaled_wide * gain_one + shift_one).astype(bf16)
        grad_wide = gather_ctx(grad_rows, ctx)
        bias = small[:, 4 * part :].reshape(3, pairs, 2, ctx, HD)
        bias = lax.dynamic_index_in_dim(bias, me, 3, keepdims=False)
        bias = bias.transpose(1, 0, 2, 3).reshape(1, near * 3 * HD)
        attended, qkv, lse = attend(dot(normed_one, joined_weight), bias, table, start)
        resid = rows.astype(f32) + scatter_ctx(dot(attended, out_full), ctx)
        scaled_two, inv_two = norm_stats(resid)
        normed_wide = gather_ctx((scaled_two * gain_two + shift_two).astype(bf16), ctx)
        gate_full = lax.all_gather(gate_weight, "dp", axis=0, tiled=True)
        up_full = lax.all_gather(up_weight, "dp", axis=0, tiled=True)
    down_full = lax.all_gather(down_weight, "dp", axis=1, tiled=True)

    gate = dot(normed_wide, gate_full)
    upward = dot(normed_wide, up_full)
    sigma = jax.nn.sigmoid(gate)
    swish = gate * sigma
    inner = (swish * upward).astype(bf16)
    d_down = dot_tn(inner, grad_wide).astype(bf16)
    grad_wide, d_down = lax.optimization_barrier((grad_wide, d_down))
    d_down = lax.psum_scatter(d_down, "dp", scatter_dimension=1, tiled=True).astype(f32)
    d_inner = dot_nt(grad_wide, down_full)
    d_gate = (d_inner * upward * sigma * (1.0 + gate * (1.0 - sigma))).astype(bf16)
    d_upward = (d_inner * swish).astype(bf16)
    d_gate_weight = dot_tn(normed_wide, d_gate).astype(bf16)
    if fused:
        d_resid, sums_two, d_proj, branch, d_up_weight, d_gate_weight = mix_back(
            dp, ctx, d_gate, d_upward, gate_full, up_full, inner, down_full, normed_wide, d_gate_weight, resid,
            grad_rows, gain_two,
        )
    else:
        d_gate_weight = lax.psum_scatter(d_gate_weight, "dp", scatter_dimension=0, tiled=True).astype(f32)
        branch = dot(inner, down_full)
        d_up_weight = dot_tn(normed_wide, d_upward).astype(bf16)
        d_normed_two = scatter_ctx(dot_nt(d_gate, gate_full) + dot_nt(d_upward, up_full), ctx)
        grad, d_gain_two, d_shift_two = norm_backward(d_normed_two, scaled_two, inv_two, gain_two)
        d_resid = grad_rows.astype(f32) + grad
        d_proj = gather_ctx(d_resid.astype(bf16), ctx)
    d_up_weight = lax.psum_scatter(d_up_weight, "dp", scatter_dimension=0, tiled=True).astype(f32)

    d_attended = dot_nt(d_proj, out_full).astype(bf16)
    d_out_weight = dot_tn(attended, d_proj).astype(bf16)
    d_attended, d_down = lax.optimization_barrier((d_attended, d_down))
    d_joined, d_bias = attend_back(qkv, d_attended, lse, table, start)
    d_joined_weight = dot_tn(normed_one, d_joined).astype(bf16)
    d_bias = d_bias.reshape(pairs, 3, 2, HD).transpose(1, 0, 2, 3)
    if fused:
        d_bias = jnp.pad(d_bias.reshape(dp, -1), ((0, 0), (0, width // dp - near * 3 * HD // dp)))
        grad_input, d_joined_weight, d_out_weight, output, vectors, d_bias = closing(
            dp, ctx, d_joined, joined_weight, d_joined_weight, d_out_weight, branch, rows, d_resid, resid,
            gain_one, sums_two, d_bias,
        )
        d_gain_one, d_shift_one, d_gain_two, d_shift_two = vectors
        d_bias = d_bias[0]
    else:
        output = (resid + scatter_ctx(branch, ctx)).astype(bf16)
        at_me = lax.broadcasted_iota(jnp.int32, (1, ctx, 1, 1), 1) == me
        d_out_weight = jnp.where(at_me, d_out_weight.reshape(near, 1, HD, width), jnp.zeros((), bf16))
        d_out_weight = lax.psum_scatter(
            d_out_weight.reshape(width, width), ("dp", "ctx"), scatter_dimension=0, tiled=True
        ).astype(f32)
        d_normed_one = scatter_ctx(dot_nt(d_joined, joined_weight), ctx)
        scaled_one, inv_one = norm_stats(rows.astype(f32))
        grad, d_gain_one, d_shift_one = norm_backward(d_normed_one, scaled_one, inv_one, gain_one)
        grad_input = d_resid + grad
        d_joined_weight = lax.psum_scatter(d_joined_weight, "dp", scatter_dimension=0, tiled=True)
        blocks = exchange_ctx(d_joined_weight.reshape(ctx, rows_here, near * 3 * HD), ctx)
        blocks = blocks.reshape(ctx, rows_here, pairs, 3, 2, HD).transpose(1, 3, 2, 4, 0, 5)
        d_joined_weight = blocks.reshape(rows_here, 3 * width).astype(f32)
        at_me = (lax.broadcasted_iota(jnp.int32, (1, 1, 1, ctx, 1), 3) == me).astype(f32)
        d_bias = (d_bias[:, :, :, None, :] * at_me).reshape(dp * ctx, -1)
        small = jnp.concatenate(
            [t.reshape(dp * ctx, part) for t in (d_gain_one, d_shift_one, d_gain_two, d_shift_two)]
            + [d_bias],
            axis=1,
        )
        small = lax.psum_scatter(small, ("dp", "ctx"), scatter_dimension=0, tiled=True)[0]
        d_gain_one, d_shift_one, d_gain_two, d_shift_two = [
            small[i * part : (i + 1) * part] for i in range(4)
        ]
        d_bias = small[4 * part :]
    return (
        output[None],
        grad_input[None],
        d_gain_one,
        d_shift_one,
        d_joined_weight,
        d_bias,
        d_out_weight,
        d_gain_two,
        d_shift_two,
        d_gate_weight,
        d_up_weight,
        d_down,
    )


def solution(mesh):
    every = ("dp", "ctx")
    return jax.shard_map(
        functools.partial(shards, mesh.shape["dp"], mesh.shape["ctx"]),
        mesh=mesh,
        in_specs=(
            P("dp", "ctx", None),
            P("dp", None),
            P(every),
            P(every),
            P(every, None),
            P(every),
            P(every, None),
            P(every),
            P(every),
            P("dp", "ctx"),
            P("dp", "ctx"),
            P("ctx", "dp"),
            P("dp", "ctx", None),
        ),
        out_specs=(
            P("dp", "ctx", None),
            P("dp", "ctx", None),
            P(every),
            P(every),
            P(every, None),
            P(every),
            P(every, None),
            P(every),
            P(every),
            P("dp", "ctx"),
            P("dp", "ctx"),
            P("ctx", "dp"),
        ),
        check_vma=False,
    )
```

```python
import functools
import math

import jax
import jax.numpy as jnp
import numpy as np
from jax import lax
from jax.experimental import pallas as pl
from jax.experimental.pallas import tpu as pltpu
from jax.sharding import PartitionSpec as P

HD = 64
ROT = 16
DOC_MAX = 512
PAIR = 2 * HD

norm_eps = 1e-05
masked_value = -1e30
f32 = jnp.float32
bf16 = jnp.bfloat16


def dot(a, b):
    return jnp.dot(a, b, preferred_element_type=f32)


def dot_nt(a, b):
    return lax.dot_general(a, b, (((1,), (1,)), ((), ())), preferred_element_type=f32)


def dot_tn(a, b):
    return lax.dot_general(a, b, (((0,), (0,)), ((), ())), preferred_element_type=f32)


def norm_stats(rows):
    row_mean = jnp.mean(rows, axis=-1, keepdims=True)
    centered = rows - row_mean
    variance = jnp.mean(centered * centered, axis=-1, keepdims=True)
    inv_std = lax.rsqrt(variance + norm_eps)
    return centered * inv_std, inv_std


def norm_backward(grad_normed, scaled, inv_std, gain):
    grad_gain = jnp.sum(grad_normed * scaled, axis=0)
    grad_shift = jnp.sum(grad_normed, axis=0)
    inner_grad = grad_normed * gain
    grad_rows = inv_std * (
        inner_grad
        - jnp.mean(inner_grad, axis=-1, keepdims=True)
        - scaled * jnp.mean(inner_grad * scaled, axis=-1, keepdims=True)
    )
    return grad_rows, grad_gain, grad_shift


def partner(n, k):
    return [(c, c ^ k) for c in range(n)]


def hop(x, n, k):
    return lax.ppermute(x, "ctx", partner(n, k))


def gather_relative(block, n):
    if n != 4:
        return [block] + [hop(block, n, k) for k in range(1, n)]
    half = block.shape[0] // 2
    one = hop(block, n, 1)
    two = hop(block, n, 2)
    low = hop(one[:half], n, 2)
    high = hop(two[half:], n, 1)
    return [block, one, two, jnp.concatenate([low, high], axis=0)]


def gather_ctx(block, n):
    me = lax.axis_index("ctx")
    size = block.shape[0]
    parts = gather_relative(block, n)
    full = jnp.zeros((n * size,) + block.shape[1:], block.dtype)
    for k, part in enumerate(parts):
        full = lax.dynamic_update_slice_in_dim(full, part, (me ^ k) * size, 0)
    return full


def scatter_ctx(partial, n):
    me = lax.axis_index("ctx")
    size = partial.shape[0] // n

    def block(k):
        return lax.dynamic_slice_in_dim(partial, (me ^ k) * size, size, 0)

    if n != 4:
        total = block(0).astype(f32)
        for k in range(1, n):
            total = total + hop(block(k).astype(bf16), n, k).astype(f32)
        return total
    half = size // 2
    far = block(3).astype(bf16)
    low = hop(far[:half], n, 1).astype(f32)
    high = hop(far[half:], n, 2).astype(f32)
    one = block(1).astype(f32)
    two = block(2).astype(f32)
    to_one = jnp.concatenate([one[:half], one[half:] + high], axis=0).astype(bf16)
    to_two = jnp.concatenate([two[:half] + low, two[half:]], axis=0).astype(bf16)
    return block(0).astype(f32) + hop(to_one, n, 1).astype(f32) + hop(to_two, n, 2).astype(f32)


def exchange_ctx(blocks, n):
    me = lax.axis_index("ctx")
    got = lax.dynamic_update_slice_in_dim(
        jnp.zeros_like(blocks), lax.dynamic_slice_in_dim(blocks, me, 1, 0), me, 0
    )
    for k in range(1, n):
        sent = lax.dynamic_slice_in_dim(blocks, me ^ k, 1, 0)
        got = lax.dynamic_update_slice_in_dim(got, hop(sent, n, k), me ^ k, 0)
    return got


MESH = pl.DeviceIdType.MESH
HBM = pl.BlockSpec(memory_space=pltpu.HBM)


class Place:
    def __init__(self, dp):
        self.row = lax.axis_index("dp")
        self.col = lax.axis_index("ctx")
        self.lines = dp // 2
        self.line = self.row // 2
        self.core = self.row % 2
        self.twin = (self.row + 1 - 2 * self.core, self.col)

    def other(self, k):
        col, bit = self.col, 1
        while bit <= k:
            if k & bit:
                col = col + bit * (1 - 2 * ((self.col // bit) % 2))
            bit *= 2
        return col

    def across(self, k):
        return (self.row, self.other(k))

    def above(self):
        return (self.row + 2, self.col)

    def below(self):
        return (self.row - 2, self.col)


def greet(place, ctx):
    barrier = pltpu.get_barrier_semaphore()
    for k in range(1, ctx):
        pl.semaphore_signal(barrier, 1, device_id=place.across(k), device_id_type=MESH)
    pl.semaphore_wait(barrier, ctx - 1)


def remote(src, dst, send, recv, device):
    return pltpu.make_async_remote_copy(
        src_ref=src, dst_ref=dst, send_sem=send, recv_sem=recv, device_id=device, device_id_type=MESH
    )


class LineGather:
    def __init__(self, place, shard, sems):
        self.place, self.shard, self.sems = place, shard, sems

    def row(self, line):
        return line * 2 + self.place.core

    def up(self, hop):
        part = self.shard(self.row(self.place.line - hop + 1))
        return remote(part, part, self.sems.at[0, hop], self.sems.at[1, hop], self.place.above())

    def down(self, hop):
        part = self.shard(self.row(self.place.line + hop - 1))
        return remote(part, part, self.sems.at[2, hop], self.sems.at[3, hop], self.place.below())

    def over(self, at, row):
        part = self.shard(row)
        return remote(part, part, self.sems.at[4, at], self.sems.at[5, at], self.place.twin)

    def sends_up(self, hop):
        return (self.place.line - hop + 1 >= 0) & (self.place.line < self.place.lines - 1)

    def sends_down(self, hop):
        return (self.place.line + hop - 1 < self.place.lines) & (self.place.line > 0)

    def send(self, hop):
        place = self.place
        pl.when(self.sends_up(hop))(lambda: self.up(hop).start())
        pl.when(self.sends_down(hop))(lambda: self.down(hop).start())
        if hop == 1:
            self.over(0, place.row).start()

    def receive(self, hop):
        place = self.place

        @pl.when(place.line - hop >= 0)
        def _():
            part = self.shard(self.row(place.line - hop))
            remote(part, part, self.sems.at[0, hop], self.sems.at[1, hop], place.twin).wait_recv()
            self.over(hop, self.row(place.line - hop)).start()

        @pl.when(place.line + hop < place.lines)
        def _():
            part = self.shard(self.row(place.line + hop))
            remote(part, part, self.sems.at[2, hop], self.sems.at[3, hop], place.twin).wait_recv()
            self.over(place.lines - 1 + hop, self.row(place.line + hop)).start()

    def came_over(self, at, row):
        part = self.shard(row)
        remote(part, part, self.sems.at[4, at], self.sems.at[5, at], self.place.twin).wait_recv()

    def settle(self, hop, use=None):
        place = self.place
        other = 1 - 2 * place.core
        if hop == 0:
            self.came_over(0, place.row + other)
            if use:
                use(place.line)
            return
        for at, line, there in (
            (hop, place.line - hop, place.line - hop >= 0),
            (place.lines - 1 + hop, place.line + hop, place.line + hop < place.lines),
        ):

            @pl.when(there)
            def _():
                self.came_over(at, self.row(line) + other)
                if use:
                    use(line)

    def finish(self):
        place = self.place
        self.over(0, place.row).wait_send()
        for hop in range(1, place.lines):
            pl.when(self.sends_up(hop))(lambda: self.up(hop).wait_send())
            pl.when(self.sends_down(hop))(lambda: self.down(hop).wait_send())
            for at, line, there in (
                (hop, place.line - hop, place.line - hop >= 0),
                (place.lines - 1 + hop, place.line + hop, place.line + hop < place.lines),
            ):
                pl.when(there)(lambda: self.over(at, self.row(line)).wait_send())

    @staticmethod
    def scratch(dp):
        return pltpu.SemaphoreType.DMA((6, dp))


class CtxGather:
    def __init__(self, place, block, full, size, sems):
        self.place, self.block, self.full, self.size, self.sems = place, block, full, size, sems

    def rows(self, col, start=0, size=None):
        size = self.size if size is None else size
        return self.full.at[pl.ds(pl.multiple_of(col * self.size + start, size), size), :]

    def copies(self):
        place, half = self.place, self.size // 2
        me = place.col
        return [
            remote(self.block, self.rows(me), self.sems.at[0, 0], self.sems.at[1, 0], place.across(1)),
            remote(self.block, self.rows(me), self.sems.at[0, 1], self.sems.at[1, 1], place.across(2)),
            remote(
                self.rows(place.other(1), 0, half), self.rows(place.other(1), 0, half),
                self.sems.at[0, 2], self.sems.at[1, 2], place.across(2),
            ),
            remote(
                self.rows(place.other(2), half, half), self.rows(place.other(2), half, half),
                self.sems.at[0, 3], self.sems.at[1, 3], place.across(1),
            ),
        ]

    def arrivals(self):
        place, half = self.place, self.size // 2
        me = place.col
        parts = [self.rows(place.other(1)), self.rows(place.other(2)), self.rows(place.other(3), 0, half), self.rows(place.other(3), half, half)]
        return [
            remote(part, part, self.sems.at[0, i], self.sems.at[1, i], place.across(1))
            for i, part in enumerate(parts)
        ]

    def first(self):
        copies = self.copies()
        copies[0].start()
        copies[1].start()

    def second(self):
        copies, arrivals = self.copies(), self.arrivals()
        arrivals[0].wait_recv()
        copies[2].start()
        arrivals[1].wait_recv()
        copies[3].start()

    def finish(self):
        copies, arrivals = self.copies(), self.arrivals()
        arrivals[2].wait_recv()
        arrivals[3].wait_recv()
        for copy in copies:
            copy.wait_send()

    @staticmethod
    def scratch():
        return pltpu.SemaphoreType.DMA((2, 4))


def greet_all(place, dp, ctx, signal=True, wait=True):
    barrier = pltpu.get_barrier_semaphore()
    if signal:
        for k in range(1, ctx):
            pl.semaphore_signal(barrier, 1, device_id=place.across(k), device_id_type=MESH)
        for k in range(1, dp):
            pl.semaphore_signal(barrier, 1, device_id=((place.row + k) % dp, place.col), device_id_type=MESH)
    if wait:
        pl.semaphore_wait(barrier, ctx + dp - 2)


CHUNKS = 4
PARTS = 2


class CtxReduce:
    def __init__(self, place, block, total, sent, got, sems):
        self.place, self.block, self.total = place, block, total
        self.sent, self.got, self.sems = sent, got, sems
        self.size = total.shape[1] // CHUNKS

    def chunk(self, j):
        return pl.ds(j * self.size, self.size)

    def copy(self, kind, j):
        way = kind if kind else 1 + j % 2
        return remote(
            self.sent.at[kind, self.chunk(j)], self.got.at[kind, self.chunk(j)],
            self.sems.at[0, kind, j], self.sems.at[1, kind, j], self.place.across(way),
        )

    def start(self):
        self.start_far()
        self.start_near()

    def start_far(self):
        self.sent[0] = self.block(self.place.other(3)).astype(bf16)
        for j in range(CHUNKS):
            self.copy(0, j).start()

    def start_near(self):
        place = self.place
        for kind in (1, 2):
            self.total[kind - 1] = self.block(place.other(kind))
            for j in range(CHUNKS):
                if kind == 1 + j % 2:
                    self.sent[kind, self.chunk(j)] = self.total[kind - 1, self.chunk(j)].astype(bf16)
                    self.copy(kind, j).start()

    def relay(self):
        for j in range(CHUNKS):
            kind = 2 - j % 2
            self.copy(0, j).wait_recv()
            share = self.total[kind - 1, self.chunk(j)] + self.got[0, self.chunk(j)].astype(f32)
            self.sent[kind, self.chunk(j)] = share.astype(bf16)
            self.copy(kind, j).start()
        self.total[0] = self.block(self.place.col)

    def sum(self, j):
        for kind in (1, 2):
            self.copy(kind, j).wait_recv()
        rows = self.chunk(j)
        return self.total[0, rows] + self.got[1, rows].astype(f32) + self.got[2, rows].astype(f32)

    def finish(self):
        for kind in range(3):
            for j in range(CHUNKS):
                self.copy(kind, j).wait_send()

    @staticmethod
    def scratch(size, width):
        return [
            pltpu.VMEM((2, size, width), f32),
            pltpu.VMEM((3, size, width), bf16),
            pltpu.VMEM((3, size, width), bf16),
            pltpu.SemaphoreType.DMA((2, 3, CHUNKS)),
        ]


class CtxSpread:
    def __init__(self, place, made, full, sems):
        self.place, self.made, self.full, self.sems = place, made, full, sems
        self.size = made.shape[0] // CHUNKS

    def rows(self, col, j):
        at = (col * CHUNKS + j) * self.size
        return self.full.at[pl.ds(pl.multiple_of(at, self.size), self.size), :]

    def copy(self, kind, j):
        place = self.place
        if kind < 2:
            part, there = self.made.at[pl.ds(j * self.size, self.size), :], self.rows(place.col, j)
            way = 1 + kind
        else:
            way = 2 - j % 2
            part = there = self.rows(place.other(3 - way), j)
        return remote(part, there, self.sems.at[0, kind, j], self.sems.at[1, kind, j], place.across(way))

    def arrived(self, kind, j):
        part = self.rows(self.place.other(kind + 1), j)
        remote(
            part, part, self.sems.at[0, kind, j], self.sems.at[1, kind, j], self.place.across(1)
        ).wait_recv()

    def local(self, j):
        part = self.made.at[pl.ds(j * self.size, self.size), :]
        return pltpu.make_async_copy(part, self.rows(self.place.col, j), self.sems.at[0, 3, j])

    def send(self, j):
        self.copy(0, j).start()
        self.copy(1, j).start()
        self.local(j).start()

    def relay(self, j):
        way = 2 - j % 2
        self.arrived(2 - way, j)
        self.copy(2, j).start()

    def finish(self):
        for j in range(CHUNKS):
            way = 2 - j % 2
            self.arrived(way - 1, j)
            self.arrived(2, j)
            self.local(j).wait()
            for kind in range(3):
                self.copy(kind, j).wait_send()

    @staticmethod
    def scratch():
        return pltpu.SemaphoreType.DMA((2, 4, CHUNKS))


def rows_of(ref, col, size):
    return ref[pl.ds(pl.multiple_of(col * size, size), size), :]


class LineReduce:
    def __init__(self, place, parts, own, pair, got, sems):
        self.place, self.parts, self.own, self.pair, self.got, self.sems = place, parts, own, pair, got, sems

    def load(self, line):
        return pltpu.make_async_copy(
            self.parts.at[2 * line + self.place.core], self.own.at[line], self.sems.at[6, line]
        )

    def swap(self, line):
        row = 2 * line + 1 - self.place.core
        return remote(
            self.parts.at[row], self.pair.at[line], self.sems.at[0, line], self.sems.at[1, line], self.place.twin
        )

    def start(self):
        for line in range(self.place.lines):
            self.swap(line).start()

    def add(self):
        for line in range(self.place.lines):
            self.load(line).wait()
            self.swap(line).wait_recv()
            self.pair[line] = (self.own[line].astype(f32) + self.pair[line].astype(f32)).astype(bf16)

    def up(self, far):
        part = self.place.line + far
        return remote(
            self.pair.at[part], self.got.at[part], self.sems.at[2, far], self.sems.at[3, far], self.place.above()
        )

    def down(self, far):
        part = self.place.line - far
        slot = part if far > 1 else self.place.lines
        return remote(
            self.pair.at[part], self.got.at[slot], self.sems.at[4, far], self.sems.at[5, far], self.place.below()
        )

    def came_up(self, far):
        slot = self.got.at[self.place.line + far]
        remote(slot, slot, self.sems.at[2, far + 1], self.sems.at[3, far + 1], self.place.twin).wait_recv()

    def came_down(self, far):
        slot = self.got.at[self.place.line - far if far else self.place.lines]
        remote(slot, slot, self.sems.at[4, far + 1], self.sems.at[5, far + 1], self.place.twin).wait_recv()

    def send(self, far):
        place = self.place

        @pl.when(place.line + far < place.lines)
        def _():
            @pl.when(place.line > 0)
            def _():
                self.came_up(far)
                part = place.line + far
                self.pair[part] = (self.pair[part].astype(f32) + self.got[part].astype(f32)).astype(bf16)

            self.up(far).start()

        @pl.when(place.line - far >= 0)
        def _():
            @pl.when(place.line < place.lines - 1)
            def _():
                self.came_down(far)
                part = place.line - far
                self.pair[part] = (self.pair[part].astype(f32) + self.got[part].astype(f32)).astype(bf16)

            self.down(far).start()

    def collect(self, out):
        place = self.place
        out[...] = self.pair[place.line].astype(f32)

        @pl.when(place.line > 0)
        def _():
            self.came_up(0)
            out[...] += self.got[place.line].astype(f32)

        @pl.when(place.line < place.lines - 1)
        def _():
            self.came_down(0)
            out[...] += self.got[place.lines].astype(f32)

    def finish(self):
        place = self.place
        for line in range(place.lines):
            self.swap(line).wait_send()
        for far in range(1, place.lines):
            pl.when(place.line + far < place.lines)(lambda: self.up(far).wait_send())
            pl.when(place.line - far >= 0)(lambda: self.down(far).wait_send())

    @staticmethod
    def scratch(dp, tile):
        return [
            pltpu.VMEM((dp // 2,) + tile, bf16),
            pltpu.VMEM((dp // 2,) + tile, bf16),
            pltpu.VMEM((dp // 2 + 1,) + tile, bf16),
            pltpu.SemaphoreType.DMA((7, dp // 2)),
        ]


def mix_back_kernel(
    dp, ctx, gate_ref, up_ref, gate_weight_hbm, up_weight_hbm, inner_hbm, down_hbm, normed_hbm, gate_parts,
    resid_ref, cot_ref, gain_ref,
    d_resid_hbm, sums_ref, wide_ref, branch_hbm, d_up_hbm, d_gate_ref,
    total, sent, got, made, gate_weight_ref, up_weight_ref, inner, down_ref, normed, branch, d_up,
    own, pair, line_got, line_sem,
    reduce_sem, spread_sem, load_sem, inner_sem, normed_sem, branch_sem, d_up_sem, d_resid_sem,
):
    place = Place(dp)
    size, width = cot_ref.shape
    cols = normed.shape[2]
    loads = [
        pltpu.make_async_copy(src, dst, load_sem.at[i])
        for i, (src, dst) in enumerate(
            ((gate_weight_hbm, gate_weight_ref), (up_weight_hbm, up_weight_ref), (down_hbm, down_ref))
        )
    ]
    for load in loads[:2]:
        load.start()
    greet_all(place, dp, ctx)
    line = LineReduce(place, gate_parts, own, pair, line_got, line_sem)
    line.start()
    for i in range(place.lines):
        line.load(i).start()
    for load in loads[:2]:
        load.wait()

    def block(col):
        return dot_nt(rows_of(gate_ref, col, size), gate_weight_ref[...]) + dot_nt(
            rows_of(up_ref, col, size), up_weight_ref[...]
        )

    d_up_count, branch_count = width // cols, ctx

    def normed_load(i):
        return pltpu.make_async_copy(
            normed_hbm.at[:, pl.ds(i * cols, cols)], normed.at[i % 2], normed_sem.at[i % 2]
        )

    def inner_load(i):
        return pltpu.make_async_copy(
            inner_hbm.at[pl.ds(i * size, size), :], inner.at[i % 2], inner_sem.at[i % 2]
        )

    def d_up_copy(i):
        return pltpu.make_async_copy(
            d_up.at[i % 2], d_up_hbm.at[pl.ds(i * cols, cols), :], d_up_sem.at[i % 2]
        )

    def branch_copy(i):
        return pltpu.make_async_copy(
            branch.at[i % 2], branch_hbm.at[pl.ds(i * size, size), :], branch_sem.at[i % 2]
        )

    def d_up_piece(i):
        normed_load(i).wait()
        if i > 1:
            d_up_copy(i - 2).wait()
        d_up[i % 2] = dot_tn(normed[i % 2], up_ref[...]).astype(bf16)
        d_up_copy(i).start()
        if i + 2 < d_up_count:
            normed_load(i + 2).start()

    def branch_piece(i):
        if i == 0:
            loads[2].wait()
        inner_load(i).wait()
        if i > 1:
            branch_copy(i - 2).wait()
        branch[i % 2] = dot(inner[i % 2], down_ref[...]).astype(bf16)
        branch_copy(i).start()
        if i + 2 < branch_count:
            inner_load(i + 2).start()

    def d_resid_copy(j):
        rows = reduce.chunk(j)
        return pltpu.make_async_copy(total.at[1, rows, :], d_resid_hbm.at[rows, :], d_resid_sem.at[j])

    pieces = [functools.partial(d_up_piece, i) for i in range(d_up_count)]
    pieces += [functools.partial(branch_piece, i) for i in range(branch_count)]

    reduce = CtxReduce(place, block, total, sent, got, reduce_sem)
    spread = CtxSpread(place, made, wide_ref, spread_sem)
    reduce.start_far()
    loads[2].start()
    for i in range(2):
        normed_load(i).start()
        inner_load(i).start()
    reduce.start_near()
    line.add()
    line.send(place.lines - 1)
    reduce.relay()
    sums_ref[...] = jnp.zeros_like(sums_ref)
    far = place.lines - 2
    for j in range(CHUNKS):
        for piece in pieces[2 * j : 2 * j + 2]:
            piece()
        rows = reduce.chunk(j)
        scaled, inv_std = norm_stats(resid_ref[rows, :])
        grad, d_gain, d_shift = norm_backward(reduce.sum(j), scaled, inv_std, gain_ref[...])
        sums_ref[0:1, :] += d_gain[None]
        sums_ref[1:2, :] += d_shift[None]
        grad = cot_ref[rows, :].astype(f32) + grad
        total[1, rows, :] = grad
        d_resid_copy(j).start()
        made[rows, :] = grad.astype(bf16)
        spread.send(j)
        if j:
            spread.relay(j - 1)
        if j % 2 == 0 and far > 0:
            line.send(far)
            far -= 1
    pieces[2 * CHUNKS]()
    spread.relay(CHUNKS - 1)
    while far > 0:
        line.send(far)
        far -= 1
    for piece in pieces[2 * CHUNKS + 1 :]:
        piece()
    spread.finish()
    line.collect(d_gate_ref)
    line.finish()
    reduce.finish()
    for i in (1, 2):
        d_up_copy(d_up_count - i).wait()
        branch_copy(branch_count - i).wait()
    for j in range(CHUNKS):
        d_resid_copy(j).wait()


def mix_back(dp, ctx, d_gate, d_up, gate_weight, up_weight, inner, down, normed, gate_parts, resid, cot, gain):
    size, width = cot.shape
    hidden = d_up.shape[1]
    own = width // dp
    cols = width // ctx // 2
    vmem = pl.BlockSpec(memory_space=pltpu.VMEM)
    return pl.pallas_call(
        functools.partial(mix_back_kernel, dp, ctx),
        in_specs=[vmem] * 2 + [HBM] * 6 + [vmem] * 3,
        out_specs=[HBM, vmem, HBM, HBM, HBM, vmem],
        out_shape=[
            jax.ShapeDtypeStruct((size, width), f32),
            jax.ShapeDtypeStruct((2, width), f32),
            jax.ShapeDtypeStruct((ctx * size, width), bf16),
            jax.ShapeDtypeStruct((ctx * size, width), bf16),
            jax.ShapeDtypeStruct((width, hidden), bf16),
            jax.ShapeDtypeStruct((own, hidden), f32),
        ],
        scratch_shapes=CtxReduce.scratch(size, width)[:3]
        + [
            pltpu.VMEM((size, width), bf16),
            pltpu.VMEM((width, hidden), bf16),
            pltpu.VMEM((width, hidden), bf16),
            pltpu.VMEM((2, size, hidden), bf16),
            pltpu.VMEM((hidden, width), bf16),
            pltpu.VMEM((2, ctx * size, cols), bf16),
            pltpu.VMEM((2, size, width), bf16),
            pltpu.VMEM((2, cols, hidden), bf16),
        ]
        + LineReduce.scratch(dp, (own, hidden))
        + [
            CtxReduce.scratch(size, width)[3],
            CtxSpread.scratch(),
            pltpu.SemaphoreType.DMA((3,)),
            pltpu.SemaphoreType.DMA((2,)),
            pltpu.SemaphoreType.DMA((2,)),
            pltpu.SemaphoreType.DMA((2,)),
            pltpu.SemaphoreType.DMA((2,)),
            pltpu.SemaphoreType.DMA((CHUNKS,)),
        ],
        compiler_params=pltpu.CompilerParams(
            collective_id=3, has_side_effects=True, vmem_limit_bytes=62 << 20
        ),
        cost_estimate=pl.CostEstimate(
            flops=8 * d_gate.size * width, transcendentals=0, bytes_accessed=180 << 20
        ),
    )(
        d_gate, d_up, gate_weight, up_weight, inner, down, normed, gate_parts.reshape(dp, own, hidden),
        resid, cot, gain.reshape(1, width),
    )


class CtxReduceReady:
    def __init__(self, place, full, have, got, sems, load_sems):
        self.place, self.full, self.have, self.got, self.sems, self.load_sems = place, full, have, got, sems, load_sems
        self.height = have.shape[1]
        self.size = self.height // CHUNKS

    def chunk(self, j):
        return pl.ds(j * self.size, self.size)

    def load(self, kind):
        col = self.place.other(kind)
        rows = pl.ds(pl.multiple_of(col * self.height, self.height), self.height)
        return pltpu.make_async_copy(self.full.at[rows, :], self.have.at[kind], self.load_sems.at[kind])

    def copy(self, kind, j):
        place = self.place
        if kind:
            part, way = self.have.at[kind, self.chunk(j)], kind
        else:
            at = (place.other(3) * CHUNKS + j) * self.size
            part, way = self.full.at[pl.ds(pl.multiple_of(at, self.size), self.size), :], 1 + j % 2
        return remote(
            part, self.got.at[kind, self.chunk(j)], self.sems.at[0, kind, j], self.sems.at[1, kind, j],
            place.across(way),
        )

    def start(self):
        for j in range(CHUNKS):
            self.copy(0, j).start()
        for kind in (1, 2):
            self.load(kind).wait()
            for j in range(CHUNKS):
                if kind == 1 + j % 2:
                    self.copy(kind, j).start()

    def relay(self):
        for j in range(CHUNKS):
            kind, rows = 2 - j % 2, self.chunk(j)
            self.copy(0, j).wait_recv()
            share = self.have[kind, rows].astype(f32) + self.got[0, rows].astype(f32)
            self.have[kind, rows] = share.astype(bf16)
            self.copy(kind, j).start()

    def sum(self, j):
        for kind in (1, 2):
            self.copy(kind, j).wait_recv()
        rows = self.chunk(j)
        return self.have[0, rows].astype(f32) + self.got[1, rows].astype(f32) + self.got[2, rows].astype(f32)

    def finish(self):
        for kind in range(3):
            for j in range(CHUNKS):
                self.copy(kind, j).wait_send()


def closing_kernel(
    dp, ctx,
    d_joined_hbm, weight_hbm, qkv_parts, out_parts, branch_hbm, rows_hbm, d_resid_hbm, resid_hbm,
    gain_ref, sums_two_ref, bias_ref,
    grad_ref, qkv_ref, out_ref, output_ref, vectors_ref, d_bias_ref,
    d_joined_ref, weight_ref, rows_ref, d_resid_ref, resid_ref, load_sem,
    total, sent, got, reduce_sem, qkv_own, qkv_pair, qkv_got, qkv_sem, out_own, out_pair, out_got, out_sem,
    have, branch_got, branch_sem, branch_load_sem,
    sums, tiles, tiles_got, small, small_sem, mine, swap_out, swap_in, swap_sem,
):
    place = Place(dp)
    me, row = place.col, place.row
    lines = [
        LineReduce(place, qkv_parts, qkv_own, qkv_pair, qkv_got, qkv_sem),
        LineReduce(place, out_parts, out_own, out_pair, out_got, out_sem),
    ]
    loads = [
        pltpu.make_async_copy(src, dst, load_sem.at[i])
        for i, (src, dst) in enumerate(
            (
                (d_joined_hbm, d_joined_ref), (weight_hbm, weight_ref), (rows_hbm, rows_ref),
                (d_resid_hbm, d_resid_ref), (resid_hbm, resid_ref),
            )
        )
    ]
    for load in loads[:2]:
        load.start()
    greet_all(place, dp, ctx)
    for line in lines:
        line.start()
    for i in range(place.lines):
        for line in lines:
            line.load(i).start()
    branch = CtxReduceReady(place, branch_hbm, have, branch_got, branch_sem, branch_load_sem)
    for kind in range(3):
        branch.load(kind).start()
    for load in loads[2:]:
        load.start()

    size, width = rows_ref.shape
    for load in loads[:2]:
        load.wait()
    reduce = CtxReduce(
        place, lambda col: dot_nt(rows_of(d_joined_ref, col, size), weight_ref[...]), total, sent, got, reduce_sem
    )
    reduce.start_far()
    for line in lines:
        line.add()
        line.send(place.lines - 1)
    reduce.start_near()
    reduce.relay()
    branch.start()
    for far in range(place.lines - 2, 1, -1):
        for line in lines:
            line.send(far)

    sums[...] = jnp.zeros_like(sums)
    for load in loads[2:]:
        load.wait()
    branch.load(0).wait()
    for j in range(CHUNKS):
        rows = reduce.chunk(j)
        scaled, inv_std = norm_stats(rows_ref[rows, :].astype(f32))
        grad, d_gain, d_shift = norm_backward(reduce.sum(j), scaled, inv_std, gain_ref[...])
        sums[0:1, :] += d_gain[None]
        sums[1:2, :] += d_shift[None]
        grad_ref[rows, :] = d_resid_ref[rows, :] + grad
    branch.relay()
    if place.lines > 2:
        for line in lines:
            line.send(1)

    part = width // dp
    tiles[...] = jnp.zeros_like(tiles)
    for i in range(dp):
        lanes = slice(i * part, (i + 1) * part)
        tiles[i, 0:2, :] = sums[:, lanes]
        tiles[i, 2:4, :] = sums_two_ref[:, lanes]
        tiles[i, 4:5, :] = bias_ref[i : i + 1, :]
    sends = [
        remote(tiles.at[(row + k) % dp], tiles_got.at[k], small_sem.at[0, k], small_sem.at[1, k], ((row + k) % dp, me))
        for k in range(1, dp)
    ]
    for copy in sends:
        copy.start()
    tile = tiles[row]
    for k in range(1, dp):
        sends[k - 1].wait()
        tile = tile + tiles_got[k]
    tiles_got[0] = tile
    small[me] = tile
    spreads = [
        remote(tiles_got.at[0], small.at[me], small_sem.at[2, k], small_sem.at[3, k], place.across(k))
        for k in range(1, ctx)
    ]
    for copy in spreads:
        copy.start()

    for j in range(CHUNKS):
        rows = branch.chunk(j)
        output_ref[rows, :] = (resid_ref[rows, :] + branch.sum(j)).astype(bf16)

    for k in range(1, ctx):
        spreads[k - 1].wait_send()
        part = small.at[place.other(k)]
        remote(part, part, small_sem.at[2, k], small_sem.at[3, k], place.across(k)).wait_recv()
    four = sum(small[c, 0:4, :] for c in range(ctx))
    piece = vectors_ref.shape[1]
    slots = d_bias_ref.shape[1] // HD
    vectors = four[:, :piece]
    biases = [small[i % ctx, 4:5, i // ctx * HD : (i // ctx + 1) * HD] for i in range(slots * ctx)]
    chosen = biases[:slots]
    for c in range(1, ctx):
        vectors = jnp.where(me == c, four[:, c * piece : (c + 1) * piece], vectors)
        chosen = [jnp.where(me == c, biases[slots * c + i], chosen[i]) for i in range(slots)]
    vectors_ref[...] = vectors
    for i in range(slots):
        d_bias_ref[:, i * HD : (i + 1) * HD] = chosen[i]

    lines[0].collect(mine)
    depth = mine.shape[0] // ctx
    swap_out[...] = mine[...].astype(bf16)
    swaps = [
        remote(
            swap_out.at[pl.ds(pl.multiple_of(place.other(k) * depth, depth), depth), :], swap_in.at[me],
            swap_sem.at[0, k], swap_sem.at[1, k], place.across(k),
        )
        for k in range(1, ctx)
    ]
    for copy in swaps:
        copy.start()
    swap_in[me] = rows_of(swap_out, me, depth)
    lines[1].collect(out_ref)
    for k in range(1, ctx):
        part = swap_in.at[place.other(k)]
        remote(part, part, swap_sem.at[0, k], swap_sem.at[1, k], place.across(k)).wait_recv()
    low = head_lanes((depth, PAIR))
    for p in range(mine.shape[1] // (3 * PAIR)):
        for t in range(3):
            lanes = slice((3 * p + t) * PAIR, (3 * p + t + 1) * PAIR)
            for c in range(0, ctx, 2):
                a = swap_in[c, :, lanes].astype(f32)
                b = swap_in[c + 1, :, lanes].astype(f32)
                at = t * width + (2 * p * ctx + c) * HD
                qkv_ref[:, at : at + PAIR] = jnp.where(low, a, pltpu.roll(b, HD, 1))
                at = at + ctx * HD
                qkv_ref[:, at : at + PAIR] = jnp.where(low, pltpu.roll(a, HD, 1), b)
    for copy in swaps:
        copy.wait_send()
    for line in lines:
        line.finish()
    branch.finish()
    reduce.finish()


def closing(dp, ctx, d_joined, weight, d_qkv, d_out, branch, rows, d_resid, resid, gain, sums_two, bias):
    size, width = rows.shape
    near = weight.shape[1]
    own, tall = width // dp, d_out.shape[0] // dp
    vmem = pl.BlockSpec(memory_space=pltpu.VMEM)
    reduce_scratch = CtxReduce.scratch(size, width)
    max_peers = max(dp, ctx)
    return pl.pallas_call(
        functools.partial(closing_kernel, dp, ctx),
        in_specs=[HBM] * 8 + [vmem] * 3,
        out_specs=[vmem] * 6,
        out_shape=[
            jax.ShapeDtypeStruct((size, width), f32),
            jax.ShapeDtypeStruct((own // ctx, 3 * width), f32),
            jax.ShapeDtypeStruct((tall, width), f32),
            jax.ShapeDtypeStruct((size, width), bf16),
            jax.ShapeDtypeStruct((4, own // ctx), f32),
            jax.ShapeDtypeStruct((1, 3 * own // ctx), f32),
        ],
        scratch_shapes=[
            pltpu.VMEM((ctx * size, near), bf16),
            pltpu.VMEM((width, near), bf16),
            pltpu.VMEM((size, width), bf16),
            pltpu.VMEM((size, width), f32),
            pltpu.VMEM((size, width), f32),
            pltpu.SemaphoreType.DMA((5,)),
        ]
        + reduce_scratch
        + LineReduce.scratch(dp, (own, near))
        + LineReduce.scratch(dp, (tall, width))
        + reduce_scratch[1:]
        + [
            pltpu.SemaphoreType.DMA((3,)),
            pltpu.VMEM((2, width), f32),
            pltpu.VMEM((dp, 8, own), f32),
            pltpu.VMEM((dp, 8, own), f32),
            pltpu.VMEM((ctx, 8, own), f32),
            pltpu.SemaphoreType.DMA((4, max_peers)),
            pltpu.VMEM((own, near), f32),
            pltpu.VMEM((own, near), bf16),
            pltpu.VMEM((ctx, own // ctx, near), bf16),
            pltpu.SemaphoreType.DMA((2, ctx)),
        ],
        compiler_params=pltpu.CompilerParams(
            collective_id=1, has_side_effects=True, vmem_limit_bytes=62 << 20
        ),
        cost_estimate=pl.CostEstimate(
            flops=2 * d_joined.size * width, transcendentals=0, bytes_accessed=200 << 20
        ),
    )(
        d_joined, weight, d_qkv.reshape(dp, own, near), d_out.reshape(dp, tall, width), branch,
        rows, d_resid, resid, gain.reshape(1, width), sums_two, bias,
    )


def turn(x, table_ref):
    return (
        x * table_ref[0]
        + pltpu.roll(x, PAIR - ROT // 2, 1) * table_ref[1]
        + pltpu.roll(x, ROT // 2, 1) * table_ref[2]
    )


def turn_back(x, table_ref):
    return (
        x * table_ref[0]
        - pltpu.roll(x, PAIR - ROT // 2, 1) * table_ref[1]
        - pltpu.roll(x, ROT // 2, 1) * table_ref[2]
    )


def head_lanes(shape):
    return lax.broadcasted_iota(jnp.int32, shape, 1) < HD


def span(full_len, step, at):
    return max(0, (at - DOC_MAX + 1) // step * step), at + step


def parts_of(low, at, step):
    return ([(low, at, False)] if low < at else []) + [(at, at + step, True)]


def masked(scores, start, first, causal):
    keys = lax.broadcasted_iota(jnp.int32, scores.shape, 1)
    allowed = keys >= start - first
    if causal:
        allowed = allowed & (keys <= lax.broadcasted_iota(jnp.int32, scores.shape, 0))
    return jnp.where(allowed, scores, masked_value)


def one_head(x, head):
    return jnp.where(head_lanes(x.shape) == (head == 0), x, jnp.zeros_like(x))


def attend_kernel(step, joined_ref, bias_ref, table_ref, start_ref, out_ref, qkv_ref, lse_ref):
    full_len = joined_ref.shape[0]
    scale = 1.0 / math.sqrt(HD)
    for t in range(3):
        lanes = slice(t * PAIR, (t + 1) * PAIR)
        x = joined_ref[:, lanes] + bias_ref[:, lanes]
        if t < 2:
            x = turn(x, table_ref)
        qkv_ref[:, lanes] = x.astype(bf16)
    for at in range(0, full_len, step):
        parts = parts_of(span(full_len, step, at)[0], at, step)
        start = start_ref[at : at + step, :1]
        q = qkv_ref[at : at + step, :PAIR] * bf16(scale)
        total = jnp.zeros((step, PAIR), f32)
        logs = []
        for head in range(2):
            qm = one_head(q, head)
            scores = [
                masked(dot_nt(qm, qkv_ref[low:high, PAIR : 2 * PAIR]), start, low, causal)
                for low, high, causal in parts
            ]
            tops = [jnp.max(s, axis=1, keepdims=True) for s in scores]
            top = functools.reduce(jnp.maximum, tops)
            norm, sums = 0.0, 0.0
            for s, (low, high, _) in zip(scores, parts):
                e = jnp.exp(s - top)
                norm = norm + jnp.sum(e, axis=1, keepdims=True)
                sums = sums + dot(e.astype(bf16), one_head(qkv_ref[low:high, 2 * PAIR :], head))
            total = total + sums * (1.0 / norm)
            logs.append(top + jnp.log(norm))
        out_ref[at : at + step, :] = total.astype(bf16)
        lse_ref[at : at + step, :] = jnp.where(head_lanes((step, PAIR)), logs[0], logs[1])


def attend_back_kernel(
    step, qkv_ref, grad_ref, lse_ref, table_ref, start_ref, out_ref, sum_ref, dk_ref, dv_ref
):
    full_len = qkv_ref.shape[0]
    scale = 1.0 / math.sqrt(HD)
    dk_ref[...] = jnp.zeros_like(dk_ref)
    dv_ref[...] = jnp.zeros_like(dv_ref)
    total = jnp.zeros((1, PAIR), f32)
    for at in range(0, full_len, step):
        rows = slice(at, at + step)
        parts = parts_of(span(full_len, step, at)[0], at, step)
        start = start_ref[rows, :1]
        q = qkv_ref[rows, :PAIR] * bf16(scale)
        g = grad_ref[rows, :]
        dq = jnp.zeros((step, PAIR), f32)
        dk = [jnp.zeros((high - low, PAIR), f32) for low, high, _ in parts]
        dv = [jnp.zeros((high - low, PAIR), f32) for low, high, _ in parts]
        for head in range(2):
            qm, gm = one_head(q, head), one_head(g, head)
            lse = lse_ref[rows, head * HD : head * HD + 1]
            probs, dps, mean = [], [], 0.0
            for low, high, causal in parts:
                s = masked(dot_nt(qm, qkv_ref[low:high, PAIR : 2 * PAIR]), start, low, causal)
                probs.append(jnp.exp(s - lse))
                dps.append(dot_nt(gm, qkv_ref[low:high, 2 * PAIR :]))
                mean = mean + jnp.sum(dps[-1] * probs[-1], axis=1, keepdims=True)
            for i, (low, high, _) in enumerate(parts):
                ds = (probs[i] * (dps[i] - mean)).astype(bf16)
                dq = dq + dot(ds, one_head(qkv_ref[low:high, PAIR : 2 * PAIR], head))
                dk[i] = dk[i] + dot_tn(ds, qm)
                dv[i] = dv[i] + dot_tn(probs[i].astype(bf16), gm)
        for i, (low, high, _) in enumerate(parts):
            dk_ref[low:high, :] += dk[i]
            dv_ref[low:high, :] += dv[i]
        dq = turn_back(dq * scale, table_ref.at[:, rows, :]).astype(bf16)
        out_ref[rows, :PAIR] = dq
        total = total + jnp.sum(dq.astype(f32), axis=0, keepdims=True)
    sum_ref[:, :PAIR] = total
    dk = turn_back(dk_ref[...], table_ref).astype(bf16)
    out_ref[:, PAIR : 2 * PAIR] = dk
    sum_ref[:, PAIR : 2 * PAIR] = jnp.sum(dk.astype(f32), axis=0, keepdims=True)
    dv = dv_ref[...].astype(bf16)
    out_ref[:, 2 * PAIR :] = dv
    sum_ref[:, 2 * PAIR :] = jnp.sum(dv.astype(f32), axis=0, keepdims=True)


def whole(shape):
    return pl.BlockSpec(shape, lambda p: (0,) * len(shape))


def attend_step(full_len):
    return min(256, full_len)


def attend(joined, bias, table, start):
    full_len, width = joined.shape
    pairs = width // (3 * PAIR)
    step = attend_step(full_len)
    seen = sum(span(full_len, step, at)[1] - span(full_len, step, at)[0] for at in range(0, full_len, step)) * step
    wide = pl.BlockSpec((full_len, 3 * PAIR), lambda p: (0, p))
    thin = pl.BlockSpec((full_len, PAIR), lambda p: (0, p))
    return pl.pallas_call(
        functools.partial(attend_kernel, step),
        grid=(pairs,),
        in_specs=[
            wide,
            pl.BlockSpec((1, 3 * PAIR), lambda p: (0, p)),
            whole(table.shape),
            whole(start.shape),
        ],
        out_specs=[thin, wide, thin],
        out_shape=[
            jax.ShapeDtypeStruct((full_len, pairs * PAIR), bf16),
            jax.ShapeDtypeStruct((full_len, width), bf16),
            jax.ShapeDtypeStruct((full_len, pairs * PAIR), f32),
        ],
        compiler_params=pltpu.CompilerParams(vmem_limit_bytes=40 << 20),
        cost_estimate=pl.CostEstimate(
            flops=pairs * seen * PAIR * 8, transcendentals=pairs * seen * 2, bytes_accessed=full_len * width * 8
        ),
    )(joined, bias, table, start)


def attend_back(qkv, grad, lse, table, start):
    full_len, width = qkv.shape
    pairs = width // (3 * PAIR)
    step = attend_step(full_len)
    seen = sum(span(full_len, step, at)[1] - span(full_len, step, at)[0] for at in range(0, full_len, step)) * step
    wide = pl.BlockSpec((full_len, 3 * PAIR), lambda p: (0, p))
    thin = pl.BlockSpec((full_len, PAIR), lambda p: (0, p))
    return pl.pallas_call(
        functools.partial(attend_back_kernel, step),
        grid=(pairs,),
        in_specs=[wide, thin, thin, whole(table.shape), whole(start.shape)],
        out_specs=[wide, pl.BlockSpec((1, 3 * PAIR), lambda p: (0, p))],
        out_shape=[
            jax.ShapeDtypeStruct((full_len, width), bf16),
            jax.ShapeDtypeStruct((1, width), f32),
        ],
        scratch_shapes=[pltpu.VMEM((full_len, PAIR), f32), pltpu.VMEM((full_len, PAIR), f32)],
        compiler_params=pltpu.CompilerParams(vmem_limit_bytes=40 << 20),
        cost_estimate=pl.CostEstimate(
            flops=pairs * seen * PAIR * 20, transcendentals=pairs * seen * 2, bytes_accessed=full_len * width * 8
        ),
    )(*[pltpu.with_memory_space_constraint(x, pltpu.HBM) for x in (qkv, grad, lse, table, start)])


def forward_kernel(
    dp, ctx, step,
    gain_one, shift_one, gain_two, shift_two, bias, start_ref, table_hbm,
    qkv_hbm, out_weight_ref, rows_ref, cot_ref, gate_hbm, up_hbm,
    params_ref, weight_hbm, out_hbm, normed_hbm, cot_all, attended_hbm, heads_hbm, lse_hbm, resid_hbm, wide_ref,
    gate_all, up_all,
    small_all, table_ref, small_ref, qkv_ref, blocks, rows_all, weight_ref, normed_ref, joined_ref, bias_ref, out_all,
    attended_ref, heads_ref, lse_ref, total, sent, got, made, resid_ref,
    normed_sem, weight_sem, local_sem, swap_sem, small_sem, line_joined, line_out, line_gate, line_up, rows_sem, cot_sem,
    late_sem, reduce_sem, spread_sem, resid_sem,
):
    place = Place(dp)
    me, row = place.col, place.row
    depth = qkv_ref.shape[0]
    length, width = rows_ref.shape
    rows_out = out_weight_ref.shape[0]
    tall = ctx * depth

    qkv_copy = pltpu.make_async_copy(qkv_hbm, qkv_ref, local_sem.at[4])
    qkv_copy.start()
    table_copy = pltpu.make_async_copy(table_hbm, table_ref, late_sem.at[0])
    table_copy.start()
    greet_all(place, dp, ctx, wait=False)
    small_ref[...] = jnp.zeros_like(small_ref)
    for i, vector in enumerate((gain_one, shift_one, gain_two, shift_two)):
        small_ref[i // 2 : i // 2 + 1, i % 2 * HD : (i % 2 + 1) * HD] = vector[...].astype(f32)
    for i in range(bias.shape[1] // HD):
        small_ref[2 + i // 2 : 3 + i // 2, i % 2 * HD : (i % 2 + 1) * HD] = bias[
            :, i * HD : (i + 1) * HD
        ].astype(f32)
    small_all[row, me] = small_ref[...]
    qkv_copy.wait()

    low = head_lanes((depth, PAIR))
    for p in range(width // HD // ctx // 2):
        for t in range(3):
            lanes = slice((3 * p + t) * PAIR, (3 * p + t + 1) * PAIR)
            for c in range(0, ctx, 2):
                at = t * width + (2 * p * ctx + c) * HD
                a = qkv_ref[:, at : at + PAIR].astype(f32)
                at = at + ctx * HD
                b = qkv_ref[:, at : at + PAIR].astype(f32)
                blocks[c, :, lanes] = jnp.where(low, a, pltpu.roll(b, HD, 1)).astype(bf16)
                blocks[c + 1, :, lanes] = jnp.where(low, pltpu.roll(a, HD, 1), b).astype(bf16)
    greet_all(place, dp, ctx, signal=False)

    def weight_rows(row, col):
        return weight_ref.at[pl.ds(pl.multiple_of((row * ctx + col) * depth, depth), depth), :]

    def out_shard(row):
        return out_all.at[pl.ds(pl.multiple_of(row * rows_out, rows_out), rows_out), :]

    def block(ref, col):
        return ref.at[pl.ds(pl.multiple_of(col * length, length), length), :]

    part_cols = weight_ref.shape[1] // PARTS

    def weight_part(i, row):
        return weight_ref.at[
            pl.ds(pl.multiple_of(row * tall, tall), tall), pl.ds(i * part_cols, part_cols)
        ]

    local = [
        pltpu.make_async_copy(blocks.at[me], weight_rows(row, me), local_sem.at[0]),
        pltpu.make_async_copy(out_weight_ref, out_shard(row), local_sem.at[1]),
        pltpu.make_async_copy(rows_ref, block(rows_all, me), local_sem.at[2]),
        pltpu.make_async_copy(cot_ref, block(cot_all, me), local_sem.at[3]),
    ]
    swaps = [
        remote(small_ref, small_all.at[row, me], swap_sem.at[0, k], swap_sem.at[1, k], place.across(k))
        for k in range(1, ctx)
    ] + [
        remote(
            blocks.at[place.other(k)], weight_rows(row, me), swap_sem.at[2, k], swap_sem.at[3, k], place.across(k)
        )
        for k in range(1, ctx)
    ]
    for copy in swaps:
        copy.start()
    for copy in local:
        copy.start()

    def gate_shard(row):
        tall = gate_hbm.shape[0]
        return gate_all.at[pl.ds(pl.multiple_of(row * tall, tall), tall), :]

    def up_shard(row):
        tall = up_hbm.shape[0]
        return up_all.at[pl.ds(pl.multiple_of(row * tall, tall), tall), :]

    gate_line, up_line = LineGather(place, gate_shard, line_gate), LineGather(place, up_shard, line_up)
    late = [
        pltpu.make_async_copy(gate_hbm, gate_shard(row), late_sem.at[1]),
        pltpu.make_async_copy(up_hbm, up_shard(row), late_sem.at[2]),
    ]
    for copy in late:
        copy.start()
    rows_gather = CtxGather(place, rows_ref, rows_all, length, rows_sem)
    cot_gather = CtxGather(place, cot_ref, cot_all, length, cot_sem)
    out_line = LineGather(place, out_shard, line_out)
    lines = [
        LineGather(place, functools.partial(weight_part, i), line_joined.at[i]) for i in range(PARTS)
    ] + [out_line]
    local[1].wait()
    out_line.send(1)
    rows_gather.first()
    for k in range(1, ctx):
        remote(
            small_ref, small_all.at[row, place.other(k)], swap_sem.at[0, k], swap_sem.at[1, k], place.across(k)
        ).wait_recv()
    small_sends = [
        remote(
            small_all.at[row], small_all.at[row], small_sem.at[0, k], small_sem.at[1, k], ((row + k) % dp, me)
        )
        for k in range(1, dp)
    ]
    for copy in small_sends:
        copy.start()
    local[0].wait()
    for k in range(1, ctx):
        part = weight_rows(row, place.other(k))
        remote(part, part, swap_sem.at[2, k], swap_sem.at[3, k], place.across(k)).wait_recv()
    for line in lines[:PARTS]:
        line.send(1)

    for k in range(1, dp):
        part = small_all.at[(row + dp - k) % dp]
        remote(part, part, small_sem.at[0, k], small_sem.at[1, k], place.twin).wait_recv()
    low = head_lanes((1, PAIR))
    for i in range(dp * ctx // 2):
        lanes = slice(i * PAIR, (i + 1) * PAIR)
        a = small_all[2 * i // ctx, 2 * i % ctx]
        b = small_all[(2 * i + 1) // ctx, (2 * i + 1) % ctx]
        for r in range(2):
            ar, br = a[r : r + 1, :], b[r : r + 1, :]
            params_ref[2 * r : 2 * r + 1, lanes] = jnp.where(low, ar, pltpu.roll(br, HD, 1))
            params_ref[2 * r + 1 : 2 * r + 2, lanes] = jnp.where(low, pltpu.roll(ar, HD, 1), br)

    def normalize(col):
        step = 64

        @pl.loop(0, length // step)
        def _(i):
            rows = pl.ds(pl.multiple_of(col * length + i * step, step), step)
            scaled, _ = norm_stats(rows_all[rows, :].astype(f32))
            normed_ref[rows, :] = (scaled * params_ref[0:1, :] + params_ref[1:2, :]).astype(bf16)

        normed_copy(col).start()

    def normed_copy(col):
        return pltpu.make_async_copy(block(normed_ref, col), block(normed_hbm, col), normed_sem.at[col])

    def weight_copy(i, line):
        part = (
            pl.ds(pl.multiple_of(line * (2 * tall), 2 * tall), 2 * tall),
            pl.ds(i * part_cols, part_cols),
        )
        return pltpu.make_async_copy(weight_ref.at[part], weight_hbm.at[part], weight_sem.at[i, line])

    def multiply(i, line):
        weight_copy(i, line).start()
        at = pl.multiple_of(line * (2 * tall), 2 * tall)
        cols = slice(i * part_cols, (i + 1) * part_cols)

        @pl.loop(0, ctx)
        def _(b):
            rows = pl.ds(pl.multiple_of(b * length, length), length)
            joined_ref[rows, cols] += dot(
                normed_ref[rows, pl.ds(at, 2 * tall)], weight_ref[pl.ds(at, 2 * tall), cols]
            )

    def forward(hop):
        for line in lines:
            line.receive(hop)
            if hop < place.lines - 1:
                line.send(hop + 1)

    def absorb(hop):
        for i in range(PARTS):
            lines[i].settle(hop, functools.partial(multiply, i))

    joined_ref[...] = jnp.zeros_like(joined_ref)
    local[2].wait()
    normalize(me)
    rows_gather.second()
    cot_gather.first()
    for hop in range(1, place.lines):
        forward(hop)
        if hop == 1:
            for col in (place.other(1), place.other(2)):
                normalize(col)
            rows_gather.finish()
            normalize(place.other(3))
        if hop == min(2, place.lines - 1):
            cot_gather.second()
        absorb(hop - 1)
    late[0].wait()
    gate_line.send(1)
    absorb(place.lines - 1)
    late[1].wait()

    low = head_lanes((1, PAIR))
    pairs = joined_ref.shape[1] // (3 * PAIR)
    per_device = bias.shape[1] // HD
    for p in range(pairs):
        for t in range(3):
            chosen = [None, None]
            for c in range(ctx):
                for half in range(2):
                    slot = t * (width // HD) + (2 * p + half) * ctx + c
                    owner, at = slot // per_device, slot % per_device
                    piece = small_all[owner // ctx, owner % ctx, 2 + at // 2 : 3 + at // 2, :]
                    if at % 2 != half:
                        piece = pltpu.roll(piece, HD, 1)
                    chosen[half] = piece if c == 0 else jnp.where(me == c, piece, chosen[half])
            lanes = slice((3 * p + t) * PAIR, (3 * p + t + 1) * PAIR)
            bias_ref[:, lanes] = jnp.where(low, chosen[0], chosen[1])

    def heads_copies():
        return [
            pltpu.make_async_copy(attended_ref, attended_hbm, late_sem.at[3]),
            pltpu.make_async_copy(heads_ref, heads_hbm, late_sem.at[4]),
            pltpu.make_async_copy(lse_ref, lse_hbm, late_sem.at[5]),
            pltpu.make_async_copy(out_all, out_hbm, late_sem.at[6]),
        ]

    def attend_pairs(first, last):
        @pl.loop(first, last)
        def _(p):
            wide = pl.ds(pl.multiple_of(p * (3 * PAIR), 3 * PAIR), 3 * PAIR)
            thin = pl.ds(pl.multiple_of(p * PAIR, PAIR), PAIR)
            attend_kernel(
                step, joined_ref.at[:, wide], bias_ref.at[:, wide], table_ref, start_ref,
                attended_ref.at[:, thin], heads_ref.at[:, wide], lse_ref.at[:, thin],
            )

    def pass_on(line, hop):
        line.receive(hop)
        if hop < place.lines - 1:
            line.send(hop + 1)

    table_copy.wait()
    up_line.send(1)
    attend_pairs(0, pairs // 2)
    if place.lines > 1:
        pass_on(gate_line, 1)
    attend_pairs(pairs // 2, pairs)
    for hop in range(place.lines):
        out_line.settle(hop)
    for line in lines:
        line.finish()
    cot_gather.finish()
    for copy in heads_copies():
        copy.start()

    reduce = CtxReduce(
        place, lambda col: dot(rows_of(attended_ref, col, length), out_all[...]), total, sent, got, reduce_sem
    )
    spread = CtxSpread(place, made, wide_ref, spread_sem)

    def resid_copy(j):
        rows = reduce.chunk(j)
        return pltpu.make_async_copy(resid_ref.at[rows, :], resid_hbm.at[rows, :], resid_sem.at[j])

    reduce.start()
    reduce.relay()
    if place.lines > 2:
        pass_on(gate_line, 2)
    for j in range(CHUNKS):
        rows = reduce.chunk(j)
        at = pl.multiple_of(me * length + j * reduce.size, reduce.size)
        resid = rows_all[pl.ds(at, reduce.size), :].astype(f32) + reduce.sum(j)
        resid_ref[rows, :] = resid
        resid_copy(j).start()
        scaled, _ = norm_stats(resid)
        made[rows, :] = (scaled * params_ref[2:3, :] + params_ref[3:4, :]).astype(bf16)
        spread.send(j)
        if j:
            spread.relay(j - 1)
        if j == 0 and place.lines > 1:
            pass_on(up_line, 1)
        if j == 3 and place.lines > 2:
            pass_on(up_line, 2)
    spread.relay(CHUNKS - 1)
    for hop in range(3, place.lines):
        pass_on(gate_line, hop)
    for hop in range(3, place.lines):
        pass_on(up_line, hop)
    spread.finish()
    for line in (gate_line, up_line):
        for hop in range(place.lines):
            line.settle(hop)
        line.finish()
    reduce.finish()
    for copy in swaps + small_sends:
        copy.wait_send()
    local[3].wait()
    for col in range(ctx):
        normed_copy(col).wait()
    for line in range(place.lines):
        for i in range(PARTS):
            weight_copy(i, line).wait()
    for j in range(CHUNKS):
        resid_copy(j).wait()
    for copy in heads_copies():
        copy.wait()


def forward(dp, ctx, vectors, start, table, qkv_weight, out_weight, rows, cot, gate_weight, up_weight):
    depth, width = qkv_weight.shape[0], rows.shape[1]
    length = rows.shape[0]
    full_len = ctx * length
    near = 3 * width // ctx
    thin = near // 3
    hidden = gate_weight.shape[1]
    vmem = pl.BlockSpec(memory_space=pltpu.VMEM)
    reduce_scratch = CtxReduce.scratch(length, width)
    return pl.pallas_call(
        functools.partial(forward_kernel, dp, ctx, attend_step(full_len)),
        in_specs=[vmem] * (len(vectors) + 1) + [HBM] * 7,
        out_specs=[vmem] + [HBM] * 11,
        out_shape=[
            jax.ShapeDtypeStruct((4, width), f32),
            jax.ShapeDtypeStruct((dp * ctx * depth, near), bf16),
            jax.ShapeDtypeStruct((dp * out_weight.shape[0], width), bf16),
            jax.ShapeDtypeStruct((full_len, width), bf16),
            jax.ShapeDtypeStruct((full_len, width), bf16),
            jax.ShapeDtypeStruct((full_len, thin), bf16),
            jax.ShapeDtypeStruct((full_len, near), bf16),
            jax.ShapeDtypeStruct((full_len, thin), f32),
            jax.ShapeDtypeStruct((length, width), f32),
            jax.ShapeDtypeStruct((full_len, width), bf16),
            jax.ShapeDtypeStruct((dp * gate_weight.shape[0], hidden), bf16),
            jax.ShapeDtypeStruct((dp * up_weight.shape[0], hidden), bf16),
        ],
        scratch_shapes=[
            pltpu.VMEM((dp, ctx, 8, PAIR), f32),
            pltpu.VMEM(table.shape, f32),
            pltpu.VMEM((8, PAIR), f32),
            pltpu.VMEM((depth, 3 * width), bf16),
            pltpu.VMEM((ctx, depth, near), bf16),
            pltpu.VMEM((full_len, width), bf16),
            pltpu.VMEM((dp * ctx * depth, near), bf16),
            pltpu.VMEM((full_len, width), bf16),
            pltpu.VMEM((full_len, near), f32),
            pltpu.VMEM((1, near), f32),
            pltpu.VMEM((dp * out_weight.shape[0], width), bf16),
            pltpu.VMEM((full_len, thin), bf16),
            pltpu.VMEM((full_len, near), bf16),
            pltpu.VMEM((full_len, thin), f32),
        ]
        + reduce_scratch[:3]
        + [
            pltpu.VMEM((length, width), bf16),
            pltpu.VMEM((length, width), f32),
            pltpu.SemaphoreType.DMA((ctx,)),
            pltpu.SemaphoreType.DMA((PARTS, dp // 2)),
            pltpu.SemaphoreType.DMA((5,)),
            pltpu.SemaphoreType.DMA((4, ctx)),
            pltpu.SemaphoreType.DMA((2, dp)),
            pltpu.SemaphoreType.DMA((PARTS, 6, dp)),
            LineGather.scratch(dp),
            LineGather.scratch(dp),
            LineGather.scratch(dp),
            CtxGather.scratch(),
            CtxGather.scratch(),
            pltpu.SemaphoreType.DMA((7,)),
            reduce_scratch[3],
            CtxSpread.scratch(),
            pltpu.SemaphoreType.DMA((CHUNKS,)),
        ],
        compiler_params=pltpu.CompilerParams(
            collective_id=0, has_side_effects=True, vmem_limit_bytes=62 << 20
        ),
        cost_estimate=pl.CostEstimate(
            flops=2 * full_len * width * near, transcendentals=0, bytes_accessed=400 << 20
        ),
    )(*vectors, start, table, qkv_weight, out_weight, rows, cot, gate_weight, up_weight)


def rotary_table(full_len):
    half = ROT // 2
    inverse = 10000.0 ** (-2.0 * np.arange(half) / ROT)
    angles = np.arange(full_len)[:, None] * inverse[None, :]
    table = np.zeros((3, full_len, HD), np.float32)
    table[0, :, :half] = table[0, :, half:ROT] = np.cos(angles)
    table[0, :, ROT:] = 1.0
    table[1, :, :half] = -np.sin(angles)
    table[2, :, half:ROT] = np.sin(angles)
    return jnp.asarray(np.concatenate([table, table], axis=2))


def shards(
    dp,
    ctx,
    inputs,
    segments,
    ln1_gain,
    ln1_bias,
    qkv_weight,
    qkv_bias,
    out_weight,
    ln2_gain,
    ln2_bias,
    gate_weight,
    up_weight,
    down_weight,
    cotangent,
):
    local_len, width = inputs.shape[1], inputs.shape[2]
    full_len = segments.shape[1]
    heads = width // HD
    near = heads // ctx
    pairs = near // 2
    me = lax.axis_index("ctx")
    own = me * local_len

    segment = segments[0]
    start = jnp.sum((segment[None, :] < segment[:, None]).astype(jnp.int32), axis=1)
    start = jnp.broadcast_to(start[:, None], (full_len, 128))
    table = rotary_table(full_len)
    part = ln1_gain.shape[0]
    vectors = [v[None, :] for v in (ln1_gain, ln1_bias, ln2_gain, ln2_bias, qkv_bias)]
    rows_here = qkv_weight.shape[0]
    rows, grad_rows = inputs[0], cotangent[0]
    fused = ctx == 4 and dp % 2 == 0 and part == HD
    if fused:
        (
            params, joined_weight, out_full, normed_one, grad_wide, attended, qkv, lse, resid, normed_wide,
            gate_full, up_full,
        ) = forward(
            dp, ctx, vectors, start, table, qkv_weight, out_weight, rows, grad_rows, gate_weight, up_weight
        )
        gain_one, _, gain_two, _ = params
        down_weight, _ = lax.optimization_barrier((down_weight, normed_wide))
    else:
        small = jnp.concatenate(vectors, axis=1).astype(f32)
        small = lax.all_gather(small, ("dp", "ctx"), axis=0, tiled=True)
        blocks = qkv_weight.reshape(rows_here, 3, pairs, 2, ctx, HD).transpose(4, 0, 2, 1, 3, 5)
        blocks = exchange_ctx(blocks.reshape(ctx, rows_here, near * 3 * HD), ctx)
        joined_weight = lax.all_gather(
            blocks.reshape(ctx * rows_here, near * 3 * HD), "dp", axis=0, tiled=True
        )
        out_full = lax.all_gather(out_weight, ("dp", "ctx"), axis=0, tiled=True)
        out_full = out_full.reshape(near, ctx, HD, width)
        out_full = lax.dynamic_index_in_dim(out_full, me, 1, keepdims=False)
        out_full = out_full.reshape(near * HD, width)
        gain_one, shift_one, gain_two, shift_two = [
            small[:, i * part : (i + 1) * part].reshape(width) for i in range(4)
        ]
        scaled_wide, _ = norm_stats(gather_ctx(rows, ctx).astype(f32))
        normed_one = (scaled_wide * gain_one + shift_one).astype(bf16)
        grad_wide = gather_ctx(grad_rows, ctx)
        bias = small[:, 4 * part :].reshape(3, pairs, 2, ctx, HD)
        bias = lax.dynamic_index_in_dim(bias, me, 3, keepdims=False)
        bias = bias.transpose(1, 0, 2, 3).reshape(1, near * 3 * HD)
        attended, qkv, lse = attend(dot(normed_one, joined_weight), bias, table, start)
        resid = rows.astype(f32) + scatter_ctx(dot(attended, out_full), ctx)
        scaled_two, inv_two = norm_stats(resid)
        normed_wide = gather_ctx((scaled_two * gain_two + shift_two).astype(bf16), ctx)
        gate_full = lax.all_gather(gate_weight, "dp", axis=0, tiled=True)
        up_full = lax.all_gather(up_weight, "dp", axis=0, tiled=True)
    down_full = lax.all_gather(down_weight, "dp", axis=1, tiled=True)

    gate = dot(normed_wide, gate_full)
    upward = dot(normed_wide, up_full)
    sigma = jax.nn.sigmoid(gate)
    swish = gate * sigma
    inner = (swish * upward).astype(bf16)
    d_down = dot_tn(inner, grad_wide).astype(bf16)
    grad_wide, d_down = lax.optimization_barrier((grad_wide, d_down))
    d_down = lax.psum_scatter(d_down, "dp", scatter_dimension=1, tiled=True).astype(f32)
    d_inner = dot_nt(grad_wide, down_full)
    d_gate = (d_inner * upward * sigma * (1.0 + gate * (1.0 - sigma))).astype(bf16)
    d_upward = (d_inner * swish).astype(bf16)
    d_gate_weight = dot_tn(normed_wide, d_gate).astype(bf16)
    if fused:
        d_resid, sums_two, d_proj, branch, d_up_weight, d_gate_weight = mix_back(
            dp, ctx, d_gate, d_upward, gate_full, up_full, inner, down_full, normed_wide, d_gate_weight, resid,
            grad_rows, gain_two,
        )
    else:
        d_gate_weight = lax.psum_scatter(d_gate_weight, "dp", scatter_dimension=0, tiled=True).astype(f32)
        branch = dot(inner, down_full)
        d_up_weight = dot_tn(normed_wide, d_upward).astype(bf16)
        d_normed_two = scatter_ctx(dot_nt(d_gate, gate_full) + dot_nt(d_upward, up_full), ctx)
        grad, d_gain_two, d_shift_two = norm_backward(d_normed_two, scaled_two, inv_two, gain_two)
        d_resid = grad_rows.astype(f32) + grad
        d_proj = gather_ctx(d_resid.astype(bf16), ctx)
    d_up_weight = lax.psum_scatter(d_up_weight, "dp", scatter_dimension=0, tiled=True).astype(f32)

    d_attended = dot_nt(d_proj, out_full).astype(bf16)
    d_out_weight = dot_tn(attended, d_proj).astype(bf16)
    d_attended, d_down = lax.optimization_barrier((d_attended, d_down))
    d_joined, d_bias = attend_back(qkv, d_attended, lse, table, start)
    d_joined_weight = dot_tn(normed_one, d_joined).astype(bf16)
    d_bias = d_bias.reshape(pairs, 3, 2, HD).transpose(1, 0, 2, 3)
    if fused:
        d_bias = jnp.pad(d_bias.reshape(dp, -1), ((0, 0), (0, width // dp - near * 3 * HD // dp)))
        grad_input, d_joined_weight, d_out_weight, output, vectors, d_bias = closing(
            dp, ctx, d_joined, joined_weight, d_joined_weight, d_out_weight, branch, rows, d_resid, resid,
            gain_one, sums_two, d_bias,
        )
        d_gain_one, d_shift_one, d_gain_two, d_shift_two = vectors
        d_bias = d_bias[0]
    else:
        output = (resid + scatter_ctx(branch, ctx)).astype(bf16)
        at_me = lax.broadcasted_iota(jnp.int32, (1, ctx, 1, 1), 1) == me
        d_out_weight = jnp.where(at_me, d_out_weight.reshape(near, 1, HD, width), jnp.zeros((), bf16))
        d_out_weight = lax.psum_scatter(
            d_out_weight.reshape(width, width), ("dp", "ctx"), scatter_dimension=0, tiled=True
        ).astype(f32)
        d_normed_one = scatter_ctx(dot_nt(d_joined, joined_weight), ctx)
        scaled_one, inv_one = norm_stats(rows.astype(f32))
        grad, d_gain_one, d_shift_one = norm_backward(d_normed_one, scaled_one, inv_one, gain_one)
        grad_input = d_resid + grad
        d_joined_weight = lax.psum_scatter(d_joined_weight, "dp", scatter_dimension=0, tiled=True)
        blocks = exchange_ctx(d_joined_weight.reshape(ctx, rows_here, near * 3 * HD), ctx)
        blocks = blocks.reshape(ctx, rows_here, pairs, 3, 2, HD).transpose(1, 3, 2, 4, 0, 5)
        d_joined_weight = blocks.reshape(rows_here, 3 * width).astype(f32)
        at_me = (lax.broadcasted_iota(jnp.int32, (1, 1, 1, ctx, 1), 3) == me).astype(f32)
        d_bias = (d_bias[:, :, :, None, :] * at_me).reshape(dp * ctx, -1)
        small = jnp.concatenate(
            [t.reshape(dp * ctx, part) for t in (d_gain_one, d_shift_one, d_gain_two, d_shift_two)]
            + [d_bias],
            axis=1,
        )
        small = lax.psum_scatter(small, ("dp", "ctx"), scatter_dimension=0, tiled=True)[0]
        d_gain_one, d_shift_one, d_gain_two, d_shift_two = [
            small[i * part : (i + 1) * part] for i in range(4)
        ]
        d_bias = small[4 * part :]
    return (
        output[None],
        grad_input[None],
        d_gain_one,
        d_shift_one,
        d_joined_weight,
        d_bias,
        d_out_weight,
        d_gain_two,
        d_shift_two,
        d_gate_weight,
        d_up_weight,
        d_down,
    )


def solution(mesh):
    every = ("dp", "ctx")
    return jax.shard_map(
        functools.partial(shards, mesh.shape["dp"], mesh.shape["ctx"]),
        mesh=mesh,
        in_specs=(
            P("dp", "ctx", None),
            P("dp", None),
            P(every),
            P(every),
            P(every, None),
            P(every),
            P(every, None),
            P(every),
            P(every),
            P("dp", "ctx"),
            P("dp", "ctx"),
            P("ctx", "dp"),
            P("dp", "ctx", None),
        ),
        out_specs=(
            P("dp", "ctx", None),
            P("dp", "ctx", None),
            P(every),
            P(every),
            P(every, None),
            P(every),
            P(every, None),
            P(every),
            P(every),
            P("dp", "ctx"),
            P("dp", "ctx"),
            P("ctx", "dp"),
        ),
        check_vma=False,
    )
```

```python
import functools
import math

import jax
import jax.numpy as jnp
import numpy as np
from jax import lax
from jax.experimental import pallas as pl
from jax.experimental.pallas import tpu as pltpu
from jax.sharding import PartitionSpec as P

HD = 64
ROT = 16
DOC_MAX = 512
PAIR = 2 * HD

norm_eps = 1e-05
masked_value = -1e30
f32 = jnp.float32
bf16 = jnp.bfloat16


def dot(a, b):
    return jnp.dot(a, b, preferred_element_type=f32)


def dot_nt(a, b):
    return lax.dot_general(a, b, (((1,), (1,)), ((), ())), preferred_element_type=f32)


def dot_tn(a, b):
    return lax.dot_general(a, b, (((0,), (0,)), ((), ())), preferred_element_type=f32)


def norm_stats(rows):
    row_mean = jnp.mean(rows, axis=-1, keepdims=True)
    centered = rows - row_mean
    variance = jnp.mean(centered * centered, axis=-1, keepdims=True)
    inv_std = lax.rsqrt(variance + norm_eps)
    return centered * inv_std, inv_std


def norm_backward(grad_normed, scaled, inv_std, gain):
    grad_gain = jnp.sum(grad_normed * scaled, axis=0)
    grad_shift = jnp.sum(grad_normed, axis=0)
    inner_grad = grad_normed * gain
    grad_rows = inv_std * (
        inner_grad
        - jnp.mean(inner_grad, axis=-1, keepdims=True)
        - scaled * jnp.mean(inner_grad * scaled, axis=-1, keepdims=True)
    )
    return grad_rows, grad_gain, grad_shift


def partner(n, k):
    return [(c, c ^ k) for c in range(n)]


def hop(x, n, k):
    return lax.ppermute(x, "ctx", partner(n, k))


def gather_relative(block, n):
    if n != 4:
        return [block] + [hop(block, n, k) for k in range(1, n)]
    half = block.shape[0] // 2
    one = hop(block, n, 1)
    two = hop(block, n, 2)
    low = hop(one[:half], n, 2)
    high = hop(two[half:], n, 1)
    return [block, one, two, jnp.concatenate([low, high], axis=0)]


def gather_ctx(block, n):
    me = lax.axis_index("ctx")
    size = block.shape[0]
    parts = gather_relative(block, n)
    full = jnp.zeros((n * size,) + block.shape[1:], block.dtype)
    for k, part in enumerate(parts):
        full = lax.dynamic_update_slice_in_dim(full, part, (me ^ k) * size, 0)
    return full


def scatter_ctx(partial, n):
    me = lax.axis_index("ctx")
    size = partial.shape[0] // n

    def block(k):
        return lax.dynamic_slice_in_dim(partial, (me ^ k) * size, size, 0)

    if n != 4:
        total = block(0).astype(f32)
        for k in range(1, n):
            total = total + hop(block(k).astype(bf16), n, k).astype(f32)
        return total
    half = size // 2
    far = block(3).astype(bf16)
    low = hop(far[:half], n, 1).astype(f32)
    high = hop(far[half:], n, 2).astype(f32)
    one = block(1).astype(f32)
    two = block(2).astype(f32)
    to_one = jnp.concatenate([one[:half], one[half:] + high], axis=0).astype(bf16)
    to_two = jnp.concatenate([two[:half] + low, two[half:]], axis=0).astype(bf16)
    return block(0).astype(f32) + hop(to_one, n, 1).astype(f32) + hop(to_two, n, 2).astype(f32)


def exchange_ctx(blocks, n):
    me = lax.axis_index("ctx")
    got = lax.dynamic_update_slice_in_dim(
        jnp.zeros_like(blocks), lax.dynamic_slice_in_dim(blocks, me, 1, 0), me, 0
    )
    for k in range(1, n):
        sent = lax.dynamic_slice_in_dim(blocks, me ^ k, 1, 0)
        got = lax.dynamic_update_slice_in_dim(got, hop(sent, n, k), me ^ k, 0)
    return got


MESH = pl.DeviceIdType.MESH
HBM = pl.BlockSpec(memory_space=pltpu.HBM)


class Place:
    def __init__(self, dp):
        self.row = lax.axis_index("dp")
        self.col = lax.axis_index("ctx")
        self.lines = dp // 2
        self.line = self.row // 2
        self.core = self.row % 2
        self.twin = (self.row + 1 - 2 * self.core, self.col)

    def other(self, k):
        col, bit = self.col, 1
        while bit <= k:
            if k & bit:
                col = col + bit * (1 - 2 * ((self.col // bit) % 2))
            bit *= 2
        return col

    def across(self, k):
        return (self.row, self.other(k))

    def above(self):
        return (self.row + 2, self.col)

    def below(self):
        return (self.row - 2, self.col)


def greet(place, ctx):
    barrier = pltpu.get_barrier_semaphore()
    for k in range(1, ctx):
        pl.semaphore_signal(barrier, 1, device_id=place.across(k), device_id_type=MESH)
    pl.semaphore_wait(barrier, ctx - 1)


def remote(src, dst, send, recv, device):
    return pltpu.make_async_remote_copy(
        src_ref=src, dst_ref=dst, send_sem=send, recv_sem=recv, device_id=device, device_id_type=MESH
    )


class LineGather:
    def __init__(self, place, shard, sems):
        self.place, self.shard, self.sems = place, shard, sems

    def row(self, line):
        return line * 2 + self.place.core

    def up(self, hop):
        part = self.shard(self.row(self.place.line - hop + 1))
        return remote(part, part, self.sems.at[0, hop], self.sems.at[1, hop], self.place.above())

    def down(self, hop):
        part = self.shard(self.row(self.place.line + hop - 1))
        return remote(part, part, self.sems.at[2, hop], self.sems.at[3, hop], self.place.below())

    def over(self, at, row):
        part = self.shard(row)
        return remote(part, part, self.sems.at[4, at], self.sems.at[5, at], self.place.twin)

    def sends_up(self, hop):
        return (self.place.line - hop + 1 >= 0) & (self.place.line < self.place.lines - 1)

    def sends_down(self, hop):
        return (self.place.line + hop - 1 < self.place.lines) & (self.place.line > 0)

    def send(self, hop):
        place = self.place
        pl.when(self.sends_up(hop))(lambda: self.up(hop).start())
        pl.when(self.sends_down(hop))(lambda: self.down(hop).start())
        if hop == 1:
            self.over(0, place.row).start()

    def receive(self, hop):
        place = self.place

        @pl.when(place.line - hop >= 0)
        def _():
            part = self.shard(self.row(place.line - hop))
            remote(part, part, self.sems.at[0, hop], self.sems.at[1, hop], place.twin).wait_recv()
            self.over(hop, self.row(place.line - hop)).start()

        @pl.when(place.line + hop < place.lines)
        def _():
            part = self.shard(self.row(place.line + hop))
            remote(part, part, self.sems.at[2, hop], self.sems.at[3, hop], place.twin).wait_recv()
            self.over(place.lines - 1 + hop, self.row(place.line + hop)).start()

    def came_over(self, at, row):
        part = self.shard(row)
        remote(part, part, self.sems.at[4, at], self.sems.at[5, at], self.place.twin).wait_recv()

    def settle(self, hop, use=None):
        place = self.place
        other = 1 - 2 * place.core
        if hop == 0:
            self.came_over(0, place.row + other)
            if use:
                use(place.line)
            return
        for at, line, there in (
            (hop, place.line - hop, place.line - hop >= 0),
            (place.lines - 1 + hop, place.line + hop, place.line + hop < place.lines),
        ):

            @pl.when(there)
            def _():
                self.came_over(at, self.row(line) + other)
                if use:
                    use(line)

    def finish(self):
        place = self.place
        self.over(0, place.row).wait_send()
        for hop in range(1, place.lines):
            pl.when(self.sends_up(hop))(lambda: self.up(hop).wait_send())
            pl.when(self.sends_down(hop))(lambda: self.down(hop).wait_send())
            for at, line, there in (
                (hop, place.line - hop, place.line - hop >= 0),
                (place.lines - 1 + hop, place.line + hop, place.line + hop < place.lines),
            ):
                pl.when(there)(lambda: self.over(at, self.row(line)).wait_send())

    @staticmethod
    def scratch(dp):
        return pltpu.SemaphoreType.DMA((6, dp))


class CtxGather:
    def __init__(self, place, block, full, size, sems):
        self.place, self.block, self.full, self.size, self.sems = place, block, full, size, sems

    def rows(self, col, start=0, size=None):
        size = self.size if size is None else size
        return self.full.at[pl.ds(pl.multiple_of(col * self.size + start, size), size), :]

    def copies(self):
        place, half = self.place, self.size // 2
        me = place.col
        return [
            remote(self.block, self.rows(me), self.sems.at[0, 0], self.sems.at[1, 0], place.across(1)),
            remote(self.block, self.rows(me), self.sems.at[0, 1], self.sems.at[1, 1], place.across(2)),
            remote(
                self.rows(place.other(1), 0, half), self.rows(place.other(1), 0, half),
                self.sems.at[0, 2], self.sems.at[1, 2], place.across(2),
            ),
            remote(
                self.rows(place.other(2), half, half), self.rows(place.other(2), half, half),
                self.sems.at[0, 3], self.sems.at[1, 3], place.across(1),
            ),
        ]

    def arrivals(self):
        place, half = self.place, self.size // 2
        me = place.col
        parts = [self.rows(place.other(1)), self.rows(place.other(2)), self.rows(place.other(3), 0, half), self.rows(place.other(3), half, half)]
        return [
            remote(part, part, self.sems.at[0, i], self.sems.at[1, i], place.across(1))
            for i, part in enumerate(parts)
        ]

    def first(self):
        copies = self.copies()
        copies[0].start()
        copies[1].start()

    def second(self):
        copies, arrivals = self.copies(), self.arrivals()
        arrivals[0].wait_recv()
        copies[2].start()
        arrivals[1].wait_recv()
        copies[3].start()

    def finish(self):
        copies, arrivals = self.copies(), self.arrivals()
        arrivals[2].wait_recv()
        arrivals[3].wait_recv()
        for copy in copies:
            copy.wait_send()

    @staticmethod
    def scratch():
        return pltpu.SemaphoreType.DMA((2, 4))


def greet_all(place, dp, ctx, signal=True, wait=True):
    barrier = pltpu.get_barrier_semaphore()
    if signal:
        for k in range(1, ctx):
            pl.semaphore_signal(barrier, 1, device_id=place.across(k), device_id_type=MESH)
        for k in range(1, dp):
            pl.semaphore_signal(barrier, 1, device_id=((place.row + k) % dp, place.col), device_id_type=MESH)
    if wait:
        pl.semaphore_wait(barrier, ctx + dp - 2)


CHUNKS = 4
PARTS = 2


class CtxReduce:
    def __init__(self, place, block, total, sent, got, sems):
        self.place, self.block, self.total = place, block, total
        self.sent, self.got, self.sems = sent, got, sems
        self.size = total.shape[1] // CHUNKS

    def chunk(self, j):
        return pl.ds(j * self.size, self.size)

    def copy(self, kind, j):
        way = kind if kind else 1 + j % 2
        return remote(
            self.sent.at[kind, self.chunk(j)], self.got.at[kind, self.chunk(j)],
            self.sems.at[0, kind, j], self.sems.at[1, kind, j], self.place.across(way),
        )

    def start(self):
        self.start_far()
        self.start_near()

    def start_far(self):
        self.sent[0] = self.block(self.place.other(3)).astype(bf16)
        for j in range(CHUNKS):
            self.copy(0, j).start()

    def start_near(self):
        place = self.place
        for kind in (1, 2):
            self.total[kind - 1] = self.block(place.other(kind))
            for j in range(CHUNKS):
                if kind == 1 + j % 2:
                    self.sent[kind, self.chunk(j)] = self.total[kind - 1, self.chunk(j)].astype(bf16)
                    self.copy(kind, j).start()

    def relay(self):
        for j in range(CHUNKS):
            kind = 2 - j % 2
            self.copy(0, j).wait_recv()
            share = self.total[kind - 1, self.chunk(j)] + self.got[0, self.chunk(j)].astype(f32)
            self.sent[kind, self.chunk(j)] = share.astype(bf16)
            self.copy(kind, j).start()
        self.total[0] = self.block(self.place.col)

    def sum(self, j):
        for kind in (1, 2):
            self.copy(kind, j).wait_recv()
        rows = self.chunk(j)
        return self.total[0, rows] + self.got[1, rows].astype(f32) + self.got[2, rows].astype(f32)

    def finish(self):
        for kind in range(3):
            for j in range(CHUNKS):
                self.copy(kind, j).wait_send()

    @staticmethod
    def scratch(size, width):
        return [
            pltpu.VMEM((2, size, width), f32),
            pltpu.VMEM((3, size, width), bf16),
            pltpu.VMEM((3, size, width), bf16),
            pltpu.SemaphoreType.DMA((2, 3, CHUNKS)),
        ]


class CtxSpread:
    def __init__(self, place, made, full, sems):
        self.place, self.made, self.full, self.sems = place, made, full, sems
        self.size = made.shape[0] // CHUNKS

    def rows(self, col, j):
        at = (col * CHUNKS + j) * self.size
        return self.full.at[pl.ds(pl.multiple_of(at, self.size), self.size), :]

    def copy(self, kind, j):
        place = self.place
        if kind < 2:
            part, there = self.made.at[pl.ds(j * self.size, self.size), :], self.rows(place.col, j)
            way = 1 + kind
        else:
            way = 2 - j % 2
            part = there = self.rows(place.other(3 - way), j)
        return remote(part, there, self.sems.at[0, kind, j], self.sems.at[1, kind, j], place.across(way))

    def arrived(self, kind, j):
        part = self.rows(self.place.other(kind + 1), j)
        remote(
            part, part, self.sems.at[0, kind, j], self.sems.at[1, kind, j], self.place.across(1)
        ).wait_recv()

    def local(self, j):
        part = self.made.at[pl.ds(j * self.size, self.size), :]
        return pltpu.make_async_copy(part, self.rows(self.place.col, j), self.sems.at[0, 3, j])

    def send(self, j):
        self.copy(0, j).start()
        self.copy(1, j).start()
        self.local(j).start()

    def relay(self, j):
        way = 2 - j % 2
        self.arrived(2 - way, j)
        self.copy(2, j).start()

    def finish(self):
        for j in range(CHUNKS):
            way = 2 - j % 2
            self.arrived(way - 1, j)
            self.arrived(2, j)
            self.local(j).wait()
            for kind in range(3):
                self.copy(kind, j).wait_send()

    @staticmethod
    def scratch():
        return pltpu.SemaphoreType.DMA((2, 4, CHUNKS))


def rows_of(ref, col, size):
    return ref[pl.ds(pl.multiple_of(col * size, size), size), :]


class LineReduce:
    def __init__(self, place, parts, own, pair, got, sems):
        self.place, self.parts, self.own, self.pair, self.got, self.sems = place, parts, own, pair, got, sems

    def load(self, line):
        return pltpu.make_async_copy(
            self.parts.at[2 * line + self.place.core], self.own.at[line], self.sems.at[6, line]
        )

    def swap(self, line):
        row = 2 * line + 1 - self.place.core
        return remote(
            self.parts.at[row], self.pair.at[line], self.sems.at[0, line], self.sems.at[1, line], self.place.twin
        )

    def start(self):
        for line in range(self.place.lines):
            self.swap(line).start()

    def add_at(self, line):
        self.load(line).wait()
        self.swap(line).wait_recv()
        self.pair[line] = (self.own[line].astype(f32) + self.pair[line].astype(f32)).astype(bf16)

    def add(self, far):
        place = self.place
        if far == 0:
            self.add_at(place.line)
            return
        pl.when(place.line + far < place.lines)(lambda: self.add_at(place.line + far))
        pl.when(place.line - far >= 0)(lambda: self.add_at(place.line - far))

    def begin(self):
        for far in range(self.place.lines - 1, -1, -1):
            self.add(far)
            if far == self.place.lines - 1:
                self.send(far)

    def up(self, far):
        part = self.place.line + far
        return remote(
            self.pair.at[part], self.got.at[part], self.sems.at[2, far], self.sems.at[3, far], self.place.above()
        )

    def down(self, far):
        part = self.place.line - far
        slot = part if far > 1 else self.place.lines
        return remote(
            self.pair.at[part], self.got.at[slot], self.sems.at[4, far], self.sems.at[5, far], self.place.below()
        )

    def came_up(self, far):
        slot = self.got.at[self.place.line + far]
        remote(slot, slot, self.sems.at[2, far + 1], self.sems.at[3, far + 1], self.place.twin).wait_recv()

    def came_down(self, far):
        slot = self.got.at[self.place.line - far if far else self.place.lines]
        remote(slot, slot, self.sems.at[4, far + 1], self.sems.at[5, far + 1], self.place.twin).wait_recv()

    def send(self, far):
        place = self.place

        @pl.when(place.line + far < place.lines)
        def _():
            @pl.when(place.line > 0)
            def _():
                self.came_up(far)
                part = place.line + far
                self.pair[part] = (self.pair[part].astype(f32) + self.got[part].astype(f32)).astype(bf16)

            self.up(far).start()

        @pl.when(place.line - far >= 0)
        def _():
            @pl.when(place.line < place.lines - 1)
            def _():
                self.came_down(far)
                part = place.line - far
                self.pair[part] = (self.pair[part].astype(f32) + self.got[part].astype(f32)).astype(bf16)

            self.down(far).start()

    def collect(self, out):
        place = self.place
        out[...] = self.pair[place.line].astype(f32)

        @pl.when(place.line > 0)
        def _():
            self.came_up(0)
            out[...] += self.got[place.line].astype(f32)

        @pl.when(place.line < place.lines - 1)
        def _():
            self.came_down(0)
            out[...] += self.got[place.lines].astype(f32)

    def finish(self):
        place = self.place
        for line in range(place.lines):
            self.swap(line).wait_send()
        for far in range(1, place.lines):
            pl.when(place.line + far < place.lines)(lambda: self.up(far).wait_send())
            pl.when(place.line - far >= 0)(lambda: self.down(far).wait_send())

    @staticmethod
    def scratch(dp, tile):
        return [
            pltpu.VMEM((dp // 2,) + tile, bf16),
            pltpu.VMEM((dp // 2,) + tile, bf16),
            pltpu.VMEM((dp // 2 + 1,) + tile, bf16),
            pltpu.SemaphoreType.DMA((7, dp // 2)),
        ]


def mix_back_kernel(
    dp, ctx, gate_ref, up_ref, gate_weight_hbm, up_weight_hbm, inner_hbm, down_hbm, normed_hbm, gate_parts,
    resid_ref, cot_ref, gain_ref,
    d_resid_hbm, sums_ref, wide_ref, branch_hbm, d_up_hbm, d_gate_ref,
    total, sent, got, made, gate_weight_ref, up_weight_ref, inner, down_ref, normed, branch, d_up,
    own, pair, line_got, line_sem,
    reduce_sem, spread_sem, load_sem, inner_sem, normed_sem, branch_sem, d_up_sem, d_resid_sem,
):
    place = Place(dp)
    size, width = cot_ref.shape
    cols = normed.shape[2]
    loads = [
        pltpu.make_async_copy(src, dst, load_sem.at[i])
        for i, (src, dst) in enumerate(
            ((gate_weight_hbm, gate_weight_ref), (up_weight_hbm, up_weight_ref), (down_hbm, down_ref))
        )
    ]
    for load in loads[:2]:
        load.start()
    greet_all(place, dp, ctx)
    line = LineReduce(place, gate_parts, own, pair, line_got, line_sem)
    line.start()
    for i in range(place.lines):
        line.load(i).start()
    for load in loads[:2]:
        load.wait()

    def block(col):
        return dot_nt(rows_of(gate_ref, col, size), gate_weight_ref[...]) + dot_nt(
            rows_of(up_ref, col, size), up_weight_ref[...]
        )

    d_up_count, branch_count = width // cols, ctx

    def normed_load(i):
        return pltpu.make_async_copy(
            normed_hbm.at[:, pl.ds(i * cols, cols)], normed.at[i % 2], normed_sem.at[i % 2]
        )

    def inner_load(i):
        return pltpu.make_async_copy(
            inner_hbm.at[pl.ds(i * size, size), :], inner.at[i % 2], inner_sem.at[i % 2]
        )

    def d_up_copy(i):
        return pltpu.make_async_copy(
            d_up.at[i % 2], d_up_hbm.at[pl.ds(i * cols, cols), :], d_up_sem.at[i % 2]
        )

    def branch_copy(i):
        return pltpu.make_async_copy(
            branch.at[i % 2], branch_hbm.at[pl.ds(i * size, size), :], branch_sem.at[i % 2]
        )

    def d_up_piece(i):
        normed_load(i).wait()
        if i > 1:
            d_up_copy(i - 2).wait()
        d_up[i % 2] = dot_tn(normed[i % 2], up_ref[...]).astype(bf16)
        d_up_copy(i).start()
        if i + 2 < d_up_count:
            normed_load(i + 2).start()

    def branch_piece(i):
        if i == 0:
            loads[2].wait()
        inner_load(i).wait()
        if i > 1:
            branch_copy(i - 2).wait()
        branch[i % 2] = dot(inner[i % 2], down_ref[...]).astype(bf16)
        branch_copy(i).start()
        if i + 2 < branch_count:
            inner_load(i + 2).start()

    def d_resid_copy(j):
        rows = reduce.chunk(j)
        return pltpu.make_async_copy(total.at[1, rows, :], d_resid_hbm.at[rows, :], d_resid_sem.at[j])

    pieces = [functools.partial(d_up_piece, i) for i in range(d_up_count)]
    pieces += [functools.partial(branch_piece, i) for i in range(branch_count)]

    reduce = CtxReduce(place, block, total, sent, got, reduce_sem)
    spread = CtxSpread(place, made, wide_ref, spread_sem)
    reduce.start_far()
    loads[2].start()
    for i in range(2):
        normed_load(i).start()
        inner_load(i).start()
    reduce.start_near()
    line.begin()
    reduce.relay()
    sums_ref[...] = jnp.zeros_like(sums_ref)
    far = place.lines - 2
    for j in range(CHUNKS):
        for piece in pieces[2 * j : 2 * j + 2]:
            piece()
        rows = reduce.chunk(j)
        scaled, inv_std = norm_stats(resid_ref[rows, :])
        grad, d_gain, d_shift = norm_backward(reduce.sum(j), scaled, inv_std, gain_ref[...])
        sums_ref[0:1, :] += d_gain[None]
        sums_ref[1:2, :] += d_shift[None]
        grad = cot_ref[rows, :].astype(f32) + grad
        total[1, rows, :] = grad
        d_resid_copy(j).start()
        made[rows, :] = grad.astype(bf16)
        spread.send(j)
        if j:
            spread.relay(j - 1)
        if j % 2 == 0 and far > 0:
            line.send(far)
            far -= 1
    pieces[2 * CHUNKS]()
    spread.relay(CHUNKS - 1)
    while far > 0:
        line.send(far)
        far -= 1
    for piece in pieces[2 * CHUNKS + 1 :]:
        piece()
    spread.finish()
    line.collect(d_gate_ref)
    line.finish()
    reduce.finish()
    for i in (1, 2):
        d_up_copy(d_up_count - i).wait()
        branch_copy(branch_count - i).wait()
    for j in range(CHUNKS):
        d_resid_copy(j).wait()


def mix_back(dp, ctx, d_gate, d_up, gate_weight, up_weight, inner, down, normed, gate_parts, resid, cot, gain):
    size, width = cot.shape
    hidden = d_up.shape[1]
    own = width // dp
    cols = width // ctx // 2
    vmem = pl.BlockSpec(memory_space=pltpu.VMEM)
    return pl.pallas_call(
        functools.partial(mix_back_kernel, dp, ctx),
        in_specs=[vmem] * 2 + [HBM] * 6 + [vmem] * 3,
        out_specs=[HBM, vmem, HBM, HBM, HBM, vmem],
        out_shape=[
            jax.ShapeDtypeStruct((size, width), f32),
            jax.ShapeDtypeStruct((2, width), f32),
            jax.ShapeDtypeStruct((ctx * size, width), bf16),
            jax.ShapeDtypeStruct((ctx * size, width), bf16),
            jax.ShapeDtypeStruct((width, hidden), bf16),
            jax.ShapeDtypeStruct((own, hidden), f32),
        ],
        scratch_shapes=CtxReduce.scratch(size, width)[:3]
        + [
            pltpu.VMEM((size, width), bf16),
            pltpu.VMEM((width, hidden), bf16),
            pltpu.VMEM((width, hidden), bf16),
            pltpu.VMEM((2, size, hidden), bf16),
            pltpu.VMEM((hidden, width), bf16),
            pltpu.VMEM((2, ctx * size, cols), bf16),
            pltpu.VMEM((2, size, width), bf16),
            pltpu.VMEM((2, cols, hidden), bf16),
        ]
        + LineReduce.scratch(dp, (own, hidden))
        + [
            CtxReduce.scratch(size, width)[3],
            CtxSpread.scratch(),
            pltpu.SemaphoreType.DMA((3,)),
            pltpu.SemaphoreType.DMA((2,)),
            pltpu.SemaphoreType.DMA((2,)),
            pltpu.SemaphoreType.DMA((2,)),
            pltpu.SemaphoreType.DMA((2,)),
            pltpu.SemaphoreType.DMA((CHUNKS,)),
        ],
        compiler_params=pltpu.CompilerParams(
            collective_id=3, has_side_effects=True, vmem_limit_bytes=62 << 20
        ),
        cost_estimate=pl.CostEstimate(
            flops=8 * d_gate.size * width, transcendentals=0, bytes_accessed=180 << 20
        ),
    )(
        d_gate, d_up, gate_weight, up_weight, inner, down, normed, gate_parts.reshape(dp, own, hidden),
        resid, cot, gain.reshape(1, width),
    )


class CtxReduceReady:
    def __init__(self, place, full, have, got, sems, load_sems):
        self.place, self.full, self.have, self.got, self.sems, self.load_sems = place, full, have, got, sems, load_sems
        self.height = have.shape[1]
        self.size = self.height // CHUNKS

    def chunk(self, j):
        return pl.ds(j * self.size, self.size)

    def load(self, kind):
        col = self.place.other(kind)
        rows = pl.ds(pl.multiple_of(col * self.height, self.height), self.height)
        return pltpu.make_async_copy(self.full.at[rows, :], self.have.at[kind], self.load_sems.at[kind])

    def copy(self, kind, j):
        place = self.place
        if kind:
            part, way = self.have.at[kind, self.chunk(j)], kind
        else:
            at = (place.other(3) * CHUNKS + j) * self.size
            part, way = self.full.at[pl.ds(pl.multiple_of(at, self.size), self.size), :], 1 + j % 2
        return remote(
            part, self.got.at[kind, self.chunk(j)], self.sems.at[0, kind, j], self.sems.at[1, kind, j],
            place.across(way),
        )

    def start(self):
        for j in range(CHUNKS):
            self.copy(0, j).start()
        for kind in (1, 2):
            self.load(kind).wait()
            for j in range(CHUNKS):
                if kind == 1 + j % 2:
                    self.copy(kind, j).start()

    def relay(self):
        for j in range(CHUNKS):
            kind, rows = 2 - j % 2, self.chunk(j)
            self.copy(0, j).wait_recv()
            share = self.have[kind, rows].astype(f32) + self.got[0, rows].astype(f32)
            self.have[kind, rows] = share.astype(bf16)
            self.copy(kind, j).start()

    def sum(self, j):
        for kind in (1, 2):
            self.copy(kind, j).wait_recv()
        rows = self.chunk(j)
        return self.have[0, rows].astype(f32) + self.got[1, rows].astype(f32) + self.got[2, rows].astype(f32)

    def finish(self):
        for kind in range(3):
            for j in range(CHUNKS):
                self.copy(kind, j).wait_send()


def closing_kernel(
    dp, ctx,
    d_joined_hbm, weight_hbm, qkv_parts, out_parts, branch_hbm, rows_hbm, d_resid_hbm, resid_hbm,
    gain_ref, sums_two_ref, bias_ref,
    grad_ref, qkv_ref, out_ref, output_ref, vectors_ref, d_bias_ref,
    d_joined_ref, weight_ref, rows_ref, d_resid_ref, resid_ref, load_sem,
    total, sent, got, reduce_sem, qkv_own, qkv_pair, qkv_got, qkv_sem, out_own, out_pair, out_got, out_sem,
    have, branch_got, branch_sem, branch_load_sem,
    sums, tiles, tiles_got, small, small_sem, mine, swap_out, swap_in, swap_sem,
):
    place = Place(dp)
    me, row = place.col, place.row
    lines = [
        LineReduce(place, qkv_parts, qkv_own, qkv_pair, qkv_got, qkv_sem),
        LineReduce(place, out_parts, out_own, out_pair, out_got, out_sem),
    ]
    loads = [
        pltpu.make_async_copy(src, dst, load_sem.at[i])
        for i, (src, dst) in enumerate(
            (
                (d_joined_hbm, d_joined_ref), (weight_hbm, weight_ref), (rows_hbm, rows_ref),
                (d_resid_hbm, d_resid_ref), (resid_hbm, resid_ref),
            )
        )
    ]
    for load in loads[:2]:
        load.start()
    greet_all(place, dp, ctx)
    for line in lines:
        line.start()
    for i in range(place.lines):
        for line in lines:
            line.load(i).start()
    branch = CtxReduceReady(place, branch_hbm, have, branch_got, branch_sem, branch_load_sem)
    for kind in range(3):
        branch.load(kind).start()
    for load in loads[2:]:
        load.start()

    size, width = rows_ref.shape
    for load in loads[:2]:
        load.wait()
    reduce = CtxReduce(
        place, lambda col: dot_nt(rows_of(d_joined_ref, col, size), weight_ref[...]), total, sent, got, reduce_sem
    )
    reduce.start_far()
    for line in lines:
        line.begin()
    reduce.start_near()
    reduce.relay()
    branch.start()
    for far in range(place.lines - 2, 1, -1):
        for line in lines:
            line.send(far)

    sums[...] = jnp.zeros_like(sums)
    for load in loads[2:]:
        load.wait()
    branch.load(0).wait()
    for j in range(CHUNKS):
        rows = reduce.chunk(j)
        scaled, inv_std = norm_stats(rows_ref[rows, :].astype(f32))
        grad, d_gain, d_shift = norm_backward(reduce.sum(j), scaled, inv_std, gain_ref[...])
        sums[0:1, :] += d_gain[None]
        sums[1:2, :] += d_shift[None]
        grad_ref[rows, :] = d_resid_ref[rows, :] + grad
    branch.relay()
    if place.lines > 2:
        for line in lines:
            line.send(1)

    part = width // dp
    tiles[...] = jnp.zeros_like(tiles)
    for i in range(dp):
        lanes = slice(i * part, (i + 1) * part)
        tiles[i, 0:2, :] = sums[:, lanes]
        tiles[i, 2:4, :] = sums_two_ref[:, lanes]
        tiles[i, 4:5, :] = bias_ref[i : i + 1, :]
    sends = [
        remote(tiles.at[(row + k) % dp], tiles_got.at[k], small_sem.at[0, k], small_sem.at[1, k], ((row + k) % dp, me))
        for k in range(1, dp)
    ]
    for copy in sends:
        copy.start()
    tile = tiles[row]
    for k in range(1, dp):
        sends[k - 1].wait()
        tile = tile + tiles_got[k]
    tiles_got[0] = tile
    small[me] = tile
    spreads = [
        remote(tiles_got.at[0], small.at[me], small_sem.at[2, k], small_sem.at[3, k], place.across(k))
        for k in range(1, ctx)
    ]
    for copy in spreads:
        copy.start()

    for j in range(CHUNKS):
        rows = branch.chunk(j)
        output_ref[rows, :] = (resid_ref[rows, :] + branch.sum(j)).astype(bf16)

    for k in range(1, ctx):
        spreads[k - 1].wait_send()
        part = small.at[place.other(k)]
        remote(part, part, small_sem.at[2, k], small_sem.at[3, k], place.across(k)).wait_recv()
    four = sum(small[c, 0:4, :] for c in range(ctx))
    piece = vectors_ref.shape[1]
    slots = d_bias_ref.shape[1] // HD
    vectors = four[:, :piece]
    biases = [small[i % ctx, 4:5, i // ctx * HD : (i // ctx + 1) * HD] for i in range(slots * ctx)]
    chosen = biases[:slots]
    for c in range(1, ctx):
        vectors = jnp.where(me == c, four[:, c * piece : (c + 1) * piece], vectors)
        chosen = [jnp.where(me == c, biases[slots * c + i], chosen[i]) for i in range(slots)]
    vectors_ref[...] = vectors
    for i in range(slots):
        d_bias_ref[:, i * HD : (i + 1) * HD] = chosen[i]

    lines[0].collect(mine)
    depth = mine.shape[0] // ctx
    swap_out[...] = mine[...].astype(bf16)
    swaps = [
        remote(
            swap_out.at[pl.ds(pl.multiple_of(place.other(k) * depth, depth), depth), :], swap_in.at[me],
            swap_sem.at[0, k], swap_sem.at[1, k], place.across(k),
        )
        for k in range(1, ctx)
    ]
    for copy in swaps:
        copy.start()
    swap_in[me] = rows_of(swap_out, me, depth)
    lines[1].collect(out_ref)
    for k in range(1, ctx):
        part = swap_in.at[place.other(k)]
        remote(part, part, swap_sem.at[0, k], swap_sem.at[1, k], place.across(k)).wait_recv()
    low = head_lanes((depth, PAIR))
    for p in range(mine.shape[1] // (3 * PAIR)):
        for t in range(3):
            lanes = slice((3 * p + t) * PAIR, (3 * p + t + 1) * PAIR)
            for c in range(0, ctx, 2):
                a = swap_in[c, :, lanes].astype(f32)
                b = swap_in[c + 1, :, lanes].astype(f32)
                at = t * width + (2 * p * ctx + c) * HD
                qkv_ref[:, at : at + PAIR] = jnp.where(low, a, pltpu.roll(b, HD, 1))
                at = at + ctx * HD
                qkv_ref[:, at : at + PAIR] = jnp.where(low, pltpu.roll(a, HD, 1), b)
    for copy in swaps:
        copy.wait_send()
    for line in lines:
        line.finish()
    branch.finish()
    reduce.finish()


def closing(dp, ctx, d_joined, weight, d_qkv, d_out, branch, rows, d_resid, resid, gain, sums_two, bias):
    size, width = rows.shape
    near = weight.shape[1]
    own, tall = width // dp, d_out.shape[0] // dp
    vmem = pl.BlockSpec(memory_space=pltpu.VMEM)
    reduce_scratch = CtxReduce.scratch(size, width)
    max_peers = max(dp, ctx)
    return pl.pallas_call(
        functools.partial(closing_kernel, dp, ctx),
        in_specs=[HBM] * 8 + [vmem] * 3,
        out_specs=[vmem] * 6,
        out_shape=[
            jax.ShapeDtypeStruct((size, width), f32),
            jax.ShapeDtypeStruct((own // ctx, 3 * width), f32),
            jax.ShapeDtypeStruct((tall, width), f32),
            jax.ShapeDtypeStruct((size, width), bf16),
            jax.ShapeDtypeStruct((4, own // ctx), f32),
            jax.ShapeDtypeStruct((1, 3 * own // ctx), f32),
        ],
        scratch_shapes=[
            pltpu.VMEM((ctx * size, near), bf16),
            pltpu.VMEM((width, near), bf16),
            pltpu.VMEM((size, width), bf16),
            pltpu.VMEM((size, width), f32),
            pltpu.VMEM((size, width), f32),
            pltpu.SemaphoreType.DMA((5,)),
        ]
        + reduce_scratch
        + LineReduce.scratch(dp, (own, near))
        + LineReduce.scratch(dp, (tall, width))
        + reduce_scratch[1:]
        + [
            pltpu.SemaphoreType.DMA((3,)),
            pltpu.VMEM((2, width), f32),
            pltpu.VMEM((dp, 8, own), f32),
            pltpu.VMEM((dp, 8, own), f32),
            pltpu.VMEM((ctx, 8, own), f32),
            pltpu.SemaphoreType.DMA((4, max_peers)),
            pltpu.VMEM((own, near), f32),
            pltpu.VMEM((own, near), bf16),
            pltpu.VMEM((ctx, own // ctx, near), bf16),
            pltpu.SemaphoreType.DMA((2, ctx)),
        ],
        compiler_params=pltpu.CompilerParams(
            collective_id=1, has_side_effects=True, vmem_limit_bytes=62 << 20
        ),
        cost_estimate=pl.CostEstimate(
            flops=2 * d_joined.size * width, transcendentals=0, bytes_accessed=200 << 20
        ),
    )(
        d_joined, weight, d_qkv.reshape(dp, own, near), d_out.reshape(dp, tall, width), branch,
        rows, d_resid, resid, gain.reshape(1, width), sums_two, bias,
    )


def turn(x, table_ref):
    return (
        x * table_ref[0]
        + pltpu.roll(x, PAIR - ROT // 2, 1) * table_ref[1]
        + pltpu.roll(x, ROT // 2, 1) * table_ref[2]
    )


def turn_back(x, table_ref):
    return (
        x * table_ref[0]
        - pltpu.roll(x, PAIR - ROT // 2, 1) * table_ref[1]
        - pltpu.roll(x, ROT // 2, 1) * table_ref[2]
    )


def head_lanes(shape):
    return lax.broadcasted_iota(jnp.int32, shape, 1) < HD


def span(full_len, step, at):
    return max(0, (at - DOC_MAX + 1) // step * step), at + step


def parts_of(low, at, step):
    return ([(low, at, False)] if low < at else []) + [(at, at + step, True)]


def masked(scores, start, first, causal):
    keys = lax.broadcasted_iota(jnp.int32, scores.shape, 1)
    allowed = keys >= start - first
    if causal:
        allowed = allowed & (keys <= lax.broadcasted_iota(jnp.int32, scores.shape, 0))
    return jnp.where(allowed, scores, masked_value)


def one_head(x, head):
    return jnp.where(head_lanes(x.shape) == (head == 0), x, jnp.zeros_like(x))


def attend_kernel(step, joined_ref, bias_ref, table_ref, start_ref, out_ref, qkv_ref, lse_ref):
    full_len = joined_ref.shape[0]
    scale = 1.0 / math.sqrt(HD)
    for t in range(3):
        lanes = slice(t * PAIR, (t + 1) * PAIR)
        x = joined_ref[:, lanes] + bias_ref[:, lanes]
        if t < 2:
            x = turn(x, table_ref)
        qkv_ref[:, lanes] = x.astype(bf16)
    for at in range(0, full_len, step):
        parts = parts_of(span(full_len, step, at)[0], at, step)
        start = start_ref[at : at + step, :1]
        q = qkv_ref[at : at + step, :PAIR] * bf16(scale)
        total = jnp.zeros((step, PAIR), f32)
        logs = []
        for head in range(2):
            qm = one_head(q, head)
            scores = [
                masked(dot_nt(qm, qkv_ref[low:high, PAIR : 2 * PAIR]), start, low, causal)
                for low, high, causal in parts
            ]
            tops = [jnp.max(s, axis=1, keepdims=True) for s in scores]
            top = functools.reduce(jnp.maximum, tops)
            norm, sums = 0.0, 0.0
            for s, (low, high, _) in zip(scores, parts):
                e = jnp.exp(s - top)
                norm = norm + jnp.sum(e, axis=1, keepdims=True)
                sums = sums + dot(e.astype(bf16), one_head(qkv_ref[low:high, 2 * PAIR :], head))
            total = total + sums * (1.0 / norm)
            logs.append(top + jnp.log(norm))
        out_ref[at : at + step, :] = total.astype(bf16)
        lse_ref[at : at + step, :] = jnp.where(head_lanes((step, PAIR)), logs[0], logs[1])


def attend_back_kernel(
    step, qkv_ref, grad_ref, lse_ref, table_ref, start_ref, out_ref, sum_ref, dk_ref, dv_ref
):
    full_len = qkv_ref.shape[0]
    scale = 1.0 / math.sqrt(HD)
    dk_ref[...] = jnp.zeros_like(dk_ref)
    dv_ref[...] = jnp.zeros_like(dv_ref)
    total = jnp.zeros((1, PAIR), f32)
    for at in range(0, full_len, step):
        rows = slice(at, at + step)
        parts = parts_of(span(full_len, step, at)[0], at, step)
        start = start_ref[rows, :1]
        q = qkv_ref[rows, :PAIR] * bf16(scale)
        g = grad_ref[rows, :]
        dq = jnp.zeros((step, PAIR), f32)
        dk = [jnp.zeros((high - low, PAIR), f32) for low, high, _ in parts]
        dv = [jnp.zeros((high - low, PAIR), f32) for low, high, _ in parts]
        for head in range(2):
            qm, gm = one_head(q, head), one_head(g, head)
            lse = lse_ref[rows, head * HD : head * HD + 1]
            probs, dps, mean = [], [], 0.0
            for low, high, causal in parts:
                s = masked(dot_nt(qm, qkv_ref[low:high, PAIR : 2 * PAIR]), start, low, causal)
                probs.append(jnp.exp(s - lse))
                dps.append(dot_nt(gm, qkv_ref[low:high, 2 * PAIR :]))
                mean = mean + jnp.sum(dps[-1] * probs[-1], axis=1, keepdims=True)
            for i, (low, high, _) in enumerate(parts):
                ds = (probs[i] * (dps[i] - mean)).astype(bf16)
                dq = dq + dot(ds, one_head(qkv_ref[low:high, PAIR : 2 * PAIR], head))
                dk[i] = dk[i] + dot_tn(ds, qm)
                dv[i] = dv[i] + dot_tn(probs[i].astype(bf16), gm)
        for i, (low, high, _) in enumerate(parts):
            dk_ref[low:high, :] += dk[i]
            dv_ref[low:high, :] += dv[i]
        dq = turn_back(dq * scale, table_ref.at[:, rows, :]).astype(bf16)
        out_ref[rows, :PAIR] = dq
        total = total + jnp.sum(dq.astype(f32), axis=0, keepdims=True)
    sum_ref[:, :PAIR] = total
    dk = turn_back(dk_ref[...], table_ref).astype(bf16)
    out_ref[:, PAIR : 2 * PAIR] = dk
    sum_ref[:, PAIR : 2 * PAIR] = jnp.sum(dk.astype(f32), axis=0, keepdims=True)
    dv = dv_ref[...].astype(bf16)
    out_ref[:, 2 * PAIR :] = dv
    sum_ref[:, 2 * PAIR :] = jnp.sum(dv.astype(f32), axis=0, keepdims=True)


def whole(shape):
    return pl.BlockSpec(shape, lambda p: (0,) * len(shape))


def attend_step(full_len):
    return min(256, full_len)


def attend(joined, bias, table, start):
    full_len, width = joined.shape
    pairs = width // (3 * PAIR)
    step = attend_step(full_len)
    seen = sum(span(full_len, step, at)[1] - span(full_len, step, at)[0] for at in range(0, full_len, step)) * step
    wide = pl.BlockSpec((full_len, 3 * PAIR), lambda p: (0, p))
    thin = pl.BlockSpec((full_len, PAIR), lambda p: (0, p))
    return pl.pallas_call(
        functools.partial(attend_kernel, step),
        grid=(pairs,),
        in_specs=[
            wide,
            pl.BlockSpec((1, 3 * PAIR), lambda p: (0, p)),
            whole(table.shape),
            whole(start.shape),
        ],
        out_specs=[thin, wide, thin],
        out_shape=[
            jax.ShapeDtypeStruct((full_len, pairs * PAIR), bf16),
            jax.ShapeDtypeStruct((full_len, width), bf16),
            jax.ShapeDtypeStruct((full_len, pairs * PAIR), f32),
        ],
        compiler_params=pltpu.CompilerParams(vmem_limit_bytes=40 << 20),
        cost_estimate=pl.CostEstimate(
            flops=pairs * seen * PAIR * 8, transcendentals=pairs * seen * 2, bytes_accessed=full_len * width * 8
        ),
    )(joined, bias, table, start)


def attend_back(qkv, grad, lse, table, start):
    full_len, width = qkv.shape
    pairs = width // (3 * PAIR)
    step = attend_step(full_len)
    seen = sum(span(full_len, step, at)[1] - span(full_len, step, at)[0] for at in range(0, full_len, step)) * step
    wide = pl.BlockSpec((full_len, 3 * PAIR), lambda p: (0, p))
    thin = pl.BlockSpec((full_len, PAIR), lambda p: (0, p))
    return pl.pallas_call(
        functools.partial(attend_back_kernel, step),
        grid=(pairs,),
        in_specs=[wide, thin, thin, whole(table.shape), whole(start.shape)],
        out_specs=[wide, pl.BlockSpec((1, 3 * PAIR), lambda p: (0, p))],
        out_shape=[
            jax.ShapeDtypeStruct((full_len, width), bf16),
            jax.ShapeDtypeStruct((1, width), f32),
        ],
        scratch_shapes=[pltpu.VMEM((full_len, PAIR), f32), pltpu.VMEM((full_len, PAIR), f32)],
        compiler_params=pltpu.CompilerParams(vmem_limit_bytes=40 << 20),
        cost_estimate=pl.CostEstimate(
            flops=pairs * seen * PAIR * 20, transcendentals=pairs * seen * 2, bytes_accessed=full_len * width * 8
        ),
    )(*[pltpu.with_memory_space_constraint(x, pltpu.HBM) for x in (qkv, grad, lse, table, start)])


def forward_kernel(
    dp, ctx, step,
    gain_one, shift_one, gain_two, shift_two, bias, start_ref, table_hbm,
    qkv_hbm, out_weight_ref, rows_ref, cot_ref, gate_hbm, up_hbm,
    params_ref, weight_hbm, out_hbm, normed_hbm, cot_all, attended_hbm, heads_hbm, lse_hbm, resid_hbm, wide_ref,
    gate_all, up_all,
    small_all, table_ref, small_ref, qkv_ref, blocks, rows_all, weight_ref, normed_ref, joined_ref, bias_ref, out_all,
    attended_ref, heads_ref, lse_ref, total, sent, got, made, resid_ref,
    normed_sem, weight_sem, local_sem, swap_sem, small_sem, line_joined, line_out, line_gate, line_up, rows_sem, cot_sem,
    late_sem, reduce_sem, spread_sem, resid_sem,
):
    place = Place(dp)
    me, row = place.col, place.row
    depth = qkv_ref.shape[0]
    length, width = rows_ref.shape
    rows_out = out_weight_ref.shape[0]
    tall = ctx * depth

    qkv_copy = pltpu.make_async_copy(qkv_hbm, qkv_ref, local_sem.at[4])
    qkv_copy.start()
    table_copy = pltpu.make_async_copy(table_hbm, table_ref, late_sem.at[0])
    table_copy.start()
    greet_all(place, dp, ctx, wait=False)
    small_ref[...] = jnp.zeros_like(small_ref)
    for i, vector in enumerate((gain_one, shift_one, gain_two, shift_two)):
        small_ref[i // 2 : i // 2 + 1, i % 2 * HD : (i % 2 + 1) * HD] = vector[...].astype(f32)
    for i in range(bias.shape[1] // HD):
        small_ref[2 + i // 2 : 3 + i // 2, i % 2 * HD : (i % 2 + 1) * HD] = bias[
            :, i * HD : (i + 1) * HD
        ].astype(f32)
    small_all[row, me] = small_ref[...]
    qkv_copy.wait()

    low = head_lanes((depth, PAIR))
    for p in range(width // HD // ctx // 2):
        for t in range(3):
            lanes = slice((3 * p + t) * PAIR, (3 * p + t + 1) * PAIR)
            for c in range(0, ctx, 2):
                at = t * width + (2 * p * ctx + c) * HD
                a = qkv_ref[:, at : at + PAIR].astype(f32)
                at = at + ctx * HD
                b = qkv_ref[:, at : at + PAIR].astype(f32)
                blocks[c, :, lanes] = jnp.where(low, a, pltpu.roll(b, HD, 1)).astype(bf16)
                blocks[c + 1, :, lanes] = jnp.where(low, pltpu.roll(a, HD, 1), b).astype(bf16)
    greet_all(place, dp, ctx, signal=False)

    def weight_rows(row, col):
        return weight_ref.at[pl.ds(pl.multiple_of((row * ctx + col) * depth, depth), depth), :]

    def out_shard(row):
        return out_all.at[pl.ds(pl.multiple_of(row * rows_out, rows_out), rows_out), :]

    def block(ref, col):
        return ref.at[pl.ds(pl.multiple_of(col * length, length), length), :]

    part_cols = weight_ref.shape[1] // PARTS

    def weight_part(i, row):
        return weight_ref.at[
            pl.ds(pl.multiple_of(row * tall, tall), tall), pl.ds(i * part_cols, part_cols)
        ]

    local = [
        pltpu.make_async_copy(blocks.at[me], weight_rows(row, me), local_sem.at[0]),
        pltpu.make_async_copy(out_weight_ref, out_shard(row), local_sem.at[1]),
        pltpu.make_async_copy(rows_ref, block(rows_all, me), local_sem.at[2]),
        pltpu.make_async_copy(cot_ref, block(cot_all, me), local_sem.at[3]),
    ]
    swaps = [
        remote(small_ref, small_all.at[row, me], swap_sem.at[0, k], swap_sem.at[1, k], place.across(k))
        for k in range(1, ctx)
    ] + [
        remote(
            blocks.at[place.other(k)], weight_rows(row, me), swap_sem.at[2, k], swap_sem.at[3, k], place.across(k)
        )
        for k in range(1, ctx)
    ]
    for copy in swaps:
        copy.start()
    for copy in local:
        copy.start()

    def gate_shard(row):
        tall = gate_hbm.shape[0]
        return gate_all.at[pl.ds(pl.multiple_of(row * tall, tall), tall), :]

    def up_shard(row):
        tall = up_hbm.shape[0]
        return up_all.at[pl.ds(pl.multiple_of(row * tall, tall), tall), :]

    gate_line, up_line = LineGather(place, gate_shard, line_gate), LineGather(place, up_shard, line_up)
    late = [
        pltpu.make_async_copy(gate_hbm, gate_shard(row), late_sem.at[1]),
        pltpu.make_async_copy(up_hbm, up_shard(row), late_sem.at[2]),
    ]
    for copy in late:
        copy.start()
    rows_gather = CtxGather(place, rows_ref, rows_all, length, rows_sem)
    cot_gather = CtxGather(place, cot_ref, cot_all, length, cot_sem)
    out_line = LineGather(place, out_shard, line_out)
    lines = [
        LineGather(place, functools.partial(weight_part, i), line_joined.at[i]) for i in range(PARTS)
    ] + [out_line]
    local[1].wait()
    out_line.send(1)
    rows_gather.first()
    for k in range(1, ctx):
        remote(
            small_ref, small_all.at[row, place.other(k)], swap_sem.at[0, k], swap_sem.at[1, k], place.across(k)
        ).wait_recv()
    small_sends = [
        remote(
            small_all.at[row], small_all.at[row], small_sem.at[0, k], small_sem.at[1, k], ((row + k) % dp, me)
        )
        for k in range(1, dp)
    ]
    for copy in small_sends:
        copy.start()
    local[0].wait()
    for k in range(1, ctx):
        part = weight_rows(row, place.other(k))
        remote(part, part, swap_sem.at[2, k], swap_sem.at[3, k], place.across(k)).wait_recv()
    for line in lines[:PARTS]:
        line.send(1)

    for k in range(1, dp):
        part = small_all.at[(row + dp - k) % dp]
        remote(part, part, small_sem.at[0, k], small_sem.at[1, k], place.twin).wait_recv()
    low = head_lanes((1, PAIR))
    for i in range(dp * ctx // 2):
        lanes = slice(i * PAIR, (i + 1) * PAIR)
        a = small_all[2 * i // ctx, 2 * i % ctx]
        b = small_all[(2 * i + 1) // ctx, (2 * i + 1) % ctx]
        for r in range(2):
            ar, br = a[r : r + 1, :], b[r : r + 1, :]
            params_ref[2 * r : 2 * r + 1, lanes] = jnp.where(low, ar, pltpu.roll(br, HD, 1))
            params_ref[2 * r + 1 : 2 * r + 2, lanes] = jnp.where(low, pltpu.roll(ar, HD, 1), br)

    def normalize(col):
        step = 64

        @pl.loop(0, length // step)
        def _(i):
            rows = pl.ds(pl.multiple_of(col * length + i * step, step), step)
            scaled, _ = norm_stats(rows_all[rows, :].astype(f32))
            normed_ref[rows, :] = (scaled * params_ref[0:1, :] + params_ref[1:2, :]).astype(bf16)

        normed_copy(col).start()

    def normed_copy(col):
        return pltpu.make_async_copy(block(normed_ref, col), block(normed_hbm, col), normed_sem.at[col])

    def weight_copy(i, line):
        part = (
            pl.ds(pl.multiple_of(line * (2 * tall), 2 * tall), 2 * tall),
            pl.ds(i * part_cols, part_cols),
        )
        return pltpu.make_async_copy(weight_ref.at[part], weight_hbm.at[part], weight_sem.at[i, line])

    def multiply(i, line):
        weight_copy(i, line).start()
        at = pl.multiple_of(line * (2 * tall), 2 * tall)
        cols = slice(i * part_cols, (i + 1) * part_cols)

        @pl.loop(0, ctx)
        def _(b):
            rows = pl.ds(pl.multiple_of(b * length, length), length)
            joined_ref[rows, cols] += dot(
                normed_ref[rows, pl.ds(at, 2 * tall)], weight_ref[pl.ds(at, 2 * tall), cols]
            )

    def forward(hop):
        for line in lines:
            line.receive(hop)
            if hop < place.lines - 1:
                line.send(hop + 1)

    def absorb(hop):
        for i in range(PARTS):
            lines[i].settle(hop, functools.partial(multiply, i))

    joined_ref[...] = jnp.zeros_like(joined_ref)
    local[2].wait()
    normalize(me)
    rows_gather.second()
    cot_gather.first()
    for hop in range(1, place.lines):
        forward(hop)
        if hop == 1:
            for col in (place.other(1), place.other(2)):
                normalize(col)
            rows_gather.finish()
            normalize(place.other(3))
        if hop == min(2, place.lines - 1):
            cot_gather.second()
        absorb(hop - 1)
    late[0].wait()
    gate_line.send(1)
    absorb(place.lines - 1)
    late[1].wait()

    low = head_lanes((1, PAIR))
    pairs = joined_ref.shape[1] // (3 * PAIR)
    per_device = bias.shape[1] // HD
    for p in range(pairs):
        for t in range(3):
            chosen = [None, None]
            for c in range(ctx):
                for half in range(2):
                    slot = t * (width // HD) + (2 * p + half) * ctx + c
                    owner, at = slot // per_device, slot % per_device
                    piece = small_all[owner // ctx, owner % ctx, 2 + at // 2 : 3 + at // 2, :]
                    if at % 2 != half:
                        piece = pltpu.roll(piece, HD, 1)
                    chosen[half] = piece if c == 0 else jnp.where(me == c, piece, chosen[half])
            lanes = slice((3 * p + t) * PAIR, (3 * p + t + 1) * PAIR)
            bias_ref[:, lanes] = jnp.where(low, chosen[0], chosen[1])

    def heads_copies():
        return [
            pltpu.make_async_copy(attended_ref, attended_hbm, late_sem.at[3]),
            pltpu.make_async_copy(heads_ref, heads_hbm, late_sem.at[4]),
            pltpu.make_async_copy(lse_ref, lse_hbm, late_sem.at[5]),
            pltpu.make_async_copy(out_all, out_hbm, late_sem.at[6]),
        ]

    def attend_pairs(first, last):
        @pl.loop(first, last)
        def _(p):
            wide = pl.ds(pl.multiple_of(p * (3 * PAIR), 3 * PAIR), 3 * PAIR)
            thin = pl.ds(pl.multiple_of(p * PAIR, PAIR), PAIR)
            attend_kernel(
                step, joined_ref.at[:, wide], bias_ref.at[:, wide], table_ref, start_ref,
                attended_ref.at[:, thin], heads_ref.at[:, wide], lse_ref.at[:, thin],
            )

    def pass_on(line, hop):
        line.receive(hop)
        if hop < place.lines - 1:
            line.send(hop + 1)

    table_copy.wait()
    up_line.send(1)
    attend_pairs(0, pairs // 2)
    if place.lines > 1:
        pass_on(gate_line, 1)
    attend_pairs(pairs // 2, pairs)
    for hop in range(place.lines):
        out_line.settle(hop)
    for line in lines:
        line.finish()
    cot_gather.finish()
    for copy in heads_copies():
        copy.start()

    reduce = CtxReduce(
        place, lambda col: dot(rows_of(attended_ref, col, length), out_all[...]), total, sent, got, reduce_sem
    )
    spread = CtxSpread(place, made, wide_ref, spread_sem)

    def resid_copy(j):
        rows = reduce.chunk(j)
        return pltpu.make_async_copy(resid_ref.at[rows, :], resid_hbm.at[rows, :], resid_sem.at[j])

    reduce.start()
    reduce.relay()
    if place.lines > 2:
        pass_on(gate_line, 2)
    for j in range(CHUNKS):
        rows = reduce.chunk(j)
        at = pl.multiple_of(me * length + j * reduce.size, reduce.size)
        resid = rows_all[pl.ds(at, reduce.size), :].astype(f32) + reduce.sum(j)
        resid_ref[rows, :] = resid
        resid_copy(j).start()
        scaled, _ = norm_stats(resid)
        made[rows, :] = (scaled * params_ref[2:3, :] + params_ref[3:4, :]).astype(bf16)
        spread.send(j)
        if j:
            spread.relay(j - 1)
        if j == 0 and place.lines > 1:
            pass_on(up_line, 1)
        if j == 3 and place.lines > 2:
            pass_on(up_line, 2)
    spread.relay(CHUNKS - 1)
    for hop in range(3, place.lines):
        pass_on(gate_line, hop)
    for hop in range(3, place.lines):
        pass_on(up_line, hop)
    spread.finish()
    for line in (gate_line, up_line):
        for hop in range(place.lines):
            line.settle(hop)
        line.finish()
    reduce.finish()
    for copy in swaps + small_sends:
        copy.wait_send()
    local[3].wait()
    for col in range(ctx):
        normed_copy(col).wait()
    for line in range(place.lines):
        for i in range(PARTS):
            weight_copy(i, line).wait()
    for j in range(CHUNKS):
        resid_copy(j).wait()
    for copy in heads_copies():
        copy.wait()


def forward(dp, ctx, vectors, start, table, qkv_weight, out_weight, rows, cot, gate_weight, up_weight):
    depth, width = qkv_weight.shape[0], rows.shape[1]
    length = rows.shape[0]
    full_len = ctx * length
    near = 3 * width // ctx
    thin = near // 3
    hidden = gate_weight.shape[1]
    vmem = pl.BlockSpec(memory_space=pltpu.VMEM)
    reduce_scratch = CtxReduce.scratch(length, width)
    return pl.pallas_call(
        functools.partial(forward_kernel, dp, ctx, attend_step(full_len)),
        in_specs=[vmem] * (len(vectors) + 1) + [HBM] * 7,
        out_specs=[vmem] + [HBM] * 11,
        out_shape=[
            jax.ShapeDtypeStruct((4, width), f32),
            jax.ShapeDtypeStruct((dp * ctx * depth, near), bf16),
            jax.ShapeDtypeStruct((dp * out_weight.shape[0], width), bf16),
            jax.ShapeDtypeStruct((full_len, width), bf16),
            jax.ShapeDtypeStruct((full_len, width), bf16),
            jax.ShapeDtypeStruct((full_len, thin), bf16),
            jax.ShapeDtypeStruct((full_len, near), bf16),
            jax.ShapeDtypeStruct((full_len, thin), f32),
            jax.ShapeDtypeStruct((length, width), f32),
            jax.ShapeDtypeStruct((full_len, width), bf16),
            jax.ShapeDtypeStruct((dp * gate_weight.shape[0], hidden), bf16),
            jax.ShapeDtypeStruct((dp * up_weight.shape[0], hidden), bf16),
        ],
        scratch_shapes=[
            pltpu.VMEM((dp, ctx, 8, PAIR), f32),
            pltpu.VMEM(table.shape, f32),
            pltpu.VMEM((8, PAIR), f32),
            pltpu.VMEM((depth, 3 * width), bf16),
            pltpu.VMEM((ctx, depth, near), bf16),
            pltpu.VMEM((full_len, width), bf16),
            pltpu.VMEM((dp * ctx * depth, near), bf16),
            pltpu.VMEM((full_len, width), bf16),
            pltpu.VMEM((full_len, near), f32),
            pltpu.VMEM((1, near), f32),
            pltpu.VMEM((dp * out_weight.shape[0], width), bf16),
            pltpu.VMEM((full_len, thin), bf16),
            pltpu.VMEM((full_len, near), bf16),
            pltpu.VMEM((full_len, thin), f32),
        ]
        + reduce_scratch[:3]
        + [
            pltpu.VMEM((length, width), bf16),
            pltpu.VMEM((length, width), f32),
            pltpu.SemaphoreType.DMA((ctx,)),
            pltpu.SemaphoreType.DMA((PARTS, dp // 2)),
            pltpu.SemaphoreType.DMA((5,)),
            pltpu.SemaphoreType.DMA((4, ctx)),
            pltpu.SemaphoreType.DMA((2, dp)),
            pltpu.SemaphoreType.DMA((PARTS, 6, dp)),
            LineGather.scratch(dp),
            LineGather.scratch(dp),
            LineGather.scratch(dp),
            CtxGather.scratch(),
            CtxGather.scratch(),
            pltpu.SemaphoreType.DMA((7,)),
            reduce_scratch[3],
            CtxSpread.scratch(),
            pltpu.SemaphoreType.DMA((CHUNKS,)),
        ],
        compiler_params=pltpu.CompilerParams(
            collective_id=0, has_side_effects=True, vmem_limit_bytes=62 << 20
        ),
        cost_estimate=pl.CostEstimate(
            flops=2 * full_len * width * near, transcendentals=0, bytes_accessed=400 << 20
        ),
    )(*vectors, start, table, qkv_weight, out_weight, rows, cot, gate_weight, up_weight)


def rotary_table(full_len):
    half = ROT // 2
    inverse = 10000.0 ** (-2.0 * np.arange(half) / ROT)
    angles = np.arange(full_len)[:, None] * inverse[None, :]
    table = np.zeros((3, full_len, HD), np.float32)
    table[0, :, :half] = table[0, :, half:ROT] = np.cos(angles)
    table[0, :, ROT:] = 1.0
    table[1, :, :half] = -np.sin(angles)
    table[2, :, half:ROT] = np.sin(angles)
    return jnp.asarray(np.concatenate([table, table], axis=2))


def shards(
    dp,
    ctx,
    inputs,
    segments,
    ln1_gain,
    ln1_bias,
    qkv_weight,
    qkv_bias,
    out_weight,
    ln2_gain,
    ln2_bias,
    gate_weight,
    up_weight,
    down_weight,
    cotangent,
):
    local_len, width = inputs.shape[1], inputs.shape[2]
    full_len = segments.shape[1]
    heads = width // HD
    near = heads // ctx
    pairs = near // 2
    me = lax.axis_index("ctx")
    own = me * local_len

    segment = segments[0]
    start = jnp.sum((segment[None, :] < segment[:, None]).astype(jnp.int32), axis=1)
    start = jnp.broadcast_to(start[:, None], (full_len, 128))
    table = rotary_table(full_len)
    part = ln1_gain.shape[0]
    vectors = [v[None, :] for v in (ln1_gain, ln1_bias, ln2_gain, ln2_bias, qkv_bias)]
    rows_here = qkv_weight.shape[0]
    rows, grad_rows = inputs[0], cotangent[0]
    fused = ctx == 4 and dp % 2 == 0 and part == HD
    if fused:
        (
            params, joined_weight, out_full, normed_one, grad_wide, attended, qkv, lse, resid, normed_wide,
            gate_full, up_full,
        ) = forward(
            dp, ctx, vectors, start, table, qkv_weight, out_weight, rows, grad_rows, gate_weight, up_weight
        )
        gain_one, _, gain_two, _ = params
        down_weight, _ = lax.optimization_barrier((down_weight, normed_wide))
    else:
        small = jnp.concatenate(vectors, axis=1).astype(f32)
        small = lax.all_gather(small, ("dp", "ctx"), axis=0, tiled=True)
        blocks = qkv_weight.reshape(rows_here, 3, pairs, 2, ctx, HD).transpose(4, 0, 2, 1, 3, 5)
        blocks = exchange_ctx(blocks.reshape(ctx, rows_here, near * 3 * HD), ctx)
        joined_weight = lax.all_gather(
            blocks.reshape(ctx * rows_here, near * 3 * HD), "dp", axis=0, tiled=True
        )
        out_full = lax.all_gather(out_weight, ("dp", "ctx"), axis=0, tiled=True)
        out_full = out_full.reshape(near, ctx, HD, width)
        out_full = lax.dynamic_index_in_dim(out_full, me, 1, keepdims=False)
        out_full = out_full.reshape(near * HD, width)
        gain_one, shift_one, gain_two, shift_two = [
            small[:, i * part : (i + 1) * part].reshape(width) for i in range(4)
        ]
        scaled_wide, _ = norm_stats(gather_ctx(rows, ctx).astype(f32))
        normed_one = (scaled_wide * gain_one + shift_one).astype(bf16)
        grad_wide = gather_ctx(grad_rows, ctx)
        bias = small[:, 4 * part :].reshape(3, pairs, 2, ctx, HD)
        bias = lax.dynamic_index_in_dim(bias, me, 3, keepdims=False)
        bias = bias.transpose(1, 0, 2, 3).reshape(1, near * 3 * HD)
        attended, qkv, lse = attend(dot(normed_one, joined_weight), bias, table, start)
        resid = rows.astype(f32) + scatter_ctx(dot(attended, out_full), ctx)
        scaled_two, inv_two = norm_stats(resid)
        normed_wide = gather_ctx((scaled_two * gain_two + shift_two).astype(bf16), ctx)
        gate_full = lax.all_gather(gate_weight, "dp", axis=0, tiled=True)
        up_full = lax.all_gather(up_weight, "dp", axis=0, tiled=True)
    down_full = lax.all_gather(down_weight, "dp", axis=1, tiled=True)

    gate = dot(normed_wide, gate_full)
    upward = dot(normed_wide, up_full)
    sigma = jax.nn.sigmoid(gate)
    swish = gate * sigma
    inner = (swish * upward).astype(bf16)
    d_down = dot_tn(inner, grad_wide).astype(bf16)
    grad_wide, d_down = lax.optimization_barrier((grad_wide, d_down))
    d_down = lax.psum_scatter(d_down, "dp", scatter_dimension=1, tiled=True).astype(f32)
    d_inner = dot_nt(grad_wide, down_full)
    d_gate = (d_inner * upward * sigma * (1.0 + gate * (1.0 - sigma))).astype(bf16)
    d_upward = (d_inner * swish).astype(bf16)
    d_gate_weight = dot_tn(normed_wide, d_gate).astype(bf16)
    if fused:
        d_resid, sums_two, d_proj, branch, d_up_weight, d_gate_weight = mix_back(
            dp, ctx, d_gate, d_upward, gate_full, up_full, inner, down_full, normed_wide, d_gate_weight, resid,
            grad_rows, gain_two,
        )
    else:
        d_gate_weight = lax.psum_scatter(d_gate_weight, "dp", scatter_dimension=0, tiled=True).astype(f32)
        branch = dot(inner, down_full)
        d_up_weight = dot_tn(normed_wide, d_upward).astype(bf16)
        d_normed_two = scatter_ctx(dot_nt(d_gate, gate_full) + dot_nt(d_upward, up_full), ctx)
        grad, d_gain_two, d_shift_two = norm_backward(d_normed_two, scaled_two, inv_two, gain_two)
        d_resid = grad_rows.astype(f32) + grad
        d_proj = gather_ctx(d_resid.astype(bf16), ctx)
    d_up_weight = lax.psum_scatter(d_up_weight, "dp", scatter_dimension=0, tiled=True).astype(f32)

    d_attended = dot_nt(d_proj, out_full).astype(bf16)
    d_out_weight = dot_tn(attended, d_proj).astype(bf16)
    d_attended, d_down = lax.optimization_barrier((d_attended, d_down))
    d_joined, d_bias = attend_back(qkv, d_attended, lse, table, start)
    d_joined_weight = dot_tn(normed_one, d_joined).astype(bf16)
    d_bias = d_bias.reshape(pairs, 3, 2, HD).transpose(1, 0, 2, 3)
    if fused:
        d_bias = jnp.pad(d_bias.reshape(dp, -1), ((0, 0), (0, width // dp - near * 3 * HD // dp)))
        grad_input, d_joined_weight, d_out_weight, output, vectors, d_bias = closing(
            dp, ctx, d_joined, joined_weight, d_joined_weight, d_out_weight, branch, rows, d_resid, resid,
            gain_one, sums_two, d_bias,
        )
        d_gain_one, d_shift_one, d_gain_two, d_shift_two = vectors
        d_bias = d_bias[0]
    else:
        output = (resid + scatter_ctx(branch, ctx)).astype(bf16)
        at_me = lax.broadcasted_iota(jnp.int32, (1, ctx, 1, 1), 1) == me
        d_out_weight = jnp.where(at_me, d_out_weight.reshape(near, 1, HD, width), jnp.zeros((), bf16))
        d_out_weight = lax.psum_scatter(
            d_out_weight.reshape(width, width), ("dp", "ctx"), scatter_dimension=0, tiled=True
        ).astype(f32)
        d_normed_one = scatter_ctx(dot_nt(d_joined, joined_weight), ctx)
        scaled_one, inv_one = norm_stats(rows.astype(f32))
        grad, d_gain_one, d_shift_one = norm_backward(d_normed_one, scaled_one, inv_one, gain_one)
        grad_input = d_resid + grad
        d_joined_weight = lax.psum_scatter(d_joined_weight, "dp", scatter_dimension=0, tiled=True)
        blocks = exchange_ctx(d_joined_weight.reshape(ctx, rows_here, near * 3 * HD), ctx)
        blocks = blocks.reshape(ctx, rows_here, pairs, 3, 2, HD).transpose(1, 3, 2, 4, 0, 5)
        d_joined_weight = blocks.reshape(rows_here, 3 * width).astype(f32)
        at_me = (lax.broadcasted_iota(jnp.int32, (1, 1, 1, ctx, 1), 3) == me).astype(f32)
        d_bias = (d_bias[:, :, :, None, :] * at_me).reshape(dp * ctx, -1)
        small = jnp.concatenate(
            [t.reshape(dp * ctx, part) for t in (d_gain_one, d_shift_one, d_gain_two, d_shift_two)]
            + [d_bias],
            axis=1,
        )
        small = lax.psum_scatter(small, ("dp", "ctx"), scatter_dimension=0, tiled=True)[0]
        d_gain_one, d_shift_one, d_gain_two, d_shift_two = [
            small[i * part : (i + 1) * part] for i in range(4)
        ]
        d_bias = small[4 * part :]
    return (
        output[None],
        grad_input[None],
        d_gain_one,
        d_shift_one,
        d_joined_weight,
        d_bias,
        d_out_weight,
        d_gain_two,
        d_shift_two,
        d_gate_weight,
        d_up_weight,
        d_down,
    )


def solution(mesh):
    every = ("dp", "ctx")
    return jax.shard_map(
        functools.partial(shards, mesh.shape["dp"], mesh.shape["ctx"]),
        mesh=mesh,
        in_specs=(
            P("dp", "ctx", None),
            P("dp", None),
            P(every),
            P(every),
            P(every, None),
            P(every),
            P(every, None),
            P(every),
            P(every),
            P("dp", "ctx"),
            P("dp", "ctx"),
            P("ctx", "dp"),
            P("dp", "ctx", None),
        ),
        out_specs=(
            P("dp", "ctx", None),
            P("dp", "ctx", None),
            P(every),
            P(every),
            P(every, None),
            P(every),
            P(every, None),
            P(every),
            P(every),
            P("dp", "ctx"),
            P("dp", "ctx"),
            P("ctx", "dp"),
        ),
        check_vma=False,
    )
```
